32 devices in a mesh: mod: 2 (over x), page: 16 (over z, y, core).
Axes of the slice: x: 2, y: 2, z: 4, core: 2. Of those that a mesh axis runs over, the one named last changes fastest.
Arguments:
- states: bfloat16 [2, 16, 512, 768], P('mod', 'page'), may hold values from -6 to 6
- cotangent: bfloat16 [2, 16, 512, 768], P('mod', 'page'), may hold values from -6 to 6
- segments: int32 [16, 512], P('page'), may hold values from 0 to 7, never falling along the last dimension, each value on 1 to 128 neighbouring positions
- box_x: int32 [16, 512], P('page'), may hold values from 0 to 31
- box_y: int32 [16, 512], P('page'), may hold values from 0 to 31
- conv_weight: float32 [3, 768], replicated, may hold values from -3 to 3
- conv_bias: float32 [768], replicated, may hold values from -2 to 2
- w_query: bfloat16 [768, 768], P('page'), may hold values from -0.21875 to 0.21875
- b_query: float32 [768], replicated, may hold values from -3 to 3
- w_key: bfloat16 [768, 768], P('page'), may hold values from -0.21875 to 0.21875
- w_value: bfloat16 [768, 768], P('page'), may hold values from -0.21875 to 0.21875
- b_value: float32 [768], replicated, may hold values from -3 to 3
- w_out: bfloat16 [768, 768], P('page'), may hold values from -0.875 to 0.875
- b_out: float32 [768], replicated, may hold values from -2 to 2
- table_pos: float32 [12, 127], replicated, may hold values from -3 to 3
- table_x: float32 [12, 63], replicated, may hold values from -3 to 3
- table_y: float32 [12, 63], replicated, may hold values from -3 to 3
- gain_one: float32 [768], replicated, may hold values from 0.5 to 1.5
- bias_one: float32 [768], replicated, may hold values from -2 to 2
- w_up: bfloat16 [768, 3072], P('page'), may hold values from -0.21875 to 0.21875
- b_up: float32 [3072], replicated, may hold values from -3 to 3
- w_down: bfloat16 [3072, 768], P('page'), may hold values from -0.109375 to 0.109375
- b_down: float32 [768], replicated, may hold values from -2 to 2
- gain_two: float32 [768], replicated, may hold values from 0.5 to 1.5
- bias_two: float32 [768], replicated, may hold values from -2 to 2
Outputs:
- output: bfloat16 [2, 16, 512, 768], P('mod', 'page')
- grad_states: bfloat16 [2, 16, 512, 768], P('mod', 'page')
- grad_conv_weight: float32 [3, 768], replicated
- grad_conv_bias: float32 [768], replicated
- grad_w_query: float32 [768, 768], P('page')
- grad_b_query: float32 [768], replicated
- grad_w_key: float32 [768, 768], P('page')
- grad_w_value: float32 [768, 768], P('page')
- grad_b_value: float32 [768], replicated
- grad_w_out: float32 [768, 768], P('page')
- grad_b_out: float32 [768], replicated
- grad_table_pos: float32 [12, 127], replicated
- grad_table_x: float32 [12, 63], replicated
- grad_table_y: float32 [12, 63], replicated
- grad_gain_one: float32 [768], replicated
- grad_bias_one: float32 [768], replicated
- grad_w_up: float32 [768, 3072], P('page')
- grad_b_up: float32 [3072], replicated
- grad_w_down: float32 [3072, 768], P('page')
- grad_b_down: float32 [768], replicated
- grad_gain_two: float32 [768], replicated
- grad_bias_two: float32 [768], replicated
The draws below stay inside these ranges and needn't reach their ends.
Inputs may be any that keep to these rules, and one draw needn't show every extreme that they name: `segments`: in each row the page ids never fall and each of the 8 pages has 1 to 128 text tokens, one page exactly 128.
All inputs are finite; a program needn't handle non-finite values.
Results may differ from the reference program's by a relative error of at most 0.017.
The reference program's roundings to bfloat16 on the way count: a program that leaves them out, or rounds other values in their place, can miss the bound.
Values may be sent and summed in bfloat16 or wider, within the bound.
No kernel may reach another device: no remote copies, remote signals or barrier semaphores. Data moves between devices by JAX's collectives and lax.ppermute only.
A program may use at most 192 MiB of HBM per device.

```python
import math
import jax
import jax.numpy as jnp
import numpy as np
from jax import lax

D = 768
FF = 3072
HEADS = 12
HEAD = 64
GRID = 8
PAGES = 8
POS_BINS = 64
BOX_BINS = 32
PATCH = 64
TEXT = 512
ROWS = 16


def place_ends(values, own_key, low, largest):
    longest = values.shape.index(max(values.shape))
    spots = []
    for shift in (0, 1):
        where = [jax.random.randint(jax.random.fold_in(own_key, axis), (), 0, length) for axis, length in enumerate(values.shape)]
        where[longest] = (where[longest] + shift) % values.shape[longest]
        spots.append(tuple(where))
    return values.at[spots[0]].set(low).at[spots[1]].set(largest)


def shard_levels(own_key, extent, cuts, smallest, high):
    gain = 1.0
    for position, blocks in cuts:
        draws = jax.random.uniform(jax.random.fold_in(jax.random.fold_in(own_key, 6), position), (blocks,), jnp.float32, smallest / len(cuts), high / len(cuts))
        gain = gain * jnp.repeat(jnp.exp(draws), extent[position] // blocks).reshape((-1,) + (1,) * (len(extent) - 1 - position))
    return gain


def profile(count, total, limit, skew):
    weights = [(1 << 20) // math.isqrt(grade ** skew) + 1 for grade in range(2, count + 1)]
    rest, holding = total - limit - (count - 1), [1] * (count - 1)
    while rest > 0:
        movable = [i for i in range(count - 1) if holding[i] < limit]
        pool, budget = sum([weights[i] for i in movable]), rest
        for i in movable:
            addition = min(limit - holding[i], max(1, budget * weights[i] // pool), rest)
            holding[i] = holding[i] + addition
            rest = rest - addition
    return np.array([limit] + holding)


def ragged_sizes(stream_key, amount, total, reach, skew):
    if amount == 2:
        one = jax.random.randint(stream_key, (), max(1, total - reach), min(reach, total - 1) + 1)
        return jnp.stack([one, total - one])
    lengths = jnp.asarray(profile(amount, total, reach, skew), jnp.int32)
    twos = (amount - 1) // 2
    giver, sink = lengths[1:1 + 2 * twos:2], lengths[2:2 + 2 * twos:2]
    margin = jnp.minimum(giver - 1, reach - sink)
    moved = jax.random.randint(jax.random.fold_in(stream_key, 1), (twos,), 0, 1 << 20) % (margin + 1)
    lengths = lengths.at[1:1 + 2 * twos:2].set(giver - moved).at[2:2 + 2 * twos:2].set(sink + moved)
    return lengths[jax.random.permutation(jax.random.fold_in(stream_key, 2), amount)]


def noise(rng, dims, width, reach, cuts=(), held_as=jnp.bfloat16):
    values = jax.random.normal(rng, dims, jnp.float32) * width
    if len(cuts) > 0:
        values = shard_levels(rng, dims, cuts, -0.22, 0.18) * values
    return jnp.clip(values, min=-reach, max=reach).astype(held_as)


def setup_inputs(seed: int = 0) -> dict:
    keys = jax.random.split(jax.random.key(seed), 26)
    states = noise(keys[0], (2, ROWS, TEXT, D), 1.0, 6.0, ((0, 2), (1, 16)))
    cotangent = noise(keys[1], (2, ROWS, TEXT, D), 1.0, 6.0, ((0, 2), (1, 16)))
    segments = jax.vmap(lambda own: jnp.searchsorted(jnp.cumsum(ragged_sizes(own, PAGES, TEXT, TEXT // 4, 2)), jnp.arange(TEXT), side="right"))(jax.random.split(keys[2], ROWS)).reshape((ROWS, TEXT)).astype(jnp.int32)
    box_x = place_ends(jax.random.randint(keys[3], (ROWS, TEXT), 0, BOX_BINS), jax.random.fold_in(keys[3], 1), 0, BOX_BINS - 1).astype(jnp.int32)
    box_y = place_ends(jax.random.randint(keys[4], (ROWS, TEXT), 0, BOX_BINS), jax.random.fold_in(keys[4], 1), 0, BOX_BINS - 1).astype(jnp.int32)
    conv_weight = noise(keys[5], (3, D), 0.5, 3.0, (), jnp.float32)
    conv_bias = noise(keys[6], (D,), 0.3, 2.0, (), jnp.float32)
    w_query = noise(keys[7], (D, D), D ** -0.5, 0.21875, ((0, 16),))
    b_query = noise(keys[8], (D,), 0.5, 3.0, (), jnp.float32)
    w_key = noise(keys[9], (D, D), D ** -0.5, 0.21875, ((0, 16),))
    w_value = noise(keys[10], (D, D), D ** -0.5, 0.21875, ((0, 16),))
    b_value = noise(keys[11], (D,), 0.5, 3.0, (), jnp.float32)
    w_out = noise(keys[12], (D, D), (D // 16) ** -0.5, 0.875, ((0, 16),))
    b_out = noise(keys[13], (D,), 0.3, 2.0, (), jnp.float32)
    table_pos = noise(keys[14], (HEADS, 2 * POS_BINS - 1), 0.5, 3.0, (), jnp.float32)
    table_x = noise(keys[15], (HEADS, 2 * BOX_BINS - 1), 0.5, 3.0, (), jnp.float32)
    table_y = noise(keys[16], (HEADS, 2 * BOX_BINS - 1), 0.5, 3.0, (), jnp.float32)
    gain_one = jnp.clip(1.0 + 0.1 * jax.random.normal(keys[17], (D,), jnp.float32), 0.5, 1.5)
    bias_one = noise(keys[18], (D,), 0.3, 2.0, (), jnp.float32)
    w_up = noise(keys[19], (D, FF), D ** -0.5, 0.21875, ((0, 16),))
    b_up = noise(keys[20], (FF,), 0.5, 3.0, (), jnp.float32)
    w_down = noise(keys[21], (FF, D), FF ** -0.5, 0.109375, ((0, 16),))
    b_down = noise(keys[22], (D,), 0.3, 2.0, (), jnp.float32)
    gain_two = jnp.clip(1.0 + 0.1 * jax.random.normal(keys[23], (D,), jnp.float32), 0.5, 1.5)
    bias_two = noise(keys[24], (D,), 0.3, 2.0, (), jnp.float32)
    return dict(states=states, cotangent=cotangent, segments=segments, box_x=box_x, box_y=box_y, conv_weight=conv_weight, conv_bias=conv_bias, w_query=w_query, b_query=b_query, w_key=w_key, w_value=w_value, b_value=b_value, w_out=w_out, b_out=b_out, table_pos=table_pos, table_x=table_x, table_y=table_y, gain_one=gain_one, bias_one=bias_one, w_up=w_up, b_up=b_up, w_down=w_down, b_down=b_down, gain_two=gain_two, bias_two=bias_two)


@jax.custom_vjp
def low(v):
    return lax.optimization_barrier(v.astype(jnp.bfloat16)).astype(jnp.float32)

@jax.custom_vjp
def low_back(v):
    return v

def low_keep(v):
    return (low(v), None)

def low_pass(kept, grad):
    return (grad,)

def back_keep(v):
    return (v, None)

def back_low(kept, grad):
    return (low(grad),)
low.defvjp(low_keep, low_pass)
low_back.defvjp(back_keep, back_low)
dilation = 2
norm_eps = 1e-05
mask_fill = -1000000000.0
highest = lax.Precision.HIGHEST

def shifted(values, offset, fill_value):
    padding = jnp.full((abs(offset),) + values.shape[1:], fill_value, values.dtype)
    if offset > 0:
        return jnp.concatenate([values[offset:], padding], axis=0)
    return jnp.concatenate([padding, values[:offset]], axis=0)

def dilated_mix(inputs, page_ids, conv_weight, conv_bias):
    summed = inputs + conv_bias + conv_weight[1] * inputs
    for tap_index, offset in ((0, -dilation), (2, dilation)):
        moved_rows = shifted(inputs, offset, 0.0)
        moved_pages = shifted(page_ids, offset, -1)
        same_page = (moved_pages == page_ids)[:, None]
        summed = summed + conv_weight[tap_index] * jnp.where(same_page, moved_rows, 0.0)
    return summed

def bias_blocks(table_pos, table_x, table_y):
    head_count = table_pos.shape[0]
    width_all = POS_BINS + 2 * BOX_BINS
    rows_list = []
    offset_col = 0
    for rel_table, bin_count in ((table_pos, POS_BINS), (table_x, BOX_BINS), (table_y, BOX_BINS)):
        index_grid = np.arange(bin_count)[None, :] - np.arange(bin_count)[:, None] + bin_count - 1
        one_block = jnp.take(rel_table, jnp.asarray(index_grid, dtype=jnp.int32), axis=1)
        left_zero = jnp.zeros((head_count, bin_count, offset_col), one_block.dtype)
        right_zero = jnp.zeros((head_count, bin_count, width_all - offset_col - bin_count), one_block.dtype)
        rows_list.append(jnp.concatenate([left_zero, one_block, right_zero], axis=2))
        offset_col = offset_col + bin_count
    return jnp.concatenate(rows_list, axis=1)

def bin_features(pos_bins, bins_x, bins_y):
    return jnp.concatenate([jax.nn.one_hot(pos_bins, POS_BINS, dtype=jnp.float32), jax.nn.one_hot(bins_x, BOX_BINS, dtype=jnp.float32), jax.nn.one_hot(bins_y, BOX_BINS, dtype=jnp.float32)], axis=1)

def token_ids(text_pages, text_x, text_y):
    text_index = jnp.arange(TEXT, dtype=jnp.int32)
    text_pos = text_index * POS_BINS // TEXT
    patch_pos = text_index % PATCH * POS_BINS // PATCH
    patch_page = text_index // PATCH
    patch_x = text_index % GRID * BOX_BINS // GRID
    patch_y = text_index // GRID % GRID * BOX_BINS // GRID
    page_ids = jnp.stack([text_pages.astype(jnp.int32), patch_page])
    pos_bins = jnp.stack([text_pos, patch_pos])
    bins_x = jnp.stack([text_x.astype(jnp.int32), patch_x])
    bins_y = jnp.stack([text_y.astype(jnp.int32), patch_y])
    return (page_ids, pos_bins, bins_x, bins_y)

def layer_norm(values, gain_vec, bias_vec):
    centered = values - lax.optimization_barrier(jnp.mean(values, axis=-1, keepdims=True))
    variance = lax.optimization_barrier(jnp.mean(centered * centered, axis=-1, keepdims=True))
    return centered * lax.rsqrt(variance + norm_eps) * gain_vec + bias_vec

def matmul_high(left_side, right_side):
    return jnp.dot(left_side, right_side, precision=highest)

def forward_row(states_in, params_in, row_ids):
    conv_weight, conv_bias, w_query, b_query, w_key, w_value, b_value, w_out, b_out, table_pos, table_x, table_y, gain_one, bias_one, w_up, b_up, w_down, b_down, gain_two, bias_two = params_in
    page_ids, pos_bins, bins_x, bins_y = row_ids
    mixed = jnp.stack([dilated_mix(states_in[0], page_ids[0], conv_weight, conv_bias), dilated_mix(states_in[1], page_ids[1], conv_weight, conv_bias)])
    flat_mixed = mixed.reshape(2 * TEXT, D)
    mixed_low = low(flat_mixed)
    queries = low(low_back(matmul_high(mixed_low, w_query) + b_query))
    keys_all = low(low_back(matmul_high(mixed_low, w_key)))
    values_all = low(low_back(matmul_high(mixed_low, w_value) + b_value))
    head_q = queries.reshape(2 * TEXT, HEADS, HEAD)
    head_k = keys_all.reshape(2 * TEXT, HEADS, HEAD)
    head_v = values_all.reshape(2 * TEXT, HEADS, HEAD)
    scores = jnp.einsum('qhd,khd->hqk', head_q, head_k, precision=highest) * HEAD ** (-0.5)
    features = bin_features(pos_bins.reshape(-1), bins_x.reshape(-1), bins_y.reshape(-1))
    blocks = bias_blocks(low(table_pos), low(table_x), low(table_y))
    lookup = jnp.einsum('qa,hab->hqb', features, blocks, precision=highest)
    scores = scores + jnp.einsum('hqb,kb->hqk', lookup, features, precision=highest)
    flat_pages = page_ids.reshape(-1)
    same_page = flat_pages[:, None] == flat_pages[None, :]
    scores = low_back(jnp.where(same_page[None], scores, mask_fill))
    attn_prob = jax.nn.softmax(scores, axis=-1)
    context = jnp.einsum('hqk,khd->qhd', low(attn_prob), head_v, precision=highest).reshape(2 * TEXT, D)
    context = low(low_back(context))
    branch = low_back(matmul_high(context, w_out) + b_out)
    first_sum = flat_mixed + branch
    normed = layer_norm(first_sum, gain_one, bias_one)
    hidden = low_back(matmul_high(low(normed), w_up) + b_up)
    active = low(jax.nn.gelu(hidden, approximate=False))
    ffn_out = low_back(matmul_high(active, w_down) + b_down)
    result = layer_norm(normed + ffn_out, gain_two, bias_two)
    return result.reshape(2, TEXT, D)

def reference(states, cotangent, segments, box_x, box_y, conv_weight, conv_bias, w_query, b_query, w_key, w_value, b_value, w_out, b_out, table_pos, table_x, table_y, gain_one, bias_one, w_up, b_up, w_down, b_down, gain_two, bias_two):
    params = tuple((item.astype(jnp.float32) for item in (conv_weight, conv_bias, w_query, b_query, w_key, w_value, b_value, w_out, b_out, table_pos, table_x, table_y, gain_one, bias_one, w_up, b_up, w_down, b_down, gain_two, bias_two)))
    row_states = jnp.swapaxes(states, 0, 1).astype(jnp.float32)
    row_cots = jnp.swapaxes(cotangent, 0, 1).astype(jnp.float32)

    def row_step(grad_total, row_items):
        states_row, cot_row, seg_row, x_row, y_row = row_items
        row_ids = token_ids(seg_row, x_row, y_row)

        def run_row(states_in, params_in):
            return forward_row(states_in, params_in, row_ids)
        out_row, pullback = jax.vjp(run_row, states_row, params)
        grad_in, grad_params = pullback(cot_row)
        grad_total = jax.tree.map(jnp.add, grad_total, grad_params)
        return (grad_total, (out_row.astype(jnp.bfloat16), grad_in.astype(jnp.bfloat16)))
    zero_grads = tuple((jnp.zeros_like(item) for item in params))
    grad_total, (out_rows, grad_rows) = lax.scan(row_step, zero_grads, (row_states, row_cots, segments, box_x, box_y))
    g_conv_w, g_conv_b, g_wq, g_bq, g_wk, g_wv, g_bv, g_wo, g_bo, g_tpos, g_tx, g_ty, g_gain1, g_bias1, g_wup, g_bup, g_wdown, g_bdown, g_gain2, g_bias2 = grad_total
    return (jnp.swapaxes(out_rows, 0, 1), jnp.swapaxes(grad_rows, 0, 1), g_conv_w, g_conv_b, g_wq, g_bq, g_wk, g_wv, g_bv, g_wo, g_bo, g_tpos, g_tx, g_ty, g_gain1, g_bias1, g_wup, g_bup, g_wdown, g_bdown, g_gain2, g_bias2)
```

```python
import functools

import jax
import jax.numpy as jnp
import numpy as np
from jax import lax
from jax.experimental import pallas as pl
from jax.experimental.pallas import tpu as pltpu
from jax.sharding import PartitionSpec as P

HEADS = 12
HEAD = 64
GRID = 8
PAGES = 8
POS_BINS = 64
BOX_BINS = 32
PATCH = 64
TEXT = 512
PAIRS = HEADS // 2
LANES = 2 * HEAD
WINDOW = 144
KEYS = WINDOW + PATCH

dilation = 2
norm_eps = 1e-05
mask_fill = -1000000000.0
bf16 = jnp.bfloat16
f32 = jnp.float32


def shifted(values, offset, fill_value):
    padding = jnp.full((abs(offset),) + values.shape[1:], fill_value, values.dtype)
    if offset > 0:
        return jnp.concatenate([values[offset:], padding], axis=0)
    return jnp.concatenate([padding, values[:offset]], axis=0)


def dilated_mix(inputs, page_ids, conv_weight, conv_bias):
    summed = inputs + conv_bias + conv_weight[1] * inputs
    for tap_index, offset in ((0, -dilation), (2, dilation)):
        moved_rows = shifted(inputs, offset, 0.0)
        moved_pages = shifted(page_ids, offset, -1)
        same_page = (moved_pages == page_ids)[:, None]
        summed = summed + conv_weight[tap_index] * jnp.where(same_page, moved_rows, 0.0)
    return summed


def bin_features(pos_bins, bins_x, bins_y):
    return jnp.concatenate(
        [
            jax.nn.one_hot(pos_bins, POS_BINS, dtype=bf16),
            jax.nn.one_hot(bins_x, BOX_BINS, dtype=bf16),
            jax.nn.one_hot(bins_y, BOX_BINS, dtype=bf16),
        ],
        axis=1,
    )


def token_ids(text_pages, text_x, text_y):
    text_index = jnp.arange(TEXT, dtype=jnp.int32)
    text_pos = text_index * POS_BINS // TEXT
    patch_pos = text_index % PATCH * POS_BINS // PATCH
    patch_page = text_index // PATCH
    patch_x = text_index % GRID * BOX_BINS // GRID
    patch_y = text_index // GRID % GRID * BOX_BINS // GRID
    page_ids = jnp.stack([text_pages, patch_page])
    pos_bins = jnp.stack([text_pos, patch_pos])
    bins_x = jnp.stack([text_x, patch_x])
    bins_y = jnp.stack([text_y, patch_y])
    return (page_ids, pos_bins, bins_x, bins_y)


def layer_norm(values, gain_vec, bias_vec):
    centered = values - jnp.mean(values, axis=-1, keepdims=True)
    variance = jnp.mean(centered * centered, axis=-1, keepdims=True)
    return centered * lax.rsqrt(variance + norm_eps) * gain_vec + bias_vec


def exact_gelu(values):
    return jax.nn.gelu(values, approximate=False)


def plain_dot(left_side, right_side):
    return jnp.dot(left_side, right_side, preferred_element_type=f32)


def dot_left_t(left_side, right_side):
    return lax.dot_general(
        left_side, right_side, (((0,), (0,)), ((), ())), preferred_element_type=f32
    )


def dot_right_t(left_side, right_side):
    return lax.dot_general(
        left_side, right_side, (((1,), (1,)), ((), ())), preferred_element_type=f32
    )


def column_sum(values):
    return jnp.sum(values, axis=0, keepdims=True, dtype=f32)


def iota(shape, axis):
    return lax.broadcasted_iota(jnp.int32, shape, axis)


def bias_block(table_rows):
    pos_part = pltpu.roll(
        jnp.broadcast_to(table_rows[0:1], (POS_BINS, LANES)), 65, 1, stride=1, stride_axis=0
    )
    x_part = pltpu.roll(
        jnp.broadcast_to(table_rows[1:2], (BOX_BINS, LANES)), 33, 1, stride=1, stride_axis=0
    )
    y_part = pltpu.roll(
        jnp.broadcast_to(table_rows[2:3], (BOX_BINS, LANES)), 65, 1, stride=1, stride_axis=0
    )
    lane = iota((POS_BINS, LANES), 1)
    pos_part = jnp.where(lane < POS_BINS, pos_part, 0.0)
    lane = iota((BOX_BINS, LANES), 1)
    x_part = jnp.where((lane >= 64) & (lane < 96), x_part, 0.0)
    y_part = jnp.where(lane >= 96, y_part, 0.0)
    return jnp.concatenate([pos_part, x_part, y_part], axis=0).astype(bf16)


def diagonal_sums(grad_block):
    lane = iota((POS_BINS, LANES), 1)
    pos_part = jnp.where(lane < POS_BINS, grad_block[:64], 0.0)
    lane = iota((BOX_BINS, LANES), 1)
    x_part = jnp.where((lane >= 64) & (lane < 96), grad_block[64:96], 0.0)
    y_part = jnp.where(lane >= 96, grad_block[96:], 0.0)
    pos_part = pltpu.roll(pos_part, 0, 1, stride=1, stride_axis=0)
    x_part = pltpu.roll(x_part, 0, 1, stride=1, stride_axis=0)
    y_part = pltpu.roll(y_part, 96, 1, stride=1, stride_axis=0)
    rows = [jnp.sum(part, axis=0, keepdims=True) for part in (pos_part, x_part, y_part)]
    return jnp.concatenate(rows + [jnp.zeros((5, LANES), f32)], axis=0)


def stacked_heads(rows, low_lane):
    zero = jnp.zeros_like(rows)
    return jnp.concatenate(
        [jnp.where(low_lane, rows, zero), jnp.where(low_lane, zero, rows)], axis=0
    )


def page_operands(page, bounds, q_ref, k_ref, feat_ref, lookup):
    own_at = pl.multiple_of(bounds[page], 16)
    key_at = pl.multiple_of(bounds[3 * PAGES + page], 16)
    low_lane = iota((WINDOW, LANES), 1) < HEAD
    queries = stacked_heads(q_ref[pl.ds(own_at, WINDOW), :], low_lane)
    rel = jnp.concatenate(
        [lookup[pl.ds(own_at, WINDOW), :LANES], lookup[pl.ds(own_at, WINDOW), LANES:]], axis=0
    )
    query_side = jnp.concatenate([rel, queries], axis=1)
    patch_rows = pl.ds(TEXT + PATCH * page, PATCH)
    text_rows = pl.ds(key_at, WINDOW)
    key_side = jnp.concatenate(
        [
            jnp.concatenate([feat_ref[text_rows, :], k_ref[text_rows, :]], axis=1),
            jnp.concatenate([feat_ref[patch_rows, :], k_ref[patch_rows, :]], axis=1),
        ],
        axis=0,
    )
    own_row = iota((WINDOW, LANES), 0) + own_at
    own_ok = (own_row >= bounds[PAGES + page]) & (own_row < bounds[2 * PAGES + page])
    return own_at, key_at, low_lane, own_ok, queries, query_side, key_side, text_rows, patch_rows


def attend_kernel(bounds, q_ref, k_ref, v_ref, feat_ref, own_feat_ref, table_ref, context_ref, lookup):
    blocks = jnp.concatenate([bias_block(table_ref[0]), bias_block(table_ref[1])], axis=1)
    lookup[...] = jnp.dot(own_feat_ref[...], blocks, preferred_element_type=f32).astype(bf16)
    for page in range(PAGES):
        own_at, key_at, low_lane, own_ok, queries, query_side, key_side, text_rows, patch_rows = (
            page_operands(page, bounds, q_ref, k_ref, feat_ref, lookup)
        )
        scores = dot_right_t(query_side, key_side)
        column = iota((1, KEYS), 1)
        key_row = column + key_at
        key_ok = (column >= WINDOW) | (
            (key_row >= bounds[4 * PAGES + page]) & (key_row < bounds[5 * PAGES + page])
        )
        scores = jnp.where(key_ok, scores, mask_fill)
        row_max = jnp.max(scores, axis=1, keepdims=True)
        weights = jnp.exp(scores - row_max)
        total = jnp.sum(weights, axis=1, keepdims=True)
        prob = (weights * (1.0 / total)).astype(bf16)
        values = jnp.concatenate([v_ref[text_rows, :], v_ref[patch_rows, :]], axis=0)
        mixed = jnp.dot(prob, values, preferred_element_type=f32)
        picked = jnp.where(low_lane, mixed[:WINDOW], mixed[WINDOW:])
        before = context_ref[pl.ds(own_at, WINDOW), :].astype(f32)
        context_ref[pl.ds(own_at, WINDOW), :] = jnp.where(own_ok, picked, before).astype(bf16)


def attend_back_kernel(
    bounds,
    q_ref,
    k_ref,
    v_ref,
    grad_ref,
    feat_ref,
    own_feat_ref,
    flip_feat_ref,
    table_ref,
    grad_q_ref,
    grad_k_ref,
    grad_v_ref,
    grad_table_ref,
    lookup,
    grad_lookup,
):
    blocks = jnp.concatenate([bias_block(table_ref[0]), bias_block(table_ref[1])], axis=1)
    lookup[...] = jnp.dot(own_feat_ref[...], blocks, preferred_element_type=f32).astype(bf16)
    for page in range(PAGES):
        own_at, key_at, low_lane, own_ok, queries, query_side, key_side, text_rows, patch_rows = (
            page_operands(page, bounds, q_ref, k_ref, feat_ref, lookup)
        )
        scores = dot_right_t(key_side, query_side)
        row = iota((KEYS, 1), 0)
        key_row = row + key_at
        key_in = (key_row >= bounds[4 * PAGES + page]) & (key_row < bounds[5 * PAGES + page])
        scores = jnp.where((row >= WINDOW) | key_in, scores, mask_fill)
        col_max = jnp.max(scores, axis=0, keepdims=True)
        weights = jnp.exp(scores - col_max)
        total = jnp.sum(weights, axis=0, keepdims=True)
        prob = weights * (1.0 / total)
        grad_rows = grad_ref[pl.ds(own_at, WINDOW), :]
        grad_rows = jnp.where(own_ok, grad_rows, jnp.zeros_like(grad_rows))
        grads = stacked_heads(grad_rows, low_lane)
        values = jnp.concatenate([v_ref[text_rows, :], v_ref[patch_rows, :]], axis=0)
        grad_prob = dot_right_t(values, grads)
        inner = jnp.sum(prob * grad_prob, axis=0, keepdims=True)
        grad_scores = (prob * (grad_prob - inner)).astype(bf16)
        grad_v = jnp.dot(prob.astype(bf16), grads, preferred_element_type=f32)
        grad_k = jnp.dot(grad_scores, queries, preferred_element_type=f32)
        back = dot_left_t(grad_scores, key_side)
        grad_q = jnp.where(low_lane, back[:WINDOW, LANES:], back[WINDOW:, LANES:]) * 0.125
        own_rows = pl.ds(own_at, WINDOW)
        before = grad_q_ref[own_rows, :].astype(f32)
        grad_q_ref[own_rows, :] = jnp.where(own_ok, grad_q, before).astype(bf16)
        grad_lookup[own_rows, :LANES] = jnp.where(
            own_ok, back[:WINDOW, :LANES], grad_lookup[own_rows, :LANES]
        )
        grad_lookup[own_rows, LANES:] = jnp.where(
            own_ok, back[WINDOW:, :LANES], grad_lookup[own_rows, LANES:]
        )
        wide_row = iota((WINDOW, LANES), 0) + key_at
        text_ok = (wide_row >= bounds[4 * PAGES + page]) & (wide_row < bounds[5 * PAGES + page])
        for grad, ref in ((grad_k, grad_k_ref), (grad_v, grad_v_ref)):
            before = ref[text_rows, :].astype(f32)
            ref[text_rows, :] = jnp.where(text_ok, grad[:WINDOW], before).astype(bf16)
            ref[patch_rows, :] = grad[WINDOW:].astype(bf16)
    grad_high = grad_lookup[...].astype(bf16)
    grad_rest = (grad_lookup[...] - grad_high.astype(f32)).astype(bf16)
    flip = flip_feat_ref[...]
    grad_block = dot_left_t(flip, grad_high) + dot_left_t(flip, grad_rest)
    grad_table_ref[0] = diagonal_sums(grad_block[:, :LANES])
    grad_table_ref[1] = diagonal_sums(grad_block[:, LANES:])


def column_spec(rows, first=0):
    return pl.BlockSpec((rows, LANES), lambda pair, bounds: (0, pair + first))


def whole_spec(rows):
    return pl.BlockSpec((rows, LANES), lambda pair, bounds: (0, 0))


table_spec = pl.BlockSpec((2, 8, LANES), lambda pair, bounds: (pair, 0, 0))


def attend(bounds, queries, keys_values, features, own_features, tables):
    return pl.pallas_call(
        attend_kernel,
        grid_spec=pltpu.PrefetchScalarGridSpec(
            num_scalar_prefetch=1,
            grid=(PAIRS,),
            in_specs=[
                column_spec(TEXT),
                column_spec(2 * TEXT),
                column_spec(2 * TEXT, PAIRS),
                whole_spec(2 * TEXT),
                whole_spec(TEXT),
                table_spec,
            ],
            out_specs=column_spec(TEXT),
            scratch_shapes=[pltpu.VMEM((TEXT, 2 * LANES), bf16)],
        ),
        out_shape=jax.ShapeDtypeStruct((TEXT, HEADS * HEAD), bf16),
        cost_estimate=pl.CostEstimate(
            flops=4_000_000_000, bytes_accessed=6_000_000, transcendentals=3_000_000
        ),
        name="attend",
    )(bounds, queries, keys_values, keys_values, features, own_features, tables)


def attend_back(bounds, queries, keys_values, grad_context, features, own_features, flip, tables):
    return pl.pallas_call(
        attend_back_kernel,
        grid_spec=pltpu.PrefetchScalarGridSpec(
            num_scalar_prefetch=1,
            grid=(PAIRS,),
            in_specs=[
                column_spec(TEXT),
                column_spec(2 * TEXT),
                column_spec(2 * TEXT, PAIRS),
                column_spec(TEXT),
                whole_spec(2 * TEXT),
                whole_spec(TEXT),
                whole_spec(TEXT),
                table_spec,
            ],
            out_specs=[
                column_spec(TEXT),
                column_spec(2 * TEXT),
                column_spec(2 * TEXT),
                table_spec,
            ],
            scratch_shapes=[
                pltpu.VMEM((TEXT, 2 * LANES), bf16),
                pltpu.VMEM((TEXT, 2 * LANES), f32),
            ],
        ),
        out_shape=[
            jax.ShapeDtypeStruct((TEXT, HEADS * HEAD), bf16),
            jax.ShapeDtypeStruct((2 * TEXT, HEADS * HEAD), bf16),
            jax.ShapeDtypeStruct((2 * TEXT, HEADS * HEAD), bf16),
            jax.ShapeDtypeStruct((HEADS, 8, LANES), f32),
        ],
        cost_estimate=pl.CostEstimate(
            flops=9_000_000_000, bytes_accessed=9_000_000, transcendentals=3_000_000
        ),
        name="attend_back",
    )(
        bounds,
        queries,
        keys_values,
        keys_values,
        grad_context,
        features,
        own_features,
        flip,
        tables,
    )


def page_bounds(segments, is_text):
    pages = jnp.arange(PAGES, dtype=jnp.int32)
    low = jnp.sum(segments[None, :] < pages[:, None], axis=1, dtype=jnp.int32)
    high = jnp.sum(segments[None, :] <= pages[:, None], axis=1, dtype=jnp.int32)
    own_low = jnp.where(is_text, low, pages * PATCH)
    own_high = jnp.where(is_text, high, (pages + 1) * PATCH)

    def aligned(start):
        return jnp.minimum(start // 16 * 16, TEXT - WINDOW)

    return jnp.concatenate([aligned(own_low), own_low, own_high, aligned(low), low, high])


def sum_everywhere(values):
    count = lax.axis_size("page")
    if count & (count - 1):
        values = lax.psum(values, "page")
    else:
        step = 1
        while step < count:
            values = values + lax.ppermute(values, "page", [(i, i ^ step) for i in range(count)])
            step = step * 2
    return values + swap(values)


def swap(values):
    return lax.ppermute(values, "mod", [(0, 1), (1, 0)])


def local(
    states,
    cotangent,
    segments,
    box_x,
    box_y,
    conv_weight,
    conv_bias,
    w_query,
    b_query,
    w_key,
    w_value,
    b_value,
    w_out,
    b_out,
    table_pos,
    table_x,
    table_y,
    gain_one,
    bias_one,
    w_up,
    b_up,
    w_down,
    b_down,
    gain_two,
    bias_two,
):
    is_text = lax.axis_index("mod") == 0
    d_model = states.shape[3]
    own_low = states[0, 0]
    other_low = swap(own_low)
    rows_each = w_query.shape[0]
    d_ff = w_up.shape[1]
    pack_qkv = jnp.concatenate([w_query, w_key, w_value], axis=1)
    full_qkv = lax.all_gather(pack_qkv, "page", axis=0, tiled=True)
    full_query = full_qkv[:, :d_model]
    full_kv = full_qkv[:, d_model:]
    pack_rest = jnp.concatenate([w_out, w_up], axis=1)
    pack_rest, w_down = lax.optimization_barrier((pack_rest, w_down, full_qkv))[:2]
    full_rest = lax.all_gather(pack_rest, "page", axis=0, tiled=True)
    full_out = full_rest[:, :d_model]
    full_up = full_rest[:, d_model:]
    full_down = lax.all_gather(w_down, "page", axis=0, tiled=True)

    page_ids, pos_bins, bins_x, bins_y = token_ids(segments[0], box_x[0], box_y[0])
    bounds = page_bounds(segments[0], is_text)
    own_pages = jnp.where(is_text, page_ids[0], page_ids[1])
    features = bin_features(pos_bins.reshape(-1), bins_x.reshape(-1), bins_y.reshape(-1))
    flipped = bin_features(
        POS_BINS - 1 - pos_bins.reshape(-1),
        BOX_BINS - 1 - bins_x.reshape(-1),
        BOX_BINS - 1 - bins_y.reshape(-1),
    )
    own_feats = jnp.where(is_text, features[:TEXT], features[TEXT:])
    own_flip = jnp.where(is_text, flipped[:TEXT], flipped[TEXT:])
    tables = jnp.stack(
        [
            jnp.pad(table_pos, ((0, 0), (0, LANES - table_pos.shape[1]))),
            jnp.pad(table_x, ((0, 0), (0, LANES - table_x.shape[1]))),
            jnp.pad(table_y, ((0, 0), (0, LANES - table_y.shape[1]))),
        ],
        axis=1,
    )
    tables = jnp.pad(tables, ((0, 0), (0, 5), (0, 0)))

    def mix_fn(inputs_f, weight_f, bias_f):
        return dilated_mix(inputs_f, own_pages, weight_f, bias_f)

    own_states = own_low.astype(f32)
    mixed, mix_pull = jax.vjp(mix_fn, own_states, conv_weight, conv_bias)
    mixed_low = mixed.astype(bf16)
    other_pages = jnp.where(is_text, page_ids[1], page_ids[0])
    other_mixed = dilated_mix(other_low.astype(f32), other_pages, conv_weight, conv_bias)
    other_mixed = other_mixed.astype(bf16)
    mixed_all = jnp.concatenate(
        [jnp.where(is_text, mixed_low, other_mixed), jnp.where(is_text, other_mixed, mixed_low)],
        axis=0,
    )
    queries = ((plain_dot(mixed_low, full_query) + b_query).astype(bf16) * 0.125).astype(bf16)
    kv_bias = jnp.concatenate([jnp.zeros_like(b_value), b_value])
    keys_values = (plain_dot(mixed_all, full_kv) + kv_bias).astype(bf16)
    context = attend(bounds, queries, keys_values, features, own_feats, tables)

    first_sum = mixed + plain_dot(context, full_out) + b_out
    normed, norm_one_pull = jax.vjp(layer_norm, first_sum, gain_one, bias_one)
    normed_low = normed.astype(bf16)
    hidden = plain_dot(normed_low, full_up) + b_up
    active, gelu_pull = jax.vjp(exact_gelu, hidden)
    active_low = active.astype(bf16)
    ffn_out = plain_dot(active_low, full_down) + b_down
    output_row, norm_two_pull = jax.vjp(layer_norm, normed + ffn_out, gain_two, bias_two)
    grad_out = cotangent[0, 0].astype(f32)
    grad_sum_two, grad_gain_two, grad_bias_two = norm_two_pull(grad_out)
    grad_ffn = grad_sum_two.astype(bf16)
    g_wdown = dot_left_t(active_low, grad_ffn).astype(bf16)
    grad_b_down = column_sum(grad_ffn)
    (grad_hidden_f,) = gelu_pull(dot_right_t(grad_ffn, full_down))
    grad_hidden = grad_hidden_f.astype(bf16)
    g_wup = dot_left_t(normed_low, grad_hidden).astype(bf16)
    grad_b_up = column_sum(grad_hidden)
    grad_normed = grad_sum_two + dot_right_t(grad_hidden, full_up)
    grad_first, grad_gain_one, grad_bias_one = norm_one_pull(grad_normed)
    grad_branch = grad_first.astype(bf16)
    g_wout = dot_left_t(context, grad_branch).astype(bf16)
    grad_b_out = column_sum(grad_branch)
    shard_down = lax.psum_scatter(g_wdown, "page", scatter_dimension=0, tiled=True)
    shard_rest = lax.psum_scatter(
        jnp.concatenate([g_wout, g_wup], axis=1), "page", scatter_dimension=0, tiled=True
    )
    grad_context = dot_right_t(grad_branch, full_out).astype(bf16)
    grad_queries, grad_keys, grad_values, grad_tables = attend_back(
        bounds, queries, keys_values, grad_context, features, own_feats, own_flip, tables
    )
    g_wq = dot_left_t(mixed_low, grad_queries).astype(bf16)
    g_wk = dot_left_t(mixed_all, grad_keys).astype(bf16)
    g_wv = dot_left_t(mixed_all, grad_values).astype(bf16)
    shard_qkv = lax.psum_scatter(
        jnp.concatenate([g_wq, g_wk, g_wv], axis=1), "page", scatter_dimension=0, tiled=True
    )
    grad_b_query = column_sum(grad_queries)
    grad_b_value = column_sum(grad_values)
    from_keys = dot_right_t(grad_keys, full_kv[:, :d_model]) + dot_right_t(
        grad_values, full_kv[:, d_model:]
    )
    to_other = jnp.where(is_text, from_keys[TEXT:], from_keys[:TEXT]).astype(bf16)
    from_other = swap(to_other).astype(f32)
    grad_mixed = (
        grad_first
        + dot_right_t(grad_queries, full_query)
        + jnp.where(is_text, from_keys[:TEXT], from_keys[TEXT:])
        + from_other
    )
    grad_in, grad_conv_w, grad_conv_b = mix_pull(grad_mixed)

    table_rows = grad_tables[:, :3].reshape(6, 768)
    packed = jnp.concatenate(
        [
            grad_conv_w,
            grad_conv_b[None],
            grad_b_query,
            grad_b_value,
            grad_b_out,
            grad_gain_one[None],
            grad_bias_one[None],
            grad_b_down,
            grad_gain_two[None],
            grad_bias_two[None],
            grad_b_up.reshape(d_ff // d_model, d_model),
            table_rows,
            jnp.zeros((2, d_model), f32),
        ],
        axis=0,
    )
    packed = sum_everywhere(packed)
    g_tables = packed[16:22].reshape(HEADS, 3, LANES)

    def both(shard):
        return shard.astype(f32) + swap(shard).astype(f32)

    shard_down = both(shard_down)
    shard_rest = both(shard_rest)
    shard_qkv = both(shard_qkv)
    return (
        output_row.astype(bf16)[None, None],
        grad_in.astype(bf16)[None, None],
        packed[0:3],
        packed[3],
        shard_qkv[:, :d_model],
        packed[4],
        shard_qkv[:, d_model : 2 * d_model],
        shard_qkv[:, 2 * d_model :],
        packed[5],
        shard_rest[:, :d_model],
        packed[6],
        g_tables[:, 0, : table_pos.shape[1]],
        g_tables[:, 1, 64 : 64 + table_x.shape[1]],
        g_tables[:, 2, 64 : 64 + table_y.shape[1]],
        packed[7],
        packed[8],
        shard_rest[:, d_model:],
        packed[12:16].reshape(d_ff),
        shard_down,
        packed[9],
        packed[10],
        packed[11],
    )


def solution(mesh):
    rows = P("mod", "page", None, None)
    ids = P("page", None)
    cut = P("page", None)
    return jax.shard_map(
        local,
        mesh=mesh,
        in_specs=(
            rows, rows, ids, ids, ids, P(), P(), cut, P(), cut, cut, P(), cut,
            P(), P(), P(), P(), P(), P(), cut, P(), cut, P(), P(), P(),
        ),
        out_specs=(
            rows, rows, P(), P(), cut, P(), cut, cut, P(), cut, P(), P(), P(),
            P(), P(), P(), cut, P(), cut, P(), P(), P(),
        ),
        check_vma=False,
    )
```

```python
import functools

import jax
import jax.numpy as jnp
import numpy as np
from jax import lax
from jax.experimental import pallas as pl
from jax.experimental.pallas import tpu as pltpu
from jax.sharding import PartitionSpec as P

HEADS = 12
HEAD = 64
GRID = 8
PAGES = 8
POS_BINS = 64
BOX_BINS = 32
PATCH = 64
TEXT = 512
PAIRS = HEADS // 2
LANES = 2 * HEAD
WINDOW = 144
KEYS = WINDOW + PATCH

dilation = 2
norm_eps = 1e-05
mask_fill = -1000000000.0
bf16 = jnp.bfloat16
f32 = jnp.float32


def shifted(values, offset, fill_value):
    padding = jnp.full((abs(offset),) + values.shape[1:], fill_value, values.dtype)
    if offset > 0:
        return jnp.concatenate([values[offset:], padding], axis=0)
    return jnp.concatenate([padding, values[:offset]], axis=0)


def dilated_mix(inputs, page_ids, conv_weight, conv_bias):
    summed = inputs + conv_bias + conv_weight[1] * inputs
    for tap_index, offset in ((0, -dilation), (2, dilation)):
        moved_rows = shifted(inputs, offset, 0.0)
        moved_pages = shifted(page_ids, offset, -1)
        same_page = (moved_pages == page_ids)[:, None]
        summed = summed + conv_weight[tap_index] * jnp.where(same_page, moved_rows, 0.0)
    return summed


def bin_features(pos_bins, bins_x, bins_y):
    return jnp.concatenate(
        [
            jax.nn.one_hot(pos_bins, POS_BINS, dtype=bf16),
            jax.nn.one_hot(bins_x, BOX_BINS, dtype=bf16),
            jax.nn.one_hot(bins_y, BOX_BINS, dtype=bf16),
        ],
        axis=1,
    )


def token_ids(text_pages, text_x, text_y):
    text_index = jnp.arange(TEXT, dtype=jnp.int32)
    text_pos = text_index * POS_BINS // TEXT
    patch_pos = text_index % PATCH * POS_BINS // PATCH
    patch_page = text_index // PATCH
    patch_x = text_index % GRID * BOX_BINS // GRID
    patch_y = text_index // GRID % GRID * BOX_BINS // GRID
    page_ids = jnp.stack([text_pages, patch_page])
    pos_bins = jnp.stack([text_pos, patch_pos])
    bins_x = jnp.stack([text_x, patch_x])
    bins_y = jnp.stack([text_y, patch_y])
    return (page_ids, pos_bins, bins_x, bins_y)


def layer_norm(values, gain_vec, bias_vec):
    centered = values - jnp.mean(values, axis=-1, keepdims=True)
    variance = jnp.mean(centered * centered, axis=-1, keepdims=True)
    return centered * lax.rsqrt(variance + norm_eps) * gain_vec + bias_vec


def exact_gelu(values):
    return jax.nn.gelu(values, approximate=False)


def plain_dot(left_side, right_side):
    return jnp.dot(left_side, right_side, preferred_element_type=f32)


def dot_left_t(left_side, right_side):
    return lax.dot_general(
        left_side, right_side, (((0,), (0,)), ((), ())), preferred_element_type=f32
    )


def dot_right_t(left_side, right_side):
    return lax.dot_general(
        left_side, right_side, (((1,), (1,)), ((), ())), preferred_element_type=f32
    )


def column_sum(values):
    return jnp.sum(values, axis=0, keepdims=True, dtype=f32)


def iota(shape, axis):
    return lax.broadcasted_iota(jnp.int32, shape, axis)


def bias_block(table_rows):
    pos_part = pltpu.roll(
        jnp.broadcast_to(table_rows[0:1], (POS_BINS, LANES)), 65, 1, stride=1, stride_axis=0
    )
    x_part = pltpu.roll(
        jnp.broadcast_to(table_rows[1:2], (BOX_BINS, LANES)), 33, 1, stride=1, stride_axis=0
    )
    y_part = pltpu.roll(
        jnp.broadcast_to(table_rows[2:3], (BOX_BINS, LANES)), 65, 1, stride=1, stride_axis=0
    )
    lane = iota((POS_BINS, LANES), 1)
    pos_part = jnp.where(lane < POS_BINS, pos_part, 0.0)
    lane = iota((BOX_BINS, LANES), 1)
    x_part = jnp.where((lane >= 64) & (lane < 96), x_part, 0.0)
    y_part = jnp.where(lane >= 96, y_part, 0.0)
    return jnp.concatenate([pos_part, x_part, y_part], axis=0).astype(bf16)


def diagonal_sums(grad_block):
    lane = iota((POS_BINS, LANES), 1)
    pos_part = jnp.where(lane < POS_BINS, grad_block[:64], 0.0)
    lane = iota((BOX_BINS, LANES), 1)
    x_part = jnp.where((lane >= 64) & (lane < 96), grad_block[64:96], 0.0)
    y_part = jnp.where(lane >= 96, grad_block[96:], 0.0)
    pos_part = pltpu.roll(pos_part, 0, 1, stride=1, stride_axis=0)
    x_part = pltpu.roll(x_part, 0, 1, stride=1, stride_axis=0)
    y_part = pltpu.roll(y_part, 96, 1, stride=1, stride_axis=0)
    rows = [jnp.sum(part, axis=0, keepdims=True) for part in (pos_part, x_part, y_part)]
    return jnp.concatenate(rows + [jnp.zeros((5, LANES), f32)], axis=0)


def stacked_heads(rows, low_lane):
    zero = jnp.zeros_like(rows)
    return jnp.concatenate(
        [jnp.where(low_lane, rows, zero), jnp.where(low_lane, zero, rows)], axis=0
    )


def page_operands(page, bounds, q_ref, k_ref, feat_ref, lookup):
    own_at = pl.multiple_of(bounds[page], 16)
    key_at = pl.multiple_of(bounds[3 * PAGES + page], 16)
    low_lane = iota((WINDOW, LANES), 1) < HEAD
    queries = stacked_heads(q_ref[pl.ds(own_at, WINDOW), :], low_lane)
    rel = jnp.concatenate(
        [lookup[pl.ds(own_at, WINDOW), :LANES], lookup[pl.ds(own_at, WINDOW), LANES:]], axis=0
    )
    query_side = jnp.concatenate([rel, queries], axis=1)
    patch_rows = pl.ds(TEXT + PATCH * page, PATCH)
    text_rows = pl.ds(key_at, WINDOW)
    key_side = jnp.concatenate(
        [
            jnp.concatenate([feat_ref[text_rows, :], k_ref[text_rows, :]], axis=1),
            jnp.concatenate([feat_ref[patch_rows, :], k_ref[patch_rows, :]], axis=1),
        ],
        axis=0,
    )
    own_row = iota((WINDOW, LANES), 0) + own_at
    own_ok = (own_row >= bounds[PAGES + page]) & (own_row < bounds[2 * PAGES + page])
    return own_at, key_at, low_lane, own_ok, queries, query_side, key_side, text_rows, patch_rows


def attend_kernel(bounds, q_ref, k_ref, v_ref, feat_ref, own_feat_ref, table_ref, context_ref, lookup):
    blocks = jnp.concatenate([bias_block(table_ref[0]), bias_block(table_ref[1])], axis=1)
    lookup[...] = jnp.dot(own_feat_ref[...], blocks, preferred_element_type=f32).astype(bf16)
    for page in range(PAGES):
        own_at, key_at, low_lane, own_ok, queries, query_side, key_side, text_rows, patch_rows = (
            page_operands(page, bounds, q_ref, k_ref, feat_ref, lookup)
        )
        scores = dot_right_t(query_side, key_side)
        column = iota((1, KEYS), 1)
        key_row = column + key_at
        key_ok = (column >= WINDOW) | (
            (key_row >= bounds[4 * PAGES + page]) & (key_row < bounds[5 * PAGES + page])
        )
        scores = jnp.where(key_ok, scores, mask_fill)
        row_max = jnp.max(scores, axis=1, keepdims=True)
        weights = jnp.exp(scores - row_max)
        total = jnp.sum(weights, axis=1, keepdims=True)
        prob = (weights * (1.0 / total)).astype(bf16)
        values = jnp.concatenate([v_ref[text_rows, :], v_ref[patch_rows, :]], axis=0)
        mixed = jnp.dot(prob, values, preferred_element_type=f32)
        picked = jnp.where(low_lane, mixed[:WINDOW], mixed[WINDOW:])
        before = context_ref[pl.ds(own_at, WINDOW), :].astype(f32)
        context_ref[pl.ds(own_at, WINDOW), :] = jnp.where(own_ok, picked, before).astype(bf16)


def attend_back_kernel(
    bounds,
    q_ref,
    k_ref,
    v_ref,
    grad_ref,
    feat_ref,
    own_feat_ref,
    flip_feat_ref,
    table_ref,
    grad_q_ref,
    grad_k_ref,
    grad_v_ref,
    grad_table_ref,
    lookup,
    grad_lookup,
):
    blocks = jnp.concatenate([bias_block(table_ref[0]), bias_block(table_ref[1])], axis=1)
    lookup[...] = jnp.dot(own_feat_ref[...], blocks, preferred_element_type=f32).astype(bf16)
    for page in range(PAGES):
        own_at, key_at, low_lane, own_ok, queries, query_side, key_side, text_rows, patch_rows = (
            page_operands(page, bounds, q_ref, k_ref, feat_ref, lookup)
        )
        scores = dot_right_t(key_side, query_side)
        row = iota((KEYS, 1), 0)
        key_row = row + key_at
        key_in = (key_row >= bounds[4 * PAGES + page]) & (key_row < bounds[5 * PAGES + page])
        scores = jnp.where((row >= WINDOW) | key_in, scores, mask_fill)
        col_max = jnp.max(scores, axis=0, keepdims=True)
        weights = jnp.exp(scores - col_max)
        total = jnp.sum(weights, axis=0, keepdims=True)
        prob = weights * (1.0 / total)
        grad_rows = grad_ref[pl.ds(own_at, WINDOW), :]
        grad_rows = jnp.where(own_ok, grad_rows, jnp.zeros_like(grad_rows))
        grads = stacked_heads(grad_rows, low_lane)
        values = jnp.concatenate([v_ref[text_rows, :], v_ref[patch_rows, :]], axis=0)
        grad_prob = dot_right_t(values, grads)
        inner = jnp.sum(prob * grad_prob, axis=0, keepdims=True)
        grad_scores = (prob * (grad_prob - inner)).astype(bf16)
        grad_v = jnp.dot(prob.astype(bf16), grads, preferred_element_type=f32)
        grad_k = jnp.dot(grad_scores, queries, preferred_element_type=f32)
        back = dot_left_t(grad_scores, key_side)
        grad_q = jnp.where(low_lane, back[:WINDOW, LANES:], back[WINDOW:, LANES:]) * 0.125
        own_rows = pl.ds(own_at, WINDOW)
        before = grad_q_ref[own_rows, :].astype(f32)
        grad_q_ref[own_rows, :] = jnp.where(own_ok, grad_q, before).astype(bf16)
        grad_lookup[own_rows, :LANES] = jnp.where(
            own_ok, back[:WINDOW, :LANES], grad_lookup[own_rows, :LANES]
        )
        grad_lookup[own_rows, LANES:] = jnp.where(
            own_ok, back[WINDOW:, :LANES], grad_lookup[own_rows, LANES:]
        )
        wide_row = iota((WINDOW, LANES), 0) + key_at
        text_ok = (wide_row >= bounds[4 * PAGES + page]) & (wide_row < bounds[5 * PAGES + page])
        for grad, ref in ((grad_k, grad_k_ref), (grad_v, grad_v_ref)):
            before = ref[text_rows, :].astype(f32)
            ref[text_rows, :] = jnp.where(text_ok, grad[:WINDOW], before).astype(bf16)
            ref[patch_rows, :] = grad[WINDOW:].astype(bf16)
    grad_high = grad_lookup[...].astype(bf16)
    grad_rest = (grad_lookup[...] - grad_high.astype(f32)).astype(bf16)
    flip = flip_feat_ref[...]
    grad_block = dot_left_t(flip, grad_high) + dot_left_t(flip, grad_rest)
    grad_table_ref[0] = diagonal_sums(grad_block[:, :LANES])
    grad_table_ref[1] = diagonal_sums(grad_block[:, LANES:])


def column_spec(rows, first=0):
    return pl.BlockSpec((rows, LANES), lambda pair, bounds: (0, pair + first))


def whole_spec(rows):
    return pl.BlockSpec((rows, LANES), lambda pair, bounds: (0, 0))


table_spec = pl.BlockSpec((2, 8, LANES), lambda pair, bounds: (pair, 0, 0))


def attend(bounds, queries, keys_values, features, own_features, tables):
    return pl.pallas_call(
        attend_kernel,
        grid_spec=pltpu.PrefetchScalarGridSpec(
            num_scalar_prefetch=1,
            grid=(PAIRS,),
            in_specs=[
                column_spec(TEXT),
                column_spec(2 * TEXT),
                column_spec(2 * TEXT, PAIRS),
                whole_spec(2 * TEXT),
                whole_spec(TEXT),
                table_spec,
            ],
            out_specs=column_spec(TEXT),
            scratch_shapes=[pltpu.VMEM((TEXT, 2 * LANES), bf16)],
        ),
        out_shape=jax.ShapeDtypeStruct((TEXT, HEADS * HEAD), bf16),
        cost_estimate=pl.CostEstimate(
            flops=4_000_000_000, bytes_accessed=6_000_000, transcendentals=3_000_000
        ),
        name="attend",
    )(bounds, queries, keys_values, keys_values, features, own_features, tables)


def attend_back(bounds, queries, keys_values, grad_context, features, own_features, flip, tables):
    return pl.pallas_call(
        attend_back_kernel,
        grid_spec=pltpu.PrefetchScalarGridSpec(
            num_scalar_prefetch=1,
            grid=(PAIRS,),
            in_specs=[
                column_spec(TEXT),
                column_spec(2 * TEXT),
                column_spec(2 * TEXT, PAIRS),
                column_spec(TEXT),
                whole_spec(2 * TEXT),
                whole_spec(TEXT),
                whole_spec(TEXT),
                table_spec,
            ],
            out_specs=[
                column_spec(TEXT),
                column_spec(2 * TEXT),
                column_spec(2 * TEXT),
                table_spec,
            ],
            scratch_shapes=[
                pltpu.VMEM((TEXT, 2 * LANES), bf16),
                pltpu.VMEM((TEXT, 2 * LANES), f32),
            ],
        ),
        out_shape=[
            jax.ShapeDtypeStruct((TEXT, HEADS * HEAD), bf16),
            jax.ShapeDtypeStruct((2 * TEXT, HEADS * HEAD), bf16),
            jax.ShapeDtypeStruct((2 * TEXT, HEADS * HEAD), bf16),
            jax.ShapeDtypeStruct((HEADS, 8, LANES), f32),
        ],
        cost_estimate=pl.CostEstimate(
            flops=9_000_000_000, bytes_accessed=9_000_000, transcendentals=3_000_000
        ),
        name="attend_back",
    )(
        bounds,
        queries,
        keys_values,
        keys_values,
        grad_context,
        features,
        own_features,
        flip,
        tables,
    )


def exchange(values, mask):
    count = lax.axis_size("page")
    return lax.ppermute(values, "page", [(i, i ^ mask) for i in range(count)])


def place_kernel(page, *refs):
    pieces, full_ref, sems = refs[:4], refs[4], refs[5]
    rows = pieces[0].shape[1]
    copies = []
    for mask in range(16):
        at = pl.multiple_of((page[0] ^ mask) * rows, 16)
        copies.append(
            pltpu.make_async_copy(
                pieces[mask & 3].at[mask >> 2], full_ref.at[pl.ds(at, rows)], sems.at[mask]
            )
        )
    for copy in copies:
        copy.start()
    for copy in copies:
        copy.wait()


def gathered(shard, page):
    rows, width = shard.shape
    column = jnp.stack([shard] + [exchange(shard, 4 * step) for step in (1, 2, 3)])
    across = exchange(column, 2)
    partner = exchange(column, 1)
    partner_across = exchange(across, 1)
    full = pl.pallas_call(
        place_kernel,
        grid_spec=pltpu.PrefetchScalarGridSpec(
            num_scalar_prefetch=1,
            grid=(),
            in_specs=[pl.BlockSpec(memory_space=pl.ANY)] * 4,
            out_specs=pl.BlockSpec(memory_space=pltpu.VMEM),
            scratch_shapes=[pltpu.SemaphoreType.DMA((16,))],
        ),
        out_shape=jax.ShapeDtypeStruct((16 * rows, width), shard.dtype),
        cost_estimate=pl.CostEstimate(
            flops=0, bytes_accessed=64 * rows * width, transcendentals=0
        ),
        name="place_rows",
    )(page, column, partner, across, partner_across)
    return full, column


def grad_rows_kernel(page, x_ref, h_ref, keep_ref, send_ref, product):
    rows = keep_ref.shape[1]
    product[...] = dot_left_t(x_ref[...], h_ref[...])
    mine = pl.multiple_of((page[0] & 1) * rows, 16)
    theirs = pl.multiple_of((1 - (page[0] & 1)) * rows, 16)
    keep_ref[0] = product[pl.ds(mine, rows), :].astype(bf16)
    send_ref[0] = product[pl.ds(theirs, rows), :].astype(bf16)


def grad_by_rows(inputs, grads, page):
    tokens, width = inputs.shape
    columns = grads.shape[1]
    rows = width // 16

    def slot(block, page):
        mask = block ^ (page[0] >> 1)
        return ((mask & 1) * 4 + (mask >> 1), 0, 0)

    half = jax.ShapeDtypeStruct((8, rows, columns), bf16)
    return pl.pallas_call(
        grad_rows_kernel,
        grid_spec=pltpu.PrefetchScalarGridSpec(
            num_scalar_prefetch=1,
            grid=(8,),
            in_specs=[
                pl.BlockSpec((tokens, 2 * rows), lambda block, page: (0, block)),
                pl.BlockSpec((tokens, columns), lambda block, page: (0, 0)),
            ],
            out_specs=[pl.BlockSpec((1, rows, columns), slot)] * 2,
            scratch_shapes=[pltpu.VMEM((2 * rows, columns), f32)],
        ),
        out_shape=[half, half],
        cost_estimate=pl.CostEstimate(
            flops=2 * tokens * width * columns,
            bytes_accessed=2 * (tokens * (width + columns) + width * columns),
            transcendentals=0,
        ),
        name="grad_rows",
    )(page, inputs, grads)


def grad_columns_kernel(parts, page, *refs):
    ins, keep_ref, send_ref, product = refs[: 2 * len(parts)], refs[-3], refs[-2], refs[-1]
    rows, width = keep_ref.shape[1], keep_ref.shape[2]
    step = pl.program_id(0)
    first = 0
    for index, count in enumerate(parts):
        x_ref, h_ref = ins[2 * index], ins[2 * index + 1]

        @pl.when((step >= first) & (step < first + count))
        def _():
            product[...] = dot_left_t(x_ref[...], h_ref[...])

        first = first + count
    for slot in range(8):
        mask = (slot & 3) * 4 + (slot >> 2) * 2
        mine = pl.multiple_of((page[0] ^ mask) * rows, 16)
        theirs = pl.multiple_of((page[0] ^ (mask + 1)) * rows, 16)
        keep_ref[slot] = product[pl.ds(mine, rows), :].astype(bf16)
        send_ref[slot] = product[pl.ds(theirs, rows), :].astype(bf16)


def grad_by_columns(pairs, page, tile):
    width = pairs[0][0].shape[1]
    rows = width // 16
    parts = tuple(grads.shape[1] // tile for _, grads in pairs)
    steps = sum(parts)
    specs = []
    operands = []
    first = 0
    flops = 0
    for (inputs, grads), count in zip(pairs, parts):
        specs.append(pl.BlockSpec(inputs.shape, lambda step, page: (0, 0)))

        def column(step, page, first=first, count=count):
            return (0, jnp.clip(step - first, 0, count - 1))

        specs.append(pl.BlockSpec((grads.shape[0], tile), column))
        operands += [inputs, grads]
        first = first + count
        flops = flops + 2 * inputs.shape[0] * width * grads.shape[1]
    half = jax.ShapeDtypeStruct((8, rows, steps * tile), bf16)
    return pl.pallas_call(
        functools.partial(grad_columns_kernel, parts),
        grid_spec=pltpu.PrefetchScalarGridSpec(
            num_scalar_prefetch=1,
            grid=(steps,),
            in_specs=specs,
            out_specs=[pl.BlockSpec((8, rows, tile), lambda step, page: (0, 0, step))] * 2,
            scratch_shapes=[pltpu.VMEM((width, tile), f32)],
        ),
        out_shape=[half, half],
        cost_estimate=pl.CostEstimate(
            flops=flops, bytes_accessed=4 * width * steps * tile, transcendentals=0
        ),
        name="grad_columns",
    )(page, *operands)


def scattered(keep, send):
    partner = exchange(send, 1)

    def pair(at):
        return keep[at].astype(f32) + partner[at].astype(f32)

    across = exchange(pair(slice(4, 8)).astype(bf16), 2)

    def four(z):
        return pair(z) + across[z].astype(f32)

    total = four(0)
    for step in (1, 2, 3):
        total = total + exchange(four(step).astype(bf16), 4 * step).astype(f32)
    low = total.astype(bf16)
    return low.astype(f32) + swap(low).astype(f32)


def summed_rows(pairs):
    grads = jnp.concatenate([dot_left_t(*pair).astype(bf16) for pair in pairs], axis=1)
    shard = lax.psum_scatter(grads, "page", scatter_dimension=0, tiled=True)
    return shard.astype(f32) + swap(shard).astype(f32)


def page_bounds(segments, is_text):
    pages = jnp.arange(PAGES, dtype=jnp.int32)
    low = jnp.sum(segments[None, :] < pages[:, None], axis=1, dtype=jnp.int32)
    high = jnp.sum(segments[None, :] <= pages[:, None], axis=1, dtype=jnp.int32)
    own_low = jnp.where(is_text, low, pages * PATCH)
    own_high = jnp.where(is_text, high, (pages + 1) * PATCH)

    def aligned(start):
        return jnp.minimum(start // 16 * 16, TEXT - WINDOW)

    return jnp.concatenate([aligned(own_low), own_low, own_high, aligned(low), low, high])


def sum_everywhere(values):
    count = lax.axis_size("page")
    if count & (count - 1):
        values = lax.psum(values, "page")
    else:
        step = 1
        while step < count:
            values = values + lax.ppermute(values, "page", [(i, i ^ step) for i in range(count)])
            step = step * 2
    return values + swap(values)


def swap(values):
    return lax.ppermute(values, "mod", [(0, 1), (1, 0)])


def local(
    states,
    cotangent,
    segments,
    box_x,
    box_y,
    conv_weight,
    conv_bias,
    w_query,
    b_query,
    w_key,
    w_value,
    b_value,
    w_out,
    b_out,
    table_pos,
    table_x,
    table_y,
    gain_one,
    bias_one,
    w_up,
    b_up,
    w_down,
    b_down,
    gain_two,
    bias_two,
):
    is_text = lax.axis_index("mod") == 0
    d_model = states.shape[3]
    own_low = states[0, 0]
    other_low = swap(own_low)
    rows_each = w_query.shape[0]
    d_ff = w_up.shape[1]
    page = lax.axis_index("page").astype(jnp.int32)[None]
    fast = lax.axis_size("page") == 16 and rows_each % 16 == 0 and w_down.shape[0] % 16 == 0
    pack_qkv = jnp.concatenate([w_query, w_key, w_value], axis=1)
    pack_rest = jnp.concatenate([w_out, w_up], axis=1)
    if fast:
        full_qkv, column = gathered(pack_qkv, page)
        pack_rest, column = lax.optimization_barrier((pack_rest, column))
        full_rest, column = gathered(pack_rest, page)
        w_down, column = lax.optimization_barrier((w_down, column))
        full_down, column = gathered(w_down, page)
    else:
        full_qkv = lax.all_gather(pack_qkv, "page", axis=0, tiled=True)
        full_rest = lax.all_gather(pack_rest, "page", axis=0, tiled=True)
        full_down = lax.all_gather(w_down, "page", axis=0, tiled=True)
    full_query = full_qkv[:, :d_model]
    full_kv = full_qkv[:, d_model:]
    full_out = full_rest[:, :d_model]
    full_up = full_rest[:, d_model:]

    page_ids, pos_bins, bins_x, bins_y = token_ids(segments[0], box_x[0], box_y[0])
    bounds = page_bounds(segments[0], is_text)
    own_pages = jnp.where(is_text, page_ids[0], page_ids[1])
    features = bin_features(pos_bins.reshape(-1), bins_x.reshape(-1), bins_y.reshape(-1))
    flipped = bin_features(
        POS_BINS - 1 - pos_bins.reshape(-1),
        BOX_BINS - 1 - bins_x.reshape(-1),
        BOX_BINS - 1 - bins_y.reshape(-1),
    )
    own_feats = jnp.where(is_text, features[:TEXT], features[TEXT:])
    own_flip = jnp.where(is_text, flipped[:TEXT], flipped[TEXT:])
    tables = jnp.stack(
        [
            jnp.pad(table_pos, ((0, 0), (0, LANES - table_pos.shape[1]))),
            jnp.pad(table_x, ((0, 0), (0, LANES - table_x.shape[1]))),
            jnp.pad(table_y, ((0, 0), (0, LANES - table_y.shape[1]))),
        ],
        axis=1,
    )
    tables = jnp.pad(tables, ((0, 0), (0, 5), (0, 0)))

    def mix_fn(inputs_f, weight_f, bias_f):
        return dilated_mix(inputs_f, own_pages, weight_f, bias_f)

    own_states = own_low.astype(f32)
    mixed, mix_pull = jax.vjp(mix_fn, own_states, conv_weight, conv_bias)
    mixed_low = mixed.astype(bf16)
    other_pages = jnp.where(is_text, page_ids[1], page_ids[0])
    other_mixed = dilated_mix(other_low.astype(f32), other_pages, conv_weight, conv_bias)
    other_mixed = other_mixed.astype(bf16)
    mixed_all = jnp.concatenate(
        [jnp.where(is_text, mixed_low, other_mixed), jnp.where(is_text, other_mixed, mixed_low)],
        axis=0,
    )
    queries = ((plain_dot(mixed_low, full_query) + b_query).astype(bf16) * 0.125).astype(bf16)
    kv_bias = jnp.concatenate([jnp.zeros_like(b_value), b_value])
    keys_values = (plain_dot(mixed_all, full_kv) + kv_bias).astype(bf16)
    context = attend(bounds, queries, keys_values, features, own_feats, tables)

    first_sum = mixed + plain_dot(context, full_out) + b_out
    normed, norm_one_pull = jax.vjp(layer_norm, first_sum, gain_one, bias_one)
    normed_low = normed.astype(bf16)
    hidden = plain_dot(normed_low, full_up) + b_up
    active, gelu_pull = jax.vjp(exact_gelu, hidden)
    active_low = active.astype(bf16)
    ffn_out = plain_dot(active_low, full_down) + b_down
    output_row, norm_two_pull = jax.vjp(layer_norm, normed + ffn_out, gain_two, bias_two)
    grad_out = cotangent[0, 0].astype(f32)
    grad_sum_two, grad_gain_two, grad_bias_two = norm_two_pull(grad_out)
    grad_ffn = grad_sum_two.astype(bf16)
    if fast:
        shard_down = scattered(*grad_by_rows(active_low, grad_ffn, page))
    else:
        shard_down = summed_rows([(active_low, grad_ffn)])
    grad_b_down = column_sum(grad_ffn)
    (grad_hidden_f,) = gelu_pull(dot_right_t(grad_ffn, full_down))
    grad_hidden = grad_hidden_f.astype(bf16)
    grad_b_up = column_sum(grad_hidden)
    grad_normed = grad_sum_two + dot_right_t(grad_hidden, full_up)
    grad_first, grad_gain_one, grad_bias_one = norm_one_pull(grad_normed)
    grad_branch = grad_first.astype(bf16)
    grad_b_out = column_sum(grad_branch)
    pairs = [(context, grad_branch), (normed_low, grad_hidden)]
    if fast:
        shard_rest = scattered(*grad_by_columns(pairs, page, d_model))
    else:
        shard_rest = summed_rows(pairs)
    grad_context = dot_right_t(grad_branch, full_out).astype(bf16)
    grad_queries, grad_keys, grad_values, grad_tables = attend_back(
        bounds, queries, keys_values, grad_context, features, own_feats, own_flip, tables
    )
    pairs = [(mixed_low, grad_queries), (mixed_all, grad_keys), (mixed_all, grad_values)]
    if fast:
        shard_qkv = scattered(*grad_by_columns(pairs, page, d_model))
    else:
        shard_qkv = summed_rows(pairs)
    grad_b_query = column_sum(grad_queries)
    grad_b_value = column_sum(grad_values)
    from_keys = dot_right_t(grad_keys, full_kv[:, :d_model]) + dot_right_t(
        grad_values, full_kv[:, d_model:]
    )
    to_other = jnp.where(is_text, from_keys[TEXT:], from_keys[:TEXT]).astype(bf16)
    from_other = swap(to_other).astype(f32)
    grad_mixed = (
        grad_first
        + dot_right_t(grad_queries, full_query)
        + jnp.where(is_text, from_keys[:TEXT], from_keys[TEXT:])
        + from_other
    )
    grad_in, grad_conv_w, grad_conv_b = mix_pull(grad_mixed)

    table_rows = grad_tables[:, :3].reshape(6, 768)
    packed = jnp.concatenate(
        [
            grad_conv_w,
            grad_conv_b[None],
            grad_b_query,
            grad_b_value,
            grad_b_out,
            grad_gain_one[None],
            grad_bias_one[None],
            grad_b_down,
            grad_gain_two[None],
            grad_bias_two[None],
            grad_b_up.reshape(d_ff // d_model, d_model),
            table_rows,
            jnp.zeros((2, d_model), f32),
        ],
        axis=0,
    )
    packed = sum_everywhere(packed)
    g_tables = packed[16:22].reshape(HEADS, 3, LANES)

    return (
        output_row.astype(bf16)[None, None],
        grad_in.astype(bf16)[None, None],
        packed[0:3],
        packed[3],
        shard_qkv[:, :d_model],
        packed[4],
        shard_qkv[:, d_model : 2 * d_model],
        shard_qkv[:, 2 * d_model :],
        packed[5],
        shard_rest[:, :d_model],
        packed[6],
        g_tables[:, 0, : table_pos.shape[1]],
        g_tables[:, 1, 64 : 64 + table_x.shape[1]],
        g_tables[:, 2, 64 : 64 + table_y.shape[1]],
        packed[7],
        packed[8],
        shard_rest[:, d_model:],
        packed[12:16].reshape(d_ff),
        shard_down,
        packed[9],
        packed[10],
        packed[11],
    )


def solution(mesh):
    rows = P("mod", "page", None, None)
    ids = P("page", None)
    cut = P("page", None)
    return jax.shard_map(
        local,
        mesh=mesh,
        in_specs=(
            rows, rows, ids, ids, ids, P(), P(), cut, P(), cut, cut, P(), cut,
            P(), P(), P(), P(), P(), P(), cut, P(), cut, P(), P(), P(),
        ),
        out_specs=(
            rows, rows, P(), P(), cut, P(), cut, cut, P(), cut, P(), P(), P(),
            P(), P(), P(), cut, P(), cut, P(), P(), P(),
        ),
        check_vma=False,
    )
```

```python
import functools

import jax
import jax.numpy as jnp
import numpy as np
from jax import lax
from jax.experimental import pallas as pl
from jax.experimental.pallas import tpu as pltpu
from jax.sharding import PartitionSpec as P

HEADS = 12
HEAD = 64
GRID = 8
PAGES = 8
POS_BINS = 64
BOX_BINS = 32
PATCH = 64
TEXT = 512
PAIRS = HEADS // 2
LANES = 2 * HEAD
WINDOW = 144
KEYS = WINDOW + PATCH

dilation = 2
norm_eps = 1e-05
mask_fill = -1000000000.0
bf16 = jnp.bfloat16
f32 = jnp.float32


def shifted(values, offset, fill_value):
    padding = jnp.full((abs(offset),) + values.shape[1:], fill_value, values.dtype)
    if offset > 0:
        return jnp.concatenate([values[offset:], padding], axis=0)
    return jnp.concatenate([padding, values[:offset]], axis=0)


def dilated_mix(inputs, page_ids, conv_weight, conv_bias):
    summed = inputs + conv_bias + conv_weight[1] * inputs
    for tap_index, offset in ((0, -dilation), (2, dilation)):
        moved_rows = shifted(inputs, offset, 0.0)
        moved_pages = shifted(page_ids, offset, -1)
        same_page = (moved_pages == page_ids)[:, None]
        summed = summed + conv_weight[tap_index] * jnp.where(same_page, moved_rows, 0.0)
    return summed


def bin_features(pos_bins, bins_x, bins_y):
    return jnp.concatenate(
        [
            jax.nn.one_hot(pos_bins, POS_BINS, dtype=bf16),
            jax.nn.one_hot(bins_x, BOX_BINS, dtype=bf16),
            jax.nn.one_hot(bins_y, BOX_BINS, dtype=bf16),
        ],
        axis=1,
    )


def token_ids(text_pages, text_x, text_y):
    text_index = jnp.arange(TEXT, dtype=jnp.int32)
    text_pos = text_index * POS_BINS // TEXT
    patch_pos = text_index % PATCH * POS_BINS // PATCH
    patch_page = text_index // PATCH
    patch_x = text_index % GRID * BOX_BINS // GRID
    patch_y = text_index // GRID % GRID * BOX_BINS // GRID
    page_ids = jnp.stack([text_pages, patch_page])
    pos_bins = jnp.stack([text_pos, patch_pos])
    bins_x = jnp.stack([text_x, patch_x])
    bins_y = jnp.stack([text_y, patch_y])
    return (page_ids, pos_bins, bins_x, bins_y)


def layer_norm(values, gain_vec, bias_vec):
    centered = values - jnp.mean(values, axis=-1, keepdims=True)
    variance = jnp.mean(centered * centered, axis=-1, keepdims=True)
    return centered * lax.rsqrt(variance + norm_eps) * gain_vec + bias_vec


def exact_gelu(values):
    return jax.nn.gelu(values, approximate=False)


def plain_dot(left_side, right_side):
    return jnp.dot(left_side, right_side, preferred_element_type=f32)


def dot_left_t(left_side, right_side):
    return lax.dot_general(
        left_side, right_side, (((0,), (0,)), ((), ())), preferred_element_type=f32
    )


def dot_right_t(left_side, right_side):
    return lax.dot_general(
        left_side, right_side, (((1,), (1,)), ((), ())), preferred_element_type=f32
    )


def column_sum(values):
    return jnp.sum(values, axis=0, keepdims=True, dtype=f32)


def iota(shape, axis):
    return lax.broadcasted_iota(jnp.int32, shape, axis)


def bias_block(table_rows):
    pos_part = pltpu.roll(
        jnp.broadcast_to(table_rows[0:1], (POS_BINS, LANES)), 65, 1, stride=1, stride_axis=0
    )
    x_part = pltpu.roll(
        jnp.broadcast_to(table_rows[1:2], (BOX_BINS, LANES)), 33, 1, stride=1, stride_axis=0
    )
    y_part = pltpu.roll(
        jnp.broadcast_to(table_rows[2:3], (BOX_BINS, LANES)), 65, 1, stride=1, stride_axis=0
    )
    lane = iota((POS_BINS, LANES), 1)
    pos_part = jnp.where(lane < POS_BINS, pos_part, 0.0)
    lane = iota((BOX_BINS, LANES), 1)
    x_part = jnp.where((lane >= 64) & (lane < 96), x_part, 0.0)
    y_part = jnp.where(lane >= 96, y_part, 0.0)
    return jnp.concatenate([pos_part, x_part, y_part], axis=0).astype(bf16)


def diagonal_sums(grad_block):
    lane = iota((POS_BINS, LANES), 1)
    pos_part = jnp.where(lane < POS_BINS, grad_block[:64], 0.0)
    lane = iota((BOX_BINS, LANES), 1)
    x_part = jnp.where((lane >= 64) & (lane < 96), grad_block[64:96], 0.0)
    y_part = jnp.where(lane >= 96, grad_block[96:], 0.0)
    pos_part = pltpu.roll(pos_part, 0, 1, stride=1, stride_axis=0)
    x_part = pltpu.roll(x_part, 0, 1, stride=1, stride_axis=0)
    y_part = pltpu.roll(y_part, 96, 1, stride=1, stride_axis=0)
    rows = [jnp.sum(part, axis=0, keepdims=True) for part in (pos_part, x_part, y_part)]
    return jnp.concatenate(rows + [jnp.zeros((5, LANES), f32)], axis=0)


def stacked_heads(rows, low_lane):
    zero = jnp.zeros_like(rows)
    return jnp.concatenate(
        [jnp.where(low_lane, rows, zero), jnp.where(low_lane, zero, rows)], axis=0
    )


def page_operands(page, bounds, q_ref, k_ref, feat_ref, lookup):
    own_at = pl.multiple_of(bounds[page], 16)
    key_at = pl.multiple_of(bounds[3 * PAGES + page], 16)
    low_lane = iota((WINDOW, LANES), 1) < HEAD
    queries = stacked_heads(q_ref[pl.ds(own_at, WINDOW), :], low_lane)
    rel = jnp.concatenate(
        [lookup[pl.ds(own_at, WINDOW), :LANES], lookup[pl.ds(own_at, WINDOW), LANES:]], axis=0
    )
    query_side = jnp.concatenate([rel, queries], axis=1)
    patch_rows = pl.ds(TEXT + PATCH * page, PATCH)
    text_rows = pl.ds(key_at, WINDOW)
    key_side = jnp.concatenate(
        [
            jnp.concatenate([feat_ref[text_rows, :], k_ref[text_rows, :]], axis=1),
            jnp.concatenate([feat_ref[patch_rows, :], k_ref[patch_rows, :]], axis=1),
        ],
        axis=0,
    )
    own_row = iota((WINDOW, LANES), 0) + own_at
    own_ok = (own_row >= bounds[PAGES + page]) & (own_row < bounds[2 * PAGES + page])
    return own_at, key_at, low_lane, own_ok, queries, query_side, key_side, text_rows, patch_rows


def attend_kernel(bounds, q_ref, k_ref, v_ref, feat_ref, own_feat_ref, table_ref, context_ref, lookup):
    blocks = jnp.concatenate([bias_block(table_ref[0]), bias_block(table_ref[1])], axis=1)
    lookup[...] = jnp.dot(own_feat_ref[...], blocks, preferred_element_type=f32).astype(bf16)
    for page in range(PAGES):
        own_at, key_at, low_lane, own_ok, queries, query_side, key_side, text_rows, patch_rows = (
            page_operands(page, bounds, q_ref, k_ref, feat_ref, lookup)
        )
        scores = dot_right_t(query_side, key_side)
        column = iota((1, KEYS), 1)
        key_row = column + key_at
        key_ok = (column >= WINDOW) | (
            (key_row >= bounds[4 * PAGES + page]) & (key_row < bounds[5 * PAGES + page])
        )
        scores = jnp.where(key_ok, scores, mask_fill)
        row_max = jnp.max(scores, axis=1, keepdims=True)
        weights = jnp.exp(scores - row_max)
        total = jnp.sum(weights, axis=1, keepdims=True)
        prob = (weights * (1.0 / total)).astype(bf16)
        values = jnp.concatenate([v_ref[text_rows, :], v_ref[patch_rows, :]], axis=0)
        mixed = jnp.dot(prob, values, preferred_element_type=f32)
        picked = jnp.where(low_lane, mixed[:WINDOW], mixed[WINDOW:])
        before = context_ref[pl.ds(own_at, WINDOW), :].astype(f32)
        context_ref[pl.ds(own_at, WINDOW), :] = jnp.where(own_ok, picked, before).astype(bf16)


def attend_back_kernel(
    bounds,
    q_ref,
    k_ref,
    v_ref,
    grad_ref,
    feat_ref,
    own_feat_ref,
    flip_feat_ref,
    table_ref,
    grad_q_ref,
    grad_k_ref,
    grad_v_ref,
    grad_table_ref,
    lookup,
    grad_lookup,
):
    blocks = jnp.concatenate([bias_block(table_ref[0]), bias_block(table_ref[1])], axis=1)
    lookup[...] = jnp.dot(own_feat_ref[...], blocks, preferred_element_type=f32).astype(bf16)
    for page in range(PAGES):
        own_at, key_at, low_lane, own_ok, queries, query_side, key_side, text_rows, patch_rows = (
            page_operands(page, bounds, q_ref, k_ref, feat_ref, lookup)
        )
        scores = dot_right_t(key_side, query_side)
        row = iota((KEYS, 1), 0)
        key_row = row + key_at
        key_in = (key_row >= bounds[4 * PAGES + page]) & (key_row < bounds[5 * PAGES + page])
        scores = jnp.where((row >= WINDOW) | key_in, scores, mask_fill)
        col_max = jnp.max(scores, axis=0, keepdims=True)
        weights = jnp.exp(scores - col_max)
        total = jnp.sum(weights, axis=0, keepdims=True)
        prob = weights * (1.0 / total)
        grad_rows = grad_ref[pl.ds(own_at, WINDOW), :]
        grad_rows = jnp.where(own_ok, grad_rows, jnp.zeros_like(grad_rows))
        grads = stacked_heads(grad_rows, low_lane)
        values = jnp.concatenate([v_ref[text_rows, :], v_ref[patch_rows, :]], axis=0)
        grad_prob = dot_right_t(values, grads)
        inner = jnp.sum(prob * grad_prob, axis=0, keepdims=True)
        grad_scores = (prob * (grad_prob - inner)).astype(bf16)
        grad_v = jnp.dot(prob.astype(bf16), grads, preferred_element_type=f32)
        grad_k = jnp.dot(grad_scores, queries, preferred_element_type=f32)
        back = dot_left_t(grad_scores, key_side)
        grad_q = jnp.where(low_lane, back[:WINDOW, LANES:], back[WINDOW:, LANES:]) * 0.125
        own_rows = pl.ds(own_at, WINDOW)
        before = grad_q_ref[own_rows, :].astype(f32)
        grad_q_ref[own_rows, :] = jnp.where(own_ok, grad_q, before).astype(bf16)
        grad_lookup[own_rows, :LANES] = jnp.where(
            own_ok, back[:WINDOW, :LANES], grad_lookup[own_rows, :LANES]
        )
        grad_lookup[own_rows, LANES:] = jnp.where(
            own_ok, back[WINDOW:, :LANES], grad_lookup[own_rows, LANES:]
        )
        wide_row = iota((WINDOW, LANES), 0) + key_at
        text_ok = (wide_row >= bounds[4 * PAGES + page]) & (wide_row < bounds[5 * PAGES + page])
        for grad, ref in ((grad_k, grad_k_ref), (grad_v, grad_v_ref)):
            before = ref[text_rows, :].astype(f32)
            ref[text_rows, :] = jnp.where(text_ok, grad[:WINDOW], before).astype(bf16)
            ref[patch_rows, :] = grad[WINDOW:].astype(bf16)
    grad_high = grad_lookup[...].astype(bf16)
    grad_rest = (grad_lookup[...] - grad_high.astype(f32)).astype(bf16)
    flip = flip_feat_ref[...]
    grad_block = dot_left_t(flip, grad_high) + dot_left_t(flip, grad_rest)
    grad_table_ref[0] = diagonal_sums(grad_block[:, :LANES])
    grad_table_ref[1] = diagonal_sums(grad_block[:, LANES:])


def column_spec(rows, first=0):
    return pl.BlockSpec((rows, LANES), lambda pair, bounds: (0, pair + first))


def tables_spec(first=0):
    return pl.BlockSpec((2, 8, LANES), lambda pair, bounds: (pair + first, 0, 0))


def whole_spec(rows):
    return pl.BlockSpec((rows, LANES), lambda pair, bounds: (0, 0))


def attend(bounds, queries, keys_values, features, own_features, tables):
    return pl.pallas_call(
        attend_kernel,
        grid_spec=pltpu.PrefetchScalarGridSpec(
            num_scalar_prefetch=1,
            grid=(PAIRS,),
            in_specs=[
                column_spec(TEXT),
                column_spec(2 * TEXT),
                column_spec(2 * TEXT, PAIRS),
                whole_spec(2 * TEXT),
                whole_spec(TEXT),
                tables_spec(),
            ],
            out_specs=column_spec(TEXT),
            scratch_shapes=[pltpu.VMEM((TEXT, 2 * LANES), bf16)],
        ),
        out_shape=jax.ShapeDtypeStruct((TEXT, HEADS * HEAD), bf16),
        cost_estimate=pl.CostEstimate(
            flops=4_000_000_000, bytes_accessed=6_000_000, transcendentals=3_000_000
        ),
        name="attend",
    )(bounds, queries, keys_values, keys_values, features, own_features, tables)


def attend_back(
    bounds, queries, keys_values, grad_context, features, own_features, flip, tables, first, count
):
    return pl.pallas_call(
        attend_back_kernel,
        grid_spec=pltpu.PrefetchScalarGridSpec(
            num_scalar_prefetch=1,
            grid=(count,),
            in_specs=[
                column_spec(TEXT, first),
                column_spec(2 * TEXT, first),
                column_spec(2 * TEXT, PAIRS + first),
                column_spec(TEXT, first),
                whole_spec(2 * TEXT),
                whole_spec(TEXT),
                whole_spec(TEXT),
                tables_spec(first),
            ],
            out_specs=[
                column_spec(TEXT),
                column_spec(2 * TEXT),
                column_spec(2 * TEXT),
                tables_spec(),
            ],
            scratch_shapes=[
                pltpu.VMEM((TEXT, 2 * LANES), bf16),
                pltpu.VMEM((TEXT, 2 * LANES), f32),
            ],
        ),
        out_shape=[
            jax.ShapeDtypeStruct((TEXT, count * LANES), bf16),
            jax.ShapeDtypeStruct((2 * TEXT, count * LANES), bf16),
            jax.ShapeDtypeStruct((2 * TEXT, count * LANES), bf16),
            jax.ShapeDtypeStruct((2 * count, 8, LANES), f32),
        ],
        cost_estimate=pl.CostEstimate(
            flops=4_000_000_000 * count, bytes_accessed=1_500_000 * count, transcendentals=500_000
        ),
        name="attend_back",
    )(
        bounds,
        queries,
        keys_values,
        keys_values,
        grad_context,
        features,
        own_features,
        flip,
        tables,
    )


def exchange(values, mask):
    count = lax.axis_size("page")
    return lax.ppermute(values, "page", [(i, i ^ mask) for i in range(count)])


def after(value, *earlier):
    return lax.optimization_barrier((value, *earlier))[0]


def slot_mask(slot):
    return (slot & 3) * 4 + (slot >> 2) * 2


def place_kernel(place, *refs):
    pieces, full_ref, sems = refs[:4], refs[4], refs[5]
    rows = pieces[0].shape[1]
    copies = []
    for index in range(16):
        mask = (index >> 2) * 4 + (index & 3)
        at = pl.multiple_of((place[0] ^ mask) * rows, 16)
        copies.append(
            pltpu.make_async_copy(
                pieces[index & 3].at[index >> 2], full_ref.at[pl.ds(at, rows)], sems.at[index]
            )
        )
    for copy in copies:
        copy.start()
    for copy in copies:
        copy.wait()


def place_halves_kernel(place, *refs):
    pieces, full_ref, sems = refs[:4], refs[4], refs[5]
    rows, half = pieces[0].shape[1], pieces[0].shape[2]
    copies = []
    for index in range(32):
        kind = index >> 3
        mask = slot_mask(index & 7) + (kind & 1)
        at = pl.multiple_of((place[0] ^ mask) * rows, 16)
        column = pl.multiple_of((place[1] ^ (kind >> 1)) * half, 128)
        copies.append(
            pltpu.make_async_copy(
                pieces[kind].at[index & 7],
                full_ref.at[pl.ds(at, rows), pl.ds(column, half)],
                sems.at[index],
            )
        )
    for copy in copies:
        copy.start()
    for copy in copies:
        copy.wait()


def place_rows(place, pieces, width, kernel):
    rows = pieces[0].shape[1]
    return pl.pallas_call(
        kernel,
        grid_spec=pltpu.PrefetchScalarGridSpec(
            num_scalar_prefetch=1,
            grid=(),
            in_specs=[pl.BlockSpec(memory_space=pl.ANY)] * 4,
            out_specs=pl.BlockSpec(memory_space=pltpu.VMEM),
            scratch_shapes=[pltpu.SemaphoreType.DMA((32,))],
        ),
        out_shape=jax.ShapeDtypeStruct((16 * rows, width), bf16),
        cost_estimate=pl.CostEstimate(
            flops=0, bytes_accessed=64 * rows * width, transcendentals=0
        ),
        name="place_rows",
    )(place, *pieces)


def column_of(shard):
    return jnp.stack([shard] + [exchange(shard, 4 * step) for step in (1, 2, 3)])


def pieces_of(column):
    across = exchange(column, 2)
    return column, exchange(column, 1), across, exchange(across, 1)


def grad_rows_kernel(page, x_ref, h_ref, keep_ref, send_ref, product):
    rows = keep_ref.shape[1]
    product[...] = dot_left_t(x_ref[...], h_ref[...])
    mine = pl.multiple_of((page[0] & 1) * rows, 16)
    theirs = pl.multiple_of((1 - (page[0] & 1)) * rows, 16)
    keep_ref[0] = product[pl.ds(mine, rows), :].astype(bf16)
    send_ref[0] = product[pl.ds(theirs, rows), :].astype(bf16)


def grad_by_rows(inputs, grads, page):
    tokens, width = inputs.shape
    columns = grads.shape[1]
    rows = width // 16

    def slot(block, page):
        mask = block ^ (page[0] >> 1)
        return ((mask & 1) * 4 + (mask >> 1), 0, 0)

    half = jax.ShapeDtypeStruct((8, rows, columns), bf16)
    return pl.pallas_call(
        grad_rows_kernel,
        grid_spec=pltpu.PrefetchScalarGridSpec(
            num_scalar_prefetch=1,
            grid=(8,),
            in_specs=[
                pl.BlockSpec((tokens, 2 * rows), lambda block, page: (0, block)),
                pl.BlockSpec((tokens, columns), lambda block, page: (0, 0)),
            ],
            out_specs=[pl.BlockSpec((1, rows, columns), slot)] * 2,
            scratch_shapes=[pltpu.VMEM((2 * rows, columns), f32)],
        ),
        out_shape=[half, half],
        cost_estimate=pl.CostEstimate(
            flops=2 * tokens * width * columns,
            bytes_accessed=2 * (tokens * (width + columns) + width * columns),
            transcendentals=0,
        ),
        name="grad_rows",
    )(page, inputs, grads)


def grad_columns_kernel(parts, page, *refs):
    ins, keep_ref, send_ref, product = refs[: 2 * len(parts)], refs[-3], refs[-2], refs[-1]
    rows, width = keep_ref.shape[1], keep_ref.shape[2]
    step = pl.program_id(0)
    first = 0
    for index, count in enumerate(parts):
        x_ref, h_ref = ins[2 * index], ins[2 * index + 1]

        @pl.when((step >= first) & (step < first + count))
        def _():
            product[...] = dot_left_t(x_ref[...], h_ref[...])

        first = first + count
    for slot in range(8):
        mask = slot_mask(slot)
        mine = pl.multiple_of((page[0] ^ mask) * rows, 16)
        theirs = pl.multiple_of((page[0] ^ (mask + 1)) * rows, 16)
        keep_ref[slot] = product[pl.ds(mine, rows), :].astype(bf16)
        send_ref[slot] = product[pl.ds(theirs, rows), :].astype(bf16)


def grad_by_columns(pairs, page, tile):
    width = pairs[0][0].shape[1]
    rows = width // 16
    parts = tuple(grads.shape[1] // tile for _, grads in pairs)
    steps = sum(parts)
    specs = []
    operands = []
    first = 0
    flops = 0
    for (inputs, grads), count in zip(pairs, parts):
        specs.append(pl.BlockSpec(inputs.shape, lambda step, page: (0, 0)))

        def column(step, page, first=first, count=count):
            return (0, jnp.clip(step - first, 0, count - 1))

        specs.append(pl.BlockSpec((grads.shape[0], tile), column))
        operands += [inputs, grads]
        first = first + count
        flops = flops + 2 * inputs.shape[0] * width * grads.shape[1]
    half = jax.ShapeDtypeStruct((8, rows, steps * tile), bf16)
    return pl.pallas_call(
        functools.partial(grad_columns_kernel, parts),
        grid_spec=pltpu.PrefetchScalarGridSpec(
            num_scalar_prefetch=1,
            grid=(steps,),
            in_specs=specs,
            out_specs=[pl.BlockSpec((8, rows, tile), lambda step, page: (0, 0, step))] * 2,
            scratch_shapes=[pltpu.VMEM((width, tile), f32)],
        ),
        out_shape=[half, half],
        cost_estimate=pl.CostEstimate(
            flops=flops, bytes_accessed=4 * width * steps * tile, transcendentals=0
        ),
        name="grad_columns",
    )(page, *operands)


def pair_sum(keep, partner, at):
    return keep[at].astype(f32) + partner[at].astype(f32)


def across_send(keep, partner):
    return pair_sum(keep, partner, slice(4, 8)).astype(bf16)


def column_sends(keep, partner, across):
    return [
        (pair_sum(keep, partner, step) + across[step].astype(f32)).astype(bf16)
        for step in (1, 2, 3)
    ]


def column_total(keep, partner, across, arrived):
    total = pair_sum(keep, partner, 0) + across[0].astype(f32)
    for part in arrived:
        total = total + part.astype(f32)
    return total.astype(bf16)


def half_columns(values, first):
    half = values.shape[-1] // 2
    return jnp.where(first, values[..., :half], values[..., half:])


def summed_rows(pairs):
    grads = jnp.concatenate([dot_left_t(*pair).astype(bf16) for pair in pairs], axis=1)
    shard = lax.psum_scatter(grads, "page", scatter_dimension=0, tiled=True)
    return shard.astype(f32) + swap(shard).astype(f32)


def page_bounds(segments, is_text):
    pages = jnp.arange(PAGES, dtype=jnp.int32)
    low = jnp.sum(segments[None, :] < pages[:, None], axis=1, dtype=jnp.int32)
    high = jnp.sum(segments[None, :] <= pages[:, None], axis=1, dtype=jnp.int32)
    own_low = jnp.where(is_text, low, pages * PATCH)
    own_high = jnp.where(is_text, high, (pages + 1) * PATCH)

    def aligned(start):
        return jnp.minimum(start // 16 * 16, TEXT - WINDOW)

    return jnp.concatenate([aligned(own_low), own_low, own_high, aligned(low), low, high])


def sum_everywhere(values):
    count = lax.axis_size("page")
    if count & (count - 1):
        values = lax.psum(values, "page")
    else:
        step = 1
        while step < count:
            values = values + lax.ppermute(values, "page", [(i, i ^ step) for i in range(count)])
            step = step * 2
    return values + swap(values)


def swap(values):
    return lax.ppermute(values, "mod", [(0, 1), (1, 0)])


def local(
    states,
    cotangent,
    segments,
    box_x,
    box_y,
    conv_weight,
    conv_bias,
    w_query,
    b_query,
    w_key,
    w_value,
    b_value,
    w_out,
    b_out,
    table_pos,
    table_x,
    table_y,
    gain_one,
    bias_one,
    w_up,
    b_up,
    w_down,
    b_down,
    gain_two,
    bias_two,
):
    is_text = lax.axis_index("mod") == 0
    d_model = states.shape[3]
    own_low = states[0, 0]
    rows_each = w_query.shape[0]
    d_ff = w_up.shape[1]
    half = d_model // 2
    fast = lax.axis_size("page") == 16 and rows_each % 16 == 0 and w_down.shape[0] % 16 == 0
    place = jnp.stack([lax.axis_index("page"), lax.axis_index("mod")]).astype(jnp.int32)
    pack_qkv = jnp.concatenate([w_query, w_key, w_value], axis=1)
    pack_rest = jnp.concatenate([w_out, w_up], axis=1)
    other_low = swap(own_low)
    if fast:
        column_qkv = column_of(half_columns(pack_qkv, is_text))
        eight = jnp.concatenate([column_qkv, exchange(column_qkv, 2)])
        far = swap(eight)
        pieces = [eight, exchange(eight, 1), far, exchange(far, 1)]
        column_rest = column_of(after(pack_rest, column_qkv))
        column_down = column_of(after(w_down, column_rest))
        pieces[0] = after(pieces[0], column_rest)
        full_qkv = place_rows(place, pieces, pack_qkv.shape[1], place_halves_kernel)
    else:
        full_qkv = lax.all_gather(pack_qkv, "page", axis=0, tiled=True)
    full_query = full_qkv[:, :d_model]
    full_kv = full_qkv[:, d_model:]

    page_ids, pos_bins, bins_x, bins_y = token_ids(segments[0], box_x[0], box_y[0])
    bounds = page_bounds(segments[0], is_text)
    own_pages = jnp.where(is_text, page_ids[0], page_ids[1])
    features = bin_features(pos_bins.reshape(-1), bins_x.reshape(-1), bins_y.reshape(-1))
    flipped = bin_features(
        POS_BINS - 1 - pos_bins.reshape(-1),
        BOX_BINS - 1 - bins_x.reshape(-1),
        BOX_BINS - 1 - bins_y.reshape(-1),
    )
    own_feats = jnp.where(is_text, features[:TEXT], features[TEXT:])
    own_flip = jnp.where(is_text, flipped[:TEXT], flipped[TEXT:])
    tables = jnp.stack(
        [
            jnp.pad(table_pos, ((0, 0), (0, LANES - table_pos.shape[1]))),
            jnp.pad(table_x, ((0, 0), (0, LANES - table_x.shape[1]))),
            jnp.pad(table_y, ((0, 0), (0, LANES - table_y.shape[1]))),
        ],
        axis=1,
    )
    tables = jnp.pad(tables, ((0, 0), (0, 5), (0, 0)))

    def mix_fn(inputs_f, weight_f, bias_f):
        return dilated_mix(inputs_f, own_pages, weight_f, bias_f)

    own_states = own_low.astype(f32)
    mixed, mix_pull = jax.vjp(mix_fn, own_states, conv_weight, conv_bias)
    mixed_low = mixed.astype(bf16)
    other_pages = jnp.where(is_text, page_ids[1], page_ids[0])
    other_mixed = dilated_mix(other_low.astype(f32), other_pages, conv_weight, conv_bias)
    other_mixed = other_mixed.astype(bf16)
    mixed_all = jnp.concatenate(
        [jnp.where(is_text, mixed_low, other_mixed), jnp.where(is_text, other_mixed, mixed_low)],
        axis=0,
    )
    if fast:
        full_qkv = after(full_qkv, mixed_all, features, tables, bounds, own_flip)
        full_query = full_qkv[:, :d_model]
        full_kv = full_qkv[:, d_model:]
    queries = ((plain_dot(mixed_low, full_query) + b_query).astype(bf16) * 0.125).astype(bf16)
    kv_bias = jnp.concatenate([jnp.zeros_like(b_value), b_value])
    keys_values = (plain_dot(mixed_all, full_kv) + kv_bias).astype(bf16)
    context = attend(bounds, queries, keys_values, features, own_feats, tables)
    if fast:
        column_down = after(column_down, context)
        pieces_rest = list(pieces_of(column_rest))
        pieces_rest[0] = after(pieces_rest[0], column_down)
        full_rest = place_rows(place, pieces_rest, pack_rest.shape[1], place_kernel)
        pieces_down = pieces_of(column_down)
        full_down = place_rows(place, pieces_down, d_model, place_kernel)
    else:
        full_rest = lax.all_gather(pack_rest, "page", axis=0, tiled=True)
        full_down = lax.all_gather(w_down, "page", axis=0, tiled=True)
    full_out = full_rest[:, :d_model]
    full_up = full_rest[:, d_model:]

    first_sum = mixed + plain_dot(context, full_out) + b_out
    normed, norm_one_pull = jax.vjp(layer_norm, first_sum, gain_one, bias_one)
    normed_low = normed.astype(bf16)
    hidden = plain_dot(normed_low, full_up) + b_up
    active, gelu_pull = jax.vjp(exact_gelu, hidden)
    active_low = active.astype(bf16)
    ffn_out = plain_dot(active_low, full_down) + b_down
    output_row, norm_two_pull = jax.vjp(layer_norm, normed + ffn_out, gain_two, bias_two)
    grad_out = cotangent[0, 0].astype(f32)
    grad_sum_two, grad_gain_two, grad_bias_two = norm_two_pull(grad_out)
    grad_ffn = grad_sum_two.astype(bf16)
    grad_b_down = column_sum(grad_ffn)
    if fast:
        keep_down, send_down = grad_by_rows(active_low, grad_ffn, place)
        partner_down = exchange(send_down, 1)
        grad_hidden_in = after(grad_ffn, keep_down, send_down)
    else:
        shard_down = summed_rows([(active_low, grad_ffn)])
        grad_hidden_in = grad_ffn
    (grad_hidden_f,) = gelu_pull(dot_right_t(grad_hidden_in, full_down))
    grad_hidden = grad_hidden_f.astype(bf16)
    grad_b_up = column_sum(grad_hidden)
    grad_up_in = grad_hidden
    if fast:
        partner_down = after(partner_down, grad_hidden)
        across_out = across_send(keep_down, partner_down)
        across_down = exchange(across_out, 2)
        grad_up_in = after(grad_hidden, across_out)
    grad_normed = grad_sum_two + dot_right_t(grad_up_in, full_up)
    grad_first, grad_gain_one, grad_bias_one = norm_one_pull(grad_normed)
    grad_branch = grad_first.astype(bf16)
    grad_b_out = column_sum(grad_branch)
    pairs = [(context, grad_branch), (normed_low, grad_hidden)]
    grad_context_in = grad_branch
    if fast:
        keep_rest, send_rest = grad_by_columns(pairs, place, d_model)
        partner_rest = exchange(send_rest, 1)
        grad_context_in = after(grad_branch, keep_rest, send_rest)
    else:
        shard_rest = summed_rows(pairs)
    grad_context = dot_right_t(grad_context_in, full_out).astype(bf16)
    back = functools.partial(attend_back, bounds, queries, keys_values)
    rest = (features, own_feats, own_flip, tables)
    grad_q1, grad_k1, grad_v1, grad_t1 = back(grad_context, *rest, 0, PAIRS // 2)
    pairs = [(mixed_low, grad_q1), (mixed_all, grad_k1), (mixed_all, grad_v1)]
    grad_context_in = grad_context
    if fast:
        keep_one, send_one = grad_by_columns(pairs, place, half)
        partner_one = exchange(send_one, 1)
        partner_rest = after(partner_rest, grad_q1)
        both_rest = pair_sum(keep_rest, partner_rest, slice(0, 8))
        plane_out = half_columns(both_rest, ~is_text).astype(bf16)
        plane_rest = swap(plane_out)
        across_down = after(across_down, grad_q1)
        sends_down = column_sends(keep_down, partner_down, across_down)
        column_in_down = [exchange(x, 4 * i) for i, x in enumerate(sends_down, 1)]
        grad_context_in = after(grad_context, keep_one, send_one, plane_out, *sends_down)
    else:
        shard_one = summed_rows(pairs)
    grad_q2, grad_k2, grad_v2, grad_t2 = back(grad_context_in, *rest, PAIRS // 2, PAIRS // 2)
    pairs = [(mixed_low, grad_q2), (mixed_all, grad_k2), (mixed_all, grad_v2)]
    if fast:
        keep_two, send_two = grad_by_columns(pairs, place, half)
        partner_two = exchange(send_two, 1)
        partner_one = after(partner_one, send_two)
        across_one_out = across_send(keep_one, partner_one)
        across_one = exchange(across_one_out, 2)
        plane_rest = after(plane_rest, send_two)
        both_rest = half_columns(both_rest, is_text) + plane_rest.astype(f32)
        across_rest_out = both_rest[4:].astype(bf16)
        across_rest = exchange(across_rest_out, 2)
        grad_keys_in = [
            after(x, across_one_out, across_rest_out, send_two) for x in (grad_k1, grad_v1)
        ]
    else:
        shard_two = summed_rows(pairs)
        grad_keys_in = [grad_k1, grad_v1]
    grad_b_query = jnp.concatenate([column_sum(grad_q1), column_sum(grad_q2)], axis=1)
    grad_b_value = jnp.concatenate([column_sum(grad_v1), column_sum(grad_v2)], axis=1)
    from_keys = (
        dot_right_t(grad_keys_in[0], full_kv[:, :half])
        + dot_right_t(grad_k2, full_kv[:, half:d_model])
        + dot_right_t(grad_keys_in[1], full_kv[:, d_model : d_model + half])
        + dot_right_t(grad_v2, full_kv[:, d_model + half :])
    )
    to_other = jnp.where(is_text, from_keys[TEXT:], from_keys[:TEXT]).astype(bf16)
    from_other = swap(to_other)
    from_queries = dot_right_t(grad_q1, full_query[:, :half]) + dot_right_t(
        grad_q2, full_query[:, half:]
    )
    if fast:
        column_in_down = [after(x, to_other) for x in column_in_down]
        total_down = column_total(keep_down, partner_down, across_down, column_in_down)
        shard_down = total_down.astype(f32) + swap(total_down).astype(f32)
        partner_two = after(partner_two, to_other)
        across_two_out = across_send(keep_two, partner_two)
        across_two = exchange(across_two_out, 2)
        sends_one = column_sends(keep_one, partner_one, across_one)
        column_in_one = [exchange(x, 4 * i) for i, x in enumerate(sends_one, 1)]
        sum_rest = both_rest[:4] + across_rest.astype(f32)
        sends_rest = [sum_rest[step].astype(bf16) for step in (1, 2, 3)]
        column_in_rest = [exchange(x, 4 * i) for i, x in enumerate(sends_rest, 1)]
    grad_mixed = (
        grad_first
        + from_queries
        + jnp.where(is_text, from_keys[:TEXT], from_keys[TEXT:])
        + from_other.astype(f32)
    )
    grad_in, grad_conv_w, grad_conv_b = mix_pull(grad_mixed)

    table_rows = jnp.concatenate([grad_t1[:, :3], grad_t2[:, :3]]).reshape(6, 768)
    packed = jnp.concatenate(
        [
            grad_conv_w,
            grad_conv_b[None],
            grad_b_query,
            grad_b_value,
            grad_b_out,
            grad_gain_one[None],
            grad_bias_one[None],
            grad_b_down,
            grad_gain_two[None],
            grad_bias_two[None],
            grad_b_up.reshape(d_ff // d_model, d_model),
            table_rows,
            jnp.zeros((2, d_model), f32),
        ],
        axis=0,
    )
    packed = sum_everywhere(packed)
    g_tables = packed[16:22].reshape(HEADS, 3, LANES)
    if fast:
        sends_two = column_sends(keep_two, partner_two, across_two)
        column_in_two = [exchange(x, 4 * i) for i, x in enumerate(sends_two, 1)]
        total_one = column_total(keep_one, partner_one, across_one, column_in_one)
        shard_one = total_one.astype(f32) + swap(total_one).astype(f32)
        total_rest = sum_rest[0]
        for part in column_in_rest:
            total_rest = total_rest + part.astype(f32)
        low_rest = total_rest.astype(bf16)
        far_rest = swap(low_rest)
        shard_rest = jnp.where(
            is_text,
            jnp.concatenate([low_rest, far_rest], axis=1),
            jnp.concatenate([far_rest, low_rest], axis=1),
        ).astype(f32)
        total_two = column_total(keep_two, partner_two, across_two, column_in_two)
        shard_two = total_two.astype(f32) + swap(total_two).astype(f32)
    shard_q, shard_k, shard_v = [
        jnp.concatenate(
            [shard_one[:, i * half : (i + 1) * half], shard_two[:, i * half : (i + 1) * half]],
            axis=1,
        )
        for i in range(3)
    ]
    return (
        output_row.astype(bf16)[None, None],
        grad_in.astype(bf16)[None, None],
        packed[0:3],
        packed[3],
        shard_q,
        packed[4],
        shard_k,
        shard_v,
        packed[5],
        shard_rest[:, :d_model],
        packed[6],
        g_tables[:, 0, : table_pos.shape[1]],
        g_tables[:, 1, 64 : 64 + table_x.shape[1]],
        g_tables[:, 2, 64 : 64 + table_y.shape[1]],
        packed[7],
        packed[8],
        shard_rest[:, d_model:],
        packed[12:16].reshape(d_ff),
        shard_down,
        packed[9],
        packed[10],
        packed[11],
    )


def solution(mesh):
    rows = P("mod", "page", None, None)
    ids = P("page", None)
    cut = P("page", None)
    return jax.shard_map(
        local,
        mesh=mesh,
        in_specs=(
            rows, rows, ids, ids, ids, P(), P(), cut, P(), cut, cut, P(), cut,
            P(), P(), P(), P(), P(), P(), cut, P(), cut, P(), P(), P(),
        ),
        out_specs=(
            rows, rows, P(), P(), cut, P(), cut, cut, P(), cut, P(), P(), P(),
            P(), P(), P(), cut, P(), cut, P(), P(), P(),
        ),
        check_vma=False,
    )
```

```python
import functools

import jax
import jax.numpy as jnp
import numpy as np
from jax import lax
from jax.experimental import pallas as pl
from jax.experimental.pallas import tpu as pltpu
from jax.sharding import PartitionSpec as P

HEADS = 12
HEAD = 64
GRID = 8
PAGES = 8
POS_BINS = 64
BOX_BINS = 32
PATCH = 64
TEXT = 512
PAIRS = HEADS // 2
LANES = 2 * HEAD
WINDOW = 144
KEYS = WINDOW + PATCH

dilation = 2
small_cost = pl.CostEstimate(flops=1000, bytes_accessed=1000, transcendentals=0)
norm_eps = 1e-05
mask_fill = -1000000000.0
bf16 = jnp.bfloat16
f32 = jnp.float32


def shifted(values, offset, fill_value):
    padding = jnp.full((abs(offset),) + values.shape[1:], fill_value, values.dtype)
    if offset > 0:
        return jnp.concatenate([values[offset:], padding], axis=0)
    return jnp.concatenate([padding, values[:offset]], axis=0)


def dilated_mix(inputs, page_ids, conv_weight, conv_bias):
    summed = inputs + conv_bias + conv_weight[1] * inputs
    for tap_index, offset in ((0, -dilation), (2, dilation)):
        moved_rows = shifted(inputs, offset, 0.0)
        moved_pages = shifted(page_ids, offset, -1)
        same_page = (moved_pages == page_ids)[:, None]
        summed = summed + conv_weight[tap_index] * jnp.where(same_page, moved_rows, 0.0)
    return summed


def bin_features(pos_bins, bins_x, bins_y):
    return jnp.concatenate(
        [
            jax.nn.one_hot(pos_bins, POS_BINS, dtype=bf16),
            jax.nn.one_hot(bins_x, BOX_BINS, dtype=bf16),
            jax.nn.one_hot(bins_y, BOX_BINS, dtype=bf16),
        ],
        axis=1,
    )


def token_ids(text_pages, text_x, text_y):
    text_index = jnp.arange(TEXT, dtype=jnp.int32)
    text_pos = text_index * POS_BINS // TEXT
    patch_pos = text_index % PATCH * POS_BINS // PATCH
    patch_page = text_index // PATCH
    patch_x = text_index % GRID * BOX_BINS // GRID
    patch_y = text_index // GRID % GRID * BOX_BINS // GRID
    page_ids = jnp.stack([text_pages, patch_page])
    pos_bins = jnp.stack([text_pos, patch_pos])
    bins_x = jnp.stack([text_x, patch_x])
    bins_y = jnp.stack([text_y, patch_y])
    return (page_ids, pos_bins, bins_x, bins_y)


def layer_norm(values, gain_vec, bias_vec):
    centered = values - jnp.mean(values, axis=-1, keepdims=True)
    variance = jnp.mean(centered * centered, axis=-1, keepdims=True)
    return centered * lax.rsqrt(variance + norm_eps) * gain_vec + bias_vec


def exact_gelu(values):
    return jax.nn.gelu(values, approximate=False)


def plain_dot(left_side, right_side):
    return jnp.dot(left_side, right_side, preferred_element_type=f32)


def dot_left_t(left_side, right_side):
    return lax.dot_general(
        left_side, right_side, (((0,), (0,)), ((), ())), preferred_element_type=f32
    )


def dot_right_t(left_side, right_side):
    return lax.dot_general(
        left_side, right_side, (((1,), (1,)), ((), ())), preferred_element_type=f32
    )


def column_sum(values):
    return jnp.sum(values, axis=0, keepdims=True, dtype=f32)


def iota(shape, axis):
    return lax.broadcasted_iota(jnp.int32, shape, axis)


def bias_block(table_rows):
    pos_part = pltpu.roll(
        jnp.broadcast_to(table_rows[0:1], (POS_BINS, LANES)), 65, 1, stride=1, stride_axis=0
    )
    x_part = pltpu.roll(
        jnp.broadcast_to(table_rows[1:2], (BOX_BINS, LANES)), 33, 1, stride=1, stride_axis=0
    )
    y_part = pltpu.roll(
        jnp.broadcast_to(table_rows[2:3], (BOX_BINS, LANES)), 65, 1, stride=1, stride_axis=0
    )
    lane = iota((POS_BINS, LANES), 1)
    pos_part = jnp.where(lane < POS_BINS, pos_part, 0.0)
    lane = iota((BOX_BINS, LANES), 1)
    x_part = jnp.where((lane >= 64) & (lane < 96), x_part, 0.0)
    y_part = jnp.where(lane >= 96, y_part, 0.0)
    return jnp.concatenate([pos_part, x_part, y_part], axis=0).astype(bf16)


def diagonal_sums(grad_block):
    lane = iota((POS_BINS, LANES), 1)
    pos_part = jnp.where(lane < POS_BINS, grad_block[:64], 0.0)
    lane = iota((BOX_BINS, LANES), 1)
    x_part = jnp.where((lane >= 64) & (lane < 96), grad_block[64:96], 0.0)
    y_part = jnp.where(lane >= 96, grad_block[96:], 0.0)
    pos_part = pltpu.roll(pos_part, 0, 1, stride=1, stride_axis=0)
    x_part = pltpu.roll(x_part, 0, 1, stride=1, stride_axis=0)
    y_part = pltpu.roll(y_part, 96, 1, stride=1, stride_axis=0)
    rows = [jnp.sum(part, axis=0, keepdims=True) for part in (pos_part, x_part, y_part)]
    return jnp.concatenate(rows + [jnp.zeros((5, LANES), f32)], axis=0)


def stacked_heads(rows, low_lane):
    zero = jnp.zeros_like(rows)
    return jnp.concatenate(
        [jnp.where(low_lane, rows, zero), jnp.where(low_lane, zero, rows)], axis=0
    )


def page_operands(page, bounds, q_ref, k_ref, feat_ref, lookup):
    own_at = pl.multiple_of(bounds[page], 16)
    key_at = pl.multiple_of(bounds[3 * PAGES + page], 16)
    low_lane = iota((WINDOW, LANES), 1) < HEAD
    queries = stacked_heads(q_ref[pl.ds(own_at, WINDOW), :], low_lane)
    rel = jnp.concatenate(
        [lookup[pl.ds(own_at, WINDOW), :LANES], lookup[pl.ds(own_at, WINDOW), LANES:]], axis=0
    )
    query_side = jnp.concatenate([rel, queries], axis=1)
    patch_rows = pl.ds(TEXT + PATCH * page, PATCH)
    text_rows = pl.ds(key_at, WINDOW)
    key_side = jnp.concatenate(
        [
            jnp.concatenate([feat_ref[text_rows, :], k_ref[text_rows, :]], axis=1),
            jnp.concatenate([feat_ref[patch_rows, :], k_ref[patch_rows, :]], axis=1),
        ],
        axis=0,
    )
    own_row = iota((WINDOW, LANES), 0) + own_at
    own_ok = (own_row >= bounds[PAGES + page]) & (own_row < bounds[2 * PAGES + page])
    return own_at, key_at, low_lane, own_ok, queries, query_side, key_side, text_rows, patch_rows


def attend_kernel(bounds, q_ref, k_ref, v_ref, feat_ref, own_feat_ref, table_ref, context_ref, lookup):
    blocks = jnp.concatenate([bias_block(table_ref[0]), bias_block(table_ref[1])], axis=1)
    lookup[...] = jnp.dot(own_feat_ref[...], blocks, preferred_element_type=f32).astype(bf16)
    for page in range(PAGES):
        own_at, key_at, low_lane, own_ok, queries, query_side, key_side, text_rows, patch_rows = (
            page_operands(page, bounds, q_ref, k_ref, feat_ref, lookup)
        )
        scores = dot_right_t(query_side, key_side)
        column = iota((1, KEYS), 1)
        key_row = column + key_at
        key_ok = (column >= WINDOW) | (
            (key_row >= bounds[4 * PAGES + page]) & (key_row < bounds[5 * PAGES + page])
        )
        scores = jnp.where(key_ok, scores, mask_fill)
        row_max = jnp.max(scores, axis=1, keepdims=True)
        weights = jnp.exp(scores - row_max)
        total = jnp.sum(weights, axis=1, keepdims=True)
        prob = (weights * (1.0 / total)).astype(bf16)
        values = jnp.concatenate([v_ref[text_rows, :], v_ref[patch_rows, :]], axis=0)
        mixed = jnp.dot(prob, values, preferred_element_type=f32)
        picked = jnp.where(low_lane, mixed[:WINDOW], mixed[WINDOW:])
        before = context_ref[pl.ds(own_at, WINDOW), :].astype(f32)
        context_ref[pl.ds(own_at, WINDOW), :] = jnp.where(own_ok, picked, before).astype(bf16)


def attend_back_kernel(
    bounds,
    q_ref,
    k_ref,
    v_ref,
    grad_ref,
    feat_ref,
    own_feat_ref,
    flip_feat_ref,
    table_ref,
    grad_q_ref,
    grad_k_ref,
    grad_v_ref,
    grad_table_ref,
    lookup,
    grad_lookup,
):
    blocks = jnp.concatenate([bias_block(table_ref[0]), bias_block(table_ref[1])], axis=1)
    lookup[...] = jnp.dot(own_feat_ref[...], blocks, preferred_element_type=f32).astype(bf16)
    for page in range(PAGES):
        own_at, key_at, low_lane, own_ok, queries, query_side, key_side, text_rows, patch_rows = (
            page_operands(page, bounds, q_ref, k_ref, feat_ref, lookup)
        )
        scores = dot_right_t(key_side, query_side)
        row = iota((KEYS, 1), 0)
        key_row = row + key_at
        key_in = (key_row >= bounds[4 * PAGES + page]) & (key_row < bounds[5 * PAGES + page])
        scores = jnp.where((row >= WINDOW) | key_in, scores, mask_fill)
        col_max = jnp.max(scores, axis=0, keepdims=True)
        weights = jnp.exp(scores - col_max)
        total = jnp.sum(weights, axis=0, keepdims=True)
        prob = weights * (1.0 / total)
        grad_rows = grad_ref[pl.ds(own_at, WINDOW), :]
        grad_rows = jnp.where(own_ok, grad_rows, jnp.zeros_like(grad_rows))
        grads = stacked_heads(grad_rows, low_lane)
        values = jnp.concatenate([v_ref[text_rows, :], v_ref[patch_rows, :]], axis=0)
        grad_prob = dot_right_t(values, grads)
        inner = jnp.sum(prob * grad_prob, axis=0, keepdims=True)
        grad_scores = (prob * (grad_prob - inner)).astype(bf16)
        grad_v = jnp.dot(prob.astype(bf16), grads, preferred_element_type=f32)
        grad_k = jnp.dot(grad_scores, queries, preferred_element_type=f32)
        back = dot_left_t(grad_scores, key_side)
        grad_q = jnp.where(low_lane, back[:WINDOW, LANES:], back[WINDOW:, LANES:]) * 0.125
        own_rows = pl.ds(own_at, WINDOW)
        before = grad_q_ref[own_rows, :].astype(f32)
        grad_q_ref[own_rows, :] = jnp.where(own_ok, grad_q, before).astype(bf16)
        grad_lookup[own_rows, :LANES] = jnp.where(
            own_ok, back[:WINDOW, :LANES], grad_lookup[own_rows, :LANES]
        )
        grad_lookup[own_rows, LANES:] = jnp.where(
            own_ok, back[WINDOW:, :LANES], grad_lookup[own_rows, LANES:]
        )
        wide_row = iota((WINDOW, LANES), 0) + key_at
        text_ok = (wide_row >= bounds[4 * PAGES + page]) & (wide_row < bounds[5 * PAGES + page])
        for grad, ref in ((grad_k, grad_k_ref), (grad_v, grad_v_ref)):
            before = ref[text_rows, :].astype(f32)
            ref[text_rows, :] = jnp.where(text_ok, grad[:WINDOW], before).astype(bf16)
            ref[patch_rows, :] = grad[WINDOW:].astype(bf16)
    grad_high = grad_lookup[...].astype(bf16)
    grad_rest = (grad_lookup[...] - grad_high.astype(f32)).astype(bf16)
    flip = flip_feat_ref[...]
    grad_block = dot_left_t(flip, grad_high) + dot_left_t(flip, grad_rest)
    grad_table_ref[0] = diagonal_sums(grad_block[:, :LANES])
    grad_table_ref[1] = diagonal_sums(grad_block[:, LANES:])


def column_spec(rows, first=0):
    return pl.BlockSpec((rows, LANES), lambda pair, bounds: (0, pair + first))


def tables_spec(first=0):
    return pl.BlockSpec((2, 8, LANES), lambda pair, bounds: (pair + first, 0, 0))


def whole_spec(rows):
    return pl.BlockSpec((rows, LANES), lambda pair, bounds: (0, 0))


def attend(bounds, queries, keys_values, features, own_features, tables):
    return pl.pallas_call(
        attend_kernel,
        grid_spec=pltpu.PrefetchScalarGridSpec(
            num_scalar_prefetch=1,
            grid=(PAIRS,),
            in_specs=[
                column_spec(TEXT),
                column_spec(2 * TEXT),
                column_spec(2 * TEXT, PAIRS),
                whole_spec(2 * TEXT),
                whole_spec(TEXT),
                tables_spec(),
            ],
            out_specs=column_spec(TEXT),
            scratch_shapes=[pltpu.VMEM((TEXT, 2 * LANES), bf16)],
        ),
        out_shape=jax.ShapeDtypeStruct((TEXT, HEADS * HEAD), bf16),
        cost_estimate=small_cost,
        name="attend",
    )(bounds, queries, keys_values, keys_values, features, own_features, tables)


def attend_back(
    bounds, queries, keys_values, grad_context, features, own_features, flip, tables, first, count
):
    return pl.pallas_call(
        attend_back_kernel,
        grid_spec=pltpu.PrefetchScalarGridSpec(
            num_scalar_prefetch=1,
            grid=(count,),
            in_specs=[
                column_spec(TEXT, first),
                column_spec(2 * TEXT, first),
                column_spec(2 * TEXT, PAIRS + first),
                column_spec(TEXT, first),
                whole_spec(2 * TEXT),
                whole_spec(TEXT),
                whole_spec(TEXT),
                tables_spec(first),
            ],
            out_specs=[
                column_spec(TEXT),
                column_spec(2 * TEXT),
                column_spec(2 * TEXT),
                tables_spec(),
            ],
            scratch_shapes=[
                pltpu.VMEM((TEXT, 2 * LANES), bf16),
                pltpu.VMEM((TEXT, 2 * LANES), f32),
            ],
        ),
        out_shape=[
            jax.ShapeDtypeStruct((TEXT, count * LANES), bf16),
            jax.ShapeDtypeStruct((2 * TEXT, count * LANES), bf16),
            jax.ShapeDtypeStruct((2 * TEXT, count * LANES), bf16),
            jax.ShapeDtypeStruct((2 * count, 8, LANES), f32),
        ],
        cost_estimate=small_cost,
        name="attend_back",
    )(
        bounds,
        queries,
        keys_values,
        keys_values,
        grad_context,
        features,
        own_features,
        flip,
        tables,
    )


def exchange(values, mask):
    count = lax.axis_size("page")
    return lax.ppermute(values, "page", [(i, i ^ mask) for i in range(count)])


def after(value, *earlier):
    return lax.optimization_barrier((value, *earlier))[0]


def slot_mask(slot):
    return (slot & 3) * 4 + (slot >> 2) * 2


def place_kernel(place, *refs):
    pieces, full_ref, sems = refs[:4], refs[4], refs[5]
    rows = pieces[0].shape[1]
    copies = []
    for index in range(16):
        mask = (index >> 2) * 4 + (index & 3)
        at = pl.multiple_of((place[0] ^ mask) * rows, 16)
        copies.append(
            pltpu.make_async_copy(
                pieces[index & 3].at[index >> 2], full_ref.at[pl.ds(at, rows)], sems.at[index]
            )
        )
    for copy in copies:
        copy.start()
    for copy in copies:
        copy.wait()


def place_halves_kernel(place, *refs):
    pieces, full_ref, sems = refs[:4], refs[4], refs[5]
    rows, half = pieces[0].shape[1], pieces[0].shape[2]
    copies = []
    for index in range(32):
        kind = index >> 3
        mask = slot_mask(index & 7) + (kind & 1)
        at = pl.multiple_of((place[0] ^ mask) * rows, 16)
        column = pl.multiple_of((place[1] ^ (kind >> 1)) * half, 128)
        copies.append(
            pltpu.make_async_copy(
                pieces[kind].at[index & 7],
                full_ref.at[pl.ds(at, rows), pl.ds(column, half)],
                sems.at[index],
            )
        )
    for copy in copies:
        copy.start()
    for copy in copies:
        copy.wait()


def place_rows(place, pieces, width, kernel):
    rows = pieces[0].shape[1]
    return pl.pallas_call(
        kernel,
        grid_spec=pltpu.PrefetchScalarGridSpec(
            num_scalar_prefetch=1,
            grid=(),
            in_specs=[pl.BlockSpec(memory_space=pl.ANY)] * 4,
            out_specs=pl.BlockSpec(memory_space=pltpu.VMEM),
            scratch_shapes=[pltpu.SemaphoreType.DMA((32,))],
        ),
        out_shape=jax.ShapeDtypeStruct((16 * rows, width), bf16),
        cost_estimate=small_cost,
        name="place_rows",
    )(place, *pieces)


def column_parts(shard):
    return [shard] + [exchange(shard, 4 * step) for step in (1, 2, 3)]


def column_of(shard):
    return jnp.stack(column_parts(shard))


def grad_rows_kernel(page, x_ref, h_ref, keep_ref, send_ref, product):
    rows = keep_ref.shape[1]
    product[...] = dot_left_t(x_ref[...], h_ref[...])
    mine = pl.multiple_of((page[0] & 1) * rows, 16)
    theirs = pl.multiple_of((1 - (page[0] & 1)) * rows, 16)
    keep_ref[0] = product[pl.ds(mine, rows), :].astype(bf16)
    send_ref[0] = product[pl.ds(theirs, rows), :].astype(bf16)


def grad_by_rows(inputs, grads, page):
    tokens, width = inputs.shape
    columns = grads.shape[1]
    rows = width // 16

    def slot(block, page):
        mask = block ^ (page[0] >> 1)
        return ((mask & 1) * 4 + (mask >> 1), 0, 0)

    half = jax.ShapeDtypeStruct((8, rows, columns), bf16)
    return pl.pallas_call(
        grad_rows_kernel,
        grid_spec=pltpu.PrefetchScalarGridSpec(
            num_scalar_prefetch=1,
            grid=(8,),
            in_specs=[
                pl.BlockSpec((tokens, 2 * rows), lambda block, page: (0, block)),
                pl.BlockSpec((tokens, columns), lambda block, page: (0, 0)),
            ],
            out_specs=[pl.BlockSpec((1, rows, columns), slot)] * 2,
            scratch_shapes=[pltpu.VMEM((2 * rows, columns), f32)],
        ),
        out_shape=[half, half],
        cost_estimate=small_cost,
        name="grad_rows",
    )(page, inputs, grads)


def grad_columns_kernel(parts, page, *refs):
    ins, keep_ref, send_ref, product = refs[: 2 * len(parts)], refs[-3], refs[-2], refs[-1]
    rows, width = keep_ref.shape[1], keep_ref.shape[2]
    step = pl.program_id(0)
    first = 0
    for index, count in enumerate(parts):
        x_ref, h_ref = ins[2 * index], ins[2 * index + 1]

        @pl.when((step >= first) & (step < first + count))
        def _():
            product[...] = dot_left_t(x_ref[...], h_ref[...])

        first = first + count
    for slot in range(8):
        mask = slot_mask(slot)
        mine = pl.multiple_of((page[0] ^ mask) * rows, 16)
        theirs = pl.multiple_of((page[0] ^ (mask + 1)) * rows, 16)
        keep_ref[slot] = product[pl.ds(mine, rows), :].astype(bf16)
        send_ref[slot] = product[pl.ds(theirs, rows), :].astype(bf16)


def grad_by_columns(pairs, page, tile):
    width = pairs[0][0].shape[1]
    rows = width // 16
    parts = tuple(grads.shape[1] // tile for _, grads in pairs)
    steps = sum(parts)
    specs = []
    operands = []
    first = 0
    flops = 0
    for (inputs, grads), count in zip(pairs, parts):
        specs.append(pl.BlockSpec(inputs.shape, lambda step, page: (0, 0)))

        def column(step, page, first=first, count=count):
            return (0, jnp.clip(step - first, 0, count - 1))

        specs.append(pl.BlockSpec((grads.shape[0], tile), column))
        operands += [inputs, grads]
        first = first + count
        flops = flops + 2 * inputs.shape[0] * width * grads.shape[1]
    half = jax.ShapeDtypeStruct((8, rows, steps * tile), bf16)
    return pl.pallas_call(
        functools.partial(grad_columns_kernel, parts),
        grid_spec=pltpu.PrefetchScalarGridSpec(
            num_scalar_prefetch=1,
            grid=(steps,),
            in_specs=specs,
            out_specs=[pl.BlockSpec((8, rows, tile), lambda step, page: (0, 0, step))] * 2,
            scratch_shapes=[pltpu.VMEM((width, tile), f32)],
        ),
        out_shape=[half, half],
        cost_estimate=small_cost,
        name="grad_columns",
    )(page, *operands)


def first_half_kernel(place, keep_near, part_near, keep_far, part_far, held_ref, out_ref):
    held_ref[...] = keep_near[...].astype(f32) + part_near[...].astype(f32)
    out_ref[...] = (keep_far[...].astype(f32) + part_far[...].astype(f32)).astype(bf16)


def halve_call(place, keep, partner, specs, half_shape, steps):
    near, far, out = specs
    return pl.pallas_call(
        first_half_kernel,
        grid_spec=pltpu.PrefetchScalarGridSpec(
            num_scalar_prefetch=1,
            grid=(steps,),
            in_specs=[near, near, far, far],
            out_specs=[out, out],
        ),
        out_shape=[
            jax.ShapeDtypeStruct(half_shape, f32),
            jax.ShapeDtypeStruct(half_shape, bf16),
        ],
        cost_estimate=small_cost,
        name="halve",
    )(place, keep, partner, keep, partner)


def halve_across(place, keep, partner):
    _, rows, width = keep.shape
    near = pl.BlockSpec((1, rows, width), lambda step, place: (step, 0, 0))
    far = pl.BlockSpec((1, rows, width), lambda step, place: (step + 4, 0, 0))
    return halve_call(place, keep, partner, (near, far, near), (4, rows, width), 4)


def halve_plane(place, keep, partner):
    _, rows, width = keep.shape
    block = (2, rows, width // 2)
    near = pl.BlockSpec(block, lambda step, place: (step, 0, place[1]))
    far = pl.BlockSpec(block, lambda step, place: (step, 0, 1 - place[1]))
    out = pl.BlockSpec(block, lambda step, place: (step, 0, 0))
    return halve_call(place, keep, partner, (near, far, out), (8, rows, width // 2), 4)


def column_kernel(held_ref, across_ref, own_ref, *sends):
    own_ref[...] = held_ref[0] + across_ref[0].astype(f32)
    for step, send in enumerate(sends, 1):
        send[...] = (held_ref[step] + across_ref[step].astype(f32)).astype(bf16)


def column_sends(held, across):
    _, rows, width = held.shape
    tile = 384
    out = pl.BlockSpec((rows, tile), lambda step: (0, step))
    block = pl.BlockSpec((4, rows, tile), lambda step: (0, 0, step))
    own, *sends = pl.pallas_call(
        column_kernel,
        grid=(width // tile,),
        in_specs=[block, block],
        out_specs=[out] * 4,
        out_shape=[jax.ShapeDtypeStruct((rows, width), f32)]
        + [jax.ShapeDtypeStruct((rows, width), bf16)] * 3,
        cost_estimate=small_cost,
        name="column_sends",
    )(held, across)
    return own, sends


def column_arrivals(sends):
    return [exchange(send, 4 * step) for step, send in enumerate(sends, 1)]


def column_total(own, arrived):
    total = own
    for part in arrived:
        total = total + part.astype(f32)
    return total.astype(bf16)


def half_columns(values, first):
    half = values.shape[-1] // 2
    return jnp.where(first, values[..., :half], values[..., half:])


def summed_rows(pairs):
    grads = jnp.concatenate([dot_left_t(*pair).astype(bf16) for pair in pairs], axis=1)
    shard = lax.psum_scatter(grads, "page", scatter_dimension=0, tiled=True)
    return shard.astype(f32) + swap(shard).astype(f32)


def page_bounds(segments, is_text):
    pages = jnp.arange(PAGES, dtype=jnp.int32)
    low = jnp.sum(segments[None, :] < pages[:, None], axis=1, dtype=jnp.int32)
    high = jnp.sum(segments[None, :] <= pages[:, None], axis=1, dtype=jnp.int32)
    own_low = jnp.where(is_text, low, pages * PATCH)
    own_high = jnp.where(is_text, high, (pages + 1) * PATCH)

    def aligned(start):
        return jnp.minimum(start // 16 * 16, TEXT - WINDOW)

    return jnp.concatenate([aligned(own_low), own_low, own_high, aligned(low), low, high])


def sum_everywhere(values):
    count = lax.axis_size("page")
    if count & (count - 1):
        values = lax.psum(values, "page")
    else:
        step = 1
        while step < count:
            values = values + lax.ppermute(values, "page", [(i, i ^ step) for i in range(count)])
            step = step * 2
    return values + swap(values)


def swap(values):
    return lax.ppermute(values, "mod", [(0, 1), (1, 0)])


def local(
    states,
    cotangent,
    segments,
    box_x,
    box_y,
    conv_weight,
    conv_bias,
    w_query,
    b_query,
    w_key,
    w_value,
    b_value,
    w_out,
    b_out,
    table_pos,
    table_x,
    table_y,
    gain_one,
    bias_one,
    w_up,
    b_up,
    w_down,
    b_down,
    gain_two,
    bias_two,
):
    is_text = lax.axis_index("mod") == 0
    d_model = states.shape[3]
    own_low = states[0, 0]
    rows_each = w_query.shape[0]
    d_ff = w_up.shape[1]
    fast = lax.axis_size("page") == 16 and rows_each % 16 == 0 and w_down.shape[0] % 16 == 0
    place = jnp.stack([lax.axis_index("page"), lax.axis_index("mod")]).astype(jnp.int32)
    pack_qkv = jnp.concatenate([w_query, w_key, w_value], axis=1)
    pack_rest = jnp.concatenate([w_out, w_up], axis=1)
    other_low = swap(own_low)
    if fast:
        column_qkv = column_of(half_columns(pack_qkv, is_text))
        parts_rest = column_parts(after(pack_rest, column_qkv))
        eight = jnp.concatenate([column_qkv, exchange(column_qkv, 2)])
        far = swap(eight)
        pieces = [eight, exchange(eight, 1), far, exchange(far, 1)]
        column_rest = jnp.stack([after(part, eight, far) for part in parts_rest])
        parts_down = column_parts(after(w_down, column_rest))
        pieces[0] = after(pieces[0], column_rest)
        full_qkv = place_rows(place, pieces, pack_qkv.shape[1], place_halves_kernel)
    else:
        full_qkv = lax.all_gather(pack_qkv, "page", axis=0, tiled=True)

    page_ids, pos_bins, bins_x, bins_y = token_ids(segments[0], box_x[0], box_y[0])
    bounds = page_bounds(segments[0], is_text)
    own_pages = jnp.where(is_text, page_ids[0], page_ids[1])
    features = bin_features(pos_bins.reshape(-1), bins_x.reshape(-1), bins_y.reshape(-1))
    flipped = bin_features(
        POS_BINS - 1 - pos_bins.reshape(-1),
        BOX_BINS - 1 - bins_x.reshape(-1),
        BOX_BINS - 1 - bins_y.reshape(-1),
    )
    own_feats = jnp.where(is_text, features[:TEXT], features[TEXT:])
    own_flip = jnp.where(is_text, flipped[:TEXT], flipped[TEXT:])
    tables = jnp.stack(
        [
            jnp.pad(table_pos, ((0, 0), (0, LANES - table_pos.shape[1]))),
            jnp.pad(table_x, ((0, 0), (0, LANES - table_x.shape[1]))),
            jnp.pad(table_y, ((0, 0), (0, LANES - table_y.shape[1]))),
        ],
        axis=1,
    )
    tables = jnp.pad(tables, ((0, 0), (0, 5), (0, 0)))

    def mix_fn(inputs_f, weight_f, bias_f):
        return dilated_mix(inputs_f, own_pages, weight_f, bias_f)

    own_states = own_low.astype(f32)
    mixed, mix_pull = jax.vjp(mix_fn, own_states, conv_weight, conv_bias)
    mixed_low = mixed.astype(bf16)
    other_pages = jnp.where(is_text, page_ids[1], page_ids[0])
    other_mixed = dilated_mix(other_low.astype(f32), other_pages, conv_weight, conv_bias)
    other_mixed = other_mixed.astype(bf16)
    mixed_all = jnp.concatenate(
        [jnp.where(is_text, mixed_low, other_mixed), jnp.where(is_text, other_mixed, mixed_low)],
        axis=0,
    )
    if fast:
        full_qkv = after(full_qkv, mixed_all, features, tables, bounds, own_flip)
    full_query = full_qkv[:, :d_model]
    full_kv = full_qkv[:, d_model:]
    queries = ((plain_dot(mixed_low, full_query) + b_query).astype(bf16) * 0.125).astype(bf16)
    kv_bias = jnp.concatenate([jnp.zeros_like(b_value), b_value])
    keys_values = (plain_dot(mixed_all, full_kv) + kv_bias).astype(bf16)
    context = attend(bounds, queries, keys_values, features, own_feats, tables)
    if fast:
        across_rest = exchange(column_rest, 2)
        column_down = jnp.stack([after(part, context) for part in parts_down])
        across_rest = after(across_rest, column_down)
        pieces_rest = [column_rest, exchange(column_rest, 1), across_rest, exchange(across_rest, 1)]
        full_rest = place_rows(place, pieces_rest, pack_rest.shape[1], place_kernel)
    else:
        full_rest = lax.all_gather(pack_rest, "page", axis=0, tiled=True)
    full_out = full_rest[:, :d_model]
    full_up = full_rest[:, d_model:]

    first_sum = mixed + plain_dot(context, full_out) + b_out
    normed, norm_one_pull = jax.vjp(layer_norm, first_sum, gain_one, bias_one)
    normed_low = normed.astype(bf16)
    hidden = plain_dot(normed_low, full_up) + b_up
    active, gelu_pull = jax.vjp(exact_gelu, hidden)
    active_low = active.astype(bf16)
    if fast:
        across_down = after(exchange(column_down, 2), normed_low)
        pieces_down = [column_down, exchange(column_down, 1), across_down, exchange(across_down, 1)]
        pieces_down[0] = after(pieces_down[0], active_low)
        full_down = place_rows(place, pieces_down, d_model, place_kernel)
    else:
        full_down = lax.all_gather(w_down, "page", axis=0, tiled=True)
    ffn_out = plain_dot(active_low, full_down) + b_down
    output_row, norm_two_pull = jax.vjp(layer_norm, normed + ffn_out, gain_two, bias_two)
    grad_out = cotangent[0, 0].astype(f32)
    grad_sum_two, grad_gain_two, grad_bias_two = norm_two_pull(grad_out)
    grad_ffn = grad_sum_two.astype(bf16)
    grad_b_down = column_sum(grad_ffn)
    grad_hidden_in = grad_ffn
    if fast:
        keep_down, send_down = grad_by_rows(active_low, grad_ffn, place)
        partner_down = exchange(send_down, 1)
        grad_hidden_in = after(grad_ffn, keep_down, send_down)
    else:
        shard_down = summed_rows([(active_low, grad_ffn)])
    (grad_hidden_f,) = gelu_pull(dot_right_t(grad_hidden_in, full_down))
    grad_hidden = grad_hidden_f.astype(bf16)
    grad_b_up = column_sum(grad_hidden)
    grad_up_in = grad_hidden
    if fast:
        partner_down = after(partner_down, grad_hidden)
        held_down, across_out_down = halve_across(place, keep_down, partner_down)
        across_down = exchange(across_out_down, 2)
        grad_up_in = after(grad_hidden, across_out_down)
    grad_normed = grad_sum_two + dot_right_t(grad_up_in, full_up)
    grad_first, grad_gain_one, grad_bias_one = norm_one_pull(grad_normed)
    grad_branch = grad_first.astype(bf16)
    grad_b_out = column_sum(grad_branch)
    pairs = [(context, grad_branch), (normed_low, grad_hidden)]
    grad_context_in = grad_branch
    if fast:
        keep_rest, send_rest = grad_by_columns(pairs, place, d_model)
        partner_rest = exchange(send_rest, 1)
        across_down = after(across_down, send_rest)
        grad_context_in = after(grad_branch, keep_rest, across_down)
    else:
        shard_rest = summed_rows(pairs)
    grad_context = dot_right_t(grad_context_in, full_out).astype(bf16)
    attend_in = grad_context
    if fast:
        partner_rest = after(partner_rest, grad_context)
        held_rest, plane_out = halve_plane(place, keep_rest, partner_rest)
        plane_rest = swap(plane_out)
        own_down, sends_down = column_sends(held_down, across_down)
        arrived_down = column_arrivals(sends_down)
        attend_in = after(grad_context, plane_out, *sends_down)
    grad_queries, grad_keys, grad_values, grad_tables = attend_back(
        bounds, queries, keys_values, attend_in, features, own_feats, own_flip, tables, 0, PAIRS
    )
    grad_keys_in, grad_queries_in = grad_keys, grad_queries
    if fast:
        plane_rest = after(plane_rest, grad_queries)
        held_rest, across_out_rest = halve_across(place, held_rest, plane_rest)
        across_rest = exchange(across_out_rest, 2)
        arrived_down = [after(part, grad_queries) for part in arrived_down]
        total_down = column_total(own_down, arrived_down)
        far_down = swap(total_down)
        grad_queries_in = after(grad_queries, across_out_rest, total_down)
    pairs = [(mixed_low, grad_queries_in), (mixed_all, grad_keys), (mixed_all, grad_values)]
    if fast:
        keep_qkv, send_qkv = grad_by_columns(pairs, place, d_model)
        partner_qkv = exchange(send_qkv, 1)
        across_rest = after(across_rest, send_qkv)
        own_rest, sends_rest = column_sends(held_rest, across_rest)
        arrived_rest = column_arrivals(sends_rest)
        far_down = after(far_down, send_qkv)
        partner_qkv = after(partner_qkv, far_down, *sends_rest)
        held_qkv, across_out_qkv = halve_across(place, keep_qkv, partner_qkv)
        across_qkv = exchange(across_out_qkv, 2)
        grad_keys_in = after(grad_keys, across_out_qkv)
    else:
        shard_qkv = summed_rows(pairs)
    grad_b_query = column_sum(grad_queries)
    grad_b_value = column_sum(grad_values)
    from_keys = dot_right_t(grad_keys_in, full_kv[:, :d_model]) + dot_right_t(
        grad_values, full_kv[:, d_model:]
    )
    to_other = jnp.where(is_text, from_keys[TEXT:], from_keys[:TEXT]).astype(bf16)
    from_other = swap(to_other)
    if fast:
        grad_queries = after(grad_queries, to_other)
    from_queries = dot_right_t(grad_queries, full_query)
    if fast:
        across_qkv = after(across_qkv, from_queries)
        own_qkv, sends_qkv = column_sends(held_qkv, across_qkv)
        arrived_qkv = column_arrivals(sends_qkv)
        from_other = after(from_other, *sends_qkv)
    grad_mixed = (
        grad_first
        + from_queries
        + jnp.where(is_text, from_keys[:TEXT], from_keys[TEXT:])
        + from_other.astype(f32)
    )
    grad_in, grad_conv_w, grad_conv_b = mix_pull(grad_mixed)

    table_rows = grad_tables[:, :3].reshape(6, 768)
    packed = jnp.concatenate(
        [
            grad_conv_w,
            grad_conv_b[None],
            grad_b_query,
            grad_b_value,
            grad_b_out,
            grad_gain_one[None],
            grad_bias_one[None],
            grad_b_down,
            grad_gain_two[None],
            grad_bias_two[None],
            grad_b_up.reshape(d_ff // d_model, d_model),
            table_rows,
            jnp.zeros((2, d_model), f32),
        ],
        axis=0,
    )
    if fast:
        arrived_rest = [after(part, packed) for part in arrived_rest]
        total_rest = column_total(own_rest, arrived_rest)
        far_rest = swap(total_rest)
        arrived_qkv = [after(part, total_rest) for part in arrived_qkv]
        total_qkv = column_total(own_qkv, arrived_qkv)
        far_qkv = swap(total_qkv)
    packed = sum_everywhere(packed)
    g_tables = packed[16:22].reshape(HEADS, 3, LANES)
    if fast:
        shard_down = total_down.astype(f32) + far_down.astype(f32)
        shard_qkv = total_qkv.astype(f32) + far_qkv.astype(f32)
        shard_rest = jnp.where(
            is_text,
            jnp.concatenate([total_rest, far_rest], axis=1),
            jnp.concatenate([far_rest, total_rest], axis=1),
        ).astype(f32)
    return (
        output_row.astype(bf16)[None, None],
        grad_in.astype(bf16)[None, None],
        packed[0:3],
        packed[3],
        shard_qkv[:, :d_model],
        packed[4],
        shard_qkv[:, d_model : 2 * d_model],
        shard_qkv[:, 2 * d_model :],
        packed[5],
        shard_rest[:, :d_model],
        packed[6],
        g_tables[:, 0, : table_pos.shape[1]],
        g_tables[:, 1, 64 : 64 + table_x.shape[1]],
        g_tables[:, 2, 64 : 64 + table_y.shape[1]],
        packed[7],
        packed[8],
        shard_rest[:, d_model:],
        packed[12:16].reshape(d_ff),
        shard_down,
        packed[9],
        packed[10],
        packed[11],
    )


def solution(mesh):
    rows = P("mod", "page", None, None)
    ids = P("page", None)
    cut = P("page", None)
    return jax.shard_map(
        local,
        mesh=mesh,
        in_specs=(
            rows, rows, ids, ids, ids, P(), P(), cut, P(), cut, cut, P(), cut,
            P(), P(), P(), P(), P(), P(), cut, P(), cut, P(), P(), P(),
        ),
        out_specs=(
            rows, rows, P(), P(), cut, P(), cut, cut, P(), cut, P(), P(), P(),
            P(), P(), P(), cut, P(), cut, P(), P(), P(),
        ),
        check_vma=False,
    )
```

```python
import functools

import jax
import jax.numpy as jnp
import numpy as np
from jax import lax
from jax.experimental import pallas as pl
from jax.experimental.pallas import tpu as pltpu
from jax.sharding import PartitionSpec as P

HEADS = 12
HEAD = 64
GRID = 8
PAGES = 8
POS_BINS = 64
BOX_BINS = 32
PATCH = 64
TEXT = 512
PAIRS = HEADS // 2
LANES = 2 * HEAD
WINDOW = 144
KEYS = WINDOW + PATCH

dilation = 2
small_cost = pl.CostEstimate(flops=1000, bytes_accessed=1000, transcendentals=0)
norm_eps = 1e-05
mask_fill = -1000000000.0
erfc_poly = (
    0.2367515965428487,
    0.24062179898991767,
    0.18865103029313968,
    0.2877518531132804,
    -0.1648672439458568,
    0.4765735350541787,
    -0.34041833366480423,
    0.07493571514857543,
)
bf16 = jnp.bfloat16
f32 = jnp.float32


def shifted(values, offset, fill_value):
    padding = jnp.full((abs(offset),) + values.shape[1:], fill_value, values.dtype)
    if offset > 0:
        return jnp.concatenate([values[offset:], padding], axis=0)
    return jnp.concatenate([padding, values[:offset]], axis=0)


def dilated_mix(inputs, page_ids, conv_weight, conv_bias):
    summed = inputs + conv_bias + conv_weight[1] * inputs
    for tap_index, offset in ((0, -dilation), (2, dilation)):
        moved_rows = shifted(inputs, offset, 0.0)
        moved_pages = shifted(page_ids, offset, -1)
        same_page = (moved_pages == page_ids)[:, None]
        summed = summed + conv_weight[tap_index] * jnp.where(same_page, moved_rows, 0.0)
    return summed


def bin_features(pos_bins, bins_x, bins_y):
    return jnp.concatenate(
        [
            jax.nn.one_hot(pos_bins, POS_BINS, dtype=bf16),
            jax.nn.one_hot(bins_x, BOX_BINS, dtype=bf16),
            jax.nn.one_hot(bins_y, BOX_BINS, dtype=bf16),
        ],
        axis=1,
    )


def token_ids(text_pages, text_x, text_y):
    text_index = jnp.arange(TEXT, dtype=jnp.int32)
    text_pos = text_index * POS_BINS // TEXT
    patch_pos = text_index % PATCH * POS_BINS // PATCH
    patch_page = text_index // PATCH
    patch_x = text_index % GRID * BOX_BINS // GRID
    patch_y = text_index // GRID % GRID * BOX_BINS // GRID
    page_ids = jnp.stack([text_pages, patch_page])
    pos_bins = jnp.stack([text_pos, patch_pos])
    bins_x = jnp.stack([text_x, patch_x])
    bins_y = jnp.stack([text_y, patch_y])
    return (page_ids, pos_bins, bins_x, bins_y)


def plain_dot(left_side, right_side):
    return jnp.dot(left_side, right_side, preferred_element_type=f32)


def dot_left_t(left_side, right_side):
    return lax.dot_general(
        left_side, right_side, (((0,), (0,)), ((), ())), preferred_element_type=f32
    )


def dot_right_t(left_side, right_side):
    return lax.dot_general(
        left_side, right_side, (((1,), (1,)), ((), ())), preferred_element_type=f32
    )


def column_sum(values):
    return jnp.sum(values, axis=0, keepdims=True, dtype=f32)


def iota(shape, axis):
    return lax.broadcasted_iota(jnp.int32, shape, axis)


def bias_block(table_rows):
    pos_part = pltpu.roll(
        jnp.broadcast_to(table_rows[0:1], (POS_BINS, LANES)), 65, 1, stride=1, stride_axis=0
    )
    x_part = pltpu.roll(
        jnp.broadcast_to(table_rows[1:2], (BOX_BINS, LANES)), 33, 1, stride=1, stride_axis=0
    )
    y_part = pltpu.roll(
        jnp.broadcast_to(table_rows[2:3], (BOX_BINS, LANES)), 65, 1, stride=1, stride_axis=0
    )
    lane = iota((POS_BINS, LANES), 1)
    pos_part = jnp.where(lane < POS_BINS, pos_part, 0.0)
    lane = iota((BOX_BINS, LANES), 1)
    x_part = jnp.where((lane >= 64) & (lane < 96), x_part, 0.0)
    y_part = jnp.where(lane >= 96, y_part, 0.0)
    return jnp.concatenate([pos_part, x_part, y_part], axis=0).astype(bf16)


def diagonal_sums(grad_block):
    lane = iota((POS_BINS, LANES), 1)
    pos_part = jnp.where(lane < POS_BINS, grad_block[:64], 0.0)
    lane = iota((BOX_BINS, LANES), 1)
    x_part = jnp.where((lane >= 64) & (lane < 96), grad_block[64:96], 0.0)
    y_part = jnp.where(lane >= 96, grad_block[96:], 0.0)
    pos_part = pltpu.roll(pos_part, 0, 1, stride=1, stride_axis=0)
    x_part = pltpu.roll(x_part, 0, 1, stride=1, stride_axis=0)
    y_part = pltpu.roll(y_part, 96, 1, stride=1, stride_axis=0)
    rows = [jnp.sum(part, axis=0, keepdims=True) for part in (pos_part, x_part, y_part)]
    return jnp.concatenate(rows + [jnp.zeros((5, LANES), f32)], axis=0)


def stacked_heads(rows, low_lane):
    zero = jnp.zeros_like(rows)
    return jnp.concatenate(
        [jnp.where(low_lane, rows, zero), jnp.where(low_lane, zero, rows)], axis=0
    )


def page_operands(page, bounds, q_ref, k_ref, feat_ref, lookup):
    own_at = pl.multiple_of(bounds[page], 16)
    key_at = pl.multiple_of(bounds[3 * PAGES + page], 16)
    low_lane = iota((WINDOW, LANES), 1) < HEAD
    queries = stacked_heads(q_ref[pl.ds(own_at, WINDOW), :], low_lane)
    rel = jnp.concatenate(
        [lookup[pl.ds(own_at, WINDOW), :LANES], lookup[pl.ds(own_at, WINDOW), LANES:]], axis=0
    )
    query_side = jnp.concatenate([rel, queries], axis=1)
    patch_rows = pl.ds(TEXT + PATCH * page, PATCH)
    text_rows = pl.ds(key_at, WINDOW)
    key_side = jnp.concatenate(
        [
            jnp.concatenate([feat_ref[text_rows, :], k_ref[text_rows, :]], axis=1),
            jnp.concatenate([feat_ref[patch_rows, :], k_ref[patch_rows, :]], axis=1),
        ],
        axis=0,
    )
    own_row = iota((WINDOW, LANES), 0) + own_at
    own_ok = (own_row >= bounds[PAGES + page]) & (own_row < bounds[2 * PAGES + page])
    return own_at, key_at, low_lane, own_ok, queries, query_side, key_side, text_rows, patch_rows


def attend_kernel(bounds, q_ref, k_ref, v_ref, feat_ref, own_feat_ref, table_ref, context_ref, lookup):
    blocks = jnp.concatenate([bias_block(table_ref[0]), bias_block(table_ref[1])], axis=1)
    lookup[...] = jnp.dot(own_feat_ref[...], blocks, preferred_element_type=f32).astype(bf16)
    for page in range(PAGES):
        own_at, key_at, low_lane, own_ok, queries, query_side, key_side, text_rows, patch_rows = (
            page_operands(page, bounds, q_ref, k_ref, feat_ref, lookup)
        )
        scores = dot_right_t(query_side, key_side)
        column = iota((1, KEYS), 1)
        key_row = column + key_at
        key_ok = (column >= WINDOW) | (
            (key_row >= bounds[4 * PAGES + page]) & (key_row < bounds[5 * PAGES + page])
        )
        scores = jnp.where(key_ok, scores, mask_fill)
        row_max = jnp.max(scores, axis=1, keepdims=True)
        weights = jnp.exp(scores - row_max)
        total = jnp.sum(weights, axis=1, keepdims=True)
        prob = (weights * (1.0 / total)).astype(bf16)
        values = jnp.concatenate([v_ref[text_rows, :], v_ref[patch_rows, :]], axis=0)
        mixed = jnp.dot(prob, values, preferred_element_type=f32)
        picked = jnp.where(low_lane, mixed[:WINDOW], mixed[WINDOW:])
        before = context_ref[pl.ds(own_at, WINDOW), :].astype(f32)
        context_ref[pl.ds(own_at, WINDOW), :] = jnp.where(own_ok, picked, before).astype(bf16)


def attend_back_kernel(
    bounds,
    q_ref,
    k_ref,
    v_ref,
    grad_ref,
    feat_ref,
    own_feat_ref,
    flip_feat_ref,
    table_ref,
    grad_q_ref,
    grad_k_ref,
    grad_v_ref,
    grad_table_ref,
    lookup,
    grad_lookup,
):
    blocks = jnp.concatenate([bias_block(table_ref[0]), bias_block(table_ref[1])], axis=1)
    lookup[...] = jnp.dot(own_feat_ref[...], blocks, preferred_element_type=f32).astype(bf16)
    for page in range(PAGES):
        own_at, key_at, low_lane, own_ok, queries, query_side, key_side, text_rows, patch_rows = (
            page_operands(page, bounds, q_ref, k_ref, feat_ref, lookup)
        )
        scores = dot_right_t(key_side, query_side)
        row = iota((KEYS, 1), 0)
        key_row = row + key_at
        key_in = (key_row >= bounds[4 * PAGES + page]) & (key_row < bounds[5 * PAGES + page])
        scores = jnp.where((row >= WINDOW) | key_in, scores, mask_fill)
        col_max = jnp.max(scores, axis=0, keepdims=True)
        weights = jnp.exp(scores - col_max)
        total = jnp.sum(weights, axis=0, keepdims=True)
        prob = weights * (1.0 / total)
        grad_rows = grad_ref[pl.ds(own_at, WINDOW), :]
        grad_rows = jnp.where(own_ok, grad_rows, jnp.zeros_like(grad_rows))
        grads = stacked_heads(grad_rows, low_lane)
        values = jnp.concatenate([v_ref[text_rows, :], v_ref[patch_rows, :]], axis=0)
        grad_prob = dot_right_t(values, grads)
        inner = jnp.sum(prob * grad_prob, axis=0, keepdims=True)
        grad_scores = (prob * (grad_prob - inner)).astype(bf16)
        grad_v = jnp.dot(prob.astype(bf16), grads, preferred_element_type=f32)
        grad_k = jnp.dot(grad_scores, queries, preferred_element_type=f32)
        back = dot_left_t(grad_scores, key_side)
        grad_q = jnp.where(low_lane, back[:WINDOW, LANES:], back[WINDOW:, LANES:]) * 0.125
        own_rows = pl.ds(own_at, WINDOW)
        before = grad_q_ref[own_rows, :].astype(f32)
        grad_q_ref[own_rows, :] = jnp.where(own_ok, grad_q, before).astype(bf16)
        grad_lookup[own_rows, :LANES] = jnp.where(
            own_ok, back[:WINDOW, :LANES], grad_lookup[own_rows, :LANES]
        )
        grad_lookup[own_rows, LANES:] = jnp.where(
            own_ok, back[WINDOW:, :LANES], grad_lookup[own_rows, LANES:]
        )
        wide_row = iota((WINDOW, LANES), 0) + key_at
        text_ok = (wide_row >= bounds[4 * PAGES + page]) & (wide_row < bounds[5 * PAGES + page])
        for grad, ref in ((grad_k, grad_k_ref), (grad_v, grad_v_ref)):
            before = ref[text_rows, :].astype(f32)
            ref[text_rows, :] = jnp.where(text_ok, grad[:WINDOW], before).astype(bf16)
            ref[patch_rows, :] = grad[WINDOW:].astype(bf16)
    grad_high = grad_lookup[...].astype(bf16)
    grad_rest = (grad_lookup[...] - grad_high.astype(f32)).astype(bf16)
    flip = flip_feat_ref[...]
    grad_block = dot_left_t(flip, grad_high) + dot_left_t(flip, grad_rest)
    grad_table_ref[0] = diagonal_sums(grad_block[:, :LANES])
    grad_table_ref[1] = diagonal_sums(grad_block[:, LANES:])


def column_spec(rows, first=0):
    return pl.BlockSpec((rows, LANES), lambda pair, bounds: (0, pair + first))


def tables_spec(first=0):
    return pl.BlockSpec((2, 8, LANES), lambda pair, bounds: (pair + first, 0, 0))


def whole_spec(rows):
    return pl.BlockSpec((rows, LANES), lambda pair, bounds: (0, 0))


def attend(bounds, queries, keys_values, features, own_features, tables):
    return pl.pallas_call(
        attend_kernel,
        grid_spec=pltpu.PrefetchScalarGridSpec(
            num_scalar_prefetch=1,
            grid=(PAIRS,),
            in_specs=[
                column_spec(TEXT),
                column_spec(2 * TEXT),
                column_spec(2 * TEXT, PAIRS),
                whole_spec(2 * TEXT),
                whole_spec(TEXT),
                tables_spec(),
            ],
            out_specs=column_spec(TEXT),
            scratch_shapes=[pltpu.VMEM((TEXT, 2 * LANES), bf16)],
        ),
        out_shape=jax.ShapeDtypeStruct((TEXT, HEADS * HEAD), bf16),
        cost_estimate=small_cost,
        name="attend",
    )(bounds, queries, keys_values, keys_values, features, own_features, tables)


def attend_back(
    bounds, queries, keys_values, grad_context, features, own_features, flip, tables, first, count
):
    return pl.pallas_call(
        attend_back_kernel,
        grid_spec=pltpu.PrefetchScalarGridSpec(
            num_scalar_prefetch=1,
            grid=(count,),
            in_specs=[
                column_spec(TEXT, first),
                column_spec(2 * TEXT, first),
                column_spec(2 * TEXT, PAIRS + first),
                column_spec(TEXT, first),
                whole_spec(2 * TEXT),
                whole_spec(TEXT),
                whole_spec(TEXT),
                tables_spec(first),
            ],
            out_specs=[
                column_spec(TEXT),
                column_spec(2 * TEXT),
                column_spec(2 * TEXT),
                tables_spec(),
            ],
            scratch_shapes=[
                pltpu.VMEM((TEXT, 2 * LANES), bf16),
                pltpu.VMEM((TEXT, 2 * LANES), f32),
            ],
        ),
        out_shape=[
            jax.ShapeDtypeStruct((TEXT, count * LANES), bf16),
            jax.ShapeDtypeStruct((2 * TEXT, count * LANES), bf16),
            jax.ShapeDtypeStruct((2 * TEXT, count * LANES), bf16),
            jax.ShapeDtypeStruct((2 * count, 8, LANES), f32),
        ],
        cost_estimate=small_cost,
        name="attend_back",
    )(
        bounds,
        queries,
        keys_values,
        keys_values,
        grad_context,
        features,
        own_features,
        flip,
        tables,
    )


def exchange(values, mask):
    count = lax.axis_size("page")
    return lax.ppermute(values, "page", [(i, i ^ mask) for i in range(count)])


def after(value, *earlier):
    return lax.optimization_barrier((value, *earlier))[0]


def slot_mask(slot):
    return (slot & 3) * 4 + (slot >> 2) * 2


def place_halves_kernel(place, *refs):
    pieces, full_ref, sems = refs[:4], refs[4], refs[5]
    rows, half = pieces[0].shape[1], pieces[0].shape[2]
    copies = []
    for index in range(32):
        kind = index >> 3
        mask = slot_mask(index & 7) + (kind & 1)
        at = pl.multiple_of((place[0] ^ mask) * rows, 16)
        column = pl.multiple_of((place[1] ^ (kind >> 1)) * half, 128)
        copies.append(
            pltpu.make_async_copy(
                pieces[kind].at[index & 7],
                full_ref.at[pl.ds(at, rows), pl.ds(column, half)],
                sems.at[index],
            )
        )
    for copy in copies:
        copy.start()
    for copy in copies:
        copy.wait()


def place_rows(place, pieces, width, kernel):
    rows = pieces[0].shape[1]
    return pl.pallas_call(
        kernel,
        grid_spec=pltpu.PrefetchScalarGridSpec(
            num_scalar_prefetch=1,
            grid=(),
            in_specs=[pl.BlockSpec(memory_space=pl.ANY)] * 4,
            out_specs=pl.BlockSpec(memory_space=pltpu.VMEM),
            scratch_shapes=[pltpu.SemaphoreType.DMA((32,))],
        ),
        out_shape=jax.ShapeDtypeStruct((16 * rows, width), bf16),
        cost_estimate=small_cost,
        name="place_rows",
    )(place, *pieces)


def column_parts(shard):
    return [shard] + [exchange(shard, 4 * step) for step in (1, 2, 3)]


def column_of(shard):
    return jnp.stack(column_parts(shard))


def start_rows(place, pieces, full, sems, first=0):
    if len(pieces) == 1:
        copies = [pltpu.make_async_copy(pieces[0], full, sems.at[first])]
    else:
        rows = pieces[0].shape[1]
        copies = []
        for index in range(16):
            mask = (index >> 2) * 4 + (index & 3)
            at = pl.multiple_of((place[0] ^ mask) * rows, 16)
            copies.append(
                pltpu.make_async_copy(
                    pieces[index & 3].at[index >> 2],
                    full.at[pl.ds(at, rows)],
                    sems.at[first + index],
                )
            )
    for copy in copies:
        copy.start()
    return copies


def gelu_parts(values):
    size = jnp.abs(values)
    t = 1.0 / (1.0 + (0.42 * 0.7071067811865476) * size)
    poly = jnp.full_like(t, erfc_poly[-1])
    for coefficient in erfc_poly[-2::-1]:
        poly = poly * t + coefficient
    bell = jnp.exp(-0.5 * values * values)
    tail = (0.5 * t) * (poly * bell)
    cdf = jnp.where(values >= 0.0, 1.0 - tail, tail)
    return values * cdf, cdf + (values * 0.3989422804014327) * bell


def normalized(values):
    centered = values - jnp.mean(values, axis=1, keepdims=True)
    variance = jnp.mean(centered * centered, axis=1, keepdims=True)
    scale = lax.rsqrt(variance + norm_eps)
    return centered * scale, scale


def norm_back(grads, unit, scale, gain):
    scaled = grads * gain
    mean = jnp.mean(scaled, axis=1, keepdims=True)
    inner = jnp.mean(scaled * unit, axis=1, keepdims=True)
    return scale * (scaled - mean - unit * inner)


def up_kernel(place, context_ref, mixed_ref, vec_ref, bias_ref, *refs):
    *pieces, unit_ref, scale_ref, low_ref, low_t_ref, active_ref, active_t_ref, slope_ref = refs[:-4]
    weight, hidden, low, sems = refs[-4:]
    step = pl.program_id(0)
    tiles = pl.num_programs(0) - 1
    width = context_ref.shape[1]
    tile = active_ref.shape[1]

    @pl.when(step == 0)
    def _():
        for copy in start_rows(place, pieces, weight, sems):
            copy.wait()
        branch = jnp.dot(context_ref[...], weight[:, :width], preferred_element_type=f32)
        unit, scale = normalized(mixed_ref[...] + branch + vec_ref[0:1])
        unit_ref[...] = unit
        scale_ref[...] = jnp.broadcast_to(scale, scale_ref.shape)
        normed = (unit * vec_ref[1:2] + vec_ref[2:3]).astype(bf16)
        low[...] = normed
        low_ref[...] = normed
        low_t_ref[...] = normed.T

    def product():
        at = pl.multiple_of(width + step * tile, 128)
        return jnp.dot(low[...], weight[:, pl.ds(at, tile)], preferred_element_type=f32)

    def activate():
        active, slope = gelu_parts(hidden[(step + 1) % 2] + bias_ref[...])
        active = active.astype(bf16)
        active_ref[...] = active
        active_t_ref[...] = active.T
        slope_ref[...] = slope

    @pl.when(step == 0)
    def _():
        hidden[step % 2] = product()

    @pl.when((step > 0) & (step < tiles))
    def _():
        hidden[step % 2] = product()
        activate()

    @pl.when(step == tiles)
    def _():
        activate()


def any_specs(count):
    return [pl.BlockSpec(memory_space=pl.ANY)] * count


def up_forward(place, context, mixed, vectors, bias_up, pieces):
    tokens, width = mixed.shape
    hidden_width = bias_up.shape[1]
    tile = 512
    whole = lambda step, place: (0, 0)
    last = lambda step, place: (0, jnp.maximum(step - 1, 0))
    last_t = lambda step, place: (jnp.maximum(step - 1, 0), 0)
    return pl.pallas_call(
        up_kernel,
        grid_spec=pltpu.PrefetchScalarGridSpec(
            num_scalar_prefetch=1,
            grid=(hidden_width // tile + 1,),
            in_specs=[
                pl.BlockSpec((tokens, width), whole),
                pl.BlockSpec((tokens, width), whole),
                pl.BlockSpec(vectors.shape, whole),
                pl.BlockSpec((1, tile), last),
            ]
            + any_specs(len(pieces)),
            out_specs=[
                pl.BlockSpec((tokens, width), whole),
                pl.BlockSpec((tokens, 128), whole),
                pl.BlockSpec((tokens, width), whole),
                pl.BlockSpec((width, tokens), whole),
                pl.BlockSpec((tokens, tile), last),
                pl.BlockSpec((tile, tokens), last_t),
                pl.BlockSpec((tokens, tile), last),
            ],
            scratch_shapes=[
                pltpu.VMEM((width, width + hidden_width), bf16),
                pltpu.VMEM((2, tokens, tile), f32),
                pltpu.VMEM((tokens, width), bf16),
                pltpu.SemaphoreType.DMA((16,)),
            ],
        ),
        out_shape=[
            jax.ShapeDtypeStruct((tokens, width), f32),
            jax.ShapeDtypeStruct((tokens, 128), f32),
            jax.ShapeDtypeStruct((tokens, width), bf16),
            jax.ShapeDtypeStruct((width, tokens), bf16),
            jax.ShapeDtypeStruct((tokens, hidden_width), bf16),
            jax.ShapeDtypeStruct((hidden_width, tokens), bf16),
            jax.ShapeDtypeStruct((tokens, hidden_width), f32),
        ],
        cost_estimate=small_cost,
        name="up_forward",
    )(place, context, mixed, vectors, bias_up, *pieces)


def down_kernel(place, active_ref, unit_ref, vec_ref, grad_ref, *refs):
    *pieces, out_ref, sum_ref, low_ref, small_ref = refs[:-2]
    weight, sems = refs[-2:]
    for copy in start_rows(place, pieces, weight, sems):
        copy.wait()
    tokens, width = unit_ref.shape
    half = tokens // 2
    smalls = [jnp.zeros((1, width), f32)] * 3
    for part in range(2):
        rows = pl.ds(part * half, half)
        ffn = jnp.dot(active_ref[rows, :], weight[...], preferred_element_type=f32)
        normed = unit_ref[rows, :] * vec_ref[1:2] + vec_ref[2:3]
        unit, scale = normalized(normed + ffn + vec_ref[3:4])
        out_ref[rows, :] = (unit * vec_ref[4:5] + vec_ref[5:6]).astype(bf16)
        grads = grad_ref[rows, :].astype(f32)
        total = norm_back(grads, unit, scale, vec_ref[4:5])
        low = total.astype(bf16)
        sum_ref[rows, :] = total
        low_ref[rows, :] = low
        for index, term in enumerate((grads * unit, grads, low.astype(f32))):
            smalls[index] = smalls[index] + jnp.sum(term, axis=0, keepdims=True)
    small_ref[...] = jnp.concatenate(smalls + [jnp.zeros((5, width), f32)], axis=0)


def down_forward(place, active, unit, vectors, grads, pieces):
    tokens, width = unit.shape
    hidden_width = active.shape[1]
    vmem = pl.BlockSpec(memory_space=pltpu.VMEM)
    return pl.pallas_call(
        down_kernel,
        grid_spec=pltpu.PrefetchScalarGridSpec(
            num_scalar_prefetch=1,
            grid=(),
            in_specs=[vmem] * 4 + any_specs(len(pieces)),
            out_specs=[vmem] * 4,
            scratch_shapes=[
                pltpu.VMEM((hidden_width, width), bf16),
                pltpu.SemaphoreType.DMA((16,)),
            ],
        ),
        out_shape=[
            jax.ShapeDtypeStruct((tokens, width), bf16),
            jax.ShapeDtypeStruct((tokens, width), f32),
            jax.ShapeDtypeStruct((tokens, width), bf16),
            jax.ShapeDtypeStruct((8, width), f32),
        ],
        cost_estimate=small_cost,
        name="down_forward",
    )(place, active, unit, vectors, grads, *pieces)


def ffn_back_kernel(count, place, low_ref, slope_ref, sum_ref, unit_ref, scale_ref, vec_ref, *refs):
    rest, down = refs[:count], refs[count : 2 * count]
    hidden_ref, bias_ref, first_ref, branch_ref, context_ref, small_ref = refs[2 * count : -4]
    weight, weight_down, total, sems = refs[-4:]
    step = pl.program_id(0)
    tokens, width = unit_ref.shape
    tile = slope_ref.shape[1]
    half = tokens // 2

    @pl.when(step == 0)
    def _():
        copies = start_rows(place, down, weight_down, sems)
        copies += start_rows(place, rest, weight, sems, 16)
        total[...] = sum_ref[...]
        for copy in copies:
            copy.wait()

    rows_down = weight_down[pl.ds(pl.multiple_of(step * tile, 128), tile), :]
    columns = weight[:, pl.ds(pl.multiple_of(width + step * tile, 128), tile)]
    bias = jnp.zeros((1, tile), f32)
    for part in range(2):
        rows = pl.ds(part * half, half)
        grads = (dot_right_t(low_ref[rows, :], rows_down) * slope_ref[rows, :]).astype(bf16)
        hidden_ref[rows, :] = grads
        bias = bias + jnp.sum(grads.astype(f32), axis=0, keepdims=True)
        total[rows, :] += dot_right_t(grads, columns)
    bias_ref[...] = bias

    @pl.when(step == pl.num_programs(0) - 1)
    def _():
        grads = total[...]
        unit = unit_ref[...]
        first = norm_back(grads, unit, scale_ref[:, 0:1], vec_ref[1:2])
        branch = first.astype(bf16)
        first_ref[...] = first
        branch_ref[...] = branch
        context_ref[...] = dot_right_t(branch, weight[:, :width]).astype(bf16)
        smalls = [
            jnp.sum(term, axis=0, keepdims=True)
            for term in (grads * unit, grads, branch.astype(f32))
        ]
        small_ref[...] = jnp.concatenate(smalls + [jnp.zeros((5, width), f32)], axis=0)


def ffn_back(place, low, slope, total, unit, scale, vectors, pieces_rest, pieces_down):
    tokens, width = unit.shape
    hidden_width = slope.shape[1]
    tile = 512
    count = len(pieces_rest)
    whole = lambda step, place: (0, 0)
    column = lambda step, place: (0, step)
    return pl.pallas_call(
        functools.partial(ffn_back_kernel, count),
        grid_spec=pltpu.PrefetchScalarGridSpec(
            num_scalar_prefetch=1,
            grid=(hidden_width // tile,),
            in_specs=[
                pl.BlockSpec((tokens, width), whole),
                pl.BlockSpec((tokens, tile), column),
                pl.BlockSpec((tokens, width), whole),
                pl.BlockSpec((tokens, width), whole),
                pl.BlockSpec((tokens, 128), whole),
                pl.BlockSpec(vectors.shape, whole),
            ]
            + any_specs(2 * count),
            out_specs=[
                pl.BlockSpec((tokens, tile), column),
                pl.BlockSpec((1, tile), column),
                pl.BlockSpec((tokens, width), whole),
                pl.BlockSpec((tokens, width), whole),
                pl.BlockSpec((tokens, width), whole),
                pl.BlockSpec((8, width), whole),
            ],
            scratch_shapes=[
                pltpu.VMEM((width, width + hidden_width), bf16),
                pltpu.VMEM((hidden_width, width), bf16),
                pltpu.VMEM((tokens, width), f32),
                pltpu.SemaphoreType.DMA((32,)),
            ],
        ),
        out_shape=[
            jax.ShapeDtypeStruct((tokens, hidden_width), bf16),
            jax.ShapeDtypeStruct((1, hidden_width), f32),
            jax.ShapeDtypeStruct((tokens, width), f32),
            jax.ShapeDtypeStruct((tokens, width), bf16),
            jax.ShapeDtypeStruct((tokens, width), bf16),
            jax.ShapeDtypeStruct((8, width), f32),
        ],
        cost_estimate=small_cost,
        name="ffn_back",
    )(place, low, slope, total, unit, scale, vectors, *pieces_rest, *pieces_down)


def grad_rows_kernel(place, mine_ref, theirs_ref, h_ref, keep_ref, send_ref):
    rows = keep_ref.shape[1]
    both = jnp.concatenate([mine_ref[0], theirs_ref[0]], axis=0)
    product = jnp.dot(both, h_ref[...], preferred_element_type=f32)
    keep_ref[0] = product[:rows].astype(bf16)
    send_ref[0] = product[rows:].astype(bf16)


def grad_by_rows(inputs_t, grads, place):
    width, tokens = inputs_t.shape
    columns = grads.shape[1]
    rows = width // 16
    inputs_t = inputs_t.reshape(16, rows, tokens)
    half = jax.ShapeDtypeStruct((8, rows, columns), bf16)
    out = pl.BlockSpec((1, rows, columns), lambda slot, place: (slot, 0, 0))
    return pl.pallas_call(
        grad_rows_kernel,
        grid_spec=pltpu.PrefetchScalarGridSpec(
            num_scalar_prefetch=1,
            grid=(8,),
            in_specs=[
                pl.BlockSpec((1, rows, tokens), lambda slot, place: (place[0] ^ slot_mask(slot), 0, 0)),
                pl.BlockSpec(
                    (1, rows, tokens), lambda slot, place: (place[0] ^ (slot_mask(slot) + 1), 0, 0)
                ),
                pl.BlockSpec((tokens, columns), lambda slot, place: (0, 0)),
            ],
            out_specs=[out, out],
        ),
        out_shape=[half, half],
        cost_estimate=small_cost,
        name="grad_rows",
    )(place, inputs_t, inputs_t, grads)


def grad_columns_kernel(parts, place, *refs):
    count = len(parts)
    ins, keep_ref, send_ref, scratch = (
        refs[: 2 * count],
        refs[2 * count],
        refs[2 * count + 1],
        refs[2 * count + 2 :],
    )
    rows, tile = keep_ref.shape[1], keep_ref.shape[2]
    step = pl.program_id(0)
    first = 0
    for index, steps in enumerate(parts):
        x_ref, h_ref, ordered = ins[2 * index], ins[2 * index + 1], scratch[index]

        @pl.when(step == first)
        def _():
            for slot in range(16):
                mask = slot_mask(slot & 7) + (slot >> 3)
                at = pl.multiple_of((place[0] ^ mask) * rows, 16)
                ordered[pl.ds(slot * rows, rows), :] = x_ref[pl.ds(at, rows), :]

        @pl.when((step >= first) & (step < first + steps))
        def _():
            product = jnp.dot(ordered[...], h_ref[...], preferred_element_type=f32).astype(bf16)
            keep_ref[...] = product[: 8 * rows].reshape(8, rows, tile)
            send_ref[...] = product[8 * rows :].reshape(8, rows, tile)

        first = first + steps


def grad_by_columns(pairs, place, tile):
    width = pairs[0][0].shape[0]
    rows = width // 16
    parts = tuple(sum(grad.shape[1] for grad in grads) // tile for _, _, *grads in pairs)
    steps = sum(parts)
    specs = []
    operands = []
    scratch = []
    first = 0
    for (inputs_t, own, *grads), count in zip(pairs, parts):
        tokens = grads[0].shape[0]
        block = (lambda step, place: (0, place[1])) if own else (lambda step, place: (0, 0))
        specs.append(pl.BlockSpec((width, tokens), block))

        def column(step, place, first=first, count=count):
            return (0, jnp.clip(step - first, 0, count - 1))

        specs.append(pl.BlockSpec((tokens, tile), column))
        operands += [inputs_t, *grads]
        scratch.append(pltpu.VMEM((width, tokens), bf16))
        first = first + count
    half = jax.ShapeDtypeStruct((8, rows, steps * tile), bf16)
    return pl.pallas_call(
        functools.partial(grad_columns_kernel, parts),
        grid_spec=pltpu.PrefetchScalarGridSpec(
            num_scalar_prefetch=1,
            grid=(steps,),
            in_specs=specs,
            out_specs=[pl.BlockSpec((8, rows, tile), lambda step, place: (0, 0, step))] * 2,
            scratch_shapes=scratch,
        ),
        out_shape=[half, half],
        cost_estimate=small_cost,
        name="grad_columns",
    )(place, *operands)


def first_half_kernel(place, keep_near, part_near, keep_far, part_far, held_ref, out_ref):
    held_ref[...] = keep_near[...].astype(f32) + part_near[...].astype(f32)
    out_ref[...] = (keep_far[...].astype(f32) + part_far[...].astype(f32)).astype(bf16)


def halve_call(place, keep, partner, specs, half_shape, steps):
    near, far, out = specs
    return pl.pallas_call(
        first_half_kernel,
        grid_spec=pltpu.PrefetchScalarGridSpec(
            num_scalar_prefetch=1,
            grid=(steps,),
            in_specs=[near, near, far, far],
            out_specs=[out, out],
        ),
        out_shape=[
            jax.ShapeDtypeStruct(half_shape, f32),
            jax.ShapeDtypeStruct(half_shape, bf16),
        ],
        cost_estimate=small_cost,
        name="halve",
    )(place, keep, partner, keep, partner)


def halve_across(place, keep, partner):
    _, rows, width = keep.shape
    near = pl.BlockSpec((1, rows, width), lambda step, place: (step, 0, 0))
    far = pl.BlockSpec((1, rows, width), lambda step, place: (step + 4, 0, 0))
    return halve_call(place, keep, partner, (near, far, near), (4, rows, width), 4)


def halve_plane(place, keep, partner):
    _, rows, width = keep.shape
    block = (2, rows, width // 2)
    near = pl.BlockSpec(block, lambda step, place: (step, 0, place[1]))
    far = pl.BlockSpec(block, lambda step, place: (step, 0, 1 - place[1]))
    out = pl.BlockSpec(block, lambda step, place: (step, 0, 0))
    return halve_call(place, keep, partner, (near, far, out), (8, rows, width // 2), 4)


def column_kernel(held_ref, across_ref, own_ref, *sends):
    own_ref[...] = held_ref[0] + across_ref[0].astype(f32)
    for step, send in enumerate(sends, 1):
        send[...] = (held_ref[step] + across_ref[step].astype(f32)).astype(bf16)


def column_sends(held, across):
    _, rows, width = held.shape
    tile = 384
    out = pl.BlockSpec((rows, tile), lambda step: (0, step))
    block = pl.BlockSpec((4, rows, tile), lambda step: (0, 0, step))
    own, *sends = pl.pallas_call(
        column_kernel,
        grid=(width // tile,),
        in_specs=[block, block],
        out_specs=[out] * 4,
        out_shape=[jax.ShapeDtypeStruct((rows, width), f32)]
        + [jax.ShapeDtypeStruct((rows, width), bf16)] * 3,
        cost_estimate=small_cost,
        name="column_sends",
    )(held, across)
    return own, sends


def column_arrivals(sends):
    return [exchange(send, 4 * step) for step, send in enumerate(sends, 1)]


def column_total(own, arrived):
    total = own
    for part in arrived:
        total = total + part.astype(f32)
    return total.astype(bf16)


def half_columns(values, first):
    half = values.shape[-1] // 2
    return jnp.where(first, values[..., :half], values[..., half:])


def summed_rows(pairs):
    grads = jnp.concatenate([plain_dot(*pair).astype(bf16) for pair in pairs], axis=1)
    shard = lax.psum_scatter(grads, "page", scatter_dimension=0, tiled=True)
    return shard.astype(f32) + swap(shard).astype(f32)


def page_bounds(segments, is_text):
    pages = jnp.arange(PAGES, dtype=jnp.int32)
    low = jnp.sum(segments[None, :] < pages[:, None], axis=1, dtype=jnp.int32)
    high = jnp.sum(segments[None, :] <= pages[:, None], axis=1, dtype=jnp.int32)
    own_low = jnp.where(is_text, low, pages * PATCH)
    own_high = jnp.where(is_text, high, (pages + 1) * PATCH)

    def aligned(start):
        return jnp.minimum(start // 16 * 16, TEXT - WINDOW)

    return jnp.concatenate([aligned(own_low), own_low, own_high, aligned(low), low, high])


def sum_everywhere(values):
    count = lax.axis_size("page")
    if count & (count - 1):
        values = lax.psum(values, "page")
    else:
        step = 1
        while step < count:
            values = values + lax.ppermute(values, "page", [(i, i ^ step) for i in range(count)])
            step = step * 2
    return values + swap(values)


def swap(values):
    return lax.ppermute(values, "mod", [(0, 1), (1, 0)])


def local(
    states,
    cotangent,
    segments,
    box_x,
    box_y,
    conv_weight,
    conv_bias,
    w_query,
    b_query,
    w_key,
    w_value,
    b_value,
    w_out,
    b_out,
    table_pos,
    table_x,
    table_y,
    gain_one,
    bias_one,
    w_up,
    b_up,
    w_down,
    b_down,
    gain_two,
    bias_two,
):
    is_text = lax.axis_index("mod") == 0
    d_model = states.shape[3]
    own_low = states[0, 0]
    rows_each = w_query.shape[0]
    d_ff = w_up.shape[1]
    fast = lax.axis_size("page") == 16 and rows_each % 16 == 0 and w_down.shape[0] % 16 == 0
    place = jnp.stack([lax.axis_index("page"), lax.axis_index("mod")]).astype(jnp.int32)
    pack_qkv = jnp.concatenate([w_query, w_key, w_value], axis=1)
    pack_rest = jnp.concatenate([w_out, w_up], axis=1)
    other_low = swap(own_low)
    if fast:
        column_qkv = column_of(half_columns(pack_qkv, is_text))
        parts_rest = column_parts(after(pack_rest, column_qkv))
        eight = jnp.concatenate([column_qkv, exchange(column_qkv, 2)])
        far = swap(eight)
        pieces = [eight, exchange(eight, 1), far, exchange(far, 1)]
        column_rest = jnp.stack([after(part, eight, far) for part in parts_rest])
        parts_down = column_parts(after(w_down, column_rest))
        pieces[0] = after(pieces[0], column_rest)
        full_qkv = place_rows(place, pieces, pack_qkv.shape[1], place_halves_kernel)
    else:
        full_qkv = lax.all_gather(pack_qkv, "page", axis=0, tiled=True)

    page_ids, pos_bins, bins_x, bins_y = token_ids(segments[0], box_x[0], box_y[0])
    bounds = page_bounds(segments[0], is_text)
    own_pages = jnp.where(is_text, page_ids[0], page_ids[1])
    features = bin_features(pos_bins.reshape(-1), bins_x.reshape(-1), bins_y.reshape(-1))
    flipped = bin_features(
        POS_BINS - 1 - pos_bins.reshape(-1),
        BOX_BINS - 1 - bins_x.reshape(-1),
        BOX_BINS - 1 - bins_y.reshape(-1),
    )
    own_feats = jnp.where(is_text, features[:TEXT], features[TEXT:])
    own_flip = jnp.where(is_text, flipped[:TEXT], flipped[TEXT:])
    tables = jnp.stack(
        [
            jnp.pad(table_pos, ((0, 0), (0, LANES - table_pos.shape[1]))),
            jnp.pad(table_x, ((0, 0), (0, LANES - table_x.shape[1]))),
            jnp.pad(table_y, ((0, 0), (0, LANES - table_y.shape[1]))),
        ],
        axis=1,
    )
    tables = jnp.pad(tables, ((0, 0), (0, 5), (0, 0)))

    def mix_fn(inputs_f, weight_f, bias_f):
        return dilated_mix(inputs_f, own_pages, weight_f, bias_f)

    own_states = own_low.astype(f32)
    mixed, mix_pull = jax.vjp(mix_fn, own_states, conv_weight, conv_bias)
    mixed_low = mixed.astype(bf16)
    other_pages = jnp.where(is_text, page_ids[1], page_ids[0])
    other_mixed = dilated_mix(other_low.astype(f32), other_pages, conv_weight, conv_bias)
    other_mixed = other_mixed.astype(bf16)
    mixed_all = jnp.concatenate(
        [jnp.where(is_text, mixed_low, other_mixed), jnp.where(is_text, other_mixed, mixed_low)],
        axis=0,
    )
    mixed_t = mixed_all.T
    if fast:
        full_qkv = after(full_qkv, mixed_all, mixed_t, features, tables, bounds, own_flip)
    full_query = full_qkv[:, :d_model]
    full_kv = full_qkv[:, d_model:]
    queries = ((plain_dot(mixed_low, full_query) + b_query).astype(bf16) * 0.125).astype(bf16)
    kv_bias = jnp.concatenate([jnp.zeros_like(b_value), b_value])
    keys_values = (plain_dot(mixed_all, full_kv) + kv_bias).astype(bf16)
    context = attend(bounds, queries, keys_values, features, own_feats, tables)
    if fast:
        across_rest = exchange(column_rest, 2)
        column_down = jnp.stack([after(part, context) for part in parts_down])
        across_rest = after(across_rest, column_down)
        pieces_rest = [column_rest, exchange(column_rest, 1), across_rest, exchange(across_rest, 1)]
    else:
        pieces_rest = [lax.all_gather(pack_rest, "page", axis=0, tiled=True)]
    vectors = jnp.stack(
        [b_out, gain_one, bias_one, b_down, gain_two, bias_two, jnp.zeros_like(b_out), b_out]
    )
    unit, scale, normed_low, normed_t, active, active_t, slope = up_forward(
        place, context, mixed, vectors, b_up[None], pieces_rest
    )
    if fast:
        across_down = exchange(column_down, 2)
        pieces_down = [column_down, exchange(column_down, 1), across_down, exchange(across_down, 1)]
        pieces_down[0] = after(pieces_down[0], active)
    else:
        pieces_down = [lax.all_gather(w_down, "page", axis=0, tiled=True)]
    output_row, grad_sum_two, grad_ffn, small_two = down_forward(
        place, active, unit, vectors, cotangent[0, 0], pieces_down
    )
    grad_ffn_in = grad_ffn
    if fast:
        keep_down, send_down = grad_by_rows(active_t, grad_ffn, place)
        partner_down = exchange(send_down, 1)
        context_t = after(context, send_down).T
        partner_down = after(partner_down, context_t)
        held_down, across_out_down = halve_across(place, keep_down, partner_down)
        across_down = exchange(across_out_down, 2)
        grad_ffn_in = after(grad_ffn, across_out_down)
    else:
        shard_down = summed_rows([(active_t, grad_ffn)])
        context_t = context.T
    grad_hidden, grad_b_up, grad_first, grad_branch, grad_context, small_one = ffn_back(
        place, grad_ffn_in, slope, grad_sum_two, unit, scale, vectors, pieces_rest, pieces_down
    )
    attend_in = grad_context
    if fast:
        pairs = [(context_t, False, grad_branch), (normed_t, False, grad_hidden)]
        keep_rest, send_rest = grad_by_columns(pairs, place, d_model)
        partner_rest = exchange(send_rest, 1)
        across_down = after(across_down, send_rest)
        own_down, sends_down = column_sends(held_down, across_down)
        arrived_down = column_arrivals(sends_down)
        partner_rest = after(partner_rest, *sends_down)
        held_rest, plane_out = halve_plane(place, keep_rest, partner_rest)
        plane_rest = swap(plane_out)
        attend_in = after(grad_context, plane_out)
    else:
        shard_rest = summed_rows([(context_t, grad_branch), (normed_t, grad_hidden)])
    grad_queries, grad_keys, grad_values, grad_tables = attend_back(
        bounds, queries, keys_values, attend_in, features, own_feats, own_flip, tables, 0, PAIRS
    )
    grad_keys_in, grad_queries_in = grad_keys, grad_queries
    if fast:
        plane_rest = after(plane_rest, grad_queries)
        held_rest, across_out_rest = halve_across(place, held_rest, plane_rest)
        across_rest = exchange(across_out_rest, 2)
        arrived_down = [after(part, grad_queries) for part in arrived_down]
        total_down = column_total(own_down, arrived_down)
        far_down = swap(total_down)
        grad_queries_in = after(grad_queries, across_out_rest, total_down)
    pairs = [(mixed_t, True, grad_queries_in), (mixed_t, False, grad_keys), (mixed_t, False, grad_values)]
    if fast:
        keep_qkv, send_qkv = grad_by_columns(pairs, place, d_model)
        partner_qkv = exchange(send_qkv, 1)
        across_rest = after(across_rest, send_qkv)
        own_rest, sends_rest = column_sends(held_rest, across_rest)
        arrived_rest = column_arrivals(sends_rest)
        far_down = after(far_down, send_qkv)
        partner_qkv = after(partner_qkv, far_down, *sends_rest)
        held_qkv, across_out_qkv = halve_across(place, keep_qkv, partner_qkv)
        across_qkv = exchange(across_out_qkv, 2)
        grad_keys_in = after(grad_keys, across_out_qkv)
    else:
        shard_qkv = summed_rows(
            [(mixed_low.T, grad_queries), (mixed_t, grad_keys), (mixed_t, grad_values)]
        )
    grad_b_query = column_sum(grad_queries)
    grad_b_value = column_sum(grad_values)
    from_keys = dot_right_t(grad_keys_in, full_kv[:, :d_model]) + dot_right_t(
        grad_values, full_kv[:, d_model:]
    )
    to_other = jnp.where(is_text, from_keys[TEXT:], from_keys[:TEXT]).astype(bf16)
    from_other = swap(to_other)
    if fast:
        grad_queries = after(grad_queries, to_other)
    from_queries = dot_right_t(grad_queries, full_query)
    if fast:
        across_qkv = after(across_qkv, from_queries)
        own_qkv, sends_qkv = column_sends(held_qkv, across_qkv)
        arrived_qkv = column_arrivals(sends_qkv)
        from_other = after(from_other, *sends_qkv)
    grad_mixed = (
        grad_first
        + from_queries
        + jnp.where(is_text, from_keys[:TEXT], from_keys[TEXT:])
        + from_other.astype(f32)
    )
    grad_in, grad_conv_w, grad_conv_b = mix_pull(grad_mixed)

    table_rows = grad_tables[:, :3].reshape(6, 768)
    packed = jnp.concatenate(
        [
            grad_conv_w,
            grad_conv_b[None],
            grad_b_query,
            grad_b_value,
            small_one[2:3],
            small_one[0:2],
            small_two[2:3],
            small_two[0:2],
            grad_b_up.reshape(d_ff // d_model, d_model),
            table_rows,
            jnp.zeros((2, d_model), f32),
        ],
        axis=0,
    )
    if fast:
        arrived_rest = [after(part, packed) for part in arrived_rest]
        total_rest = column_total(own_rest, arrived_rest)
        far_rest = swap(total_rest)
        arrived_qkv = [after(part, total_rest) for part in arrived_qkv]
        total_qkv = column_total(own_qkv, arrived_qkv)
        far_qkv = swap(total_qkv)
    packed = sum_everywhere(packed)
    g_tables = packed[16:22].reshape(HEADS, 3, LANES)
    if fast:
        shard_down = total_down.astype(f32) + far_down.astype(f32)
        shard_qkv = total_qkv.astype(f32) + far_qkv.astype(f32)
        shard_rest = jnp.where(
            is_text,
            jnp.concatenate([total_rest, far_rest], axis=1),
            jnp.concatenate([far_rest, total_rest], axis=1),
        ).astype(f32)
    return (
        output_row[None, None],
        grad_in.astype(bf16)[None, None],
        packed[0:3],
        packed[3],
        shard_qkv[:, :d_model],
        packed[4],
        shard_qkv[:, d_model : 2 * d_model],
        shard_qkv[:, 2 * d_model :],
        packed[5],
        shard_rest[:, :d_model],
        packed[6],
        g_tables[:, 0, : table_pos.shape[1]],
        g_tables[:, 1, 64 : 64 + table_x.shape[1]],
        g_tables[:, 2, 64 : 64 + table_y.shape[1]],
        packed[7],
        packed[8],
        shard_rest[:, d_model:],
        packed[12:16].reshape(d_ff),
        shard_down,
        packed[9],
        packed[10],
        packed[11],
    )


def solution(mesh):
    rows = P("mod", "page", None, None)
    ids = P("page", None)
    cut = P("page", None)
    return jax.shard_map(
        local,
        mesh=mesh,
        in_specs=(
            rows, rows, ids, ids, ids, P(), P(), cut, P(), cut, cut, P(), cut,
            P(), P(), P(), P(), P(), P(), cut, P(), cut, P(), P(), P(),
        ),
        out_specs=(
            rows, rows, P(), P(), cut, P(), cut, cut, P(), cut, P(), P(), P(),
            P(), P(), P(), cut, P(), cut, P(), P(), P(),
        ),
        check_vma=False,
    )
```

```python
import functools

import jax
import jax.numpy as jnp
import numpy as np
from jax import lax
from jax.experimental import pallas as pl
from jax.experimental.pallas import tpu as pltpu
from jax.sharding import PartitionSpec as P

HEADS = 12
HEAD = 64
GRID = 8
PAGES = 8
POS_BINS = 64
BOX_BINS = 32
PATCH = 64
TEXT = 512
PAIRS = HEADS // 2
LANES = 2 * HEAD
WINDOW = 144
KEYS = WINDOW + PATCH

dilation = 2
small_cost = pl.CostEstimate(flops=1000, bytes_accessed=1000, transcendentals=0)
norm_eps = 1e-05
mask_fill = -1000000000.0
erfc_poly = (
    0.2367515965428487,
    0.24062179898991767,
    0.18865103029313968,
    0.2877518531132804,
    -0.1648672439458568,
    0.4765735350541787,
    -0.34041833366480423,
    0.07493571514857543,
)
bf16 = jnp.bfloat16
f32 = jnp.float32


def shifted(values, offset, fill_value):
    padding = jnp.full((abs(offset),) + values.shape[1:], fill_value, values.dtype)
    if offset > 0:
        return jnp.concatenate([values[offset:], padding], axis=0)
    return jnp.concatenate([padding, values[:offset]], axis=0)


def dilated_mix(inputs, page_ids, conv_weight, conv_bias):
    summed = inputs + conv_bias + conv_weight[1] * inputs
    for tap_index, offset in ((0, -dilation), (2, dilation)):
        moved_rows = shifted(inputs, offset, 0.0)
        moved_pages = shifted(page_ids, offset, -1)
        same_page = (moved_pages == page_ids)[:, None]
        summed = summed + conv_weight[tap_index] * jnp.where(same_page, moved_rows, 0.0)
    return summed


def bin_features(pos_bins, bins_x, bins_y):
    return jnp.concatenate(
        [
            jax.nn.one_hot(pos_bins, POS_BINS, dtype=bf16),
            jax.nn.one_hot(bins_x, BOX_BINS, dtype=bf16),
            jax.nn.one_hot(bins_y, BOX_BINS, dtype=bf16),
        ],
        axis=1,
    )


def token_ids(text_pages, text_x, text_y):
    text_index = jnp.arange(TEXT, dtype=jnp.int32)
    text_pos = text_index * POS_BINS // TEXT
    patch_pos = text_index % PATCH * POS_BINS // PATCH
    patch_page = text_index // PATCH
    patch_x = text_index % GRID * BOX_BINS // GRID
    patch_y = text_index // GRID % GRID * BOX_BINS // GRID
    page_ids = jnp.stack([text_pages, patch_page])
    pos_bins = jnp.stack([text_pos, patch_pos])
    bins_x = jnp.stack([text_x, patch_x])
    bins_y = jnp.stack([text_y, patch_y])
    return (page_ids, pos_bins, bins_x, bins_y)


def plain_dot(left_side, right_side):
    return jnp.dot(left_side, right_side, preferred_element_type=f32)


def dot_left_t(left_side, right_side):
    return lax.dot_general(
        left_side, right_side, (((0,), (0,)), ((), ())), preferred_element_type=f32
    )


def dot_right_t(left_side, right_side):
    return lax.dot_general(
        left_side, right_side, (((1,), (1,)), ((), ())), preferred_element_type=f32
    )


def column_sum(values):
    return jnp.sum(values, axis=0, keepdims=True, dtype=f32)


def iota(shape, axis):
    return lax.broadcasted_iota(jnp.int32, shape, axis)


def bias_block(table_rows):
    pos_part = pltpu.roll(
        jnp.broadcast_to(table_rows[0:1], (POS_BINS, LANES)), 65, 1, stride=1, stride_axis=0
    )
    x_part = pltpu.roll(
        jnp.broadcast_to(table_rows[1:2], (BOX_BINS, LANES)), 33, 1, stride=1, stride_axis=0
    )
    y_part = pltpu.roll(
        jnp.broadcast_to(table_rows[2:3], (BOX_BINS, LANES)), 65, 1, stride=1, stride_axis=0
    )
    lane = iota((POS_BINS, LANES), 1)
    pos_part = jnp.where(lane < POS_BINS, pos_part, 0.0)
    lane = iota((BOX_BINS, LANES), 1)
    x_part = jnp.where((lane >= 64) & (lane < 96), x_part, 0.0)
    y_part = jnp.where(lane >= 96, y_part, 0.0)
    return jnp.concatenate([pos_part, x_part, y_part], axis=0).astype(bf16)


def diagonal_sums(grad_block):
    lane = iota((POS_BINS, LANES), 1)
    pos_part = jnp.where(lane < POS_BINS, grad_block[:64], 0.0)
    lane = iota((BOX_BINS, LANES), 1)
    x_part = jnp.where((lane >= 64) & (lane < 96), grad_block[64:96], 0.0)
    y_part = jnp.where(lane >= 96, grad_block[96:], 0.0)
    pos_part = pltpu.roll(pos_part, 0, 1, stride=1, stride_axis=0)
    x_part = pltpu.roll(x_part, 0, 1, stride=1, stride_axis=0)
    y_part = pltpu.roll(y_part, 96, 1, stride=1, stride_axis=0)
    rows = [jnp.sum(part, axis=0, keepdims=True) for part in (pos_part, x_part, y_part)]
    return jnp.concatenate(rows + [jnp.zeros((5, LANES), f32)], axis=0)


def stacked_heads(rows, low_lane):
    zero = jnp.zeros_like(rows)
    return jnp.concatenate(
        [jnp.where(low_lane, rows, zero), jnp.where(low_lane, zero, rows)], axis=0
    )


def page_operands(page, bounds, q_ref, k_ref, feat_ref, lookup):
    own_at = pl.multiple_of(bounds[page], 16)
    key_at = pl.multiple_of(bounds[3 * PAGES + page], 16)
    low_lane = iota((WINDOW, LANES), 1) < HEAD
    queries = stacked_heads(q_ref[pl.ds(own_at, WINDOW), :], low_lane)
    rel = jnp.concatenate(
        [lookup[pl.ds(own_at, WINDOW), :LANES], lookup[pl.ds(own_at, WINDOW), LANES:]], axis=0
    )
    query_side = jnp.concatenate([rel, queries], axis=1)
    patch_rows = pl.ds(TEXT + PATCH * page, PATCH)
    text_rows = pl.ds(key_at, WINDOW)
    key_side = jnp.concatenate(
        [
            jnp.concatenate([feat_ref[text_rows, :], k_ref[text_rows, :]], axis=1),
            jnp.concatenate([feat_ref[patch_rows, :], k_ref[patch_rows, :]], axis=1),
        ],
        axis=0,
    )
    own_row = iota((WINDOW, LANES), 0) + own_at
    own_ok = (own_row >= bounds[PAGES + page]) & (own_row < bounds[2 * PAGES + page])
    return own_at, key_at, low_lane, own_ok, queries, query_side, key_side, text_rows, patch_rows


def attend_kernel(bounds, q_ref, k_ref, v_ref, feat_ref, own_feat_ref, table_ref, context_ref, lookup):
    blocks = jnp.concatenate([bias_block(table_ref[0]), bias_block(table_ref[1])], axis=1)
    lookup[...] = jnp.dot(own_feat_ref[...], blocks, preferred_element_type=f32).astype(bf16)
    for page in range(PAGES):
        own_at, key_at, low_lane, own_ok, queries, query_side, key_side, text_rows, patch_rows = (
            page_operands(page, bounds, q_ref, k_ref, feat_ref, lookup)
        )
        scores = dot_right_t(query_side, key_side)
        column = iota((1, KEYS), 1)
        key_row = column + key_at
        key_ok = (column >= WINDOW) | (
            (key_row >= bounds[4 * PAGES + page]) & (key_row < bounds[5 * PAGES + page])
        )
        scores = jnp.where(key_ok, scores, mask_fill)
        row_max = jnp.max(scores, axis=1, keepdims=True)
        weights = jnp.exp(scores - row_max)
        total = jnp.sum(weights, axis=1, keepdims=True)
        prob = (weights * (1.0 / total)).astype(bf16)
        values = jnp.concatenate([v_ref[text_rows, :], v_ref[patch_rows, :]], axis=0)
        mixed = jnp.dot(prob, values, preferred_element_type=f32)
        picked = jnp.where(low_lane, mixed[:WINDOW], mixed[WINDOW:])
        before = context_ref[pl.ds(own_at, WINDOW), :].astype(f32)
        context_ref[pl.ds(own_at, WINDOW), :] = jnp.where(own_ok, picked, before).astype(bf16)


def attend_back_kernel(
    bounds,
    q_ref,
    k_ref,
    v_ref,
    grad_ref,
    feat_ref,
    own_feat_ref,
    flip_feat_ref,
    table_ref,
    grad_q_ref,
    grad_k_ref,
    grad_v_ref,
    grad_table_ref,
    lookup,
    grad_lookup,
):
    blocks = jnp.concatenate([bias_block(table_ref[0]), bias_block(table_ref[1])], axis=1)
    lookup[...] = jnp.dot(own_feat_ref[...], blocks, preferred_element_type=f32).astype(bf16)
    for page in range(PAGES):
        own_at, key_at, low_lane, own_ok, queries, query_side, key_side, text_rows, patch_rows = (
            page_operands(page, bounds, q_ref, k_ref, feat_ref, lookup)
        )
        scores = dot_right_t(key_side, query_side)
        row = iota((KEYS, 1), 0)
        key_row = row + key_at
        key_in = (key_row >= bounds[4 * PAGES + page]) & (key_row < bounds[5 * PAGES + page])
        scores = jnp.where((row >= WINDOW) | key_in, scores, mask_fill)
        col_max = jnp.max(scores, axis=0, keepdims=True)
        weights = jnp.exp(scores - col_max)
        total = jnp.sum(weights, axis=0, keepdims=True)
        prob = weights * (1.0 / total)
        grad_rows = grad_ref[pl.ds(own_at, WINDOW), :]
        grad_rows = jnp.where(own_ok, grad_rows, jnp.zeros_like(grad_rows))
        grads = stacked_heads(grad_rows, low_lane)
        values = jnp.concatenate([v_ref[text_rows, :], v_ref[patch_rows, :]], axis=0)
        grad_prob = dot_right_t(values, grads)
        inner = jnp.sum(prob * grad_prob, axis=0, keepdims=True)
        grad_scores = (prob * (grad_prob - inner)).astype(bf16)
        grad_v = jnp.dot(prob.astype(bf16), grads, preferred_element_type=f32)
        grad_k = jnp.dot(grad_scores, queries, preferred_element_type=f32)
        back = dot_left_t(grad_scores, key_side)
        grad_q = jnp.where(low_lane, back[:WINDOW, LANES:], back[WINDOW:, LANES:]) * 0.125
        own_rows = pl.ds(own_at, WINDOW)
        before = grad_q_ref[own_rows, :].astype(f32)
        grad_q_ref[own_rows, :] = jnp.where(own_ok, grad_q, before).astype(bf16)
        grad_lookup[own_rows, :LANES] = jnp.where(
            own_ok, back[:WINDOW, :LANES], grad_lookup[own_rows, :LANES]
        )
        grad_lookup[own_rows, LANES:] = jnp.where(
            own_ok, back[WINDOW:, :LANES], grad_lookup[own_rows, LANES:]
        )
        wide_row = iota((WINDOW, LANES), 0) + key_at
        text_ok = (wide_row >= bounds[4 * PAGES + page]) & (wide_row < bounds[5 * PAGES + page])
        for grad, ref in ((grad_k, grad_k_ref), (grad_v, grad_v_ref)):
            before = ref[text_rows, :].astype(f32)
            ref[text_rows, :] = jnp.where(text_ok, grad[:WINDOW], before).astype(bf16)
            ref[patch_rows, :] = grad[WINDOW:].astype(bf16)
    grad_high = grad_lookup[...].astype(bf16)
    grad_rest = (grad_lookup[...] - grad_high.astype(f32)).astype(bf16)
    flip = flip_feat_ref[...]
    grad_block = dot_left_t(flip, grad_high) + dot_left_t(flip, grad_rest)
    grad_table_ref[0] = diagonal_sums(grad_block[:, :LANES])
    grad_table_ref[1] = diagonal_sums(grad_block[:, LANES:])


def column_spec(rows, first=0):
    return pl.BlockSpec((rows, LANES), lambda pair, bounds: (0, pair + first))


def tables_spec(first=0):
    return pl.BlockSpec((2, 8, LANES), lambda pair, bounds: (pair + first, 0, 0))


def whole_spec(rows):
    return pl.BlockSpec((rows, LANES), lambda pair, bounds: (0, 0))


def attend(bounds, queries, keys_values, features, own_features, tables):
    return pl.pallas_call(
        attend_kernel,
        grid_spec=pltpu.PrefetchScalarGridSpec(
            num_scalar_prefetch=1,
            grid=(PAIRS,),
            in_specs=[
                column_spec(TEXT),
                column_spec(2 * TEXT),
                column_spec(2 * TEXT, PAIRS),
                whole_spec(2 * TEXT),
                whole_spec(TEXT),
                tables_spec(),
            ],
            out_specs=column_spec(TEXT),
            scratch_shapes=[pltpu.VMEM((TEXT, 2 * LANES), bf16)],
        ),
        out_shape=jax.ShapeDtypeStruct((TEXT, HEADS * HEAD), bf16),
        cost_estimate=small_cost,
        name="attend",
    )(bounds, queries, keys_values, keys_values, features, own_features, tables)


def attend_back(
    bounds, queries, keys_values, grad_context, features, own_features, flip, tables, first, count
):
    return pl.pallas_call(
        attend_back_kernel,
        grid_spec=pltpu.PrefetchScalarGridSpec(
            num_scalar_prefetch=1,
            grid=(count,),
            in_specs=[
                column_spec(TEXT, first),
                column_spec(2 * TEXT, first),
                column_spec(2 * TEXT, PAIRS + first),
                column_spec(TEXT, first),
                whole_spec(2 * TEXT),
                whole_spec(TEXT),
                whole_spec(TEXT),
                tables_spec(first),
            ],
            out_specs=[
                column_spec(TEXT),
                column_spec(2 * TEXT),
                column_spec(2 * TEXT),
                tables_spec(),
            ],
            scratch_shapes=[
                pltpu.VMEM((TEXT, 2 * LANES), bf16),
                pltpu.VMEM((TEXT, 2 * LANES), f32),
            ],
        ),
        out_shape=[
            jax.ShapeDtypeStruct((TEXT, count * LANES), bf16),
            jax.ShapeDtypeStruct((2 * TEXT, count * LANES), bf16),
            jax.ShapeDtypeStruct((2 * TEXT, count * LANES), bf16),
            jax.ShapeDtypeStruct((2 * count, 8, LANES), f32),
        ],
        cost_estimate=small_cost,
        name="attend_back",
    )(
        bounds,
        queries,
        keys_values,
        keys_values,
        grad_context,
        features,
        own_features,
        flip,
        tables,
    )


def exchange(values, mask):
    count = lax.axis_size("page")
    return lax.ppermute(values, "page", [(i, i ^ mask) for i in range(count)])


def after(value, *earlier):
    return lax.optimization_barrier((value, *earlier))[0]


def slot_mask(slot):
    return (slot & 3) * 4 + (slot >> 2) * 2


def place_kernel(groups, place, *refs):
    for copy in start_rows(place, groups, refs[:-2], refs[-2], refs[-1]):
        copy.wait()


def place_rows(place, groups, pieces, shape):
    return pl.pallas_call(
        functools.partial(place_kernel, groups),
        grid_spec=pltpu.PrefetchScalarGridSpec(
            num_scalar_prefetch=1,
            grid=(),
            in_specs=any_specs(len(pieces)),
            out_specs=pl.BlockSpec(memory_space=pltpu.VMEM),
            scratch_shapes=[pltpu.SemaphoreType.DMA((32,))],
        ),
        out_shape=jax.ShapeDtypeStruct(shape, bf16),
        cost_estimate=small_cost,
        name="place_rows",
    )(place, *pieces)


def column_parts(shard):
    return [shard] + [exchange(shard, 4 * step) for step in (1, 2, 3)]


def half_pieces(column):
    eight = jnp.concatenate([column, exchange(column, 2)])
    far = swap(eight)
    return [eight, exchange(eight, 1), far, exchange(far, 1)]


def row_pieces(column, across):
    return [column, exchange(column, 1), across, exchange(across, 1)]


def column_of(shard):
    return jnp.stack(column_parts(shard))


def start_rows(place, groups, refs, full, sems, first=0):
    copies = []
    for kind, column in groups:
        if kind == "full":
            piece, *refs = refs
            width = piece.shape[1]
            target = full.at[:, pl.ds(column, width)]
            copies.append(pltpu.make_async_copy(piece, target, sems.at[first + len(copies)]))
            continue
        pieces, refs = refs[:4], refs[4:]
        _, rows, width = pieces[0].shape
        for index in range(32 if kind == "halves" else 16):
            at = column
            if kind == "halves":
                source, slot = index >> 3, index & 7
                mask = slot_mask(slot) + (source & 1)
                at = pl.multiple_of(column + (place[1] ^ (source >> 1)) * width, 128)
            else:
                source, slot = index & 3, index >> 2
                mask = slot * 4 + source
            row = pl.multiple_of((place[0] ^ mask) * rows, 16)
            copies.append(
                pltpu.make_async_copy(
                    pieces[source].at[slot],
                    full.at[pl.ds(row, rows), pl.ds(at, width)],
                    sems.at[first + len(copies)],
                )
            )
    for copy in copies:
        copy.start()
    return copies


def gelu_parts(values):
    size = jnp.abs(values)
    t = 1.0 / (1.0 + (0.42 * 0.7071067811865476) * size)
    poly = jnp.full_like(t, erfc_poly[-1])
    for coefficient in erfc_poly[-2::-1]:
        poly = poly * t + coefficient
    bell = jnp.exp(-0.5 * values * values)
    tail = (0.5 * t) * (poly * bell)
    cdf = jnp.where(values >= 0.0, 1.0 - tail, tail)
    return values * cdf, cdf + (values * 0.3989422804014327) * bell


def normalized(values):
    centered = values - jnp.mean(values, axis=1, keepdims=True)
    variance = jnp.mean(centered * centered, axis=1, keepdims=True)
    scale = lax.rsqrt(variance + norm_eps)
    return centered * scale, scale


def norm_back(grads, unit, scale, gain):
    scaled = grads * gain
    mean = jnp.mean(scaled, axis=1, keepdims=True)
    inner = jnp.mean(scaled * unit, axis=1, keepdims=True)
    return scale * (scaled - mean - unit * inner)


def up_kernel(groups, place, context_ref, mixed_ref, vec_ref, bias_ref, *refs):
    *pieces, unit_ref, scale_ref, low_ref, low_t_ref, active_ref, active_t_ref, slope_ref = refs[:-4]
    weight, hidden, low, sems = refs[-4:]
    step = pl.program_id(0)
    tiles = pl.num_programs(0) - 1
    width = context_ref.shape[1]
    tile = active_ref.shape[1]

    @pl.when(step == 0)
    def _():
        for copy in start_rows(place, groups, pieces, weight, sems):
            copy.wait()
        branch = jnp.dot(context_ref[...], weight[:, :width], preferred_element_type=f32)
        unit, scale = normalized(mixed_ref[...] + branch + vec_ref[0:1])
        unit_ref[...] = unit
        scale_ref[...] = jnp.broadcast_to(scale, scale_ref.shape)
        normed = (unit * vec_ref[1:2] + vec_ref[2:3]).astype(bf16)
        low[...] = normed
        low_ref[...] = normed
        low_t_ref[...] = normed.T

    def product():
        at = pl.multiple_of(width + step * tile, 128)
        return jnp.dot(low[...], weight[:, pl.ds(at, tile)], preferred_element_type=f32)

    def activate():
        active, slope = gelu_parts(hidden[(step + 1) % 2] + bias_ref[...])
        active = active.astype(bf16)
        active_ref[...] = active
        active_t_ref[...] = active.T
        slope_ref[...] = slope

    @pl.when(step == 0)
    def _():
        hidden[step % 2] = product()

    @pl.when((step > 0) & (step < tiles))
    def _():
        hidden[step % 2] = product()
        activate()

    @pl.when(step == tiles)
    def _():
        activate()


def any_specs(count):
    return [pl.BlockSpec(memory_space=pl.ANY)] * count


def up_forward(place, context, mixed, vectors, bias_up, groups, pieces):
    tokens, width = mixed.shape
    hidden_width = bias_up.shape[1]
    tile = 512
    whole = lambda step, place: (0, 0)
    last = lambda step, place: (0, jnp.maximum(step - 1, 0))
    last_t = lambda step, place: (jnp.maximum(step - 1, 0), 0)
    return pl.pallas_call(
        functools.partial(up_kernel, groups),
        grid_spec=pltpu.PrefetchScalarGridSpec(
            num_scalar_prefetch=1,
            grid=(hidden_width // tile + 1,),
            in_specs=[
                pl.BlockSpec((tokens, width), whole),
                pl.BlockSpec((tokens, width), whole),
                pl.BlockSpec(vectors.shape, whole),
                pl.BlockSpec((1, tile), last),
            ]
            + any_specs(len(pieces)),
            out_specs=[
                pl.BlockSpec((tokens, width), whole),
                pl.BlockSpec((tokens, 128), whole),
                pl.BlockSpec((tokens, width), whole),
                pl.BlockSpec((width, tokens), whole),
                pl.BlockSpec((tokens, tile), last),
                pl.BlockSpec((tile, tokens), last_t),
                pl.BlockSpec((tokens, tile), last),
            ],
            scratch_shapes=[
                pltpu.VMEM((width, width + hidden_width), bf16),
                pltpu.VMEM((2, tokens, tile), f32),
                pltpu.VMEM((tokens, width), bf16),
                pltpu.SemaphoreType.DMA((48,)),
            ],
        ),
        out_shape=[
            jax.ShapeDtypeStruct((tokens, width), f32),
            jax.ShapeDtypeStruct((tokens, 128), f32),
            jax.ShapeDtypeStruct((tokens, width), bf16),
            jax.ShapeDtypeStruct((width, tokens), bf16),
            jax.ShapeDtypeStruct((tokens, hidden_width), bf16),
            jax.ShapeDtypeStruct((hidden_width, tokens), bf16),
            jax.ShapeDtypeStruct((tokens, hidden_width), f32),
        ],
        cost_estimate=small_cost,
        name="up_forward",
    )(place, context, mixed, vectors, bias_up, *pieces)


def down_kernel(groups, place, active_ref, unit_ref, vec_ref, grad_ref, *refs):
    *pieces, out_ref, sum_ref, low_ref, small_ref = refs[:-2]
    weight, sems = refs[-2:]
    for copy in start_rows(place, groups, pieces, weight, sems):
        copy.wait()
    tokens, width = unit_ref.shape
    half = tokens // 2
    smalls = [jnp.zeros((1, width), f32)] * 3
    for part in range(2):
        rows = pl.ds(part * half, half)
        ffn = jnp.dot(active_ref[rows, :], weight[...], preferred_element_type=f32)
        normed = unit_ref[rows, :] * vec_ref[1:2] + vec_ref[2:3]
        unit, scale = normalized(normed + ffn + vec_ref[3:4])
        out_ref[rows, :] = (unit * vec_ref[4:5] + vec_ref[5:6]).astype(bf16)
        grads = grad_ref[rows, :].astype(f32)
        total = norm_back(grads, unit, scale, vec_ref[4:5])
        low = total.astype(bf16)
        sum_ref[rows, :] = total
        low_ref[rows, :] = low
        for index, term in enumerate((grads * unit, grads, low.astype(f32))):
            smalls[index] = smalls[index] + jnp.sum(term, axis=0, keepdims=True)
    small_ref[...] = jnp.concatenate(smalls + [jnp.zeros((5, width), f32)], axis=0)


def down_forward(place, active, unit, vectors, grads, groups, pieces):
    tokens, width = unit.shape
    hidden_width = active.shape[1]
    vmem = pl.BlockSpec(memory_space=pltpu.VMEM)
    return pl.pallas_call(
        functools.partial(down_kernel, groups),
        grid_spec=pltpu.PrefetchScalarGridSpec(
            num_scalar_prefetch=1,
            grid=(),
            in_specs=[vmem] * 4 + any_specs(len(pieces)),
            out_specs=[vmem] * 4,
            scratch_shapes=[
                pltpu.VMEM((hidden_width, width), bf16),
                pltpu.SemaphoreType.DMA((16,)),
            ],
        ),
        out_shape=[
            jax.ShapeDtypeStruct((tokens, width), bf16),
            jax.ShapeDtypeStruct((tokens, width), f32),
            jax.ShapeDtypeStruct((tokens, width), bf16),
            jax.ShapeDtypeStruct((8, width), f32),
        ],
        cost_estimate=small_cost,
        name="down_forward",
    )(place, active, unit, vectors, grads, *pieces)


def ffn_back_kernel(groups, groups_down, count, place, low_ref, slope_ref, sum_ref, unit_ref, scale_ref, vec_ref, *refs):
    rest, down = refs[: count[0]], refs[count[0] : sum(count)]
    hidden_ref, bias_ref, first_ref, branch_ref, context_ref, small_ref = refs[sum(count) : -4]
    weight, weight_down, total, sems = refs[-4:]
    step = pl.program_id(0)
    tokens, width = unit_ref.shape
    tile = slope_ref.shape[1]
    half = tokens // 2

    @pl.when(step == 0)
    def _():
        copies = start_rows(place, groups_down, down, weight_down, sems)
        copies += start_rows(place, groups, rest, weight, sems, 16)
        total[...] = sum_ref[...]
        for copy in copies:
            copy.wait()

    rows_down = weight_down[pl.ds(pl.multiple_of(step * tile, 128), tile), :]
    columns = weight[:, pl.ds(pl.multiple_of(width + step * tile, 128), tile)]
    bias = jnp.zeros((1, tile), f32)
    for part in range(2):
        rows = pl.ds(part * half, half)
        grads = (dot_right_t(low_ref[rows, :], rows_down) * slope_ref[rows, :]).astype(bf16)
        hidden_ref[rows, :] = grads
        bias = bias + jnp.sum(grads.astype(f32), axis=0, keepdims=True)
        total[rows, :] += dot_right_t(grads, columns)
    bias_ref[...] = bias

    @pl.when(step == pl.num_programs(0) - 1)
    def _():
        grads = total[...]
        unit = unit_ref[...]
        first = norm_back(grads, unit, scale_ref[:, 0:1], vec_ref[1:2])
        branch = first.astype(bf16)
        first_ref[...] = first
        branch_ref[...] = branch
        context_ref[...] = dot_right_t(branch, weight[:, :width]).astype(bf16)
        smalls = [
            jnp.sum(term, axis=0, keepdims=True)
            for term in (grads * unit, grads, branch.astype(f32))
        ]
        small_ref[...] = jnp.concatenate(smalls + [jnp.zeros((5, width), f32)], axis=0)


def ffn_back(
    place, low, slope, total, unit, scale, vectors, groups, pieces_rest, groups_down, pieces_down
):
    tokens, width = unit.shape
    hidden_width = slope.shape[1]
    tile = 512
    count = (len(pieces_rest), len(pieces_down))
    whole = lambda step, place: (0, 0)
    column = lambda step, place: (0, step)
    return pl.pallas_call(
        functools.partial(ffn_back_kernel, groups, groups_down, count),
        grid_spec=pltpu.PrefetchScalarGridSpec(
            num_scalar_prefetch=1,
            grid=(hidden_width // tile,),
            in_specs=[
                pl.BlockSpec((tokens, width), whole),
                pl.BlockSpec((tokens, tile), column),
                pl.BlockSpec((tokens, width), whole),
                pl.BlockSpec((tokens, width), whole),
                pl.BlockSpec((tokens, 128), whole),
                pl.BlockSpec(vectors.shape, whole),
            ]
            + any_specs(sum(count)),
            out_specs=[
                pl.BlockSpec((tokens, tile), column),
                pl.BlockSpec((1, tile), column),
                pl.BlockSpec((tokens, width), whole),
                pl.BlockSpec((tokens, width), whole),
                pl.BlockSpec((tokens, width), whole),
                pl.BlockSpec((8, width), whole),
            ],
            scratch_shapes=[
                pltpu.VMEM((width, width + hidden_width), bf16),
                pltpu.VMEM((hidden_width, width), bf16),
                pltpu.VMEM((tokens, width), f32),
                pltpu.SemaphoreType.DMA((64,)),
            ],
        ),
        out_shape=[
            jax.ShapeDtypeStruct((tokens, hidden_width), bf16),
            jax.ShapeDtypeStruct((1, hidden_width), f32),
            jax.ShapeDtypeStruct((tokens, width), f32),
            jax.ShapeDtypeStruct((tokens, width), bf16),
            jax.ShapeDtypeStruct((tokens, width), bf16),
            jax.ShapeDtypeStruct((8, width), f32),
        ],
        cost_estimate=small_cost,
        name="ffn_back",
    )(place, low, slope, total, unit, scale, vectors, *pieces_rest, *pieces_down)


def grad_rows_kernel(place, *refs):
    *inputs, h_ref, keep_ref, send_ref = refs
    rows = keep_ref.shape[1]
    both = jnp.concatenate([ref[0] for ref in inputs], axis=0)
    product = jnp.dot(both, h_ref[...], preferred_element_type=f32).astype(bf16)
    for index in range(2):
        keep_ref[index] = product[index * rows : (index + 1) * rows]
        send_ref[index] = product[(index + 2) * rows : (index + 3) * rows]


def grad_by_rows(inputs_t, grads, place):
    width, tokens = inputs_t.shape
    columns = grads.shape[1]
    rows = width // 16
    inputs_t = inputs_t.reshape(16, rows, tokens)
    half = jax.ShapeDtypeStruct((8, rows, columns), bf16)
    out = pl.BlockSpec((2, rows, columns), lambda step, place: (step, 0, 0))

    def input_spec(index):
        return pl.BlockSpec(
            (1, rows, tokens),
            lambda step, place: (
                place[0] ^ (slot_mask(2 * step + (index & 1)) + (index >> 1)),
                0,
                0,
            ),
        )

    return pl.pallas_call(
        grad_rows_kernel,
        grid_spec=pltpu.PrefetchScalarGridSpec(
            num_scalar_prefetch=1,
            grid=(4,),
            in_specs=[input_spec(index) for index in range(4)]
            + [pl.BlockSpec((tokens, columns), lambda step, place: (0, 0))],
            out_specs=[out, out],
        ),
        out_shape=[half, half],
        cost_estimate=small_cost,
        name="grad_rows",
    )(place, *[inputs_t] * 4, grads)


def grad_columns_kernel(parts, place, *refs):
    count = len(parts)
    ins, keep_ref, send_ref, scratch = (
        refs[: 2 * count],
        refs[2 * count],
        refs[2 * count + 1],
        refs[2 * count + 2 :],
    )
    rows, tile = keep_ref.shape[1], keep_ref.shape[2]
    step = pl.program_id(0)
    first = 0
    for index, steps in enumerate(parts):
        x_ref, h_ref, ordered = ins[2 * index], ins[2 * index + 1], scratch[index]

        @pl.when(step == first)
        def _():
            for slot in range(16):
                mask = slot_mask(slot & 7) + (slot >> 3)
                at = pl.multiple_of((place[0] ^ mask) * rows, 16)
                ordered[pl.ds(slot * rows, rows), :] = x_ref[pl.ds(at, rows), :]

        @pl.when((step >= first) & (step < first + steps))
        def _():
            product = jnp.dot(ordered[...], h_ref[...], preferred_element_type=f32).astype(bf16)
            keep_ref[...] = product[: 8 * rows].reshape(8, rows, tile)
            send_ref[...] = product[8 * rows :].reshape(8, rows, tile)

        first = first + steps


def grad_by_columns(pairs, place, tile):
    width = pairs[0][0].shape[0]
    rows = width // 16
    parts = tuple(sum(grad.shape[1] for grad in grads) // tile for _, _, *grads in pairs)
    steps = sum(parts)
    specs = []
    operands = []
    scratch = []
    first = 0
    for (inputs_t, own, *grads), count in zip(pairs, parts):
        tokens = grads[0].shape[0]
        block = (lambda step, place: (0, place[1])) if own else (lambda step, place: (0, 0))
        specs.append(pl.BlockSpec((width, tokens), block))

        def column(step, place, first=first, count=count):
            return (0, jnp.clip(step - first, 0, count - 1))

        specs.append(pl.BlockSpec((tokens, tile), column))
        operands += [inputs_t, *grads]
        scratch.append(pltpu.VMEM((width, tokens), bf16))
        first = first + count
    half = jax.ShapeDtypeStruct((8, rows, steps * tile), bf16)
    return pl.pallas_call(
        functools.partial(grad_columns_kernel, parts),
        grid_spec=pltpu.PrefetchScalarGridSpec(
            num_scalar_prefetch=1,
            grid=(steps,),
            in_specs=specs,
            out_specs=[pl.BlockSpec((8, rows, tile), lambda step, place: (0, 0, step))] * 2,
            scratch_shapes=scratch,
        ),
        out_shape=[half, half],
        cost_estimate=small_cost,
        name="grad_columns",
    )(place, *operands)


def key_back_kernel(place, gk_ref, gv_ref, wk_ref, wv_ref, out_ref):
    total = dot_right_t(gk_ref[...], wk_ref[...]) + dot_right_t(gv_ref[...], wv_ref[...])
    out_ref[...] = total.astype(out_ref.dtype)


def own_back_kernel(place, first_ref, gq_ref, gk_ref, gv_ref, wq_ref, wk_ref, wv_ref, out_ref):
    total = dot_right_t(gk_ref[...], wk_ref[...]) + dot_right_t(gv_ref[...], wv_ref[...])
    out_ref[...] = first_ref[...] + total + dot_right_t(gq_ref[...], wq_ref[...])


def input_back(place, weights, grad_keys, grad_values, others):
    width = weights.shape[0]
    tokens = grad_keys.shape[0] // 2
    whole = pl.BlockSpec((tokens, width), lambda step, place: (0, 0))
    row = lambda step, place: ((place[1] if others else 1 - place[1]), 0)
    if others:
        kernel, leading, first, dtype = own_back_kernel, [whole, whole], 0, f32
    else:
        kernel, leading, first, dtype = key_back_kernel, [], 1, bf16
    operands = list(others) + [grad_keys, grad_values] + [weights] * (3 - first)
    specs = [pl.BlockSpec((tokens, width), row)] * 2
    for block in range(first, 3):
        specs.append(pl.BlockSpec((width, width), lambda step, place, block=block: (0, block)))
    return pl.pallas_call(
        kernel,
        grid_spec=pltpu.PrefetchScalarGridSpec(
            num_scalar_prefetch=1, grid=(1,), in_specs=leading + specs, out_specs=whole
        ),
        out_shape=jax.ShapeDtypeStruct((tokens, width), dtype),
        cost_estimate=small_cost,
        name="input_back",
    )(place, *operands)


def first_half_kernel(place, keep_near, part_near, keep_far, part_far, held_ref, out_ref):
    held_ref[...] = keep_near[...].astype(f32) + part_near[...].astype(f32)
    out_ref[...] = (keep_far[...].astype(f32) + part_far[...].astype(f32)).astype(bf16)


def halve_call(place, keep, partner, specs, half_shape, steps):
    near, far, out = specs
    return pl.pallas_call(
        first_half_kernel,
        grid_spec=pltpu.PrefetchScalarGridSpec(
            num_scalar_prefetch=1,
            grid=(steps,),
            in_specs=[near, near, far, far],
            out_specs=[out, out],
        ),
        out_shape=[
            jax.ShapeDtypeStruct(half_shape, f32),
            jax.ShapeDtypeStruct(half_shape, bf16),
        ],
        cost_estimate=small_cost,
        name="halve",
    )(place, keep, partner, keep, partner)


def halve_across(place, keep, partner):
    _, rows, width = keep.shape
    near = pl.BlockSpec((1, rows, width), lambda step, place: (step, 0, 0))
    far = pl.BlockSpec((1, rows, width), lambda step, place: (step + 4, 0, 0))
    return halve_call(place, keep, partner, (near, far, near), (4, rows, width), 4)


def halve_plane(place, keep, partner):
    _, rows, width = keep.shape
    block = (2, rows, width // 2)
    near = pl.BlockSpec(block, lambda step, place: (step, 0, place[1]))
    far = pl.BlockSpec(block, lambda step, place: (step, 0, 1 - place[1]))
    out = pl.BlockSpec(block, lambda step, place: (step, 0, 0))
    return halve_call(place, keep, partner, (near, far, out), (8, rows, width // 2), 4)


def column_kernel(held_ref, across_ref, own_ref, *sends):
    own_ref[...] = held_ref[0] + across_ref[0].astype(f32)
    for step, send in enumerate(sends, 1):
        send[...] = (held_ref[step] + across_ref[step].astype(f32)).astype(bf16)


def column_sends(held, across):
    _, rows, width = held.shape
    tile = 384
    out = pl.BlockSpec((rows, tile), lambda step: (0, step))
    block = pl.BlockSpec((4, rows, tile), lambda step: (0, 0, step))
    own, *sends = pl.pallas_call(
        column_kernel,
        grid=(width // tile,),
        in_specs=[block, block],
        out_specs=[out] * 4,
        out_shape=[jax.ShapeDtypeStruct((rows, width), f32)]
        + [jax.ShapeDtypeStruct((rows, width), bf16)] * 3,
        cost_estimate=small_cost,
        name="column_sends",
    )(held, across)
    return own, sends


def column_arrivals(sends):
    return [exchange(send, 4 * step) for step, send in enumerate(sends, 1)]


def column_total(own, arrived):
    total = own
    for part in arrived:
        total = total + part.astype(f32)
    return total.astype(bf16)


def half_columns(values, first):
    half = values.shape[-1] // 2
    return jnp.where(first, values[..., :half], values[..., half:])


def summed_rows(pairs):
    grads = jnp.concatenate([plain_dot(*pair).astype(bf16) for pair in pairs], axis=1)
    shard = lax.psum_scatter(grads, "page", scatter_dimension=0, tiled=True)
    return shard.astype(f32) + swap(shard).astype(f32)


def page_bounds(segments, is_text):
    pages = jnp.arange(PAGES, dtype=jnp.int32)
    low = jnp.sum(segments[None, :] < pages[:, None], axis=1, dtype=jnp.int32)
    high = jnp.sum(segments[None, :] <= pages[:, None], axis=1, dtype=jnp.int32)
    own_low = jnp.where(is_text, low, pages * PATCH)
    own_high = jnp.where(is_text, high, (pages + 1) * PATCH)

    def aligned(start):
        return jnp.minimum(start // 16 * 16, TEXT - WINDOW)

    return jnp.concatenate([aligned(own_low), own_low, own_high, aligned(low), low, high])


def sum_everywhere(values):
    count = lax.axis_size("page")
    if count & (count - 1):
        values = lax.psum(values, "page")
    else:
        step = 1
        while step < count:
            values = values + lax.ppermute(values, "page", [(i, i ^ step) for i in range(count)])
            step = step * 2
    return values + swap(values)


def swap(values):
    return lax.ppermute(values, "mod", [(0, 1), (1, 0)])


def local(
    states,
    cotangent,
    segments,
    box_x,
    box_y,
    conv_weight,
    conv_bias,
    w_query,
    b_query,
    w_key,
    w_value,
    b_value,
    w_out,
    b_out,
    table_pos,
    table_x,
    table_y,
    gain_one,
    bias_one,
    w_up,
    b_up,
    w_down,
    b_down,
    gain_two,
    bias_two,
):
    is_text = lax.axis_index("mod") == 0
    d_model = states.shape[3]
    own_low = states[0, 0]
    rows_each = w_query.shape[0]
    d_ff = w_up.shape[1]
    fast = lax.axis_size("page") == 16 and rows_each % 16 == 0 and w_down.shape[0] % 16 == 0
    place = jnp.stack([lax.axis_index("page"), lax.axis_index("mod")]).astype(jnp.int32)
    pack_qkv = jnp.concatenate([w_query, w_key, w_value], axis=1)
    pack_rest = jnp.concatenate([w_out, w_up], axis=1)
    other_low = swap(own_low)
    if fast:
        split = (pack_rest.shape[1] // 2 + 127) // 256 * 256
        column_qkv = column_of(half_columns(pack_qkv, is_text))
        parts_near = column_parts(after(half_columns(pack_rest[:, :split], is_text), column_qkv))
        pieces_qkv = half_pieces(column_qkv)
        column_near = jnp.stack([after(part, pieces_qkv[0]) for part in parts_near])
        parts_far = column_parts(after(pack_rest[:, split:], column_near))
        pieces_near = half_pieces(column_near)
        pieces_qkv[2] = after(pieces_qkv[2], pieces_near[0])
        pieces_qkv[3] = exchange(pieces_qkv[2], 1)
        groups_qkv = (("halves", 0),)
    else:
        groups_qkv = (("full", 0),)
        pieces_qkv = [lax.all_gather(pack_qkv, "page", axis=0, tiled=True)]

    page_ids, pos_bins, bins_x, bins_y = token_ids(segments[0], box_x[0], box_y[0])
    bounds = page_bounds(segments[0], is_text)
    own_pages = jnp.where(is_text, page_ids[0], page_ids[1])
    features = bin_features(pos_bins.reshape(-1), bins_x.reshape(-1), bins_y.reshape(-1))
    flipped = bin_features(
        POS_BINS - 1 - pos_bins.reshape(-1),
        BOX_BINS - 1 - bins_x.reshape(-1),
        BOX_BINS - 1 - bins_y.reshape(-1),
    )
    own_feats = jnp.where(is_text, features[:TEXT], features[TEXT:])
    own_flip = jnp.where(is_text, flipped[:TEXT], flipped[TEXT:])
    tables = jnp.stack(
        [
            jnp.pad(table_pos, ((0, 0), (0, LANES - table_pos.shape[1]))),
            jnp.pad(table_x, ((0, 0), (0, LANES - table_x.shape[1]))),
            jnp.pad(table_y, ((0, 0), (0, LANES - table_y.shape[1]))),
        ],
        axis=1,
    )
    tables = jnp.pad(tables, ((0, 0), (0, 5), (0, 0)))

    def mix_fn(inputs_f, weight_f, bias_f):
        return dilated_mix(inputs_f, own_pages, weight_f, bias_f)

    own_states = own_low.astype(f32)
    mixed, mix_pull = jax.vjp(mix_fn, own_states, conv_weight, conv_bias)
    mixed_low = mixed.astype(bf16)
    other_pages = jnp.where(is_text, page_ids[1], page_ids[0])
    other_mixed = dilated_mix(other_low.astype(f32), other_pages, conv_weight, conv_bias)
    other_mixed = other_mixed.astype(bf16)
    mixed_all = jnp.concatenate(
        [jnp.where(is_text, mixed_low, other_mixed), jnp.where(is_text, other_mixed, mixed_low)],
        axis=0,
    )
    mixed_t = mixed_all.T
    if fast:
        pieces_qkv[0] = after(pieces_qkv[0], mixed_all, mixed_t, features, tables, bounds, own_flip)
    full_qkv = place_rows(place, groups_qkv, pieces_qkv, (d_model, pack_qkv.shape[1]))
    full_query = full_qkv[:, :d_model]
    full_kv = full_qkv[:, d_model:]
    queries = ((plain_dot(mixed_low, full_query) + b_query).astype(bf16) * 0.125).astype(bf16)
    kv_bias = jnp.concatenate([jnp.zeros_like(b_value), b_value])
    keys_values = (plain_dot(mixed_all, full_kv) + kv_bias).astype(bf16)
    attend_in = queries
    if fast:
        column_far = jnp.stack([after(part, keys_values, queries) for part in parts_far])
        parts_down = column_parts(after(w_down, column_far))
        across_far = exchange(column_far, 2)
        attend_in = after(queries, column_far)
    context = attend(bounds, attend_in, keys_values, features, own_feats, tables)
    if fast:
        column_down = jnp.stack([after(part, context) for part in parts_down])
        pieces_near[2] = after(pieces_near[2], column_down)
        pieces_near[3] = exchange(pieces_near[2], 1)
        across_far = after(across_far, column_down)
        pieces_rest = pieces_near + row_pieces(column_far, across_far)
        groups_rest = (("halves", 0), ("rows", split))
    else:
        pieces_rest = [lax.all_gather(pack_rest, "page", axis=0, tiled=True)]
        groups_rest = (("full", 0),)
    vectors = jnp.stack(
        [b_out, gain_one, bias_one, b_down, gain_two, bias_two, jnp.zeros_like(b_out), b_out]
    )
    unit, scale, normed_low, normed_t, active, active_t, slope = up_forward(
        place, context, mixed, vectors, b_up[None], groups_rest, pieces_rest
    )
    if fast:
        across_down = after(exchange(column_down, 2), active)
        pieces_down = row_pieces(column_down, across_down)
        groups_down = (("rows", 0),)
    else:
        groups_down = (("full", 0),)
        pieces_down = [lax.all_gather(w_down, "page", axis=0, tiled=True)]
    output_row, grad_sum_two, grad_ffn, small_two = down_forward(
        place, active, unit, vectors, cotangent[0, 0], groups_down, pieces_down
    )
    grad_ffn_in = grad_ffn
    if fast:
        keep_down, send_down = grad_by_rows(active_t, grad_ffn, place)
        partner_down = exchange(send_down, 1)
        context_t = after(context, send_down).T
        partner_down = after(partner_down, context_t)
        held_down, plane_out = halve_plane(place, keep_down, partner_down)
        plane_down = swap(plane_out)
        grad_ffn_in = after(grad_ffn, plane_out)
    else:
        shard_down = summed_rows([(active_t, grad_ffn)])
        context_t = context.T
    grad_hidden, grad_b_up, grad_first, grad_branch, grad_context, small_one = ffn_back(
        place,
        grad_ffn_in,
        slope,
        grad_sum_two,
        unit,
        scale,
        vectors,
        groups_rest,
        pieces_rest,
        groups_down,
        pieces_down,
    )
    attend_in = grad_context
    if fast:
        plane_down = after(plane_down, grad_branch)
        held_down, across_out = halve_across(place, held_down, plane_down)
        across_down = exchange(across_out, 2)
        branch_in = after(grad_branch, across_out)
        pairs = [(context_t, False, branch_in), (normed_t, False, grad_hidden)]
        keep_rest, send_rest = grad_by_columns(pairs, place, d_model)
        across_down = after(across_down, keep_rest)
        partner_rest = exchange(after(send_rest, across_down), 1)
        own_down, sends_down = column_sends(held_down, across_down)
        arrived_down = column_arrivals(sends_down)
        partner_rest = after(partner_rest, *sends_down)
        held_rest, across_out = halve_across(place, keep_rest, partner_rest)
        across_rest = exchange(across_out, 2)
        attend_in = after(grad_context, across_out)
    else:
        shard_rest = summed_rows([(context_t, grad_branch), (normed_t, grad_hidden)])
    grad_queries, grad_keys, grad_values, grad_tables = attend_back(
        bounds, queries, keys_values, attend_in, features, own_feats, own_flip, tables, 0, PAIRS
    )
    grad_keys_in, grad_queries_in = grad_keys, grad_queries
    if fast:
        arrived_down = [after(part, grad_queries) for part in arrived_down]
        total_down = column_total(own_down, arrived_down)
        far_down = swap(total_down)
        across_rest = after(across_rest, total_down)
        own_rest, sends_rest = column_sends(held_rest, across_rest)
        arrived_rest = column_arrivals(sends_rest)
        grad_queries_in = after(grad_queries, *sends_rest)
    pairs = [(mixed_t, True, grad_queries_in), (mixed_t, False, grad_keys), (mixed_t, False, grad_values)]
    if fast:
        keep_qkv, send_qkv = grad_by_columns(pairs, place, d_model)
        partner_qkv = exchange(send_qkv, 1)
        grad_keys_in = after(grad_keys, send_qkv)
    else:
        shard_qkv = summed_rows(
            [(mixed_low.T, grad_queries), (mixed_t, grad_keys), (mixed_t, grad_values)]
        )
    grad_b_query = column_sum(grad_queries)
    grad_b_value = column_sum(grad_values)
    to_other = input_back(place, full_qkv, grad_keys_in, grad_values, ())
    from_other = swap(to_other)
    grad_values_in = grad_values
    if fast:
        partner_qkv = after(partner_qkv, to_other)
        held_qkv, across_out = halve_across(place, keep_qkv, partner_qkv)
        across_qkv = exchange(across_out, 2)
        grad_values_in = after(grad_values, across_out)
    own_part = input_back(place, full_qkv, grad_keys, grad_values_in, (grad_first, grad_queries))
    if fast:
        from_other = after(from_other, own_part)
    grad_mixed = own_part + from_other.astype(f32)
    grad_in, grad_conv_w, grad_conv_b = mix_pull(grad_mixed)

    table_rows = grad_tables[:, :3].reshape(6, 768)
    packed = jnp.concatenate(
        [
            grad_conv_w,
            grad_conv_b[None],
            grad_b_query,
            grad_b_value,
            small_one[2:3],
            small_one[0:2],
            small_two[2:3],
            small_two[0:2],
            grad_b_up.reshape(d_ff // d_model, d_model),
            table_rows,
            jnp.zeros((2, d_model), f32),
        ],
        axis=0,
    )
    if fast:
        arrived_rest = [after(part, packed) for part in arrived_rest]
        total_rest = column_total(own_rest, arrived_rest)
        far_rest = swap(total_rest)
        across_qkv = after(across_qkv, total_rest)
        own_qkv, sends_qkv = column_sends(held_qkv, across_qkv)
        arrived_qkv = column_arrivals(sends_qkv)
        packed = after(packed, *sends_qkv)
    packed = sum_everywhere(packed)
    if fast:
        arrived_qkv = [after(part, packed) for part in arrived_qkv]
        total_qkv = column_total(own_qkv, arrived_qkv)
        far_qkv = swap(total_qkv)
    g_tables = packed[16:22].reshape(HEADS, 3, LANES)
    if fast:
        shard_down = jnp.where(
            is_text,
            jnp.concatenate([total_down, far_down], axis=1),
            jnp.concatenate([far_down, total_down], axis=1),
        ).astype(f32)
        shard_qkv = total_qkv.astype(f32) + far_qkv.astype(f32)
        shard_rest = total_rest.astype(f32) + far_rest.astype(f32)
    return (
        output_row[None, None],
        grad_in.astype(bf16)[None, None],
        packed[0:3],
        packed[3],
        shard_qkv[:, :d_model],
        packed[4],
        shard_qkv[:, d_model : 2 * d_model],
        shard_qkv[:, 2 * d_model :],
        packed[5],
        shard_rest[:, :d_model],
        packed[6],
        g_tables[:, 0, : table_pos.shape[1]],
        g_tables[:, 1, 64 : 64 + table_x.shape[1]],
        g_tables[:, 2, 64 : 64 + table_y.shape[1]],
        packed[7],
        packed[8],
        shard_rest[:, d_model:],
        packed[12:16].reshape(d_ff),
        shard_down,
        packed[9],
        packed[10],
        packed[11],
    )


def solution(mesh):
    rows = P("mod", "page", None, None)
    ids = P("page", None)
    cut = P("page", None)
    return jax.shard_map(
        local,
        mesh=mesh,
        in_specs=(
            rows, rows, ids, ids, ids, P(), P(), cut, P(), cut, cut, P(), cut,
            P(), P(), P(), P(), P(), P(), cut, P(), cut, P(), P(), P(),
        ),
        out_specs=(
            rows, rows, P(), P(), cut, P(), cut, cut, P(), cut, P(), P(), P(),
            P(), P(), P(), cut, P(), cut, P(), P(), P(),
        ),
        check_vma=False,
    )
```

```python
import functools

import jax
import jax.numpy as jnp
import numpy as np
from jax import lax
from jax.experimental import pallas as pl
from jax.experimental.pallas import tpu as pltpu
from jax.sharding import PartitionSpec as P

HEADS = 12
HEAD = 64
GRID = 8
PAGES = 8
POS_BINS = 64
BOX_BINS = 32
PATCH = 64
TEXT = 512
PAIRS = HEADS // 2
LANES = 2 * HEAD
WINDOW = 144
KEYS = WINDOW + PATCH

dilation = 2
small_cost = pl.CostEstimate(flops=1000, bytes_accessed=1000, transcendentals=0)
norm_eps = 1e-05
mask_fill = -1000000000.0
erfc_poly = (
    0.2367515965428487,
    0.24062179898991767,
    0.18865103029313968,
    0.2877518531132804,
    -0.1648672439458568,
    0.4765735350541787,
    -0.34041833366480423,
    0.07493571514857543,
)
bf16 = jnp.bfloat16
f32 = jnp.float32


def shifted(values, offset, fill_value):
    padding = jnp.full((abs(offset),) + values.shape[1:], fill_value, values.dtype)
    if offset > 0:
        return jnp.concatenate([values[offset:], padding], axis=0)
    return jnp.concatenate([padding, values[:offset]], axis=0)


def dilated_mix(inputs, page_ids, conv_weight, conv_bias):
    summed = inputs + conv_bias + conv_weight[1] * inputs
    for tap_index, offset in ((0, -dilation), (2, dilation)):
        moved_rows = shifted(inputs, offset, 0.0)
        moved_pages = shifted(page_ids, offset, -1)
        same_page = (moved_pages == page_ids)[:, None]
        summed = summed + conv_weight[tap_index] * jnp.where(same_page, moved_rows, 0.0)
    return summed


def bin_features(pos_bins, bins_x, bins_y):
    return jnp.concatenate(
        [
            jax.nn.one_hot(pos_bins, POS_BINS, dtype=bf16),
            jax.nn.one_hot(bins_x, BOX_BINS, dtype=bf16),
            jax.nn.one_hot(bins_y, BOX_BINS, dtype=bf16),
        ],
        axis=1,
    )


def token_ids(text_pages, text_x, text_y):
    text_index = jnp.arange(TEXT, dtype=jnp.int32)
    text_pos = text_index * POS_BINS // TEXT
    patch_pos = text_index % PATCH * POS_BINS // PATCH
    patch_page = text_index // PATCH
    patch_x = text_index % GRID * BOX_BINS // GRID
    patch_y = text_index // GRID % GRID * BOX_BINS // GRID
    page_ids = jnp.stack([text_pages, patch_page])
    pos_bins = jnp.stack([text_pos, patch_pos])
    bins_x = jnp.stack([text_x, patch_x])
    bins_y = jnp.stack([text_y, patch_y])
    return (page_ids, pos_bins, bins_x, bins_y)


def plain_dot(left_side, right_side):
    return jnp.dot(left_side, right_side, preferred_element_type=f32)


def dot_left_t(left_side, right_side):
    return lax.dot_general(
        left_side, right_side, (((0,), (0,)), ((), ())), preferred_element_type=f32
    )


def dot_right_t(left_side, right_side):
    return lax.dot_general(
        left_side, right_side, (((1,), (1,)), ((), ())), preferred_element_type=f32
    )


def iota(shape, axis):
    return lax.broadcasted_iota(jnp.int32, shape, axis)


def bias_block(table_rows):
    pos_part = pltpu.roll(
        jnp.broadcast_to(table_rows[0:1], (POS_BINS, LANES)), 65, 1, stride=1, stride_axis=0
    )
    x_part = pltpu.roll(
        jnp.broadcast_to(table_rows[1:2], (BOX_BINS, LANES)), 33, 1, stride=1, stride_axis=0
    )
    y_part = pltpu.roll(
        jnp.broadcast_to(table_rows[2:3], (BOX_BINS, LANES)), 65, 1, stride=1, stride_axis=0
    )
    lane = iota((POS_BINS, LANES), 1)
    pos_part = jnp.where(lane < POS_BINS, pos_part, 0.0)
    lane = iota((BOX_BINS, LANES), 1)
    x_part = jnp.where((lane >= 64) & (lane < 96), x_part, 0.0)
    y_part = jnp.where(lane >= 96, y_part, 0.0)
    return jnp.concatenate([pos_part, x_part, y_part], axis=0).astype(bf16)


def diagonal_sums(grad_block):
    lane = iota((POS_BINS, LANES), 1)
    pos_part = jnp.where(lane < POS_BINS, grad_block[:64], 0.0)
    lane = iota((BOX_BINS, LANES), 1)
    x_part = jnp.where((lane >= 64) & (lane < 96), grad_block[64:96], 0.0)
    y_part = jnp.where(lane >= 96, grad_block[96:], 0.0)
    pos_part = pltpu.roll(pos_part, 0, 1, stride=1, stride_axis=0)
    x_part = pltpu.roll(x_part, 0, 1, stride=1, stride_axis=0)
    y_part = pltpu.roll(y_part, 96, 1, stride=1, stride_axis=0)
    rows = [jnp.sum(part, axis=0, keepdims=True) for part in (pos_part, x_part, y_part)]
    return jnp.concatenate(rows + [jnp.zeros((5, LANES), f32)], axis=0)


def stacked_heads(rows, low_lane):
    zero = jnp.zeros_like(rows)
    return jnp.concatenate(
        [jnp.where(low_lane, rows, zero), jnp.where(low_lane, zero, rows)], axis=0
    )


def page_operands(page, bounds, q_ref, k_ref, feat_ref, lookup):
    own_at = pl.multiple_of(bounds[page], 16)
    key_at = pl.multiple_of(bounds[3 * PAGES + page], 16)
    low_lane = iota((WINDOW, LANES), 1) < HEAD
    queries = stacked_heads(q_ref[pl.ds(own_at, WINDOW), :], low_lane)
    rel = jnp.concatenate(
        [lookup[pl.ds(own_at, WINDOW), :LANES], lookup[pl.ds(own_at, WINDOW), LANES:]], axis=0
    )
    query_side = jnp.concatenate([rel, queries], axis=1)
    patch_rows = pl.ds(TEXT + PATCH * page, PATCH)
    text_rows = pl.ds(key_at, WINDOW)
    key_side = jnp.concatenate(
        [
            jnp.concatenate([feat_ref[text_rows, :], k_ref[text_rows, :]], axis=1),
            jnp.concatenate([feat_ref[patch_rows, :], k_ref[patch_rows, :]], axis=1),
        ],
        axis=0,
    )
    own_row = iota((WINDOW, LANES), 0) + own_at
    own_ok = (own_row >= bounds[PAGES + page]) & (own_row < bounds[2 * PAGES + page])
    return own_at, key_at, low_lane, own_ok, queries, query_side, key_side, text_rows, patch_rows


def attend_kernel(bounds, q_ref, k_ref, v_ref, feat_ref, own_feat_ref, table_ref, context_ref, lookup):
    blocks = jnp.concatenate([bias_block(table_ref[0]), bias_block(table_ref[1])], axis=1)
    lookup[...] = jnp.dot(own_feat_ref[...], blocks, preferred_element_type=f32).astype(bf16)
    for page in range(PAGES):
        own_at, key_at, low_lane, own_ok, queries, query_side, key_side, text_rows, patch_rows = (
            page_operands(page, bounds, q_ref, k_ref, feat_ref, lookup)
        )
        scores = dot_right_t(query_side, key_side)
        column = iota((1, KEYS), 1)
        key_row = column + key_at
        key_ok = (column >= WINDOW) | (
            (key_row >= bounds[4 * PAGES + page]) & (key_row < bounds[5 * PAGES + page])
        )
        scores = jnp.where(key_ok, scores, mask_fill)
        row_max = jnp.max(scores, axis=1, keepdims=True)
        weights = jnp.exp(scores - row_max)
        total = jnp.sum(weights, axis=1, keepdims=True)
        prob = (weights * (1.0 / total)).astype(bf16)
        values = jnp.concatenate([v_ref[text_rows, :], v_ref[patch_rows, :]], axis=0)
        mixed = jnp.dot(prob, values, preferred_element_type=f32)
        picked = jnp.where(low_lane, mixed[:WINDOW], mixed[WINDOW:])
        before = context_ref[pl.ds(own_at, WINDOW), :].astype(f32)
        context_ref[pl.ds(own_at, WINDOW), :] = jnp.where(own_ok, picked, before).astype(bf16)


def attend_back_kernel(
    bounds,
    q_ref,
    k_ref,
    v_ref,
    grad_ref,
    feat_ref,
    own_feat_ref,
    flip_feat_ref,
    table_ref,
    grad_q_ref,
    grad_k_ref,
    grad_v_ref,
    grad_table_ref,
    lookup,
    grad_lookup,
):
    blocks = jnp.concatenate([bias_block(table_ref[0]), bias_block(table_ref[1])], axis=1)
    lookup[...] = jnp.dot(own_feat_ref[...], blocks, preferred_element_type=f32).astype(bf16)
    for page in range(PAGES):
        own_at, key_at, low_lane, own_ok, queries, query_side, key_side, text_rows, patch_rows = (
            page_operands(page, bounds, q_ref, k_ref, feat_ref, lookup)
        )
        scores = dot_right_t(key_side, query_side)
        row = iota((KEYS, 1), 0)
        key_row = row + key_at
        key_in = (key_row >= bounds[4 * PAGES + page]) & (key_row < bounds[5 * PAGES + page])
        scores = jnp.where((row >= WINDOW) | key_in, scores, mask_fill)
        col_max = jnp.max(scores, axis=0, keepdims=True)
        weights = jnp.exp(scores - col_max)
        total = jnp.sum(weights, axis=0, keepdims=True)
        prob = weights * (1.0 / total)
        grad_rows = grad_ref[pl.ds(own_at, WINDOW), :]
        grad_rows = jnp.where(own_ok, grad_rows, jnp.zeros_like(grad_rows))
        grads = stacked_heads(grad_rows, low_lane)
        values = jnp.concatenate([v_ref[text_rows, :], v_ref[patch_rows, :]], axis=0)
        grad_prob = dot_right_t(values, grads)
        inner = jnp.sum(prob * grad_prob, axis=0, keepdims=True)
        grad_scores = (prob * (grad_prob - inner)).astype(bf16)
        grad_v = jnp.dot(prob.astype(bf16), grads, preferred_element_type=f32)
        grad_k = jnp.dot(grad_scores, queries, preferred_element_type=f32)
        back = dot_left_t(grad_scores, key_side)
        grad_q = jnp.where(low_lane, back[:WINDOW, LANES:], back[WINDOW:, LANES:]) * 0.125
        own_rows = pl.ds(own_at, WINDOW)
        before = grad_q_ref[own_rows, :].astype(f32)
        grad_q_ref[own_rows, :] = jnp.where(own_ok, grad_q, before).astype(bf16)
        grad_lookup[own_rows, :LANES] = jnp.where(
            own_ok, back[:WINDOW, :LANES], grad_lookup[own_rows, :LANES]
        )
        grad_lookup[own_rows, LANES:] = jnp.where(
            own_ok, back[WINDOW:, :LANES], grad_lookup[own_rows, LANES:]
        )
        wide_row = iota((WINDOW, LANES), 0) + key_at
        text_ok = (wide_row >= bounds[4 * PAGES + page]) & (wide_row < bounds[5 * PAGES + page])
        for grad, ref in ((grad_k, grad_k_ref), (grad_v, grad_v_ref)):
            before = ref[text_rows, :].astype(f32)
            ref[text_rows, :] = jnp.where(text_ok, grad[:WINDOW], before).astype(bf16)
            ref[patch_rows, :] = grad[WINDOW:].astype(bf16)
    grad_high = grad_lookup[...].astype(bf16)
    grad_rest = (grad_lookup[...] - grad_high.astype(f32)).astype(bf16)
    flip = flip_feat_ref[...]
    grad_block = dot_left_t(flip, grad_high) + dot_left_t(flip, grad_rest)
    grad_table_ref[0] = diagonal_sums(grad_block[:, :LANES])
    grad_table_ref[1] = diagonal_sums(grad_block[:, LANES:])


def column_spec(rows, first=0):
    return pl.BlockSpec((rows, LANES), lambda pair, bounds: (0, pair + first))


def tables_spec(first=0):
    return pl.BlockSpec((2, 8, LANES), lambda pair, bounds: (pair + first, 0, 0))


def whole_spec(rows):
    return pl.BlockSpec((rows, LANES), lambda pair, bounds: (0, 0))


def attend(bounds, queries, keys_values, features, own_features, tables):
    return pl.pallas_call(
        attend_kernel,
        grid_spec=pltpu.PrefetchScalarGridSpec(
            num_scalar_prefetch=1,
            grid=(PAIRS,),
            in_specs=[
                column_spec(TEXT),
                column_spec(2 * TEXT),
                column_spec(2 * TEXT, PAIRS),
                whole_spec(2 * TEXT),
                whole_spec(TEXT),
                tables_spec(),
            ],
            out_specs=column_spec(TEXT),
            scratch_shapes=[pltpu.VMEM((TEXT, 2 * LANES), bf16)],
        ),
        out_shape=jax.ShapeDtypeStruct((TEXT, HEADS * HEAD), bf16),
        cost_estimate=small_cost,
        name="attend",
    )(bounds, queries, keys_values, keys_values, features, own_features, tables)


def attend_back(
    bounds, queries, keys_values, grad_context, features, own_features, flip, tables, first, count
):
    return pl.pallas_call(
        attend_back_kernel,
        grid_spec=pltpu.PrefetchScalarGridSpec(
            num_scalar_prefetch=1,
            grid=(count,),
            in_specs=[
                column_spec(TEXT, first),
                column_spec(2 * TEXT, first),
                column_spec(2 * TEXT, PAIRS + first),
                column_spec(TEXT, first),
                whole_spec(2 * TEXT),
                whole_spec(TEXT),
                whole_spec(TEXT),
                tables_spec(first),
            ],
            out_specs=[
                column_spec(TEXT),
                column_spec(2 * TEXT),
                column_spec(2 * TEXT),
                tables_spec(),
            ],
            scratch_shapes=[
                pltpu.VMEM((TEXT, 2 * LANES), bf16),
                pltpu.VMEM((TEXT, 2 * LANES), f32),
            ],
        ),
        out_shape=[
            jax.ShapeDtypeStruct((TEXT, count * LANES), bf16),
            jax.ShapeDtypeStruct((2 * TEXT, count * LANES), bf16),
            jax.ShapeDtypeStruct((2 * TEXT, count * LANES), bf16),
            jax.ShapeDtypeStruct((2 * count, 8, LANES), f32),
        ],
        cost_estimate=small_cost,
        name="attend_back",
    )(
        bounds,
        queries,
        keys_values,
        keys_values,
        grad_context,
        features,
        own_features,
        flip,
        tables,
    )


def exchange(values, mask):
    count = lax.axis_size("page")
    return lax.ppermute(values, "page", [(i, i ^ mask) for i in range(count)])


def after(value, *earlier):
    return lax.optimization_barrier((value, *earlier))[0]


def slot_mask(slot):
    return (slot & 3) * 4 + (slot >> 2) * 2


def project_kernel(groups, place, mixed_ref, bias_ref, *refs):
    *pieces, query_ref, both_ref, weight_ref, sems = refs
    width = mixed_ref.shape[1]
    tokens = query_ref.shape[0]
    for copy in start_rows(place, groups, pieces, weight_ref, sems):
        copy.wait()
    own = mixed_ref[pl.ds(pl.multiple_of(place[1] * tokens, 16), tokens), :]
    queries = jnp.dot(own, weight_ref[:, :width], preferred_element_type=f32) + bias_ref[:, :width]
    query_ref[...] = (queries.astype(bf16).astype(f32) * 0.125).astype(bf16)
    for part in range(2):
        rows = pl.ds(part * tokens, tokens)
        for column in (1, 2):
            at = slice(column * width, (column + 1) * width)
            out = slice((column - 1) * width, column * width)
            values = jnp.dot(mixed_ref[rows, :], weight_ref[:, at], preferred_element_type=f32)
            both_ref[rows, out] = (values + bias_ref[:, at]).astype(bf16)


def project(place, mixed, biases, groups, pieces):
    rows, width = mixed.shape
    vmem = pl.BlockSpec(memory_space=pltpu.VMEM)
    return pl.pallas_call(
        functools.partial(project_kernel, groups),
        grid_spec=pltpu.PrefetchScalarGridSpec(
            num_scalar_prefetch=1,
            grid=(),
            in_specs=[vmem] * 2 + any_specs(len(pieces)),
            out_specs=[vmem] * 3,
            scratch_shapes=[pltpu.SemaphoreType.DMA((32,))],
        ),
        out_shape=[
            jax.ShapeDtypeStruct((rows // 2, width), bf16),
            jax.ShapeDtypeStruct((rows, 2 * width), bf16),
            jax.ShapeDtypeStruct((width, 3 * width), bf16),
        ],
        cost_estimate=small_cost,
        compiler_params=pltpu.CompilerParams(vmem_limit_bytes=16 << 20),
        name="project",
    )(place, mixed, biases, *pieces)


def column_parts(shard):
    return [shard] + [exchange(shard, 4 * step) for step in (1, 2, 3)]


def half_pieces(column):
    eight = jnp.concatenate([column, exchange(column, 2)])
    far = swap(eight)
    return [eight, exchange(eight, 1), far, exchange(far, 1)]


def row_pieces(column, across):
    return [column, exchange(column, 1), across, exchange(across, 1)]


def column_of(shard):
    return jnp.stack(column_parts(shard))


def start_rows(place, groups, refs, full, sems, first=0):
    copies = []
    for kind, column in groups:
        if kind == "full":
            piece, *refs = refs
            width = piece.shape[1]
            target = full.at[:, pl.ds(column, width)]
            copies.append(pltpu.make_async_copy(piece, target, sems.at[first + len(copies)]))
            continue
        pieces, refs = refs[:4], refs[4:]
        _, rows, width = pieces[0].shape
        for index in range(32 if kind == "halves" else 16):
            at = column
            if kind == "halves":
                source, slot = index >> 3, index & 7
                mask = slot_mask(slot) + (source & 1)
                at = pl.multiple_of(column + (place[1] ^ (source >> 1)) * width, 128)
            else:
                source, slot = index & 3, index >> 2
                mask = slot * 4 + source
            row = pl.multiple_of((place[0] ^ mask) * rows, 16)
            copies.append(
                pltpu.make_async_copy(
                    pieces[source].at[slot],
                    full.at[pl.ds(row, rows), pl.ds(at, width)],
                    sems.at[first + len(copies)],
                )
            )
    for copy in copies:
        copy.start()
    return copies


def gelu_parts(values):
    size = jnp.abs(values)
    t = 1.0 / (1.0 + (0.42 * 0.7071067811865476) * size)
    poly = jnp.full_like(t, erfc_poly[-1])
    for coefficient in erfc_poly[-2::-1]:
        poly = poly * t + coefficient
    bell = jnp.exp(-0.5 * values * values)
    tail = (0.5 * t) * (poly * bell)
    cdf = jnp.where(values >= 0.0, 1.0 - tail, tail)
    return values * cdf, cdf + (values * 0.3989422804014327) * bell


def normalized(values):
    centered = values - jnp.mean(values, axis=1, keepdims=True)
    variance = jnp.mean(centered * centered, axis=1, keepdims=True)
    scale = lax.rsqrt(variance + norm_eps)
    return centered * scale, scale


def norm_back(grads, unit, scale, gain):
    scaled = grads * gain
    mean = jnp.mean(scaled, axis=1, keepdims=True)
    inner = jnp.mean(scaled * unit, axis=1, keepdims=True)
    return scale * (scaled - mean - unit * inner)


def up_kernel(groups, place, context_ref, mixed_ref, vec_ref, bias_ref, *refs):
    *pieces, unit_ref, scale_ref, low_ref, low_t_ref, active_ref, active_t_ref, slope_ref = refs[:-4]
    weight, hidden, low, sems = refs[-4:]
    step = pl.program_id(0)
    tiles = pl.num_programs(0) - 1
    width = context_ref.shape[1]
    tile = active_ref.shape[1]

    @pl.when(step == 0)
    def _():
        for copy in start_rows(place, groups, pieces, weight, sems):
            copy.wait()
        branch = jnp.dot(context_ref[...], weight[:, :width], preferred_element_type=f32)
        unit, scale = normalized(mixed_ref[...] + branch + vec_ref[0:1])
        unit_ref[...] = unit
        scale_ref[...] = jnp.broadcast_to(scale, scale_ref.shape)
        normed = (unit * vec_ref[1:2] + vec_ref[2:3]).astype(bf16)
        low[...] = normed
        low_ref[...] = normed
        low_t_ref[...] = normed.T

    def product():
        at = pl.multiple_of(width + step * tile, 128)
        return jnp.dot(low[...], weight[:, pl.ds(at, tile)], preferred_element_type=f32)

    def activate():
        active, slope = gelu_parts(hidden[(step + 1) % 2] + bias_ref[...])
        active = active.astype(bf16)
        active_ref[...] = active
        active_t_ref[...] = active.T
        slope_ref[...] = slope

    @pl.when(step == 0)
    def _():
        hidden[step % 2] = product()

    @pl.when((step > 0) & (step < tiles))
    def _():
        hidden[step % 2] = product()
        activate()

    @pl.when(step == tiles)
    def _():
        activate()


def any_specs(count):
    return [pl.BlockSpec(memory_space=pl.ANY)] * count


def up_forward(place, context, mixed, vectors, bias_up, groups, pieces):
    tokens, width = mixed.shape
    hidden_width = bias_up.shape[1]
    tile = 512
    whole = lambda step, place: (0, 0)
    last = lambda step, place: (0, jnp.maximum(step - 1, 0))
    last_t = lambda step, place: (jnp.maximum(step - 1, 0), 0)
    return pl.pallas_call(
        functools.partial(up_kernel, groups),
        grid_spec=pltpu.PrefetchScalarGridSpec(
            num_scalar_prefetch=1,
            grid=(hidden_width // tile + 1,),
            in_specs=[
                pl.BlockSpec((tokens, width), whole),
                pl.BlockSpec((tokens, width), whole),
                pl.BlockSpec(vectors.shape, whole),
                pl.BlockSpec((1, tile), last),
            ]
            + any_specs(len(pieces)),
            out_specs=[
                pl.BlockSpec((tokens, width), whole),
                pl.BlockSpec((tokens, 128), whole),
                pl.BlockSpec((tokens, width), whole),
                pl.BlockSpec((width, tokens), whole),
                pl.BlockSpec((tokens, tile), last),
                pl.BlockSpec((tile, tokens), last_t),
                pl.BlockSpec((tokens, tile), last),
            ],
            scratch_shapes=[
                pltpu.VMEM((width, width + hidden_width), bf16),
                pltpu.VMEM((2, tokens, tile), f32),
                pltpu.VMEM((tokens, width), bf16),
                pltpu.SemaphoreType.DMA((48,)),
            ],
        ),
        out_shape=[
            jax.ShapeDtypeStruct((tokens, width), f32),
            jax.ShapeDtypeStruct((tokens, 128), f32),
            jax.ShapeDtypeStruct((tokens, width), bf16),
            jax.ShapeDtypeStruct((width, tokens), bf16),
            jax.ShapeDtypeStruct((tokens, hidden_width), bf16),
            jax.ShapeDtypeStruct((hidden_width, tokens), bf16),
            jax.ShapeDtypeStruct((tokens, hidden_width), f32),
        ],
        cost_estimate=small_cost,
        compiler_params=pltpu.CompilerParams(vmem_limit_bytes=28 << 20),
        name="up_forward",
    )(place, context, mixed, vectors, bias_up, *pieces)


def down_kernel(groups, place, active_ref, unit_ref, vec_ref, grad_ref, *refs):
    *pieces, out_ref, sum_ref, low_ref, small_ref = refs[:-2]
    weight, sems = refs[-2:]
    for copy in start_rows(place, groups, pieces, weight, sems):
        copy.wait()
    tokens, width = unit_ref.shape
    half = tokens // 2
    smalls = [jnp.zeros((1, width), f32)] * 3
    for part in range(2):
        rows = pl.ds(part * half, half)
        ffn = jnp.dot(active_ref[rows, :], weight[...], preferred_element_type=f32)
        normed = unit_ref[rows, :] * vec_ref[1:2] + vec_ref[2:3]
        unit, scale = normalized(normed + ffn + vec_ref[3:4])
        out_ref[rows, :] = (unit * vec_ref[4:5] + vec_ref[5:6]).astype(bf16)
        grads = grad_ref[rows, :].astype(f32)
        total = norm_back(grads, unit, scale, vec_ref[4:5])
        low = total.astype(bf16)
        sum_ref[rows, :] = total
        low_ref[rows, :] = low
        for index, term in enumerate((grads * unit, grads, low.astype(f32))):
            smalls[index] = smalls[index] + jnp.sum(term, axis=0, keepdims=True)
    small_ref[...] = jnp.concatenate(smalls + [jnp.zeros((5, width), f32)], axis=0)


def down_forward(place, active, unit, vectors, grads, groups, pieces):
    tokens, width = unit.shape
    hidden_width = active.shape[1]
    vmem = pl.BlockSpec(memory_space=pltpu.VMEM)
    return pl.pallas_call(
        functools.partial(down_kernel, groups),
        grid_spec=pltpu.PrefetchScalarGridSpec(
            num_scalar_prefetch=1,
            grid=(),
            in_specs=[vmem] * 4 + any_specs(len(pieces)),
            out_specs=[vmem] * 4,
            scratch_shapes=[
                pltpu.VMEM((hidden_width, width), bf16),
                pltpu.SemaphoreType.DMA((16,)),
            ],
        ),
        out_shape=[
            jax.ShapeDtypeStruct((tokens, width), bf16),
            jax.ShapeDtypeStruct((tokens, width), f32),
            jax.ShapeDtypeStruct((tokens, width), bf16),
            jax.ShapeDtypeStruct((8, width), f32),
        ],
        cost_estimate=small_cost,
        compiler_params=pltpu.CompilerParams(vmem_limit_bytes=24 << 20),
        name="down_forward",
    )(place, active, unit, vectors, grads, *pieces)


def ffn_back_kernel(groups, groups_down, count, place, low_ref, slope_ref, sum_ref, unit_ref, scale_ref, vec_ref, *refs):
    rest, down = refs[: count[0]], refs[count[0] : sum(count)]
    hidden_ref, bias_ref, first_ref, branch_ref, context_ref, small_ref = refs[sum(count) : -4]
    weight, weight_down, total, sems = refs[-4:]
    step = pl.program_id(0)
    tokens, width = unit_ref.shape
    tile = slope_ref.shape[1]
    half = tokens // 2

    @pl.when(step == 0)
    def _():
        copies = start_rows(place, groups_down, down, weight_down, sems)
        copies += start_rows(place, groups, rest, weight, sems, 16)
        total[...] = sum_ref[...]
        for copy in copies:
            copy.wait()

    rows_down = weight_down[pl.ds(pl.multiple_of(step * tile, 128), tile), :]
    columns = weight[:, pl.ds(pl.multiple_of(width + step * tile, 128), tile)]
    bias = jnp.zeros((1, tile), f32)
    for part in range(2):
        rows = pl.ds(part * half, half)
        grads = (dot_right_t(low_ref[rows, :], rows_down) * slope_ref[rows, :]).astype(bf16)
        hidden_ref[rows, :] = grads
        bias = bias + jnp.sum(grads.astype(f32), axis=0, keepdims=True)
        total[rows, :] += dot_right_t(grads, columns)
    bias_ref[...] = bias

    @pl.when(step == pl.num_programs(0) - 1)
    def _():
        grads = total[...]
        unit = unit_ref[...]
        first = norm_back(grads, unit, scale_ref[:, 0:1], vec_ref[1:2])
        branch = first.astype(bf16)
        first_ref[...] = first
        branch_ref[...] = branch
        context_ref[...] = dot_right_t(branch, weight[:, :width]).astype(bf16)
        smalls = [
            jnp.sum(term, axis=0, keepdims=True)
            for term in (grads * unit, grads, branch.astype(f32))
        ]
        small_ref[...] = jnp.concatenate(smalls + [jnp.zeros((5, width), f32)], axis=0)


def ffn_back(
    place, low, slope, total, unit, scale, vectors, groups, pieces_rest, groups_down, pieces_down
):
    tokens, width = unit.shape
    hidden_width = slope.shape[1]
    tile = 512
    count = (len(pieces_rest), len(pieces_down))
    whole = lambda step, place: (0, 0)
    column = lambda step, place: (0, step)
    return pl.pallas_call(
        functools.partial(ffn_back_kernel, groups, groups_down, count),
        grid_spec=pltpu.PrefetchScalarGridSpec(
            num_scalar_prefetch=1,
            grid=(hidden_width // tile,),
            in_specs=[
                pl.BlockSpec((tokens, width), whole),
                pl.BlockSpec((tokens, tile), column),
                pl.BlockSpec((tokens, width), whole),
                pl.BlockSpec((tokens, width), whole),
                pl.BlockSpec((tokens, 128), whole),
                pl.BlockSpec(vectors.shape, whole),
            ]
            + any_specs(sum(count)),
            out_specs=[
                pl.BlockSpec((tokens, tile), column),
                pl.BlockSpec((1, tile), column),
                pl.BlockSpec((tokens, width), whole),
                pl.BlockSpec((tokens, width), whole),
                pl.BlockSpec((tokens, width), whole),
                pl.BlockSpec((8, width), whole),
            ],
            scratch_shapes=[
                pltpu.VMEM((width, width + hidden_width), bf16),
                pltpu.VMEM((hidden_width, width), bf16),
                pltpu.VMEM((tokens, width), f32),
                pltpu.SemaphoreType.DMA((64,)),
            ],
        ),
        out_shape=[
            jax.ShapeDtypeStruct((tokens, hidden_width), bf16),
            jax.ShapeDtypeStruct((1, hidden_width), f32),
            jax.ShapeDtypeStruct((tokens, width), f32),
            jax.ShapeDtypeStruct((tokens, width), bf16),
            jax.ShapeDtypeStruct((tokens, width), bf16),
            jax.ShapeDtypeStruct((8, width), f32),
        ],
        cost_estimate=small_cost,
        compiler_params=pltpu.CompilerParams(vmem_limit_bytes=32 << 20),
        name="ffn_back",
    )(place, low, slope, total, unit, scale, vectors, *pieces_rest, *pieces_down)


def grad_rows_kernel(x_ref, h_ref, out_ref):
    out_ref[...] = jnp.dot(x_ref[...], h_ref[...], preferred_element_type=f32).astype(bf16)


def grad_rows(inputs_t, grads):
    width, tokens = inputs_t.shape
    columns = grads.shape[1]
    return pl.pallas_call(
        grad_rows_kernel,
        grid=(4,),
        in_specs=[
            pl.BlockSpec((width // 4, tokens), lambda step: (step, 0)),
            pl.BlockSpec((tokens, columns), lambda step: (0, 0)),
        ],
        out_specs=pl.BlockSpec((width // 4, columns), lambda step: (step, 0)),
        out_shape=jax.ShapeDtypeStruct((width, columns), bf16),
        cost_estimate=small_cost,
        compiler_params=pltpu.CompilerParams(vmem_limit_bytes=12 << 20),
        name="grad_rows",
    )(inputs_t, grads)


def grad_columns_kernel(parts, place, *refs):
    count = len(parts)
    ins, keep_ref, send_ref, scratch = (
        refs[: 2 * count],
        refs[2 * count],
        refs[2 * count + 1],
        refs[2 * count + 2 :],
    )
    rows, tile = keep_ref.shape[1], keep_ref.shape[2]
    step = pl.program_id(0)
    first = 0
    for index, steps in enumerate(parts):
        x_ref, h_ref, ordered = ins[2 * index], ins[2 * index + 1], scratch[index]

        @pl.when(step == first)
        def _():
            for slot in range(16):
                mask = slot_mask(slot & 7) + (slot >> 3)
                at = pl.multiple_of((place[0] ^ mask) * rows, 16)
                ordered[pl.ds(slot * rows, rows), :] = x_ref[pl.ds(at, rows), :]

        @pl.when((step >= first) & (step < first + steps))
        def _():
            product = jnp.dot(ordered[...], h_ref[...], preferred_element_type=f32).astype(bf16)
            keep_ref[...] = product[: 8 * rows].reshape(8, rows, tile)
            send_ref[...] = product[8 * rows :].reshape(8, rows, tile)

        first = first + steps


def grad_by_columns(pairs, place, tile):
    width = pairs[0][0].shape[0]
    rows = width // 16
    parts = tuple(sum(grad.shape[1] for grad in grads) // tile for _, _, *grads in pairs)
    steps = sum(parts)
    specs = []
    operands = []
    scratch = []
    first = 0
    for (inputs_t, own, *grads), count in zip(pairs, parts):
        tokens = grads[0].shape[0]
        block = (lambda step, place: (0, place[1])) if own else (lambda step, place: (0, 0))
        specs.append(pl.BlockSpec((width, tokens), block))

        def column(step, place, first=first, count=count):
            return (0, jnp.clip(step - first, 0, count - 1))

        specs.append(pl.BlockSpec((tokens, tile), column))
        operands += [inputs_t, *grads]
        scratch.append(pltpu.VMEM((width, tokens), bf16))
        first = first + count
    half = jax.ShapeDtypeStruct((8, rows, steps * tile), bf16)
    return pl.pallas_call(
        functools.partial(grad_columns_kernel, parts),
        grid_spec=pltpu.PrefetchScalarGridSpec(
            num_scalar_prefetch=1,
            grid=(steps,),
            in_specs=specs,
            out_specs=[pl.BlockSpec((8, rows, tile), lambda step, place: (0, 0, step))] * 2,
            scratch_shapes=scratch,
        ),
        out_shape=[half, half],
        cost_estimate=small_cost,
        compiler_params=pltpu.CompilerParams(vmem_limit_bytes=16 << 20),
        name="grad_columns",
    )(place, *operands)


def key_back_kernel(place, gk_ref, gv_ref, wk_ref, wv_ref, out_ref):
    total = dot_right_t(gk_ref[...], wk_ref[...]) + dot_right_t(gv_ref[...], wv_ref[...])
    out_ref[...] = total.astype(out_ref.dtype)


def own_back_kernel(place, first_ref, gq_ref, gk_ref, gv_ref, wq_ref, wk_ref, wv_ref, out_ref):
    total = dot_right_t(gk_ref[...], wk_ref[...]) + dot_right_t(gv_ref[...], wv_ref[...])
    out_ref[...] = first_ref[...] + total + dot_right_t(gq_ref[...], wq_ref[...])


def input_back(place, weights, grad_keys, grad_values, others):
    width = weights.shape[0]
    tokens = grad_keys.shape[0] // 2
    whole = pl.BlockSpec((tokens, width), lambda step, place: (0, 0))
    row = lambda step, place: ((place[1] if others else 1 - place[1]), 0)
    if others:
        kernel, leading, first, dtype = own_back_kernel, [whole, whole], 0, f32
    else:
        kernel, leading, first, dtype = key_back_kernel, [], 1, bf16
    operands = list(others) + [grad_keys, grad_values] + [weights] * (3 - first)
    specs = [pl.BlockSpec((tokens, width), row)] * 2
    for block in range(first, 3):
        specs.append(pl.BlockSpec((width, width), lambda step, place, block=block: (0, block)))
    return pl.pallas_call(
        kernel,
        grid_spec=pltpu.PrefetchScalarGridSpec(
            num_scalar_prefetch=1, grid=(1,), in_specs=leading + specs, out_specs=whole
        ),
        out_shape=jax.ShapeDtypeStruct((tokens, width), dtype),
        cost_estimate=small_cost,
        compiler_params=pltpu.CompilerParams(vmem_limit_bytes=16 << 20),
        name="input_back",
    )(place, *operands)


def back_rows(values, mask):
    return jnp.where(mask, pltpu.roll(values, dilation, 0), 0.0)


def ahead_rows(values, mask):
    return jnp.where(mask, pltpu.roll(values, values.shape[0] - dilation, 0), 0.0)


def tap_sums(grads, inputs, ahead, back):
    terms = (grads * back_rows(inputs, back), grads * inputs, grads * ahead_rows(inputs, ahead), grads)
    return [jnp.sum(term, axis=0, keepdims=True) for term in terms]


def small_sums_kernel(
    own_ref, other_ref, x_ref, x_other_ref, mask_ref, gq_ref, gv_ref, one_ref, two_ref, up_ref, table_ref, out_ref
):
    width = own_ref.shape[1]
    mask = mask_ref[...] > 0.0
    own = tap_sums(own_ref[...], x_ref[...].astype(f32), mask[:, 0:1], mask[:, 1:2])
    other = tap_sums(
        other_ref[...].astype(f32), x_other_ref[...].astype(f32), mask[:, 2:3], mask[:, 3:4]
    )
    rows = [a + b for a, b in zip(own, other)]
    for ref in (gq_ref, gv_ref):
        rows.append(jnp.sum(ref[...].astype(f32), axis=0, keepdims=True))
    rows.append(jnp.zeros((2, width), f32))
    out_ref[0:8] = jnp.concatenate(rows, axis=0)
    out_ref[8:16] = one_ref[...]
    out_ref[16:24] = two_ref[...]
    count = up_ref.shape[1] // width
    for index in range(count):
        out_ref[24 + index : 25 + index] = up_ref[:, index * width : (index + 1) * width]
    for index in range(3 * HEADS):
        row, lane = 28 + index // 6, index % 6 * LANES
        table = table_ref[index // 3]
        out_ref[row : row + 1, lane : lane + LANES] = table[index % 3 : index % 3 + 1]
    out_ref[34:40] = jnp.zeros((6, width), f32)


def small_sums(*operands):
    return pl.pallas_call(
        small_sums_kernel,
        out_shape=jax.ShapeDtypeStruct((40, operands[0].shape[1]), f32),
        cost_estimate=small_cost,
        compiler_params=pltpu.CompilerParams(vmem_limit_bytes=24 << 20),
        name="small_sums",
    )(*operands)


def state_back_kernel(own_ref, other_ref, mask_ref, tap_ref, out_ref):
    grads = own_ref[...] + other_ref[...].astype(f32)
    mask = mask_ref[...] > 0.0
    total = grads + tap_ref[1:2] * grads
    total = total + tap_ref[0:1] * ahead_rows(grads, mask[:, 0:1])
    total = total + tap_ref[2:3] * back_rows(grads, mask[:, 1:2])
    out_ref[...] = total.astype(bf16)


def state_back(own, other, masks, taps):
    return pl.pallas_call(
        state_back_kernel,
        out_shape=jax.ShapeDtypeStruct(own.shape, bf16),
        cost_estimate=small_cost,
        compiler_params=pltpu.CompilerParams(vmem_limit_bytes=20 << 20),
        name="state_back",
    )(own, other, masks, taps)


def first_half_kernel(place, keep_near, part_near, keep_far, part_far, held_ref, out_ref):
    held_ref[...] = keep_near[...].astype(f32) + part_near[...].astype(f32)
    out_ref[...] = (keep_far[...].astype(f32) + part_far[...].astype(f32)).astype(bf16)


def halve_call(place, keep, partner, specs, half_shape, steps):
    near, far, out = specs
    return pl.pallas_call(
        first_half_kernel,
        grid_spec=pltpu.PrefetchScalarGridSpec(
            num_scalar_prefetch=1,
            grid=(steps,),
            in_specs=[near, near, far, far],
            out_specs=[out, out],
        ),
        out_shape=[
            jax.ShapeDtypeStruct(half_shape, f32),
            jax.ShapeDtypeStruct(half_shape, bf16),
        ],
        cost_estimate=small_cost,
        compiler_params=pltpu.CompilerParams(vmem_limit_bytes=12 << 20),
        name="halve",
    )(place, keep, partner, keep, partner)


def halve_across(place, keep, partner):
    _, rows, width = keep.shape
    near = pl.BlockSpec((1, rows, width), lambda step, place: (step, 0, 0))
    far = pl.BlockSpec((1, rows, width), lambda step, place: (step + 4, 0, 0))
    return halve_call(place, keep, partner, (near, far, near), (4, rows, width), 4)


def halve_plane(place, keep, partner):
    _, rows, width = keep.shape
    block = (2, rows, width // 2)
    near = pl.BlockSpec(block, lambda step, place: (step, 0, place[1]))
    far = pl.BlockSpec(block, lambda step, place: (step, 0, 1 - place[1]))
    out = pl.BlockSpec(block, lambda step, place: (step, 0, 0))
    return halve_call(place, keep, partner, (near, far, out), (8, rows, width // 2), 4)


def column_kernel(held_ref, across_ref, own_ref, *sends):
    own_ref[...] = held_ref[0] + across_ref[0].astype(f32)
    for step, send in enumerate(sends, 1):
        send[...] = (held_ref[step] + across_ref[step].astype(f32)).astype(bf16)


def column_sends(held, across):
    _, rows, width = held.shape
    tile = 384
    out = pl.BlockSpec((rows, tile), lambda step: (0, step))
    block = pl.BlockSpec((4, rows, tile), lambda step: (0, 0, step))
    own, *sends = pl.pallas_call(
        column_kernel,
        grid=(width // tile,),
        in_specs=[block, block],
        out_specs=[out] * 4,
        out_shape=[jax.ShapeDtypeStruct((rows, width), f32)]
        + [jax.ShapeDtypeStruct((rows, width), bf16)] * 3,
        cost_estimate=small_cost,
        compiler_params=pltpu.CompilerParams(vmem_limit_bytes=12 << 20),
        name="column_sends",
    )(held, across)
    return own, sends


def column_arrivals(sends):
    return [exchange(send, 4 * step) for step, send in enumerate(sends, 1)]


def column_total(own, arrived):
    total = own
    for part in arrived:
        total = total + part.astype(f32)
    return total.astype(bf16)


def half_columns(values, first):
    half = values.shape[-1] // 2
    return jnp.where(first, values[..., :half], values[..., half:])


def summed_rows(pairs):
    grads = jnp.concatenate([plain_dot(*pair).astype(bf16) for pair in pairs], axis=1)
    shard = lax.psum_scatter(grads, "page", scatter_dimension=0, tiled=True)
    return shard.astype(f32) + swap(shard).astype(f32)


def page_bounds(segments, is_text):
    pages = jnp.arange(PAGES, dtype=jnp.int32)
    low = jnp.sum(segments[None, :] < pages[:, None], axis=1, dtype=jnp.int32)
    high = jnp.sum(segments[None, :] <= pages[:, None], axis=1, dtype=jnp.int32)
    own_low = jnp.where(is_text, low, pages * PATCH)
    own_high = jnp.where(is_text, high, (pages + 1) * PATCH)

    def aligned(start):
        return jnp.minimum(start // 16 * 16, TEXT - WINDOW)

    return jnp.concatenate([aligned(own_low), own_low, own_high, aligned(low), low, high])


def sum_everywhere(values):
    count = lax.axis_size("page")
    if count & (count - 1):
        values = lax.psum(values, "page")
    else:
        step = 1
        while step < count:
            values = values + lax.ppermute(values, "page", [(i, i ^ step) for i in range(count)])
            step = step * 2
    return values + swap(values)


def swap(values):
    return lax.ppermute(values, "mod", [(0, 1), (1, 0)])


def local(
    states,
    cotangent,
    segments,
    box_x,
    box_y,
    conv_weight,
    conv_bias,
    w_query,
    b_query,
    w_key,
    w_value,
    b_value,
    w_out,
    b_out,
    table_pos,
    table_x,
    table_y,
    gain_one,
    bias_one,
    w_up,
    b_up,
    w_down,
    b_down,
    gain_two,
    bias_two,
):
    is_text = lax.axis_index("mod") == 0
    d_model = states.shape[3]
    own_low = states[0, 0]
    rows_each = w_query.shape[0]
    d_ff = w_up.shape[1]
    fast = lax.axis_size("page") == 16 and rows_each % 16 == 0 and w_down.shape[0] % 16 == 0
    place = jnp.stack([lax.axis_index("page"), lax.axis_index("mod")]).astype(jnp.int32)
    pack_qkv = jnp.concatenate([w_query, w_key, w_value], axis=1)
    pack_rest = jnp.concatenate([w_out, w_up], axis=1)
    other_low = swap(own_low)
    if fast:
        split = (pack_rest.shape[1] // 2 + 127) // 256 * 256
        column_qkv = column_of(half_columns(pack_qkv, is_text))
        parts_near = column_parts(after(half_columns(pack_rest[:, :split], is_text), column_qkv))
        pieces_qkv = half_pieces(column_qkv)
        w_down = after(w_down, column_qkv)
        column_near = jnp.stack([after(part, pieces_qkv[0]) for part in parts_near])
        parts_far = column_parts(after(pack_rest[:, split:], column_near))
        pieces_near = half_pieces(column_near)
        pieces_qkv[2] = after(pieces_qkv[2], pieces_near[0])
        pieces_qkv[3] = exchange(pieces_qkv[2], 1)
        groups_qkv = (("halves", 0),)
    else:
        groups_qkv = (("full", 0),)
        pieces_qkv = [lax.all_gather(pack_qkv, "page", axis=0, tiled=True)]
    full_down = lax.all_gather(w_down, "page", axis=0, tiled=True)

    page_ids, pos_bins, bins_x, bins_y = token_ids(segments[0], box_x[0], box_y[0])
    bounds = page_bounds(segments[0], is_text)
    own_pages = jnp.where(is_text, page_ids[0], page_ids[1])
    features = bin_features(pos_bins.reshape(-1), bins_x.reshape(-1), bins_y.reshape(-1))
    flipped = bin_features(
        POS_BINS - 1 - pos_bins.reshape(-1),
        BOX_BINS - 1 - bins_x.reshape(-1),
        BOX_BINS - 1 - bins_y.reshape(-1),
    )
    own_feats = jnp.where(is_text, features[:TEXT], features[TEXT:])
    own_flip = jnp.where(is_text, flipped[:TEXT], flipped[TEXT:])
    tables = jnp.stack(
        [
            jnp.pad(table_pos, ((0, 0), (0, LANES - table_pos.shape[1]))),
            jnp.pad(table_x, ((0, 0), (0, LANES - table_x.shape[1]))),
            jnp.pad(table_y, ((0, 0), (0, LANES - table_y.shape[1]))),
        ],
        axis=1,
    )
    tables = jnp.pad(tables, ((0, 0), (0, 5), (0, 0)))

    own_states = own_low.astype(f32)
    mixed = dilated_mix(own_states, own_pages, conv_weight, conv_bias)
    mixed_low = mixed.astype(bf16)
    other_pages = jnp.where(is_text, page_ids[1], page_ids[0])
    other_mixed = dilated_mix(other_low.astype(f32), other_pages, conv_weight, conv_bias)
    other_mixed = other_mixed.astype(bf16)
    masks = jnp.pad(
        jnp.stack(
            [
                own_pages == shifted(own_pages, dilation, -1),
                own_pages == shifted(own_pages, -dilation, -1),
                other_pages == shifted(other_pages, dilation, -1),
                other_pages == shifted(other_pages, -dilation, -1),
            ],
            axis=1,
        ).astype(f32),
        ((0, 0), (0, LANES - 4)),
    )
    mixed_all = jnp.concatenate(
        [jnp.where(is_text, mixed_low, other_mixed), jnp.where(is_text, other_mixed, mixed_low)],
        axis=0,
    )
    mixed_t = mixed_all.T
    if fast:
        early = (mixed_all, mixed_t, features, tables, bounds, own_flip, own_feats, masks)
        pieces_qkv[0] = after(pieces_qkv[0], *early)
    biases = jnp.concatenate([b_query, jnp.zeros_like(b_value), b_value])[None]
    queries, keys_values, full_qkv = project(place, mixed_all, biases, groups_qkv, pieces_qkv)
    attend_in = queries
    if fast:
        column_far = jnp.stack([after(part, queries) for part in parts_far])
        across_far = exchange(column_far, 2)
        attend_in = after(queries, column_far)
    context = attend(bounds, attend_in, keys_values, features, own_feats, tables)
    if fast:
        pieces_near[2] = after(pieces_near[2], context)
        pieces_near[3] = exchange(pieces_near[2], 1)
        across_far = after(across_far, context)
        pieces_rest = pieces_near + row_pieces(column_far, across_far)
        groups_rest = (("halves", 0), ("rows", split))
    else:
        pieces_rest = [lax.all_gather(pack_rest, "page", axis=0, tiled=True)]
        groups_rest = (("full", 0),)
    vectors = jnp.stack(
        [b_out, gain_one, bias_one, b_down, gain_two, bias_two, jnp.zeros_like(b_out), b_out]
    )
    unit, scale, normed_low, normed_t, active, active_t, slope = up_forward(
        place, context, mixed, vectors, b_up[None], groups_rest, pieces_rest
    )
    groups_down = (("full", 0),)
    pieces_down = [full_down]
    output_row, grad_sum_two, grad_ffn, small_two = down_forward(
        place, active, unit, vectors, cotangent[0, 0], groups_down, pieces_down
    )
    rows_down = grad_rows(active_t, grad_ffn)
    shard_down = lax.psum_scatter(rows_down, "page", scatter_dimension=0, tiled=True)
    context_t = context.T
    grad_hidden, grad_b_up, grad_first, grad_branch, grad_context, small_one = ffn_back(
        place,
        after(grad_ffn, rows_down),
        slope,
        grad_sum_two,
        unit,
        scale,
        vectors,
        groups_rest,
        pieces_rest,
        groups_down,
        pieces_down,
    )
    attend_in = grad_context
    if fast:
        pairs = [(context_t, False, grad_branch), (normed_t, False, grad_hidden)]
        keep_rest, send_rest = grad_by_columns(pairs, place, d_model)
        partner_rest = exchange(send_rest, 1)
        held_rest, plane_out = halve_plane(place, keep_rest, partner_rest)
        plane_rest = swap(plane_out)
        attend_in = after(grad_context, plane_out)
    else:
        shard_rest = summed_rows([(context_t, grad_branch), (normed_t, grad_hidden)])
    grad_queries, grad_keys, grad_values, grad_tables = attend_back(
        bounds, queries, keys_values, attend_in, features, own_feats, own_flip, tables, 0, PAIRS
    )
    grad_keys_in, grad_queries_in = grad_keys, grad_queries
    if fast:
        plane_rest = after(plane_rest, grad_queries)
        held_rest, across_out = halve_across(place, held_rest, plane_rest)
        across_rest = exchange(across_out, 2)
        grad_queries_in = after(grad_queries, across_out)
    pairs = [(mixed_t, True, grad_queries_in), (mixed_t, False, grad_keys), (mixed_t, False, grad_values)]
    if fast:
        keep_qkv, send_qkv = grad_by_columns(pairs, place, d_model)
        partner_qkv = exchange(send_qkv, 1)
        grad_keys_in = after(grad_keys, send_qkv)
    else:
        shard_qkv = summed_rows(
            [(mixed_low.T, grad_queries), (mixed_t, grad_keys), (mixed_t, grad_values)]
        )
    to_other = input_back(place, full_qkv, grad_keys_in, grad_values, ())
    from_other = swap(to_other)
    grad_values_in = grad_values
    if fast:
        partner_qkv = after(partner_qkv, to_other)
        held_qkv, across_out = halve_across(place, keep_qkv, partner_qkv)
        across_qkv = exchange(across_out, 2)
        across_rest = after(across_rest, across_out)
        own_rest, sends_rest = column_sends(held_rest, across_rest)
        arrived_rest = column_arrivals(sends_rest)
        grad_values_in = after(grad_values, *sends_rest)
    own_part = input_back(place, full_qkv, grad_keys, grad_values_in, (grad_first, grad_queries))
    packed = small_sums(
        own_part,
        to_other,
        own_low,
        other_low,
        masks,
        grad_queries,
        grad_values,
        small_one,
        small_two,
        grad_b_up,
        grad_tables,
    )
    packed = sum_everywhere(packed)
    if fast:
        across_qkv = after(across_qkv, packed)
        own_qkv, sends_qkv = column_sends(held_qkv, across_qkv)
        arrived_qkv = column_arrivals(sends_qkv)
        from_other = after(from_other, *sends_qkv)
    grad_in = state_back(own_part, from_other, masks, jnp.pad(conv_weight, ((0, 5), (0, 0))))
    if fast:
        arrived_rest = [after(part, grad_in) for part in arrived_rest]
        total_rest = column_total(own_rest, arrived_rest)
        far_rest = swap(total_rest)
        arrived_qkv = [after(part, total_rest) for part in arrived_qkv]
        total_qkv = column_total(own_qkv, arrived_qkv)
        far_qkv = swap(total_qkv)
    g_tables = packed[28:34].reshape(HEADS, 3, LANES)
    shard_down = shard_down.astype(f32) + swap(shard_down).astype(f32)
    if fast:
        shard_rest = jnp.where(
            is_text,
            jnp.concatenate([total_rest, far_rest], axis=1),
            jnp.concatenate([far_rest, total_rest], axis=1),
        ).astype(f32)
        shard_qkv = total_qkv.astype(f32) + far_qkv.astype(f32)
    return (
        output_row[None, None],
        grad_in[None, None],
        packed[0:3],
        packed[3],
        shard_qkv[:, :d_model],
        packed[4],
        shard_qkv[:, d_model : 2 * d_model],
        shard_qkv[:, 2 * d_model :],
        packed[5],
        shard_rest[:, :d_model],
        packed[10],
        g_tables[:, 0, : table_pos.shape[1]],
        g_tables[:, 1, 64 : 64 + table_x.shape[1]],
        g_tables[:, 2, 64 : 64 + table_y.shape[1]],
        packed[8],
        packed[9],
        shard_rest[:, d_model:],
        packed[24:28].reshape(d_ff),
        shard_down,
        packed[18],
        packed[16],
        packed[17],
    )


def solution(mesh):
    rows = P("mod", "page", None, None)
    ids = P("page", None)
    cut = P("page", None)
    return jax.shard_map(
        local,
        mesh=mesh,
        in_specs=(
            rows, rows, ids, ids, ids, P(), P(), cut, P(), cut, cut, P(), cut,
            P(), P(), P(), P(), P(), P(), cut, P(), cut, P(), P(), P(),
        ),
        out_specs=(
            rows, rows, P(), P(), cut, P(), cut, cut, P(), cut, P(), P(), P(),
            P(), P(), P(), cut, P(), cut, P(), P(), P(),
        ),
        check_vma=False,
    )
```

```python
import functools

import jax
import jax.numpy as jnp
import numpy as np
from jax import lax
from jax.experimental import pallas as pl
from jax.experimental.pallas import tpu as pltpu
from jax.sharding import PartitionSpec as P

HEADS = 12
HEAD = 64
GRID = 8
PAGES = 8
POS_BINS = 64
BOX_BINS = 32
PATCH = 64
TEXT = 512
PAIRS = HEADS // 2
LANES = 2 * HEAD
WINDOW = 144
KEYS = WINDOW + PATCH

dilation = 2
small_cost = pl.CostEstimate(flops=1000, bytes_accessed=1000, transcendentals=0)
norm_eps = 1e-05
mask_fill = -1000000000.0
erfc_poly = (
    0.2367515965428487,
    0.24062179898991767,
    0.18865103029313968,
    0.2877518531132804,
    -0.1648672439458568,
    0.4765735350541787,
    -0.34041833366480423,
    0.07493571514857543,
)
bf16 = jnp.bfloat16
f32 = jnp.float32


def shifted(values, offset, fill_value):
    padding = jnp.full((abs(offset),) + values.shape[1:], fill_value, values.dtype)
    if offset > 0:
        return jnp.concatenate([values[offset:], padding], axis=0)
    return jnp.concatenate([padding, values[:offset]], axis=0)


def dilated_mix(inputs, page_ids, conv_weight, conv_bias):
    summed = inputs + conv_bias + conv_weight[1] * inputs
    for tap_index, offset in ((0, -dilation), (2, dilation)):
        moved_rows = shifted(inputs, offset, 0.0)
        moved_pages = shifted(page_ids, offset, -1)
        same_page = (moved_pages == page_ids)[:, None]
        summed = summed + conv_weight[tap_index] * jnp.where(same_page, moved_rows, 0.0)
    return summed


def bin_features(pos_bins, bins_x, bins_y):
    return jnp.concatenate(
        [
            jax.nn.one_hot(pos_bins, POS_BINS, dtype=bf16),
            jax.nn.one_hot(bins_x, BOX_BINS, dtype=bf16),
            jax.nn.one_hot(bins_y, BOX_BINS, dtype=bf16),
        ],
        axis=1,
    )


def token_ids(text_pages, text_x, text_y):
    text_index = jnp.arange(TEXT, dtype=jnp.int32)
    text_pos = text_index * POS_BINS // TEXT
    patch_pos = text_index % PATCH * POS_BINS // PATCH
    patch_page = text_index // PATCH
    patch_x = text_index % GRID * BOX_BINS // GRID
    patch_y = text_index // GRID % GRID * BOX_BINS // GRID
    page_ids = jnp.stack([text_pages, patch_page])
    pos_bins = jnp.stack([text_pos, patch_pos])
    bins_x = jnp.stack([text_x, patch_x])
    bins_y = jnp.stack([text_y, patch_y])
    return (page_ids, pos_bins, bins_x, bins_y)


def plain_dot(left_side, right_side):
    return jnp.dot(left_side, right_side, preferred_element_type=f32)


def dot_left_t(left_side, right_side):
    return lax.dot_general(
        left_side, right_side, (((0,), (0,)), ((), ())), preferred_element_type=f32
    )


def dot_right_t(left_side, right_side):
    return lax.dot_general(
        left_side, right_side, (((1,), (1,)), ((), ())), preferred_element_type=f32
    )


def iota(shape, axis):
    return lax.broadcasted_iota(jnp.int32, shape, axis)


def bias_block(table_rows):
    pos_part = pltpu.roll(
        jnp.broadcast_to(table_rows[0:1], (POS_BINS, LANES)), 65, 1, stride=1, stride_axis=0
    )
    x_part = pltpu.roll(
        jnp.broadcast_to(table_rows[1:2], (BOX_BINS, LANES)), 33, 1, stride=1, stride_axis=0
    )
    y_part = pltpu.roll(
        jnp.broadcast_to(table_rows[2:3], (BOX_BINS, LANES)), 65, 1, stride=1, stride_axis=0
    )
    lane = iota((POS_BINS, LANES), 1)
    pos_part = jnp.where(lane < POS_BINS, pos_part, 0.0)
    lane = iota((BOX_BINS, LANES), 1)
    x_part = jnp.where((lane >= 64) & (lane < 96), x_part, 0.0)
    y_part = jnp.where(lane >= 96, y_part, 0.0)
    return jnp.concatenate([pos_part, x_part, y_part], axis=0).astype(bf16)


def diagonal_sums(grad_block):
    lane = iota((POS_BINS, LANES), 1)
    pos_part = jnp.where(lane < POS_BINS, grad_block[:64], 0.0)
    lane = iota((BOX_BINS, LANES), 1)
    x_part = jnp.where((lane >= 64) & (lane < 96), grad_block[64:96], 0.0)
    y_part = jnp.where(lane >= 96, grad_block[96:], 0.0)
    pos_part = pltpu.roll(pos_part, 0, 1, stride=1, stride_axis=0)
    x_part = pltpu.roll(x_part, 0, 1, stride=1, stride_axis=0)
    y_part = pltpu.roll(y_part, 96, 1, stride=1, stride_axis=0)
    rows = [jnp.sum(part, axis=0, keepdims=True) for part in (pos_part, x_part, y_part)]
    return jnp.concatenate(rows + [jnp.zeros((5, LANES), f32)], axis=0)


def stacked_heads(rows, low_lane):
    zero = jnp.zeros_like(rows)
    return jnp.concatenate(
        [jnp.where(low_lane, rows, zero), jnp.where(low_lane, zero, rows)], axis=0
    )


def page_operands(page, bounds, q_ref, k_ref, feat_ref, lookup):
    own_at = pl.multiple_of(bounds[page], 16)
    key_at = pl.multiple_of(bounds[3 * PAGES + page], 16)
    low_lane = iota((WINDOW, LANES), 1) < HEAD
    queries = stacked_heads(q_ref[pl.ds(own_at, WINDOW), :], low_lane)
    rel = jnp.concatenate(
        [lookup[pl.ds(own_at, WINDOW), :LANES], lookup[pl.ds(own_at, WINDOW), LANES:]], axis=0
    )
    query_side = jnp.concatenate([rel, queries], axis=1)
    patch_rows = pl.ds(TEXT + PATCH * page, PATCH)
    text_rows = pl.ds(key_at, WINDOW)
    key_side = jnp.concatenate(
        [
            jnp.concatenate([feat_ref[text_rows, :], k_ref[text_rows, :]], axis=1),
            jnp.concatenate([feat_ref[patch_rows, :], k_ref[patch_rows, :]], axis=1),
        ],
        axis=0,
    )
    own_row = iota((WINDOW, LANES), 0) + own_at
    own_ok = (own_row >= bounds[PAGES + page]) & (own_row < bounds[2 * PAGES + page])
    return own_at, key_at, low_lane, own_ok, queries, query_side, key_side, text_rows, patch_rows


def attend_kernel(bounds, q_ref, k_ref, v_ref, feat_ref, own_feat_ref, table_ref, context_ref, lookup):
    blocks = jnp.concatenate([bias_block(table_ref[0]), bias_block(table_ref[1])], axis=1)
    lookup[...] = jnp.dot(own_feat_ref[...], blocks, preferred_element_type=f32).astype(bf16)
    for page in range(PAGES):
        own_at, key_at, low_lane, own_ok, queries, query_side, key_side, text_rows, patch_rows = (
            page_operands(page, bounds, q_ref, k_ref, feat_ref, lookup)
        )
        scores = dot_right_t(query_side, key_side)
        column = iota((1, KEYS), 1)
        key_row = column + key_at
        key_ok = (column >= WINDOW) | (
            (key_row >= bounds[4 * PAGES + page]) & (key_row < bounds[5 * PAGES + page])
        )
        scores = jnp.where(key_ok, scores, mask_fill)
        row_max = jnp.max(scores, axis=1, keepdims=True)
        weights = jnp.exp(scores - row_max)
        total = jnp.sum(weights, axis=1, keepdims=True)
        prob = (weights * (1.0 / total)).astype(bf16)
        values = jnp.concatenate([v_ref[text_rows, :], v_ref[patch_rows, :]], axis=0)
        mixed = jnp.dot(prob, values, preferred_element_type=f32)
        picked = jnp.where(low_lane, mixed[:WINDOW], mixed[WINDOW:])
        before = context_ref[pl.ds(own_at, WINDOW), :].astype(f32)
        context_ref[pl.ds(own_at, WINDOW), :] = jnp.where(own_ok, picked, before).astype(bf16)


def attend_back_kernel(
    bounds,
    q_ref,
    k_ref,
    v_ref,
    grad_ref,
    feat_ref,
    own_feat_ref,
    flip_feat_ref,
    table_ref,
    grad_q_ref,
    grad_k_ref,
    grad_v_ref,
    grad_table_ref,
    lookup,
    grad_lookup,
):
    blocks = jnp.concatenate([bias_block(table_ref[0]), bias_block(table_ref[1])], axis=1)
    lookup[...] = jnp.dot(own_feat_ref[...], blocks, preferred_element_type=f32).astype(bf16)
    for page in range(PAGES):
        own_at, key_at, low_lane, own_ok, queries, query_side, key_side, text_rows, patch_rows = (
            page_operands(page, bounds, q_ref, k_ref, feat_ref, lookup)
        )
        scores = dot_right_t(key_side, query_side)
        row = iota((KEYS, 1), 0)
        key_row = row + key_at
        key_in = (key_row >= bounds[4 * PAGES + page]) & (key_row < bounds[5 * PAGES + page])
        scores = jnp.where((row >= WINDOW) | key_in, scores, mask_fill)
        col_max = jnp.max(scores, axis=0, keepdims=True)
        weights = jnp.exp(scores - col_max)
        total = jnp.sum(weights, axis=0, keepdims=True)
        prob = weights * (1.0 / total)
        grad_rows = grad_ref[pl.ds(own_at, WINDOW), :]
        grad_rows = jnp.where(own_ok, grad_rows, jnp.zeros_like(grad_rows))
        grads = stacked_heads(grad_rows, low_lane)
        values = jnp.concatenate([v_ref[text_rows, :], v_ref[patch_rows, :]], axis=0)
        grad_prob = dot_right_t(values, grads)
        inner = jnp.sum(prob * grad_prob, axis=0, keepdims=True)
        grad_scores = (prob * (grad_prob - inner)).astype(bf16)
        grad_v = jnp.dot(prob.astype(bf16), grads, preferred_element_type=f32)
        grad_k = jnp.dot(grad_scores, queries, preferred_element_type=f32)
        back = dot_left_t(grad_scores, key_side)
        grad_q = jnp.where(low_lane, back[:WINDOW, LANES:], back[WINDOW:, LANES:]) * 0.125
        own_rows = pl.ds(own_at, WINDOW)
        before = grad_q_ref[own_rows, :].astype(f32)
        grad_q_ref[own_rows, :] = jnp.where(own_ok, grad_q, before).astype(bf16)
        grad_lookup[own_rows, :LANES] = jnp.where(
            own_ok, back[:WINDOW, :LANES], grad_lookup[own_rows, :LANES]
        )
        grad_lookup[own_rows, LANES:] = jnp.where(
            own_ok, back[WINDOW:, :LANES], grad_lookup[own_rows, LANES:]
        )
        wide_row = iota((WINDOW, LANES), 0) + key_at
        text_ok = (wide_row >= bounds[4 * PAGES + page]) & (wide_row < bounds[5 * PAGES + page])
        for grad, ref in ((grad_k, grad_k_ref), (grad_v, grad_v_ref)):
            before = ref[text_rows, :].astype(f32)
            ref[text_rows, :] = jnp.where(text_ok, grad[:WINDOW], before).astype(bf16)
            ref[patch_rows, :] = grad[WINDOW:].astype(bf16)
    grad_high = grad_lookup[...].astype(bf16)
    grad_rest = (grad_lookup[...] - grad_high.astype(f32)).astype(bf16)
    flip = flip_feat_ref[...]
    grad_block = dot_left_t(flip, grad_high) + dot_left_t(flip, grad_rest)
    grad_table_ref[0] = diagonal_sums(grad_block[:, :LANES])
    grad_table_ref[1] = diagonal_sums(grad_block[:, LANES:])


def column_spec(rows, first=0):
    return pl.BlockSpec((rows, LANES), lambda pair, bounds: (0, pair + first))


def tables_spec(first=0):
    return pl.BlockSpec((2, 8, LANES), lambda pair, bounds: (pair + first, 0, 0))


def whole_spec(rows):
    return pl.BlockSpec((rows, LANES), lambda pair, bounds: (0, 0))


def attend(bounds, queries, keys_values, features, own_features, tables):
    return pl.pallas_call(
        attend_kernel,
        grid_spec=pltpu.PrefetchScalarGridSpec(
            num_scalar_prefetch=1,
            grid=(PAIRS,),
            in_specs=[
                column_spec(TEXT),
                column_spec(2 * TEXT),
                column_spec(2 * TEXT, PAIRS),
                whole_spec(2 * TEXT),
                whole_spec(TEXT),
                tables_spec(),
            ],
            out_specs=column_spec(TEXT),
            scratch_shapes=[pltpu.VMEM((TEXT, 2 * LANES), bf16)],
        ),
        out_shape=jax.ShapeDtypeStruct((TEXT, HEADS * HEAD), bf16),
        cost_estimate=small_cost,
        name="attend",
    )(bounds, queries, keys_values, keys_values, features, own_features, tables)


def attend_back(
    bounds, queries, keys_values, grad_context, features, own_features, flip, tables, first, count
):
    return pl.pallas_call(
        attend_back_kernel,
        grid_spec=pltpu.PrefetchScalarGridSpec(
            num_scalar_prefetch=1,
            grid=(count,),
            in_specs=[
                column_spec(TEXT, first),
                column_spec(2 * TEXT, first),
                column_spec(2 * TEXT, PAIRS + first),
                column_spec(TEXT, first),
                whole_spec(2 * TEXT),
                whole_spec(TEXT),
                whole_spec(TEXT),
                tables_spec(first),
            ],
            out_specs=[
                column_spec(TEXT),
                column_spec(2 * TEXT),
                column_spec(2 * TEXT),
                tables_spec(),
            ],
            scratch_shapes=[
                pltpu.VMEM((TEXT, 2 * LANES), bf16),
                pltpu.VMEM((TEXT, 2 * LANES), f32),
            ],
        ),
        out_shape=[
            jax.ShapeDtypeStruct((TEXT, count * LANES), bf16),
            jax.ShapeDtypeStruct((2 * TEXT, count * LANES), bf16),
            jax.ShapeDtypeStruct((2 * TEXT, count * LANES), bf16),
            jax.ShapeDtypeStruct((2 * count, 8, LANES), f32),
        ],
        cost_estimate=small_cost,
        name="attend_back",
    )(
        bounds,
        queries,
        keys_values,
        keys_values,
        grad_context,
        features,
        own_features,
        flip,
        tables,
    )


def exchange(values, mask):
    count = lax.axis_size("page")
    return lax.ppermute(values, "page", [(i, i ^ mask) for i in range(count)])


def after(value, *earlier):
    return lax.optimization_barrier((value, *earlier))[0]


def slot_mask(slot):
    return (slot & 3) * 4 + (slot >> 2) * 2


def project_kernel(groups, place, mixed_ref, bias_ref, *refs):
    *pieces, query_ref, both_ref, weight_ref, sems = refs
    width = mixed_ref.shape[1]
    tokens = query_ref.shape[0]
    for copy in start_rows(place, groups, pieces, weight_ref, sems):
        copy.wait()
    own = mixed_ref[pl.ds(pl.multiple_of(place[1] * tokens, 16), tokens), :]
    queries = jnp.dot(own, weight_ref[:, :width], preferred_element_type=f32) + bias_ref[:, :width]
    query_ref[...] = (queries.astype(bf16).astype(f32) * 0.125).astype(bf16)
    for part in range(2):
        rows = pl.ds(part * tokens, tokens)
        for column in (1, 2):
            at = slice(column * width, (column + 1) * width)
            out = slice((column - 1) * width, column * width)
            values = jnp.dot(mixed_ref[rows, :], weight_ref[:, at], preferred_element_type=f32)
            both_ref[rows, out] = (values + bias_ref[:, at]).astype(bf16)


def project(place, mixed, biases, groups, pieces):
    rows, width = mixed.shape
    vmem = pl.BlockSpec(memory_space=pltpu.VMEM)
    return pl.pallas_call(
        functools.partial(project_kernel, groups),
        grid_spec=pltpu.PrefetchScalarGridSpec(
            num_scalar_prefetch=1,
            grid=(),
            in_specs=[vmem] * 2 + any_specs(len(pieces)),
            out_specs=[vmem] * 3,
            scratch_shapes=[pltpu.SemaphoreType.DMA((32,))],
        ),
        out_shape=[
            jax.ShapeDtypeStruct((rows // 2, width), bf16),
            jax.ShapeDtypeStruct((rows, 2 * width), bf16),
            jax.ShapeDtypeStruct((width, 3 * width), bf16),
        ],
        cost_estimate=small_cost,
        compiler_params=pltpu.CompilerParams(vmem_limit_bytes=16 << 20),
        name="project",
    )(place, mixed, biases, *pieces)


def column_parts(shard):
    return [shard] + [exchange(shard, 4 * step) for step in (1, 2, 3)]


def half_pieces(column):
    eight = jnp.concatenate([column, exchange(column, 2)])
    far = swap(eight)
    return [eight, exchange(eight, 1), far, exchange(far, 1)]


def row_pieces(column, across):
    return [column, exchange(column, 1), across, exchange(across, 1)]


def column_of(shard):
    return jnp.stack(column_parts(shard))


def start_rows(place, groups, refs, full, sems, first=0):
    copies = []
    for kind, column in groups:
        if kind == "full":
            piece, *refs = refs
            width = piece.shape[1]
            target = full.at[:, pl.ds(column, width)]
            copies.append(pltpu.make_async_copy(piece, target, sems.at[first + len(copies)]))
            continue
        pieces, refs = refs[:4], refs[4:]
        _, rows, width = pieces[0].shape
        for index in range(32 if kind == "halves" else 16):
            at = column
            if kind == "halves":
                source, slot = index >> 3, index & 7
                mask = slot_mask(slot) + (source & 1)
                at = pl.multiple_of(column + (place[1] ^ (source >> 1)) * width, 128)
            else:
                source, slot = index & 3, index >> 2
                mask = slot * 4 + source
            row = pl.multiple_of((place[0] ^ mask) * rows, 16)
            copies.append(
                pltpu.make_async_copy(
                    pieces[source].at[slot],
                    full.at[pl.ds(row, rows), pl.ds(at, width)],
                    sems.at[first + len(copies)],
                )
            )
    for copy in copies:
        copy.start()
    return copies


def gelu_parts(values):
    size = jnp.abs(values)
    t = 1.0 / (1.0 + (0.42 * 0.7071067811865476) * size)
    poly = jnp.full_like(t, erfc_poly[-1])
    for coefficient in erfc_poly[-2::-1]:
        poly = poly * t + coefficient
    bell = jnp.exp(-0.5 * values * values)
    tail = (0.5 * t) * (poly * bell)
    cdf = jnp.where(values >= 0.0, 1.0 - tail, tail)
    return values * cdf, cdf + (values * 0.3989422804014327) * bell


def normalized(values):
    centered = values - jnp.mean(values, axis=1, keepdims=True)
    variance = jnp.mean(centered * centered, axis=1, keepdims=True)
    scale = lax.rsqrt(variance + norm_eps)
    return centered * scale, scale


def norm_back(grads, unit, scale, gain):
    scaled = grads * gain
    mean = jnp.mean(scaled, axis=1, keepdims=True)
    inner = jnp.mean(scaled * unit, axis=1, keepdims=True)
    return scale * (scaled - mean - unit * inner)


def up_kernel(groups, place, context_ref, mixed_ref, vec_ref, bias_ref, *refs):
    *pieces, unit_ref, scale_ref, low_ref, low_t_ref, active_ref, active_t_ref, slope_ref = refs[:-4]
    weight, hidden, low, sems = refs[-4:]
    step = pl.program_id(0)
    tiles = pl.num_programs(0) - 1
    width = context_ref.shape[1]
    tile = active_ref.shape[1]

    @pl.when(step == 0)
    def _():
        for copy in start_rows(place, groups, pieces, weight, sems):
            copy.wait()
        branch = jnp.dot(context_ref[...], weight[:, :width], preferred_element_type=f32)
        unit, scale = normalized(mixed_ref[...] + branch + vec_ref[0:1])
        unit_ref[...] = unit
        scale_ref[...] = jnp.broadcast_to(scale, scale_ref.shape)
        normed = (unit * vec_ref[1:2] + vec_ref[2:3]).astype(bf16)
        low[...] = normed
        low_ref[...] = normed
        low_t_ref[...] = normed.T

    def product():
        at = pl.multiple_of(width + step * tile, 128)
        return jnp.dot(low[...], weight[:, pl.ds(at, tile)], preferred_element_type=f32)

    def activate():
        active, slope = gelu_parts(hidden[(step + 1) % 2] + bias_ref[...])
        active = active.astype(bf16)
        active_ref[...] = active
        active_t_ref[...] = active.T
        slope_ref[...] = slope.astype(bf16)

    @pl.when(step == 0)
    def _():
        hidden[step % 2] = product()

    @pl.when((step > 0) & (step < tiles))
    def _():
        hidden[step % 2] = product()
        activate()

    @pl.when(step == tiles)
    def _():
        activate()


def any_specs(count):
    return [pl.BlockSpec(memory_space=pl.ANY)] * count


def up_forward(place, context, mixed, vectors, bias_up, groups, pieces):
    tokens, width = mixed.shape
    hidden_width = bias_up.shape[1]
    tile = 512
    whole = lambda step, place: (0, 0)
    last = lambda step, place: (0, jnp.maximum(step - 1, 0))
    last_t = lambda step, place: (jnp.maximum(step - 1, 0), 0)
    return pl.pallas_call(
        functools.partial(up_kernel, groups),
        grid_spec=pltpu.PrefetchScalarGridSpec(
            num_scalar_prefetch=1,
            grid=(hidden_width // tile + 1,),
            in_specs=[
                pl.BlockSpec((tokens, width), whole),
                pl.BlockSpec((tokens, width), whole),
                pl.BlockSpec(vectors.shape, whole),
                pl.BlockSpec((1, tile), last),
            ]
            + any_specs(len(pieces)),
            out_specs=[
                pl.BlockSpec((tokens, width), whole),
                pl.BlockSpec((tokens, 128), whole),
                pl.BlockSpec((tokens, width), whole),
                pl.BlockSpec((width, tokens), whole),
                pl.BlockSpec((tokens, tile), last),
                pl.BlockSpec((tile, tokens), last_t),
                pl.BlockSpec((tokens, tile), last),
            ],
            scratch_shapes=[
                pltpu.VMEM((width, width + hidden_width), bf16),
                pltpu.VMEM((2, tokens, tile), f32),
                pltpu.VMEM((tokens, width), bf16),
                pltpu.SemaphoreType.DMA((48,)),
            ],
        ),
        out_shape=[
            jax.ShapeDtypeStruct((tokens, width), f32),
            jax.ShapeDtypeStruct((tokens, 128), f32),
            jax.ShapeDtypeStruct((tokens, width), bf16),
            jax.ShapeDtypeStruct((width, tokens), bf16),
            jax.ShapeDtypeStruct((tokens, hidden_width), bf16),
            jax.ShapeDtypeStruct((hidden_width, tokens), bf16),
            jax.ShapeDtypeStruct((tokens, hidden_width), bf16),
        ],
        cost_estimate=small_cost,
        name="up_forward",
    )(place, context, mixed, vectors, bias_up, *pieces)


def down_kernel(groups, place, active_ref, unit_ref, vec_ref, grad_ref, *refs):
    *pieces, out_ref, sum_ref, low_ref, small_ref = refs[:-2]
    weight, sems = refs[-2:]
    for copy in start_rows(place, groups, pieces, weight, sems):
        copy.wait()
    tokens, width = unit_ref.shape
    half = tokens // 2
    smalls = [jnp.zeros((1, width), f32)] * 3
    for part in range(2):
        rows = pl.ds(part * half, half)
        ffn = jnp.dot(active_ref[rows, :], weight[...], preferred_element_type=f32)
        normed = unit_ref[rows, :] * vec_ref[1:2] + vec_ref[2:3]
        unit, scale = normalized(normed + ffn + vec_ref[3:4])
        out_ref[rows, :] = (unit * vec_ref[4:5] + vec_ref[5:6]).astype(bf16)
        grads = grad_ref[rows, :].astype(f32)
        total = norm_back(grads, unit, scale, vec_ref[4:5])
        low = total.astype(bf16)
        sum_ref[rows, :] = total
        low_ref[rows, :] = low
        for index, term in enumerate((grads * unit, grads, low.astype(f32))):
            smalls[index] = smalls[index] + jnp.sum(term, axis=0, keepdims=True)
    small_ref[...] = jnp.concatenate(smalls + [jnp.zeros((5, width), f32)], axis=0)


def down_forward(place, active, unit, vectors, grads, groups, pieces):
    tokens, width = unit.shape
    hidden_width = active.shape[1]
    vmem = pl.BlockSpec(memory_space=pltpu.VMEM)
    return pl.pallas_call(
        functools.partial(down_kernel, groups),
        grid_spec=pltpu.PrefetchScalarGridSpec(
            num_scalar_prefetch=1,
            grid=(),
            in_specs=[vmem] * 4 + any_specs(len(pieces)),
            out_specs=[vmem] * 4,
            scratch_shapes=[
                pltpu.VMEM((hidden_width, width), bf16),
                pltpu.SemaphoreType.DMA((16,)),
            ],
        ),
        out_shape=[
            jax.ShapeDtypeStruct((tokens, width), bf16),
            jax.ShapeDtypeStruct((tokens, width), f32),
            jax.ShapeDtypeStruct((tokens, width), bf16),
            jax.ShapeDtypeStruct((8, width), f32),
        ],
        cost_estimate=small_cost,
        name="down_forward",
    )(place, active, unit, vectors, grads, *pieces)


def ffn_back_kernel(groups, groups_down, count, place, low_ref, slope_ref, sum_ref, unit_ref, scale_ref, vec_ref, *refs):
    rest, down = refs[: count[0]], refs[count[0] : sum(count)]
    hidden_ref, bias_ref, first_ref, branch_ref, context_ref, small_ref = refs[sum(count) : -4]
    weight, weight_down, total, sems = refs[-4:]
    step = pl.program_id(0)
    tokens, width = unit_ref.shape
    tile = slope_ref.shape[1]
    half = tokens // 2

    @pl.when(step == 0)
    def _():
        copies = start_rows(place, groups_down, down, weight_down, sems)
        copies += start_rows(place, groups, rest, weight, sems, 16)
        total[...] = sum_ref[...]
        for copy in copies:
            copy.wait()

    rows_down = weight_down[pl.ds(pl.multiple_of(step * tile, 128), tile), :]
    columns = weight[:, pl.ds(pl.multiple_of(width + step * tile, 128), tile)]
    bias = jnp.zeros((1, tile), f32)
    for part in range(2):
        rows = pl.ds(part * half, half)
        grads = (dot_right_t(low_ref[rows, :], rows_down) * slope_ref[rows, :].astype(f32)).astype(bf16)
        hidden_ref[rows, :] = grads
        bias = bias + jnp.sum(grads.astype(f32), axis=0, keepdims=True)
        total[rows, :] += dot_right_t(grads, columns)
    bias_ref[...] = bias

    @pl.when(step == pl.num_programs(0) - 1)
    def _():
        grads = total[...]
        unit = unit_ref[...]
        first = norm_back(grads, unit, scale_ref[:, 0:1], vec_ref[1:2])
        branch = first.astype(bf16)
        first_ref[...] = first
        branch_ref[...] = branch
        context_ref[...] = dot_right_t(branch, weight[:, :width]).astype(bf16)
        smalls = [
            jnp.sum(term, axis=0, keepdims=True)
            for term in (grads * unit, grads, branch.astype(f32))
        ]
        small_ref[...] = jnp.concatenate(smalls + [jnp.zeros((5, width), f32)], axis=0)


def ffn_back(
    place, low, slope, total, unit, scale, vectors, groups, pieces_rest, groups_down, pieces_down
):
    tokens, width = unit.shape
    hidden_width = slope.shape[1]
    tile = 512
    count = (len(pieces_rest), len(pieces_down))
    whole = lambda step, place: (0, 0)
    column = lambda step, place: (0, step)
    return pl.pallas_call(
        functools.partial(ffn_back_kernel, groups, groups_down, count),
        grid_spec=pltpu.PrefetchScalarGridSpec(
            num_scalar_prefetch=1,
            grid=(hidden_width // tile,),
            in_specs=[
                pl.BlockSpec((tokens, width), whole),
                pl.BlockSpec((tokens, tile), column),
                pl.BlockSpec((tokens, width), whole),
                pl.BlockSpec((tokens, width), whole),
                pl.BlockSpec((tokens, 128), whole),
                pl.BlockSpec(vectors.shape, whole),
            ]
            + any_specs(sum(count)),
            out_specs=[
                pl.BlockSpec((tokens, tile), column),
                pl.BlockSpec((1, tile), column),
                pl.BlockSpec((tokens, width), whole),
                pl.BlockSpec((tokens, width), whole),
                pl.BlockSpec((tokens, width), whole),
                pl.BlockSpec((8, width), whole),
            ],
            scratch_shapes=[
                pltpu.VMEM((width, width + hidden_width), bf16),
                pltpu.VMEM((hidden_width, width), bf16),
                pltpu.VMEM((tokens, width), f32),
                pltpu.SemaphoreType.DMA((64,)),
            ],
        ),
        out_shape=[
            jax.ShapeDtypeStruct((tokens, hidden_width), bf16),
            jax.ShapeDtypeStruct((1, hidden_width), f32),
            jax.ShapeDtypeStruct((tokens, width), f32),
            jax.ShapeDtypeStruct((tokens, width), bf16),
            jax.ShapeDtypeStruct((tokens, width), bf16),
            jax.ShapeDtypeStruct((8, width), f32),
        ],
        cost_estimate=small_cost,
        name="ffn_back",
    )(place, low, slope, total, unit, scale, vectors, *pieces_rest, *pieces_down)


def grad_rows_kernel(x_ref, h_ref, out_ref):
    out_ref[...] = jnp.dot(x_ref[...], h_ref[...], preferred_element_type=f32).astype(bf16)


def grad_rows(inputs_t, grads):
    width, tokens = inputs_t.shape
    columns = grads.shape[1]
    return pl.pallas_call(
        grad_rows_kernel,
        grid=(4,),
        in_specs=[
            pl.BlockSpec((width // 4, tokens), lambda step: (step, 0)),
            pl.BlockSpec((tokens, columns), lambda step: (0, 0)),
        ],
        out_specs=pl.BlockSpec((width // 4, columns), lambda step: (step, 0)),
        out_shape=jax.ShapeDtypeStruct((width, columns), bf16),
        cost_estimate=small_cost,
        compiler_params=pltpu.CompilerParams(vmem_limit_bytes=12 << 20),
        name="grad_rows",
    )(inputs_t, grads)


def grad_columns_kernel(parts, place, *refs):
    count = len(parts)
    ins, keep_ref, send_ref, scratch = (
        refs[: 2 * count],
        refs[2 * count],
        refs[2 * count + 1],
        refs[2 * count + 2 :],
    )
    rows, tile = keep_ref.shape[1], keep_ref.shape[2]
    step = pl.program_id(0)
    first = 0
    for index, steps in enumerate(parts):
        x_ref, h_ref, ordered = ins[2 * index], ins[2 * index + 1], scratch[index]

        @pl.when(step == first)
        def _():
            for slot in range(16):
                mask = slot_mask(slot & 7) + (slot >> 3)
                at = pl.multiple_of((place[0] ^ mask) * rows, 16)
                ordered[pl.ds(slot * rows, rows), :] = x_ref[pl.ds(at, rows), :]

        @pl.when((step >= first) & (step < first + steps))
        def _():
            product = jnp.dot(ordered[...], h_ref[...], preferred_element_type=f32).astype(bf16)
            keep_ref[...] = product[: 8 * rows].reshape(8, rows, tile)
            send_ref[...] = product[8 * rows :].reshape(8, rows, tile)

        first = first + steps


def grad_by_columns(pairs, place, tile):
    width = pairs[0][0].shape[0]
    rows = width // 16
    parts = tuple(sum(grad.shape[1] for grad in grads) // tile for _, _, *grads in pairs)
    steps = sum(parts)
    specs = []
    operands = []
    scratch = []
    first = 0
    for (inputs_t, own, *grads), count in zip(pairs, parts):
        tokens = grads[0].shape[0]
        block = (lambda step, place: (0, place[1])) if own else (lambda step, place: (0, 0))
        specs.append(pl.BlockSpec((width, tokens), block))

        def column(step, place, first=first, count=count):
            return (0, jnp.clip(step - first, 0, count - 1))

        specs.append(pl.BlockSpec((tokens, tile), column))
        operands += [inputs_t, *grads]
        scratch.append(pltpu.VMEM((width, tokens), bf16))
        first = first + count
    half = jax.ShapeDtypeStruct((8, rows, steps * tile), bf16)
    return pl.pallas_call(
        functools.partial(grad_columns_kernel, parts),
        grid_spec=pltpu.PrefetchScalarGridSpec(
            num_scalar_prefetch=1,
            grid=(steps,),
            in_specs=specs,
            out_specs=[pl.BlockSpec((8, rows, tile), lambda step, place: (0, 0, step))] * 2,
            scratch_shapes=scratch,
        ),
        out_shape=[half, half],
        cost_estimate=small_cost,
        compiler_params=pltpu.CompilerParams(vmem_limit_bytes=16 << 20),
        name="grad_columns",
    )(place, *operands)


def key_back_kernel(place, gk_ref, gv_ref, wk_ref, wv_ref, out_ref):
    total = dot_right_t(gk_ref[...], wk_ref[...]) + dot_right_t(gv_ref[...], wv_ref[...])
    out_ref[...] = total.astype(out_ref.dtype)


def own_back_kernel(place, first_ref, gq_ref, gk_ref, gv_ref, wq_ref, wk_ref, wv_ref, out_ref):
    total = dot_right_t(gk_ref[...], wk_ref[...]) + dot_right_t(gv_ref[...], wv_ref[...])
    out_ref[...] = first_ref[...] + total + dot_right_t(gq_ref[...], wq_ref[...])


def input_back(place, weights, grad_keys, grad_values, others):
    width = weights.shape[0]
    tokens = grad_keys.shape[0] // 2
    whole = pl.BlockSpec((tokens, width), lambda step, place: (0, 0))
    row = lambda step, place: ((place[1] if others else 1 - place[1]), 0)
    if others:
        kernel, leading, first, dtype = own_back_kernel, [whole, whole], 0, f32
    else:
        kernel, leading, first, dtype = key_back_kernel, [], 1, bf16
    operands = list(others) + [grad_keys, grad_values] + [weights] * (3 - first)
    specs = [pl.BlockSpec((tokens, width), row)] * 2
    for block in range(first, 3):
        specs.append(pl.BlockSpec((width, width), lambda step, place, block=block: (0, block)))
    return pl.pallas_call(
        kernel,
        grid_spec=pltpu.PrefetchScalarGridSpec(
            num_scalar_prefetch=1, grid=(1,), in_specs=leading + specs, out_specs=whole
        ),
        out_shape=jax.ShapeDtypeStruct((tokens, width), dtype),
        cost_estimate=small_cost,
        compiler_params=pltpu.CompilerParams(vmem_limit_bytes=16 << 20),
        name="input_back",
    )(place, *operands)


def back_rows(values, mask):
    return jnp.where(mask, pltpu.roll(values, dilation, 0), 0.0)


def ahead_rows(values, mask):
    return jnp.where(mask, pltpu.roll(values, values.shape[0] - dilation, 0), 0.0)


def tap_sums(grads, inputs, ahead, back):
    terms = (grads * back_rows(inputs, back), grads * inputs, grads * ahead_rows(inputs, ahead), grads)
    return [jnp.sum(term, axis=0, keepdims=True) for term in terms]


def small_sums_kernel(
    own_ref, other_ref, x_ref, x_other_ref, mask_ref, gq_ref, gv_ref, one_ref, two_ref, up_ref, table_ref, out_ref
):
    width = own_ref.shape[1]
    mask = mask_ref[...] > 0.0
    own = tap_sums(own_ref[...], x_ref[...].astype(f32), mask[:, 0:1], mask[:, 1:2])
    other = tap_sums(
        other_ref[...].astype(f32), x_other_ref[...].astype(f32), mask[:, 2:3], mask[:, 3:4]
    )
    rows = [a + b for a, b in zip(own, other)]
    for ref in (gq_ref, gv_ref):
        rows.append(jnp.sum(ref[...].astype(f32), axis=0, keepdims=True))
    rows.append(jnp.zeros((2, width), f32))
    out_ref[0:8] = jnp.concatenate(rows, axis=0)
    out_ref[8:16] = one_ref[...]
    out_ref[16:24] = two_ref[...]
    count = up_ref.shape[1] // width
    for index in range(count):
        out_ref[24 + index : 25 + index] = up_ref[:, index * width : (index + 1) * width]
    for index in range(3 * HEADS):
        row, lane = 28 + index // 6, index % 6 * LANES
        table = table_ref[index // 3]
        out_ref[row : row + 1, lane : lane + LANES] = table[index % 3 : index % 3 + 1]
    out_ref[34:40] = jnp.zeros((6, width), f32)


def small_sums(*operands):
    return pl.pallas_call(
        small_sums_kernel,
        out_shape=jax.ShapeDtypeStruct((40, operands[0].shape[1]), f32),
        cost_estimate=small_cost,
        compiler_params=pltpu.CompilerParams(vmem_limit_bytes=24 << 20),
        name="small_sums",
    )(*operands)


def state_back_kernel(own_ref, other_ref, mask_ref, tap_ref, out_ref):
    grads = own_ref[...] + other_ref[...].astype(f32)
    mask = mask_ref[...] > 0.0
    total = grads + tap_ref[1:2] * grads
    total = total + tap_ref[0:1] * ahead_rows(grads, mask[:, 0:1])
    total = total + tap_ref[2:3] * back_rows(grads, mask[:, 1:2])
    out_ref[...] = total.astype(bf16)


def state_back(own, other, masks, taps):
    return pl.pallas_call(
        state_back_kernel,
        out_shape=jax.ShapeDtypeStruct(own.shape, bf16),
        cost_estimate=small_cost,
        compiler_params=pltpu.CompilerParams(vmem_limit_bytes=20 << 20),
        name="state_back",
    )(own, other, masks, taps)


def first_half_kernel(place, keep_near, part_near, keep_far, part_far, held_ref, out_ref):
    held_ref[...] = keep_near[...].astype(f32) + part_near[...].astype(f32)
    out_ref[...] = (keep_far[...].astype(f32) + part_far[...].astype(f32)).astype(bf16)


def halve_call(place, keep, partner, specs, half_shape, steps):
    near, far, out = specs
    return pl.pallas_call(
        first_half_kernel,
        grid_spec=pltpu.PrefetchScalarGridSpec(
            num_scalar_prefetch=1,
            grid=(steps,),
            in_specs=[near, near, far, far],
            out_specs=[out, out],
        ),
        out_shape=[
            jax.ShapeDtypeStruct(half_shape, f32),
            jax.ShapeDtypeStruct(half_shape, bf16),
        ],
        cost_estimate=small_cost,
        compiler_params=pltpu.CompilerParams(vmem_limit_bytes=12 << 20),
        name="halve",
    )(place, keep, partner, keep, partner)


def halve_across(place, keep, partner):
    _, rows, width = keep.shape
    near = pl.BlockSpec((1, rows, width), lambda step, place: (step, 0, 0))
    far = pl.BlockSpec((1, rows, width), lambda step, place: (step + 4, 0, 0))
    return halve_call(place, keep, partner, (near, far, near), (4, rows, width), 4)


def halve_plane(place, keep, partner):
    _, rows, width = keep.shape
    block = (2, rows, width // 2)
    near = pl.BlockSpec(block, lambda step, place: (step, 0, place[1]))
    far = pl.BlockSpec(block, lambda step, place: (step, 0, 1 - place[1]))
    out = pl.BlockSpec(block, lambda step, place: (step, 0, 0))
    return halve_call(place, keep, partner, (near, far, out), (8, rows, width // 2), 4)


def column_kernel(held_ref, across_ref, own_ref, *sends):
    own_ref[...] = held_ref[0] + across_ref[0].astype(f32)
    for step, send in enumerate(sends, 1):
        send[...] = (held_ref[step] + across_ref[step].astype(f32)).astype(bf16)


def column_sends(held, across):
    _, rows, width = held.shape
    tile = 384
    out = pl.BlockSpec((rows, tile), lambda step: (0, step))
    block = pl.BlockSpec((4, rows, tile), lambda step: (0, 0, step))
    own, *sends = pl.pallas_call(
        column_kernel,
        grid=(width // tile,),
        in_specs=[block, block],
        out_specs=[out] * 4,
        out_shape=[jax.ShapeDtypeStruct((rows, width), f32)]
        + [jax.ShapeDtypeStruct((rows, width), bf16)] * 3,
        cost_estimate=small_cost,
        compiler_params=pltpu.CompilerParams(vmem_limit_bytes=12 << 20),
        name="column_sends",
    )(held, across)
    return own, sends


def column_arrivals(sends):
    return [exchange(send, 4 * step) for step, send in enumerate(sends, 1)]


def column_total(own, arrived):
    total = own
    for part in arrived:
        total = total + part.astype(f32)
    return total.astype(bf16)


def half_columns(values, first):
    half = values.shape[-1] // 2
    return jnp.where(first, values[..., :half], values[..., half:])


def summed_rows(pairs):
    grads = jnp.concatenate([plain_dot(*pair).astype(bf16) for pair in pairs], axis=1)
    shard = lax.psum_scatter(grads, "page", scatter_dimension=0, tiled=True)
    return shard.astype(f32) + swap(shard).astype(f32)


def page_bounds(segments, is_text):
    pages = jnp.arange(PAGES, dtype=jnp.int32)
    low = jnp.sum(segments[None, :] < pages[:, None], axis=1, dtype=jnp.int32)
    high = jnp.sum(segments[None, :] <= pages[:, None], axis=1, dtype=jnp.int32)
    own_low = jnp.where(is_text, low, pages * PATCH)
    own_high = jnp.where(is_text, high, (pages + 1) * PATCH)

    def aligned(start):
        return jnp.minimum(start // 16 * 16, TEXT - WINDOW)

    return jnp.concatenate([aligned(own_low), own_low, own_high, aligned(low), low, high])


def both_sum(values, mask):
    return values + exchange(values, mask)


def swap(values):
    return lax.ppermute(values, "mod", [(0, 1), (1, 0)])


def local(
    states,
    cotangent,
    segments,
    box_x,
    box_y,
    conv_weight,
    conv_bias,
    w_query,
    b_query,
    w_key,
    w_value,
    b_value,
    w_out,
    b_out,
    table_pos,
    table_x,
    table_y,
    gain_one,
    bias_one,
    w_up,
    b_up,
    w_down,
    b_down,
    gain_two,
    bias_two,
):
    is_text = lax.axis_index("mod") == 0
    d_model = states.shape[3]
    own_low = states[0, 0]
    rows_each = w_query.shape[0]
    d_ff = w_up.shape[1]
    fast = lax.axis_size("page") == 16 and rows_each % 16 == 0 and w_down.shape[0] % 16 == 0
    place = jnp.stack([lax.axis_index("page"), lax.axis_index("mod")]).astype(jnp.int32)
    pack_qkv = jnp.concatenate([w_query, w_key, w_value], axis=1)
    pack_rest = jnp.concatenate([w_out, w_up], axis=1)
    other_low = swap(own_low)
    if fast:
        split = (pack_rest.shape[1] // 2 + 127) // 256 * 256
        column_qkv = column_of(half_columns(pack_qkv, is_text))
        parts_near = column_parts(after(half_columns(pack_rest[:, :split], is_text), column_qkv))
        pieces_qkv = half_pieces(column_qkv)
        column_near = jnp.stack([after(part, pieces_qkv[0]) for part in parts_near])
        parts_far = column_parts(after(pack_rest[:, split:], column_near))
        pieces_near = half_pieces(column_near)
        w_down = after(w_down, pieces_near[0])
        pieces_qkv[2] = after(pieces_qkv[2], pieces_near[0])
        pieces_qkv[3] = exchange(pieces_qkv[2], 1)
        groups_qkv = (("halves", 0),)
    else:
        groups_qkv = (("full", 0),)
        pieces_qkv = [lax.all_gather(pack_qkv, "page", axis=0, tiled=True)]
    full_down = lax.all_gather(w_down, "page", axis=0, tiled=True)

    page_ids, pos_bins, bins_x, bins_y = token_ids(segments[0], box_x[0], box_y[0])
    bounds = page_bounds(segments[0], is_text)
    own_pages = jnp.where(is_text, page_ids[0], page_ids[1])
    features = bin_features(pos_bins.reshape(-1), bins_x.reshape(-1), bins_y.reshape(-1))
    flipped = bin_features(
        POS_BINS - 1 - pos_bins.reshape(-1),
        BOX_BINS - 1 - bins_x.reshape(-1),
        BOX_BINS - 1 - bins_y.reshape(-1),
    )
    own_feats = jnp.where(is_text, features[:TEXT], features[TEXT:])
    own_flip = jnp.where(is_text, flipped[:TEXT], flipped[TEXT:])
    tables = jnp.stack(
        [
            jnp.pad(table_pos, ((0, 0), (0, LANES - table_pos.shape[1]))),
            jnp.pad(table_x, ((0, 0), (0, LANES - table_x.shape[1]))),
            jnp.pad(table_y, ((0, 0), (0, LANES - table_y.shape[1]))),
        ],
        axis=1,
    )
    tables = jnp.pad(tables, ((0, 0), (0, 5), (0, 0)))

    own_states = own_low.astype(f32)
    mixed = dilated_mix(own_states, own_pages, conv_weight, conv_bias)
    mixed_low = mixed.astype(bf16)
    other_pages = jnp.where(is_text, page_ids[1], page_ids[0])
    other_mixed = dilated_mix(other_low.astype(f32), other_pages, conv_weight, conv_bias)
    other_mixed = other_mixed.astype(bf16)
    masks = jnp.pad(
        jnp.stack(
            [
                own_pages == shifted(own_pages, dilation, -1),
                own_pages == shifted(own_pages, -dilation, -1),
                other_pages == shifted(other_pages, dilation, -1),
                other_pages == shifted(other_pages, -dilation, -1),
            ],
            axis=1,
        ).astype(f32),
        ((0, 0), (0, LANES - 4)),
    )
    mixed_all = jnp.concatenate(
        [jnp.where(is_text, mixed_low, other_mixed), jnp.where(is_text, other_mixed, mixed_low)],
        axis=0,
    )
    mixed_t = mixed_all.T
    vectors = jnp.stack(
        [b_out, gain_one, bias_one, b_down, gain_two, bias_two, jnp.zeros_like(b_out), b_out]
    )
    biases = jnp.concatenate([b_query, jnp.zeros_like(b_value), b_value])[None]
    taps = jnp.pad(conv_weight, ((0, 5), (0, 0)))
    bias_up = b_up[None]
    if fast:
        early = (mixed_all, mixed_t, features, tables, bounds, own_flip, own_feats, masks)
        early += (vectors, biases, taps, bias_up)
        pieces_qkv[0] = after(pieces_qkv[0], *early)
    queries, keys_values, full_qkv = project(place, mixed_all, biases, groups_qkv, pieces_qkv)
    attend_in = queries
    if fast:
        column_far = jnp.stack([after(part, queries) for part in parts_far])
        across_far = exchange(column_far, 2)
        attend_in = after(queries, column_far)
    context = attend(bounds, attend_in, keys_values, features, own_feats, tables)
    if fast:
        pieces_near[2] = after(pieces_near[2], context)
        pieces_near[3] = exchange(pieces_near[2], 1)
        across_far = after(across_far, context)
        pieces_rest = pieces_near + row_pieces(column_far, across_far)
        groups_rest = (("halves", 0), ("rows", split))
    else:
        pieces_rest = [lax.all_gather(pack_rest, "page", axis=0, tiled=True)]
        groups_rest = (("full", 0),)
    unit, scale, normed_low, normed_t, active, active_t, slope = up_forward(
        place, context, mixed, vectors, bias_up, groups_rest, pieces_rest
    )
    groups_down = (("full", 0),)
    pieces_down = [full_down]
    output_row, grad_sum_two, grad_ffn, small_two = down_forward(
        place, active, unit, vectors, cotangent[0, 0], groups_down, pieces_down
    )
    rows_down = grad_rows(active_t, grad_ffn)
    shard_down = lax.psum_scatter(rows_down, "page", scatter_dimension=0, tiled=True)
    context_t = context.T
    grad_hidden, grad_b_up, grad_first, grad_branch, grad_context, small_one = ffn_back(
        place,
        after(grad_ffn, rows_down),
        slope,
        grad_sum_two,
        unit,
        scale,
        vectors,
        groups_rest,
        pieces_rest,
        groups_down,
        pieces_down,
    )
    attend_in = grad_context
    if fast:
        pairs = [(context_t, False, grad_branch), (normed_t, False, grad_hidden)]
        keep_rest, send_rest = grad_by_columns(pairs, place, d_model)
        partner_rest = exchange(send_rest, 1)
        held_rest, plane_out = halve_plane(place, keep_rest, partner_rest)
        plane_rest = swap(plane_out)
        attend_in = after(grad_context, plane_out)
    else:
        shard_rest = summed_rows([(context_t, grad_branch), (normed_t, grad_hidden)])
    grad_queries, grad_keys, grad_values, grad_tables = attend_back(
        bounds, queries, keys_values, attend_in, features, own_feats, own_flip, tables, 0, PAIRS
    )
    grad_keys_in, grad_queries_in = grad_keys, grad_queries
    if fast:
        plane_rest = after(plane_rest, grad_queries)
        held_rest, across_out = halve_across(place, held_rest, plane_rest)
        across_rest = exchange(across_out, 2)
        shard_down = after(shard_down, grad_queries)
        shard_down = shard_down.astype(f32) + swap(shard_down).astype(f32)
        grad_queries_in = after(grad_queries, across_out, shard_down)
    pairs = [(mixed_t, True, grad_queries_in), (mixed_t, False, grad_keys), (mixed_t, False, grad_values)]
    if fast:
        keep_qkv, send_qkv = grad_by_columns(pairs, place, d_model)
        partner_qkv = exchange(send_qkv, 1)
        grad_keys_in = after(grad_keys, send_qkv)
    else:
        shard_down = shard_down.astype(f32) + swap(shard_down).astype(f32)
        shard_qkv = summed_rows(
            [(mixed_low.T, grad_queries), (mixed_t, grad_keys), (mixed_t, grad_values)]
        )
    to_other = input_back(place, full_qkv, grad_keys_in, grad_values, ())
    from_other = swap(to_other)
    grad_values_in = grad_values
    if fast:
        partner_qkv = after(partner_qkv, to_other)
        held_qkv, across_out = halve_across(place, keep_qkv, partner_qkv)
        across_qkv = exchange(across_out, 2)
        grad_values_in = after(grad_values, across_out)
    own_part = input_back(place, full_qkv, grad_keys, grad_values_in, (grad_first, grad_queries))
    packed = small_sums(
        own_part,
        to_other,
        own_low,
        other_low,
        masks,
        grad_queries,
        grad_values,
        small_one,
        small_two,
        grad_b_up,
        grad_tables,
    )
    if fast:
        packed = both_sum(packed, 1)
        across_rest = after(across_rest, packed)
        own_rest, sends_rest = column_sends(held_rest, across_rest)
        arrived_rest = column_arrivals(sends_rest)
        packed = both_sum(after(packed, *sends_rest), 2)
        across_qkv = after(across_qkv, packed)
        own_qkv, sends_qkv = column_sends(held_qkv, across_qkv)
        arrived_qkv = column_arrivals(sends_qkv)
        from_other = after(from_other, *sends_qkv)
    else:
        packed = lax.psum(packed, ("mod", "page"))
    grad_in = state_back(own_part, from_other, masks, taps)
    if fast:
        arrived_rest = [after(part, grad_in) for part in arrived_rest]
        total_rest = column_total(own_rest, arrived_rest)
        far_rest = swap(total_rest)
        packed = after(packed, total_rest)
        packed = packed + swap(packed)
        arrived_qkv = [after(part, packed) for part in arrived_qkv]
        total_qkv = column_total(own_qkv, arrived_qkv)
        far_qkv = swap(total_qkv)
        packed = both_sum(both_sum(after(packed, total_qkv), 4), 8)
    g_tables = packed[28:34].reshape(HEADS, 3, LANES)
    if fast:
        shard_rest = jnp.where(
            is_text,
            jnp.concatenate([total_rest, far_rest], axis=1),
            jnp.concatenate([far_rest, total_rest], axis=1),
        ).astype(f32)
        shard_qkv = total_qkv.astype(f32) + far_qkv.astype(f32)
    return (
        output_row[None, None],
        grad_in[None, None],
        packed[0:3],
        packed[3],
        shard_qkv[:, :d_model],
        packed[4],
        shard_qkv[:, d_model : 2 * d_model],
        shard_qkv[:, 2 * d_model :],
        packed[5],
        shard_rest[:, :d_model],
        packed[10],
        g_tables[:, 0, : table_pos.shape[1]],
        g_tables[:, 1, 64 : 64 + table_x.shape[1]],
        g_tables[:, 2, 64 : 64 + table_y.shape[1]],
        packed[8],
        packed[9],
        shard_rest[:, d_model:],
        packed[24:28].reshape(d_ff),
        shard_down,
        packed[18],
        packed[16],
        packed[17],
    )


def solution(mesh):
    rows = P("mod", "page", None, None)
    ids = P("page", None)
    cut = P("page", None)
    return jax.shard_map(
        local,
        mesh=mesh,
        in_specs=(
            rows, rows, ids, ids, ids, P(), P(), cut, P(), cut, cut, P(), cut,
            P(), P(), P(), P(), P(), P(), cut, P(), cut, P(), P(), P(),
        ),
        out_specs=(
            rows, rows, P(), P(), cut, P(), cut, cut, P(), cut, P(), P(), P(),
            P(), P(), P(), cut, P(), cut, P(), P(), P(),
        ),
        check_vma=False,
    )
```

```python
import functools

import jax
import jax.numpy as jnp
import numpy as np
from jax import lax
from jax.experimental import pallas as pl
from jax.experimental.pallas import tpu as pltpu
from jax.sharding import PartitionSpec as P

HEADS = 12
HEAD = 64
GRID = 8
PAGES = 8
POS_BINS = 64
BOX_BINS = 32
PATCH = 64
TEXT = 512
PAIRS = HEADS // 2
LANES = 2 * HEAD
WINDOW = 144
KEYS = WINDOW + PATCH

dilation = 2
small_cost = pl.CostEstimate(flops=1000, bytes_accessed=1000, transcendentals=0)
norm_eps = 1e-05
mask_fill = -1000000000.0
erfc_poly = (
    0.2367515965428487,
    0.24062179898991767,
    0.18865103029313968,
    0.2877518531132804,
    -0.1648672439458568,
    0.4765735350541787,
    -0.34041833366480423,
    0.07493571514857543,
)
bf16 = jnp.bfloat16
f32 = jnp.float32


def shifted(values, offset, fill_value):
    padding = jnp.full((abs(offset),) + values.shape[1:], fill_value, values.dtype)
    if offset > 0:
        return jnp.concatenate([values[offset:], padding], axis=0)
    return jnp.concatenate([padding, values[:offset]], axis=0)


def dilated_mix(inputs, page_ids, conv_weight, conv_bias):
    summed = inputs + conv_bias + conv_weight[1] * inputs
    for tap_index, offset in ((0, -dilation), (2, dilation)):
        moved_rows = shifted(inputs, offset, 0.0)
        moved_pages = shifted(page_ids, offset, -1)
        same_page = (moved_pages == page_ids)[:, None]
        summed = summed + conv_weight[tap_index] * jnp.where(same_page, moved_rows, 0.0)
    return summed


def bin_features(pos_bins, bins_x, bins_y):
    return jnp.concatenate(
        [
            jax.nn.one_hot(pos_bins, POS_BINS, dtype=bf16),
            jax.nn.one_hot(bins_x, BOX_BINS, dtype=bf16),
            jax.nn.one_hot(bins_y, BOX_BINS, dtype=bf16),
        ],
        axis=1,
    )


def token_ids(text_pages, text_x, text_y):
    text_index = jnp.arange(TEXT, dtype=jnp.int32)
    text_pos = text_index * POS_BINS // TEXT
    patch_pos = text_index % PATCH * POS_BINS // PATCH
    patch_page = text_index // PATCH
    patch_x = text_index % GRID * BOX_BINS // GRID
    patch_y = text_index // GRID % GRID * BOX_BINS // GRID
    page_ids = jnp.stack([text_pages, patch_page])
    pos_bins = jnp.stack([text_pos, patch_pos])
    bins_x = jnp.stack([text_x, patch_x])
    bins_y = jnp.stack([text_y, patch_y])
    return (page_ids, pos_bins, bins_x, bins_y)


def plain_dot(left_side, right_side):
    return jnp.dot(left_side, right_side, preferred_element_type=f32)


def dot_left_t(left_side, right_side):
    return lax.dot_general(
        left_side, right_side, (((0,), (0,)), ((), ())), preferred_element_type=f32
    )


def dot_right_t(left_side, right_side):
    return lax.dot_general(
        left_side, right_side, (((1,), (1,)), ((), ())), preferred_element_type=f32
    )


def iota(shape, axis):
    return lax.broadcasted_iota(jnp.int32, shape, axis)


def bias_block(table_rows):
    pos_part = pltpu.roll(
        jnp.broadcast_to(table_rows[0:1], (POS_BINS, LANES)), 65, 1, stride=1, stride_axis=0
    )
    x_part = pltpu.roll(
        jnp.broadcast_to(table_rows[1:2], (BOX_BINS, LANES)), 33, 1, stride=1, stride_axis=0
    )
    y_part = pltpu.roll(
        jnp.broadcast_to(table_rows[2:3], (BOX_BINS, LANES)), 65, 1, stride=1, stride_axis=0
    )
    lane = iota((POS_BINS, LANES), 1)
    pos_part = jnp.where(lane < POS_BINS, pos_part, 0.0)
    lane = iota((BOX_BINS, LANES), 1)
    x_part = jnp.where((lane >= 64) & (lane < 96), x_part, 0.0)
    y_part = jnp.where(lane >= 96, y_part, 0.0)
    return jnp.concatenate([pos_part, x_part, y_part], axis=0).astype(bf16)


def diagonal_sums(grad_block):
    lane = iota((POS_BINS, LANES), 1)
    pos_part = jnp.where(lane < POS_BINS, grad_block[:64], 0.0)
    lane = iota((BOX_BINS, LANES), 1)
    x_part = jnp.where((lane >= 64) & (lane < 96), grad_block[64:96], 0.0)
    y_part = jnp.where(lane >= 96, grad_block[96:], 0.0)
    pos_part = pltpu.roll(pos_part, 0, 1, stride=1, stride_axis=0)
    x_part = pltpu.roll(x_part, 0, 1, stride=1, stride_axis=0)
    y_part = pltpu.roll(y_part, 96, 1, stride=1, stride_axis=0)
    rows = [jnp.sum(part, axis=0, keepdims=True) for part in (pos_part, x_part, y_part)]
    return jnp.concatenate(rows + [jnp.zeros((5, LANES), f32)], axis=0)


def stacked_heads(rows, low_lane):
    zero = jnp.zeros_like(rows)
    return jnp.concatenate(
        [jnp.where(low_lane, rows, zero), jnp.where(low_lane, zero, rows)], axis=0
    )


def page_operands(page, bounds, q_ref, k_ref, feat_ref, lookup):
    own_at = pl.multiple_of(bounds[page], 16)
    key_at = pl.multiple_of(bounds[3 * PAGES + page], 16)
    low_lane = iota((WINDOW, LANES), 1) < HEAD
    queries = stacked_heads(q_ref[pl.ds(own_at, WINDOW), :], low_lane)
    rel = jnp.concatenate(
        [lookup[pl.ds(own_at, WINDOW), :LANES], lookup[pl.ds(own_at, WINDOW), LANES:]], axis=0
    )
    query_side = jnp.concatenate([rel, queries], axis=1)
    patch_rows = pl.ds(TEXT + PATCH * page, PATCH)
    text_rows = pl.ds(key_at, WINDOW)
    key_side = jnp.concatenate(
        [
            jnp.concatenate([feat_ref[text_rows, :], k_ref[text_rows, :]], axis=1),
            jnp.concatenate([feat_ref[patch_rows, :], k_ref[patch_rows, :]], axis=1),
        ],
        axis=0,
    )
    own_row = iota((WINDOW, LANES), 0) + own_at
    own_ok = (own_row >= bounds[PAGES + page]) & (own_row < bounds[2 * PAGES + page])
    return own_at, key_at, low_lane, own_ok, queries, query_side, key_side, text_rows, patch_rows


def attend_kernel(bounds, q_ref, k_ref, v_ref, feat_ref, own_feat_ref, table_ref, context_ref, lookup):
    blocks = jnp.concatenate([bias_block(table_ref[0]), bias_block(table_ref[1])], axis=1)
    lookup[...] = jnp.dot(own_feat_ref[...], blocks, preferred_element_type=f32).astype(bf16)
    for page in range(PAGES):
        own_at, key_at, low_lane, own_ok, queries, query_side, key_side, text_rows, patch_rows = (
            page_operands(page, bounds, q_ref, k_ref, feat_ref, lookup)
        )
        scores = dot_right_t(query_side, key_side)
        column = iota((1, KEYS), 1)
        key_row = column + key_at
        key_ok = (column >= WINDOW) | (
            (key_row >= bounds[4 * PAGES + page]) & (key_row < bounds[5 * PAGES + page])
        )
        scores = jnp.where(key_ok, scores, mask_fill)
        row_max = jnp.max(scores, axis=1, keepdims=True)
        weights = jnp.exp(scores - row_max)
        total = jnp.sum(weights, axis=1, keepdims=True)
        prob = (weights * (1.0 / total)).astype(bf16)
        values = jnp.concatenate([v_ref[text_rows, :], v_ref[patch_rows, :]], axis=0)
        mixed = jnp.dot(prob, values, preferred_element_type=f32)
        picked = jnp.where(low_lane, mixed[:WINDOW], mixed[WINDOW:])
        before = context_ref[pl.ds(own_at, WINDOW), :].astype(f32)
        context_ref[pl.ds(own_at, WINDOW), :] = jnp.where(own_ok, picked, before).astype(bf16)


def attend_back_kernel(
    bounds,
    q_ref,
    k_ref,
    v_ref,
    grad_ref,
    feat_ref,
    own_feat_ref,
    flip_feat_ref,
    table_ref,
    grad_q_ref,
    grad_k_ref,
    grad_v_ref,
    grad_table_ref,
    lookup,
    grad_lookup,
):
    blocks = jnp.concatenate([bias_block(table_ref[0]), bias_block(table_ref[1])], axis=1)
    lookup[...] = jnp.dot(own_feat_ref[...], blocks, preferred_element_type=f32).astype(bf16)
    for page in range(PAGES):
        own_at, key_at, low_lane, own_ok, queries, query_side, key_side, text_rows, patch_rows = (
            page_operands(page, bounds, q_ref, k_ref, feat_ref, lookup)
        )
        scores = dot_right_t(key_side, query_side)
        row = iota((KEYS, 1), 0)
        key_row = row + key_at
        key_in = (key_row >= bounds[4 * PAGES + page]) & (key_row < bounds[5 * PAGES + page])
        scores = jnp.where((row >= WINDOW) | key_in, scores, mask_fill)
        col_max = jnp.max(scores, axis=0, keepdims=True)
        weights = jnp.exp(scores - col_max)
        total = jnp.sum(weights, axis=0, keepdims=True)
        prob = weights * (1.0 / total)
        grad_rows = grad_ref[pl.ds(own_at, WINDOW), :]
        grad_rows = jnp.where(own_ok, grad_rows, jnp.zeros_like(grad_rows))
        grads = stacked_heads(grad_rows, low_lane)
        values = jnp.concatenate([v_ref[text_rows, :], v_ref[patch_rows, :]], axis=0)
        grad_prob = dot_right_t(values, grads)
        inner = jnp.sum(prob * grad_prob, axis=0, keepdims=True)
        grad_scores = (prob * (grad_prob - inner)).astype(bf16)
        grad_v = jnp.dot(prob.astype(bf16), grads, preferred_element_type=f32)
        grad_k = jnp.dot(grad_scores, queries, preferred_element_type=f32)
        back = dot_left_t(grad_scores, key_side)
        grad_q = jnp.where(low_lane, back[:WINDOW, LANES:], back[WINDOW:, LANES:]) * 0.125
        own_rows = pl.ds(own_at, WINDOW)
        before = grad_q_ref[own_rows, :].astype(f32)
        grad_q_ref[own_rows, :] = jnp.where(own_ok, grad_q, before).astype(bf16)
        grad_lookup[own_rows, :LANES] = jnp.where(
            own_ok, back[:WINDOW, :LANES], grad_lookup[own_rows, :LANES]
        )
        grad_lookup[own_rows, LANES:] = jnp.where(
            own_ok, back[WINDOW:, :LANES], grad_lookup[own_rows, LANES:]
        )
        wide_row = iota((WINDOW, LANES), 0) + key_at
        text_ok = (wide_row >= bounds[4 * PAGES + page]) & (wide_row < bounds[5 * PAGES + page])
        for grad, ref in ((grad_k, grad_k_ref), (grad_v, grad_v_ref)):
            before = ref[text_rows, :].astype(f32)
            ref[text_rows, :] = jnp.where(text_ok, grad[:WINDOW], before).astype(bf16)
            ref[patch_rows, :] = grad[WINDOW:].astype(bf16)
    grad_high = grad_lookup[...].astype(bf16)
    grad_rest = (grad_lookup[...] - grad_high.astype(f32)).astype(bf16)
    flip = flip_feat_ref[...]
    grad_block = dot_left_t(flip, grad_high) + dot_left_t(flip, grad_rest)
    grad_table_ref[0] = diagonal_sums(grad_block[:, :LANES])
    grad_table_ref[1] = diagonal_sums(grad_block[:, LANES:])


def column_spec(rows, first=0):
    return pl.BlockSpec((rows, LANES), lambda pair, bounds: (0, pair + first))


def tables_spec(first=0):
    return pl.BlockSpec((2, 8, LANES), lambda pair, bounds: (pair + first, 0, 0))


def whole_spec(rows):
    return pl.BlockSpec((rows, LANES), lambda pair, bounds: (0, 0))


def attend(bounds, queries, keys_values, features, own_features, tables):
    return pl.pallas_call(
        attend_kernel,
        grid_spec=pltpu.PrefetchScalarGridSpec(
            num_scalar_prefetch=1,
            grid=(PAIRS,),
            in_specs=[
                column_spec(TEXT),
                column_spec(2 * TEXT),
                column_spec(2 * TEXT, PAIRS),
                whole_spec(2 * TEXT),
                whole_spec(TEXT),
                tables_spec(),
            ],
            out_specs=column_spec(TEXT),
            scratch_shapes=[pltpu.VMEM((TEXT, 2 * LANES), bf16)],
        ),
        out_shape=jax.ShapeDtypeStruct((TEXT, HEADS * HEAD), bf16),
        cost_estimate=small_cost,
        name="attend",
    )(bounds, queries, keys_values, keys_values, features, own_features, tables)


def attend_back(
    bounds, queries, keys_values, grad_context, features, own_features, flip, tables, first, count
):
    return pl.pallas_call(
        attend_back_kernel,
        grid_spec=pltpu.PrefetchScalarGridSpec(
            num_scalar_prefetch=1,
            grid=(count,),
            in_specs=[
                column_spec(TEXT, first),
                column_spec(2 * TEXT, first),
                column_spec(2 * TEXT, PAIRS + first),
                column_spec(TEXT, first),
                whole_spec(2 * TEXT),
                whole_spec(TEXT),
                whole_spec(TEXT),
                tables_spec(first),
            ],
            out_specs=[
                column_spec(TEXT),
                column_spec(2 * TEXT),
                column_spec(2 * TEXT),
                tables_spec(),
            ],
            scratch_shapes=[
                pltpu.VMEM((TEXT, 2 * LANES), bf16),
                pltpu.VMEM((TEXT, 2 * LANES), f32),
            ],
        ),
        out_shape=[
            jax.ShapeDtypeStruct((TEXT, count * LANES), bf16),
            jax.ShapeDtypeStruct((2 * TEXT, count * LANES), bf16),
            jax.ShapeDtypeStruct((2 * TEXT, count * LANES), bf16),
            jax.ShapeDtypeStruct((2 * count, 8, LANES), f32),
        ],
        cost_estimate=small_cost,
        name="attend_back",
    )(
        bounds,
        queries,
        keys_values,
        keys_values,
        grad_context,
        features,
        own_features,
        flip,
        tables,
    )


def exchange(values, mask):
    count = lax.axis_size("page")
    return lax.ppermute(values, "page", [(i, i ^ mask) for i in range(count)])


def after(value, *earlier):
    return lax.optimization_barrier((value, *earlier))[0]


def slot_mask(slot):
    return (slot & 3) * 4 + (slot >> 2) * 2


def project_kernel(groups, place, mixed_ref, bias_ref, *refs):
    *pieces, query_ref, both_ref, weight_ref, mixed_t_ref, sems = refs
    width = mixed_ref.shape[1]
    tokens = query_ref.shape[0]
    copies = start_rows(place, groups, pieces, weight_ref, sems)
    mixed_t_ref[...] = mixed_ref[...].T
    for copy in copies:
        copy.wait()
    own = mixed_ref[pl.ds(pl.multiple_of(place[1] * tokens, 16), tokens), :]
    queries = jnp.dot(own, weight_ref[:, :width], preferred_element_type=f32) + bias_ref[:, :width]
    query_ref[...] = (queries.astype(bf16).astype(f32) * 0.125).astype(bf16)
    for part in range(2):
        rows = pl.ds(part * tokens, tokens)
        for column in (1, 2):
            at = slice(column * width, (column + 1) * width)
            out = slice((column - 1) * width, column * width)
            values = jnp.dot(mixed_ref[rows, :], weight_ref[:, at], preferred_element_type=f32)
            both_ref[rows, out] = (values + bias_ref[:, at]).astype(bf16)


def project(place, mixed, biases, groups, pieces):
    rows, width = mixed.shape
    vmem = pl.BlockSpec(memory_space=pltpu.VMEM)
    return pl.pallas_call(
        functools.partial(project_kernel, groups),
        grid_spec=pltpu.PrefetchScalarGridSpec(
            num_scalar_prefetch=1,
            grid=(),
            in_specs=[vmem] * 2 + any_specs(len(pieces)),
            out_specs=[vmem] * 4,
            scratch_shapes=[pltpu.SemaphoreType.DMA((32,))],
        ),
        out_shape=[
            jax.ShapeDtypeStruct((rows // 2, width), bf16),
            jax.ShapeDtypeStruct((rows, 2 * width), bf16),
            jax.ShapeDtypeStruct((width, 3 * width), bf16),
            jax.ShapeDtypeStruct((width, rows), bf16),
        ],
        cost_estimate=small_cost,
        compiler_params=pltpu.CompilerParams(vmem_limit_bytes=16 << 20),
        name="project",
    )(place, mixed, biases, *pieces)


def column_parts(shard):
    return [shard] + [exchange(shard, 4 * step) for step in (1, 2, 3)]


def half_pieces(column):
    eight = jnp.concatenate([column, exchange(column, 2)])
    far = swap(eight)
    return [eight, exchange(eight, 1), far, exchange(far, 1)]


def row_pieces(column, across):
    return [column, exchange(column, 1), across, exchange(across, 1)]


def column_of(shard):
    return jnp.stack(column_parts(shard))


def row_copies(place, groups, refs, full, sems, first=0):
    copies = []
    for kind, column in groups:
        if kind == "full":
            piece, *refs = refs
            width = piece.shape[1]
            target = full.at[:, pl.ds(column, width)]
            copies.append(pltpu.make_async_copy(piece, target, sems.at[first + len(copies)]))
            continue
        pieces, refs = refs[:4], refs[4:]
        _, rows, width = pieces[0].shape
        for index in range(32 if kind == "halves" else 16):
            at = column
            if kind == "halves":
                source, slot = index >> 3, index & 7
                mask = slot_mask(slot) + (source & 1)
                at = pl.multiple_of(column + (place[1] ^ (source >> 1)) * width, 128)
            else:
                source, slot = index & 3, index >> 2
                mask = slot * 4 + source
            row = pl.multiple_of((place[0] ^ mask) * rows, 16)
            copies.append(
                pltpu.make_async_copy(
                    pieces[source].at[slot],
                    full.at[pl.ds(row, rows), pl.ds(at, width)],
                    sems.at[first + len(copies)],
                )
            )
    return copies


def start_rows(place, groups, refs, full, sems):
    copies = row_copies(place, groups, refs, full, sems)
    for copy in copies:
        copy.start()
    return copies


def gelu_parts(values):
    size = jnp.abs(values)
    t = 1.0 / (1.0 + (0.42 * 0.7071067811865476) * size)
    poly = jnp.full_like(t, erfc_poly[-1])
    for coefficient in erfc_poly[-2::-1]:
        poly = poly * t + coefficient
    bell = jnp.exp(-0.5 * values * values)
    tail = (0.5 * t) * (poly * bell)
    cdf = jnp.where(values >= 0.0, 1.0 - tail, tail)
    return values * cdf, cdf + (values * 0.3989422804014327) * bell


def normalized(values):
    centered = values - jnp.mean(values, axis=1, keepdims=True)
    variance = jnp.mean(centered * centered, axis=1, keepdims=True)
    scale = lax.rsqrt(variance + norm_eps)
    return centered * scale, scale


def norm_back(grads, unit, scale, gain):
    scaled = grads * gain
    mean = jnp.mean(scaled, axis=1, keepdims=True)
    inner = jnp.mean(scaled * unit, axis=1, keepdims=True)
    return scale * (scaled - mean - unit * inner)


def up_kernel(groups, place, context_ref, mixed_ref, vec_ref, bias_ref, *refs):
    *pieces, unit_ref, scale_ref, low_ref, low_t_ref, context_t_ref = refs[:-9]
    active_ref, active_t_ref, slope_ref, full_ref = refs[-9:-5]
    weight, hidden, low, sems, full_sem = refs[-5:]
    step = pl.program_id(0)
    tiles = pl.num_programs(0) - 1
    width = context_ref.shape[1]
    tile = active_ref.shape[1]
    last_group = 16 if len(groups) > 1 else 0

    def full_copy():
        return pltpu.make_async_copy(weight, full_ref, full_sem)

    @pl.when(step == 0)
    def _():
        copies = row_copies(place, groups, pieces, weight, sems)
        for copy in copies:
            copy.start()
        context_t_ref[...] = context_ref[...].T
        for copy in copies[: len(copies) - last_group]:
            copy.wait()
        branch = jnp.dot(context_ref[...], weight[:, :width], preferred_element_type=f32)
        unit, scale = normalized(mixed_ref[...] + branch + vec_ref[0:1])
        unit_ref[...] = unit
        scale_ref[...] = jnp.broadcast_to(scale, scale_ref.shape)
        normed = (unit * vec_ref[1:2] + vec_ref[2:3]).astype(bf16)
        low[...] = normed
        low_ref[...] = normed
        low_t_ref[...] = normed.T

    @pl.when(step == 1)
    def _():
        copies = row_copies(place, groups, pieces, weight, sems)
        for copy in copies[len(copies) - last_group :]:
            copy.wait()
        full_copy().start()

    def product():
        at = pl.multiple_of(width + step * tile, 128)
        return jnp.dot(low[...], weight[:, pl.ds(at, tile)], preferred_element_type=f32)

    def activate():
        active, slope = gelu_parts(hidden[(step + 1) % 2] + bias_ref[...])
        active = active.astype(bf16)
        active_ref[...] = active
        active_t_ref[...] = active.T
        slope_ref[...] = slope.astype(bf16)

    @pl.when(step == 0)
    def _():
        hidden[step % 2] = product()

    @pl.when((step > 0) & (step < tiles))
    def _():
        hidden[step % 2] = product()
        activate()

    @pl.when(step == tiles)
    def _():
        activate()
        full_copy().wait()


def any_specs(count):
    return [pl.BlockSpec(memory_space=pl.ANY)] * count


def up_forward(place, context, mixed, vectors, bias_up, groups, pieces):
    tokens, width = mixed.shape
    hidden_width = bias_up.shape[1]
    tile = 512
    whole = lambda step, place: (0, 0)
    last = lambda step, place: (0, jnp.maximum(step - 1, 0))
    last_t = lambda step, place: (jnp.maximum(step - 1, 0), 0)
    return pl.pallas_call(
        functools.partial(up_kernel, groups),
        grid_spec=pltpu.PrefetchScalarGridSpec(
            num_scalar_prefetch=1,
            grid=(hidden_width // tile + 1,),
            in_specs=[
                pl.BlockSpec((tokens, width), whole),
                pl.BlockSpec((tokens, width), whole),
                pl.BlockSpec(vectors.shape, whole),
                pl.BlockSpec((1, tile), last),
            ]
            + any_specs(len(pieces)),
            out_specs=[
                pl.BlockSpec((tokens, width), whole),
                pl.BlockSpec((tokens, 128), whole),
                pl.BlockSpec((tokens, width), whole),
                pl.BlockSpec((width, tokens), whole),
                pl.BlockSpec((width, tokens), whole),
                pl.BlockSpec((tokens, tile), last),
                pl.BlockSpec((tile, tokens), last_t),
                pl.BlockSpec((tokens, tile), last),
                pl.BlockSpec(memory_space=pl.ANY),
            ],
            scratch_shapes=[
                pltpu.VMEM((width, width + hidden_width), bf16),
                pltpu.VMEM((2, tokens, tile), f32),
                pltpu.VMEM((tokens, width), bf16),
                pltpu.SemaphoreType.DMA((48,)),
                pltpu.SemaphoreType.DMA,
            ],
        ),
        out_shape=[
            jax.ShapeDtypeStruct((tokens, width), f32),
            jax.ShapeDtypeStruct((tokens, 128), f32),
            jax.ShapeDtypeStruct((tokens, width), bf16),
            jax.ShapeDtypeStruct((width, tokens), bf16),
            jax.ShapeDtypeStruct((width, tokens), bf16),
            jax.ShapeDtypeStruct((tokens, hidden_width), bf16),
            jax.ShapeDtypeStruct((hidden_width, tokens), bf16),
            jax.ShapeDtypeStruct((tokens, hidden_width), bf16),
            jax.ShapeDtypeStruct((width, width + hidden_width), bf16),
        ],
        cost_estimate=small_cost,
        name="up_forward",
    )(place, context, mixed, vectors, bias_up, *pieces)


def down_kernel(active_ref, weight_ref, unit_ref, vec_ref, grad_ref, *refs):
    out_ref, sum_ref, low_ref, small_ref, total = refs
    step = pl.program_id(0)
    product = jnp.dot(active_ref[...], weight_ref[...], preferred_element_type=f32)

    @pl.when(step == 0)
    def _():
        total[...] = product

    @pl.when(step > 0)
    def _():
        total[...] += product

    @pl.when(step == pl.num_programs(0) - 1)
    def _():
        tokens, width = unit_ref.shape
        half = tokens // 2
        smalls = [jnp.zeros((1, width), f32)] * 3
        for part in range(2):
            rows = pl.ds(part * half, half)
            normed = unit_ref[rows, :] * vec_ref[1:2] + vec_ref[2:3]
            unit, scale = normalized(normed + total[rows, :] + vec_ref[3:4])
            out_ref[rows, :] = (unit * vec_ref[4:5] + vec_ref[5:6]).astype(bf16)
            grads = grad_ref[rows, :].astype(f32)
            back = norm_back(grads, unit, scale, vec_ref[4:5])
            low = back.astype(bf16)
            sum_ref[rows, :] = back
            low_ref[rows, :] = low
            for index, term in enumerate((grads * unit, grads, low.astype(f32))):
                smalls[index] = smalls[index] + jnp.sum(term, axis=0, keepdims=True)
        small_ref[...] = jnp.concatenate(smalls + [jnp.zeros((5, width), f32)], axis=0)


def down_forward(active, weight, unit, vectors, grads):
    tokens, width = unit.shape
    hidden_width = active.shape[1]
    tile = 768
    whole = lambda step: (0, 0)
    token_block = pl.BlockSpec((tokens, width), whole)
    return pl.pallas_call(
        down_kernel,
        grid=(hidden_width // tile,),
        in_specs=[
            pl.BlockSpec((tokens, tile), lambda step: (0, step)),
            pl.BlockSpec((tile, width), lambda step: (step, 0)),
            token_block,
            pl.BlockSpec(vectors.shape, whole),
            token_block,
        ],
        out_specs=[token_block] * 3 + [pl.BlockSpec((8, width), whole)],
        scratch_shapes=[pltpu.VMEM((tokens, width), f32)],
        out_shape=[
            jax.ShapeDtypeStruct((tokens, width), bf16),
            jax.ShapeDtypeStruct((tokens, width), f32),
            jax.ShapeDtypeStruct((tokens, width), bf16),
            jax.ShapeDtypeStruct((8, width), f32),
        ],
        cost_estimate=small_cost,
        name="down_forward",
    )(active, weight, unit, vectors, grads)


def ffn_back_kernel(*refs):
    low_ref, slope_ref, sum_ref, unit_ref, scale_ref, vec_ref = refs[:6]
    down_ref, up_ref, out_weight_ref = refs[6:9]
    hidden_ref, bias_ref, first_ref, branch_ref, context_ref, small_ref, total = refs[9:]
    step = pl.program_id(0)
    tokens, width = unit_ref.shape
    tile = slope_ref.shape[1]
    half = tokens // 2

    @pl.when(step == 0)
    def _():
        total[...] = sum_ref[...]

    bias = jnp.zeros((1, tile), f32)
    for part in range(2):
        rows = pl.ds(part * half, half)
        grads = dot_right_t(low_ref[rows, :], down_ref[...]) * slope_ref[rows, :].astype(f32)
        grads = grads.astype(bf16)
        hidden_ref[rows, :] = grads
        bias = bias + jnp.sum(grads.astype(f32), axis=0, keepdims=True)
        total[rows, :] += dot_right_t(grads, up_ref[...])
    bias_ref[...] = bias

    @pl.when(step == pl.num_programs(0) - 1)
    def _():
        grads = total[...]
        unit = unit_ref[...]
        first = norm_back(grads, unit, scale_ref[:, 0:1], vec_ref[1:2])
        branch = first.astype(bf16)
        first_ref[...] = first
        branch_ref[...] = branch
        context_ref[...] = dot_right_t(branch, out_weight_ref[...]).astype(bf16)
        smalls = [
            jnp.sum(term, axis=0, keepdims=True)
            for term in (grads * unit, grads, branch.astype(f32))
        ]
        small_ref[...] = jnp.concatenate(smalls + [jnp.zeros((5, width), f32)], axis=0)


def ffn_back(low, slope, total, unit, scale, vectors, full_rest, full_down):
    tokens, width = unit.shape
    hidden_width = slope.shape[1]
    tile = 768
    whole = lambda step: (0, 0)
    column = lambda step: (0, step)
    token_block = pl.BlockSpec((tokens, width), whole)
    return pl.pallas_call(
        ffn_back_kernel,
        grid=(hidden_width // tile,),
        in_specs=[
            token_block,
            pl.BlockSpec((tokens, tile), column),
            token_block,
            token_block,
            pl.BlockSpec((tokens, 128), whole),
            pl.BlockSpec(vectors.shape, whole),
            pl.BlockSpec((tile, width), lambda step: (step, 0)),
            pl.BlockSpec((width, tile), lambda step: (0, step + 1)),
            pl.BlockSpec((width, width), whole),
        ],
        out_specs=[
            pl.BlockSpec((tokens, tile), column),
            pl.BlockSpec((1, tile), column),
            token_block,
            token_block,
            token_block,
            pl.BlockSpec((8, width), whole),
        ],
        scratch_shapes=[pltpu.VMEM((tokens, width), f32)],
        out_shape=[
            jax.ShapeDtypeStruct((tokens, hidden_width), bf16),
            jax.ShapeDtypeStruct((1, hidden_width), f32),
            jax.ShapeDtypeStruct((tokens, width), f32),
            jax.ShapeDtypeStruct((tokens, width), bf16),
            jax.ShapeDtypeStruct((tokens, width), bf16),
            jax.ShapeDtypeStruct((8, width), f32),
        ],
        cost_estimate=small_cost,
        name="ffn_back",
    )(low, slope, total, unit, scale, vectors, full_down, full_rest, full_rest)


def grad_rows_kernel(x_ref, h_ref, out_ref):
    out_ref[...] = jnp.dot(x_ref[...], h_ref[...], preferred_element_type=f32).astype(bf16)


def grad_rows(inputs_t, grads):
    width, tokens = inputs_t.shape
    columns = grads.shape[1]
    return pl.pallas_call(
        grad_rows_kernel,
        grid=(4,),
        in_specs=[
            pl.BlockSpec((width // 4, tokens), lambda step: (step, 0)),
            pl.BlockSpec((tokens, columns), lambda step: (0, 0)),
        ],
        out_specs=pl.BlockSpec((width // 4, columns), lambda step: (step, 0)),
        out_shape=jax.ShapeDtypeStruct((width, columns), bf16),
        cost_estimate=small_cost,
        compiler_params=pltpu.CompilerParams(vmem_limit_bytes=12 << 20),
        name="grad_rows",
    )(inputs_t, grads)


def grad_columns_kernel(parts, place, *refs):
    count = len(parts)
    ins, keep_ref, send_ref, scratch = (
        refs[: 2 * count],
        refs[2 * count],
        refs[2 * count + 1],
        refs[2 * count + 2 :],
    )
    rows, tile = keep_ref.shape[1], keep_ref.shape[2]
    step = pl.program_id(0)
    first = 0
    for index, steps in enumerate(parts):
        x_ref, h_ref, ordered = ins[2 * index], ins[2 * index + 1], scratch[index]

        @pl.when(step == first)
        def _():
            for slot in range(16):
                mask = slot_mask(slot & 7) + (slot >> 3)
                at = pl.multiple_of((place[0] ^ mask) * rows, 16)
                ordered[pl.ds(slot * rows, rows), :] = x_ref[pl.ds(at, rows), :]

        @pl.when((step >= first) & (step < first + steps))
        def _():
            product = jnp.dot(ordered[...], h_ref[...], preferred_element_type=f32).astype(bf16)
            keep_ref[...] = product[: 8 * rows].reshape(8, rows, tile)
            send_ref[...] = product[8 * rows :].reshape(8, rows, tile)

        first = first + steps


def grad_by_columns(pairs, place, tile):
    width = pairs[0][0].shape[0]
    rows = width // 16
    parts = tuple(sum(grad.shape[1] for grad in grads) // tile for _, _, *grads in pairs)
    steps = sum(parts)
    specs = []
    operands = []
    scratch = []
    first = 0
    for (inputs_t, own, *grads), count in zip(pairs, parts):
        tokens = grads[0].shape[0]
        block = (lambda step, place: (0, place[1])) if own else (lambda step, place: (0, 0))
        specs.append(pl.BlockSpec((width, tokens), block))

        def column(step, place, first=first, count=count):
            return (0, jnp.clip(step - first, 0, count - 1))

        specs.append(pl.BlockSpec((tokens, tile), column))
        operands += [inputs_t, *grads]
        scratch.append(pltpu.VMEM((width, tokens), bf16))
        first = first + count
    half = jax.ShapeDtypeStruct((8, rows, steps * tile), bf16)
    return pl.pallas_call(
        functools.partial(grad_columns_kernel, parts),
        grid_spec=pltpu.PrefetchScalarGridSpec(
            num_scalar_prefetch=1,
            grid=(steps,),
            in_specs=specs,
            out_specs=[pl.BlockSpec((8, rows, tile), lambda step, place: (0, 0, step))] * 2,
            scratch_shapes=scratch,
        ),
        out_shape=[half, half],
        cost_estimate=small_cost,
        compiler_params=pltpu.CompilerParams(vmem_limit_bytes=16 << 20),
        name="grad_columns",
    )(place, *operands)


def key_back_kernel(place, gk_ref, gv_ref, wk_ref, wv_ref, out_ref):
    total = dot_right_t(gk_ref[...], wk_ref[...]) + dot_right_t(gv_ref[...], wv_ref[...])
    out_ref[...] = total.astype(out_ref.dtype)


def own_back_kernel(place, first_ref, gq_ref, gk_ref, gv_ref, wq_ref, wk_ref, wv_ref, out_ref):
    total = dot_right_t(gk_ref[...], wk_ref[...]) + dot_right_t(gv_ref[...], wv_ref[...])
    out_ref[...] = first_ref[...] + total + dot_right_t(gq_ref[...], wq_ref[...])


def input_back(place, weights, grad_keys, grad_values, others):
    width = weights.shape[0]
    tokens = grad_keys.shape[0] // 2
    whole = pl.BlockSpec((tokens, width), lambda step, place: (0, 0))
    row = lambda step, place: ((place[1] if others else 1 - place[1]), 0)
    if others:
        kernel, leading, first, dtype = own_back_kernel, [whole, whole], 0, f32
    else:
        kernel, leading, first, dtype = key_back_kernel, [], 1, bf16
    operands = list(others) + [grad_keys, grad_values] + [weights] * (3 - first)
    specs = [pl.BlockSpec((tokens, width), row)] * 2
    for block in range(first, 3):
        specs.append(pl.BlockSpec((width, width), lambda step, place, block=block: (0, block)))
    return pl.pallas_call(
        kernel,
        grid_spec=pltpu.PrefetchScalarGridSpec(
            num_scalar_prefetch=1, grid=(1,), in_specs=leading + specs, out_specs=whole
        ),
        out_shape=jax.ShapeDtypeStruct((tokens, width), dtype),
        cost_estimate=small_cost,
        compiler_params=pltpu.CompilerParams(vmem_limit_bytes=16 << 20),
        name="input_back",
    )(place, *operands)


def back_rows(values, mask):
    return jnp.where(mask, pltpu.roll(values, dilation, 0), 0.0)


def ahead_rows(values, mask):
    return jnp.where(mask, pltpu.roll(values, values.shape[0] - dilation, 0), 0.0)


def tap_sums(grads, inputs, ahead, back):
    terms = (grads * back_rows(inputs, back), grads * inputs, grads * ahead_rows(inputs, ahead), grads)
    return [jnp.sum(term, axis=0, keepdims=True) for term in terms]


def small_sums_kernel(
    own_ref, other_ref, x_ref, x_other_ref, mask_ref, gq_ref, gv_ref, one_ref, two_ref, up_ref, table_ref, out_ref
):
    width = own_ref.shape[1]
    mask = mask_ref[...] > 0.0
    own = tap_sums(own_ref[...], x_ref[...].astype(f32), mask[:, 0:1], mask[:, 1:2])
    other = tap_sums(
        other_ref[...].astype(f32), x_other_ref[...].astype(f32), mask[:, 2:3], mask[:, 3:4]
    )
    rows = [a + b for a, b in zip(own, other)]
    for ref in (gq_ref, gv_ref):
        rows.append(jnp.sum(ref[...].astype(f32), axis=0, keepdims=True))
    rows.append(jnp.zeros((2, width), f32))
    out_ref[0:8] = jnp.concatenate(rows, axis=0)
    out_ref[8:16] = one_ref[...]
    out_ref[16:24] = two_ref[...]
    count = up_ref.shape[1] // width
    for index in range(count):
        out_ref[24 + index : 25 + index] = up_ref[:, index * width : (index + 1) * width]
    for index in range(3 * HEADS):
        row, lane = 28 + index // 6, index % 6 * LANES
        table = table_ref[index // 3]
        out_ref[row : row + 1, lane : lane + LANES] = table[index % 3 : index % 3 + 1]
    out_ref[34:40] = jnp.zeros((6, width), f32)


def small_sums(*operands):
    return pl.pallas_call(
        small_sums_kernel,
        out_shape=jax.ShapeDtypeStruct((40, operands[0].shape[1]), f32),
        cost_estimate=small_cost,
        compiler_params=pltpu.CompilerParams(vmem_limit_bytes=24 << 20),
        name="small_sums",
    )(*operands)


def state_back_kernel(own_ref, other_ref, mask_ref, tap_ref, out_ref):
    grads = own_ref[...] + other_ref[...].astype(f32)
    mask = mask_ref[...] > 0.0
    total = grads + tap_ref[1:2] * grads
    total = total + tap_ref[0:1] * ahead_rows(grads, mask[:, 0:1])
    total = total + tap_ref[2:3] * back_rows(grads, mask[:, 1:2])
    out_ref[...] = total.astype(bf16)


def state_back(own, other, masks, taps):
    return pl.pallas_call(
        state_back_kernel,
        out_shape=jax.ShapeDtypeStruct(own.shape, bf16),
        cost_estimate=small_cost,
        compiler_params=pltpu.CompilerParams(vmem_limit_bytes=20 << 20),
        name="state_back",
    )(own, other, masks, taps)


def first_half_kernel(place, keep_near, part_near, keep_far, part_far, held_ref, out_ref):
    held_ref[...] = keep_near[...].astype(f32) + part_near[...].astype(f32)
    out_ref[...] = (keep_far[...].astype(f32) + part_far[...].astype(f32)).astype(bf16)


def halve_call(place, keep, partner, specs, half_shape, steps):
    near, far, out = specs
    return pl.pallas_call(
        first_half_kernel,
        grid_spec=pltpu.PrefetchScalarGridSpec(
            num_scalar_prefetch=1,
            grid=(steps,),
            in_specs=[near, near, far, far],
            out_specs=[out, out],
        ),
        out_shape=[
            jax.ShapeDtypeStruct(half_shape, f32),
            jax.ShapeDtypeStruct(half_shape, bf16),
        ],
        cost_estimate=small_cost,
        compiler_params=pltpu.CompilerParams(vmem_limit_bytes=12 << 20),
        name="halve",
    )(place, keep, partner, keep, partner)


def halve_across(place, keep, partner):
    _, rows, width = keep.shape
    near = pl.BlockSpec((1, rows, width), lambda step, place: (step, 0, 0))
    far = pl.BlockSpec((1, rows, width), lambda step, place: (step + 4, 0, 0))
    return halve_call(place, keep, partner, (near, far, near), (4, rows, width), 4)


def halve_plane(place, keep, partner):
    _, rows, width = keep.shape
    block = (2, rows, width // 2)
    near = pl.BlockSpec(block, lambda step, place: (step, 0, place[1]))
    far = pl.BlockSpec(block, lambda step, place: (step, 0, 1 - place[1]))
    out = pl.BlockSpec(block, lambda step, place: (step, 0, 0))
    return halve_call(place, keep, partner, (near, far, out), (8, rows, width // 2), 4)


def column_kernel(held_ref, across_ref, own_ref, *sends):
    own_ref[...] = held_ref[0] + across_ref[0].astype(f32)
    for step, send in enumerate(sends, 1):
        send[...] = (held_ref[step] + across_ref[step].astype(f32)).astype(bf16)


def column_sends(held, across):
    _, rows, width = held.shape
    tile = 384
    out = pl.BlockSpec((rows, tile), lambda step: (0, step))
    block = pl.BlockSpec((4, rows, tile), lambda step: (0, 0, step))
    own, *sends = pl.pallas_call(
        column_kernel,
        grid=(width // tile,),
        in_specs=[block, block],
        out_specs=[out] * 4,
        out_shape=[jax.ShapeDtypeStruct((rows, width), f32)]
        + [jax.ShapeDtypeStruct((rows, width), bf16)] * 3,
        cost_estimate=small_cost,
        compiler_params=pltpu.CompilerParams(vmem_limit_bytes=12 << 20),
        name="column_sends",
    )(held, across)
    return own, sends


def column_arrivals(sends):
    return [exchange(send, 4 * step) for step, send in enumerate(sends, 1)]


def column_total(own, arrived):
    total = own
    for part in arrived:
        total = total + part.astype(f32)
    return total.astype(bf16)


def half_columns(values, first):
    half = values.shape[-1] // 2
    return jnp.where(first, values[..., :half], values[..., half:])


def summed_rows(pairs):
    grads = jnp.concatenate([plain_dot(*pair).astype(bf16) for pair in pairs], axis=1)
    shard = lax.psum_scatter(grads, "page", scatter_dimension=0, tiled=True)
    return shard.astype(f32) + swap(shard).astype(f32)


def page_bounds(segments, is_text):
    pages = jnp.arange(PAGES, dtype=jnp.int32)
    low = jnp.sum(segments[None, :] < pages[:, None], axis=1, dtype=jnp.int32)
    high = jnp.sum(segments[None, :] <= pages[:, None], axis=1, dtype=jnp.int32)
    own_low = jnp.where(is_text, low, pages * PATCH)
    own_high = jnp.where(is_text, high, (pages + 1) * PATCH)

    def aligned(start):
        return jnp.minimum(start // 16 * 16, TEXT - WINDOW)

    return jnp.concatenate([aligned(own_low), own_low, own_high, aligned(low), low, high])


def both_sum(values, mask):
    return values + exchange(values, mask)


def swap(values):
    return lax.ppermute(values, "mod", [(0, 1), (1, 0)])


def local(
    states,
    cotangent,
    segments,
    box_x,
    box_y,
    conv_weight,
    conv_bias,
    w_query,
    b_query,
    w_key,
    w_value,
    b_value,
    w_out,
    b_out,
    table_pos,
    table_x,
    table_y,
    gain_one,
    bias_one,
    w_up,
    b_up,
    w_down,
    b_down,
    gain_two,
    bias_two,
):
    is_text = lax.axis_index("mod") == 0
    d_model = states.shape[3]
    own_low = states[0, 0]
    rows_each = w_query.shape[0]
    d_ff = w_up.shape[1]
    fast = lax.axis_size("page") == 16 and rows_each % 16 == 0 and w_down.shape[0] % 16 == 0
    place = jnp.stack([lax.axis_index("page"), lax.axis_index("mod")]).astype(jnp.int32)
    pack_qkv = jnp.concatenate([w_query, w_key, w_value], axis=1)
    pack_rest = jnp.concatenate([w_out, w_up], axis=1)
    other_low = swap(own_low)
    page_ids, pos_bins, bins_x, bins_y = token_ids(segments[0], box_x[0], box_y[0])
    bounds = page_bounds(segments[0], is_text)
    own_pages = jnp.where(is_text, page_ids[0], page_ids[1])
    features = bin_features(pos_bins.reshape(-1), bins_x.reshape(-1), bins_y.reshape(-1))
    flipped = bin_features(
        POS_BINS - 1 - pos_bins.reshape(-1),
        BOX_BINS - 1 - bins_x.reshape(-1),
        BOX_BINS - 1 - bins_y.reshape(-1),
    )
    own_feats = jnp.where(is_text, features[:TEXT], features[TEXT:])
    own_flip = jnp.where(is_text, flipped[:TEXT], flipped[TEXT:])
    tables = jnp.stack(
        [
            jnp.pad(table_pos, ((0, 0), (0, LANES - table_pos.shape[1]))),
            jnp.pad(table_x, ((0, 0), (0, LANES - table_x.shape[1]))),
            jnp.pad(table_y, ((0, 0), (0, LANES - table_y.shape[1]))),
        ],
        axis=1,
    )
    tables = jnp.pad(tables, ((0, 0), (0, 5), (0, 0)))

    own_states = own_low.astype(f32)
    mixed = dilated_mix(own_states, own_pages, conv_weight, conv_bias)
    mixed_low = mixed.astype(bf16)
    other_pages = jnp.where(is_text, page_ids[1], page_ids[0])
    masks = jnp.pad(
        jnp.stack(
            [
                own_pages == shifted(own_pages, dilation, -1),
                own_pages == shifted(own_pages, -dilation, -1),
                other_pages == shifted(other_pages, dilation, -1),
                other_pages == shifted(other_pages, -dilation, -1),
            ],
            axis=1,
        ).astype(f32),
        ((0, 0), (0, LANES - 4)),
    )
    vectors = jnp.stack(
        [b_out, gain_one, bias_one, b_down, gain_two, bias_two, jnp.zeros_like(b_out), b_out]
    )
    biases = jnp.concatenate([b_query, jnp.zeros_like(b_value), b_value])[None]
    taps = jnp.pad(conv_weight, ((0, 5), (0, 0)))
    bias_up = b_up[None]
    if fast:
        split = (pack_rest.shape[1] // 2 + 127) // 256 * 256
        column_qkv = column_of(half_columns(pack_qkv, is_text))
        early = (features, own_feats, own_flip, tables, bounds, masks, vectors, biases, taps)
        early += (bias_up, mixed_low)
        parts_near = column_parts(
            after(half_columns(pack_rest[:, :split], is_text), column_qkv, other_low, *early)
        )
        pieces_qkv = half_pieces(column_qkv)
        w_down = after(w_down, pieces_qkv[0])
        column_near = jnp.stack([after(part, pieces_qkv[0]) for part in parts_near])
        parts_far = column_parts(after(pack_rest[:, split:], column_near))
        pieces_near = half_pieces(column_near)
        pieces_qkv[2] = after(pieces_qkv[2], pieces_near[0])
        pieces_qkv[3] = exchange(pieces_qkv[2], 1)
        groups_qkv = (("halves", 0),)
    else:
        groups_qkv = (("full", 0),)
        pieces_qkv = [lax.all_gather(pack_qkv, "page", axis=0, tiled=True)]
    full_down = lax.all_gather(w_down, "page", axis=0, tiled=True)

    other_mixed = dilated_mix(other_low.astype(f32), other_pages, conv_weight, conv_bias)
    other_mixed = other_mixed.astype(bf16)
    mixed_all = jnp.concatenate(
        [jnp.where(is_text, mixed_low, other_mixed), jnp.where(is_text, other_mixed, mixed_low)],
        axis=0,
    )
    if fast:
        pieces_qkv[0] = after(pieces_qkv[0], mixed_all)
    queries, keys_values, full_qkv, mixed_t = project(
        place, mixed_all, biases, groups_qkv, pieces_qkv
    )
    attend_in = queries
    if fast:
        column_far = jnp.stack([after(part, queries) for part in parts_far])
        across_far = exchange(column_far, 2)
        attend_in = after(queries, column_far)
    context = attend(bounds, attend_in, keys_values, features, own_feats, tables)
    if fast:
        pieces_near[2] = after(pieces_near[2], context)
        pieces_near[3] = exchange(pieces_near[2], 1)
        across_far = after(across_far, context)
        pieces_rest = pieces_near + row_pieces(column_far, across_far)
        groups_rest = (("halves", 0), ("rows", split))
    else:
        pieces_rest = [lax.all_gather(pack_rest, "page", axis=0, tiled=True)]
        groups_rest = (("full", 0),)
    unit, scale, normed_low, normed_t, context_t, active, active_t, slope, full_rest = up_forward(
        place, context, mixed, vectors, bias_up, groups_rest, pieces_rest
    )
    output_row, grad_sum_two, grad_ffn, small_two = down_forward(
        active, full_down, unit, vectors, cotangent[0, 0]
    )
    rows_down = grad_rows(active_t, grad_ffn)
    shard_down = lax.psum_scatter(rows_down, "page", scatter_dimension=0, tiled=True)
    grad_hidden, grad_b_up, grad_first, grad_branch, grad_context, small_one = ffn_back(
        after(grad_ffn, rows_down), slope, grad_sum_two, unit, scale, vectors, full_rest, full_down
    )
    attend_in = grad_context
    if fast:
        pairs = [(context_t, False, grad_branch), (normed_t, False, grad_hidden)]
        keep_rest, send_rest = grad_by_columns(pairs, place, d_model)
        partner_rest = exchange(send_rest, 1)
        held_rest, plane_out = halve_plane(place, keep_rest, partner_rest)
        plane_rest = swap(plane_out)
        attend_in = after(grad_context, plane_out)
    else:
        shard_rest = summed_rows([(context_t, grad_branch), (normed_t, grad_hidden)])
    grad_queries, grad_keys, grad_values, grad_tables = attend_back(
        bounds, queries, keys_values, attend_in, features, own_feats, own_flip, tables, 0, PAIRS
    )
    grad_keys_in, grad_queries_in = grad_keys, grad_queries
    if fast:
        plane_rest = after(plane_rest, grad_queries)
        held_rest, across_out = halve_across(place, held_rest, plane_rest)
        across_rest = exchange(across_out, 2)
        shard_down = after(shard_down, grad_queries)
        shard_down = shard_down.astype(f32) + swap(shard_down).astype(f32)
        grad_queries_in = after(grad_queries, across_out, shard_down)
    pairs = [(mixed_t, True, grad_queries_in), (mixed_t, False, grad_keys), (mixed_t, False, grad_values)]
    if fast:
        keep_qkv, send_qkv = grad_by_columns(pairs, place, d_model)
        partner_qkv = exchange(send_qkv, 1)
        grad_keys_in = after(grad_keys, send_qkv)
    else:
        shard_down = shard_down.astype(f32) + swap(shard_down).astype(f32)
        shard_qkv = summed_rows(
            [(mixed_low.T, grad_queries), (mixed_t, grad_keys), (mixed_t, grad_values)]
        )
    to_other = input_back(place, full_qkv, grad_keys_in, grad_values, ())
    from_other = swap(to_other)
    grad_values_in = grad_values
    if fast:
        partner_qkv = after(partner_qkv, to_other)
        held_qkv, across_out = halve_across(place, keep_qkv, partner_qkv)
        across_qkv = exchange(across_out, 2)
        grad_values_in = after(grad_values, across_out)
    own_part = input_back(place, full_qkv, grad_keys, grad_values_in, (grad_first, grad_queries))
    packed = small_sums(
        own_part,
        to_other,
        own_low,
        other_low,
        masks,
        grad_queries,
        grad_values,
        small_one,
        small_two,
        grad_b_up,
        grad_tables,
    )
    if fast:
        packed = both_sum(packed, 1)
        across_rest = after(across_rest, packed)
        own_rest, sends_rest = column_sends(held_rest, across_rest)
        arrived_rest = column_arrivals(sends_rest)
        packed = after(packed, *sends_rest)
        packed = packed + swap(packed)
        across_qkv = after(across_qkv, packed)
        own_qkv, sends_qkv = column_sends(held_qkv, across_qkv)
        arrived_qkv = column_arrivals(sends_qkv)
        from_other = after(from_other, *sends_qkv)
    else:
        packed = lax.psum(packed, ("mod", "page"))
    grad_in = state_back(own_part, from_other, masks, taps)
    if fast:
        arrived_rest = [after(part, grad_in) for part in arrived_rest]
        total_rest = column_total(own_rest, arrived_rest)
        far_rest = swap(total_rest)
        packed = both_sum(after(packed, total_rest), 2)
        arrived_qkv = [after(part, packed) for part in arrived_qkv]
        total_qkv = column_total(own_qkv, arrived_qkv)
        far_qkv = swap(total_qkv)
        packed = both_sum(both_sum(after(packed, total_qkv), 4), 8)
    g_tables = packed[28:34].reshape(HEADS, 3, LANES)
    if fast:
        shard_rest = jnp.where(
            is_text,
            jnp.concatenate([total_rest, far_rest], axis=1),
            jnp.concatenate([far_rest, total_rest], axis=1),
        ).astype(f32)
        shard_qkv = total_qkv.astype(f32) + far_qkv.astype(f32)
    return (
        output_row[None, None],
        grad_in[None, None],
        packed[0:3],
        packed[3],
        shard_qkv[:, :d_model],
        packed[4],
        shard_qkv[:, d_model : 2 * d_model],
        shard_qkv[:, 2 * d_model :],
        packed[5],
        shard_rest[:, :d_model],
        packed[10],
        g_tables[:, 0, : table_pos.shape[1]],
        g_tables[:, 1, 64 : 64 + table_x.shape[1]],
        g_tables[:, 2, 64 : 64 + table_y.shape[1]],
        packed[8],
        packed[9],
        shard_rest[:, d_model:],
        packed[24:28].reshape(d_ff),
        shard_down,
        packed[18],
        packed[16],
        packed[17],
    )


def solution(mesh):
    rows = P("mod", "page", None, None)
    ids = P("page", None)
    cut = P("page", None)
    return jax.shard_map(
        local,
        mesh=mesh,
        in_specs=(
            rows, rows, ids, ids, ids, P(), P(), cut, P(), cut, cut, P(), cut,
            P(), P(), P(), P(), P(), P(), cut, P(), cut, P(), P(), P(),
        ),
        out_specs=(
            rows, rows, P(), P(), cut, P(), cut, cut, P(), cut, P(), P(), P(),
            P(), P(), P(), cut, P(), cut, P(), P(), P(),
        ),
        check_vma=False,
    )
```

```python
import functools

import jax
import jax.numpy as jnp
import numpy as np
from jax import lax
from jax.experimental import pallas as pl
from jax.experimental.pallas import tpu as pltpu
from jax.sharding import PartitionSpec as P

HEADS = 12
HEAD = 64
GRID = 8
PAGES = 8
POS_BINS = 64
BOX_BINS = 32
PATCH = 64
TEXT = 512
PAIRS = HEADS // 2
LANES = 2 * HEAD
WINDOW = 144
SMALL = 80

dilation = 2
small_cost = pl.CostEstimate(flops=1000, bytes_accessed=1000, transcendentals=0)
norm_eps = 1e-05
mask_fill = -1000000000.0
erfc_poly = (
    0.2367515965428487,
    0.24062179898991767,
    0.18865103029313968,
    0.2877518531132804,
    -0.1648672439458568,
    0.4765735350541787,
    -0.34041833366480423,
    0.07493571514857543,
)
bf16 = jnp.bfloat16
f32 = jnp.float32


def shifted(values, offset, fill_value):
    padding = jnp.full((abs(offset),) + values.shape[1:], fill_value, values.dtype)
    if offset > 0:
        return jnp.concatenate([values[offset:], padding], axis=0)
    return jnp.concatenate([padding, values[:offset]], axis=0)


def dilated_mix(inputs, page_ids, conv_weight, conv_bias):
    summed = inputs + conv_bias + conv_weight[1] * inputs
    for tap_index, offset in ((0, -dilation), (2, dilation)):
        moved_rows = shifted(inputs, offset, 0.0)
        moved_pages = shifted(page_ids, offset, -1)
        same_page = (moved_pages == page_ids)[:, None]
        summed = summed + conv_weight[tap_index] * jnp.where(same_page, moved_rows, 0.0)
    return summed


def bin_features(pos_bins, bins_x, bins_y):
    return jnp.concatenate(
        [
            jax.nn.one_hot(pos_bins, POS_BINS, dtype=bf16),
            jax.nn.one_hot(bins_x, BOX_BINS, dtype=bf16),
            jax.nn.one_hot(bins_y, BOX_BINS, dtype=bf16),
        ],
        axis=1,
    )


def token_ids(text_pages, text_x, text_y):
    text_index = jnp.arange(TEXT, dtype=jnp.int32)
    text_pos = text_index * POS_BINS // TEXT
    patch_pos = text_index % PATCH * POS_BINS // PATCH
    patch_page = text_index // PATCH
    patch_x = text_index % GRID * BOX_BINS // GRID
    patch_y = text_index // GRID % GRID * BOX_BINS // GRID
    page_ids = jnp.stack([text_pages, patch_page])
    pos_bins = jnp.stack([text_pos, patch_pos])
    bins_x = jnp.stack([text_x, patch_x])
    bins_y = jnp.stack([text_y, patch_y])
    return (page_ids, pos_bins, bins_x, bins_y)


def plain_dot(left_side, right_side):
    return jnp.dot(left_side, right_side, preferred_element_type=f32)


def dot_left_t(left_side, right_side):
    return lax.dot_general(
        left_side, right_side, (((0,), (0,)), ((), ())), preferred_element_type=f32
    )


def dot_right_t(left_side, right_side):
    return lax.dot_general(
        left_side, right_side, (((1,), (1,)), ((), ())), preferred_element_type=f32
    )


def iota(shape, axis):
    return lax.broadcasted_iota(jnp.int32, shape, axis)


def bias_block(table_rows):
    pos_part = pltpu.roll(
        jnp.broadcast_to(table_rows[0:1], (POS_BINS, LANES)), 65, 1, stride=1, stride_axis=0
    )
    x_part = pltpu.roll(
        jnp.broadcast_to(table_rows[1:2], (BOX_BINS, LANES)), 33, 1, stride=1, stride_axis=0
    )
    y_part = pltpu.roll(
        jnp.broadcast_to(table_rows[2:3], (BOX_BINS, LANES)), 65, 1, stride=1, stride_axis=0
    )
    lane = iota((POS_BINS, LANES), 1)
    pos_part = jnp.where(lane < POS_BINS, pos_part, 0.0)
    lane = iota((BOX_BINS, LANES), 1)
    x_part = jnp.where((lane >= 64) & (lane < 96), x_part, 0.0)
    y_part = jnp.where(lane >= 96, y_part, 0.0)
    return jnp.concatenate([pos_part, x_part, y_part], axis=0).astype(bf16)


def diagonal_sums(grad_block):
    lane = iota((POS_BINS, LANES), 1)
    pos_part = jnp.where(lane < POS_BINS, grad_block[:64], 0.0)
    lane = iota((BOX_BINS, LANES), 1)
    x_part = jnp.where((lane >= 64) & (lane < 96), grad_block[64:96], 0.0)
    y_part = jnp.where(lane >= 96, grad_block[96:], 0.0)
    pos_part = pltpu.roll(pos_part, 0, 1, stride=1, stride_axis=0)
    x_part = pltpu.roll(x_part, 0, 1, stride=1, stride_axis=0)
    y_part = pltpu.roll(y_part, 96, 1, stride=1, stride_axis=0)
    rows = [jnp.sum(part, axis=0, keepdims=True) for part in (pos_part, x_part, y_part)]
    return jnp.concatenate(rows + [jnp.zeros((5, LANES), f32)], axis=0)


def stacked_heads(rows, low_lane):
    zero = jnp.zeros_like(rows)
    return jnp.concatenate(
        [jnp.where(low_lane, rows, zero), jnp.where(low_lane, zero, rows)], axis=0
    )


def window_start(first, window):
    return pl.multiple_of(jnp.minimum(first // 16 * 16, TEXT - window), 16)


def fits(first, end, window):
    return end - jnp.minimum(first // 16 * 16, TEXT - window) <= window


def for_each_page(bounds, step):
    def body(page, carry):
        own_low, own_high = bounds[page], bounds[PAGES + page]
        key_low, key_high = bounds[2 * PAGES + page], bounds[3 * PAGES + page]
        own_small = fits(own_low, own_high, SMALL)
        key_small = fits(key_low, key_high, SMALL)
        span = (own_low, own_high, key_low, key_high)
        small = own_small & key_small
        mixed = own_small & ~key_small
        for chosen, own_window, key_window in (
            (small, SMALL, SMALL),
            (mixed, SMALL, WINDOW),
            (~own_small, WINDOW, WINDOW),
        ):

            @pl.when(chosen)
            def _():
                step(page, span, own_window, key_window)

        return carry

    lax.fori_loop(0, PAGES, body, 0)


def page_operands(page, span, own_window, key_window, pair, q_ref, k_ref, feat_ref, lookup):
    own_at = window_start(span[0], own_window)
    key_at = window_start(span[2], key_window)
    own_rows, text_rows = pl.ds(own_at, own_window), pl.ds(key_at, key_window)
    patch_at = TEXT + PATCH * page
    if not isinstance(page, int):
        patch_at = pl.multiple_of(patch_at, PATCH)
    patch_rows = pl.ds(patch_at, PATCH)
    lanes = slice(pair * LANES, (pair + 1) * LANES)
    low_lane = iota((own_window, LANES), 1) < HEAD
    queries = stacked_heads(q_ref[own_rows, lanes], low_lane)
    first = 2 * pair * LANES
    rel = jnp.concatenate(
        [
            lookup[own_rows, first : first + LANES],
            lookup[own_rows, first + LANES : first + 2 * LANES],
        ],
        axis=0,
    )
    query_side = jnp.concatenate([rel, queries], axis=1)
    key_side = jnp.concatenate(
        [
            jnp.concatenate([feat_ref[text_rows, :], k_ref[text_rows, lanes]], axis=1),
            jnp.concatenate([feat_ref[patch_rows, :], k_ref[patch_rows, lanes]], axis=1),
        ],
        axis=0,
    )
    own_row = iota((own_window, LANES), 0) + own_at
    own_ok = (own_row >= span[0]) & (own_row < span[1])
    return (
        lanes, low_lane, own_ok, queries, query_side, key_side, own_rows, text_rows, patch_rows, key_at
    )


def set_lookup(lookup, own_feat_ref, table_ref):
    blocks = [bias_block(table_ref[head]) for head in range(table_ref.shape[0])]
    product = jnp.dot(
        own_feat_ref[...], jnp.concatenate(blocks, axis=1), preferred_element_type=f32
    )
    lookup[...] = product.astype(bf16)


def attend_kernel(bounds, q_ref, k_ref, v_ref, feat_ref, own_feat_ref, table_ref, context_ref, lookup):
    set_lookup(lookup, own_feat_ref, table_ref)

    def step(page, span, own_window, key_window):
        column = iota((1, key_window + PATCH), 1)
        key_row = column + window_start(span[2], key_window)
        key_ok = (column >= key_window) | ((key_row >= span[2]) & (key_row < span[3]))
        for pair in range(q_ref.shape[1] // LANES):
            lanes, low_lane, own_ok, _, query_side, key_side, own_rows, text_rows, patch_rows, _ = (
                page_operands(
                    page, span, own_window, key_window, pair, q_ref, k_ref, feat_ref, lookup
                )
            )
            scores = jnp.where(key_ok, dot_right_t(query_side, key_side), mask_fill)
            row_max = jnp.max(scores, axis=1, keepdims=True)
            weights = jnp.exp(scores - row_max)
            total = jnp.sum(weights, axis=1, keepdims=True)
            prob = (weights * (1.0 / total)).astype(bf16)
            values = jnp.concatenate([v_ref[text_rows, lanes], v_ref[patch_rows, lanes]], axis=0)
            mixed = jnp.dot(prob, values, preferred_element_type=f32)
            picked = jnp.where(low_lane, mixed[:own_window], mixed[own_window:])
            before = context_ref[own_rows, lanes].astype(f32)
            context_ref[own_rows, lanes] = jnp.where(own_ok, picked, before).astype(bf16)

    for page in range(PAGES):
        span = [bounds[part * PAGES + page] for part in range(4)]
        step(page, span, WINDOW, WINDOW)


def attend_back_kernel(
    bounds,
    q_ref,
    k_ref,
    v_ref,
    grad_ref,
    feat_ref,
    own_feat_ref,
    flip_feat_ref,
    table_ref,
    grad_q_ref,
    grad_k_ref,
    grad_v_ref,
    grad_table_ref,
    lookup,
    grad_lookup,
):
    set_lookup(lookup, own_feat_ref, table_ref)

    def step(page, span, own_window, key_window):
        row = iota((key_window + PATCH, 1), 0)
        key_row = row + window_start(span[2], key_window)
        key_ok = (row >= key_window) | ((key_row >= span[2]) & (key_row < span[3]))
        for pair in range(q_ref.shape[1] // LANES):
            lanes, low_lane, own_ok, queries, query_side, key_side, own_rows, text_rows, patch_rows, key_at = (
                page_operands(
                    page, span, own_window, key_window, pair, q_ref, k_ref, feat_ref, lookup
                )
            )
            scores = jnp.where(key_ok, dot_right_t(key_side, query_side), mask_fill)
            col_max = jnp.max(scores, axis=0, keepdims=True)
            weights = jnp.exp(scores - col_max)
            total = jnp.sum(weights, axis=0, keepdims=True)
            prob = weights * (1.0 / total)
            grad_rows = grad_ref[own_rows, lanes]
            grad_rows = jnp.where(own_ok, grad_rows, jnp.zeros_like(grad_rows))
            grads = stacked_heads(grad_rows, low_lane)
            values = jnp.concatenate([v_ref[text_rows, lanes], v_ref[patch_rows, lanes]], axis=0)
            grad_prob = dot_right_t(values, grads)
            inner = jnp.sum(prob * grad_prob, axis=0, keepdims=True)
            grad_scores = (prob * (grad_prob - inner)).astype(bf16)
            grad_v = jnp.dot(prob.astype(bf16), grads, preferred_element_type=f32)
            grad_k = jnp.dot(grad_scores, queries, preferred_element_type=f32)
            back = dot_left_t(grad_scores, key_side)
            low, high = back[:own_window], back[own_window:]
            grad_q = jnp.where(low_lane, low[:, LANES:], high[:, LANES:]) * 0.125
            before = grad_q_ref[own_rows, lanes].astype(f32)
            grad_q_ref[own_rows, lanes] = jnp.where(own_ok, grad_q, before).astype(bf16)
            first = 2 * pair * LANES
            for part, at in ((low, first), (high, first + LANES)):
                place_at = slice(at, at + LANES)
                grad_lookup[own_rows, place_at] = jnp.where(
                    own_ok, part[:, :LANES], grad_lookup[own_rows, place_at]
                )
            wide_row = iota((key_window, LANES), 0) + key_at
            text_ok = (wide_row >= span[2]) & (wide_row < span[3])
            for grad, ref in ((grad_k, grad_k_ref), (grad_v, grad_v_ref)):
                before = ref[text_rows, lanes].astype(f32)
                ref[text_rows, lanes] = jnp.where(text_ok, grad[:key_window], before).astype(bf16)
                ref[patch_rows, lanes] = grad[key_window:].astype(bf16)

    for_each_page(bounds, step)
    grad_high = grad_lookup[...].astype(bf16)
    grad_rest = (grad_lookup[...] - grad_high.astype(f32)).astype(bf16)
    flip = flip_feat_ref[...]
    grad_block = dot_left_t(flip, grad_high) + dot_left_t(flip, grad_rest)
    for head in range(table_ref.shape[0]):
        grad_table_ref[head] = diagonal_sums(grad_block[:, head * LANES : (head + 1) * LANES])


def column_spec(rows, group, first=0):
    return pl.BlockSpec((rows, group * LANES), lambda step, bounds: (0, step + first))


def whole_spec(rows):
    return pl.BlockSpec((rows, LANES), lambda step, bounds: (0, 0))


def tables_spec(group):
    return pl.BlockSpec((2 * group, 8, LANES), lambda step, bounds: (step, 0, 0))


def attend(bounds, queries, keys_values, features, own_features, tables):
    group = 1
    return pl.pallas_call(
        attend_kernel,
        grid_spec=pltpu.PrefetchScalarGridSpec(
            num_scalar_prefetch=1,
            grid=(PAIRS // group,),
            in_specs=[
                column_spec(TEXT, group),
                column_spec(2 * TEXT, group),
                column_spec(2 * TEXT, group, PAIRS // group),
                whole_spec(2 * TEXT),
                whole_spec(TEXT),
                tables_spec(group),
            ],
            out_specs=column_spec(TEXT, group),
            scratch_shapes=[pltpu.VMEM((TEXT, 2 * group * LANES), bf16)],
        ),
        out_shape=jax.ShapeDtypeStruct((TEXT, HEADS * HEAD), bf16),
        cost_estimate=small_cost,
        name="attend",
    )(bounds, queries, keys_values, keys_values, features, own_features, tables)


def attend_back(
    bounds, queries, keys_values, grad_context, features, own_features, flip, tables
):
    group = 6
    return pl.pallas_call(
        attend_back_kernel,
        grid_spec=pltpu.PrefetchScalarGridSpec(
            num_scalar_prefetch=1,
            grid=(PAIRS // group,),
            in_specs=[
                column_spec(TEXT, group),
                column_spec(2 * TEXT, group),
                column_spec(2 * TEXT, group, PAIRS // group),
                column_spec(TEXT, group),
                whole_spec(2 * TEXT),
                whole_spec(TEXT),
                whole_spec(TEXT),
                tables_spec(group),
            ],
            out_specs=[
                column_spec(TEXT, group),
                column_spec(2 * TEXT, group),
                column_spec(2 * TEXT, group),
                tables_spec(group),
            ],
            scratch_shapes=[
                pltpu.VMEM((TEXT, 2 * group * LANES), bf16),
                pltpu.VMEM((TEXT, 2 * group * LANES), f32),
            ],
        ),
        out_shape=[
            jax.ShapeDtypeStruct((TEXT, HEADS * HEAD), bf16),
            jax.ShapeDtypeStruct((2 * TEXT, HEADS * HEAD), bf16),
            jax.ShapeDtypeStruct((2 * TEXT, HEADS * HEAD), bf16),
            jax.ShapeDtypeStruct((HEADS, 8, LANES), f32),
        ],
        cost_estimate=small_cost,
        name="attend_back",
    )(
        bounds,
        queries,
        keys_values,
        keys_values,
        grad_context,
        features,
        own_features,
        flip,
        tables,
    )


def exchange(values, mask):
    count = lax.axis_size("page")
    return lax.ppermute(values, "page", [(i, i ^ mask) for i in range(count)])


def after(value, *earlier):
    return lax.optimization_barrier((value, *earlier))[0]


def slot_mask(slot):
    return (slot & 3) * 4 + (slot >> 2) * 2


def project_kernel(groups, place, mixed_ref, bias_ref, *refs):
    *pieces, query_ref, both_ref, weight_ref, mixed_t_ref, sems = refs
    width = mixed_ref.shape[1]
    tokens = query_ref.shape[0]
    copies = start_rows(place, groups, pieces, weight_ref, sems)
    mixed_t_ref[...] = mixed_ref[...].T
    for copy in copies:
        copy.wait()
    own = mixed_ref[pl.ds(pl.multiple_of(place[1] * tokens, 16), tokens), :]
    queries = jnp.dot(own, weight_ref[:, :width], preferred_element_type=f32) + bias_ref[:, :width]
    query_ref[...] = (queries.astype(bf16).astype(f32) * 0.125).astype(bf16)
    for part in range(2):
        rows = pl.ds(part * tokens, tokens)
        for column in (1, 2):
            at = slice(column * width, (column + 1) * width)
            out = slice((column - 1) * width, column * width)
            values = jnp.dot(mixed_ref[rows, :], weight_ref[:, at], preferred_element_type=f32)
            both_ref[rows, out] = (values + bias_ref[:, at]).astype(bf16)


def project(place, mixed, biases, groups, pieces):
    rows, width = mixed.shape
    vmem = pl.BlockSpec(memory_space=pltpu.VMEM)
    return pl.pallas_call(
        functools.partial(project_kernel, groups),
        grid_spec=pltpu.PrefetchScalarGridSpec(
            num_scalar_prefetch=1,
            grid=(),
            in_specs=[vmem] * 2 + any_specs(len(pieces)),
            out_specs=[vmem] * 4,
            scratch_shapes=[pltpu.SemaphoreType.DMA((32,))],
        ),
        out_shape=[
            jax.ShapeDtypeStruct((rows // 2, width), bf16),
            jax.ShapeDtypeStruct((rows, 2 * width), bf16),
            jax.ShapeDtypeStruct((width, 3 * width), bf16),
            jax.ShapeDtypeStruct((width, rows), bf16),
        ],
        cost_estimate=small_cost,
        compiler_params=pltpu.CompilerParams(vmem_limit_bytes=16 << 20),
        name="project",
    )(place, mixed, biases, *pieces)


def column_parts(shard):
    return [shard] + [exchange(shard, 4 * step) for step in (1, 2, 3)]


def half_pieces(column):
    eight = jnp.concatenate([column, exchange(column, 2)])
    far = swap(eight)
    return [eight, exchange(eight, 1), far, exchange(far, 1)]


def row_pieces(column, across):
    return [column, exchange(column, 1), across, exchange(across, 1)]


def column_of(shard):
    return jnp.stack(column_parts(shard))


def row_copies(place, groups, refs, full, sems, first=0):
    copies = []
    for kind, column in groups:
        if kind == "full":
            piece, *refs = refs
            width = piece.shape[1]
            target = full.at[:, pl.ds(column, width)]
            copies.append(pltpu.make_async_copy(piece, target, sems.at[first + len(copies)]))
            continue
        pieces, refs = refs[:4], refs[4:]
        _, rows, width = pieces[0].shape
        for index in range(32 if kind == "halves" else 16):
            at = column
            if kind == "halves":
                source, slot = index >> 3, index & 7
                mask = slot_mask(slot) + (source & 1)
                at = pl.multiple_of(column + (place[1] ^ (source >> 1)) * width, 128)
            else:
                source, slot = index & 3, index >> 2
                mask = slot * 4 + source
            row = pl.multiple_of((place[0] ^ mask) * rows, 16)
            copies.append(
                pltpu.make_async_copy(
                    pieces[source].at[slot],
                    full.at[pl.ds(row, rows), pl.ds(at, width)],
                    sems.at[first + len(copies)],
                )
            )
    return copies


def start_rows(place, groups, refs, full, sems):
    copies = row_copies(place, groups, refs, full, sems)
    for copy in copies:
        copy.start()
    return copies


def gelu_parts(values):
    size = jnp.abs(values)
    t = 1.0 / (1.0 + (0.42 * 0.7071067811865476) * size)
    poly = jnp.full_like(t, erfc_poly[-1])
    for coefficient in erfc_poly[-2::-1]:
        poly = poly * t + coefficient
    bell = jnp.exp(-0.5 * values * values)
    tail = (0.5 * t) * (poly * bell)
    cdf = jnp.where(values >= 0.0, 1.0 - tail, tail)
    return values * cdf, cdf + (values * 0.3989422804014327) * bell


def normalized(values):
    centered = values - jnp.mean(values, axis=1, keepdims=True)
    variance = jnp.mean(centered * centered, axis=1, keepdims=True)
    scale = lax.rsqrt(variance + norm_eps)
    return centered * scale, scale


def norm_back(grads, unit, scale, gain):
    scaled = grads * gain
    mean = jnp.mean(scaled, axis=1, keepdims=True)
    inner = jnp.mean(scaled * unit, axis=1, keepdims=True)
    return scale * (scaled - mean - unit * inner)


def up_kernel(groups, place, context_ref, mixed_ref, vec_ref, bias_ref, *refs):
    *pieces, unit_ref, scale_ref, low_ref, low_t_ref, context_t_ref = refs[:-9]
    active_ref, active_t_ref, slope_ref, full_ref = refs[-9:-5]
    weight, hidden, low, sems, full_sem = refs[-5:]
    step = pl.program_id(0)
    tiles = pl.num_programs(0) - 1
    width = context_ref.shape[1]
    tile = active_ref.shape[1]
    last_group = 16 if len(groups) > 1 else 0

    def full_copy():
        return pltpu.make_async_copy(weight, full_ref, full_sem)

    @pl.when(step == 0)
    def _():
        copies = row_copies(place, groups, pieces, weight, sems)
        for copy in copies:
            copy.start()
        context_t_ref[...] = context_ref[...].T
        for copy in copies[: len(copies) - last_group]:
            copy.wait()
        branch = jnp.dot(context_ref[...], weight[:, :width], preferred_element_type=f32)
        unit, scale = normalized(mixed_ref[...] + branch + vec_ref[0:1])
        unit_ref[...] = unit
        scale_ref[...] = jnp.broadcast_to(scale, scale_ref.shape)
        normed = (unit * vec_ref[1:2] + vec_ref[2:3]).astype(bf16)
        low[...] = normed
        low_ref[...] = normed
        low_t_ref[...] = normed.T

    @pl.when(step == 1)
    def _():
        if last_group:
            for copy in row_copies(place, groups[1:], pieces[4:], weight, sems, 32):
                copy.wait()
        full_copy().start()

    def product():
        at = pl.multiple_of(width + step * tile, 128)
        return jnp.dot(low[...], weight[:, pl.ds(at, tile)], preferred_element_type=f32)

    def activate():
        active, slope = gelu_parts(hidden[(step + 1) % 2] + bias_ref[...])
        active = active.astype(bf16)
        active_ref[...] = active
        active_t_ref[...] = active.T
        slope_ref[...] = slope.astype(bf16)

    @pl.when(step == 0)
    def _():
        hidden[step % 2] = product()

    @pl.when((step > 0) & (step < tiles))
    def _():
        hidden[step % 2] = product()
        activate()

    @pl.when(step == tiles)
    def _():
        activate()
        full_copy().wait()


def any_specs(count):
    return [pl.BlockSpec(memory_space=pl.ANY)] * count


def up_forward(place, context, mixed, vectors, bias_up, groups, pieces):
    tokens, width = mixed.shape
    hidden_width = bias_up.shape[1]
    tile = 512
    whole = lambda step, place: (0, 0)
    last = lambda step, place: (0, jnp.maximum(step - 1, 0))
    last_t = lambda step, place: (jnp.maximum(step - 1, 0), 0)
    return pl.pallas_call(
        functools.partial(up_kernel, groups),
        grid_spec=pltpu.PrefetchScalarGridSpec(
            num_scalar_prefetch=1,
            grid=(hidden_width // tile + 1,),
            in_specs=[
                pl.BlockSpec((tokens, width), whole),
                pl.BlockSpec((tokens, width), whole),
                pl.BlockSpec(vectors.shape, whole),
                pl.BlockSpec((1, tile), last),
            ]
            + any_specs(len(pieces)),
            out_specs=[
                pl.BlockSpec((tokens, width), whole),
                pl.BlockSpec((tokens, 128), whole),
                pl.BlockSpec((tokens, width), whole),
                pl.BlockSpec((width, tokens), whole),
                pl.BlockSpec((width, tokens), whole),
                pl.BlockSpec((tokens, tile), last),
                pl.BlockSpec((tile, tokens), last_t),
                pl.BlockSpec((tokens, tile), last),
                pl.BlockSpec(memory_space=pl.ANY),
            ],
            scratch_shapes=[
                pltpu.VMEM((width, width + hidden_width), bf16),
                pltpu.VMEM((2, tokens, tile), f32),
                pltpu.VMEM((tokens, width), bf16),
                pltpu.SemaphoreType.DMA((48,)),
                pltpu.SemaphoreType.DMA,
            ],
        ),
        out_shape=[
            jax.ShapeDtypeStruct((tokens, width), f32),
            jax.ShapeDtypeStruct((tokens, 128), f32),
            jax.ShapeDtypeStruct((tokens, width), bf16),
            jax.ShapeDtypeStruct((width, tokens), bf16),
            jax.ShapeDtypeStruct((width, tokens), bf16),
            jax.ShapeDtypeStruct((tokens, hidden_width), bf16),
            jax.ShapeDtypeStruct((hidden_width, tokens), bf16),
            jax.ShapeDtypeStruct((tokens, hidden_width), bf16),
            jax.ShapeDtypeStruct((width, width + hidden_width), bf16),
        ],
        cost_estimate=small_cost,
        name="up_forward",
    )(place, context, mixed, vectors, bias_up, *pieces)


def down_kernel(active_ref, weight_ref, unit_ref, vec_ref, grad_ref, *refs):
    out_ref, sum_ref, low_ref, small_ref, total = refs
    step = pl.program_id(0)
    product = jnp.dot(active_ref[...], weight_ref[...], preferred_element_type=f32)

    @pl.when(step == 0)
    def _():
        total[...] = product

    @pl.when(step > 0)
    def _():
        total[...] += product

    @pl.when(step == pl.num_programs(0) - 1)
    def _():
        tokens, width = unit_ref.shape
        half = tokens // 2
        smalls = [jnp.zeros((1, width), f32)] * 3
        for part in range(2):
            rows = pl.ds(part * half, half)
            normed = unit_ref[rows, :] * vec_ref[1:2] + vec_ref[2:3]
            unit, scale = normalized(normed + total[rows, :] + vec_ref[3:4])
            out_ref[rows, :] = (unit * vec_ref[4:5] + vec_ref[5:6]).astype(bf16)
            grads = grad_ref[rows, :].astype(f32)
            back = norm_back(grads, unit, scale, vec_ref[4:5])
            low = back.astype(bf16)
            sum_ref[rows, :] = back
            low_ref[rows, :] = low
            for index, term in enumerate((grads * unit, grads, low.astype(f32))):
                smalls[index] = smalls[index] + jnp.sum(term, axis=0, keepdims=True)
        small_ref[...] = jnp.concatenate(smalls + [jnp.zeros((5, width), f32)], axis=0)


def down_forward(active, weight, unit, vectors, grads):
    tokens, width = unit.shape
    hidden_width = active.shape[1]
    tile = 768
    whole = lambda step: (0, 0)
    token_block = pl.BlockSpec((tokens, width), whole)
    return pl.pallas_call(
        down_kernel,
        grid=(hidden_width // tile,),
        in_specs=[
            pl.BlockSpec((tokens, tile), lambda step: (0, step)),
            pl.BlockSpec((tile, width), lambda step: (step, 0)),
            token_block,
            pl.BlockSpec(vectors.shape, whole),
            token_block,
        ],
        out_specs=[token_block] * 3 + [pl.BlockSpec((8, width), whole)],
        scratch_shapes=[pltpu.VMEM((tokens, width), f32)],
        out_shape=[
            jax.ShapeDtypeStruct((tokens, width), bf16),
            jax.ShapeDtypeStruct((tokens, width), f32),
            jax.ShapeDtypeStruct((tokens, width), bf16),
            jax.ShapeDtypeStruct((8, width), f32),
        ],
        cost_estimate=small_cost,
        name="down_forward",
    )(active, weight, unit, vectors, grads)


def ffn_back_kernel(*refs):
    low_ref, slope_ref, sum_ref, unit_ref, scale_ref, vec_ref = refs[:6]
    down_ref, up_ref, out_weight_ref = refs[6:9]
    hidden_ref, bias_ref, first_ref, branch_ref, context_ref, small_ref, total = refs[9:]
    step = pl.program_id(0)
    tokens, width = unit_ref.shape
    tile = slope_ref.shape[1]
    half = tokens // 2

    @pl.when(step == 0)
    def _():
        total[...] = sum_ref[...]

    bias = jnp.zeros((1, tile), f32)
    for part in range(2):
        rows = pl.ds(part * half, half)
        grads = dot_right_t(low_ref[rows, :], down_ref[...]) * slope_ref[rows, :].astype(f32)
        grads = grads.astype(bf16)
        hidden_ref[rows, :] = grads
        bias = bias + jnp.sum(grads.astype(f32), axis=0, keepdims=True)
        total[rows, :] += dot_right_t(grads, up_ref[...])
    bias_ref[...] = bias

    @pl.when(step == pl.num_programs(0) - 1)
    def _():
        grads = total[...]
        unit = unit_ref[...]
        first = norm_back(grads, unit, scale_ref[:, 0:1], vec_ref[1:2])
        branch = first.astype(bf16)
        first_ref[...] = first
        branch_ref[...] = branch
        context_ref[...] = dot_right_t(branch, out_weight_ref[...]).astype(bf16)
        smalls = [
            jnp.sum(term, axis=0, keepdims=True)
            for term in (grads * unit, grads, branch.astype(f32))
        ]
        small_ref[...] = jnp.concatenate(smalls + [jnp.zeros((5, width), f32)], axis=0)


def ffn_back(low, slope, total, unit, scale, vectors, full_rest, full_down):
    tokens, width = unit.shape
    hidden_width = slope.shape[1]
    tile = 768
    whole = lambda step: (0, 0)
    column = lambda step: (0, step)
    token_block = pl.BlockSpec((tokens, width), whole)
    return pl.pallas_call(
        ffn_back_kernel,
        grid=(hidden_width // tile,),
        in_specs=[
            token_block,
            pl.BlockSpec((tokens, tile), column),
            token_block,
            token_block,
            pl.BlockSpec((tokens, 128), whole),
            pl.BlockSpec(vectors.shape, whole),
            pl.BlockSpec((tile, width), lambda step: (step, 0)),
            pl.BlockSpec((width, tile), lambda step: (0, step + 1)),
            pl.BlockSpec((width, width), whole),
        ],
        out_specs=[
            pl.BlockSpec((tokens, tile), column),
            pl.BlockSpec((1, tile), column),
            token_block,
            token_block,
            token_block,
            pl.BlockSpec((8, width), whole),
        ],
        scratch_shapes=[pltpu.VMEM((tokens, width), f32)],
        out_shape=[
            jax.ShapeDtypeStruct((tokens, hidden_width), bf16),
            jax.ShapeDtypeStruct((1, hidden_width), f32),
            jax.ShapeDtypeStruct((tokens, width), f32),
            jax.ShapeDtypeStruct((tokens, width), bf16),
            jax.ShapeDtypeStruct((tokens, width), bf16),
            jax.ShapeDtypeStruct((8, width), f32),
        ],
        cost_estimate=small_cost,
        name="ffn_back",
    )(low, slope, total, unit, scale, vectors, full_down, full_rest, full_rest)


def grad_rows_kernel(x_ref, h_ref, out_ref):
    out_ref[...] = jnp.dot(x_ref[...], h_ref[...], preferred_element_type=f32).astype(bf16)


def grad_rows(inputs_t, grads):
    width, tokens = inputs_t.shape
    columns = grads.shape[1]
    return pl.pallas_call(
        grad_rows_kernel,
        grid=(4,),
        in_specs=[
            pl.BlockSpec((width // 4, tokens), lambda step: (step, 0)),
            pl.BlockSpec((tokens, columns), lambda step: (0, 0)),
        ],
        out_specs=pl.BlockSpec((width // 4, columns), lambda step: (step, 0)),
        out_shape=jax.ShapeDtypeStruct((width, columns), bf16),
        cost_estimate=small_cost,
        name="grad_rows",
    )(inputs_t, grads)


def grad_columns_kernel(parts, place, *refs):
    count = len(parts)
    ins, keep_ref, send_ref, scratch = (
        refs[: 2 * count],
        refs[2 * count],
        refs[2 * count + 1],
        refs[2 * count + 2 :],
    )
    rows, tile = keep_ref.shape[1], keep_ref.shape[2]
    step = pl.program_id(0)
    first = 0
    for index, steps in enumerate(parts):
        x_ref, h_ref, ordered = ins[2 * index], ins[2 * index + 1], scratch[index]

        @pl.when(step == first)
        def _():
            for slot in range(16):
                mask = slot_mask(slot & 7) + (slot >> 3)
                at = pl.multiple_of((place[0] ^ mask) * rows, 16)
                ordered[pl.ds(slot * rows, rows), :] = x_ref[pl.ds(at, rows), :]

        @pl.when((step >= first) & (step < first + steps))
        def _():
            product = jnp.dot(ordered[...], h_ref[...], preferred_element_type=f32).astype(bf16)
            keep_ref[...] = product[: 8 * rows].reshape(8, rows, tile)
            send_ref[...] = product[8 * rows :].reshape(8, rows, tile)

        first = first + steps


def grad_by_columns(pairs, place, tile):
    width = pairs[0][0].shape[0]
    rows = width // 16
    parts = tuple(sum(grad.shape[1] for grad in grads) // tile for _, _, *grads in pairs)
    steps = sum(parts)
    specs = []
    operands = []
    scratch = []
    first = 0
    for (inputs_t, own, *grads), count in zip(pairs, parts):
        tokens = grads[0].shape[0]
        block = (lambda step, place: (0, place[1])) if own else (lambda step, place: (0, 0))
        specs.append(pl.BlockSpec((width, tokens), block))

        def column(step, place, first=first, count=count):
            return (0, jnp.clip(step - first, 0, count - 1))

        specs.append(pl.BlockSpec((tokens, tile), column))
        operands += [inputs_t, *grads]
        scratch.append(pltpu.VMEM((width, tokens), bf16))
        first = first + count
    half = jax.ShapeDtypeStruct((8, rows, steps * tile), bf16)
    return pl.pallas_call(
        functools.partial(grad_columns_kernel, parts),
        grid_spec=pltpu.PrefetchScalarGridSpec(
            num_scalar_prefetch=1,
            grid=(steps,),
            in_specs=specs,
            out_specs=[pl.BlockSpec((8, rows, tile), lambda step, place: (0, 0, step))] * 2,
            scratch_shapes=scratch,
        ),
        out_shape=[half, half],
        cost_estimate=small_cost,
        compiler_params=pltpu.CompilerParams(vmem_limit_bytes=16 << 20),
        name="grad_columns",
    )(place, *operands)


def key_back_kernel(place, gk_ref, gv_ref, wk_ref, wv_ref, out_ref):
    total = dot_right_t(gk_ref[...], wk_ref[...]) + dot_right_t(gv_ref[...], wv_ref[...])
    out_ref[...] = total.astype(out_ref.dtype)


def own_back_kernel(place, first_ref, gq_ref, gk_ref, gv_ref, wq_ref, wk_ref, wv_ref, out_ref):
    total = dot_right_t(gk_ref[...], wk_ref[...]) + dot_right_t(gv_ref[...], wv_ref[...])
    out_ref[...] = first_ref[...] + total + dot_right_t(gq_ref[...], wq_ref[...])


def input_back(place, weights, grad_keys, grad_values, others):
    width = weights.shape[0]
    tokens = grad_keys.shape[0] // 2
    whole = pl.BlockSpec((tokens, width), lambda step, place: (0, 0))
    row = lambda step, place: ((place[1] if others else 1 - place[1]), 0)
    if others:
        kernel, leading, first, dtype = own_back_kernel, [whole, whole], 0, f32
    else:
        kernel, leading, first, dtype = key_back_kernel, [], 1, bf16
    operands = list(others) + [grad_keys, grad_values] + [weights] * (3 - first)
    specs = [pl.BlockSpec((tokens, width), row)] * 2
    for block in range(first, 3):
        specs.append(pl.BlockSpec((width, width), lambda step, place, block=block: (0, block)))
    return pl.pallas_call(
        kernel,
        grid_spec=pltpu.PrefetchScalarGridSpec(
            num_scalar_prefetch=1, grid=(1,), in_specs=leading + specs, out_specs=whole
        ),
        out_shape=jax.ShapeDtypeStruct((tokens, width), dtype),
        cost_estimate=small_cost,
        compiler_params=pltpu.CompilerParams(vmem_limit_bytes=16 << 20),
        name="input_back",
    )(place, *operands)


def back_rows(values, mask):
    return jnp.where(mask, pltpu.roll(values, dilation, 0), 0.0)


def ahead_rows(values, mask):
    return jnp.where(mask, pltpu.roll(values, values.shape[0] - dilation, 0), 0.0)


def tap_sums(grads, inputs, ahead, back):
    terms = (grads * back_rows(inputs, back), grads * inputs, grads * ahead_rows(inputs, ahead), grads)
    return [jnp.sum(term, axis=0, keepdims=True) for term in terms]


def small_sums_kernel(
    own_ref, other_ref, x_ref, x_other_ref, mask_ref, gq_ref, gv_ref, one_ref, two_ref, up_ref, table_ref, out_ref
):
    width = own_ref.shape[1]
    mask = mask_ref[...] > 0.0
    own = tap_sums(own_ref[...], x_ref[...].astype(f32), mask[:, 0:1], mask[:, 1:2])
    other = tap_sums(
        other_ref[...].astype(f32), x_other_ref[...].astype(f32), mask[:, 2:3], mask[:, 3:4]
    )
    rows = [a + b for a, b in zip(own, other)]
    for ref in (gq_ref, gv_ref):
        rows.append(jnp.sum(ref[...].astype(f32), axis=0, keepdims=True))
    rows.append(jnp.zeros((2, width), f32))
    out_ref[0:8] = jnp.concatenate(rows, axis=0)
    out_ref[8:16] = one_ref[...]
    out_ref[16:24] = two_ref[...]
    count = up_ref.shape[1] // width
    for index in range(count):
        out_ref[24 + index : 25 + index] = up_ref[:, index * width : (index + 1) * width]
    for index in range(3 * HEADS):
        row, lane = 28 + index // 6, index % 6 * LANES
        table = table_ref[index // 3]
        out_ref[row : row + 1, lane : lane + LANES] = table[index % 3 : index % 3 + 1]
    out_ref[34:40] = jnp.zeros((6, width), f32)


def small_sums(*operands):
    return pl.pallas_call(
        small_sums_kernel,
        out_shape=jax.ShapeDtypeStruct((40, operands[0].shape[1]), f32),
        cost_estimate=small_cost,
        compiler_params=pltpu.CompilerParams(vmem_limit_bytes=24 << 20),
        name="small_sums",
    )(*operands)


def state_back_kernel(own_ref, other_ref, mask_ref, tap_ref, out_ref):
    grads = own_ref[...] + other_ref[...].astype(f32)
    mask = mask_ref[...] > 0.0
    total = grads + tap_ref[1:2] * grads
    total = total + tap_ref[0:1] * ahead_rows(grads, mask[:, 0:1])
    total = total + tap_ref[2:3] * back_rows(grads, mask[:, 1:2])
    out_ref[...] = total.astype(bf16)


def state_back(own, other, masks, taps):
    return pl.pallas_call(
        state_back_kernel,
        out_shape=jax.ShapeDtypeStruct(own.shape, bf16),
        cost_estimate=small_cost,
        compiler_params=pltpu.CompilerParams(vmem_limit_bytes=20 << 20),
        name="state_back",
    )(own, other, masks, taps)


def first_half_kernel(place, keep_near, part_near, keep_far, part_far, held_ref, out_ref):
    held_ref[...] = keep_near[...].astype(f32) + part_near[...].astype(f32)
    out_ref[...] = (keep_far[...].astype(f32) + part_far[...].astype(f32)).astype(bf16)


def halve_call(place, keep, partner, specs, half_shape, steps):
    near, far, out = specs
    return pl.pallas_call(
        first_half_kernel,
        grid_spec=pltpu.PrefetchScalarGridSpec(
            num_scalar_prefetch=1,
            grid=(steps,),
            in_specs=[near, near, far, far],
            out_specs=[out, out],
        ),
        out_shape=[
            jax.ShapeDtypeStruct(half_shape, f32),
            jax.ShapeDtypeStruct(half_shape, bf16),
        ],
        cost_estimate=small_cost,
        compiler_params=pltpu.CompilerParams(vmem_limit_bytes=12 << 20),
        name="halve",
    )(place, keep, partner, keep, partner)


def halve_across(place, keep, partner):
    _, rows, width = keep.shape
    near = pl.BlockSpec((1, rows, width), lambda step, place: (step, 0, 0))
    far = pl.BlockSpec((1, rows, width), lambda step, place: (step + 4, 0, 0))
    return halve_call(place, keep, partner, (near, far, near), (4, rows, width), 4)


def halve_plane(place, keep, partner):
    _, rows, width = keep.shape
    block = (2, rows, width // 2)
    near = pl.BlockSpec(block, lambda step, place: (step, 0, place[1]))
    far = pl.BlockSpec(block, lambda step, place: (step, 0, 1 - place[1]))
    out = pl.BlockSpec(block, lambda step, place: (step, 0, 0))
    return halve_call(place, keep, partner, (near, far, out), (8, rows, width // 2), 4)


def column_kernel(held_ref, across_ref, own_ref, *sends):
    own_ref[...] = held_ref[0] + across_ref[0].astype(f32)
    for step, send in enumerate(sends, 1):
        send[...] = (held_ref[step] + across_ref[step].astype(f32)).astype(bf16)


def column_sends(held, across):
    _, rows, width = held.shape
    tile = 384
    out = pl.BlockSpec((rows, tile), lambda step: (0, step))
    block = pl.BlockSpec((4, rows, tile), lambda step: (0, 0, step))
    own, *sends = pl.pallas_call(
        column_kernel,
        grid=(width // tile,),
        in_specs=[block, block],
        out_specs=[out] * 4,
        out_shape=[jax.ShapeDtypeStruct((rows, width), f32)]
        + [jax.ShapeDtypeStruct((rows, width), bf16)] * 3,
        cost_estimate=small_cost,
        compiler_params=pltpu.CompilerParams(vmem_limit_bytes=12 << 20),
        name="column_sends",
    )(held, across)
    return own, sends


def column_arrivals(sends):
    return [exchange(send, 4 * step) for step, send in enumerate(sends, 1)]


def column_total(own, arrived):
    total = own
    for part in arrived:
        total = total + part.astype(f32)
    return total.astype(bf16)


def half_columns(values, first):
    half = values.shape[-1] // 2
    return jnp.where(first, values[..., :half], values[..., half:])


def summed_rows(pairs):
    grads = jnp.concatenate([plain_dot(*pair).astype(bf16) for pair in pairs], axis=1)
    shard = lax.psum_scatter(grads, "page", scatter_dimension=0, tiled=True)
    return shard.astype(f32) + swap(shard).astype(f32)


def page_bounds(segments, is_text):
    pages = jnp.arange(PAGES, dtype=jnp.int32)
    low = jnp.sum(segments[None, :] < pages[:, None], axis=1, dtype=jnp.int32)
    high = jnp.sum(segments[None, :] <= pages[:, None], axis=1, dtype=jnp.int32)
    own_low = jnp.where(is_text, low, pages * PATCH)
    own_high = jnp.where(is_text, high, (pages + 1) * PATCH)

    return jnp.concatenate([own_low, own_high, low, high])


def both_sum(values, mask):
    return values + exchange(values, mask)


def swap(values):
    return lax.ppermute(values, "mod", [(0, 1), (1, 0)])


def local(
    states,
    cotangent,
    segments,
    box_x,
    box_y,
    conv_weight,
    conv_bias,
    w_query,
    b_query,
    w_key,
    w_value,
    b_value,
    w_out,
    b_out,
    table_pos,
    table_x,
    table_y,
    gain_one,
    bias_one,
    w_up,
    b_up,
    w_down,
    b_down,
    gain_two,
    bias_two,
):
    is_text = lax.axis_index("mod") == 0
    d_model = states.shape[3]
    own_low = states[0, 0]
    rows_each = w_query.shape[0]
    d_ff = w_up.shape[1]
    fast = lax.axis_size("page") == 16 and rows_each % 16 == 0 and w_down.shape[0] % 16 == 0
    place = jnp.stack([lax.axis_index("page"), lax.axis_index("mod")]).astype(jnp.int32)
    pack_qkv = jnp.concatenate([w_query, w_key, w_value], axis=1)
    pack_rest = jnp.concatenate([w_out, w_up], axis=1)
    other_low = swap(own_low)
    page_ids, pos_bins, bins_x, bins_y = token_ids(segments[0], box_x[0], box_y[0])
    bounds = page_bounds(segments[0], is_text)
    own_pages = jnp.where(is_text, page_ids[0], page_ids[1])
    features = bin_features(pos_bins.reshape(-1), bins_x.reshape(-1), bins_y.reshape(-1))
    flipped = bin_features(
        POS_BINS - 1 - pos_bins.reshape(-1),
        BOX_BINS - 1 - bins_x.reshape(-1),
        BOX_BINS - 1 - bins_y.reshape(-1),
    )
    own_feats = jnp.where(is_text, features[:TEXT], features[TEXT:])
    own_flip = jnp.where(is_text, flipped[:TEXT], flipped[TEXT:])
    tables = jnp.stack(
        [
            jnp.pad(table_pos, ((0, 0), (0, LANES - table_pos.shape[1]))),
            jnp.pad(table_x, ((0, 0), (0, LANES - table_x.shape[1]))),
            jnp.pad(table_y, ((0, 0), (0, LANES - table_y.shape[1]))),
        ],
        axis=1,
    )
    tables = jnp.pad(tables, ((0, 0), (0, 5), (0, 0)))

    own_states = own_low.astype(f32)
    mixed = dilated_mix(own_states, own_pages, conv_weight, conv_bias)
    mixed_low = mixed.astype(bf16)
    other_pages = jnp.where(is_text, page_ids[1], page_ids[0])
    masks = jnp.pad(
        jnp.stack(
            [
                own_pages == shifted(own_pages, dilation, -1),
                own_pages == shifted(own_pages, -dilation, -1),
                other_pages == shifted(other_pages, dilation, -1),
                other_pages == shifted(other_pages, -dilation, -1),
            ],
            axis=1,
        ).astype(f32),
        ((0, 0), (0, LANES - 4)),
    )
    vectors = jnp.stack(
        [b_out, gain_one, bias_one, b_down, gain_two, bias_two, jnp.zeros_like(b_out), b_out]
    )
    biases = jnp.concatenate([b_query, jnp.zeros_like(b_value), b_value])[None]
    taps = jnp.pad(conv_weight, ((0, 5), (0, 0)))
    bias_up = b_up[None]
    if fast:
        split = (pack_rest.shape[1] // 2 + 127) // 256 * 256
        column_qkv = column_of(half_columns(pack_qkv, is_text))
        early = (features, own_feats, own_flip, tables, bounds, masks, vectors, biases, taps)
        early += (bias_up, mixed_low)
        parts_near = column_parts(
            after(half_columns(pack_rest[:, :split], is_text), column_qkv, other_low, *early)
        )
        w_down = after(w_down, column_qkv)
        pieces_qkv = half_pieces(column_qkv)
        column_near = jnp.stack([after(part, pieces_qkv[0]) for part in parts_near])
        parts_far = column_parts(after(pack_rest[:, split:], column_near))
        pieces_near = half_pieces(column_near)
        pieces_qkv[2] = after(pieces_qkv[2], pieces_near[0])
        pieces_qkv[3] = exchange(pieces_qkv[2], 1)
        groups_qkv = (("halves", 0),)
    else:
        groups_qkv = (("full", 0),)
        pieces_qkv = [lax.all_gather(pack_qkv, "page", axis=0, tiled=True)]
    full_down = lax.all_gather(w_down, "page", axis=0, tiled=True)

    other_mixed = dilated_mix(other_low.astype(f32), other_pages, conv_weight, conv_bias)
    other_mixed = other_mixed.astype(bf16)
    mixed_all = jnp.concatenate(
        [jnp.where(is_text, mixed_low, other_mixed), jnp.where(is_text, other_mixed, mixed_low)],
        axis=0,
    )
    if fast:
        pieces_qkv[0] = after(pieces_qkv[0], mixed_all)
    queries, keys_values, full_qkv, mixed_t = project(
        place, mixed_all, biases, groups_qkv, pieces_qkv
    )
    attend_in = queries
    if fast:
        column_far = jnp.stack([after(part, queries) for part in parts_far])
        across_far = exchange(column_far, 2)
        attend_in = after(queries, column_far)
    context = attend(bounds, attend_in, keys_values, features, own_feats, tables)
    if fast:
        pieces_near[2] = after(pieces_near[2], context)
        pieces_near[3] = exchange(pieces_near[2], 1)
        across_far = after(across_far, context)
        pieces_rest = pieces_near + row_pieces(column_far, across_far)
        groups_rest = (("halves", 0), ("rows", split))
    else:
        pieces_rest = [lax.all_gather(pack_rest, "page", axis=0, tiled=True)]
        groups_rest = (("full", 0),)
    unit, scale, normed_low, normed_t, context_t, active, active_t, slope, full_rest = up_forward(
        place, context, mixed, vectors, bias_up, groups_rest, pieces_rest
    )
    output_row, grad_sum_two, grad_ffn, small_two = down_forward(
        active, full_down, unit, vectors, cotangent[0, 0]
    )
    rows_down = grad_rows(active_t, grad_ffn)
    shard_down = lax.psum_scatter(rows_down, "page", scatter_dimension=0, tiled=True)
    grad_hidden, grad_b_up, grad_first, grad_branch, grad_context, small_one = ffn_back(
        after(grad_ffn, rows_down), slope, grad_sum_two, unit, scale, vectors, full_rest, full_down
    )
    attend_in = grad_context
    if fast:
        pairs = [(context_t, False, grad_branch), (normed_t, False, grad_hidden)]
        keep_rest, send_rest = grad_by_columns(pairs, place, d_model)
        partner_rest = exchange(send_rest, 1)
        held_rest, plane_out = halve_plane(place, keep_rest, partner_rest)
        plane_rest = swap(plane_out)
        attend_in = after(grad_context, plane_out)
    else:
        shard_rest = summed_rows([(context_t, grad_branch), (normed_t, grad_hidden)])
    grad_queries, grad_keys, grad_values, grad_tables = attend_back(
        bounds, queries, keys_values, attend_in, features, own_feats, own_flip, tables
    )
    grad_keys_in, grad_queries_in = grad_keys, grad_queries
    if fast:
        plane_rest = after(plane_rest, grad_queries)
        held_rest, across_out = halve_across(place, held_rest, plane_rest)
        across_rest = exchange(across_out, 2)
        shard_down = after(shard_down, grad_queries)
        shard_down = shard_down.astype(f32) + swap(shard_down).astype(f32)
        grad_queries_in = after(grad_queries, across_out, shard_down)
    pairs = [(mixed_t, True, grad_queries_in), (mixed_t, False, grad_keys), (mixed_t, False, grad_values)]
    if fast:
        keep_qkv, send_qkv = grad_by_columns(pairs, place, d_model)
        partner_qkv = exchange(send_qkv, 1)
        grad_keys_in = after(grad_keys, send_qkv)
    else:
        shard_down = shard_down.astype(f32) + swap(shard_down).astype(f32)
        shard_qkv = summed_rows(
            [(mixed_low.T, grad_queries), (mixed_t, grad_keys), (mixed_t, grad_values)]
        )
    to_other = input_back(place, full_qkv, grad_keys_in, grad_values, ())
    from_other = swap(to_other)
    grad_values_in = grad_values
    if fast:
        partner_qkv = after(partner_qkv, to_other)
        held_qkv, across_out = halve_across(place, keep_qkv, partner_qkv)
        across_qkv = exchange(across_out, 2)
        grad_values_in = after(grad_values, across_out)
    own_part = input_back(place, full_qkv, grad_keys, grad_values_in, (grad_first, grad_queries))
    packed = small_sums(
        own_part,
        to_other,
        own_low,
        other_low,
        masks,
        grad_queries,
        grad_values,
        small_one,
        small_two,
        grad_b_up,
        grad_tables,
    )
    if fast:
        packed = both_sum(packed, 1)
        across_rest = after(across_rest, packed)
        own_rest, sends_rest = column_sends(held_rest, across_rest)
        arrived_rest = column_arrivals(sends_rest)
        packed = after(packed, *sends_rest)
        packed = packed + swap(packed)
        across_qkv = after(across_qkv, packed)
        own_qkv, sends_qkv = column_sends(held_qkv, across_qkv)
        arrived_qkv = column_arrivals(sends_qkv)
        from_other = after(from_other, *sends_qkv)
    else:
        packed = lax.psum(packed, ("mod", "page"))
    grad_in = state_back(own_part, from_other, masks, taps)
    if fast:
        arrived_rest = [after(part, grad_in) for part in arrived_rest]
        total_rest = column_total(own_rest, arrived_rest)
        far_rest = swap(total_rest)
        packed = both_sum(after(packed, total_rest), 2)
        arrived_qkv = [after(part, packed) for part in arrived_qkv]
        total_qkv = column_total(own_qkv, arrived_qkv)
        far_qkv = swap(total_qkv)
        packed = both_sum(both_sum(after(packed, total_qkv), 4), 8)
    g_tables = packed[28:34].reshape(HEADS, 3, LANES)
    if fast:
        shard_rest = jnp.where(
            is_text,
            jnp.concatenate([total_rest, far_rest], axis=1),
            jnp.concatenate([far_rest, total_rest], axis=1),
        ).astype(f32)
        shard_qkv = total_qkv.astype(f32) + far_qkv.astype(f32)
    return (
        output_row[None, None],
        grad_in[None, None],
        packed[0:3],
        packed[3],
        shard_qkv[:, :d_model],
        packed[4],
        shard_qkv[:, d_model : 2 * d_model],
        shard_qkv[:, 2 * d_model :],
        packed[5],
        shard_rest[:, :d_model],
        packed[10],
        g_tables[:, 0, : table_pos.shape[1]],
        g_tables[:, 1, 64 : 64 + table_x.shape[1]],
        g_tables[:, 2, 64 : 64 + table_y.shape[1]],
        packed[8],
        packed[9],
        shard_rest[:, d_model:],
        packed[24:28].reshape(d_ff),
        shard_down,
        packed[18],
        packed[16],
        packed[17],
    )


def solution(mesh):
    rows = P("mod", "page", None, None)
    ids = P("page", None)
    cut = P("page", None)
    return jax.shard_map(
        local,
        mesh=mesh,
        in_specs=(
            rows, rows, ids, ids, ids, P(), P(), cut, P(), cut, cut, P(), cut,
            P(), P(), P(), P(), P(), P(), cut, P(), cut, P(), P(), P(),
        ),
        out_specs=(
            rows, rows, P(), P(), cut, P(), cut, cut, P(), cut, P(), P(), P(),
            P(), P(), P(), cut, P(), cut, P(), P(), P(),
        ),
        check_vma=False,
    )
```

```python
import functools

import jax
import jax.numpy as jnp
import numpy as np
from jax import lax
from jax.experimental import pallas as pl
from jax.experimental.pallas import tpu as pltpu
from jax.sharding import PartitionSpec as P

HEADS = 12
HEAD = 64
GRID = 8
PAGES = 8
POS_BINS = 64
BOX_BINS = 32
PATCH = 64
TEXT = 512
PAIRS = HEADS // 2
LANES = 2 * HEAD
WINDOW = 144
SMALL = 80

dilation = 2
small_cost = pl.CostEstimate(flops=1000, bytes_accessed=1000, transcendentals=0)
norm_eps = 1e-05
mask_fill = -1000000000.0
erfc_poly = (
    0.2367515965428487,
    0.24062179898991767,
    0.18865103029313968,
    0.2877518531132804,
    -0.1648672439458568,
    0.4765735350541787,
    -0.34041833366480423,
    0.07493571514857543,
)
bf16 = jnp.bfloat16
f32 = jnp.float32


def shifted(values, offset, fill_value):
    padding = jnp.full((abs(offset),) + values.shape[1:], fill_value, values.dtype)
    if offset > 0:
        return jnp.concatenate([values[offset:], padding], axis=0)
    return jnp.concatenate([padding, values[:offset]], axis=0)


def dilated_mix(inputs, page_ids, conv_weight, conv_bias):
    summed = inputs + conv_bias + conv_weight[1] * inputs
    for tap_index, offset in ((0, -dilation), (2, dilation)):
        moved_rows = shifted(inputs, offset, 0.0)
        moved_pages = shifted(page_ids, offset, -1)
        same_page = (moved_pages == page_ids)[:, None]
        summed = summed + conv_weight[tap_index] * jnp.where(same_page, moved_rows, 0.0)
    return summed


def bin_features(pos_bins, bins_x, bins_y):
    return jnp.concatenate(
        [
            jax.nn.one_hot(pos_bins, POS_BINS, dtype=bf16),
            jax.nn.one_hot(bins_x, BOX_BINS, dtype=bf16),
            jax.nn.one_hot(bins_y, BOX_BINS, dtype=bf16),
        ],
        axis=1,
    )


def token_ids(text_pages, text_x, text_y):
    text_index = jnp.arange(TEXT, dtype=jnp.int32)
    text_pos = text_index * POS_BINS // TEXT
    patch_pos = text_index % PATCH * POS_BINS // PATCH
    patch_page = text_index // PATCH
    patch_x = text_index % GRID * BOX_BINS // GRID
    patch_y = text_index // GRID % GRID * BOX_BINS // GRID
    page_ids = jnp.stack([text_pages, patch_page])
    pos_bins = jnp.stack([text_pos, patch_pos])
    bins_x = jnp.stack([text_x, patch_x])
    bins_y = jnp.stack([text_y, patch_y])
    return (page_ids, pos_bins, bins_x, bins_y)


def plain_dot(left_side, right_side):
    return jnp.dot(left_side, right_side, preferred_element_type=f32)


def dot_left_t(left_side, right_side):
    return lax.dot_general(
        left_side, right_side, (((0,), (0,)), ((), ())), preferred_element_type=f32
    )


def dot_right_t(left_side, right_side):
    return lax.dot_general(
        left_side, right_side, (((1,), (1,)), ((), ())), preferred_element_type=f32
    )


def iota(shape, axis):
    return lax.broadcasted_iota(jnp.int32, shape, axis)


def bias_block(table_rows):
    pos_part = pltpu.roll(
        jnp.broadcast_to(table_rows[0:1], (POS_BINS, LANES)), 65, 1, stride=1, stride_axis=0
    )
    x_part = pltpu.roll(
        jnp.broadcast_to(table_rows[1:2], (BOX_BINS, LANES)), 33, 1, stride=1, stride_axis=0
    )
    y_part = pltpu.roll(
        jnp.broadcast_to(table_rows[2:3], (BOX_BINS, LANES)), 65, 1, stride=1, stride_axis=0
    )
    lane = iota((POS_BINS, LANES), 1)
    pos_part = jnp.where(lane < POS_BINS, pos_part, 0.0)
    lane = iota((BOX_BINS, LANES), 1)
    x_part = jnp.where((lane >= 64) & (lane < 96), x_part, 0.0)
    y_part = jnp.where(lane >= 96, y_part, 0.0)
    return jnp.concatenate([pos_part, x_part, y_part], axis=0).astype(bf16)


def diagonal_sums(grad_block):
    lane = iota((POS_BINS, LANES), 1)
    pos_part = jnp.where(lane < POS_BINS, grad_block[:64], 0.0)
    lane = iota((BOX_BINS, LANES), 1)
    x_part = jnp.where((lane >= 64) & (lane < 96), grad_block[64:96], 0.0)
    y_part = jnp.where(lane >= 96, grad_block[96:], 0.0)
    pos_part = pltpu.roll(pos_part, 0, 1, stride=1, stride_axis=0)
    x_part = pltpu.roll(x_part, 0, 1, stride=1, stride_axis=0)
    y_part = pltpu.roll(y_part, 96, 1, stride=1, stride_axis=0)
    rows = [jnp.sum(part, axis=0, keepdims=True) for part in (pos_part, x_part, y_part)]
    return jnp.concatenate(rows + [jnp.zeros((5, LANES), f32)], axis=0)


def stacked_heads(rows, low_lane):
    zero = jnp.zeros_like(rows)
    return jnp.concatenate(
        [jnp.where(low_lane, rows, zero), jnp.where(low_lane, zero, rows)], axis=0
    )


def window_start(first, window):
    return pl.multiple_of(jnp.minimum(first // 16 * 16, TEXT - window), 16)


def fits(first, end, window):
    return end - jnp.minimum(first // 16 * 16, TEXT - window) <= window


def for_each_page(bounds, step):
    def body(page, carry):
        own_low, own_high = bounds[page], bounds[PAGES + page]
        key_low, key_high = bounds[2 * PAGES + page], bounds[3 * PAGES + page]
        own_small = fits(own_low, own_high, SMALL)
        key_small = fits(key_low, key_high, SMALL)
        span = (own_low, own_high, key_low, key_high)
        small = own_small & key_small
        mixed = own_small & ~key_small
        for chosen, own_window, key_window in (
            (small, SMALL, SMALL),
            (mixed, SMALL, WINDOW),
            (~own_small, WINDOW, WINDOW),
        ):

            @pl.when(chosen)
            def _():
                step(page, span, own_window, key_window)

        return carry

    lax.fori_loop(0, PAGES, body, 0)


def page_operands(page, span, own_window, key_window, pair, q_ref, k_ref, feat_ref, lookup):
    own_at = window_start(span[0], own_window)
    key_at = window_start(span[2], key_window)
    own_rows, text_rows = pl.ds(own_at, own_window), pl.ds(key_at, key_window)
    patch_at = TEXT + PATCH * page
    if not isinstance(page, int):
        patch_at = pl.multiple_of(patch_at, PATCH)
    patch_rows = pl.ds(patch_at, PATCH)
    lanes = slice(pair * LANES, (pair + 1) * LANES)
    low_lane = iota((own_window, LANES), 1) < HEAD
    queries = stacked_heads(q_ref[own_rows, lanes], low_lane)
    first = 2 * pair * LANES
    rel = jnp.concatenate(
        [
            lookup[own_rows, first : first + LANES],
            lookup[own_rows, first + LANES : first + 2 * LANES],
        ],
        axis=0,
    )
    query_side = jnp.concatenate([rel, queries], axis=1)
    key_side = jnp.concatenate(
        [
            jnp.concatenate([feat_ref[text_rows, :], k_ref[text_rows, lanes]], axis=1),
            jnp.concatenate([feat_ref[patch_rows, :], k_ref[patch_rows, lanes]], axis=1),
        ],
        axis=0,
    )
    own_row = iota((own_window, LANES), 0) + own_at
    own_ok = (own_row >= span[0]) & (own_row < span[1])
    return (
        lanes, low_lane, own_ok, queries, query_side, key_side, own_rows, text_rows, patch_rows, key_at
    )


def set_lookup(lookup, own_feat_ref, table_ref):
    blocks = [bias_block(table_ref[head]) for head in range(table_ref.shape[0])]
    product = jnp.dot(
        own_feat_ref[...], jnp.concatenate(blocks, axis=1), preferred_element_type=f32
    )
    lookup[...] = product.astype(bf16)


def attend_kernel(bounds, q_ref, k_ref, v_ref, feat_ref, own_feat_ref, table_ref, context_ref, lookup):
    set_lookup(lookup, own_feat_ref, table_ref)

    def step(page, span, own_window, key_window):
        column = iota((1, key_window + PATCH), 1)
        key_row = column + window_start(span[2], key_window)
        key_ok = (column >= key_window) | ((key_row >= span[2]) & (key_row < span[3]))
        for pair in range(q_ref.shape[1] // LANES):
            lanes, low_lane, own_ok, _, query_side, key_side, own_rows, text_rows, patch_rows, _ = (
                page_operands(
                    page, span, own_window, key_window, pair, q_ref, k_ref, feat_ref, lookup
                )
            )
            scores = jnp.where(key_ok, dot_right_t(query_side, key_side), mask_fill)
            row_max = jnp.max(scores, axis=1, keepdims=True)
            weights = jnp.exp(scores - row_max)
            total = jnp.sum(weights, axis=1, keepdims=True)
            prob = (weights * (1.0 / total)).astype(bf16)
            values = jnp.concatenate([v_ref[text_rows, lanes], v_ref[patch_rows, lanes]], axis=0)
            mixed = jnp.dot(prob, values, preferred_element_type=f32)
            picked = jnp.where(low_lane, mixed[:own_window], mixed[own_window:])
            before = context_ref[own_rows, lanes].astype(f32)
            context_ref[own_rows, lanes] = jnp.where(own_ok, picked, before).astype(bf16)

    for page in range(PAGES):
        span = [bounds[part * PAGES + page] for part in range(4)]
        step(page, span, WINDOW, WINDOW)


def attend_back_kernel(
    bounds,
    q_ref,
    k_ref,
    v_ref,
    grad_ref,
    feat_ref,
    own_feat_ref,
    flip_feat_ref,
    table_ref,
    grad_q_ref,
    grad_k_ref,
    grad_v_ref,
    grad_table_ref,
    lookup,
    grad_lookup,
):
    set_lookup(lookup, own_feat_ref, table_ref)

    def step(page, span, own_window, key_window):
        row = iota((key_window + PATCH, 1), 0)
        key_row = row + window_start(span[2], key_window)
        key_ok = (row >= key_window) | ((key_row >= span[2]) & (key_row < span[3]))
        for pair in range(q_ref.shape[1] // LANES):
            lanes, low_lane, own_ok, queries, query_side, key_side, own_rows, text_rows, patch_rows, key_at = (
                page_operands(
                    page, span, own_window, key_window, pair, q_ref, k_ref, feat_ref, lookup
                )
            )
            scores = jnp.where(key_ok, dot_right_t(key_side, query_side), mask_fill)
            col_max = jnp.max(scores, axis=0, keepdims=True)
            weights = jnp.exp(scores - col_max)
            total = jnp.sum(weights, axis=0, keepdims=True)
            prob = weights * (1.0 / total)
            grad_rows = grad_ref[own_rows, lanes]
            grad_rows = jnp.where(own_ok, grad_rows, jnp.zeros_like(grad_rows))
            grads = stacked_heads(grad_rows, low_lane)
            values = jnp.concatenate([v_ref[text_rows, lanes], v_ref[patch_rows, lanes]], axis=0)
            grad_prob = dot_right_t(values, grads)
            inner = jnp.sum(prob * grad_prob, axis=0, keepdims=True)
            grad_scores = (prob * (grad_prob - inner)).astype(bf16)
            grad_v = jnp.dot(prob.astype(bf16), grads, preferred_element_type=f32)
            grad_k = jnp.dot(grad_scores, queries, preferred_element_type=f32)
            back = dot_left_t(grad_scores, key_side)
            low, high = back[:own_window], back[own_window:]
            grad_q = jnp.where(low_lane, low[:, LANES:], high[:, LANES:]) * 0.125
            before = grad_q_ref[own_rows, lanes].astype(f32)
            grad_q_ref[own_rows, lanes] = jnp.where(own_ok, grad_q, before).astype(bf16)
            first = 2 * pair * LANES
            for part, at in ((low, first), (high, first + LANES)):
                place_at = slice(at, at + LANES)
                grad_lookup[own_rows, place_at] = jnp.where(
                    own_ok, part[:, :LANES], grad_lookup[own_rows, place_at]
                )
            wide_row = iota((key_window, LANES), 0) + key_at
            text_ok = (wide_row >= span[2]) & (wide_row < span[3])
            for grad, ref in ((grad_k, grad_k_ref), (grad_v, grad_v_ref)):
                before = ref[text_rows, lanes].astype(f32)
                ref[text_rows, lanes] = jnp.where(text_ok, grad[:key_window], before).astype(bf16)
                ref[patch_rows, lanes] = grad[key_window:].astype(bf16)

    for_each_page(bounds, step)
    grad_high = grad_lookup[...].astype(bf16)
    grad_rest = (grad_lookup[...] - grad_high.astype(f32)).astype(bf16)
    flip = flip_feat_ref[...]
    grad_block = dot_left_t(flip, grad_high) + dot_left_t(flip, grad_rest)
    for head in range(table_ref.shape[0]):
        grad_table_ref[head] = diagonal_sums(grad_block[:, head * LANES : (head + 1) * LANES])


def column_spec(rows, group, first=0):
    return pl.BlockSpec((rows, group * LANES), lambda step, bounds: (0, step + first))


def whole_spec(rows):
    return pl.BlockSpec((rows, LANES), lambda step, bounds: (0, 0))


def tables_spec(group):
    return pl.BlockSpec((2 * group, 8, LANES), lambda step, bounds: (step, 0, 0))


def attend(bounds, queries, keys_values, features, own_features, tables):
    group = 1
    return pl.pallas_call(
        attend_kernel,
        grid_spec=pltpu.PrefetchScalarGridSpec(
            num_scalar_prefetch=1,
            grid=(PAIRS // group,),
            in_specs=[
                column_spec(TEXT, group),
                column_spec(2 * TEXT, group),
                column_spec(2 * TEXT, group, PAIRS // group),
                whole_spec(2 * TEXT),
                whole_spec(TEXT),
                tables_spec(group),
            ],
            out_specs=column_spec(TEXT, group),
            scratch_shapes=[pltpu.VMEM((TEXT, 2 * group * LANES), bf16)],
        ),
        out_shape=jax.ShapeDtypeStruct((TEXT, HEADS * HEAD), bf16),
        cost_estimate=small_cost,
        name="attend",
    )(bounds, queries, keys_values, keys_values, features, own_features, tables)


def attend_back(
    bounds, queries, keys_values, grad_context, features, own_features, flip, tables
):
    group = 6
    return pl.pallas_call(
        attend_back_kernel,
        grid_spec=pltpu.PrefetchScalarGridSpec(
            num_scalar_prefetch=1,
            grid=(PAIRS // group,),
            in_specs=[
                column_spec(TEXT, group),
                column_spec(2 * TEXT, group),
                column_spec(2 * TEXT, group, PAIRS // group),
                column_spec(TEXT, group),
                whole_spec(2 * TEXT),
                whole_spec(TEXT),
                whole_spec(TEXT),
                tables_spec(group),
            ],
            out_specs=[
                column_spec(TEXT, group),
                column_spec(2 * TEXT, group),
                column_spec(2 * TEXT, group),
                tables_spec(group),
            ],
            scratch_shapes=[
                pltpu.VMEM((TEXT, 2 * group * LANES), bf16),
                pltpu.VMEM((TEXT, 2 * group * LANES), f32),
            ],
        ),
        out_shape=[
            jax.ShapeDtypeStruct((TEXT, HEADS * HEAD), bf16),
            jax.ShapeDtypeStruct((2 * TEXT, HEADS * HEAD), bf16),
            jax.ShapeDtypeStruct((2 * TEXT, HEADS * HEAD), bf16),
            jax.ShapeDtypeStruct((HEADS, 8, LANES), f32),
        ],
        cost_estimate=small_cost,
        name="attend_back",
    )(
        bounds,
        queries,
        keys_values,
        keys_values,
        grad_context,
        features,
        own_features,
        flip,
        tables,
    )


def exchange(values, mask):
    count = lax.axis_size("page")
    return lax.ppermute(values, "page", [(i, i ^ mask) for i in range(count)])


def after(value, *earlier):
    return lax.optimization_barrier((value, *earlier))[0]


def slot_mask(slot):
    return (slot & 3) * 4 + (slot >> 2) * 2


def project_kernel(groups, place, mixed_ref, bias_ref, *refs):
    *pieces, query_ref, both_ref, weight_ref, mixed_t_ref, sems = refs
    width = mixed_ref.shape[1]
    tokens = query_ref.shape[0]
    copies = start_rows(place, groups, pieces, weight_ref, sems)
    mixed_t_ref[...] = mixed_ref[...].T
    for copy in copies:
        copy.wait()
    own = mixed_ref[pl.ds(pl.multiple_of(place[1] * tokens, 16), tokens), :]
    queries = jnp.dot(own, weight_ref[:, :width], preferred_element_type=f32) + bias_ref[:, :width]
    query_ref[...] = (queries.astype(bf16).astype(f32) * 0.125).astype(bf16)
    for part in range(2):
        rows = pl.ds(part * tokens, tokens)
        for column in (1, 2):
            at = slice(column * width, (column + 1) * width)
            out = slice((column - 1) * width, column * width)
            values = jnp.dot(mixed_ref[rows, :], weight_ref[:, at], preferred_element_type=f32)
            both_ref[rows, out] = (values + bias_ref[:, at]).astype(bf16)


def project(place, mixed, biases, groups, pieces):
    rows, width = mixed.shape
    vmem = pl.BlockSpec(memory_space=pltpu.VMEM)
    return pl.pallas_call(
        functools.partial(project_kernel, groups),
        grid_spec=pltpu.PrefetchScalarGridSpec(
            num_scalar_prefetch=1,
            grid=(),
            in_specs=[vmem] * 2 + any_specs(len(pieces)),
            out_specs=[vmem] * 4,
            scratch_shapes=[pltpu.SemaphoreType.DMA((32,))],
        ),
        out_shape=[
            jax.ShapeDtypeStruct((rows // 2, width), bf16),
            jax.ShapeDtypeStruct((rows, 2 * width), bf16),
            jax.ShapeDtypeStruct((width, 3 * width), bf16),
            jax.ShapeDtypeStruct((width, rows), bf16),
        ],
        cost_estimate=small_cost,
        compiler_params=pltpu.CompilerParams(vmem_limit_bytes=16 << 20),
        name="project",
    )(place, mixed, biases, *pieces)


def column_parts(shard):
    return [shard] + [exchange(shard, 4 * step) for step in (1, 2, 3)]


def half_pieces(column):
    eight = jnp.concatenate([column, exchange(column, 2)])
    far = swap(eight)
    return [eight, exchange(eight, 1), far, exchange(far, 1)]


def row_pieces(column, across):
    return [column, exchange(column, 1), across, exchange(across, 1)]


def column_of(shard):
    return jnp.stack(column_parts(shard))


def row_copies(place, groups, refs, full, sems, first=0):
    copies = []
    for kind, column in groups:
        if kind == "full":
            piece, *refs = refs
            width = piece.shape[1]
            target = full.at[:, pl.ds(column, width)]
            copies.append(pltpu.make_async_copy(piece, target, sems.at[first + len(copies)]))
            continue
        pieces, refs = refs[:4], refs[4:]
        _, rows, width = pieces[0].shape
        for index in range(32 if kind == "halves" else 16):
            at = column
            if kind == "halves":
                source, slot = index >> 3, index & 7
                mask = slot_mask(slot) + (source & 1)
                at = pl.multiple_of(column + (place[1] ^ (source >> 1)) * width, 128)
            else:
                source, slot = index & 3, index >> 2
                mask = slot * 4 + source
            row = pl.multiple_of((place[0] ^ mask) * rows, 16)
            copies.append(
                pltpu.make_async_copy(
                    pieces[source].at[slot],
                    full.at[pl.ds(row, rows), pl.ds(at, width)],
                    sems.at[first + len(copies)],
                )
            )
    return copies


def start_rows(place, groups, refs, full, sems):
    copies = row_copies(place, groups, refs, full, sems)
    for copy in copies:
        copy.start()
    return copies


def gelu_parts(values):
    size = jnp.abs(values)
    t = 1.0 / (1.0 + (0.42 * 0.7071067811865476) * size)
    poly = jnp.full_like(t, erfc_poly[-1])
    for coefficient in erfc_poly[-2::-1]:
        poly = poly * t + coefficient
    bell = jnp.exp(-0.5 * values * values)
    tail = (0.5 * t) * (poly * bell)
    cdf = jnp.where(values >= 0.0, 1.0 - tail, tail)
    return values * cdf, cdf + (values * 0.3989422804014327) * bell


def normalized(values):
    centered = values - jnp.mean(values, axis=1, keepdims=True)
    variance = jnp.mean(centered * centered, axis=1, keepdims=True)
    scale = lax.rsqrt(variance + norm_eps)
    return centered * scale, scale


def norm_back(grads, unit, scale, gain):
    scaled = grads * gain
    mean = jnp.mean(scaled, axis=1, keepdims=True)
    inner = jnp.mean(scaled * unit, axis=1, keepdims=True)
    return scale * (scaled - mean - unit * inner)


def up_kernel(groups, place, context_ref, mixed_ref, vec_ref, bias_ref, *refs):
    *pieces, unit_ref, scale_ref, low_ref, low_t_ref, context_t_ref = refs[:-9]
    active_ref, active_t_ref, slope_ref, full_ref = refs[-9:-5]
    weight, hidden, low, sems, full_sem = refs[-5:]
    step = pl.program_id(0)
    tiles = pl.num_programs(0) - 1
    width = context_ref.shape[1]
    tile = active_ref.shape[1]
    last_group = 16 if len(groups) > 1 else 0

    def full_copy():
        return pltpu.make_async_copy(weight, full_ref, full_sem)

    @pl.when(step == 0)
    def _():
        copies = row_copies(place, groups, pieces, weight, sems)
        for copy in copies:
            copy.start()
        context_t_ref[...] = context_ref[...].T
        for copy in copies[: len(copies) - last_group]:
            copy.wait()
        branch = jnp.dot(context_ref[...], weight[:, :width], preferred_element_type=f32)
        unit, scale = normalized(mixed_ref[...] + branch + vec_ref[0:1])
        unit_ref[...] = unit
        scale_ref[...] = jnp.broadcast_to(scale, scale_ref.shape)
        normed = (unit * vec_ref[1:2] + vec_ref[2:3]).astype(bf16)
        low[...] = normed
        low_ref[...] = normed
        low_t_ref[...] = normed.T

    @pl.when(step == 1)
    def _():
        if last_group:
            for copy in row_copies(place, groups[1:], pieces[4:], weight, sems, 32):
                copy.wait()
        full_copy().start()

    def product():
        at = pl.multiple_of(width + step * tile, 128)
        return jnp.dot(low[...], weight[:, pl.ds(at, tile)], preferred_element_type=f32)

    def activate():
        active, slope = gelu_parts(hidden[(step + 1) % 2] + bias_ref[...])
        active = active.astype(bf16)
        active_ref[...] = active
        active_t_ref[...] = active.T
        slope_ref[...] = slope.astype(bf16)

    @pl.when(step == 0)
    def _():
        hidden[step % 2] = product()

    @pl.when((step > 0) & (step < tiles))
    def _():
        hidden[step % 2] = product()
        activate()

    @pl.when(step == tiles)
    def _():
        activate()
        full_copy().wait()


def any_specs(count):
    return [pl.BlockSpec(memory_space=pl.ANY)] * count


def up_forward(place, context, mixed, vectors, bias_up, groups, pieces):
    tokens, width = mixed.shape
    hidden_width = bias_up.shape[1]
    tile = 512
    whole = lambda step, place: (0, 0)
    last = lambda step, place: (0, jnp.maximum(step - 1, 0))
    last_t = lambda step, place: (jnp.maximum(step - 1, 0), 0)
    return pl.pallas_call(
        functools.partial(up_kernel, groups),
        grid_spec=pltpu.PrefetchScalarGridSpec(
            num_scalar_prefetch=1,
            grid=(hidden_width // tile + 1,),
            in_specs=[
                pl.BlockSpec((tokens, width), whole),
                pl.BlockSpec((tokens, width), whole),
                pl.BlockSpec(vectors.shape, whole),
                pl.BlockSpec((1, tile), last),
            ]
            + any_specs(len(pieces)),
            out_specs=[
                pl.BlockSpec((tokens, width), whole),
                pl.BlockSpec((tokens, 128), whole),
                pl.BlockSpec((tokens, width), whole),
                pl.BlockSpec((width, tokens), whole),
                pl.BlockSpec((width, tokens), whole),
                pl.BlockSpec((tokens, tile), last),
                pl.BlockSpec((tile, tokens), last_t),
                pl.BlockSpec((tokens, tile), last),
                pl.BlockSpec(memory_space=pl.ANY),
            ],
            scratch_shapes=[
                pltpu.VMEM((width, width + hidden_width), bf16),
                pltpu.VMEM((2, tokens, tile), f32),
                pltpu.VMEM((tokens, width), bf16),
                pltpu.SemaphoreType.DMA((48,)),
                pltpu.SemaphoreType.DMA,
            ],
        ),
        out_shape=[
            jax.ShapeDtypeStruct((tokens, width), f32),
            jax.ShapeDtypeStruct((tokens, 128), f32),
            jax.ShapeDtypeStruct((tokens, width), bf16),
            jax.ShapeDtypeStruct((width, tokens), bf16),
            jax.ShapeDtypeStruct((width, tokens), bf16),
            jax.ShapeDtypeStruct((tokens, hidden_width), bf16),
            jax.ShapeDtypeStruct((hidden_width, tokens), bf16),
            jax.ShapeDtypeStruct((tokens, hidden_width), bf16),
            jax.ShapeDtypeStruct((width, width + hidden_width), bf16),
        ],
        cost_estimate=small_cost,
        name="up_forward",
    )(place, context, mixed, vectors, bias_up, *pieces)


def down_kernel(active_ref, weight_ref, unit_ref, vec_ref, grad_ref, *refs):
    out_ref, sum_ref, low_ref, small_ref, total = refs
    step = pl.program_id(0)
    product = jnp.dot(active_ref[...], weight_ref[...], preferred_element_type=f32)

    @pl.when(step == 0)
    def _():
        total[...] = product

    @pl.when(step > 0)
    def _():
        total[...] += product

    @pl.when(step == pl.num_programs(0) - 1)
    def _():
        tokens, width = unit_ref.shape
        half = tokens // 2
        smalls = [jnp.zeros((1, width), f32)] * 3
        for part in range(2):
            rows = pl.ds(part * half, half)
            normed = unit_ref[rows, :] * vec_ref[1:2] + vec_ref[2:3]
            unit, scale = normalized(normed + total[rows, :] + vec_ref[3:4])
            out_ref[rows, :] = (unit * vec_ref[4:5] + vec_ref[5:6]).astype(bf16)
            grads = grad_ref[rows, :].astype(f32)
            back = norm_back(grads, unit, scale, vec_ref[4:5])
            low = back.astype(bf16)
            sum_ref[rows, :] = back
            low_ref[rows, :] = low
            for index, term in enumerate((grads * unit, grads, low.astype(f32))):
                smalls[index] = smalls[index] + jnp.sum(term, axis=0, keepdims=True)
        small_ref[...] = jnp.concatenate(smalls + [jnp.zeros((5, width), f32)], axis=0)


def down_forward(active, weight, unit, vectors, grads):
    tokens, width = unit.shape
    hidden_width = active.shape[1]
    tile = 768
    whole = lambda step: (0, 0)
    token_block = pl.BlockSpec((tokens, width), whole)
    return pl.pallas_call(
        down_kernel,
        grid=(hidden_width // tile,),
        in_specs=[
            pl.BlockSpec((tokens, tile), lambda step: (0, step)),
            pl.BlockSpec((tile, width), lambda step: (step, 0)),
            token_block,
            pl.BlockSpec(vectors.shape, whole),
            token_block,
        ],
        out_specs=[token_block] * 3 + [pl.BlockSpec((8, width), whole)],
        scratch_shapes=[pltpu.VMEM((tokens, width), f32)],
        out_shape=[
            jax.ShapeDtypeStruct((tokens, width), bf16),
            jax.ShapeDtypeStruct((tokens, width), f32),
            jax.ShapeDtypeStruct((tokens, width), bf16),
            jax.ShapeDtypeStruct((8, width), f32),
        ],
        cost_estimate=small_cost,
        name="down_forward",
    )(active, weight, unit, vectors, grads)


def ffn_back_kernel(*refs):
    low_ref, slope_ref, sum_ref, unit_ref, scale_ref, vec_ref = refs[:6]
    down_ref, up_ref, out_weight_ref = refs[6:9]
    hidden_ref, bias_ref, first_ref, branch_ref, context_ref, small_ref, total = refs[9:]
    step = pl.program_id(0)
    tokens, width = unit_ref.shape
    tile = slope_ref.shape[1]
    half = tokens // 2

    @pl.when(step == 0)
    def _():
        total[...] = sum_ref[...]

    bias = jnp.zeros((1, tile), f32)
    for part in range(2):
        rows = pl.ds(part * half, half)
        grads = dot_right_t(low_ref[rows, :], down_ref[...]) * slope_ref[rows, :].astype(f32)
        grads = grads.astype(bf16)
        hidden_ref[rows, :] = grads
        bias = bias + jnp.sum(grads.astype(f32), axis=0, keepdims=True)
        total[rows, :] += dot_right_t(grads, up_ref[...])
    bias_ref[...] = bias

    @pl.when(step == pl.num_programs(0) - 1)
    def _():
        grads = total[...]
        unit = unit_ref[...]
        first = norm_back(grads, unit, scale_ref[:, 0:1], vec_ref[1:2])
        branch = first.astype(bf16)
        first_ref[...] = first
        branch_ref[...] = branch
        context_ref[...] = dot_right_t(branch, out_weight_ref[...]).astype(bf16)
        smalls = [
            jnp.sum(term, axis=0, keepdims=True)
            for term in (grads * unit, grads, branch.astype(f32))
        ]
        small_ref[...] = jnp.concatenate(smalls + [jnp.zeros((5, width), f32)], axis=0)


def ffn_back(low, slope, total, unit, scale, vectors, full_rest, full_down):
    tokens, width = unit.shape
    hidden_width = slope.shape[1]
    tile = 768
    whole = lambda step: (0, 0)
    column = lambda step: (0, step)
    token_block = pl.BlockSpec((tokens, width), whole)
    return pl.pallas_call(
        ffn_back_kernel,
        grid=(hidden_width // tile,),
        in_specs=[
            token_block,
            pl.BlockSpec((tokens, tile), column),
            token_block,
            token_block,
            pl.BlockSpec((tokens, 128), whole),
            pl.BlockSpec(vectors.shape, whole),
            pl.BlockSpec((tile, width), lambda step: (step, 0)),
            pl.BlockSpec((width, tile), lambda step: (0, step + 1)),
            pl.BlockSpec((width, width), whole),
        ],
        out_specs=[
            pl.BlockSpec((tokens, tile), column),
            pl.BlockSpec((1, tile), column),
            token_block,
            token_block,
            token_block,
            pl.BlockSpec((8, width), whole),
        ],
        scratch_shapes=[pltpu.VMEM((tokens, width), f32)],
        out_shape=[
            jax.ShapeDtypeStruct((tokens, hidden_width), bf16),
            jax.ShapeDtypeStruct((1, hidden_width), f32),
            jax.ShapeDtypeStruct((tokens, width), f32),
            jax.ShapeDtypeStruct((tokens, width), bf16),
            jax.ShapeDtypeStruct((tokens, width), bf16),
            jax.ShapeDtypeStruct((8, width), f32),
        ],
        cost_estimate=small_cost,
        name="ffn_back",
    )(low, slope, total, unit, scale, vectors, full_down, full_rest, full_rest)


def grad_rows_kernel(x_ref, h_ref, out_ref):
    out_ref[...] = jnp.dot(x_ref[...], h_ref[...], preferred_element_type=f32).astype(bf16)


def grad_rows(inputs_t, grads):
    width, tokens = inputs_t.shape
    columns = grads.shape[1]
    return pl.pallas_call(
        grad_rows_kernel,
        grid=(4,),
        in_specs=[
            pl.BlockSpec((width // 4, tokens), lambda step: (step, 0)),
            pl.BlockSpec((tokens, columns), lambda step: (0, 0)),
        ],
        out_specs=pl.BlockSpec((width // 4, columns), lambda step: (step, 0)),
        out_shape=jax.ShapeDtypeStruct((width, columns), bf16),
        cost_estimate=small_cost,
        name="grad_rows",
    )(inputs_t, grads)


def grad_columns_kernel(parts, place, *refs):
    count = len(parts)
    ins, keep_ref, send_ref, scratch = (
        refs[: 2 * count],
        refs[2 * count],
        refs[2 * count + 1],
        refs[2 * count + 2 :],
    )
    rows, tile = keep_ref.shape[1], keep_ref.shape[2]
    step = pl.program_id(0)
    first = 0
    for index, steps in enumerate(parts):
        x_ref, h_ref, ordered = ins[2 * index], ins[2 * index + 1], scratch[index]

        @pl.when(step == first)
        def _():
            for slot in range(16):
                mask = slot_mask(slot & 7) + (slot >> 3)
                at = pl.multiple_of((place[0] ^ mask) * rows, 16)
                ordered[pl.ds(slot * rows, rows), :] = x_ref[pl.ds(at, rows), :]

        @pl.when((step >= first) & (step < first + steps))
        def _():
            product = jnp.dot(ordered[...], h_ref[...], preferred_element_type=f32).astype(bf16)
            keep_ref[...] = product[: 8 * rows].reshape(8, rows, tile)
            send_ref[...] = product[8 * rows :].reshape(8, rows, tile)

        first = first + steps


def grad_by_columns(pairs, place, tile):
    width = pairs[0][0].shape[0]
    rows = width // 16
    parts = tuple(sum(grad.shape[1] for grad in grads) // tile for _, _, *grads in pairs)
    steps = sum(parts)
    specs = []
    operands = []
    scratch = []
    first = 0
    for (inputs_t, own, *grads), count in zip(pairs, parts):
        tokens = grads[0].shape[0]
        block = (lambda step, place: (0, place[1])) if own else (lambda step, place: (0, 0))
        specs.append(pl.BlockSpec((width, tokens), block))

        def column(step, place, first=first, count=count):
            return (0, jnp.clip(step - first, 0, count - 1))

        specs.append(pl.BlockSpec((tokens, tile), column))
        operands += [inputs_t, *grads]
        scratch.append(pltpu.VMEM((width, tokens), bf16))
        first = first + count
    half = jax.ShapeDtypeStruct((8, rows, steps * tile), bf16)
    return pl.pallas_call(
        functools.partial(grad_columns_kernel, parts),
        grid_spec=pltpu.PrefetchScalarGridSpec(
            num_scalar_prefetch=1,
            grid=(steps,),
            in_specs=specs,
            out_specs=[pl.BlockSpec((8, rows, tile), lambda step, place: (0, 0, step))] * 2,
            scratch_shapes=scratch,
        ),
        out_shape=[half, half],
        cost_estimate=small_cost,
        compiler_params=pltpu.CompilerParams(vmem_limit_bytes=16 << 20),
        name="grad_columns",
    )(place, *operands)


def key_back_kernel(place, gk_ref, gv_ref, wk_ref, wv_ref, out_ref):
    total = dot_right_t(gk_ref[...], wk_ref[...]) + dot_right_t(gv_ref[...], wv_ref[...])
    out_ref[...] = total.astype(out_ref.dtype)


def own_back_kernel(place, first_ref, gq_ref, gk_ref, gv_ref, wq_ref, wk_ref, wv_ref, out_ref):
    total = dot_right_t(gk_ref[...], wk_ref[...]) + dot_right_t(gv_ref[...], wv_ref[...])
    out_ref[...] = first_ref[...] + total + dot_right_t(gq_ref[...], wq_ref[...])


def input_back(place, weights, grad_keys, grad_values, others):
    width = weights.shape[0]
    tokens = grad_keys.shape[0] // 2
    whole = pl.BlockSpec((tokens, width), lambda step, place: (0, 0))
    row = lambda step, place: ((place[1] if others else 1 - place[1]), 0)
    if others:
        kernel, leading, first, dtype = own_back_kernel, [whole, whole], 0, f32
    else:
        kernel, leading, first, dtype = key_back_kernel, [], 1, bf16
    operands = list(others) + [grad_keys, grad_values] + [weights] * (3 - first)
    specs = [pl.BlockSpec((tokens, width), row)] * 2
    for block in range(first, 3):
        specs.append(pl.BlockSpec((width, width), lambda step, place, block=block: (0, block)))
    return pl.pallas_call(
        kernel,
        grid_spec=pltpu.PrefetchScalarGridSpec(
            num_scalar_prefetch=1, grid=(1,), in_specs=leading + specs, out_specs=whole
        ),
        out_shape=jax.ShapeDtypeStruct((tokens, width), dtype),
        cost_estimate=small_cost,
        compiler_params=pltpu.CompilerParams(vmem_limit_bytes=16 << 20),
        name="input_back",
    )(place, *operands)


def back_rows(values, mask):
    return jnp.where(mask, pltpu.roll(values, dilation, 0), 0.0)


def ahead_rows(values, mask):
    return jnp.where(mask, pltpu.roll(values, values.shape[0] - dilation, 0), 0.0)


def tap_sums(grads, inputs, ahead, back):
    terms = (grads * back_rows(inputs, back), grads * inputs, grads * ahead_rows(inputs, ahead), grads)
    return [jnp.sum(term, axis=0, keepdims=True) for term in terms]


def small_sums_kernel(
    own_ref, other_ref, x_ref, x_other_ref, mask_ref, gq_ref, gv_ref, one_ref, two_ref, up_ref, table_ref, out_ref
):
    width = own_ref.shape[1]
    mask = mask_ref[...] > 0.0
    own = tap_sums(own_ref[...], x_ref[...].astype(f32), mask[:, 0:1], mask[:, 1:2])
    other = tap_sums(
        other_ref[...].astype(f32), x_other_ref[...].astype(f32), mask[:, 2:3], mask[:, 3:4]
    )
    rows = [a + b for a, b in zip(own, other)]
    for ref in (gq_ref, gv_ref):
        rows.append(jnp.sum(ref[...].astype(f32), axis=0, keepdims=True))
    rows.append(jnp.zeros((2, width), f32))
    out_ref[0:8] = jnp.concatenate(rows, axis=0)
    out_ref[8:16] = one_ref[...]
    out_ref[16:24] = two_ref[...]
    count = up_ref.shape[1] // width
    for index in range(count):
        out_ref[24 + index : 25 + index] = up_ref[:, index * width : (index + 1) * width]
    for index in range(3 * HEADS):
        row, lane = 28 + index // 6, index % 6 * LANES
        table = table_ref[index // 3]
        out_ref[row : row + 1, lane : lane + LANES] = table[index % 3 : index % 3 + 1]
    out_ref[34:40] = jnp.zeros((6, width), f32)


def small_sums(*operands):
    return pl.pallas_call(
        small_sums_kernel,
        out_shape=jax.ShapeDtypeStruct((40, operands[0].shape[1]), f32),
        cost_estimate=small_cost,
        compiler_params=pltpu.CompilerParams(vmem_limit_bytes=24 << 20),
        name="small_sums",
    )(*operands)


def state_back_kernel(own_ref, other_ref, mask_ref, tap_ref, out_ref):
    grads = own_ref[...] + other_ref[...].astype(f32)
    mask = mask_ref[...] > 0.0
    total = grads + tap_ref[1:2] * grads
    total = total + tap_ref[0:1] * ahead_rows(grads, mask[:, 0:1])
    total = total + tap_ref[2:3] * back_rows(grads, mask[:, 1:2])
    out_ref[...] = total.astype(bf16)


def state_back(own, other, masks, taps):
    return pl.pallas_call(
        state_back_kernel,
        out_shape=jax.ShapeDtypeStruct(own.shape, bf16),
        cost_estimate=small_cost,
        compiler_params=pltpu.CompilerParams(vmem_limit_bytes=20 << 20),
        name="state_back",
    )(own, other, masks, taps)


def first_half_kernel(place, keep_near, part_near, keep_far, part_far, held_ref, out_ref):
    held_ref[...] = keep_near[...].astype(f32) + part_near[...].astype(f32)
    out_ref[...] = (keep_far[...].astype(f32) + part_far[...].astype(f32)).astype(bf16)


def halve_call(place, keep, partner, specs, half_shape, steps):
    near, far, out = specs
    return pl.pallas_call(
        first_half_kernel,
        grid_spec=pltpu.PrefetchScalarGridSpec(
            num_scalar_prefetch=1,
            grid=(steps,),
            in_specs=[near, near, far, far],
            out_specs=[out, out],
        ),
        out_shape=[
            jax.ShapeDtypeStruct(half_shape, f32),
            jax.ShapeDtypeStruct(half_shape, bf16),
        ],
        cost_estimate=small_cost,
        compiler_params=pltpu.CompilerParams(vmem_limit_bytes=12 << 20),
        name="halve",
    )(place, keep, partner, keep, partner)


def halve_across(place, keep, partner):
    _, rows, width = keep.shape
    near = pl.BlockSpec((1, rows, width), lambda step, place: (step, 0, 0))
    far = pl.BlockSpec((1, rows, width), lambda step, place: (step + 4, 0, 0))
    return halve_call(place, keep, partner, (near, far, near), (4, rows, width), 4)


def halve_plane(place, keep, partner):
    _, rows, width = keep.shape
    block = (2, rows, width // 2)
    near = pl.BlockSpec(block, lambda step, place: (step, 0, place[1]))
    far = pl.BlockSpec(block, lambda step, place: (step, 0, 1 - place[1]))
    out = pl.BlockSpec(block, lambda step, place: (step, 0, 0))
    return halve_call(place, keep, partner, (near, far, out), (8, rows, width // 2), 4)


def column_kernel(held_ref, across_ref, own_ref, *sends):
    own_ref[...] = held_ref[0] + across_ref[0].astype(f32)
    for step, send in enumerate(sends, 1):
        send[...] = (held_ref[step] + across_ref[step].astype(f32)).astype(bf16)


def column_sends(held, across):
    _, rows, width = held.shape
    tile = 384
    out = pl.BlockSpec((rows, tile), lambda step: (0, step))
    block = pl.BlockSpec((4, rows, tile), lambda step: (0, 0, step))
    own, *sends = pl.pallas_call(
        column_kernel,
        grid=(width // tile,),
        in_specs=[block, block],
        out_specs=[out] * 4,
        out_shape=[jax.ShapeDtypeStruct((rows, width), f32)]
        + [jax.ShapeDtypeStruct((rows, width), bf16)] * 3,
        cost_estimate=small_cost,
        compiler_params=pltpu.CompilerParams(vmem_limit_bytes=12 << 20),
        name="column_sends",
    )(held, across)
    return own, sends


def column_arrivals(sends):
    return [exchange(send, 4 * step) for step, send in enumerate(sends, 1)]


def column_total(own, arrived):
    total = own
    for part in arrived:
        total = total + part.astype(f32)
    return total.astype(bf16)


def half_columns(values, first):
    half = values.shape[-1] // 2
    return jnp.where(first, values[..., :half], values[..., half:])


def summed_rows(pairs):
    grads = jnp.concatenate([plain_dot(*pair).astype(bf16) for pair in pairs], axis=1)
    shard = lax.psum_scatter(grads, "page", scatter_dimension=0, tiled=True)
    return shard.astype(f32) + swap(shard).astype(f32)


def page_bounds(segments, is_text):
    pages = jnp.arange(PAGES, dtype=jnp.int32)
    low = jnp.sum(segments[None, :] < pages[:, None], axis=1, dtype=jnp.int32)
    high = jnp.sum(segments[None, :] <= pages[:, None], axis=1, dtype=jnp.int32)
    own_low = jnp.where(is_text, low, pages * PATCH)
    own_high = jnp.where(is_text, high, (pages + 1) * PATCH)

    return jnp.concatenate([own_low, own_high, low, high])


def both_sum(values, mask):
    return values + exchange(values, mask)


def swap(values):
    return lax.ppermute(values, "mod", [(0, 1), (1, 0)])


def local(
    states,
    cotangent,
    segments,
    box_x,
    box_y,
    conv_weight,
    conv_bias,
    w_query,
    b_query,
    w_key,
    w_value,
    b_value,
    w_out,
    b_out,
    table_pos,
    table_x,
    table_y,
    gain_one,
    bias_one,
    w_up,
    b_up,
    w_down,
    b_down,
    gain_two,
    bias_two,
):
    is_text = lax.axis_index("mod") == 0
    d_model = states.shape[3]
    own_low = states[0, 0]
    rows_each = w_query.shape[0]
    d_ff = w_up.shape[1]
    fast = lax.axis_size("page") == 16 and rows_each % 16 == 0 and w_down.shape[0] % 16 == 0
    place = jnp.stack([lax.axis_index("page"), lax.axis_index("mod")]).astype(jnp.int32)
    pack_qkv = jnp.concatenate([w_query, w_key, w_value], axis=1)
    pack_rest = jnp.concatenate([w_out, w_up], axis=1)
    other_low = swap(own_low)
    page_ids, pos_bins, bins_x, bins_y = token_ids(segments[0], box_x[0], box_y[0])
    bounds = page_bounds(segments[0], is_text)
    own_pages = jnp.where(is_text, page_ids[0], page_ids[1])
    features = bin_features(pos_bins.reshape(-1), bins_x.reshape(-1), bins_y.reshape(-1))
    flipped = bin_features(
        POS_BINS - 1 - pos_bins.reshape(-1),
        BOX_BINS - 1 - bins_x.reshape(-1),
        BOX_BINS - 1 - bins_y.reshape(-1),
    )
    own_feats = jnp.where(is_text, features[:TEXT], features[TEXT:])
    own_flip = jnp.where(is_text, flipped[:TEXT], flipped[TEXT:])
    tables = jnp.stack(
        [
            jnp.pad(table_pos, ((0, 0), (0, LANES - table_pos.shape[1]))),
            jnp.pad(table_x, ((0, 0), (0, LANES - table_x.shape[1]))),
            jnp.pad(table_y, ((0, 0), (0, LANES - table_y.shape[1]))),
        ],
        axis=1,
    )
    tables = jnp.pad(tables, ((0, 0), (0, 5), (0, 0)))

    own_states = own_low.astype(f32)
    mixed = dilated_mix(own_states, own_pages, conv_weight, conv_bias)
    mixed_low = mixed.astype(bf16)
    other_pages = jnp.where(is_text, page_ids[1], page_ids[0])
    masks = jnp.pad(
        jnp.stack(
            [
                own_pages == shifted(own_pages, dilation, -1),
                own_pages == shifted(own_pages, -dilation, -1),
                other_pages == shifted(other_pages, dilation, -1),
                other_pages == shifted(other_pages, -dilation, -1),
            ],
            axis=1,
        ).astype(f32),
        ((0, 0), (0, LANES - 4)),
    )
    vectors = jnp.stack(
        [b_out, gain_one, bias_one, b_down, gain_two, bias_two, jnp.zeros_like(b_out), b_out]
    )
    biases = jnp.concatenate([b_query, jnp.zeros_like(b_value), b_value])[None]
    taps = jnp.pad(conv_weight, ((0, 5), (0, 0)))
    bias_up = b_up[None]
    if fast:
        split = (pack_rest.shape[1] // 2 + 127) // 256 * 256
        column_qkv = column_of(half_columns(pack_qkv, is_text))
        early = (features, own_feats, own_flip, tables, bounds, masks, vectors, biases, taps)
        parts_near = column_parts(after(half_columns(pack_rest[:, :split], is_text), column_qkv))
        w_down = after(w_down, column_qkv)
        pieces_qkv = half_pieces(column_qkv)
        column_near = jnp.stack([after(part, pieces_qkv[0]) for part in parts_near])
        parts_far = column_parts(after(pack_rest[:, split:], column_near))
        pieces_near = half_pieces(column_near)
        pieces_qkv[2] = after(pieces_qkv[2], pieces_near[0])
        pieces_qkv[3] = exchange(pieces_qkv[2], 1)
        groups_qkv = (("halves", 0),)
    else:
        groups_qkv = (("full", 0),)
        pieces_qkv = [lax.all_gather(pack_qkv, "page", axis=0, tiled=True)]
    full_down = lax.all_gather(w_down, "page", axis=0, tiled=True)

    other_mixed = dilated_mix(other_low.astype(f32), other_pages, conv_weight, conv_bias)
    other_mixed = other_mixed.astype(bf16)
    mixed_all = jnp.concatenate(
        [jnp.where(is_text, mixed_low, other_mixed), jnp.where(is_text, other_mixed, mixed_low)],
        axis=0,
    )
    if fast:
        pieces_qkv[0] = after(pieces_qkv[0], mixed_all, bias_up, *early)
    queries, keys_values, full_qkv, mixed_t = project(
        place, mixed_all, biases, groups_qkv, pieces_qkv
    )
    attend_in = queries
    if fast:
        column_far = jnp.stack([after(part, queries) for part in parts_far])
        across_far = exchange(column_far, 2)
        attend_in = after(queries, column_far)
    context = attend(bounds, attend_in, keys_values, features, own_feats, tables)
    if fast:
        pieces_near[2] = after(pieces_near[2], context)
        pieces_near[3] = exchange(pieces_near[2], 1)
        across_far = after(across_far, context)
        pieces_rest = pieces_near + row_pieces(column_far, across_far)
        groups_rest = (("halves", 0), ("rows", split))
    else:
        pieces_rest = [lax.all_gather(pack_rest, "page", axis=0, tiled=True)]
        groups_rest = (("full", 0),)
    unit, scale, normed_low, normed_t, context_t, active, active_t, slope, full_rest = up_forward(
        place, context, mixed, vectors, bias_up, groups_rest, pieces_rest
    )
    output_row, grad_sum_two, grad_ffn, small_two = down_forward(
        active, full_down, unit, vectors, cotangent[0, 0]
    )
    rows_down = grad_rows(active_t, grad_ffn)
    shard_down = lax.psum_scatter(rows_down, "page", scatter_dimension=0, tiled=True)
    grad_hidden, grad_b_up, grad_first, grad_branch, grad_context, small_one = ffn_back(
        after(grad_ffn, rows_down), slope, grad_sum_two, unit, scale, vectors, full_rest, full_down
    )
    attend_in = grad_context
    if fast:
        pairs = [(context_t, False, grad_branch), (normed_t, False, grad_hidden)]
        keep_rest, send_rest = grad_by_columns(pairs, place, d_model)
        partner_rest = exchange(send_rest, 1)
        held_rest, plane_out = halve_plane(place, keep_rest, partner_rest)
        plane_rest = swap(plane_out)
        attend_in = after(grad_context, plane_out)
    else:
        shard_rest = summed_rows([(context_t, grad_branch), (normed_t, grad_hidden)])
    grad_queries, grad_keys, grad_values, grad_tables = attend_back(
        bounds, queries, keys_values, attend_in, features, own_feats, own_flip, tables
    )
    grad_keys_in, grad_queries_in = grad_keys, grad_queries
    if fast:
        plane_rest = after(plane_rest, grad_queries)
        held_rest, across_out = halve_across(place, held_rest, plane_rest)
        across_rest = exchange(across_out, 2)
        grad_queries_in = after(grad_queries, across_out)
    pairs = [(mixed_t, True, grad_queries_in), (mixed_t, False, grad_keys), (mixed_t, False, grad_values)]
    if fast:
        keep_qkv, send_qkv = grad_by_columns(pairs, place, d_model)
        partner_qkv = exchange(send_qkv, 1)
        grad_keys_in = after(grad_keys, send_qkv)
    else:
        shard_down = shard_down.astype(f32) + swap(shard_down).astype(f32)
        shard_qkv = summed_rows(
            [(mixed_low.T, grad_queries), (mixed_t, grad_keys), (mixed_t, grad_values)]
        )
    to_other = input_back(place, full_qkv, grad_keys_in, grad_values, ())
    from_other = swap(to_other)
    grad_values_in = grad_values
    if fast:
        partner_qkv = after(partner_qkv, to_other)
        held_qkv, across_out = halve_across(place, keep_qkv, partner_qkv)
        across_qkv = exchange(across_out, 2)
        grad_values_in = after(grad_values, across_out)
    own_part = input_back(place, full_qkv, grad_keys, grad_values_in, (grad_first, grad_queries))
    packed = small_sums(
        own_part,
        to_other,
        own_low,
        other_low,
        masks,
        grad_queries,
        grad_values,
        small_one,
        small_two,
        grad_b_up,
        grad_tables,
    )
    if fast:
        packed = both_sum(packed, 1)
        shard_down = after(shard_down, packed)
        across_rest = after(across_rest, packed, shard_down)
        shard_down = shard_down.astype(f32) + swap(shard_down).astype(f32)
        own_rest, sends_rest = column_sends(held_rest, across_rest)
        arrived_rest = column_arrivals(sends_rest)
        packed = after(packed, *sends_rest)
        packed = packed + swap(packed)
        across_qkv = after(across_qkv, packed)
        own_qkv, sends_qkv = column_sends(held_qkv, across_qkv)
        arrived_qkv = column_arrivals(sends_qkv)
        from_other = after(from_other, *sends_qkv)
    else:
        packed = lax.psum(packed, ("mod", "page"))
    grad_in = state_back(own_part, from_other, masks, taps)
    if fast:
        arrived_rest = [after(part, grad_in) for part in arrived_rest]
        total_rest = column_total(own_rest, arrived_rest)
        far_rest = swap(total_rest)
        packed = both_sum(after(packed, total_rest), 2)
        arrived_qkv = [after(part, packed) for part in arrived_qkv]
        total_qkv = column_total(own_qkv, arrived_qkv)
        far_qkv = swap(total_qkv)
        packed = both_sum(both_sum(after(packed, total_qkv), 4), 8)
    g_tables = packed[28:34].reshape(HEADS, 3, LANES)
    if fast:
        shard_rest = jnp.where(
            is_text,
            jnp.concatenate([total_rest, far_rest], axis=1),
            jnp.concatenate([far_rest, total_rest], axis=1),
        ).astype(f32)
        shard_qkv = total_qkv.astype(f32) + far_qkv.astype(f32)
    return (
        output_row[None, None],
        grad_in[None, None],
        packed[0:3],
        packed[3],
        shard_qkv[:, :d_model],
        packed[4],
        shard_qkv[:, d_model : 2 * d_model],
        shard_qkv[:, 2 * d_model :],
        packed[5],
        shard_rest[:, :d_model],
        packed[10],
        g_tables[:, 0, : table_pos.shape[1]],
        g_tables[:, 1, 64 : 64 + table_x.shape[1]],
        g_tables[:, 2, 64 : 64 + table_y.shape[1]],
        packed[8],
        packed[9],
        shard_rest[:, d_model:],
        packed[24:28].reshape(d_ff),
        shard_down,
        packed[18],
        packed[16],
        packed[17],
    )


def solution(mesh):
    rows = P("mod", "page", None, None)
    ids = P("page", None)
    cut = P("page", None)
    return jax.shard_map(
        local,
        mesh=mesh,
        in_specs=(
            rows, rows, ids, ids, ids, P(), P(), cut, P(), cut, cut, P(), cut,
            P(), P(), P(), P(), P(), P(), cut, P(), cut, P(), P(), P(),
        ),
        out_specs=(
            rows, rows, P(), P(), cut, P(), cut, cut, P(), cut, P(), P(), P(),
            P(), P(), P(), cut, P(), cut, P(), P(), P(),
        ),
        check_vma=False,
    )
```

```python
import functools

import jax
import jax.numpy as jnp
import numpy as np
from jax import lax
from jax.experimental import pallas as pl
from jax.experimental.pallas import tpu as pltpu
from jax.sharding import PartitionSpec as P

HEADS = 12
HEAD = 64
GRID = 8
PAGES = 8
POS_BINS = 64
BOX_BINS = 32
PATCH = 64
TEXT = 512
PAIRS = HEADS // 2
LANES = 2 * HEAD
WINDOW = 144
SMALL = 80

dilation = 2
small_cost = pl.CostEstimate(flops=1000, bytes_accessed=1000, transcendentals=0)
norm_eps = 1e-05
mask_fill = -1000000000.0
erfc_poly = (
    0.2367515965428487,
    0.24062179898991767,
    0.18865103029313968,
    0.2877518531132804,
    -0.1648672439458568,
    0.4765735350541787,
    -0.34041833366480423,
    0.07493571514857543,
)
bf16 = jnp.bfloat16
f32 = jnp.float32


def shifted(values, offset, fill_value):
    padding = jnp.full((abs(offset),) + values.shape[1:], fill_value, values.dtype)
    if offset > 0:
        return jnp.concatenate([values[offset:], padding], axis=0)
    return jnp.concatenate([padding, values[:offset]], axis=0)


def dilated_mix(inputs, page_ids, conv_weight, conv_bias):
    summed = inputs + conv_bias + conv_weight[1] * inputs
    for tap_index, offset in ((0, -dilation), (2, dilation)):
        moved_rows = shifted(inputs, offset, 0.0)
        moved_pages = shifted(page_ids, offset, -1)
        same_page = (moved_pages == page_ids)[:, None]
        summed = summed + conv_weight[tap_index] * jnp.where(same_page, moved_rows, 0.0)
    return summed


def bin_features(pos_bins, bins_x, bins_y):
    return jnp.concatenate(
        [
            jax.nn.one_hot(pos_bins, POS_BINS, dtype=bf16),
            jax.nn.one_hot(bins_x, BOX_BINS, dtype=bf16),
            jax.nn.one_hot(bins_y, BOX_BINS, dtype=bf16),
        ],
        axis=1,
    )


def token_ids(text_pages, text_x, text_y):
    text_index = jnp.arange(TEXT, dtype=jnp.int32)
    text_pos = text_index * POS_BINS // TEXT
    patch_pos = text_index % PATCH * POS_BINS // PATCH
    patch_page = text_index // PATCH
    patch_x = text_index % GRID * BOX_BINS // GRID
    patch_y = text_index // GRID % GRID * BOX_BINS // GRID
    page_ids = jnp.stack([text_pages, patch_page])
    pos_bins = jnp.stack([text_pos, patch_pos])
    bins_x = jnp.stack([text_x, patch_x])
    bins_y = jnp.stack([text_y, patch_y])
    return (page_ids, pos_bins, bins_x, bins_y)


def plain_dot(left_side, right_side):
    return jnp.dot(left_side, right_side, preferred_element_type=f32)


def dot_left_t(left_side, right_side):
    return lax.dot_general(
        left_side, right_side, (((0,), (0,)), ((), ())), preferred_element_type=f32
    )


def dot_right_t(left_side, right_side):
    return lax.dot_general(
        left_side, right_side, (((1,), (1,)), ((), ())), preferred_element_type=f32
    )


def iota(shape, axis):
    return lax.broadcasted_iota(jnp.int32, shape, axis)


def bias_block(table_rows):
    pos_part = pltpu.roll(
        jnp.broadcast_to(table_rows[0:1], (POS_BINS, LANES)), 65, 1, stride=1, stride_axis=0
    )
    x_part = pltpu.roll(
        jnp.broadcast_to(table_rows[1:2], (BOX_BINS, LANES)), 33, 1, stride=1, stride_axis=0
    )
    y_part = pltpu.roll(
        jnp.broadcast_to(table_rows[2:3], (BOX_BINS, LANES)), 65, 1, stride=1, stride_axis=0
    )
    lane = iota((POS_BINS, LANES), 1)
    pos_part = jnp.where(lane < POS_BINS, pos_part, 0.0)
    lane = iota((BOX_BINS, LANES), 1)
    x_part = jnp.where((lane >= 64) & (lane < 96), x_part, 0.0)
    y_part = jnp.where(lane >= 96, y_part, 0.0)
    return jnp.concatenate([pos_part, x_part, y_part], axis=0).astype(bf16)


def diagonal_sums(grad_block):
    lane = iota((POS_BINS, LANES), 1)
    pos_part = jnp.where(lane < POS_BINS, grad_block[:64], 0.0)
    lane = iota((BOX_BINS, LANES), 1)
    x_part = jnp.where((lane >= 64) & (lane < 96), grad_block[64:96], 0.0)
    y_part = jnp.where(lane >= 96, grad_block[96:], 0.0)
    pos_part = pltpu.roll(pos_part, 0, 1, stride=1, stride_axis=0)
    x_part = pltpu.roll(x_part, 0, 1, stride=1, stride_axis=0)
    y_part = pltpu.roll(y_part, 96, 1, stride=1, stride_axis=0)
    rows = [jnp.sum(part, axis=0, keepdims=True) for part in (pos_part, x_part, y_part)]
    return jnp.concatenate(rows + [jnp.zeros((5, LANES), f32)], axis=0)


def stacked_heads(rows, low_lane):
    zero = jnp.zeros_like(rows)
    return jnp.concatenate(
        [jnp.where(low_lane, rows, zero), jnp.where(low_lane, zero, rows)], axis=0
    )


def window_start(first, window):
    return pl.multiple_of(jnp.minimum(first // 16 * 16, TEXT - window), 16)


def fits(first, end, window):
    return end - jnp.minimum(first // 16 * 16, TEXT - window) <= window


def for_each_page(bounds, step):
    def body(page, carry):
        own_low, own_high = bounds[page], bounds[PAGES + page]
        key_low, key_high = bounds[2 * PAGES + page], bounds[3 * PAGES + page]
        own_small = fits(own_low, own_high, SMALL)
        key_small = fits(key_low, key_high, SMALL)
        span = (own_low, own_high, key_low, key_high)
        small = own_small & key_small
        mixed = own_small & ~key_small
        for chosen, own_window, key_window in (
            (small, SMALL, SMALL),
            (mixed, SMALL, WINDOW),
            (~own_small, WINDOW, WINDOW),
        ):

            @pl.when(chosen)
            def _():
                step(page, span, own_window, key_window)

        return carry

    lax.fori_loop(0, PAGES, body, 0)


def page_operands(page, span, own_window, key_window, pair, q_ref, k_ref, feat_ref, lookup):
    own_at = window_start(span[0], own_window)
    key_at = window_start(span[2], key_window)
    own_rows, text_rows = pl.ds(own_at, own_window), pl.ds(key_at, key_window)
    patch_at = TEXT + PATCH * page
    if not isinstance(page, int):
        patch_at = pl.multiple_of(patch_at, PATCH)
    patch_rows = pl.ds(patch_at, PATCH)
    lanes = slice(pair * LANES, (pair + 1) * LANES)
    low_lane = iota((own_window, LANES), 1) < HEAD
    queries = stacked_heads(q_ref[own_rows, lanes], low_lane)
    first = 2 * pair * LANES
    rel = jnp.concatenate(
        [
            lookup[own_rows, first : first + LANES],
            lookup[own_rows, first + LANES : first + 2 * LANES],
        ],
        axis=0,
    )
    query_side = jnp.concatenate([rel, queries], axis=1)
    key_side = jnp.concatenate(
        [
            jnp.concatenate([feat_ref[text_rows, :], k_ref[text_rows, lanes]], axis=1),
            jnp.concatenate([feat_ref[patch_rows, :], k_ref[patch_rows, lanes]], axis=1),
        ],
        axis=0,
    )
    own_row = iota((own_window, LANES), 0) + own_at
    own_ok = (own_row >= span[0]) & (own_row < span[1])
    return (
        lanes, low_lane, own_ok, queries, query_side, key_side, own_rows, text_rows, patch_rows, key_at
    )


def set_lookup(lookup, own_feat_ref, table_ref):
    blocks = [bias_block(table_ref[head]) for head in range(table_ref.shape[0])]
    product = jnp.dot(
        own_feat_ref[...], jnp.concatenate(blocks, axis=1), preferred_element_type=f32
    )
    lookup[...] = product.astype(bf16)


def attend_kernel(bounds, q_ref, k_ref, v_ref, feat_ref, own_feat_ref, table_ref, context_ref, lookup):
    set_lookup(lookup, own_feat_ref, table_ref)

    def step(page, span, own_window, key_window):
        column = iota((1, key_window + PATCH), 1)
        key_row = column + window_start(span[2], key_window)
        key_ok = (column >= key_window) | ((key_row >= span[2]) & (key_row < span[3]))
        for pair in range(q_ref.shape[1] // LANES):
            lanes, low_lane, own_ok, _, query_side, key_side, own_rows, text_rows, patch_rows, _ = (
                page_operands(
                    page, span, own_window, key_window, pair, q_ref, k_ref, feat_ref, lookup
                )
            )
            scores = jnp.where(key_ok, dot_right_t(query_side, key_side), mask_fill)
            row_max = jnp.max(scores, axis=1, keepdims=True)
            weights = jnp.exp(scores - row_max)
            total = jnp.sum(weights, axis=1, keepdims=True)
            prob = (weights * (1.0 / total)).astype(bf16)
            values = jnp.concatenate([v_ref[text_rows, lanes], v_ref[patch_rows, lanes]], axis=0)
            mixed = jnp.dot(prob, values, preferred_element_type=f32)
            picked = jnp.where(low_lane, mixed[:own_window], mixed[own_window:])
            before = context_ref[own_rows, lanes].astype(f32)
            context_ref[own_rows, lanes] = jnp.where(own_ok, picked, before).astype(bf16)

    for page in range(PAGES):
        span = [bounds[part * PAGES + page] for part in range(4)]
        step(page, span, WINDOW, WINDOW)


def attend_back_kernel(
    bounds,
    q_ref,
    k_ref,
    v_ref,
    grad_ref,
    feat_ref,
    own_feat_ref,
    flip_feat_ref,
    table_ref,
    grad_q_ref,
    grad_k_ref,
    grad_v_ref,
    grad_table_ref,
    lookup,
    grad_lookup,
):
    set_lookup(lookup, own_feat_ref, table_ref)

    def step(page, span, own_window, key_window):
        row = iota((key_window + PATCH, 1), 0)
        key_row = row + window_start(span[2], key_window)
        key_ok = (row >= key_window) | ((key_row >= span[2]) & (key_row < span[3]))
        for pair in range(q_ref.shape[1] // LANES):
            lanes, low_lane, own_ok, queries, query_side, key_side, own_rows, text_rows, patch_rows, key_at = (
                page_operands(
                    page, span, own_window, key_window, pair, q_ref, k_ref, feat_ref, lookup
                )
            )
            scores = jnp.where(key_ok, dot_right_t(key_side, query_side), mask_fill)
            col_max = jnp.max(scores, axis=0, keepdims=True)
            weights = jnp.exp(scores - col_max)
            total = jnp.sum(weights, axis=0, keepdims=True)
            prob = weights * (1.0 / total)
            grad_rows = grad_ref[own_rows, lanes]
            grad_rows = jnp.where(own_ok, grad_rows, jnp.zeros_like(grad_rows))
            grads = stacked_heads(grad_rows, low_lane)
            values = jnp.concatenate([v_ref[text_rows, lanes], v_ref[patch_rows, lanes]], axis=0)
            grad_prob = dot_right_t(values, grads)
            inner = jnp.sum(prob * grad_prob, axis=0, keepdims=True)
            grad_scores = (prob * (grad_prob - inner)).astype(bf16)
            grad_v = jnp.dot(prob.astype(bf16), grads, preferred_element_type=f32)
            grad_k = jnp.dot(grad_scores, queries, preferred_element_type=f32)
            back = dot_left_t(grad_scores, key_side)
            low, high = back[:own_window], back[own_window:]
            grad_q = jnp.where(low_lane, low[:, LANES:], high[:, LANES:]) * 0.125
            before = grad_q_ref[own_rows, lanes].astype(f32)
            grad_q_ref[own_rows, lanes] = jnp.where(own_ok, grad_q, before).astype(bf16)
            first = 2 * pair * LANES
            for part, at in ((low, first), (high, first + LANES)):
                place_at = slice(at, at + LANES)
                grad_lookup[own_rows, place_at] = jnp.where(
                    own_ok, part[:, :LANES], grad_lookup[own_rows, place_at]
                )
            wide_row = iota((key_window, LANES), 0) + key_at
            text_ok = (wide_row >= span[2]) & (wide_row < span[3])
            for grad, ref in ((grad_k, grad_k_ref), (grad_v, grad_v_ref)):
                before = ref[text_rows, lanes].astype(f32)
                ref[text_rows, lanes] = jnp.where(text_ok, grad[:key_window], before).astype(bf16)
                ref[patch_rows, lanes] = grad[key_window:].astype(bf16)

    for_each_page(bounds, step)
    grad_high = grad_lookup[...].astype(bf16)
    grad_rest = (grad_lookup[...] - grad_high.astype(f32)).astype(bf16)
    flip = flip_feat_ref[...]
    grad_block = dot_left_t(flip, grad_high) + dot_left_t(flip, grad_rest)
    for head in range(table_ref.shape[0]):
        grad_table_ref[head] = diagonal_sums(grad_block[:, head * LANES : (head + 1) * LANES])


def column_spec(rows, group, first=0):
    return pl.BlockSpec((rows, group * LANES), lambda step, bounds: (0, step + first))


def whole_spec(rows):
    return pl.BlockSpec((rows, LANES), lambda step, bounds: (0, 0))


def tables_spec(group):
    return pl.BlockSpec((2 * group, 8, LANES), lambda step, bounds: (step, 0, 0))


def attend(bounds, queries, keys_values, features, own_features, tables):
    group = 1
    return pl.pallas_call(
        attend_kernel,
        grid_spec=pltpu.PrefetchScalarGridSpec(
            num_scalar_prefetch=1,
            grid=(PAIRS // group,),
            in_specs=[
                column_spec(TEXT, group),
                column_spec(2 * TEXT, group),
                column_spec(2 * TEXT, group, PAIRS // group),
                whole_spec(2 * TEXT),
                whole_spec(TEXT),
                tables_spec(group),
            ],
            out_specs=column_spec(TEXT, group),
            scratch_shapes=[pltpu.VMEM((TEXT, 2 * group * LANES), bf16)],
        ),
        out_shape=jax.ShapeDtypeStruct((TEXT, HEADS * HEAD), bf16),
        cost_estimate=small_cost,
        name="attend",
    )(bounds, queries, keys_values, keys_values, features, own_features, tables)


def attend_back(
    bounds, queries, keys_values, grad_context, features, own_features, flip, tables
):
    group = 6
    return pl.pallas_call(
        attend_back_kernel,
        grid_spec=pltpu.PrefetchScalarGridSpec(
            num_scalar_prefetch=1,
            grid=(PAIRS // group,),
            in_specs=[
                column_spec(TEXT, group),
                column_spec(2 * TEXT, group),
                column_spec(2 * TEXT, group, PAIRS // group),
                column_spec(TEXT, group),
                whole_spec(2 * TEXT),
                whole_spec(TEXT),
                whole_spec(TEXT),
                tables_spec(group),
            ],
            out_specs=[
                column_spec(TEXT, group),
                column_spec(2 * TEXT, group),
                column_spec(2 * TEXT, group),
                tables_spec(group),
            ],
            scratch_shapes=[
                pltpu.VMEM((TEXT, 2 * group * LANES), bf16),
                pltpu.VMEM((TEXT, 2 * group * LANES), f32),
            ],
        ),
        out_shape=[
            jax.ShapeDtypeStruct((TEXT, HEADS * HEAD), bf16),
            jax.ShapeDtypeStruct((2 * TEXT, HEADS * HEAD), bf16),
            jax.ShapeDtypeStruct((2 * TEXT, HEADS * HEAD), bf16),
            jax.ShapeDtypeStruct((HEADS, 8, LANES), f32),
        ],
        cost_estimate=small_cost,
        name="attend_back",
    )(
        bounds,
        queries,
        keys_values,
        keys_values,
        grad_context,
        features,
        own_features,
        flip,
        tables,
    )


def exchange(values, mask):
    count = lax.axis_size("page")
    return lax.ppermute(values, "page", [(i, i ^ mask) for i in range(count)])


def after(value, *earlier):
    return lax.optimization_barrier((value, *earlier))[0]


def slot_mask(slot):
    return (slot & 3) * 4 + (slot >> 2) * 2


def project_kernel(groups, place, mixed_ref, bias_ref, *refs):
    *pieces, query_ref, both_ref, weight_ref, mixed_t_ref, sems = refs
    width = mixed_ref.shape[1]
    tokens = query_ref.shape[0]
    copies = start_rows(place, groups, pieces, weight_ref, sems)
    mixed_t_ref[...] = mixed_ref[...].T
    for copy in copies:
        copy.wait()
    own = mixed_ref[pl.ds(pl.multiple_of(place[1] * tokens, 16), tokens), :]
    queries = jnp.dot(own, weight_ref[:, :width], preferred_element_type=f32) + bias_ref[:, :width]
    query_ref[...] = (queries.astype(bf16).astype(f32) * 0.125).astype(bf16)
    for part in range(2):
        rows = pl.ds(part * tokens, tokens)
        for column in (1, 2):
            at = slice(column * width, (column + 1) * width)
            out = slice((column - 1) * width, column * width)
            values = jnp.dot(mixed_ref[rows, :], weight_ref[:, at], preferred_element_type=f32)
            both_ref[rows, out] = (values + bias_ref[:, at]).astype(bf16)


def project(place, mixed, biases, groups, pieces):
    rows, width = mixed.shape
    vmem = pl.BlockSpec(memory_space=pltpu.VMEM)
    return pl.pallas_call(
        functools.partial(project_kernel, groups),
        grid_spec=pltpu.PrefetchScalarGridSpec(
            num_scalar_prefetch=1,
            grid=(),
            in_specs=[vmem] * 2 + any_specs(len(pieces)),
            out_specs=[vmem] * 4,
            scratch_shapes=[pltpu.SemaphoreType.DMA((32,))],
        ),
        out_shape=[
            jax.ShapeDtypeStruct((rows // 2, width), bf16),
            jax.ShapeDtypeStruct((rows, 2 * width), bf16),
            jax.ShapeDtypeStruct((width, 3 * width), bf16),
            jax.ShapeDtypeStruct((width, rows), bf16),
        ],
        cost_estimate=small_cost,
        compiler_params=pltpu.CompilerParams(vmem_limit_bytes=16 << 20),
        name="project",
    )(place, mixed, biases, *pieces)


def column_parts(shard):
    return [shard] + [exchange(shard, 4 * step) for step in (1, 2, 3)]


def half_pieces(column):
    eight = jnp.concatenate([column, exchange(column, 2)])
    far = swap(eight)
    return [eight, exchange(eight, 1), far, exchange(far, 1)]


def row_pieces(column, across):
    return [column, exchange(column, 1), across, exchange(across, 1)]


def column_of(shard):
    return jnp.stack(column_parts(shard))


def row_copies(place, groups, refs, full, sems, first=0):
    copies = []
    for kind, column in groups:
        if kind == "full":
            piece, *refs = refs
            width = piece.shape[1]
            target = full.at[:, pl.ds(column, width)]
            copies.append(pltpu.make_async_copy(piece, target, sems.at[first + len(copies)]))
            continue
        pieces, refs = refs[:4], refs[4:]
        _, rows, width = pieces[0].shape
        for index in range(32 if kind == "halves" else 16):
            at = column
            if kind == "halves":
                source, slot = index >> 3, index & 7
                mask = slot_mask(slot) + (source & 1)
                at = pl.multiple_of(column + (place[1] ^ (source >> 1)) * width, 128)
            else:
                source, slot = index & 3, index >> 2
                mask = slot * 4 + source
            row = pl.multiple_of((place[0] ^ mask) * rows, 16)
            copies.append(
                pltpu.make_async_copy(
                    pieces[source].at[slot],
                    full.at[pl.ds(row, rows), pl.ds(at, width)],
                    sems.at[first + len(copies)],
                )
            )
    return copies


def start_rows(place, groups, refs, full, sems):
    copies = row_copies(place, groups, refs, full, sems)
    for copy in copies:
        copy.start()
    return copies


def gelu_parts(values):
    size = jnp.abs(values)
    t = 1.0 / (1.0 + (0.42 * 0.7071067811865476) * size)
    poly = jnp.full_like(t, erfc_poly[-1])
    for coefficient in erfc_poly[-2::-1]:
        poly = poly * t + coefficient
    bell = jnp.exp(-0.5 * values * values)
    tail = (0.5 * t) * (poly * bell)
    cdf = jnp.where(values >= 0.0, 1.0 - tail, tail)
    return values * cdf, cdf + (values * 0.3989422804014327) * bell


def normalized(values):
    centered = values - jnp.mean(values, axis=1, keepdims=True)
    variance = jnp.mean(centered * centered, axis=1, keepdims=True)
    scale = lax.rsqrt(variance + norm_eps)
    return centered * scale, scale


def norm_back(grads, unit, scale, gain):
    scaled = grads * gain
    mean = jnp.mean(scaled, axis=1, keepdims=True)
    inner = jnp.mean(scaled * unit, axis=1, keepdims=True)
    return scale * (scaled - mean - unit * inner)


def up_kernel(groups, place, context_ref, mixed_ref, vec_ref, bias_ref, *refs):
    *pieces, unit_ref, scale_ref, low_ref, low_t_ref, context_t_ref = refs[:-9]
    active_ref, active_t_ref, slope_ref, full_ref = refs[-9:-5]
    weight, hidden, low, sems, full_sem = refs[-5:]
    step = pl.program_id(0)
    tiles = pl.num_programs(0) - 1
    width = context_ref.shape[1]
    tile = active_ref.shape[1]
    last_group = 16 if len(groups) > 1 else 0

    def full_copy():
        return pltpu.make_async_copy(weight, full_ref, full_sem)

    @pl.when(step == 0)
    def _():
        copies = row_copies(place, groups, pieces, weight, sems)
        for copy in copies:
            copy.start()
        context_t_ref[...] = context_ref[...].T
        for copy in copies[: len(copies) - last_group]:
            copy.wait()
        branch = jnp.dot(context_ref[...], weight[:, :width], preferred_element_type=f32)
        unit, scale = normalized(mixed_ref[...] + branch + vec_ref[0:1])
        unit_ref[...] = unit
        scale_ref[...] = jnp.broadcast_to(scale, scale_ref.shape)
        normed = (unit * vec_ref[1:2] + vec_ref[2:3]).astype(bf16)
        low[...] = normed
        low_ref[...] = normed
        low_t_ref[...] = normed.T

    @pl.when(step == 1)
    def _():
        if last_group:
            for copy in row_copies(place, groups[1:], pieces[4:], weight, sems, 32):
                copy.wait()
        full_copy().start()

    def product():
        at = pl.multiple_of(width + step * tile, 128)
        return jnp.dot(low[...], weight[:, pl.ds(at, tile)], preferred_element_type=f32)

    def activate():
        active, slope = gelu_parts(hidden[(step + 1) % 2] + bias_ref[...])
        active = active.astype(bf16)
        active_ref[...] = active
        active_t_ref[...] = active.T
        slope_ref[...] = slope.astype(bf16)

    @pl.when(step == 0)
    def _():
        hidden[step % 2] = product()

    @pl.when((step > 0) & (step < tiles))
    def _():
        hidden[step % 2] = product()
        activate()

    @pl.when(step == tiles)
    def _():
        activate()
        full_copy().wait()


def any_specs(count):
    return [pl.BlockSpec(memory_space=pl.ANY)] * count


def up_forward(place, context, mixed, vectors, bias_up, groups, pieces):
    tokens, width = mixed.shape
    hidden_width = bias_up.shape[1]
    tile = 512
    whole = lambda step, place: (0, 0)
    last = lambda step, place: (0, jnp.maximum(step - 1, 0))
    last_t = lambda step, place: (jnp.maximum(step - 1, 0), 0)
    return pl.pallas_call(
        functools.partial(up_kernel, groups),
        grid_spec=pltpu.PrefetchScalarGridSpec(
            num_scalar_prefetch=1,
            grid=(hidden_width // tile + 1,),
            in_specs=[
                pl.BlockSpec((tokens, width), whole),
                pl.BlockSpec((tokens, width), whole),
                pl.BlockSpec(vectors.shape, whole),
                pl.BlockSpec((1, tile), last),
            ]
            + any_specs(len(pieces)),
            out_specs=[
                pl.BlockSpec((tokens, width), whole),
                pl.BlockSpec((tokens, 128), whole),
                pl.BlockSpec((tokens, width), whole),
                pl.BlockSpec((width, tokens), whole),
                pl.BlockSpec((width, tokens), whole),
                pl.BlockSpec((tokens, tile), last),
                pl.BlockSpec((tile, tokens), last_t),
                pl.BlockSpec((tokens, tile), last),
                pl.BlockSpec(memory_space=pl.ANY),
            ],
            scratch_shapes=[
                pltpu.VMEM((width, width + hidden_width), bf16),
                pltpu.VMEM((2, tokens, tile), f32),
                pltpu.VMEM((tokens, width), bf16),
                pltpu.SemaphoreType.DMA((48,)),
                pltpu.SemaphoreType.DMA,
            ],
        ),
        out_shape=[
            jax.ShapeDtypeStruct((tokens, width), f32),
            jax.ShapeDtypeStruct((tokens, 128), f32),
            jax.ShapeDtypeStruct((tokens, width), bf16),
            jax.ShapeDtypeStruct((width, tokens), bf16),
            jax.ShapeDtypeStruct((width, tokens), bf16),
            jax.ShapeDtypeStruct((tokens, hidden_width), bf16),
            jax.ShapeDtypeStruct((hidden_width, tokens), bf16),
            jax.ShapeDtypeStruct((tokens, hidden_width), bf16),
            jax.ShapeDtypeStruct((width, width + hidden_width), bf16),
        ],
        cost_estimate=small_cost,
        name="up_forward",
    )(place, context, mixed, vectors, bias_up, *pieces)


def down_kernel(active_ref, weight_ref, unit_ref, vec_ref, grad_ref, *refs):
    out_ref, sum_ref, low_ref, small_ref, total = refs
    step = pl.program_id(0)
    product = jnp.dot(active_ref[...], weight_ref[...], preferred_element_type=f32)

    @pl.when(step == 0)
    def _():
        total[...] = product

    @pl.when(step > 0)
    def _():
        total[...] += product

    @pl.when(step == pl.num_programs(0) - 1)
    def _():
        tokens, width = unit_ref.shape
        half = tokens // 2
        smalls = [jnp.zeros((1, width), f32)] * 3
        for part in range(2):
            rows = pl.ds(part * half, half)
            normed = unit_ref[rows, :] * vec_ref[1:2] + vec_ref[2:3]
            unit, scale = normalized(normed + total[rows, :] + vec_ref[3:4])
            out_ref[rows, :] = (unit * vec_ref[4:5] + vec_ref[5:6]).astype(bf16)
            grads = grad_ref[rows, :].astype(f32)
            back = norm_back(grads, unit, scale, vec_ref[4:5])
            low = back.astype(bf16)
            sum_ref[rows, :] = back
            low_ref[rows, :] = low
            for index, term in enumerate((grads * unit, grads, low.astype(f32))):
                smalls[index] = smalls[index] + jnp.sum(term, axis=0, keepdims=True)
        small_ref[...] = jnp.concatenate(smalls + [jnp.zeros((5, width), f32)], axis=0)


def down_forward(active, weight, unit, vectors, grads):
    tokens, width = unit.shape
    hidden_width = active.shape[1]
    tile = 768
    whole = lambda step: (0, 0)
    token_block = pl.BlockSpec((tokens, width), whole)
    return pl.pallas_call(
        down_kernel,
        grid=(hidden_width // tile,),
        in_specs=[
            pl.BlockSpec((tokens, tile), lambda step: (0, step)),
            pl.BlockSpec((tile, width), lambda step: (step, 0)),
            token_block,
            pl.BlockSpec(vectors.shape, whole),
            token_block,
        ],
        out_specs=[token_block] * 3 + [pl.BlockSpec((8, width), whole)],
        scratch_shapes=[pltpu.VMEM((tokens, width), f32)],
        out_shape=[
            jax.ShapeDtypeStruct((tokens, width), bf16),
            jax.ShapeDtypeStruct((tokens, width), f32),
            jax.ShapeDtypeStruct((tokens, width), bf16),
            jax.ShapeDtypeStruct((8, width), f32),
        ],
        cost_estimate=small_cost,
        name="down_forward",
    )(active, weight, unit, vectors, grads)


def ffn_back_kernel(*refs):
    low_ref, slope_ref, sum_ref, unit_ref, scale_ref, vec_ref = refs[:6]
    down_ref, up_ref, out_weight_ref = refs[6:9]
    hidden_ref, bias_ref, first_ref, branch_ref, context_ref, small_ref, total = refs[9:]
    step = pl.program_id(0)
    tokens, width = unit_ref.shape
    tile = slope_ref.shape[1]
    half = tokens // 2

    @pl.when(step == 0)
    def _():
        total[...] = sum_ref[...]

    bias = jnp.zeros((1, tile), f32)
    for part in range(2):
        rows = pl.ds(part * half, half)
        grads = dot_right_t(low_ref[rows, :], down_ref[...]) * slope_ref[rows, :].astype(f32)
        grads = grads.astype(bf16)
        hidden_ref[rows, :] = grads
        bias = bias + jnp.sum(grads.astype(f32), axis=0, keepdims=True)
        total[rows, :] += dot_right_t(grads, up_ref[...])
    bias_ref[...] = bias

    @pl.when(step == pl.num_programs(0) - 1)
    def _():
        grads = total[...]
        unit = unit_ref[...]
        first = norm_back(grads, unit, scale_ref[:, 0:1], vec_ref[1:2])
        branch = first.astype(bf16)
        first_ref[...] = first
        branch_ref[...] = branch
        context_ref[...] = dot_right_t(branch, out_weight_ref[...]).astype(bf16)
        smalls = [
            jnp.sum(term, axis=0, keepdims=True)
            for term in (grads * unit, grads, branch.astype(f32))
        ]
        small_ref[...] = jnp.concatenate(smalls + [jnp.zeros((5, width), f32)], axis=0)


def ffn_back(low, slope, total, unit, scale, vectors, full_rest, full_down):
    tokens, width = unit.shape
    hidden_width = slope.shape[1]
    tile = 768
    whole = lambda step: (0, 0)
    column = lambda step: (0, step)
    token_block = pl.BlockSpec((tokens, width), whole)
    return pl.pallas_call(
        ffn_back_kernel,
        grid=(hidden_width // tile,),
        in_specs=[
            token_block,
            pl.BlockSpec((tokens, tile), column),
            token_block,
            token_block,
            pl.BlockSpec((tokens, 128), whole),
            pl.BlockSpec(vectors.shape, whole),
            pl.BlockSpec((tile, width), lambda step: (step, 0)),
            pl.BlockSpec((width, tile), lambda step: (0, step + 1)),
            pl.BlockSpec((width, width), whole),
        ],
        out_specs=[
            pl.BlockSpec((tokens, tile), column),
            pl.BlockSpec((1, tile), column),
            token_block,
            token_block,
            token_block,
            pl.BlockSpec((8, width), whole),
        ],
        scratch_shapes=[pltpu.VMEM((tokens, width), f32)],
        out_shape=[
            jax.ShapeDtypeStruct((tokens, hidden_width), bf16),
            jax.ShapeDtypeStruct((1, hidden_width), f32),
            jax.ShapeDtypeStruct((tokens, width), f32),
            jax.ShapeDtypeStruct((tokens, width), bf16),
            jax.ShapeDtypeStruct((tokens, width), bf16),
            jax.ShapeDtypeStruct((8, width), f32),
        ],
        cost_estimate=small_cost,
        name="ffn_back",
    )(low, slope, total, unit, scale, vectors, full_down, full_rest, full_rest)


def grad_rows_kernel(x_ref, h_ref, out_ref):
    out_ref[...] = jnp.dot(x_ref[...], h_ref[...], preferred_element_type=f32).astype(bf16)


def grad_rows(inputs_t, grads):
    width, tokens = inputs_t.shape
    columns = grads.shape[1]
    return pl.pallas_call(
        grad_rows_kernel,
        grid=(4,),
        in_specs=[
            pl.BlockSpec((width // 4, tokens), lambda step: (step, 0)),
            pl.BlockSpec((tokens, columns), lambda step: (0, 0)),
        ],
        out_specs=pl.BlockSpec((width // 4, columns), lambda step: (step, 0)),
        out_shape=jax.ShapeDtypeStruct((width, columns), bf16),
        cost_estimate=small_cost,
        name="grad_rows",
    )(inputs_t, grads)


def grad_columns_kernel(parts, place, *refs):
    count = len(parts)
    ins, keep_ref, send_ref, scratch = (
        refs[: 2 * count],
        refs[2 * count],
        refs[2 * count + 1],
        refs[2 * count + 2 :],
    )
    rows, tile = keep_ref.shape[1], keep_ref.shape[2]
    step = pl.program_id(0)
    first = 0
    for index, steps in enumerate(parts):
        x_ref, h_ref, ordered = ins[2 * index], ins[2 * index + 1], scratch[index]

        @pl.when(step == first)
        def _():
            for slot in range(16):
                mask = slot_mask(slot & 7) + (slot >> 3)
                at = pl.multiple_of((place[0] ^ mask) * rows, 16)
                ordered[pl.ds(slot * rows, rows), :] = x_ref[pl.ds(at, rows), :]

        @pl.when((step >= first) & (step < first + steps))
        def _():
            product = jnp.dot(ordered[...], h_ref[...], preferred_element_type=f32).astype(bf16)
            keep_ref[...] = product[: 8 * rows].reshape(8, rows, tile)
            send_ref[...] = product[8 * rows :].reshape(8, rows, tile)

        first = first + steps


def grad_by_columns(pairs, place, tile):
    width = pairs[0][0].shape[0]
    rows = width // 16
    parts = tuple(sum(grad.shape[1] for grad in grads) // tile for _, _, *grads in pairs)
    steps = sum(parts)
    specs = []
    operands = []
    scratch = []
    first = 0
    for (inputs_t, own, *grads), count in zip(pairs, parts):
        tokens = grads[0].shape[0]
        block = (lambda step, place: (0, place[1])) if own else (lambda step, place: (0, 0))
        specs.append(pl.BlockSpec((width, tokens), block))

        def column(step, place, first=first, count=count):
            return (0, jnp.clip(step - first, 0, count - 1))

        specs.append(pl.BlockSpec((tokens, tile), column))
        operands += [inputs_t, *grads]
        scratch.append(pltpu.VMEM((width, tokens), bf16))
        first = first + count
    half = jax.ShapeDtypeStruct((8, rows, steps * tile), bf16)
    return pl.pallas_call(
        functools.partial(grad_columns_kernel, parts),
        grid_spec=pltpu.PrefetchScalarGridSpec(
            num_scalar_prefetch=1,
            grid=(steps,),
            in_specs=specs,
            out_specs=[pl.BlockSpec((8, rows, tile), lambda step, place: (0, 0, step))] * 2,
            scratch_shapes=scratch,
        ),
        out_shape=[half, half],
        cost_estimate=small_cost,
        compiler_params=pltpu.CompilerParams(vmem_limit_bytes=16 << 20),
        name="grad_columns",
    )(place, *operands)


def key_back_kernel(place, gk_ref, gv_ref, wk_ref, wv_ref, out_ref):
    total = dot_right_t(gk_ref[...], wk_ref[...]) + dot_right_t(gv_ref[...], wv_ref[...])
    out_ref[...] = total.astype(out_ref.dtype)


def own_back_kernel(place, first_ref, gq_ref, gk_ref, gv_ref, wq_ref, wk_ref, wv_ref, out_ref):
    total = dot_right_t(gk_ref[...], wk_ref[...]) + dot_right_t(gv_ref[...], wv_ref[...])
    out_ref[...] = first_ref[...] + total + dot_right_t(gq_ref[...], wq_ref[...])


def input_back(place, weights, grad_keys, grad_values, others):
    width = weights.shape[0]
    tokens = grad_keys.shape[0] // 2
    whole = pl.BlockSpec((tokens, width), lambda step, place: (0, 0))
    row = lambda step, place: ((place[1] if others else 1 - place[1]), 0)
    if others:
        kernel, leading, first, dtype = own_back_kernel, [whole, whole], 0, f32
    else:
        kernel, leading, first, dtype = key_back_kernel, [], 1, bf16
    operands = list(others) + [grad_keys, grad_values] + [weights] * (3 - first)
    specs = [pl.BlockSpec((tokens, width), row)] * 2
    for block in range(first, 3):
        specs.append(pl.BlockSpec((width, width), lambda step, place, block=block: (0, block)))
    return pl.pallas_call(
        kernel,
        grid_spec=pltpu.PrefetchScalarGridSpec(
            num_scalar_prefetch=1, grid=(1,), in_specs=leading + specs, out_specs=whole
        ),
        out_shape=jax.ShapeDtypeStruct((tokens, width), dtype),
        cost_estimate=small_cost,
        compiler_params=pltpu.CompilerParams(vmem_limit_bytes=16 << 20),
        name="input_back",
    )(place, *operands)


def back_rows(values, mask):
    return jnp.where(mask, pltpu.roll(values, dilation, 0), 0.0)


def ahead_rows(values, mask):
    return jnp.where(mask, pltpu.roll(values, values.shape[0] - dilation, 0), 0.0)


def tap_sums(grads, inputs, ahead, back):
    terms = (grads * back_rows(inputs, back), grads * inputs, grads * ahead_rows(inputs, ahead), grads)
    return [jnp.sum(term, axis=0, keepdims=True) for term in terms]


def small_sums_kernel(
    own_ref, other_ref, x_ref, x_other_ref, mask_ref, gq_ref, gv_ref, one_ref, two_ref, up_ref, table_ref, out_ref
):
    width = own_ref.shape[1]
    mask = mask_ref[...] > 0.0
    own = tap_sums(own_ref[...], x_ref[...].astype(f32), mask[:, 0:1], mask[:, 1:2])
    other = tap_sums(
        other_ref[...].astype(f32), x_other_ref[...].astype(f32), mask[:, 2:3], mask[:, 3:4]
    )
    rows = [a + b for a, b in zip(own, other)]
    for ref in (gq_ref, gv_ref):
        rows.append(jnp.sum(ref[...].astype(f32), axis=0, keepdims=True))
    rows.append(jnp.zeros((2, width), f32))
    out_ref[0:8] = jnp.concatenate(rows, axis=0)
    out_ref[8:16] = one_ref[...]
    out_ref[16:24] = two_ref[...]
    count = up_ref.shape[1] // width
    for index in range(count):
        out_ref[24 + index : 25 + index] = up_ref[:, index * width : (index + 1) * width]
    for index in range(3 * HEADS):
        row, lane = 28 + index // 6, index % 6 * LANES
        table = table_ref[index // 3]
        out_ref[row : row + 1, lane : lane + LANES] = table[index % 3 : index % 3 + 1]
    out_ref[34:40] = jnp.zeros((6, width), f32)


def small_sums(*operands):
    return pl.pallas_call(
        small_sums_kernel,
        out_shape=jax.ShapeDtypeStruct((40, operands[0].shape[1]), f32),
        cost_estimate=small_cost,
        compiler_params=pltpu.CompilerParams(vmem_limit_bytes=24 << 20),
        name="small_sums",
    )(*operands)


def state_back_kernel(own_ref, other_ref, mask_ref, tap_ref, out_ref):
    grads = own_ref[...] + other_ref[...].astype(f32)
    mask = mask_ref[...] > 0.0
    total = grads + tap_ref[1:2] * grads
    total = total + tap_ref[0:1] * ahead_rows(grads, mask[:, 0:1])
    total = total + tap_ref[2:3] * back_rows(grads, mask[:, 1:2])
    out_ref[...] = total.astype(bf16)


def state_back(own, other, masks, taps):
    return pl.pallas_call(
        state_back_kernel,
        out_shape=jax.ShapeDtypeStruct(own.shape, bf16),
        cost_estimate=small_cost,
        compiler_params=pltpu.CompilerParams(vmem_limit_bytes=20 << 20),
        name="state_back",
    )(own, other, masks, taps)


def first_half_kernel(place, keep_near, part_near, keep_far, part_far, held_ref, out_ref):
    held_ref[...] = keep_near[...].astype(f32) + part_near[...].astype(f32)
    out_ref[...] = (keep_far[...].astype(f32) + part_far[...].astype(f32)).astype(bf16)


def halve_call(place, keep, partner, specs, half_shape, steps):
    near, far, out = specs
    return pl.pallas_call(
        first_half_kernel,
        grid_spec=pltpu.PrefetchScalarGridSpec(
            num_scalar_prefetch=1,
            grid=(steps,),
            in_specs=[near, near, far, far],
            out_specs=[out, out],
        ),
        out_shape=[
            jax.ShapeDtypeStruct(half_shape, f32),
            jax.ShapeDtypeStruct(half_shape, bf16),
        ],
        cost_estimate=small_cost,
        compiler_params=pltpu.CompilerParams(vmem_limit_bytes=12 << 20),
        name="halve",
    )(place, keep, partner, keep, partner)


def halve_across(place, keep, partner):
    _, rows, width = keep.shape
    near = pl.BlockSpec((1, rows, width), lambda step, place: (step, 0, 0))
    far = pl.BlockSpec((1, rows, width), lambda step, place: (step + 4, 0, 0))
    return halve_call(place, keep, partner, (near, far, near), (4, rows, width), 4)


def halve_plane(place, keep, partner):
    _, rows, width = keep.shape
    block = (2, rows, width // 2)
    near = pl.BlockSpec(block, lambda step, place: (step, 0, place[1]))
    far = pl.BlockSpec(block, lambda step, place: (step, 0, 1 - place[1]))
    out = pl.BlockSpec(block, lambda step, place: (step, 0, 0))
    return halve_call(place, keep, partner, (near, far, out), (8, rows, width // 2), 4)


def column_kernel(held_ref, across_ref, own_ref, *sends):
    own_ref[...] = held_ref[0] + across_ref[0].astype(f32)
    for step, send in enumerate(sends, 1):
        send[...] = (held_ref[step] + across_ref[step].astype(f32)).astype(bf16)


def column_sends(held, across):
    _, rows, width = held.shape
    tile = 384
    out = pl.BlockSpec((rows, tile), lambda step: (0, step))
    block = pl.BlockSpec((4, rows, tile), lambda step: (0, 0, step))
    own, *sends = pl.pallas_call(
        column_kernel,
        grid=(width // tile,),
        in_specs=[block, block],
        out_specs=[out] * 4,
        out_shape=[jax.ShapeDtypeStruct((rows, width), f32)]
        + [jax.ShapeDtypeStruct((rows, width), bf16)] * 3,
        cost_estimate=small_cost,
        compiler_params=pltpu.CompilerParams(vmem_limit_bytes=12 << 20),
        name="column_sends",
    )(held, across)
    return own, sends


def column_arrivals(sends):
    return [exchange(send, 4 * step) for step, send in enumerate(sends, 1)]


def column_total(own, arrived):
    total = own
    for part in arrived:
        total = total + part.astype(f32)
    return total.astype(bf16)


def half_columns(values, first):
    half = values.shape[-1] // 2
    return jnp.where(first, values[..., :half], values[..., half:])


def summed_rows(pairs):
    grads = jnp.concatenate([plain_dot(*pair).astype(bf16) for pair in pairs], axis=1)
    shard = lax.psum_scatter(grads, "page", scatter_dimension=0, tiled=True)
    return shard.astype(f32) + swap(shard).astype(f32)


def page_bounds(segments, is_text):
    pages = jnp.arange(PAGES, dtype=jnp.int32)
    low = jnp.sum(segments[None, :] < pages[:, None], axis=1, dtype=jnp.int32)
    high = jnp.sum(segments[None, :] <= pages[:, None], axis=1, dtype=jnp.int32)
    own_low = jnp.where(is_text, low, pages * PATCH)
    own_high = jnp.where(is_text, high, (pages + 1) * PATCH)

    return jnp.concatenate([own_low, own_high, low, high])


def both_sum(values, mask):
    return values + exchange(values, mask)


def swap(values):
    return lax.ppermute(values, "mod", [(0, 1), (1, 0)])


def local(
    states,
    cotangent,
    segments,
    box_x,
    box_y,
    conv_weight,
    conv_bias,
    w_query,
    b_query,
    w_key,
    w_value,
    b_value,
    w_out,
    b_out,
    table_pos,
    table_x,
    table_y,
    gain_one,
    bias_one,
    w_up,
    b_up,
    w_down,
    b_down,
    gain_two,
    bias_two,
):
    is_text = lax.axis_index("mod") == 0
    d_model = states.shape[3]
    own_low = states[0, 0]
    rows_each = w_query.shape[0]
    d_ff = w_up.shape[1]
    fast = lax.axis_size("page") == 16 and rows_each % 16 == 0 and w_down.shape[0] % 16 == 0
    place = jnp.stack([lax.axis_index("page"), lax.axis_index("mod")]).astype(jnp.int32)
    pack_qkv = jnp.concatenate([w_query, w_key, w_value], axis=1)
    pack_rest = jnp.concatenate([w_out, w_up], axis=1)
    other_low = swap(own_low)
    if fast:
        column_qkv = column_of(half_columns(pack_qkv, is_text))
        table_pos, table_x, table_y, b_out, b_down, b_query, b_value, b_up = after(
            (table_pos, table_x, table_y, b_out, b_down, b_query, b_value, b_up), column_qkv
        )
        gain_one, bias_one, gain_two, bias_two, conv_weight = after(
            (gain_one, bias_one, gain_two, bias_two, conv_weight), column_qkv
        )
        segments, box_x, box_y = after((segments, box_x, box_y), column_qkv)
    page_ids, pos_bins, bins_x, bins_y = token_ids(segments[0], box_x[0], box_y[0])
    bounds = page_bounds(segments[0], is_text)
    own_pages = jnp.where(is_text, page_ids[0], page_ids[1])
    features = bin_features(pos_bins.reshape(-1), bins_x.reshape(-1), bins_y.reshape(-1))
    flipped = bin_features(
        POS_BINS - 1 - pos_bins.reshape(-1),
        BOX_BINS - 1 - bins_x.reshape(-1),
        BOX_BINS - 1 - bins_y.reshape(-1),
    )
    own_feats = jnp.where(is_text, features[:TEXT], features[TEXT:])
    own_flip = jnp.where(is_text, flipped[:TEXT], flipped[TEXT:])
    tables = jnp.stack(
        [
            jnp.pad(table_pos, ((0, 0), (0, LANES - table_pos.shape[1]))),
            jnp.pad(table_x, ((0, 0), (0, LANES - table_x.shape[1]))),
            jnp.pad(table_y, ((0, 0), (0, LANES - table_y.shape[1]))),
        ],
        axis=1,
    )
    tables = jnp.pad(tables, ((0, 0), (0, 5), (0, 0)))

    own_states = own_low.astype(f32)
    mixed = dilated_mix(own_states, own_pages, conv_weight, conv_bias)
    mixed_low = mixed.astype(bf16)
    other_pages = jnp.where(is_text, page_ids[1], page_ids[0])
    masks = jnp.pad(
        jnp.stack(
            [
                own_pages == shifted(own_pages, dilation, -1),
                own_pages == shifted(own_pages, -dilation, -1),
                other_pages == shifted(other_pages, dilation, -1),
                other_pages == shifted(other_pages, -dilation, -1),
            ],
            axis=1,
        ).astype(f32),
        ((0, 0), (0, LANES - 4)),
    )
    vectors = jnp.stack(
        [b_out, gain_one, bias_one, b_down, gain_two, bias_two, jnp.zeros_like(b_out), b_out]
    )
    biases = jnp.concatenate([b_query, jnp.zeros_like(b_value), b_value])[None]
    taps = jnp.pad(conv_weight, ((0, 5), (0, 0)))
    bias_up = b_up[None]
    if fast:
        split = (pack_rest.shape[1] // 2 + 127) // 256 * 256
        early = (features, own_feats, own_flip, tables, bounds, masks, vectors, biases, taps)
        parts_near = column_parts(after(half_columns(pack_rest[:, :split], is_text), column_qkv))
        w_down = after(w_down, column_qkv)
        pieces_qkv = half_pieces(column_qkv)
        column_near = jnp.stack([after(part, pieces_qkv[0]) for part in parts_near])
        parts_far = column_parts(after(pack_rest[:, split:], column_near))
        pieces_near = half_pieces(column_near)
        pieces_qkv[2] = after(pieces_qkv[2], pieces_near[0])
        pieces_qkv[3] = exchange(pieces_qkv[2], 1)
        groups_qkv = (("halves", 0),)
    else:
        groups_qkv = (("full", 0),)
        pieces_qkv = [lax.all_gather(pack_qkv, "page", axis=0, tiled=True)]
    full_down = lax.all_gather(w_down, "page", axis=0, tiled=True)

    other_mixed = dilated_mix(other_low.astype(f32), other_pages, conv_weight, conv_bias)
    other_mixed = other_mixed.astype(bf16)
    mixed_all = jnp.concatenate(
        [jnp.where(is_text, mixed_low, other_mixed), jnp.where(is_text, other_mixed, mixed_low)],
        axis=0,
    )
    if fast:
        pieces_qkv[0] = after(pieces_qkv[0], mixed_all, bias_up, *early)
    queries, keys_values, full_qkv, mixed_t = project(
        place, mixed_all, biases, groups_qkv, pieces_qkv
    )
    attend_in = queries
    if fast:
        column_far = jnp.stack([after(part, queries) for part in parts_far])
        across_far = exchange(column_far, 2)
        attend_in = after(queries, column_far)
    context = attend(bounds, attend_in, keys_values, features, own_feats, tables)
    if fast:
        pieces_near[2] = after(pieces_near[2], context)
        pieces_near[3] = exchange(pieces_near[2], 1)
        across_far = after(across_far, context)
        pieces_rest = pieces_near + row_pieces(column_far, across_far)
        groups_rest = (("halves", 0), ("rows", split))
    else:
        pieces_rest = [lax.all_gather(pack_rest, "page", axis=0, tiled=True)]
        groups_rest = (("full", 0),)
    unit, scale, normed_low, normed_t, context_t, active, active_t, slope, full_rest = up_forward(
        place, context, mixed, vectors, bias_up, groups_rest, pieces_rest
    )
    output_row, grad_sum_two, grad_ffn, small_two = down_forward(
        active, full_down, unit, vectors, cotangent[0, 0]
    )
    rows_down = grad_rows(active_t, grad_ffn)
    shard_down = lax.psum_scatter(rows_down, "page", scatter_dimension=0, tiled=True)
    grad_hidden, grad_b_up, grad_first, grad_branch, grad_context, small_one = ffn_back(
        after(grad_ffn, rows_down), slope, grad_sum_two, unit, scale, vectors, full_rest, full_down
    )
    attend_in = grad_context
    if fast:
        pairs = [(context_t, False, grad_branch), (normed_t, False, grad_hidden)]
        keep_rest, send_rest = grad_by_columns(pairs, place, d_model)
        partner_rest = exchange(send_rest, 1)
        held_rest, plane_out = halve_plane(place, keep_rest, partner_rest)
        plane_rest = swap(plane_out)
        attend_in = after(grad_context, plane_out)
    else:
        shard_rest = summed_rows([(context_t, grad_branch), (normed_t, grad_hidden)])
    grad_queries, grad_keys, grad_values, grad_tables = attend_back(
        bounds, queries, keys_values, attend_in, features, own_feats, own_flip, tables
    )
    grad_keys_in, grad_queries_in = grad_keys, grad_queries
    if fast:
        plane_rest = after(plane_rest, grad_queries)
        held_rest, across_out = halve_across(place, held_rest, plane_rest)
        across_rest = exchange(across_out, 2)
        grad_queries_in = after(grad_queries, across_out)
    pairs = [(mixed_t, True, grad_queries_in), (mixed_t, False, grad_keys), (mixed_t, False, grad_values)]
    if fast:
        keep_qkv, send_qkv = grad_by_columns(pairs, place, d_model)
        partner_qkv = exchange(send_qkv, 1)
        grad_keys_in = after(grad_keys, send_qkv)
    else:
        shard_down = shard_down.astype(f32) + swap(shard_down).astype(f32)
        shard_qkv = summed_rows(
            [(mixed_low.T, grad_queries), (mixed_t, grad_keys), (mixed_t, grad_values)]
        )
    to_other = input_back(place, full_qkv, grad_keys_in, grad_values, ())
    from_other = swap(to_other)
    grad_values_in = grad_values
    if fast:
        partner_qkv = after(partner_qkv, to_other)
        held_qkv, across_out = halve_across(place, keep_qkv, partner_qkv)
        across_qkv = exchange(across_out, 2)
        grad_values_in = after(grad_values, across_out)
    own_part = input_back(place, full_qkv, grad_keys, grad_values_in, (grad_first, grad_queries))
    packed = small_sums(
        own_part,
        to_other,
        own_low,
        other_low,
        masks,
        grad_queries,
        grad_values,
        small_one,
        small_two,
        grad_b_up,
        grad_tables,
    )
    if fast:
        packed = both_sum(packed, 1)
        shard_down = after(shard_down, packed)
        across_rest = after(across_rest, packed, shard_down)
        shard_down = shard_down.astype(f32) + swap(shard_down).astype(f32)
        own_rest, sends_rest = column_sends(held_rest, across_rest)
        arrived_rest = column_arrivals(sends_rest)
        packed = after(packed, *sends_rest)
        packed = packed + swap(packed)
        across_qkv = after(across_qkv, packed)
        own_qkv, sends_qkv = column_sends(held_qkv, across_qkv)
        arrived_qkv = column_arrivals(sends_qkv)
        from_other = after(from_other, *sends_qkv)
    else:
        packed = lax.psum(packed, ("mod", "page"))
    grad_in = state_back(own_part, from_other, masks, taps)
    if fast:
        arrived_rest = [after(part, grad_in) for part in arrived_rest]
        total_rest = column_total(own_rest, arrived_rest)
        far_rest = swap(total_rest)
        packed = both_sum(both_sum(after(packed, total_rest), 2), 4)
        arrived_qkv = [after(part, packed) for part in arrived_qkv]
        total_qkv = column_total(own_qkv, arrived_qkv)
        far_qkv = swap(total_qkv)
        packed = both_sum(after(packed, total_qkv), 8)
    g_tables = packed[28:34].reshape(HEADS, 3, LANES)
    if fast:
        shard_rest = jnp.where(
            is_text,
            jnp.concatenate([total_rest, far_rest], axis=1),
            jnp.concatenate([far_rest, total_rest], axis=1),
        ).astype(f32)
        shard_qkv = total_qkv.astype(f32) + far_qkv.astype(f32)
    return (
        output_row[None, None],
        grad_in[None, None],
        packed[0:3],
        packed[3],
        shard_qkv[:, :d_model],
        packed[4],
        shard_qkv[:, d_model : 2 * d_model],
        shard_qkv[:, 2 * d_model :],
        packed[5],
        shard_rest[:, :d_model],
        packed[10],
        g_tables[:, 0, : table_pos.shape[1]],
        g_tables[:, 1, 64 : 64 + table_x.shape[1]],
        g_tables[:, 2, 64 : 64 + table_y.shape[1]],
        packed[8],
        packed[9],
        shard_rest[:, d_model:],
        packed[24:28].reshape(d_ff),
        shard_down,
        packed[18],
        packed[16],
        packed[17],
    )


def solution(mesh):
    rows = P("mod", "page", None, None)
    ids = P("page", None)
    cut = P("page", None)
    return jax.shard_map(
        local,
        mesh=mesh,
        in_specs=(
            rows, rows, ids, ids, ids, P(), P(), cut, P(), cut, cut, P(), cut,
            P(), P(), P(), P(), P(), P(), cut, P(), cut, P(), P(), P(),
        ),
        out_specs=(
            rows, rows, P(), P(), cut, P(), cut, cut, P(), cut, P(), P(), P(),
            P(), P(), P(), cut, P(), cut, P(), P(), P(),
        ),
        check_vma=False,
    )
```

```python
import functools

import jax
import jax.numpy as jnp
import numpy as np
from jax import lax
from jax.experimental import pallas as pl
from jax.experimental.pallas import tpu as pltpu
from jax.sharding import PartitionSpec as P

HEADS = 12
HEAD = 64
GRID = 8
PAGES = 8
POS_BINS = 64
BOX_BINS = 32
PATCH = 64
TEXT = 512
PAIRS = HEADS // 2
LANES = 2 * HEAD
WINDOW = 144
SMALL = 80

dilation = 2
small_cost = pl.CostEstimate(flops=1000, bytes_accessed=1000, transcendentals=0)
norm_eps = 1e-05
mask_fill = -1000000000.0
erfc_poly = (
    0.2367515965428487,
    0.24062179898991767,
    0.18865103029313968,
    0.2877518531132804,
    -0.1648672439458568,
    0.4765735350541787,
    -0.34041833366480423,
    0.07493571514857543,
)
bf16 = jnp.bfloat16
f32 = jnp.float32


def shifted(values, offset, fill_value):
    padding = jnp.full((abs(offset),) + values.shape[1:], fill_value, values.dtype)
    if offset > 0:
        return jnp.concatenate([values[offset:], padding], axis=0)
    return jnp.concatenate([padding, values[:offset]], axis=0)


def dilated_mix(inputs, page_ids, conv_weight, conv_bias):
    summed = inputs + conv_bias + conv_weight[1] * inputs
    for tap_index, offset in ((0, -dilation), (2, dilation)):
        moved_rows = shifted(inputs, offset, 0.0)
        moved_pages = shifted(page_ids, offset, -1)
        same_page = (moved_pages == page_ids)[:, None]
        summed = summed + conv_weight[tap_index] * jnp.where(same_page, moved_rows, 0.0)
    return summed


def bin_features(pos_bins, bins_x, bins_y):
    return jnp.concatenate(
        [
            jax.nn.one_hot(pos_bins, POS_BINS, dtype=bf16),
            jax.nn.one_hot(bins_x, BOX_BINS, dtype=bf16),
            jax.nn.one_hot(bins_y, BOX_BINS, dtype=bf16),
        ],
        axis=1,
    )


def token_ids(text_pages, text_x, text_y):
    text_index = jnp.arange(TEXT, dtype=jnp.int32)
    text_pos = text_index * POS_BINS // TEXT
    patch_pos = text_index % PATCH * POS_BINS // PATCH
    patch_page = text_index // PATCH
    patch_x = text_index % GRID * BOX_BINS // GRID
    patch_y = text_index // GRID % GRID * BOX_BINS // GRID
    page_ids = jnp.stack([text_pages, patch_page])
    pos_bins = jnp.stack([text_pos, patch_pos])
    bins_x = jnp.stack([text_x, patch_x])
    bins_y = jnp.stack([text_y, patch_y])
    return (page_ids, pos_bins, bins_x, bins_y)


def plain_dot(left_side, right_side):
    return jnp.dot(left_side, right_side, preferred_element_type=f32)


def dot_left_t(left_side, right_side):
    return lax.dot_general(
        left_side, right_side, (((0,), (0,)), ((), ())), preferred_element_type=f32
    )


def dot_right_t(left_side, right_side):
    return lax.dot_general(
        left_side, right_side, (((1,), (1,)), ((), ())), preferred_element_type=f32
    )


def iota(shape, axis):
    return lax.broadcasted_iota(jnp.int32, shape, axis)


def bias_block(table_rows):
    pos_part = pltpu.roll(
        jnp.broadcast_to(table_rows[0:1], (POS_BINS, LANES)), 65, 1, stride=1, stride_axis=0
    )
    x_part = pltpu.roll(
        jnp.broadcast_to(table_rows[1:2], (BOX_BINS, LANES)), 33, 1, stride=1, stride_axis=0
    )
    y_part = pltpu.roll(
        jnp.broadcast_to(table_rows[2:3], (BOX_BINS, LANES)), 65, 1, stride=1, stride_axis=0
    )
    lane = iota((POS_BINS, LANES), 1)
    pos_part = jnp.where(lane < POS_BINS, pos_part, 0.0)
    lane = iota((BOX_BINS, LANES), 1)
    x_part = jnp.where((lane >= 64) & (lane < 96), x_part, 0.0)
    y_part = jnp.where(lane >= 96, y_part, 0.0)
    return jnp.concatenate([pos_part, x_part, y_part], axis=0).astype(bf16)


def diagonal_sums(grad_block):
    lane = iota((POS_BINS, LANES), 1)
    pos_part = jnp.where(lane < POS_BINS, grad_block[:64], 0.0)
    lane = iota((BOX_BINS, LANES), 1)
    x_part = jnp.where((lane >= 64) & (lane < 96), grad_block[64:96], 0.0)
    y_part = jnp.where(lane >= 96, grad_block[96:], 0.0)
    pos_part = pltpu.roll(pos_part, 0, 1, stride=1, stride_axis=0)
    x_part = pltpu.roll(x_part, 0, 1, stride=1, stride_axis=0)
    y_part = pltpu.roll(y_part, 96, 1, stride=1, stride_axis=0)
    rows = [jnp.sum(part, axis=0, keepdims=True) for part in (pos_part, x_part, y_part)]
    return jnp.concatenate(rows + [jnp.zeros((5, LANES), f32)], axis=0)


def stacked_heads(rows, low_lane):
    zero = jnp.zeros_like(rows)
    return jnp.concatenate(
        [jnp.where(low_lane, rows, zero), jnp.where(low_lane, zero, rows)], axis=0
    )


def window_start(first, window):
    return pl.multiple_of(jnp.minimum(first // 16 * 16, TEXT - window), 16)


def fits(first, end, window):
    return end - jnp.minimum(first // 16 * 16, TEXT - window) <= window


def for_each_page(bounds, step):
    def body(page, carry):
        own_low, own_high = bounds[page], bounds[PAGES + page]
        key_low, key_high = bounds[2 * PAGES + page], bounds[3 * PAGES + page]
        own_small = fits(own_low, own_high, SMALL)
        key_small = fits(key_low, key_high, SMALL)
        span = (own_low, own_high, key_low, key_high)
        small = own_small & key_small
        for chosen, own_window, key_window in (
            (small, SMALL, SMALL),
            (~small, WINDOW, WINDOW),
        ):

            @pl.when(chosen)
            def _():
                step(page, span, own_window, key_window)

        return carry

    lax.fori_loop(0, PAGES, body, 0)


def page_operands(page, span, own_window, key_window, pair, q_ref, k_ref, feat_ref, lookup):
    own_at = window_start(span[0], own_window)
    key_at = window_start(span[2], key_window)
    own_rows, text_rows = pl.ds(own_at, own_window), pl.ds(key_at, key_window)
    patch_at = TEXT + PATCH * page
    if not isinstance(page, int):
        patch_at = pl.multiple_of(patch_at, PATCH)
    patch_rows = pl.ds(patch_at, PATCH)
    lanes = slice(pair * LANES, (pair + 1) * LANES)
    low_lane = iota((own_window, LANES), 1) < HEAD
    queries = stacked_heads(q_ref[own_rows, lanes], low_lane)
    first = 2 * pair * LANES
    rel = jnp.concatenate(
        [
            lookup[own_rows, first : first + LANES],
            lookup[own_rows, first + LANES : first + 2 * LANES],
        ],
        axis=0,
    )
    query_side = jnp.concatenate([rel, queries], axis=1)
    key_side = jnp.concatenate(
        [
            jnp.concatenate([feat_ref[text_rows, :], k_ref[text_rows, lanes]], axis=1),
            jnp.concatenate([feat_ref[patch_rows, :], k_ref[patch_rows, lanes]], axis=1),
        ],
        axis=0,
    )
    own_row = iota((own_window, LANES), 0) + own_at
    own_ok = (own_row >= span[0]) & (own_row < span[1])
    return (
        lanes, low_lane, own_ok, queries, query_side, key_side, own_rows, text_rows, patch_rows, key_at
    )


def set_lookup(lookup, own_feat_ref, table_ref):
    blocks = [bias_block(table_ref[head]) for head in range(table_ref.shape[0])]
    product = jnp.dot(
        own_feat_ref[...], jnp.concatenate(blocks, axis=1), preferred_element_type=f32
    )
    lookup[...] = product.astype(bf16)


def attend_kernel(bounds, q_ref, k_ref, v_ref, feat_ref, own_feat_ref, table_ref, context_ref, lookup):
    set_lookup(lookup, own_feat_ref, table_ref)

    def step(page, span, own_window, key_window):
        column = iota((1, key_window + PATCH), 1)
        key_row = column + window_start(span[2], key_window)
        key_ok = (column >= key_window) | ((key_row >= span[2]) & (key_row < span[3]))
        for pair in range(q_ref.shape[1] // LANES):
            lanes, low_lane, own_ok, _, query_side, key_side, own_rows, text_rows, patch_rows, _ = (
                page_operands(
                    page, span, own_window, key_window, pair, q_ref, k_ref, feat_ref, lookup
                )
            )
            scores = jnp.where(key_ok, dot_right_t(query_side, key_side), mask_fill)
            row_max = jnp.max(scores, axis=1, keepdims=True)
            weights = jnp.exp(scores - row_max)
            total = jnp.sum(weights, axis=1, keepdims=True)
            prob = (weights * (1.0 / total)).astype(bf16)
            values = jnp.concatenate([v_ref[text_rows, lanes], v_ref[patch_rows, lanes]], axis=0)
            mixed = jnp.dot(prob, values, preferred_element_type=f32)
            picked = jnp.where(low_lane, mixed[:own_window], mixed[own_window:])
            before = context_ref[own_rows, lanes].astype(f32)
            context_ref[own_rows, lanes] = jnp.where(own_ok, picked, before).astype(bf16)

    for page in range(PAGES):
        span = [bounds[part * PAGES + page] for part in range(4)]
        step(page, span, WINDOW, WINDOW)


def attend_back_kernel(
    bounds,
    q_ref,
    k_ref,
    v_ref,
    grad_ref,
    feat_ref,
    own_feat_ref,
    flip_feat_ref,
    table_ref,
    grad_q_ref,
    grad_k_ref,
    grad_v_ref,
    grad_table_ref,
    lookup,
    grad_lookup,
):
    set_lookup(lookup, own_feat_ref, table_ref)

    def step(page, span, own_window, key_window):
        row = iota((key_window + PATCH, 1), 0)
        key_row = row + window_start(span[2], key_window)
        key_ok = (row >= key_window) | ((key_row >= span[2]) & (key_row < span[3]))
        for pair in range(q_ref.shape[1] // LANES):
            lanes, low_lane, own_ok, queries, query_side, key_side, own_rows, text_rows, patch_rows, key_at = (
                page_operands(
                    page, span, own_window, key_window, pair, q_ref, k_ref, feat_ref, lookup
                )
            )
            scores = jnp.where(key_ok, dot_right_t(key_side, query_side), mask_fill)
            col_max = jnp.max(scores, axis=0, keepdims=True)
            weights = jnp.exp(scores - col_max)
            total = jnp.sum(weights, axis=0, keepdims=True)
            prob = weights * (1.0 / total)
            grad_rows = grad_ref[own_rows, lanes]
            grad_rows = jnp.where(own_ok, grad_rows, jnp.zeros_like(grad_rows))
            grads = stacked_heads(grad_rows, low_lane)
            values = jnp.concatenate([v_ref[text_rows, lanes], v_ref[patch_rows, lanes]], axis=0)
            grad_prob = dot_right_t(values, grads)
            inner = jnp.sum(prob * grad_prob, axis=0, keepdims=True)
            grad_scores = (prob * (grad_prob - inner)).astype(bf16)
            grad_v = jnp.dot(prob.astype(bf16), grads, preferred_element_type=f32)
            grad_k = jnp.dot(grad_scores, queries, preferred_element_type=f32)
            back = dot_left_t(grad_scores, key_side)
            low, high = back[:own_window], back[own_window:]
            grad_q = jnp.where(low_lane, low[:, LANES:], high[:, LANES:]) * 0.125
            before = grad_q_ref[own_rows, lanes].astype(f32)
            grad_q_ref[own_rows, lanes] = jnp.where(own_ok, grad_q, before).astype(bf16)
            first = 2 * pair * LANES
            for part, at in ((low, first), (high, first + LANES)):
                place_at = slice(at, at + LANES)
                grad_lookup[own_rows, place_at] = jnp.where(
                    own_ok, part[:, :LANES], grad_lookup[own_rows, place_at]
                )
            wide_row = iota((key_window, LANES), 0) + key_at
            text_ok = (wide_row >= span[2]) & (wide_row < span[3])
            for grad, ref in ((grad_k, grad_k_ref), (grad_v, grad_v_ref)):
                before = ref[text_rows, lanes].astype(f32)
                ref[text_rows, lanes] = jnp.where(text_ok, grad[:key_window], before).astype(bf16)
                ref[patch_rows, lanes] = grad[key_window:].astype(bf16)

    for_each_page(bounds, step)
    grad_high = grad_lookup[...].astype(bf16)
    grad_rest = (grad_lookup[...] - grad_high.astype(f32)).astype(bf16)
    flip = flip_feat_ref[...]
    grad_block = dot_left_t(flip, grad_high) + dot_left_t(flip, grad_rest)
    for head in range(table_ref.shape[0]):
        grad_table_ref[head] = diagonal_sums(grad_block[:, head * LANES : (head + 1) * LANES])


def column_spec(rows, group, first=0):
    return pl.BlockSpec((rows, group * LANES), lambda step, bounds: (0, step + first))


def whole_spec(rows):
    return pl.BlockSpec((rows, LANES), lambda step, bounds: (0, 0))


def tables_spec(group):
    return pl.BlockSpec((2 * group, 8, LANES), lambda step, bounds: (step, 0, 0))


def attend(bounds, queries, keys_values, features, own_features, tables):
    group = 1
    return pl.pallas_call(
        attend_kernel,
        grid_spec=pltpu.PrefetchScalarGridSpec(
            num_scalar_prefetch=1,
            grid=(PAIRS // group,),
            in_specs=[
                column_spec(TEXT, group),
                column_spec(2 * TEXT, group),
                column_spec(2 * TEXT, group, PAIRS // group),
                whole_spec(2 * TEXT),
                whole_spec(TEXT),
                tables_spec(group),
            ],
            out_specs=column_spec(TEXT, group),
            scratch_shapes=[pltpu.VMEM((TEXT, 2 * group * LANES), bf16)],
        ),
        out_shape=jax.ShapeDtypeStruct((TEXT, HEADS * HEAD), bf16),
        cost_estimate=small_cost,
        name="attend",
    )(bounds, queries, keys_values, keys_values, features, own_features, tables)


def attend_back(
    bounds, queries, keys_values, grad_context, features, own_features, flip, tables
):
    group = 6
    return pl.pallas_call(
        attend_back_kernel,
        grid_spec=pltpu.PrefetchScalarGridSpec(
            num_scalar_prefetch=1,
            grid=(PAIRS // group,),
            in_specs=[
                column_spec(TEXT, group),
                column_spec(2 * TEXT, group),
                column_spec(2 * TEXT, group, PAIRS // group),
                column_spec(TEXT, group),
                whole_spec(2 * TEXT),
                whole_spec(TEXT),
                whole_spec(TEXT),
                tables_spec(group),
            ],
            out_specs=[
                column_spec(TEXT, group),
                column_spec(2 * TEXT, group),
                column_spec(2 * TEXT, group),
                tables_spec(group),
            ],
            scratch_shapes=[
                pltpu.VMEM((TEXT, 2 * group * LANES), bf16),
                pltpu.VMEM((TEXT, 2 * group * LANES), f32),
            ],
        ),
        out_shape=[
            jax.ShapeDtypeStruct((TEXT, HEADS * HEAD), bf16),
            jax.ShapeDtypeStruct((2 * TEXT, HEADS * HEAD), bf16),
            jax.ShapeDtypeStruct((2 * TEXT, HEADS * HEAD), bf16),
            jax.ShapeDtypeStruct((HEADS, 8, LANES), f32),
        ],
        cost_estimate=small_cost,
        name="attend_back",
    )(
        bounds,
        queries,
        keys_values,
        keys_values,
        grad_context,
        features,
        own_features,
        flip,
        tables,
    )


def exchange(values, mask):
    count = lax.axis_size("page")
    return lax.ppermute(values, "page", [(i, i ^ mask) for i in range(count)])


def after(value, *earlier):
    return lax.optimization_barrier((value, *earlier))[0]


def slot_mask(slot):
    return (slot & 3) * 4 + (slot >> 2) * 2


def project_kernel(groups, place, mixed_ref, bias_ref, *refs):
    *pieces, query_ref, both_ref, weight_ref, mixed_t_ref, sems = refs
    width = mixed_ref.shape[1]
    tokens = query_ref.shape[0]
    copies = start_rows(place, groups, pieces, weight_ref, sems)
    mixed_t_ref[...] = mixed_ref[...].T
    for copy in copies:
        copy.wait()
    own = mixed_ref[pl.ds(pl.multiple_of(place[1] * tokens, 16), tokens), :]
    queries = jnp.dot(own, weight_ref[:, :width], preferred_element_type=f32) + bias_ref[:, :width]
    query_ref[...] = (queries.astype(bf16).astype(f32) * 0.125).astype(bf16)
    for part in range(2):
        rows = pl.ds(part * tokens, tokens)
        for column in (1, 2):
            at = slice(column * width, (column + 1) * width)
            out = slice((column - 1) * width, column * width)
            values = jnp.dot(mixed_ref[rows, :], weight_ref[:, at], preferred_element_type=f32)
            both_ref[rows, out] = (values + bias_ref[:, at]).astype(bf16)


def project(place, mixed, biases, groups, pieces):
    rows, width = mixed.shape
    vmem = pl.BlockSpec(memory_space=pltpu.VMEM)
    return pl.pallas_call(
        functools.partial(project_kernel, groups),
        grid_spec=pltpu.PrefetchScalarGridSpec(
            num_scalar_prefetch=1,
            grid=(),
            in_specs=[vmem] * 2 + any_specs(len(pieces)),
            out_specs=[vmem] * 4,
            scratch_shapes=[pltpu.SemaphoreType.DMA((32,))],
        ),
        out_shape=[
            jax.ShapeDtypeStruct((rows // 2, width), bf16),
            jax.ShapeDtypeStruct((rows, 2 * width), bf16),
            jax.ShapeDtypeStruct((width, 3 * width), bf16),
            jax.ShapeDtypeStruct((width, rows), bf16),
        ],
        cost_estimate=small_cost,
        compiler_params=pltpu.CompilerParams(vmem_limit_bytes=16 << 20),
        name="project",
    )(place, mixed, biases, *pieces)


def column_parts(shard):
    return [shard] + [exchange(shard, 4 * step) for step in (1, 2, 3)]


def half_pieces(column):
    eight = jnp.concatenate([column, exchange(column, 2)])
    far = swap(eight)
    return [eight, exchange(eight, 1), far, exchange(far, 1)]


def row_pieces(column, across):
    return [column, exchange(column, 1), across, exchange(across, 1)]


def column_of(shard):
    return jnp.stack(column_parts(shard))


def row_copies(place, groups, refs, full, sems, first=0):
    copies = []
    for kind, column in groups:
        if kind == "full":
            piece, *refs = refs
            width = piece.shape[1]
            target = full.at[:, pl.ds(column, width)]
            copies.append(pltpu.make_async_copy(piece, target, sems.at[first + len(copies)]))
            continue
        pieces, refs = refs[:4], refs[4:]
        _, rows, width = pieces[0].shape
        for index in range(32 if kind == "halves" else 16):
            at = column
            if kind == "halves":
                source, slot = index >> 3, index & 7
                mask = slot_mask(slot) + (source & 1)
                at = pl.multiple_of(column + (place[1] ^ (source >> 1)) * width, 128)
            else:
                source, slot = index & 3, index >> 2
                mask = slot * 4 + source
            row = pl.multiple_of((place[0] ^ mask) * rows, 16)
            copies.append(
                pltpu.make_async_copy(
                    pieces[source].at[slot],
                    full.at[pl.ds(row, rows), pl.ds(at, width)],
                    sems.at[first + len(copies)],
                )
            )
    return copies


def start_rows(place, groups, refs, full, sems):
    copies = row_copies(place, groups, refs, full, sems)
    for copy in copies:
        copy.start()
    return copies


def gelu_parts(values):
    size = jnp.abs(values)
    t = 1.0 / (1.0 + (0.42 * 0.7071067811865476) * size)
    poly = jnp.full_like(t, erfc_poly[-1])
    for coefficient in erfc_poly[-2::-1]:
        poly = poly * t + coefficient
    bell = jnp.exp(-0.5 * values * values)
    tail = (0.5 * t) * (poly * bell)
    cdf = jnp.where(values >= 0.0, 1.0 - tail, tail)
    return values * cdf, cdf + (values * 0.3989422804014327) * bell


def normalized(values):
    centered = values - jnp.mean(values, axis=1, keepdims=True)
    variance = jnp.mean(centered * centered, axis=1, keepdims=True)
    scale = lax.rsqrt(variance + norm_eps)
    return centered * scale, scale


def norm_back(grads, unit, scale, gain):
    scaled = grads * gain
    mean = jnp.mean(scaled, axis=1, keepdims=True)
    inner = jnp.mean(scaled * unit, axis=1, keepdims=True)
    return scale * (scaled - mean - unit * inner)


def up_kernel(groups, place, context_ref, mixed_ref, vec_ref, bias_ref, *refs):
    *pieces, unit_ref, scale_ref, low_ref, low_t_ref, context_t_ref = refs[:-9]
    active_ref, active_t_ref, slope_ref, full_ref = refs[-9:-5]
    weight, hidden, low, sems, full_sem = refs[-5:]
    step = pl.program_id(0)
    tiles = pl.num_programs(0) - 1
    width = context_ref.shape[1]
    tile = active_ref.shape[1]
    last_group = 16 if len(groups) > 1 else 0

    def full_copy():
        return pltpu.make_async_copy(weight, full_ref, full_sem)

    @pl.when(step == 0)
    def _():
        copies = row_copies(place, groups, pieces, weight, sems)
        for copy in copies:
            copy.start()
        context_t_ref[...] = context_ref[...].T
        for copy in copies[: len(copies) - last_group]:
            copy.wait()
        branch = jnp.dot(context_ref[...], weight[:, :width], preferred_element_type=f32)
        unit, scale = normalized(mixed_ref[...] + branch + vec_ref[0:1])
        unit_ref[...] = unit
        scale_ref[...] = jnp.broadcast_to(scale, scale_ref.shape)
        normed = (unit * vec_ref[1:2] + vec_ref[2:3]).astype(bf16)
        low[...] = normed
        low_ref[...] = normed
        low_t_ref[...] = normed.T

    @pl.when(step == 1)
    def _():
        if last_group:
            for copy in row_copies(place, groups[1:], pieces[4:], weight, sems, 32):
                copy.wait()
        full_copy().start()

    def product():
        at = pl.multiple_of(width + step * tile, 128)
        return jnp.dot(low[...], weight[:, pl.ds(at, tile)], preferred_element_type=f32)

    def activate():
        active, slope = gelu_parts(hidden[(step + 1) % 2] + bias_ref[...])
        active = active.astype(bf16)
        active_ref[...] = active
        active_t_ref[...] = active.T
        slope_ref[...] = slope.astype(bf16)

    @pl.when(step == 0)
    def _():
        hidden[step % 2] = product()

    @pl.when((step > 0) & (step < tiles))
    def _():
        hidden[step % 2] = product()
        activate()

    @pl.when(step == tiles)
    def _():
        activate()
        full_copy().wait()


def any_specs(count):
    return [pl.BlockSpec(memory_space=pl.ANY)] * count


def up_forward(place, context, mixed, vectors, bias_up, groups, pieces):
    tokens, width = mixed.shape
    hidden_width = bias_up.shape[1]
    tile = 768
    whole = lambda step, place: (0, 0)
    last = lambda step, place: (0, jnp.maximum(step - 1, 0))
    last_t = lambda step, place: (jnp.maximum(step - 1, 0), 0)
    return pl.pallas_call(
        functools.partial(up_kernel, groups),
        grid_spec=pltpu.PrefetchScalarGridSpec(
            num_scalar_prefetch=1,
            grid=(hidden_width // tile + 1,),
            in_specs=[
                pl.BlockSpec((tokens, width), whole),
                pl.BlockSpec((tokens, width), whole),
                pl.BlockSpec(vectors.shape, whole),
                pl.BlockSpec((1, tile), last),
            ]
            + any_specs(len(pieces)),
            out_specs=[
                pl.BlockSpec((tokens, width), whole),
                pl.BlockSpec((tokens, 128), whole),
                pl.BlockSpec((tokens, width), whole),
                pl.BlockSpec((width, tokens), whole),
                pl.BlockSpec((width, tokens), whole),
                pl.BlockSpec((tokens, tile), last),
                pl.BlockSpec((tile, tokens), last_t),
                pl.BlockSpec((tokens, tile), last),
                pl.BlockSpec(memory_space=pl.ANY),
            ],
            scratch_shapes=[
                pltpu.VMEM((width, width + hidden_width), bf16),
                pltpu.VMEM((2, tokens, tile), f32),
                pltpu.VMEM((tokens, width), bf16),
                pltpu.SemaphoreType.DMA((48,)),
                pltpu.SemaphoreType.DMA,
            ],
        ),
        out_shape=[
            jax.ShapeDtypeStruct((tokens, width), f32),
            jax.ShapeDtypeStruct((tokens, 128), f32),
            jax.ShapeDtypeStruct((tokens, width), bf16),
            jax.ShapeDtypeStruct((width, tokens), bf16),
            jax.ShapeDtypeStruct((width, tokens), bf16),
            jax.ShapeDtypeStruct((tokens, hidden_width), bf16),
            jax.ShapeDtypeStruct((hidden_width, tokens), bf16),
            jax.ShapeDtypeStruct((tokens, hidden_width), bf16),
            jax.ShapeDtypeStruct((width, width + hidden_width), bf16),
        ],
        cost_estimate=small_cost,
        name="up_forward",
    )(place, context, mixed, vectors, bias_up, *pieces)


def down_kernel(active_ref, weight_ref, unit_ref, vec_ref, grad_ref, *refs):
    out_ref, sum_ref, low_ref, small_ref, total = refs
    step = pl.program_id(0)
    product = jnp.dot(active_ref[...], weight_ref[...], preferred_element_type=f32)

    @pl.when(step == 0)
    def _():
        total[...] = product

    @pl.when(step > 0)
    def _():
        total[...] += product

    @pl.when(step == pl.num_programs(0) - 1)
    def _():
        tokens, width = unit_ref.shape
        half = tokens // 2
        smalls = [jnp.zeros((1, width), f32)] * 3
        for part in range(2):
            rows = pl.ds(part * half, half)
            normed = unit_ref[rows, :] * vec_ref[1:2] + vec_ref[2:3]
            unit, scale = normalized(normed + total[rows, :] + vec_ref[3:4])
            out_ref[rows, :] = (unit * vec_ref[4:5] + vec_ref[5:6]).astype(bf16)
            grads = grad_ref[rows, :].astype(f32)
            back = norm_back(grads, unit, scale, vec_ref[4:5])
            low = back.astype(bf16)
            sum_ref[rows, :] = back
            low_ref[rows, :] = low
            for index, term in enumerate((grads * unit, grads, low.astype(f32))):
                smalls[index] = smalls[index] + jnp.sum(term, axis=0, keepdims=True)
        small_ref[...] = jnp.concatenate(smalls + [jnp.zeros((5, width), f32)], axis=0)


def down_forward(active, weight, unit, vectors, grads):
    tokens, width = unit.shape
    hidden_width = active.shape[1]
    tile = 1536
    whole = lambda step: (0, 0)
    token_block = pl.BlockSpec((tokens, width), whole)
    return pl.pallas_call(
        down_kernel,
        grid=(hidden_width // tile,),
        in_specs=[
            pl.BlockSpec((tokens, tile), lambda step: (0, step)),
            pl.BlockSpec((tile, width), lambda step: (step, 0)),
            token_block,
            pl.BlockSpec(vectors.shape, whole),
            token_block,
        ],
        out_specs=[token_block] * 3 + [pl.BlockSpec((8, width), whole)],
        scratch_shapes=[pltpu.VMEM((tokens, width), f32)],
        out_shape=[
            jax.ShapeDtypeStruct((tokens, width), bf16),
            jax.ShapeDtypeStruct((tokens, width), f32),
            jax.ShapeDtypeStruct((tokens, width), bf16),
            jax.ShapeDtypeStruct((8, width), f32),
        ],
        cost_estimate=small_cost,
        name="down_forward",
    )(active, weight, unit, vectors, grads)


def ffn_back_kernel(*refs):
    low_ref, slope_ref, sum_ref, unit_ref, scale_ref, vec_ref = refs[:6]
    down_ref, up_ref, out_weight_ref = refs[6:9]
    hidden_ref, bias_ref, first_ref, branch_ref, context_ref, small_ref, total = refs[9:]
    step = pl.program_id(0)
    tokens, width = unit_ref.shape
    tile = slope_ref.shape[1]
    half = tokens // 2

    @pl.when(step == 0)
    def _():
        total[...] = sum_ref[...]

    bias = jnp.zeros((1, tile), f32)
    for part in range(2):
        rows = pl.ds(part * half, half)
        grads = dot_right_t(low_ref[rows, :], down_ref[...]) * slope_ref[rows, :].astype(f32)
        grads = grads.astype(bf16)
        hidden_ref[rows, :] = grads
        bias = bias + jnp.sum(grads.astype(f32), axis=0, keepdims=True)
        total[rows, :] += dot_right_t(grads, up_ref[...])
    bias_ref[...] = bias

    @pl.when(step == pl.num_programs(0) - 1)
    def _():
        grads = total[...]
        unit = unit_ref[...]
        first = norm_back(grads, unit, scale_ref[:, 0:1], vec_ref[1:2])
        branch = first.astype(bf16)
        first_ref[...] = first
        branch_ref[...] = branch
        context_ref[...] = dot_right_t(branch, out_weight_ref[...]).astype(bf16)
        smalls = [
            jnp.sum(term, axis=0, keepdims=True)
            for term in (grads * unit, grads, branch.astype(f32))
        ]
        small_ref[...] = jnp.concatenate(smalls + [jnp.zeros((5, width), f32)], axis=0)


def ffn_back(low, slope, total, unit, scale, vectors, full_rest, full_down):
    tokens, width = unit.shape
    hidden_width = slope.shape[1]
    tile = 768
    whole = lambda step: (0, 0)
    column = lambda step: (0, step)
    token_block = pl.BlockSpec((tokens, width), whole)
    return pl.pallas_call(
        ffn_back_kernel,
        grid=(hidden_width // tile,),
        in_specs=[
            token_block,
            pl.BlockSpec((tokens, tile), column),
            token_block,
            token_block,
            pl.BlockSpec((tokens, 128), whole),
            pl.BlockSpec(vectors.shape, whole),
            pl.BlockSpec((tile, width), lambda step: (step, 0)),
            pl.BlockSpec((width, tile), lambda step: (0, step + 1)),
            pl.BlockSpec((width, width), whole),
        ],
        out_specs=[
            pl.BlockSpec((tokens, tile), column),
            pl.BlockSpec((1, tile), column),
            token_block,
            token_block,
            token_block,
            pl.BlockSpec((8, width), whole),
        ],
        scratch_shapes=[pltpu.VMEM((tokens, width), f32)],
        out_shape=[
            jax.ShapeDtypeStruct((tokens, hidden_width), bf16),
            jax.ShapeDtypeStruct((1, hidden_width), f32),
            jax.ShapeDtypeStruct((tokens, width), f32),
            jax.ShapeDtypeStruct((tokens, width), bf16),
            jax.ShapeDtypeStruct((tokens, width), bf16),
            jax.ShapeDtypeStruct((8, width), f32),
        ],
        cost_estimate=small_cost,
        name="ffn_back",
    )(low, slope, total, unit, scale, vectors, full_down, full_rest, full_rest)


def grad_rows_kernel(x_ref, h_ref, out_ref):
    out_ref[...] = jnp.dot(x_ref[...], h_ref[...], preferred_element_type=f32).astype(bf16)


def grad_rows(inputs_t, grads):
    width, tokens = inputs_t.shape
    columns = grads.shape[1]
    return pl.pallas_call(
        grad_rows_kernel,
        grid=(4,),
        in_specs=[
            pl.BlockSpec((width // 4, tokens), lambda step: (step, 0)),
            pl.BlockSpec((tokens, columns), lambda step: (0, 0)),
        ],
        out_specs=pl.BlockSpec((width // 4, columns), lambda step: (step, 0)),
        out_shape=jax.ShapeDtypeStruct((width, columns), bf16),
        cost_estimate=small_cost,
        name="grad_rows",
    )(inputs_t, grads)


def grad_columns_kernel(parts, place, *refs):
    count = len(parts)
    ins, keep_ref, send_ref, scratch = (
        refs[: 2 * count],
        refs[2 * count],
        refs[2 * count + 1],
        refs[2 * count + 2 :],
    )
    rows, tile = keep_ref.shape[1], keep_ref.shape[2]
    step = pl.program_id(0)
    first = 0
    for index, steps in enumerate(parts):
        x_ref, h_ref, ordered = ins[2 * index], ins[2 * index + 1], scratch[index]

        @pl.when(step == first)
        def _():
            for slot in range(16):
                mask = slot_mask(slot & 7) + (slot >> 3)
                at = pl.multiple_of((place[0] ^ mask) * rows, 16)
                ordered[pl.ds(slot * rows, rows), :] = x_ref[pl.ds(at, rows), :]

        @pl.when((step >= first) & (step < first + steps))
        def _():
            product = jnp.dot(ordered[...], h_ref[...], preferred_element_type=f32).astype(bf16)
            keep_ref[...] = product[: 8 * rows].reshape(8, rows, tile)
            send_ref[...] = product[8 * rows :].reshape(8, rows, tile)

        first = first + steps


def grad_by_columns(pairs, place, tile):
    width = pairs[0][0].shape[0]
    rows = width // 16
    parts = tuple(count for *_, count in pairs)
    steps = sum(parts)
    specs = []
    operands = []
    scratch = []
    first = 0
    for inputs_t, own, grads, start, count in pairs:
        tokens = grads.shape[0]
        block = (lambda step, place: (0, place[1])) if own else (lambda step, place: (0, 0))
        specs.append(pl.BlockSpec((width, tokens), block))

        def column(step, place, first=first, start=start, count=count):
            return (0, start + jnp.clip(step - first, 0, count - 1))

        specs.append(pl.BlockSpec((tokens, tile), column))
        operands += [inputs_t, grads]
        scratch.append(pltpu.VMEM((width, tokens), bf16))
        first = first + count
    half = jax.ShapeDtypeStruct((8, rows, steps * tile), bf16)
    return pl.pallas_call(
        functools.partial(grad_columns_kernel, parts),
        grid_spec=pltpu.PrefetchScalarGridSpec(
            num_scalar_prefetch=1,
            grid=(steps,),
            in_specs=specs,
            out_specs=[pl.BlockSpec((8, rows, tile), lambda step, place: (0, 0, step))] * 2,
            scratch_shapes=scratch,
        ),
        out_shape=[half, half],
        cost_estimate=small_cost,
        compiler_params=pltpu.CompilerParams(vmem_limit_bytes=16 << 20),
        name="grad_columns",
    )(place, *operands)


def key_back_kernel(place, gk_ref, gv_ref, wk_ref, wv_ref, out_ref):
    total = dot_right_t(gk_ref[...], wk_ref[...]) + dot_right_t(gv_ref[...], wv_ref[...])
    out_ref[...] = total.astype(out_ref.dtype)


def own_back_kernel(place, first_ref, gq_ref, gk_ref, gv_ref, wq_ref, wk_ref, wv_ref, out_ref):
    total = dot_right_t(gk_ref[...], wk_ref[...]) + dot_right_t(gv_ref[...], wv_ref[...])
    out_ref[...] = first_ref[...] + total + dot_right_t(gq_ref[...], wq_ref[...])


def input_back(place, weights, grad_keys, grad_values, others):
    width = weights.shape[0]
    tokens = grad_keys.shape[0] // 2
    whole = pl.BlockSpec((tokens, width), lambda step, place: (0, 0))
    row = lambda step, place: ((place[1] if others else 1 - place[1]), 0)
    if others:
        kernel, leading, first, dtype = own_back_kernel, [whole, whole], 0, f32
    else:
        kernel, leading, first, dtype = key_back_kernel, [], 1, bf16
    operands = list(others) + [grad_keys, grad_values] + [weights] * (3 - first)
    specs = [pl.BlockSpec((tokens, width), row)] * 2
    for block in range(first, 3):
        specs.append(pl.BlockSpec((width, width), lambda step, place, block=block: (0, block)))
    return pl.pallas_call(
        kernel,
        grid_spec=pltpu.PrefetchScalarGridSpec(
            num_scalar_prefetch=1, grid=(1,), in_specs=leading + specs, out_specs=whole
        ),
        out_shape=jax.ShapeDtypeStruct((tokens, width), dtype),
        cost_estimate=small_cost,
        compiler_params=pltpu.CompilerParams(vmem_limit_bytes=16 << 20),
        name="input_back",
    )(place, *operands)


def back_rows(values, mask):
    return jnp.where(mask, pltpu.roll(values, dilation, 0), 0.0)


def ahead_rows(values, mask):
    return jnp.where(mask, pltpu.roll(values, values.shape[0] - dilation, 0), 0.0)


def tap_sums(grads, inputs, ahead, back):
    terms = (grads * back_rows(inputs, back), grads * inputs, grads * ahead_rows(inputs, ahead), grads)
    return [jnp.sum(term, axis=0, keepdims=True) for term in terms]


def small_sums_kernel(
    own_ref, other_ref, x_ref, x_other_ref, mask_ref, gq_ref, gv_ref, one_ref, two_ref, up_ref, table_ref, out_ref
):
    width = own_ref.shape[1]
    mask = mask_ref[...] > 0.0
    own = tap_sums(own_ref[...], x_ref[...].astype(f32), mask[:, 0:1], mask[:, 1:2])
    other = tap_sums(
        other_ref[...].astype(f32), x_other_ref[...].astype(f32), mask[:, 2:3], mask[:, 3:4]
    )
    rows = [a + b for a, b in zip(own, other)]
    for ref in (gq_ref, gv_ref):
        rows.append(jnp.sum(ref[...].astype(f32), axis=0, keepdims=True))
    rows.append(jnp.zeros((2, width), f32))
    out_ref[0:8] = jnp.concatenate(rows, axis=0)
    out_ref[8:16] = one_ref[...]
    out_ref[16:24] = two_ref[...]
    count = up_ref.shape[1] // width
    for index in range(count):
        out_ref[24 + index : 25 + index] = up_ref[:, index * width : (index + 1) * width]
    for index in range(3 * HEADS):
        row, lane = 28 + index // 6, index % 6 * LANES
        table = table_ref[index // 3]
        out_ref[row : row + 1, lane : lane + LANES] = table[index % 3 : index % 3 + 1]
    out_ref[34:40] = jnp.zeros((6, width), f32)


def small_sums(*operands):
    return pl.pallas_call(
        small_sums_kernel,
        out_shape=jax.ShapeDtypeStruct((40, operands[0].shape[1]), f32),
        cost_estimate=small_cost,
        compiler_params=pltpu.CompilerParams(vmem_limit_bytes=24 << 20),
        name="small_sums",
    )(*operands)


def state_back_kernel(own_ref, other_ref, mask_ref, tap_ref, out_ref):
    grads = own_ref[...] + other_ref[...].astype(f32)
    mask = mask_ref[...] > 0.0
    total = grads + tap_ref[1:2] * grads
    total = total + tap_ref[0:1] * ahead_rows(grads, mask[:, 0:1])
    total = total + tap_ref[2:3] * back_rows(grads, mask[:, 1:2])
    out_ref[...] = total.astype(bf16)


def state_back(own, other, masks, taps):
    return pl.pallas_call(
        state_back_kernel,
        out_shape=jax.ShapeDtypeStruct(own.shape, bf16),
        cost_estimate=small_cost,
        compiler_params=pltpu.CompilerParams(vmem_limit_bytes=20 << 20),
        name="state_back",
    )(own, other, masks, taps)


def first_half_kernel(place, keep_near, part_near, keep_far, part_far, held_ref, out_ref):
    held_ref[...] = keep_near[...].astype(f32) + part_near[...].astype(f32)
    out_ref[...] = (keep_far[...].astype(f32) + part_far[...].astype(f32)).astype(bf16)


def halve_call(place, keep, partner, specs, half_shape, steps):
    near, far, out = specs
    return pl.pallas_call(
        first_half_kernel,
        grid_spec=pltpu.PrefetchScalarGridSpec(
            num_scalar_prefetch=1,
            grid=(steps,),
            in_specs=[near, near, far, far],
            out_specs=[out, out],
        ),
        out_shape=[
            jax.ShapeDtypeStruct(half_shape, f32),
            jax.ShapeDtypeStruct(half_shape, bf16),
        ],
        cost_estimate=small_cost,
        compiler_params=pltpu.CompilerParams(vmem_limit_bytes=12 << 20),
        name="halve",
    )(place, keep, partner, keep, partner)


def halve_across(place, keep, partner):
    _, rows, width = keep.shape
    near = pl.BlockSpec((1, rows, width), lambda step, place: (step, 0, 0))
    far = pl.BlockSpec((1, rows, width), lambda step, place: (step + 4, 0, 0))
    return halve_call(place, keep, partner, (near, far, near), (4, rows, width), 4)


def halve_plane(place, keep, partner):
    _, rows, width = keep.shape
    block = (2, rows, width // 2)
    near = pl.BlockSpec(block, lambda step, place: (step, 0, place[1]))
    far = pl.BlockSpec(block, lambda step, place: (step, 0, 1 - place[1]))
    out = pl.BlockSpec(block, lambda step, place: (step, 0, 0))
    return halve_call(place, keep, partner, (near, far, out), (8, rows, width // 2), 4)


def two_kernel(near_a, far_a, near_b, far_b, *refs):
    *partners, held_ref, out_ref = refs
    split = near_a.shape[2]
    for index, (near, far) in enumerate(((near_a, far_a), (near_b, far_b))):
        lanes = slice(0, split) if index == 0 else slice(split, None)
        part_near, part_far = partners[2 * index], partners[2 * index + 1]
        held_ref[:, :, lanes] = near[...] + part_near[...].astype(f32)
        out_ref[:, :, lanes] = (far[...] + part_far[...].astype(f32)).astype(bf16)


def halve_two(held_a, part_a, held_b, part_b):
    _, rows, width_a = held_a.shape
    width_b = held_b.shape[2]
    specs = []
    for width in (width_a, width_b):
        block = (1, rows, width)
        specs.append(pl.BlockSpec(block, lambda step: (step, 0, 0)))
        specs.append(pl.BlockSpec(block, lambda step: (step + 4, 0, 0)))
    out = pl.BlockSpec((1, rows, width_a + width_b), lambda step: (step, 0, 0))
    shape = (4, rows, width_a + width_b)
    return pl.pallas_call(
        two_kernel,
        grid=(4,),
        in_specs=specs * 2,
        out_specs=[out, out],
        out_shape=[jax.ShapeDtypeStruct(shape, f32), jax.ShapeDtypeStruct(shape, bf16)],
        cost_estimate=small_cost,
        compiler_params=pltpu.CompilerParams(vmem_limit_bytes=12 << 20),
        name="halve_two",
    )(held_a, held_a, held_b, held_b, part_a, part_a, part_b, part_b)


def column_kernel(held_ref, across_ref, own_ref, *sends):
    own_ref[...] = held_ref[0] + across_ref[0].astype(f32)
    for step, send in enumerate(sends, 1):
        send[...] = (held_ref[step] + across_ref[step].astype(f32)).astype(bf16)


def column_sends(held, across):
    _, rows, width = held.shape
    tile = 384
    out = pl.BlockSpec((rows, tile), lambda step: (0, step))
    block = pl.BlockSpec((4, rows, tile), lambda step: (0, 0, step))
    own, *sends = pl.pallas_call(
        column_kernel,
        grid=(width // tile,),
        in_specs=[block, block],
        out_specs=[out] * 4,
        out_shape=[jax.ShapeDtypeStruct((rows, width), f32)]
        + [jax.ShapeDtypeStruct((rows, width), bf16)] * 3,
        cost_estimate=small_cost,
        compiler_params=pltpu.CompilerParams(vmem_limit_bytes=12 << 20),
        name="column_sends",
    )(held, across)
    return own, sends


def column_arrivals(sends):
    return [exchange(send, 4 * step) for step, send in enumerate(sends, 1)]


def column_total(own, arrived):
    total = own
    for part in arrived:
        total = total + part.astype(f32)
    return total.astype(bf16)


def half_columns(values, first):
    half = values.shape[-1] // 2
    return jnp.where(first, values[..., :half], values[..., half:])


def summed_rows(pairs):
    grads = jnp.concatenate([plain_dot(*pair).astype(bf16) for pair in pairs], axis=1)
    shard = lax.psum_scatter(grads, "page", scatter_dimension=0, tiled=True)
    return shard.astype(f32) + swap(shard).astype(f32)


def page_bounds(segments, is_text):
    pages = jnp.arange(PAGES, dtype=jnp.int32)
    low = jnp.sum(segments[None, :] < pages[:, None], axis=1, dtype=jnp.int32)
    high = jnp.sum(segments[None, :] <= pages[:, None], axis=1, dtype=jnp.int32)
    own_low = jnp.where(is_text, low, pages * PATCH)
    own_high = jnp.where(is_text, high, (pages + 1) * PATCH)

    return jnp.concatenate([own_low, own_high, low, high])


def both_sum(values, mask):
    return values + exchange(values, mask)


def swap(values):
    return lax.ppermute(values, "mod", [(0, 1), (1, 0)])


def local(
    states,
    cotangent,
    segments,
    box_x,
    box_y,
    conv_weight,
    conv_bias,
    w_query,
    b_query,
    w_key,
    w_value,
    b_value,
    w_out,
    b_out,
    table_pos,
    table_x,
    table_y,
    gain_one,
    bias_one,
    w_up,
    b_up,
    w_down,
    b_down,
    gain_two,
    bias_two,
):
    is_text = lax.axis_index("mod") == 0
    d_model = states.shape[3]
    own_low = states[0, 0]
    rows_each = w_query.shape[0]
    d_ff = w_up.shape[1]
    fast = lax.axis_size("page") == 16 and rows_each % 16 == 0 and w_down.shape[0] % 16 == 0
    place = jnp.stack([lax.axis_index("page"), lax.axis_index("mod")]).astype(jnp.int32)
    pack_qkv = jnp.concatenate([w_query, w_key, w_value], axis=1)
    pack_rest = jnp.concatenate([w_out, w_up], axis=1)
    other_low = swap(own_low)
    if fast:
        column_qkv = column_of(half_columns(pack_qkv, is_text))
        table_pos, table_x, table_y, b_out, b_down, b_query, b_value, b_up = after(
            (table_pos, table_x, table_y, b_out, b_down, b_query, b_value, b_up), column_qkv
        )
        gain_one, bias_one, gain_two, bias_two, conv_weight = after(
            (gain_one, bias_one, gain_two, bias_two, conv_weight), column_qkv
        )
        segments, box_x, box_y = after((segments, box_x, box_y), column_qkv)
    page_ids, pos_bins, bins_x, bins_y = token_ids(segments[0], box_x[0], box_y[0])
    bounds = page_bounds(segments[0], is_text)
    own_pages = jnp.where(is_text, page_ids[0], page_ids[1])
    features = bin_features(pos_bins.reshape(-1), bins_x.reshape(-1), bins_y.reshape(-1))
    flipped = bin_features(
        POS_BINS - 1 - pos_bins.reshape(-1),
        BOX_BINS - 1 - bins_x.reshape(-1),
        BOX_BINS - 1 - bins_y.reshape(-1),
    )
    own_feats = jnp.where(is_text, features[:TEXT], features[TEXT:])
    own_flip = jnp.where(is_text, flipped[:TEXT], flipped[TEXT:])
    tables = jnp.stack(
        [
            jnp.pad(table_pos, ((0, 0), (0, LANES - table_pos.shape[1]))),
            jnp.pad(table_x, ((0, 0), (0, LANES - table_x.shape[1]))),
            jnp.pad(table_y, ((0, 0), (0, LANES - table_y.shape[1]))),
        ],
        axis=1,
    )
    tables = jnp.pad(tables, ((0, 0), (0, 5), (0, 0)))

    own_states = own_low.astype(f32)
    mixed = dilated_mix(own_states, own_pages, conv_weight, conv_bias)
    mixed_low = mixed.astype(bf16)
    other_pages = jnp.where(is_text, page_ids[1], page_ids[0])
    masks = jnp.pad(
        jnp.stack(
            [
                own_pages == shifted(own_pages, dilation, -1),
                own_pages == shifted(own_pages, -dilation, -1),
                other_pages == shifted(other_pages, dilation, -1),
                other_pages == shifted(other_pages, -dilation, -1),
            ],
            axis=1,
        ).astype(f32),
        ((0, 0), (0, LANES - 4)),
    )
    vectors = jnp.stack(
        [b_out, gain_one, bias_one, b_down, gain_two, bias_two, jnp.zeros_like(b_out), b_out]
    )
    biases = jnp.concatenate([b_query, jnp.zeros_like(b_value), b_value])[None]
    taps = jnp.pad(conv_weight, ((0, 5), (0, 0)))
    bias_up = b_up[None]
    if fast:
        split = (pack_rest.shape[1] // 2 + 127) // 256 * 256
        early = (features, own_feats, own_flip, tables, bounds, masks, vectors, biases, taps)
        parts_near = column_parts(after(half_columns(pack_rest[:, :split], is_text), column_qkv))
        w_down = after(w_down, column_qkv)
        pieces_qkv = half_pieces(column_qkv)
        column_near = jnp.stack([after(part, pieces_qkv[0]) for part in parts_near])
        parts_far = column_parts(after(pack_rest[:, split:], column_near))
        pieces_near = half_pieces(column_near)
        pieces_qkv[2] = after(pieces_qkv[2], pieces_near[0])
        pieces_qkv[3] = exchange(pieces_qkv[2], 1)
        groups_qkv = (("halves", 0),)
    else:
        groups_qkv = (("full", 0),)
        pieces_qkv = [lax.all_gather(pack_qkv, "page", axis=0, tiled=True)]
    full_down = lax.all_gather(w_down, "page", axis=0, tiled=True)

    other_mixed = dilated_mix(other_low.astype(f32), other_pages, conv_weight, conv_bias)
    other_mixed = other_mixed.astype(bf16)
    mixed_all = jnp.concatenate(
        [jnp.where(is_text, mixed_low, other_mixed), jnp.where(is_text, other_mixed, mixed_low)],
        axis=0,
    )
    if fast:
        pieces_qkv[0] = after(pieces_qkv[0], mixed_all, bias_up, *early)
    queries, keys_values, full_qkv, mixed_t = project(
        place, mixed_all, biases, groups_qkv, pieces_qkv
    )
    attend_in = queries
    if fast:
        column_far = jnp.stack([after(part, queries) for part in parts_far])
        across_far = exchange(column_far, 2)
        attend_in = after(queries, column_far)
    context = attend(bounds, attend_in, keys_values, features, own_feats, tables)
    if fast:
        pieces_near[2] = after(pieces_near[2], context)
        pieces_near[3] = exchange(pieces_near[2], 1)
        across_far = after(across_far, context)
        pieces_rest = pieces_near + row_pieces(column_far, across_far)
        groups_rest = (("halves", 0), ("rows", split))
    else:
        pieces_rest = [lax.all_gather(pack_rest, "page", axis=0, tiled=True)]
        groups_rest = (("full", 0),)
    unit, scale, normed_low, normed_t, context_t, active, active_t, slope, full_rest = up_forward(
        place, context, mixed, vectors, bias_up, groups_rest, pieces_rest
    )
    output_row, grad_sum_two, grad_ffn, small_two = down_forward(
        active, full_down, unit, vectors, cotangent[0, 0]
    )
    rows_down = grad_rows(active_t, grad_ffn)
    shard_down = lax.psum_scatter(rows_down, "page", scatter_dimension=0, tiled=True)
    grad_hidden, grad_b_up, grad_first, grad_branch, grad_context, small_one = ffn_back(
        after(grad_ffn, rows_down), slope, grad_sum_two, unit, scale, vectors, full_rest, full_down
    )
    attend_in = grad_context
    if fast:
        tiles = grad_hidden.shape[1] // d_model
        pairs = [
            (context_t, False, grad_branch, 0, 1),
            (normed_t, False, grad_hidden, 0, tiles // 2),
        ]
        keep_a, send_a = grad_by_columns(pairs, place, d_model)
        partner_a = exchange(send_a, 1)
        pairs = [(normed_t, False, after(grad_hidden, send_a), tiles // 2, tiles - tiles // 2)]
        keep_b, send_b = grad_by_columns(pairs, place, d_model)
        partner_b = exchange(send_b, 1)
        held_a, plane_a = halve_plane(place, keep_a, after(partner_a, send_b))
        far_a = swap(plane_a)
        held_b, plane_b = halve_plane(place, keep_b, after(partner_b, plane_a))
        far_b = swap(plane_b)
        attend_in = after(grad_context, plane_a, plane_b)
    else:
        shard_rest = summed_rows([(context_t, grad_branch), (normed_t, grad_hidden)])
    grad_queries, grad_keys, grad_values, grad_tables = attend_back(
        bounds, queries, keys_values, attend_in, features, own_feats, own_flip, tables
    )
    grad_keys_in, grad_queries_in = grad_keys, grad_queries
    if fast:
        far_a, far_b = after((far_a, far_b), grad_queries)
        held_rest, across_out = halve_two(held_a, far_a, held_b, far_b)
        across_rest = exchange(across_out, 2)
        grad_queries_in = after(grad_queries, across_out)
    pairs = [
        (mixed_t, True, grad_queries_in, 0, 1),
        (mixed_t, False, grad_keys, 0, 1),
        (mixed_t, False, grad_values, 0, 1),
    ]
    if fast:
        keep_qkv, send_qkv = grad_by_columns(pairs, place, d_model)
        partner_qkv = exchange(send_qkv, 1)
        grad_keys_in = after(grad_keys, send_qkv)
    else:
        shard_down = shard_down.astype(f32) + swap(shard_down).astype(f32)
        shard_qkv = summed_rows(
            [(mixed_low.T, grad_queries), (mixed_t, grad_keys), (mixed_t, grad_values)]
        )
    to_other = input_back(place, full_qkv, grad_keys_in, grad_values, ())
    from_other = swap(to_other)
    grad_values_in = grad_values
    if fast:
        partner_qkv = after(partner_qkv, to_other)
        held_qkv, across_out = halve_across(place, keep_qkv, partner_qkv)
        across_qkv = exchange(across_out, 2)
        grad_values_in = after(grad_values, across_out)
    own_part = input_back(place, full_qkv, grad_keys, grad_values_in, (grad_first, grad_queries))
    packed = small_sums(
        own_part,
        to_other,
        own_low,
        other_low,
        masks,
        grad_queries,
        grad_values,
        small_one,
        small_two,
        grad_b_up,
        grad_tables,
    )
    if fast:
        packed = both_sum(packed, 1)
        shard_down = after(shard_down, packed)
        across_rest = after(across_rest, packed, shard_down)
        shard_down = shard_down.astype(f32) + swap(shard_down).astype(f32)
        own_rest, sends_rest = column_sends(held_rest, across_rest)
        arrived_rest = column_arrivals(sends_rest)
        packed = after(packed, *sends_rest)
        packed = packed + swap(packed)
        across_qkv = after(across_qkv, packed)
        own_qkv, sends_qkv = column_sends(held_qkv, across_qkv)
        arrived_qkv = column_arrivals(sends_qkv)
        from_other = after(from_other, *sends_qkv)
    else:
        packed = lax.psum(packed, ("mod", "page"))
    grad_in = state_back(own_part, from_other, masks, taps)
    if fast:
        arrived_rest = [after(part, grad_in) for part in arrived_rest]
        total_rest = column_total(own_rest, arrived_rest)
        far_rest = swap(total_rest)
        packed = both_sum(both_sum(after(packed, total_rest), 2), 4)
        arrived_qkv = [after(part, packed) for part in arrived_qkv]
        total_qkv = column_total(own_qkv, arrived_qkv)
        far_qkv = swap(total_qkv)
        packed = both_sum(after(packed, total_qkv), 8)
    g_tables = packed[28:34].reshape(HEADS, 3, LANES)
    if fast:
        cut = far_a.shape[2]
        first_plane = jnp.where(is_text, total_rest, far_rest)
        second_plane = jnp.where(is_text, far_rest, total_rest)
        shard_rest = jnp.concatenate(
            [first_plane[:, :cut], second_plane[:, :cut], first_plane[:, cut:], second_plane[:, cut:]],
            axis=1,
        ).astype(f32)
        shard_qkv = total_qkv.astype(f32) + far_qkv.astype(f32)
    return (
        output_row[None, None],
        grad_in[None, None],
        packed[0:3],
        packed[3],
        shard_qkv[:, :d_model],
        packed[4],
        shard_qkv[:, d_model : 2 * d_model],
        shard_qkv[:, 2 * d_model :],
        packed[5],
        shard_rest[:, :d_model],
        packed[10],
        g_tables[:, 0, : table_pos.shape[1]],
        g_tables[:, 1, 64 : 64 + table_x.shape[1]],
        g_tables[:, 2, 64 : 64 + table_y.shape[1]],
        packed[8],
        packed[9],
        shard_rest[:, d_model:],
        packed[24:28].reshape(d_ff),
        shard_down,
        packed[18],
        packed[16],
        packed[17],
    )


def solution(mesh):
    rows = P("mod", "page", None, None)
    ids = P("page", None)
    cut = P("page", None)
    return jax.shard_map(
        local,
        mesh=mesh,
        in_specs=(
            rows, rows, ids, ids, ids, P(), P(), cut, P(), cut, cut, P(), cut,
            P(), P(), P(), P(), P(), P(), cut, P(), cut, P(), P(), P(),
        ),
        out_specs=(
            rows, rows, P(), P(), cut, P(), cut, cut, P(), cut, P(), P(), P(),
            P(), P(), P(), cut, P(), cut, P(), P(), P(),
        ),
        check_vma=False,
    )
```

```python
import functools

import jax
import jax.numpy as jnp
import numpy as np
from jax import lax
from jax.experimental import pallas as pl
from jax.experimental.pallas import tpu as pltpu
from jax.sharding import PartitionSpec as P

HEADS = 12
HEAD = 64
GRID = 8
PAGES = 8
POS_BINS = 64
BOX_BINS = 32
PATCH = 64
TEXT = 512
PAIRS = HEADS // 2
LANES = 2 * HEAD
WINDOW = 144
SMALL = 80

dilation = 2
small_cost = pl.CostEstimate(flops=1000, bytes_accessed=1000, transcendentals=0)
norm_eps = 1e-05
mask_fill = -1000000000.0
erfc_poly = (
    0.2367515965428487,
    0.24062179898991767,
    0.18865103029313968,
    0.2877518531132804,
    -0.1648672439458568,
    0.4765735350541787,
    -0.34041833366480423,
    0.07493571514857543,
)
bf16 = jnp.bfloat16
f32 = jnp.float32


def shifted(values, offset, fill_value):
    padding = jnp.full((abs(offset),) + values.shape[1:], fill_value, values.dtype)
    if offset > 0:
        return jnp.concatenate([values[offset:], padding], axis=0)
    return jnp.concatenate([padding, values[:offset]], axis=0)


def dilated_mix(inputs, page_ids, conv_weight, conv_bias):
    summed = inputs + conv_bias + conv_weight[1] * inputs
    for tap_index, offset in ((0, -dilation), (2, dilation)):
        moved_rows = shifted(inputs, offset, 0.0)
        moved_pages = shifted(page_ids, offset, -1)
        same_page = (moved_pages == page_ids)[:, None]
        summed = summed + conv_weight[tap_index] * jnp.where(same_page, moved_rows, 0.0)
    return summed


def bin_features(pos_bins, bins_x, bins_y):
    return jnp.concatenate(
        [
            jax.nn.one_hot(pos_bins, POS_BINS, dtype=bf16),
            jax.nn.one_hot(bins_x, BOX_BINS, dtype=bf16),
            jax.nn.one_hot(bins_y, BOX_BINS, dtype=bf16),
        ],
        axis=1,
    )


def token_ids(text_pages, text_x, text_y):
    text_index = jnp.arange(TEXT, dtype=jnp.int32)
    text_pos = text_index * POS_BINS // TEXT
    patch_pos = text_index % PATCH * POS_BINS // PATCH
    patch_page = text_index // PATCH
    patch_x = text_index % GRID * BOX_BINS // GRID
    patch_y = text_index // GRID % GRID * BOX_BINS // GRID
    page_ids = jnp.stack([text_pages, patch_page])
    pos_bins = jnp.stack([text_pos, patch_pos])
    bins_x = jnp.stack([text_x, patch_x])
    bins_y = jnp.stack([text_y, patch_y])
    return (page_ids, pos_bins, bins_x, bins_y)


def plain_dot(left_side, right_side):
    return jnp.dot(left_side, right_side, preferred_element_type=f32)


def dot_left_t(left_side, right_side):
    return lax.dot_general(
        left_side, right_side, (((0,), (0,)), ((), ())), preferred_element_type=f32
    )


def dot_right_t(left_side, right_side):
    return lax.dot_general(
        left_side, right_side, (((1,), (1,)), ((), ())), preferred_element_type=f32
    )


def iota(shape, axis):
    return lax.broadcasted_iota(jnp.int32, shape, axis)


def bias_block(table_rows):
    pos_part = pltpu.roll(
        jnp.broadcast_to(table_rows[0:1], (POS_BINS, LANES)), 65, 1, stride=1, stride_axis=0
    )
    x_part = pltpu.roll(
        jnp.broadcast_to(table_rows[1:2], (BOX_BINS, LANES)), 33, 1, stride=1, stride_axis=0
    )
    y_part = pltpu.roll(
        jnp.broadcast_to(table_rows[2:3], (BOX_BINS, LANES)), 65, 1, stride=1, stride_axis=0
    )
    lane = iota((POS_BINS, LANES), 1)
    pos_part = jnp.where(lane < POS_BINS, pos_part, 0.0)
    lane = iota((BOX_BINS, LANES), 1)
    x_part = jnp.where((lane >= 64) & (lane < 96), x_part, 0.0)
    y_part = jnp.where(lane >= 96, y_part, 0.0)
    return jnp.concatenate([pos_part, x_part, y_part], axis=0).astype(bf16)


def diagonal_sums(grad_block):
    lane = iota((POS_BINS, LANES), 1)
    pos_part = jnp.where(lane < POS_BINS, grad_block[:64], 0.0)
    lane = iota((BOX_BINS, LANES), 1)
    x_part = jnp.where((lane >= 64) & (lane < 96), grad_block[64:96], 0.0)
    y_part = jnp.where(lane >= 96, grad_block[96:], 0.0)
    pos_part = pltpu.roll(pos_part, 0, 1, stride=1, stride_axis=0)
    x_part = pltpu.roll(x_part, 0, 1, stride=1, stride_axis=0)
    y_part = pltpu.roll(y_part, 96, 1, stride=1, stride_axis=0)
    rows = [jnp.sum(part, axis=0, keepdims=True) for part in (pos_part, x_part, y_part)]
    return jnp.concatenate(rows + [jnp.zeros((5, LANES), f32)], axis=0)


def stacked_heads(rows, low_lane):
    zero = jnp.zeros_like(rows)
    return jnp.concatenate(
        [jnp.where(low_lane, rows, zero), jnp.where(low_lane, zero, rows)], axis=0
    )


def window_start(first, window):
    return pl.multiple_of(jnp.minimum(first // 16 * 16, TEXT - window), 16)


def fits(first, end, window):
    return end - jnp.minimum(first // 16 * 16, TEXT - window) <= window


def for_each_page(bounds, step):
    def body(page, carry):
        own_low, own_high = bounds[page], bounds[PAGES + page]
        key_low, key_high = bounds[2 * PAGES + page], bounds[3 * PAGES + page]
        own_small = fits(own_low, own_high, SMALL)
        key_small = fits(key_low, key_high, SMALL)
        span = (own_low, own_high, key_low, key_high)
        small = own_small & key_small
        for chosen, own_window, key_window in (
            (small, SMALL, SMALL),
            (~small, WINDOW, WINDOW),
        ):

            @pl.when(chosen)
            def _():
                step(page, span, own_window, key_window)

        return carry

    lax.fori_loop(0, PAGES, body, 0)


def page_operands(page, span, own_window, key_window, pair, q_ref, k_ref, feat_ref, lookup):
    own_at = window_start(span[0], own_window)
    key_at = window_start(span[2], key_window)
    own_rows, text_rows = pl.ds(own_at, own_window), pl.ds(key_at, key_window)
    patch_at = TEXT + PATCH * page
    if not isinstance(page, int):
        patch_at = pl.multiple_of(patch_at, PATCH)
    patch_rows = pl.ds(patch_at, PATCH)
    lanes = slice(pair * LANES, (pair + 1) * LANES)
    low_lane = iota((own_window, LANES), 1) < HEAD
    queries = stacked_heads(q_ref[own_rows, lanes], low_lane)
    first = 2 * pair * LANES
    rel = jnp.concatenate(
        [
            lookup[own_rows, first : first + LANES],
            lookup[own_rows, first + LANES : first + 2 * LANES],
        ],
        axis=0,
    )
    query_side = jnp.concatenate([rel, queries], axis=1)
    key_side = jnp.concatenate(
        [
            jnp.concatenate([feat_ref[text_rows, :], k_ref[text_rows, lanes]], axis=1),
            jnp.concatenate([feat_ref[patch_rows, :], k_ref[patch_rows, lanes]], axis=1),
        ],
        axis=0,
    )
    own_row = iota((own_window, LANES), 0) + own_at
    own_ok = (own_row >= span[0]) & (own_row < span[1])
    return (
        lanes, low_lane, own_ok, queries, query_side, key_side, own_rows, text_rows, patch_rows, key_at
    )


def set_lookup(lookup, own_feat_ref, table_ref):
    blocks = [bias_block(table_ref[head]) for head in range(table_ref.shape[0])]
    product = jnp.dot(
        own_feat_ref[...], jnp.concatenate(blocks, axis=1), preferred_element_type=f32
    )
    lookup[...] = product.astype(bf16)


def attend_kernel(bounds, q_ref, k_ref, v_ref, feat_ref, own_feat_ref, table_ref, context_ref, lookup):
    set_lookup(lookup, own_feat_ref, table_ref)

    def step(page, span, own_window, key_window):
        column = iota((1, key_window + PATCH), 1)
        key_row = column + window_start(span[2], key_window)
        key_ok = (column >= key_window) | ((key_row >= span[2]) & (key_row < span[3]))
        for pair in range(q_ref.shape[1] // LANES):
            lanes, low_lane, own_ok, _, query_side, key_side, own_rows, text_rows, patch_rows, _ = (
                page_operands(
                    page, span, own_window, key_window, pair, q_ref, k_ref, feat_ref, lookup
                )
            )
            scores = jnp.where(key_ok, dot_right_t(query_side, key_side), mask_fill)
            row_max = jnp.max(scores, axis=1, keepdims=True)
            weights = jnp.exp(scores - row_max)
            total = jnp.sum(weights, axis=1, keepdims=True)
            prob = (weights * (1.0 / total)).astype(bf16)
            values = jnp.concatenate([v_ref[text_rows, lanes], v_ref[patch_rows, lanes]], axis=0)
            mixed = jnp.dot(prob, values, preferred_element_type=f32)
            picked = jnp.where(low_lane, mixed[:own_window], mixed[own_window:])
            before = context_ref[own_rows, lanes].astype(f32)
            context_ref[own_rows, lanes] = jnp.where(own_ok, picked, before).astype(bf16)

    for page in range(PAGES):
        span = [bounds[part * PAGES + page] for part in range(4)]
        step(page, span, WINDOW, WINDOW)


def attend_back_kernel(
    bounds,
    q_ref,
    k_ref,
    v_ref,
    grad_ref,
    feat_ref,
    own_feat_ref,
    flip_feat_ref,
    table_ref,
    grad_q_ref,
    grad_k_ref,
    grad_v_ref,
    grad_table_ref,
    lookup,
    grad_lookup,
):
    set_lookup(lookup, own_feat_ref, table_ref)

    def step(page, span, own_window, key_window):
        row = iota((key_window + PATCH, 1), 0)
        key_row = row + window_start(span[2], key_window)
        key_ok = (row >= key_window) | ((key_row >= span[2]) & (key_row < span[3]))
        for pair in range(q_ref.shape[1] // LANES):
            lanes, low_lane, own_ok, queries, query_side, key_side, own_rows, text_rows, patch_rows, key_at = (
                page_operands(
                    page, span, own_window, key_window, pair, q_ref, k_ref, feat_ref, lookup
                )
            )
            scores = jnp.where(key_ok, dot_right_t(key_side, query_side), mask_fill)
            col_max = jnp.max(scores, axis=0, keepdims=True)
            weights = jnp.exp(scores - col_max)
            total = jnp.sum(weights, axis=0, keepdims=True)
            prob = weights * (1.0 / total)
            grad_rows = grad_ref[own_rows, lanes]
            grad_rows = jnp.where(own_ok, grad_rows, jnp.zeros_like(grad_rows))
            grads = stacked_heads(grad_rows, low_lane)
            values = jnp.concatenate([v_ref[text_rows, lanes], v_ref[patch_rows, lanes]], axis=0)
            grad_prob = dot_right_t(values, grads)
            inner = jnp.sum(prob * grad_prob, axis=0, keepdims=True)
            grad_scores = (prob * (grad_prob - inner)).astype(bf16)
            grad_v = jnp.dot(prob.astype(bf16), grads, preferred_element_type=f32)
            grad_k = jnp.dot(grad_scores, queries, preferred_element_type=f32)
            back = dot_left_t(grad_scores, key_side)
            low, high = back[:own_window], back[own_window:]
            grad_q = jnp.where(low_lane, low[:, LANES:], high[:, LANES:]) * 0.125
            before = grad_q_ref[own_rows, lanes].astype(f32)
            grad_q_ref[own_rows, lanes] = jnp.where(own_ok, grad_q, before).astype(bf16)
            first = 2 * pair * LANES
            for part, at in ((low, first), (high, first + LANES)):
                place_at = slice(at, at + LANES)
                grad_lookup[own_rows, place_at] = jnp.where(
                    own_ok, part[:, :LANES], grad_lookup[own_rows, place_at]
                )
            wide_row = iota((key_window, LANES), 0) + key_at
            text_ok = (wide_row >= span[2]) & (wide_row < span[3])
            for grad, ref in ((grad_k, grad_k_ref), (grad_v, grad_v_ref)):
                before = ref[text_rows, lanes].astype(f32)
                ref[text_rows, lanes] = jnp.where(text_ok, grad[:key_window], before).astype(bf16)
                ref[patch_rows, lanes] = grad[key_window:].astype(bf16)

    for_each_page(bounds, step)
    grad_high = grad_lookup[...].astype(bf16)
    grad_rest = (grad_lookup[...] - grad_high.astype(f32)).astype(bf16)
    flip = flip_feat_ref[...]
    grad_block = dot_left_t(flip, grad_high) + dot_left_t(flip, grad_rest)
    for head in range(table_ref.shape[0]):
        grad_table_ref[head] = diagonal_sums(grad_block[:, head * LANES : (head + 1) * LANES])


def column_spec(rows, group, first=0):
    return pl.BlockSpec((rows, group * LANES), lambda step, bounds: (0, step + first))


def whole_spec(rows):
    return pl.BlockSpec((rows, LANES), lambda step, bounds: (0, 0))


def tables_spec(group):
    return pl.BlockSpec((2 * group, 8, LANES), lambda step, bounds: (step, 0, 0))


def attend(bounds, queries, keys_values, features, own_features, tables):
    group = 1
    return pl.pallas_call(
        attend_kernel,
        grid_spec=pltpu.PrefetchScalarGridSpec(
            num_scalar_prefetch=1,
            grid=(PAIRS // group,),
            in_specs=[
                column_spec(TEXT, group),
                column_spec(2 * TEXT, group),
                column_spec(2 * TEXT, group, PAIRS // group),
                whole_spec(2 * TEXT),
                whole_spec(TEXT),
                tables_spec(group),
            ],
            out_specs=column_spec(TEXT, group),
            scratch_shapes=[pltpu.VMEM((TEXT, 2 * group * LANES), bf16)],
        ),
        out_shape=jax.ShapeDtypeStruct((TEXT, HEADS * HEAD), bf16),
        cost_estimate=small_cost,
        name="attend",
    )(bounds, queries, keys_values, keys_values, features, own_features, tables)


def attend_back(
    bounds, queries, keys_values, grad_context, features, own_features, flip, tables
):
    group = 6
    return pl.pallas_call(
        attend_back_kernel,
        grid_spec=pltpu.PrefetchScalarGridSpec(
            num_scalar_prefetch=1,
            grid=(PAIRS // group,),
            in_specs=[
                column_spec(TEXT, group),
                column_spec(2 * TEXT, group),
                column_spec(2 * TEXT, group, PAIRS // group),
                column_spec(TEXT, group),
                whole_spec(2 * TEXT),
                whole_spec(TEXT),
                whole_spec(TEXT),
                tables_spec(group),
            ],
            out_specs=[
                column_spec(TEXT, group),
                column_spec(2 * TEXT, group),
                column_spec(2 * TEXT, group),
                tables_spec(group),
            ],
            scratch_shapes=[
                pltpu.VMEM((TEXT, 2 * group * LANES), bf16),
                pltpu.VMEM((TEXT, 2 * group * LANES), f32),
            ],
        ),
        out_shape=[
            jax.ShapeDtypeStruct((TEXT, HEADS * HEAD), bf16),
            jax.ShapeDtypeStruct((2 * TEXT, HEADS * HEAD), bf16),
            jax.ShapeDtypeStruct((2 * TEXT, HEADS * HEAD), bf16),
            jax.ShapeDtypeStruct((HEADS, 8, LANES), f32),
        ],
        cost_estimate=small_cost,
        name="attend_back",
    )(
        bounds,
        queries,
        keys_values,
        keys_values,
        grad_context,
        features,
        own_features,
        flip,
        tables,
    )


def exchange(values, mask):
    count = lax.axis_size("page")
    return lax.ppermute(values, "page", [(i, i ^ mask) for i in range(count)])


def after(value, *earlier):
    return lax.optimization_barrier((value, *earlier))[0]


def slot_mask(slot):
    return (slot & 3) * 4 + (slot >> 2) * 2


def project_kernel(groups, place, mixed_ref, bias_ref, *refs):
    *pieces, query_ref, both_ref, weight_ref, mixed_t_ref, sems = refs
    width = mixed_ref.shape[1]
    tokens = query_ref.shape[0]
    copies = start_rows(place, groups, pieces, weight_ref, sems)
    mixed_t_ref[...] = mixed_ref[...].T
    for copy in copies:
        copy.wait()
    own = mixed_ref[pl.ds(pl.multiple_of(place[1] * tokens, 16), tokens), :]
    queries = jnp.dot(own, weight_ref[:, :width], preferred_element_type=f32) + bias_ref[:, :width]
    query_ref[...] = (queries.astype(bf16).astype(f32) * 0.125).astype(bf16)
    for part in range(2):
        rows = pl.ds(part * tokens, tokens)
        for column in (1, 2):
            at = slice(column * width, (column + 1) * width)
            out = slice((column - 1) * width, column * width)
            values = jnp.dot(mixed_ref[rows, :], weight_ref[:, at], preferred_element_type=f32)
            both_ref[rows, out] = (values + bias_ref[:, at]).astype(bf16)


def project(place, mixed, biases, groups, pieces):
    rows, width = mixed.shape
    vmem = pl.BlockSpec(memory_space=pltpu.VMEM)
    return pl.pallas_call(
        functools.partial(project_kernel, groups),
        grid_spec=pltpu.PrefetchScalarGridSpec(
            num_scalar_prefetch=1,
            grid=(),
            in_specs=[vmem] * 2 + any_specs(len(pieces)),
            out_specs=[vmem] * 4,
            scratch_shapes=[pltpu.SemaphoreType.DMA((32,))],
        ),
        out_shape=[
            jax.ShapeDtypeStruct((rows // 2, width), bf16),
            jax.ShapeDtypeStruct((rows, 2 * width), bf16),
            jax.ShapeDtypeStruct((width, 3 * width), bf16),
            jax.ShapeDtypeStruct((width, rows), bf16),
        ],
        cost_estimate=small_cost,
        compiler_params=pltpu.CompilerParams(vmem_limit_bytes=16 << 20),
        name="project",
    )(place, mixed, biases, *pieces)


def column_parts(shard):
    return [shard] + [exchange(shard, 4 * step) for step in (1, 2, 3)]


def half_pieces(column):
    eight = jnp.concatenate([column, exchange(column, 2)])
    far = swap(eight)
    return [eight, exchange(eight, 1), far, exchange(far, 1)]


def row_pieces(column, across):
    return [column, exchange(column, 1), across, exchange(across, 1)]


def column_pairs(shard):
    far = exchange(shard, 8)
    near = exchange(jnp.stack([shard, far]), 4)
    return [shard, near[0], far, near[1]]


def column_of(shard):
    return jnp.stack(column_parts(shard))


def row_copies(place, groups, refs, full, sems, first=0):
    copies = []
    for kind, column in groups:
        if kind == "full":
            piece, *refs = refs
            width = piece.shape[1]
            target = full.at[:, pl.ds(column, width)]
            copies.append(pltpu.make_async_copy(piece, target, sems.at[first + len(copies)]))
            continue
        pieces, refs = refs[:4], refs[4:]
        _, rows, width = pieces[0].shape
        for index in range(32 if kind == "halves" else 16):
            at = column
            if kind == "halves":
                source, slot = index >> 3, index & 7
                mask = slot_mask(slot) + (source & 1)
                at = pl.multiple_of(column + (place[1] ^ (source >> 1)) * width, 128)
            else:
                source, slot = index & 3, index >> 2
                mask = slot * 4 + source
            row = pl.multiple_of((place[0] ^ mask) * rows, 16)
            copies.append(
                pltpu.make_async_copy(
                    pieces[source].at[slot],
                    full.at[pl.ds(row, rows), pl.ds(at, width)],
                    sems.at[first + len(copies)],
                )
            )
    return copies


def start_rows(place, groups, refs, full, sems):
    copies = row_copies(place, groups, refs, full, sems)
    for copy in copies:
        copy.start()
    return copies


def gelu_parts(values):
    size = jnp.abs(values)
    t = 1.0 / (1.0 + (0.42 * 0.7071067811865476) * size)
    poly = jnp.full_like(t, erfc_poly[-1])
    for coefficient in erfc_poly[-2::-1]:
        poly = poly * t + coefficient
    bell = jnp.exp(-0.5 * values * values)
    tail = (0.5 * t) * (poly * bell)
    cdf = jnp.where(values >= 0.0, 1.0 - tail, tail)
    return values * cdf, cdf + (values * 0.3989422804014327) * bell


def normalized(values):
    centered = values - jnp.mean(values, axis=1, keepdims=True)
    variance = jnp.mean(centered * centered, axis=1, keepdims=True)
    scale = lax.rsqrt(variance + norm_eps)
    return centered * scale, scale


def norm_back(grads, unit, scale, gain):
    scaled = grads * gain
    mean = jnp.mean(scaled, axis=1, keepdims=True)
    inner = jnp.mean(scaled * unit, axis=1, keepdims=True)
    return scale * (scaled - mean - unit * inner)


def up_kernel(groups, place, context_ref, mixed_ref, vec_ref, bias_ref, *refs):
    *pieces, unit_ref, scale_ref, low_ref, low_t_ref, context_t_ref = refs[:-9]
    active_ref, active_t_ref, slope_ref, full_ref = refs[-9:-5]
    weight, hidden, low, sems, full_sem = refs[-5:]
    step = pl.program_id(0)
    tiles = pl.num_programs(0) - 1
    width = context_ref.shape[1]
    tile = active_ref.shape[1]
    last_group = 16 if len(groups) > 1 else 0

    def full_copy():
        return pltpu.make_async_copy(weight, full_ref, full_sem)

    @pl.when(step == 0)
    def _():
        copies = row_copies(place, groups, pieces, weight, sems)
        for copy in copies:
            copy.start()
        context_t_ref[...] = context_ref[...].T
        for copy in copies[: len(copies) - last_group]:
            copy.wait()
        branch = jnp.dot(context_ref[...], weight[:, :width], preferred_element_type=f32)
        unit, scale = normalized(mixed_ref[...] + branch + vec_ref[0:1])
        unit_ref[...] = unit
        scale_ref[...] = jnp.broadcast_to(scale, scale_ref.shape)
        normed = (unit * vec_ref[1:2] + vec_ref[2:3]).astype(bf16)
        low[...] = normed
        low_ref[...] = normed
        low_t_ref[...] = normed.T

    @pl.when(step == 1)
    def _():
        if last_group:
            for copy in row_copies(place, groups[1:], pieces[4:], weight, sems, 32):
                copy.wait()
        full_copy().start()

    def product():
        at = pl.multiple_of(width + step * tile, 128)
        return jnp.dot(low[...], weight[:, pl.ds(at, tile)], preferred_element_type=f32)

    def activate():
        active, slope = gelu_parts(hidden[(step + 1) % 2] + bias_ref[...])
        active = active.astype(bf16)
        active_ref[...] = active
        active_t_ref[...] = active.T
        slope_ref[...] = slope.astype(bf16)

    @pl.when(step == 0)
    def _():
        hidden[step % 2] = product()

    @pl.when((step > 0) & (step < tiles))
    def _():
        hidden[step % 2] = product()
        activate()

    @pl.when(step == tiles)
    def _():
        activate()
        full_copy().wait()


def any_specs(count):
    return [pl.BlockSpec(memory_space=pl.ANY)] * count


def up_forward(place, context, mixed, vectors, bias_up, groups, pieces):
    tokens, width = mixed.shape
    hidden_width = bias_up.shape[1]
    tile = 768
    whole = lambda step, place: (0, 0)
    last = lambda step, place: (0, jnp.maximum(step - 1, 0))
    last_t = lambda step, place: (jnp.maximum(step - 1, 0), 0)
    return pl.pallas_call(
        functools.partial(up_kernel, groups),
        grid_spec=pltpu.PrefetchScalarGridSpec(
            num_scalar_prefetch=1,
            grid=(hidden_width // tile + 1,),
            in_specs=[
                pl.BlockSpec((tokens, width), whole),
                pl.BlockSpec((tokens, width), whole),
                pl.BlockSpec(vectors.shape, whole),
                pl.BlockSpec((1, tile), last),
            ]
            + any_specs(len(pieces)),
            out_specs=[
                pl.BlockSpec((tokens, width), whole),
                pl.BlockSpec((tokens, 128), whole),
                pl.BlockSpec((tokens, width), whole),
                pl.BlockSpec((width, tokens), whole),
                pl.BlockSpec((width, tokens), whole),
                pl.BlockSpec((tokens, tile), last),
                pl.BlockSpec((tile, tokens), last_t),
                pl.BlockSpec((tokens, tile), last),
                pl.BlockSpec(memory_space=pl.ANY),
            ],
            scratch_shapes=[
                pltpu.VMEM((width, width + hidden_width), bf16),
                pltpu.VMEM((2, tokens, tile), f32),
                pltpu.VMEM((tokens, width), bf16),
                pltpu.SemaphoreType.DMA((48,)),
                pltpu.SemaphoreType.DMA,
            ],
        ),
        out_shape=[
            jax.ShapeDtypeStruct((tokens, width), f32),
            jax.ShapeDtypeStruct((tokens, 128), f32),
            jax.ShapeDtypeStruct((tokens, width), bf16),
            jax.ShapeDtypeStruct((width, tokens), bf16),
            jax.ShapeDtypeStruct((width, tokens), bf16),
            jax.ShapeDtypeStruct((tokens, hidden_width), bf16),
            jax.ShapeDtypeStruct((hidden_width, tokens), bf16),
            jax.ShapeDtypeStruct((tokens, hidden_width), bf16),
            jax.ShapeDtypeStruct((width, width + hidden_width), bf16),
        ],
        cost_estimate=small_cost,
        name="up_forward",
    )(place, context, mixed, vectors, bias_up, *pieces)


def down_kernel(active_ref, weight_ref, unit_ref, vec_ref, grad_ref, *refs):
    out_ref, sum_ref, low_ref, small_ref, total = refs
    step = pl.program_id(0)
    product = jnp.dot(active_ref[...], weight_ref[...], preferred_element_type=f32)

    @pl.when(step == 0)
    def _():
        total[...] = product

    @pl.when(step > 0)
    def _():
        total[...] += product

    @pl.when(step == pl.num_programs(0) - 1)
    def _():
        tokens, width = unit_ref.shape
        half = tokens // 2
        smalls = [jnp.zeros((1, width), f32)] * 3
        for part in range(2):
            rows = pl.ds(part * half, half)
            normed = unit_ref[rows, :] * vec_ref[1:2] + vec_ref[2:3]
            unit, scale = normalized(normed + total[rows, :] + vec_ref[3:4])
            out_ref[rows, :] = (unit * vec_ref[4:5] + vec_ref[5:6]).astype(bf16)
            grads = grad_ref[rows, :].astype(f32)
            back = norm_back(grads, unit, scale, vec_ref[4:5])
            low = back.astype(bf16)
            sum_ref[rows, :] = back
            low_ref[rows, :] = low
            for index, term in enumerate((grads * unit, grads, low.astype(f32))):
                smalls[index] = smalls[index] + jnp.sum(term, axis=0, keepdims=True)
        small_ref[...] = jnp.concatenate(smalls + [jnp.zeros((5, width), f32)], axis=0)


def down_forward(active, weight, unit, vectors, grads):
    tokens, width = unit.shape
    hidden_width = active.shape[1]
    tile = 1536
    whole = lambda step: (0, 0)
    token_block = pl.BlockSpec((tokens, width), whole)
    return pl.pallas_call(
        down_kernel,
        grid=(hidden_width // tile,),
        in_specs=[
            pl.BlockSpec((tokens, tile), lambda step: (0, step)),
            pl.BlockSpec((tile, width), lambda step: (step, 0)),
            token_block,
            pl.BlockSpec(vectors.shape, whole),
            token_block,
        ],
        out_specs=[token_block] * 3 + [pl.BlockSpec((8, width), whole)],
        scratch_shapes=[pltpu.VMEM((tokens, width), f32)],
        out_shape=[
            jax.ShapeDtypeStruct((tokens, width), bf16),
            jax.ShapeDtypeStruct((tokens, width), f32),
            jax.ShapeDtypeStruct((tokens, width), bf16),
            jax.ShapeDtypeStruct((8, width), f32),
        ],
        cost_estimate=small_cost,
        name="down_forward",
    )(active, weight, unit, vectors, grads)


def ffn_back_kernel(*refs):
    low_ref, slope_ref, sum_ref, unit_ref, scale_ref, vec_ref = refs[:6]
    down_ref, up_ref, out_weight_ref = refs[6:9]
    hidden_ref, bias_ref, first_ref, branch_ref, context_ref, small_ref, total = refs[9:]
    step = pl.program_id(0)
    tokens, width = unit_ref.shape
    tile = slope_ref.shape[1]
    half = tokens // 2

    @pl.when(step == 0)
    def _():
        total[...] = sum_ref[...]

    bias = jnp.zeros((1, tile), f32)
    for part in range(2):
        rows = pl.ds(part * half, half)
        grads = dot_right_t(low_ref[rows, :], down_ref[...]) * slope_ref[rows, :].astype(f32)
        grads = grads.astype(bf16)
        hidden_ref[rows, :] = grads
        bias = bias + jnp.sum(grads.astype(f32), axis=0, keepdims=True)
        total[rows, :] += dot_right_t(grads, up_ref[...])
    bias_ref[...] = bias

    @pl.when(step == pl.num_programs(0) - 1)
    def _():
        grads = total[...]
        unit = unit_ref[...]
        first = norm_back(grads, unit, scale_ref[:, 0:1], vec_ref[1:2])
        branch = first.astype(bf16)
        first_ref[...] = first
        branch_ref[...] = branch
        context_ref[...] = dot_right_t(branch, out_weight_ref[...]).astype(bf16)
        smalls = [
            jnp.sum(term, axis=0, keepdims=True)
            for term in (grads * unit, grads, branch.astype(f32))
        ]
        small_ref[...] = jnp.concatenate(smalls + [jnp.zeros((5, width), f32)], axis=0)


def ffn_back(low, slope, total, unit, scale, vectors, full_rest, full_down):
    tokens, width = unit.shape
    hidden_width = slope.shape[1]
    tile = 768
    whole = lambda step: (0, 0)
    column = lambda step: (0, step)
    token_block = pl.BlockSpec((tokens, width), whole)
    return pl.pallas_call(
        ffn_back_kernel,
        grid=(hidden_width // tile,),
        in_specs=[
            token_block,
            pl.BlockSpec((tokens, tile), column),
            token_block,
            token_block,
            pl.BlockSpec((tokens, 128), whole),
            pl.BlockSpec(vectors.shape, whole),
            pl.BlockSpec((tile, width), lambda step: (step, 0)),
            pl.BlockSpec((width, tile), lambda step: (0, step + 1)),
            pl.BlockSpec((width, width), whole),
        ],
        out_specs=[
            pl.BlockSpec((tokens, tile), column),
            pl.BlockSpec((1, tile), column),
            token_block,
            token_block,
            token_block,
            pl.BlockSpec((8, width), whole),
        ],
        scratch_shapes=[pltpu.VMEM((tokens, width), f32)],
        out_shape=[
            jax.ShapeDtypeStruct((tokens, hidden_width), bf16),
            jax.ShapeDtypeStruct((1, hidden_width), f32),
            jax.ShapeDtypeStruct((tokens, width), f32),
            jax.ShapeDtypeStruct((tokens, width), bf16),
            jax.ShapeDtypeStruct((tokens, width), bf16),
            jax.ShapeDtypeStruct((8, width), f32),
        ],
        cost_estimate=small_cost,
        name="ffn_back",
    )(low, slope, total, unit, scale, vectors, full_down, full_rest, full_rest)


def grad_rows_kernel(x_ref, h_ref, out_ref):
    out_ref[...] = jnp.dot(x_ref[...], h_ref[...], preferred_element_type=f32).astype(bf16)


def grad_rows(inputs_t, grads):
    width, tokens = inputs_t.shape
    columns = grads.shape[1]
    return pl.pallas_call(
        grad_rows_kernel,
        grid=(4,),
        in_specs=[
            pl.BlockSpec((width // 4, tokens), lambda step: (step, 0)),
            pl.BlockSpec((tokens, columns), lambda step: (0, 0)),
        ],
        out_specs=pl.BlockSpec((width // 4, columns), lambda step: (step, 0)),
        out_shape=jax.ShapeDtypeStruct((width, columns), bf16),
        cost_estimate=small_cost,
        name="grad_rows",
    )(inputs_t, grads)


def grad_columns_kernel(parts, place, *refs):
    count = len(parts)
    ins, keep_ref, send_ref, scratch = (
        refs[: 2 * count],
        refs[2 * count],
        refs[2 * count + 1],
        refs[2 * count + 2 :],
    )
    rows, tile = keep_ref.shape[1], keep_ref.shape[2]
    step = pl.program_id(0)
    first = 0
    for index, steps in enumerate(parts):
        x_ref, h_ref, ordered = ins[2 * index], ins[2 * index + 1], scratch[index]

        @pl.when(step == first)
        def _():
            for slot in range(16):
                mask = slot_mask(slot & 7) + (slot >> 3)
                at = pl.multiple_of((place[0] ^ mask) * rows, 16)
                ordered[pl.ds(slot * rows, rows), :] = x_ref[pl.ds(at, rows), :]

        @pl.when((step >= first) & (step < first + steps))
        def _():
            product = jnp.dot(ordered[...], h_ref[...], preferred_element_type=f32).astype(bf16)
            keep_ref[...] = product[: 8 * rows].reshape(8, rows, tile)
            send_ref[...] = product[8 * rows :].reshape(8, rows, tile)

        first = first + steps


def grad_by_columns(pairs, place, tile):
    width = pairs[0][0].shape[0]
    rows = width // 16
    parts = tuple(count for *_, count in pairs)
    steps = sum(parts)
    specs = []
    operands = []
    scratch = []
    first = 0
    for inputs_t, own, grads, start, count in pairs:
        tokens = grads.shape[0]
        block = (lambda step, place: (0, place[1])) if own else (lambda step, place: (0, 0))
        specs.append(pl.BlockSpec((width, tokens), block))

        def column(step, place, first=first, start=start, count=count):
            return (0, start + jnp.clip(step - first, 0, count - 1))

        specs.append(pl.BlockSpec((tokens, tile), column))
        operands += [inputs_t, grads]
        scratch.append(pltpu.VMEM((width, tokens), bf16))
        first = first + count
    half = jax.ShapeDtypeStruct((8, rows, steps * tile), bf16)
    return pl.pallas_call(
        functools.partial(grad_columns_kernel, parts),
        grid_spec=pltpu.PrefetchScalarGridSpec(
            num_scalar_prefetch=1,
            grid=(steps,),
            in_specs=specs,
            out_specs=[pl.BlockSpec((8, rows, tile), lambda step, place: (0, 0, step))] * 2,
            scratch_shapes=scratch,
        ),
        out_shape=[half, half],
        cost_estimate=small_cost,
        compiler_params=pltpu.CompilerParams(vmem_limit_bytes=16 << 20),
        name="grad_columns",
    )(place, *operands)


def key_back_kernel(place, gk_ref, gv_ref, wk_ref, wv_ref, out_ref):
    total = dot_right_t(gk_ref[...], wk_ref[...]) + dot_right_t(gv_ref[...], wv_ref[...])
    out_ref[...] = total.astype(out_ref.dtype)


def own_back_kernel(place, first_ref, gq_ref, gk_ref, gv_ref, wq_ref, wk_ref, wv_ref, out_ref):
    total = dot_right_t(gk_ref[...], wk_ref[...]) + dot_right_t(gv_ref[...], wv_ref[...])
    out_ref[...] = first_ref[...] + total + dot_right_t(gq_ref[...], wq_ref[...])


def input_back(place, weights, grad_keys, grad_values, others):
    width = weights.shape[0]
    tokens = grad_keys.shape[0] // 2
    whole = pl.BlockSpec((tokens, width), lambda step, place: (0, 0))
    row = lambda step, place: ((place[1] if others else 1 - place[1]), 0)
    if others:
        kernel, leading, first, dtype = own_back_kernel, [whole, whole], 0, f32
    else:
        kernel, leading, first, dtype = key_back_kernel, [], 1, bf16
    operands = list(others) + [grad_keys, grad_values] + [weights] * (3 - first)
    specs = [pl.BlockSpec((tokens, width), row)] * 2
    for block in range(first, 3):
        specs.append(pl.BlockSpec((width, width), lambda step, place, block=block: (0, block)))
    return pl.pallas_call(
        kernel,
        grid_spec=pltpu.PrefetchScalarGridSpec(
            num_scalar_prefetch=1, grid=(1,), in_specs=leading + specs, out_specs=whole
        ),
        out_shape=jax.ShapeDtypeStruct((tokens, width), dtype),
        cost_estimate=small_cost,
        compiler_params=pltpu.CompilerParams(vmem_limit_bytes=16 << 20),
        name="input_back",
    )(place, *operands)


def back_rows(values, mask):
    return jnp.where(mask, pltpu.roll(values, dilation, 0), 0.0)


def ahead_rows(values, mask):
    return jnp.where(mask, pltpu.roll(values, values.shape[0] - dilation, 0), 0.0)


def tap_sums(grads, inputs, ahead, back):
    terms = (grads * back_rows(inputs, back), grads * inputs, grads * ahead_rows(inputs, ahead), grads)
    return [jnp.sum(term, axis=0, keepdims=True) for term in terms]


def small_sums_kernel(
    own_ref, other_ref, x_ref, x_other_ref, mask_ref, gq_ref, gv_ref, one_ref, two_ref, up_ref, table_ref, out_ref
):
    width = own_ref.shape[1]
    mask = mask_ref[...] > 0.0
    own = tap_sums(own_ref[...], x_ref[...].astype(f32), mask[:, 0:1], mask[:, 1:2])
    other = tap_sums(
        other_ref[...].astype(f32), x_other_ref[...].astype(f32), mask[:, 2:3], mask[:, 3:4]
    )
    rows = [a + b for a, b in zip(own, other)]
    for ref in (gq_ref, gv_ref):
        rows.append(jnp.sum(ref[...].astype(f32), axis=0, keepdims=True))
    rows.append(jnp.zeros((2, width), f32))
    out_ref[0:8] = jnp.concatenate(rows, axis=0)
    out_ref[8:16] = one_ref[...]
    out_ref[16:24] = two_ref[...]
    count = up_ref.shape[1] // width
    for index in range(count):
        out_ref[24 + index : 25 + index] = up_ref[:, index * width : (index + 1) * width]
    for index in range(3 * HEADS):
        row, lane = 28 + index // 6, index % 6 * LANES
        table = table_ref[index // 3]
        out_ref[row : row + 1, lane : lane + LANES] = table[index % 3 : index % 3 + 1]
    out_ref[34:40] = jnp.zeros((6, width), f32)


def small_sums(*operands):
    return pl.pallas_call(
        small_sums_kernel,
        out_shape=jax.ShapeDtypeStruct((40, operands[0].shape[1]), f32),
        cost_estimate=small_cost,
        compiler_params=pltpu.CompilerParams(vmem_limit_bytes=24 << 20),
        name="small_sums",
    )(*operands)


def state_back_kernel(own_ref, other_ref, mask_ref, tap_ref, out_ref):
    grads = own_ref[...] + other_ref[...].astype(f32)
    mask = mask_ref[...] > 0.0
    total = grads + tap_ref[1:2] * grads
    total = total + tap_ref[0:1] * ahead_rows(grads, mask[:, 0:1])
    total = total + tap_ref[2:3] * back_rows(grads, mask[:, 1:2])
    out_ref[...] = total.astype(bf16)


def state_back(own, other, masks, taps):
    return pl.pallas_call(
        state_back_kernel,
        out_shape=jax.ShapeDtypeStruct(own.shape, bf16),
        cost_estimate=small_cost,
        compiler_params=pltpu.CompilerParams(vmem_limit_bytes=20 << 20),
        name="state_back",
    )(own, other, masks, taps)


def first_half_kernel(place, keep_near, part_near, keep_far, part_far, held_ref, out_ref):
    held_ref[...] = keep_near[...].astype(f32) + part_near[...].astype(f32)
    out_ref[...] = (keep_far[...].astype(f32) + part_far[...].astype(f32)).astype(bf16)


def halve_call(place, keep, partner, specs, half_shape, steps):
    near, far, out = specs
    return pl.pallas_call(
        first_half_kernel,
        grid_spec=pltpu.PrefetchScalarGridSpec(
            num_scalar_prefetch=1,
            grid=(steps,),
            in_specs=[near, near, far, far],
            out_specs=[out, out],
        ),
        out_shape=[
            jax.ShapeDtypeStruct(half_shape, f32),
            jax.ShapeDtypeStruct(half_shape, bf16),
        ],
        cost_estimate=small_cost,
        compiler_params=pltpu.CompilerParams(vmem_limit_bytes=12 << 20),
        name="halve",
    )(place, keep, partner, keep, partner)


def halve_across(place, keep, partner):
    _, rows, width = keep.shape
    near = pl.BlockSpec((1, rows, width), lambda step, place: (step, 0, 0))
    far = pl.BlockSpec((1, rows, width), lambda step, place: (step + 4, 0, 0))
    return halve_call(place, keep, partner, (near, far, near), (4, rows, width), 4)


def halve_plane(place, keep, partner):
    _, rows, width = keep.shape
    block = (2, rows, width // 2)
    near = pl.BlockSpec(block, lambda step, place: (step, 0, place[1]))
    far = pl.BlockSpec(block, lambda step, place: (step, 0, 1 - place[1]))
    out = pl.BlockSpec(block, lambda step, place: (step, 0, 0))
    return halve_call(place, keep, partner, (near, far, out), (8, rows, width // 2), 4)


def two_kernel(near_a, far_a, near_b, far_b, *refs):
    *partners, held_ref, out_ref = refs
    split = near_a.shape[2]
    for index, (near, far) in enumerate(((near_a, far_a), (near_b, far_b))):
        lanes = slice(0, split) if index == 0 else slice(split, None)
        part_near, part_far = partners[2 * index], partners[2 * index + 1]
        held_ref[:, :, lanes] = near[...] + part_near[...].astype(f32)
        out_ref[:, :, lanes] = (far[...] + part_far[...].astype(f32)).astype(bf16)


def halve_two(held_a, part_a, held_b, part_b):
    _, rows, width_a = held_a.shape
    width_b = held_b.shape[2]
    specs = []
    for width in (width_a, width_b):
        block = (1, rows, width)
        specs.append(pl.BlockSpec(block, lambda step: (step, 0, 0)))
        specs.append(pl.BlockSpec(block, lambda step: (step + 4, 0, 0)))
    out = pl.BlockSpec((1, rows, width_a + width_b), lambda step: (step, 0, 0))
    shape = (4, rows, width_a + width_b)
    return pl.pallas_call(
        two_kernel,
        grid=(4,),
        in_specs=specs * 2,
        out_specs=[out, out],
        out_shape=[jax.ShapeDtypeStruct(shape, f32), jax.ShapeDtypeStruct(shape, bf16)],
        cost_estimate=small_cost,
        compiler_params=pltpu.CompilerParams(vmem_limit_bytes=12 << 20),
        name="halve_two",
    )(held_a, held_a, held_b, held_b, part_a, part_a, part_b, part_b)


def column_kernel(held_ref, across_ref, own_ref, *sends):
    own_ref[...] = held_ref[0] + across_ref[0].astype(f32)
    for step, send in enumerate(sends, 1):
        send[...] = (held_ref[step] + across_ref[step].astype(f32)).astype(bf16)


def column_sends(held, across):
    _, rows, width = held.shape
    tile = 384
    out = pl.BlockSpec((rows, tile), lambda step: (0, step))
    block = pl.BlockSpec((4, rows, tile), lambda step: (0, 0, step))
    own, *sends = pl.pallas_call(
        column_kernel,
        grid=(width // tile,),
        in_specs=[block, block],
        out_specs=[out] * 4,
        out_shape=[jax.ShapeDtypeStruct((rows, width), f32)]
        + [jax.ShapeDtypeStruct((rows, width), bf16)] * 3,
        cost_estimate=small_cost,
        compiler_params=pltpu.CompilerParams(vmem_limit_bytes=12 << 20),
        name="column_sends",
    )(held, across)
    return own, sends


def column_arrivals(sends):
    return [exchange(send, 4 * step) for step, send in enumerate(sends, 1)]


def column_total(own, arrived):
    total = own
    for part in arrived:
        total = total + part.astype(f32)
    return total.astype(bf16)


def half_columns(values, first):
    half = values.shape[-1] // 2
    return jnp.where(first, values[..., :half], values[..., half:])


def summed_rows(pairs):
    grads = jnp.concatenate([plain_dot(*pair).astype(bf16) for pair in pairs], axis=1)
    shard = lax.psum_scatter(grads, "page", scatter_dimension=0, tiled=True)
    return shard.astype(f32) + swap(shard).astype(f32)


def page_bounds(segments, is_text):
    pages = jnp.arange(PAGES, dtype=jnp.int32)
    low = jnp.sum(segments[None, :] < pages[:, None], axis=1, dtype=jnp.int32)
    high = jnp.sum(segments[None, :] <= pages[:, None], axis=1, dtype=jnp.int32)
    own_low = jnp.where(is_text, low, pages * PATCH)
    own_high = jnp.where(is_text, high, (pages + 1) * PATCH)

    return jnp.concatenate([own_low, own_high, low, high])


def both_sum(values, mask):
    return values + exchange(values, mask)


def swap(values):
    return lax.ppermute(values, "mod", [(0, 1), (1, 0)])


def local(
    states,
    cotangent,
    segments,
    box_x,
    box_y,
    conv_weight,
    conv_bias,
    w_query,
    b_query,
    w_key,
    w_value,
    b_value,
    w_out,
    b_out,
    table_pos,
    table_x,
    table_y,
    gain_one,
    bias_one,
    w_up,
    b_up,
    w_down,
    b_down,
    gain_two,
    bias_two,
):
    is_text = lax.axis_index("mod") == 0
    d_model = states.shape[3]
    own_low = states[0, 0]
    rows_each = w_query.shape[0]
    d_ff = w_up.shape[1]
    fast = lax.axis_size("page") == 16 and rows_each % 16 == 0 and w_down.shape[0] % 16 == 0
    place = jnp.stack([lax.axis_index("page"), lax.axis_index("mod")]).astype(jnp.int32)
    pack_qkv = jnp.concatenate([w_query, w_key, w_value], axis=1)
    pack_rest = jnp.concatenate([w_out, w_up], axis=1)
    other_low = swap(own_low)
    if fast:
        column_qkv = column_of(half_columns(pack_qkv, is_text))
        table_pos, table_x, table_y, b_out, b_down, b_query, b_value, b_up = after(
            (table_pos, table_x, table_y, b_out, b_down, b_query, b_value, b_up), column_qkv
        )
        gain_one, bias_one, gain_two, bias_two, conv_weight = after(
            (gain_one, bias_one, gain_two, bias_two, conv_weight), column_qkv
        )
        segments, box_x, box_y = after((segments, box_x, box_y), column_qkv)
    page_ids, pos_bins, bins_x, bins_y = token_ids(segments[0], box_x[0], box_y[0])
    bounds = page_bounds(segments[0], is_text)
    own_pages = jnp.where(is_text, page_ids[0], page_ids[1])
    features = bin_features(pos_bins.reshape(-1), bins_x.reshape(-1), bins_y.reshape(-1))
    flipped = bin_features(
        POS_BINS - 1 - pos_bins.reshape(-1),
        BOX_BINS - 1 - bins_x.reshape(-1),
        BOX_BINS - 1 - bins_y.reshape(-1),
    )
    own_feats = jnp.where(is_text, features[:TEXT], features[TEXT:])
    own_flip = jnp.where(is_text, flipped[:TEXT], flipped[TEXT:])
    tables = jnp.stack(
        [
            jnp.pad(table_pos, ((0, 0), (0, LANES - table_pos.shape[1]))),
            jnp.pad(table_x, ((0, 0), (0, LANES - table_x.shape[1]))),
            jnp.pad(table_y, ((0, 0), (0, LANES - table_y.shape[1]))),
        ],
        axis=1,
    )
    tables = jnp.pad(tables, ((0, 0), (0, 5), (0, 0)))

    own_states = own_low.astype(f32)
    mixed = dilated_mix(own_states, own_pages, conv_weight, conv_bias)
    mixed_low = mixed.astype(bf16)
    other_pages = jnp.where(is_text, page_ids[1], page_ids[0])
    masks = jnp.pad(
        jnp.stack(
            [
                own_pages == shifted(own_pages, dilation, -1),
                own_pages == shifted(own_pages, -dilation, -1),
                other_pages == shifted(other_pages, dilation, -1),
                other_pages == shifted(other_pages, -dilation, -1),
            ],
            axis=1,
        ).astype(f32),
        ((0, 0), (0, LANES - 4)),
    )
    vectors = jnp.stack(
        [b_out, gain_one, bias_one, b_down, gain_two, bias_two, jnp.zeros_like(b_out), b_out]
    )
    biases = jnp.concatenate([b_query, jnp.zeros_like(b_value), b_value])[None]
    taps = jnp.pad(conv_weight, ((0, 5), (0, 0)))
    bias_up = b_up[None]
    if fast:
        split = (pack_rest.shape[1] * 3 // 5) // 256 * 256
        early = (features, own_feats, own_flip, tables, bounds, masks, vectors, biases, taps)
        parts_near = column_parts(after(half_columns(pack_rest[:, :split], is_text), column_qkv))
        w_down = after(w_down, column_qkv)
        pieces_qkv = half_pieces(column_qkv)
        column_near = jnp.stack([after(part, pieces_qkv[0]) for part in parts_near])
        parts_far = column_parts(after(pack_rest[:, split:], column_near))
        pieces_near = half_pieces(column_near)
        pieces_qkv[2] = after(pieces_qkv[2], pieces_near[0])
        pieces_qkv[3] = exchange(pieces_qkv[2], 1)
        groups_qkv = (("halves", 0),)
    else:
        groups_qkv = (("full", 0),)
        pieces_qkv = [lax.all_gather(pack_qkv, "page", axis=0, tiled=True)]
    full_down = lax.all_gather(w_down, "page", axis=0, tiled=True)

    other_mixed = dilated_mix(other_low.astype(f32), other_pages, conv_weight, conv_bias)
    other_mixed = other_mixed.astype(bf16)
    mixed_all = jnp.concatenate(
        [jnp.where(is_text, mixed_low, other_mixed), jnp.where(is_text, other_mixed, mixed_low)],
        axis=0,
    )
    if fast:
        pieces_qkv[0] = after(pieces_qkv[0], mixed_all, bias_up, *early)
    queries, keys_values, full_qkv, mixed_t = project(
        place, mixed_all, biases, groups_qkv, pieces_qkv
    )
    attend_in = queries
    if fast:
        column_far = jnp.stack([after(part, queries) for part in parts_far])
        across_far = exchange(column_far, 2)
        attend_in = after(queries, column_far)
    context = attend(bounds, attend_in, keys_values, features, own_feats, tables)
    if fast:
        pieces_near[2] = after(pieces_near[2], context)
        pieces_near[3] = exchange(pieces_near[2], 1)
        across_far = after(across_far, context)
        pieces_rest = pieces_near + row_pieces(column_far, across_far)
        groups_rest = (("halves", 0), ("rows", split))
    else:
        pieces_rest = [lax.all_gather(pack_rest, "page", axis=0, tiled=True)]
        groups_rest = (("full", 0),)
    unit, scale, normed_low, normed_t, context_t, active, active_t, slope, full_rest = up_forward(
        place, context, mixed, vectors, bias_up, groups_rest, pieces_rest
    )
    output_row, grad_sum_two, grad_ffn, small_two = down_forward(
        active, full_down, unit, vectors, cotangent[0, 0]
    )
    rows_down = grad_rows(active_t, grad_ffn)
    shard_down = lax.psum_scatter(rows_down, "page", scatter_dimension=0, tiled=True)
    grad_hidden, grad_b_up, grad_first, grad_branch, grad_context, small_one = ffn_back(
        after(grad_ffn, rows_down), slope, grad_sum_two, unit, scale, vectors, full_rest, full_down
    )
    attend_in = grad_context
    if fast:
        tiles = grad_hidden.shape[1] // d_model
        pairs = [
            (context_t, False, grad_branch, 0, 1),
            (normed_t, False, grad_hidden, 0, tiles // 2),
        ]
        keep_a, send_a = grad_by_columns(pairs, place, d_model)
        partner_a = exchange(send_a, 1)
        pairs = [(normed_t, False, after(grad_hidden, send_a), tiles // 2, tiles - tiles // 2)]
        keep_b, send_b = grad_by_columns(pairs, place, d_model)
        partner_b = exchange(send_b, 1)
        held_a, plane_a = halve_plane(place, keep_a, after(partner_a, send_b))
        far_a = swap(plane_a)
        held_b, plane_b = halve_plane(place, keep_b, after(partner_b, plane_a))
        far_b = swap(plane_b)
        attend_in = after(grad_context, plane_a, plane_b)
    else:
        shard_rest = summed_rows([(context_t, grad_branch), (normed_t, grad_hidden)])
    grad_queries, grad_keys, grad_values, grad_tables = attend_back(
        bounds, queries, keys_values, attend_in, features, own_feats, own_flip, tables
    )
    grad_keys_in, grad_queries_in = grad_keys, grad_queries
    if fast:
        far_a, far_b = after((far_a, far_b), grad_queries)
        held_rest, across_out = halve_two(held_a, far_a, held_b, far_b)
        across_rest = exchange(across_out, 2)
        grad_queries_in = after(grad_queries, across_out)
    pairs = [
        (mixed_t, True, grad_queries_in, 0, 1),
        (mixed_t, False, grad_keys, 0, 1),
        (mixed_t, False, grad_values, 0, 1),
    ]
    if fast:
        keep_qkv, send_qkv = grad_by_columns(pairs, place, d_model)
        partner_qkv = exchange(send_qkv, 1)
        grad_keys_in = after(grad_keys, send_qkv)
    else:
        shard_down = shard_down.astype(f32) + swap(shard_down).astype(f32)
        shard_qkv = summed_rows(
            [(mixed_low.T, grad_queries), (mixed_t, grad_keys), (mixed_t, grad_values)]
        )
    to_other = input_back(place, full_qkv, grad_keys_in, grad_values, ())
    from_other = swap(to_other)
    grad_values_in = grad_values
    if fast:
        partner_qkv = after(partner_qkv, to_other)
        held_qkv, across_out = halve_across(place, keep_qkv, partner_qkv)
        across_qkv = exchange(across_out, 2)
        grad_values_in = after(grad_values, across_out)
    own_part = input_back(place, full_qkv, grad_keys, grad_values_in, (grad_first, grad_queries))
    packed = small_sums(
        own_part,
        to_other,
        own_low,
        other_low,
        masks,
        grad_queries,
        grad_values,
        small_one,
        small_two,
        grad_b_up,
        grad_tables,
    )
    if fast:
        packed = both_sum(packed, 1)
        shard_down = after(shard_down, packed)
        across_rest = after(across_rest, packed, shard_down)
        shard_down = shard_down.astype(f32) + swap(shard_down).astype(f32)
        own_rest, sends_rest = column_sends(held_rest, across_rest)
        arrived_rest = column_arrivals(sends_rest)
        packed = after(packed, *sends_rest)
        packed = packed + swap(packed)
        across_qkv = after(across_qkv, packed)
        own_qkv, sends_qkv = column_sends(held_qkv, across_qkv)
        arrived_qkv = column_arrivals(sends_qkv)
        from_other = after(from_other, *sends_qkv)
    else:
        packed = lax.psum(packed, ("mod", "page"))
    grad_in = state_back(own_part, from_other, masks, taps)
    if fast:
        arrived_rest = [after(part, grad_in) for part in arrived_rest]
        total_rest = column_total(own_rest, arrived_rest)
        far_rest = swap(total_rest)
        packed = both_sum(both_sum(after(packed, total_rest), 2), 4)
        arrived_qkv = [after(part, packed) for part in arrived_qkv]
        total_qkv = column_total(own_qkv, arrived_qkv)
        far_qkv = swap(total_qkv)
        packed = both_sum(after(packed, total_qkv), 8)
    g_tables = packed[28:34].reshape(HEADS, 3, LANES)
    if fast:
        cut = far_a.shape[2]
        first_plane = jnp.where(is_text, total_rest, far_rest)
        second_plane = jnp.where(is_text, far_rest, total_rest)
        shard_rest = jnp.concatenate(
            [first_plane[:, :cut], second_plane[:, :cut], first_plane[:, cut:], second_plane[:, cut:]],
            axis=1,
        ).astype(f32)
        shard_qkv = total_qkv.astype(f32) + far_qkv.astype(f32)
    return (
        output_row[None, None],
        grad_in[None, None],
        packed[0:3],
        packed[3],
        shard_qkv[:, :d_model],
        packed[4],
        shard_qkv[:, d_model : 2 * d_model],
        shard_qkv[:, 2 * d_model :],
        packed[5],
        shard_rest[:, :d_model],
        packed[10],
        g_tables[:, 0, : table_pos.shape[1]],
        g_tables[:, 1, 64 : 64 + table_x.shape[1]],
        g_tables[:, 2, 64 : 64 + table_y.shape[1]],
        packed[8],
        packed[9],
        shard_rest[:, d_model:],
        packed[24:28].reshape(d_ff),
        shard_down,
        packed[18],
        packed[16],
        packed[17],
    )


def solution(mesh):
    rows = P("mod", "page", None, None)
    ids = P("page", None)
    cut = P("page", None)
    return jax.shard_map(
        local,
        mesh=mesh,
        in_specs=(
            rows, rows, ids, ids, ids, P(), P(), cut, P(), cut, cut, P(), cut,
            P(), P(), P(), P(), P(), P(), cut, P(), cut, P(), P(), P(),
        ),
        out_specs=(
            rows, rows, P(), P(), cut, P(), cut, cut, P(), cut, P(), P(), P(),
            P(), P(), P(), cut, P(), cut, P(), P(), P(),
        ),
        check_vma=False,
    )
```

```python
import functools

import jax
import jax.numpy as jnp
import numpy as np
from jax import lax
from jax.experimental import pallas as pl
from jax.experimental.pallas import tpu as pltpu
from jax.sharding import PartitionSpec as P

HEADS = 12
HEAD = 64
GRID = 8
PAGES = 8
POS_BINS = 64
BOX_BINS = 32
PATCH = 64
TEXT = 512
PAIRS = HEADS // 2
LANES = 2 * HEAD
WINDOW = 144
SMALL = 80

dilation = 2
small_cost = pl.CostEstimate(flops=1000, bytes_accessed=1000, transcendentals=0)
norm_eps = 1e-05
mask_fill = -1000000000.0
erfc_poly = (
    0.2367515965428487,
    0.24062179898991767,
    0.18865103029313968,
    0.2877518531132804,
    -0.1648672439458568,
    0.4765735350541787,
    -0.34041833366480423,
    0.07493571514857543,
)
bf16 = jnp.bfloat16
f32 = jnp.float32


def shifted(values, offset, fill_value):
    padding = jnp.full((abs(offset),) + values.shape[1:], fill_value, values.dtype)
    if offset > 0:
        return jnp.concatenate([values[offset:], padding], axis=0)
    return jnp.concatenate([padding, values[:offset]], axis=0)


def dilated_mix(inputs, page_ids, conv_weight, conv_bias):
    summed = inputs + conv_bias + conv_weight[1] * inputs
    for tap_index, offset in ((0, -dilation), (2, dilation)):
        moved_rows = shifted(inputs, offset, 0.0)
        moved_pages = shifted(page_ids, offset, -1)
        same_page = (moved_pages == page_ids)[:, None]
        summed = summed + conv_weight[tap_index] * jnp.where(same_page, moved_rows, 0.0)
    return summed


def bin_features(pos_bins, bins_x, bins_y):
    return jnp.concatenate(
        [
            jax.nn.one_hot(pos_bins, POS_BINS, dtype=bf16),
            jax.nn.one_hot(bins_x, BOX_BINS, dtype=bf16),
            jax.nn.one_hot(bins_y, BOX_BINS, dtype=bf16),
        ],
        axis=1,
    )


def token_ids(text_pages, text_x, text_y):
    text_index = jnp.arange(TEXT, dtype=jnp.int32)
    text_pos = text_index * POS_BINS // TEXT
    patch_pos = text_index % PATCH * POS_BINS // PATCH
    patch_page = text_index // PATCH
    patch_x = text_index % GRID * BOX_BINS // GRID
    patch_y = text_index // GRID % GRID * BOX_BINS // GRID
    page_ids = jnp.stack([text_pages, patch_page])
    pos_bins = jnp.stack([text_pos, patch_pos])
    bins_x = jnp.stack([text_x, patch_x])
    bins_y = jnp.stack([text_y, patch_y])
    return (page_ids, pos_bins, bins_x, bins_y)


def plain_dot(left_side, right_side):
    return jnp.dot(left_side, right_side, preferred_element_type=f32)


def dot_left_t(left_side, right_side):
    return lax.dot_general(
        left_side, right_side, (((0,), (0,)), ((), ())), preferred_element_type=f32
    )


def dot_right_t(left_side, right_side):
    return lax.dot_general(
        left_side, right_side, (((1,), (1,)), ((), ())), preferred_element_type=f32
    )


def iota(shape, axis):
    return lax.broadcasted_iota(jnp.int32, shape, axis)


def bias_block(table_rows):
    pos_part = pltpu.roll(
        jnp.broadcast_to(table_rows[0:1], (POS_BINS, LANES)), 65, 1, stride=1, stride_axis=0
    )
    x_part = pltpu.roll(
        jnp.broadcast_to(table_rows[1:2], (BOX_BINS, LANES)), 33, 1, stride=1, stride_axis=0
    )
    y_part = pltpu.roll(
        jnp.broadcast_to(table_rows[2:3], (BOX_BINS, LANES)), 65, 1, stride=1, stride_axis=0
    )
    lane = iota((POS_BINS, LANES), 1)
    pos_part = jnp.where(lane < POS_BINS, pos_part, 0.0)
    lane = iota((BOX_BINS, LANES), 1)
    x_part = jnp.where((lane >= 64) & (lane < 96), x_part, 0.0)
    y_part = jnp.where(lane >= 96, y_part, 0.0)
    return jnp.concatenate([pos_part, x_part, y_part], axis=0).astype(bf16)


def diagonal_sums(grad_block):
    lane = iota((POS_BINS, LANES), 1)
    pos_part = jnp.where(lane < POS_BINS, grad_block[:64], 0.0)
    lane = iota((BOX_BINS, LANES), 1)
    x_part = jnp.where((lane >= 64) & (lane < 96), grad_block[64:96], 0.0)
    y_part = jnp.where(lane >= 96, grad_block[96:], 0.0)
    pos_part = pltpu.roll(pos_part, 0, 1, stride=1, stride_axis=0)
    x_part = pltpu.roll(x_part, 0, 1, stride=1, stride_axis=0)
    y_part = pltpu.roll(y_part, 96, 1, stride=1, stride_axis=0)
    rows = [jnp.sum(part, axis=0, keepdims=True) for part in (pos_part, x_part, y_part)]
    return jnp.concatenate(rows + [jnp.zeros((5, LANES), f32)], axis=0)


def stacked_heads(rows, low_lane):
    zero = jnp.zeros_like(rows)
    return jnp.concatenate(
        [jnp.where(low_lane, rows, zero), jnp.where(low_lane, zero, rows)], axis=0
    )


def window_start(first, window):
    return pl.multiple_of(jnp.minimum(first // 16 * 16, TEXT - window), 16)


def fits(first, end, window):
    return end - jnp.minimum(first // 16 * 16, TEXT - window) <= window


def for_each_page(bounds, step):
    def body(page, carry):
        own_low, own_high = bounds[page], bounds[PAGES + page]
        key_low, key_high = bounds[2 * PAGES + page], bounds[3 * PAGES + page]
        own_small = fits(own_low, own_high, SMALL)
        key_small = fits(key_low, key_high, SMALL)
        span = (own_low, own_high, key_low, key_high)
        small = own_small & key_small
        for chosen, own_window, key_window in (
            (small, SMALL, SMALL),
            (~small, WINDOW, WINDOW),
        ):

            @pl.when(chosen)
            def _():
                step(page, span, own_window, key_window)

        return carry

    lax.fori_loop(0, PAGES, body, 0)


def page_operands(page, span, own_window, key_window, pair, q_ref, k_ref, feat_ref, lookup):
    own_at = window_start(span[0], own_window)
    key_at = window_start(span[2], key_window)
    own_rows, text_rows = pl.ds(own_at, own_window), pl.ds(key_at, key_window)
    patch_at = TEXT + PATCH * page
    if not isinstance(page, int):
        patch_at = pl.multiple_of(patch_at, PATCH)
    patch_rows = pl.ds(patch_at, PATCH)
    lanes = slice(pair * LANES, (pair + 1) * LANES)
    low_lane = iota((own_window, LANES), 1) < HEAD
    queries = stacked_heads(q_ref[own_rows, lanes], low_lane)
    first = 2 * pair * LANES
    rel = jnp.concatenate(
        [
            lookup[own_rows, first : first + LANES],
            lookup[own_rows, first + LANES : first + 2 * LANES],
        ],
        axis=0,
    )
    query_side = jnp.concatenate([rel, queries], axis=1)
    key_side = jnp.concatenate(
        [
            jnp.concatenate([feat_ref[text_rows, :], k_ref[text_rows, lanes]], axis=1),
            jnp.concatenate([feat_ref[patch_rows, :], k_ref[patch_rows, lanes]], axis=1),
        ],
        axis=0,
    )
    own_row = iota((own_window, LANES), 0) + own_at
    own_ok = (own_row >= span[0]) & (own_row < span[1])
    return (
        lanes, low_lane, own_ok, queries, query_side, key_side, own_rows, text_rows, patch_rows, key_at
    )


def set_lookup(lookup, own_feat_ref, table_ref):
    blocks = [bias_block(table_ref[head]) for head in range(table_ref.shape[0])]
    product = jnp.dot(
        own_feat_ref[...], jnp.concatenate(blocks, axis=1), preferred_element_type=f32
    )
    lookup[...] = product.astype(bf16)


def attend_kernel(bounds, q_ref, k_ref, v_ref, feat_ref, own_feat_ref, table_ref, context_ref, lookup):
    set_lookup(lookup, own_feat_ref, table_ref)

    def step(page, span, own_window, key_window):
        column = iota((1, key_window + PATCH), 1)
        key_row = column + window_start(span[2], key_window)
        key_ok = (column >= key_window) | ((key_row >= span[2]) & (key_row < span[3]))
        for pair in range(q_ref.shape[1] // LANES):
            lanes, low_lane, own_ok, _, query_side, key_side, own_rows, text_rows, patch_rows, _ = (
                page_operands(
                    page, span, own_window, key_window, pair, q_ref, k_ref, feat_ref, lookup
                )
            )
            scores = jnp.where(key_ok, dot_right_t(query_side, key_side), mask_fill)
            row_max = jnp.max(scores, axis=1, keepdims=True)
            weights = jnp.exp(scores - row_max)
            total = jnp.sum(weights, axis=1, keepdims=True)
            prob = (weights * (1.0 / total)).astype(bf16)
            values = jnp.concatenate([v_ref[text_rows, lanes], v_ref[patch_rows, lanes]], axis=0)
            mixed = jnp.dot(prob, values, preferred_element_type=f32)
            picked = jnp.where(low_lane, mixed[:own_window], mixed[own_window:])
            before = context_ref[own_rows, lanes].astype(f32)
            context_ref[own_rows, lanes] = jnp.where(own_ok, picked, before).astype(bf16)

    for page in range(PAGES):
        span = [bounds[part * PAGES + page] for part in range(4)]
        step(page, span, WINDOW, WINDOW)


def attend_back_kernel(
    bounds,
    q_ref,
    k_ref,
    v_ref,
    grad_ref,
    feat_ref,
    own_feat_ref,
    flip_feat_ref,
    table_ref,
    grad_q_ref,
    grad_k_ref,
    grad_v_ref,
    grad_table_ref,
    lookup,
    grad_lookup,
):
    set_lookup(lookup, own_feat_ref, table_ref)

    def step(page, span, own_window, key_window):
        row = iota((key_window + PATCH, 1), 0)
        key_row = row + window_start(span[2], key_window)
        key_ok = (row >= key_window) | ((key_row >= span[2]) & (key_row < span[3]))
        for pair in range(q_ref.shape[1] // LANES):
            lanes, low_lane, own_ok, queries, query_side, key_side, own_rows, text_rows, patch_rows, key_at = (
                page_operands(
                    page, span, own_window, key_window, pair, q_ref, k_ref, feat_ref, lookup
                )
            )
            scores = jnp.where(key_ok, dot_right_t(key_side, query_side), mask_fill)
            col_max = jnp.max(scores, axis=0, keepdims=True)
            weights = jnp.exp(scores - col_max)
            total = jnp.sum(weights, axis=0, keepdims=True)
            prob = weights * (1.0 / total)
            grad_rows = grad_ref[own_rows, lanes]
            grad_rows = jnp.where(own_ok, grad_rows, jnp.zeros_like(grad_rows))
            grads = stacked_heads(grad_rows, low_lane)
            values = jnp.concatenate([v_ref[text_rows, lanes], v_ref[patch_rows, lanes]], axis=0)
            grad_prob = dot_right_t(values, grads)
            inner = jnp.sum(prob * grad_prob, axis=0, keepdims=True)
            grad_scores = (prob * (grad_prob - inner)).astype(bf16)
            grad_v = jnp.dot(prob.astype(bf16), grads, preferred_element_type=f32)
            grad_k = jnp.dot(grad_scores, queries, preferred_element_type=f32)
            back = dot_left_t(grad_scores, key_side)
            low, high = back[:own_window], back[own_window:]
            grad_q = jnp.where(low_lane, low[:, LANES:], high[:, LANES:]) * 0.125
            before = grad_q_ref[own_rows, lanes].astype(f32)
            grad_q_ref[own_rows, lanes] = jnp.where(own_ok, grad_q, before).astype(bf16)
            first = 2 * pair * LANES
            for part, at in ((low, first), (high, first + LANES)):
                place_at = slice(at, at + LANES)
                grad_lookup[own_rows, place_at] = jnp.where(
                    own_ok, part[:, :LANES], grad_lookup[own_rows, place_at]
                )
            wide_row = iota((key_window, LANES), 0) + key_at
            text_ok = (wide_row >= span[2]) & (wide_row < span[3])
            for grad, ref in ((grad_k, grad_k_ref), (grad_v, grad_v_ref)):
                before = ref[text_rows, lanes].astype(f32)
                ref[text_rows, lanes] = jnp.where(text_ok, grad[:key_window], before).astype(bf16)
                ref[patch_rows, lanes] = grad[key_window:].astype(bf16)

    for_each_page(bounds, step)
    grad_high = grad_lookup[...].astype(bf16)
    grad_rest = (grad_lookup[...] - grad_high.astype(f32)).astype(bf16)
    flip = flip_feat_ref[...]
    grad_block = dot_left_t(flip, grad_high) + dot_left_t(flip, grad_rest)
    for head in range(table_ref.shape[0]):
        grad_table_ref[head] = diagonal_sums(grad_block[:, head * LANES : (head + 1) * LANES])


def column_spec(rows, group, first=0):
    return pl.BlockSpec((rows, group * LANES), lambda step, bounds: (0, step + first))


def whole_spec(rows):
    return pl.BlockSpec((rows, LANES), lambda step, bounds: (0, 0))


def tables_spec(group):
    return pl.BlockSpec((2 * group, 8, LANES), lambda step, bounds: (step, 0, 0))


def attend(bounds, queries, keys_values, features, own_features, tables):
    group = 1
    return pl.pallas_call(
        attend_kernel,
        grid_spec=pltpu.PrefetchScalarGridSpec(
            num_scalar_prefetch=1,
            grid=(PAIRS // group,),
            in_specs=[
                column_spec(TEXT, group),
                column_spec(2 * TEXT, group),
                column_spec(2 * TEXT, group, PAIRS // group),
                whole_spec(2 * TEXT),
                whole_spec(TEXT),
                tables_spec(group),
            ],
            out_specs=column_spec(TEXT, group),
            scratch_shapes=[pltpu.VMEM((TEXT, 2 * group * LANES), bf16)],
        ),
        out_shape=jax.ShapeDtypeStruct((TEXT, HEADS * HEAD), bf16),
        cost_estimate=small_cost,
        name="attend",
    )(bounds, queries, keys_values, keys_values, features, own_features, tables)


def attend_back(
    bounds, queries, keys_values, grad_context, features, own_features, flip, tables
):
    group = 6
    return pl.pallas_call(
        attend_back_kernel,
        grid_spec=pltpu.PrefetchScalarGridSpec(
            num_scalar_prefetch=1,
            grid=(PAIRS // group,),
            in_specs=[
                column_spec(TEXT, group),
                column_spec(2 * TEXT, group),
                column_spec(2 * TEXT, group, PAIRS // group),
                column_spec(TEXT, group),
                whole_spec(2 * TEXT),
                whole_spec(TEXT),
                whole_spec(TEXT),
                tables_spec(group),
            ],
            out_specs=[
                column_spec(TEXT, group),
                column_spec(2 * TEXT, group),
                column_spec(2 * TEXT, group),
                tables_spec(group),
            ],
            scratch_shapes=[
                pltpu.VMEM((TEXT, 2 * group * LANES), bf16),
                pltpu.VMEM((TEXT, 2 * group * LANES), f32),
            ],
        ),
        out_shape=[
            jax.ShapeDtypeStruct((TEXT, HEADS * HEAD), bf16),
            jax.ShapeDtypeStruct((2 * TEXT, HEADS * HEAD), bf16),
            jax.ShapeDtypeStruct((2 * TEXT, HEADS * HEAD), bf16),
            jax.ShapeDtypeStruct((HEADS, 8, LANES), f32),
        ],
        cost_estimate=small_cost,
        name="attend_back",
    )(
        bounds,
        queries,
        keys_values,
        keys_values,
        grad_context,
        features,
        own_features,
        flip,
        tables,
    )


def exchange(values, mask):
    count = lax.axis_size("page")
    return lax.ppermute(values, "page", [(i, i ^ mask) for i in range(count)])


def after(value, *earlier):
    return lax.optimization_barrier((value, *earlier))[0]


def slot_mask(slot):
    return (slot & 3) * 4 + (slot >> 2) * 2


def project_kernel(groups, place, mixed_ref, bias_ref, *refs):
    *pieces, query_ref, both_ref, weight_ref, mixed_t_ref, sems = refs
    width = mixed_ref.shape[1]
    tokens = query_ref.shape[0]
    copies = start_rows(place, groups, pieces, weight_ref, sems)
    mixed_t_ref[...] = mixed_ref[...].T
    for copy in copies:
        copy.wait()
    own = mixed_ref[pl.ds(pl.multiple_of(place[1] * tokens, 16), tokens), :]
    queries = jnp.dot(own, weight_ref[:, :width], preferred_element_type=f32) + bias_ref[:, :width]
    query_ref[...] = (queries.astype(bf16).astype(f32) * 0.125).astype(bf16)
    for part in range(2):
        rows = pl.ds(part * tokens, tokens)
        for column in (1, 2):
            at = slice(column * width, (column + 1) * width)
            out = slice((column - 1) * width, column * width)
            values = jnp.dot(mixed_ref[rows, :], weight_ref[:, at], preferred_element_type=f32)
            both_ref[rows, out] = (values + bias_ref[:, at]).astype(bf16)


def project(place, mixed, biases, groups, pieces):
    rows, width = mixed.shape
    vmem = pl.BlockSpec(memory_space=pltpu.VMEM)
    return pl.pallas_call(
        functools.partial(project_kernel, groups),
        grid_spec=pltpu.PrefetchScalarGridSpec(
            num_scalar_prefetch=1,
            grid=(),
            in_specs=[vmem] * 2 + any_specs(len(pieces)),
            out_specs=[vmem] * 4,
            scratch_shapes=[pltpu.SemaphoreType.DMA((32,))],
        ),
        out_shape=[
            jax.ShapeDtypeStruct((rows // 2, width), bf16),
            jax.ShapeDtypeStruct((rows, 2 * width), bf16),
            jax.ShapeDtypeStruct((width, 3 * width), bf16),
            jax.ShapeDtypeStruct((width, rows), bf16),
        ],
        cost_estimate=small_cost,
        compiler_params=pltpu.CompilerParams(vmem_limit_bytes=16 << 20),
        name="project",
    )(place, mixed, biases, *pieces)


def column_parts(shard):
    return [shard] + [exchange(shard, 4 * step) for step in (1, 2, 3)]


def half_pieces(column):
    eight = jnp.concatenate([column, exchange(column, 2)])
    far = swap(eight)
    return [eight, exchange(eight, 1), far, exchange(far, 1)]


def row_pieces(column, across):
    return [column, exchange(column, 1), across, exchange(across, 1)]


def column_pairs(shard):
    far = exchange(shard, 8)
    near = exchange(jnp.stack([shard, far]), 4)
    return [shard, near[0], far, near[1]]


def column_of(shard):
    return jnp.stack(column_parts(shard))


def row_copies(place, groups, refs, full, sems, first=0):
    copies = []
    for kind, column in groups:
        if kind == "full":
            piece, *refs = refs
            width = piece.shape[1]
            target = full.at[:, pl.ds(column, width)]
            copies.append(pltpu.make_async_copy(piece, target, sems.at[first + len(copies)]))
            continue
        pieces, refs = refs[:4], refs[4:]
        _, rows, width = pieces[0].shape
        for index in range(32 if kind == "halves" else 16):
            at = column
            if kind == "halves":
                source, slot = index >> 3, index & 7
                mask = slot_mask(slot) + (source & 1)
                at = pl.multiple_of(column + (place[1] ^ (source >> 1)) * width, 128)
            else:
                source, slot = index & 3, index >> 2
                mask = slot * 4 + source
            row = pl.multiple_of((place[0] ^ mask) * rows, 16)
            copies.append(
                pltpu.make_async_copy(
                    pieces[source].at[slot],
                    full.at[pl.ds(row, rows), pl.ds(at, width)],
                    sems.at[first + len(copies)],
                )
            )
    return copies


def start_rows(place, groups, refs, full, sems):
    copies = row_copies(place, groups, refs, full, sems)
    for copy in copies:
        copy.start()
    return copies


def gelu_parts(values):
    size = jnp.abs(values)
    t = 1.0 / (1.0 + (0.42 * 0.7071067811865476) * size)
    poly = jnp.full_like(t, erfc_poly[-1])
    for coefficient in erfc_poly[-2::-1]:
        poly = poly * t + coefficient
    bell = jnp.exp(-0.5 * values * values)
    tail = (0.5 * t) * (poly * bell)
    cdf = jnp.where(values >= 0.0, 1.0 - tail, tail)
    return values * cdf, cdf + (values * 0.3989422804014327) * bell


def normalized(values):
    centered = values - jnp.mean(values, axis=1, keepdims=True)
    variance = jnp.mean(centered * centered, axis=1, keepdims=True)
    scale = lax.rsqrt(variance + norm_eps)
    return centered * scale, scale


def norm_back(grads, unit, scale, gain):
    scaled = grads * gain
    mean = jnp.mean(scaled, axis=1, keepdims=True)
    inner = jnp.mean(scaled * unit, axis=1, keepdims=True)
    return scale * (scaled - mean - unit * inner)


def up_kernel(groups, place, context_ref, mixed_ref, vec_ref, bias_ref, *refs):
    *pieces, unit_ref, scale_ref, low_ref, low_t_ref, context_t_ref = refs[:-9]
    active_ref, active_t_ref, slope_ref, full_ref = refs[-9:-5]
    weight, hidden, low, sems, full_sem = refs[-5:]
    step = pl.program_id(0)
    tiles = pl.num_programs(0) - 1
    width = context_ref.shape[1]
    tile = active_ref.shape[1]
    last_group = 16 if len(groups) > 1 else 0

    def full_copy():
        return pltpu.make_async_copy(weight, full_ref, full_sem)

    @pl.when(step == 0)
    def _():
        copies = row_copies(place, groups, pieces, weight, sems)
        for copy in copies:
            copy.start()
        context_t_ref[...] = context_ref[...].T
        for copy in copies[: len(copies) - last_group]:
            copy.wait()
        branch = jnp.dot(context_ref[...], weight[:, :width], preferred_element_type=f32)
        unit, scale = normalized(mixed_ref[...] + branch + vec_ref[0:1])
        unit_ref[...] = unit
        scale_ref[...] = jnp.broadcast_to(scale, scale_ref.shape)
        normed = (unit * vec_ref[1:2] + vec_ref[2:3]).astype(bf16)
        low[...] = normed
        low_ref[...] = normed
        low_t_ref[...] = normed.T

    @pl.when(step == 1)
    def _():
        if last_group:
            for copy in row_copies(place, groups[1:], pieces[4:], weight, sems, 32):
                copy.wait()
        full_copy().start()

    def product():
        at = pl.multiple_of(width + step * tile, 128)
        return jnp.dot(low[...], weight[:, pl.ds(at, tile)], preferred_element_type=f32)

    def activate():
        active, slope = gelu_parts(hidden[(step + 1) % 2] + bias_ref[...])
        active = active.astype(bf16)
        active_ref[...] = active
        active_t_ref[...] = active.T
        slope_ref[...] = slope.astype(bf16)

    @pl.when(step == 0)
    def _():
        hidden[step % 2] = product()

    @pl.when((step > 0) & (step < tiles))
    def _():
        hidden[step % 2] = product()
        activate()

    @pl.when(step == tiles)
    def _():
        activate()
        full_copy().wait()


def any_specs(count):
    return [pl.BlockSpec(memory_space=pl.ANY)] * count


def up_forward(place, context, mixed, vectors, bias_up, groups, pieces):
    tokens, width = mixed.shape
    hidden_width = bias_up.shape[1]
    tile = 768
    whole = lambda step, place: (0, 0)
    last = lambda step, place: (0, jnp.maximum(step - 1, 0))
    last_t = lambda step, place: (jnp.maximum(step - 1, 0), 0)
    return pl.pallas_call(
        functools.partial(up_kernel, groups),
        grid_spec=pltpu.PrefetchScalarGridSpec(
            num_scalar_prefetch=1,
            grid=(hidden_width // tile + 1,),
            in_specs=[
                pl.BlockSpec((tokens, width), whole),
                pl.BlockSpec((tokens, width), whole),
                pl.BlockSpec(vectors.shape, whole),
                pl.BlockSpec((1, tile), last),
            ]
            + any_specs(len(pieces)),
            out_specs=[
                pl.BlockSpec((tokens, width), whole),
                pl.BlockSpec((tokens, 128), whole),
                pl.BlockSpec((tokens, width), whole),
                pl.BlockSpec((width, tokens), whole),
                pl.BlockSpec((width, tokens), whole),
                pl.BlockSpec((tokens, tile), last),
                pl.BlockSpec((tile, tokens), last_t),
                pl.BlockSpec((tokens, tile), last),
                pl.BlockSpec(memory_space=pl.ANY),
            ],
            scratch_shapes=[
                pltpu.VMEM((width, width + hidden_width), bf16),
                pltpu.VMEM((2, tokens, tile), f32),
                pltpu.VMEM((tokens, width), bf16),
                pltpu.SemaphoreType.DMA((48,)),
                pltpu.SemaphoreType.DMA,
            ],
        ),
        out_shape=[
            jax.ShapeDtypeStruct((tokens, width), f32),
            jax.ShapeDtypeStruct((tokens, 128), f32),
            jax.ShapeDtypeStruct((tokens, width), bf16),
            jax.ShapeDtypeStruct((width, tokens), bf16),
            jax.ShapeDtypeStruct((width, tokens), bf16),
            jax.ShapeDtypeStruct((tokens, hidden_width), bf16),
            jax.ShapeDtypeStruct((hidden_width, tokens), bf16),
            jax.ShapeDtypeStruct((tokens, hidden_width), bf16),
            jax.ShapeDtypeStruct((width, width + hidden_width), bf16),
        ],
        cost_estimate=small_cost,
        name="up_forward",
    )(place, context, mixed, vectors, bias_up, *pieces)


def down_kernel(active_ref, weight_ref, unit_ref, vec_ref, grad_ref, *refs):
    out_ref, sum_ref, low_ref, small_ref, total = refs
    step = pl.program_id(0)
    product = jnp.dot(active_ref[...], weight_ref[...], preferred_element_type=f32)

    @pl.when(step == 0)
    def _():
        total[...] = product

    @pl.when(step > 0)
    def _():
        total[...] += product

    @pl.when(step == pl.num_programs(0) - 1)
    def _():
        tokens, width = unit_ref.shape
        half = tokens // 2
        smalls = [jnp.zeros((1, width), f32)] * 3
        for part in range(2):
            rows = pl.ds(part * half, half)
            normed = unit_ref[rows, :] * vec_ref[1:2] + vec_ref[2:3]
            unit, scale = normalized(normed + total[rows, :] + vec_ref[3:4])
            out_ref[rows, :] = (unit * vec_ref[4:5] + vec_ref[5:6]).astype(bf16)
            grads = grad_ref[rows, :].astype(f32)
            back = norm_back(grads, unit, scale, vec_ref[4:5])
            low = back.astype(bf16)
            sum_ref[rows, :] = back
            low_ref[rows, :] = low
            for index, term in enumerate((grads * unit, grads, low.astype(f32))):
                smalls[index] = smalls[index] + jnp.sum(term, axis=0, keepdims=True)
        small_ref[...] = jnp.concatenate(smalls + [jnp.zeros((5, width), f32)], axis=0)


def down_forward(active, weight, unit, vectors, grads):
    tokens, width = unit.shape
    hidden_width = active.shape[1]
    tile = 1536
    whole = lambda step: (0, 0)
    token_block = pl.BlockSpec((tokens, width), whole)
    return pl.pallas_call(
        down_kernel,
        grid=(hidden_width // tile,),
        in_specs=[
            pl.BlockSpec((tokens, tile), lambda step: (0, step)),
            pl.BlockSpec((tile, width), lambda step: (step, 0)),
            token_block,
            pl.BlockSpec(vectors.shape, whole),
            token_block,
        ],
        out_specs=[token_block] * 3 + [pl.BlockSpec((8, width), whole)],
        scratch_shapes=[pltpu.VMEM((tokens, width), f32)],
        out_shape=[
            jax.ShapeDtypeStruct((tokens, width), bf16),
            jax.ShapeDtypeStruct((tokens, width), f32),
            jax.ShapeDtypeStruct((tokens, width), bf16),
            jax.ShapeDtypeStruct((8, width), f32),
        ],
        cost_estimate=small_cost,
        name="down_forward",
    )(active, weight, unit, vectors, grads)


def ffn_back_kernel(*refs):
    low_ref, slope_ref, sum_ref, unit_ref, scale_ref, vec_ref = refs[:6]
    down_ref, up_ref, out_weight_ref = refs[6:9]
    hidden_ref, bias_ref, first_ref, branch_ref, context_ref, small_ref, total = refs[9:]
    step = pl.program_id(0)
    tokens, width = unit_ref.shape
    tile = slope_ref.shape[1]
    half = tokens // 2

    @pl.when(step == 0)
    def _():
        total[...] = sum_ref[...]

    bias = jnp.zeros((1, tile), f32)
    for part in range(2):
        rows = pl.ds(part * half, half)
        grads = dot_right_t(low_ref[rows, :], down_ref[...]) * slope_ref[rows, :].astype(f32)
        grads = grads.astype(bf16)
        hidden_ref[rows, :] = grads
        bias = bias + jnp.sum(grads.astype(f32), axis=0, keepdims=True)
        total[rows, :] += dot_right_t(grads, up_ref[...])
    bias_ref[...] = bias

    @pl.when(step == pl.num_programs(0) - 1)
    def _():
        grads = total[...]
        unit = unit_ref[...]
        first = norm_back(grads, unit, scale_ref[:, 0:1], vec_ref[1:2])
        branch = first.astype(bf16)
        first_ref[...] = first
        branch_ref[...] = branch
        context_ref[...] = dot_right_t(branch, out_weight_ref[...]).astype(bf16)
        smalls = [
            jnp.sum(term, axis=0, keepdims=True)
            for term in (grads * unit, grads, branch.astype(f32))
        ]
        small_ref[...] = jnp.concatenate(smalls + [jnp.zeros((5, width), f32)], axis=0)


def ffn_back(low, slope, total, unit, scale, vectors, full_rest, full_down):
    tokens, width = unit.shape
    hidden_width = slope.shape[1]
    tile = 768
    whole = lambda step: (0, 0)
    column = lambda step: (0, step)
    token_block = pl.BlockSpec((tokens, width), whole)
    return pl.pallas_call(
        ffn_back_kernel,
        grid=(hidden_width // tile,),
        in_specs=[
            token_block,
            pl.BlockSpec((tokens, tile), column),
            token_block,
            token_block,
            pl.BlockSpec((tokens, 128), whole),
            pl.BlockSpec(vectors.shape, whole),
            pl.BlockSpec((tile, width), lambda step: (step, 0)),
            pl.BlockSpec((width, tile), lambda step: (0, step + 1)),
            pl.BlockSpec((width, width), whole),
        ],
        out_specs=[
            pl.BlockSpec((tokens, tile), column),
            pl.BlockSpec((1, tile), column),
            token_block,
            token_block,
            token_block,
            pl.BlockSpec((8, width), whole),
        ],
        scratch_shapes=[pltpu.VMEM((tokens, width), f32)],
        out_shape=[
            jax.ShapeDtypeStruct((tokens, hidden_width), bf16),
            jax.ShapeDtypeStruct((1, hidden_width), f32),
            jax.ShapeDtypeStruct((tokens, width), f32),
            jax.ShapeDtypeStruct((tokens, width), bf16),
            jax.ShapeDtypeStruct((tokens, width), bf16),
            jax.ShapeDtypeStruct((8, width), f32),
        ],
        cost_estimate=small_cost,
        name="ffn_back",
    )(low, slope, total, unit, scale, vectors, full_down, full_rest, full_rest)


def grad_rows_kernel(x_ref, h_ref, out_ref):
    out_ref[...] = jnp.dot(x_ref[...], h_ref[...], preferred_element_type=f32).astype(bf16)


def grad_rows(inputs_t, grads):
    width, tokens = inputs_t.shape
    columns = grads.shape[1]
    return pl.pallas_call(
        grad_rows_kernel,
        grid=(4,),
        in_specs=[
            pl.BlockSpec((width // 4, tokens), lambda step: (step, 0)),
            pl.BlockSpec((tokens, columns), lambda step: (0, 0)),
        ],
        out_specs=pl.BlockSpec((width // 4, columns), lambda step: (step, 0)),
        out_shape=jax.ShapeDtypeStruct((width, columns), bf16),
        cost_estimate=small_cost,
        name="grad_rows",
    )(inputs_t, grads)


def grad_columns_kernel(parts, place, *refs):
    count = len(parts)
    ins, keep_ref, send_ref, scratch = (
        refs[: 2 * count],
        refs[2 * count],
        refs[2 * count + 1],
        refs[2 * count + 2 :],
    )
    rows, tile = keep_ref.shape[1], keep_ref.shape[2]
    step = pl.program_id(0)
    first = 0
    for index, steps in enumerate(parts):
        x_ref, h_ref, ordered = ins[2 * index], ins[2 * index + 1], scratch[index]

        @pl.when(step == first)
        def _():
            for slot in range(16):
                mask = slot_mask(slot & 7) + (slot >> 3)
                at = pl.multiple_of((place[0] ^ mask) * rows, 16)
                ordered[pl.ds(slot * rows, rows), :] = x_ref[pl.ds(at, rows), :]

        @pl.when((step >= first) & (step < first + steps))
        def _():
            product = jnp.dot(ordered[...], h_ref[...], preferred_element_type=f32).astype(bf16)
            keep_ref[...] = product[: 8 * rows].reshape(8, rows, tile)
            send_ref[...] = product[8 * rows :].reshape(8, rows, tile)

        first = first + steps


def grad_by_columns(pairs, place, tile):
    width = pairs[0][0].shape[0]
    rows = width // 16
    parts = tuple(count for *_, count in pairs)
    steps = sum(parts)
    specs = []
    operands = []
    scratch = []
    first = 0
    for inputs_t, own, grads, start, count in pairs:
        tokens = grads.shape[0]
        block = (lambda step, place: (0, place[1])) if own else (lambda step, place: (0, 0))
        specs.append(pl.BlockSpec((width, tokens), block))

        def column(step, place, first=first, start=start, count=count):
            return (0, start + jnp.clip(step - first, 0, count - 1))

        specs.append(pl.BlockSpec((tokens, tile), column))
        operands += [inputs_t, grads]
        scratch.append(pltpu.VMEM((width, tokens), bf16))
        first = first + count
    half = jax.ShapeDtypeStruct((8, rows, steps * tile), bf16)
    return pl.pallas_call(
        functools.partial(grad_columns_kernel, parts),
        grid_spec=pltpu.PrefetchScalarGridSpec(
            num_scalar_prefetch=1,
            grid=(steps,),
            in_specs=specs,
            out_specs=[pl.BlockSpec((8, rows, tile), lambda step, place: (0, 0, step))] * 2,
            scratch_shapes=scratch,
        ),
        out_shape=[half, half],
        cost_estimate=small_cost,
        compiler_params=pltpu.CompilerParams(vmem_limit_bytes=16 << 20),
        name="grad_columns",
    )(place, *operands)


def key_back_kernel(place, gk_ref, gv_ref, wk_ref, wv_ref, out_ref):
    total = dot_right_t(gk_ref[...], wk_ref[...]) + dot_right_t(gv_ref[...], wv_ref[...])
    out_ref[...] = total.astype(out_ref.dtype)


def own_back_kernel(place, first_ref, gq_ref, gk_ref, gv_ref, wq_ref, wk_ref, wv_ref, out_ref):
    total = dot_right_t(gk_ref[...], wk_ref[...]) + dot_right_t(gv_ref[...], wv_ref[...])
    out_ref[...] = first_ref[...] + total + dot_right_t(gq_ref[...], wq_ref[...])


def input_back(place, weights, grad_keys, grad_values, others):
    width = weights.shape[0]
    tokens = grad_keys.shape[0] // 2
    whole = pl.BlockSpec((tokens, width), lambda step, place: (0, 0))
    row = lambda step, place: ((place[1] if others else 1 - place[1]), 0)
    if others:
        kernel, leading, first, dtype = own_back_kernel, [whole, whole], 0, f32
    else:
        kernel, leading, first, dtype = key_back_kernel, [], 1, bf16
    operands = list(others) + [grad_keys, grad_values] + [weights] * (3 - first)
    specs = [pl.BlockSpec((tokens, width), row)] * 2
    for block in range(first, 3):
        specs.append(pl.BlockSpec((width, width), lambda step, place, block=block: (0, block)))
    return pl.pallas_call(
        kernel,
        grid_spec=pltpu.PrefetchScalarGridSpec(
            num_scalar_prefetch=1, grid=(1,), in_specs=leading + specs, out_specs=whole
        ),
        out_shape=jax.ShapeDtypeStruct((tokens, width), dtype),
        cost_estimate=small_cost,
        compiler_params=pltpu.CompilerParams(vmem_limit_bytes=16 << 20),
        name="input_back",
    )(place, *operands)


def back_rows(values, mask):
    return jnp.where(mask, pltpu.roll(values, dilation, 0), 0.0)


def ahead_rows(values, mask):
    return jnp.where(mask, pltpu.roll(values, values.shape[0] - dilation, 0), 0.0)


def tap_sums(grads, inputs, ahead, back):
    terms = (grads * back_rows(inputs, back), grads * inputs, grads * ahead_rows(inputs, ahead), grads)
    return [jnp.sum(term, axis=0, keepdims=True) for term in terms]


def small_sums_kernel(
    own_ref, other_ref, x_ref, x_other_ref, mask_ref, gq_ref, gv_ref, one_ref, two_ref, up_ref, table_ref, out_ref
):
    width = own_ref.shape[1]
    mask = mask_ref[...] > 0.0
    own = tap_sums(own_ref[...], x_ref[...].astype(f32), mask[:, 0:1], mask[:, 1:2])
    other = tap_sums(
        other_ref[...].astype(f32), x_other_ref[...].astype(f32), mask[:, 2:3], mask[:, 3:4]
    )
    rows = [a + b for a, b in zip(own, other)]
    for ref in (gq_ref, gv_ref):
        rows.append(jnp.sum(ref[...].astype(f32), axis=0, keepdims=True))
    rows.append(jnp.zeros((2, width), f32))
    out_ref[0:8] = jnp.concatenate(rows, axis=0)
    out_ref[8:16] = one_ref[...]
    out_ref[16:24] = two_ref[...]
    count = up_ref.shape[1] // width
    for index in range(count):
        out_ref[24 + index : 25 + index] = up_ref[:, index * width : (index + 1) * width]
    for index in range(3 * HEADS):
        row, lane = 28 + index // 6, index % 6 * LANES
        table = table_ref[index // 3]
        out_ref[row : row + 1, lane : lane + LANES] = table[index % 3 : index % 3 + 1]
    out_ref[34:40] = jnp.zeros((6, width), f32)


def small_sums(*operands):
    return pl.pallas_call(
        small_sums_kernel,
        out_shape=jax.ShapeDtypeStruct((40, operands[0].shape[1]), f32),
        cost_estimate=small_cost,
        compiler_params=pltpu.CompilerParams(vmem_limit_bytes=24 << 20),
        name="small_sums",
    )(*operands)


def state_back_kernel(own_ref, other_ref, mask_ref, tap_ref, out_ref):
    grads = own_ref[...] + other_ref[...].astype(f32)
    mask = mask_ref[...] > 0.0
    total = grads + tap_ref[1:2] * grads
    total = total + tap_ref[0:1] * ahead_rows(grads, mask[:, 0:1])
    total = total + tap_ref[2:3] * back_rows(grads, mask[:, 1:2])
    out_ref[...] = total.astype(bf16)


def state_back(own, other, masks, taps):
    return pl.pallas_call(
        state_back_kernel,
        out_shape=jax.ShapeDtypeStruct(own.shape, bf16),
        cost_estimate=small_cost,
        compiler_params=pltpu.CompilerParams(vmem_limit_bytes=20 << 20),
        name="state_back",
    )(own, other, masks, taps)


def first_half_kernel(place, keep_near, part_near, keep_far, part_far, held_ref, out_ref):
    held_ref[...] = keep_near[...].astype(f32) + part_near[...].astype(f32)
    out_ref[...] = (keep_far[...].astype(f32) + part_far[...].astype(f32)).astype(bf16)


def halve_call(place, keep, partner, specs, half_shape, steps):
    near, far, out = specs
    return pl.pallas_call(
        first_half_kernel,
        grid_spec=pltpu.PrefetchScalarGridSpec(
            num_scalar_prefetch=1,
            grid=(steps,),
            in_specs=[near, near, far, far],
            out_specs=[out, out],
        ),
        out_shape=[
            jax.ShapeDtypeStruct(half_shape, f32),
            jax.ShapeDtypeStruct(half_shape, bf16),
        ],
        cost_estimate=small_cost,
        compiler_params=pltpu.CompilerParams(vmem_limit_bytes=12 << 20),
        name="halve",
    )(place, keep, partner, keep, partner)


def halve_across(place, keep, partner):
    _, rows, width = keep.shape
    near = pl.BlockSpec((1, rows, width), lambda step, place: (step, 0, 0))
    far = pl.BlockSpec((1, rows, width), lambda step, place: (step + 4, 0, 0))
    return halve_call(place, keep, partner, (near, far, near), (4, rows, width), 4)


def halve_plane(place, keep, partner):
    _, rows, width = keep.shape
    block = (2, rows, width // 2)
    near = pl.BlockSpec(block, lambda step, place: (step, 0, place[1]))
    far = pl.BlockSpec(block, lambda step, place: (step, 0, 1 - place[1]))
    out = pl.BlockSpec(block, lambda step, place: (step, 0, 0))
    return halve_call(place, keep, partner, (near, far, out), (8, rows, width // 2), 4)


def two_kernel(near_a, far_a, near_b, far_b, *refs):
    *partners, held_ref, out_ref = refs
    split = near_a.shape[2]
    for index, (near, far) in enumerate(((near_a, far_a), (near_b, far_b))):
        lanes = slice(0, split) if index == 0 else slice(split, None)
        part_near, part_far = partners[2 * index], partners[2 * index + 1]
        held_ref[:, :, lanes] = near[...] + part_near[...].astype(f32)
        out_ref[:, :, lanes] = (far[...] + part_far[...].astype(f32)).astype(bf16)


def halve_two(held_a, part_a, held_b, part_b):
    _, rows, width_a = held_a.shape
    width_b = held_b.shape[2]
    specs = []
    for width in (width_a, width_b):
        block = (1, rows, width)
        specs.append(pl.BlockSpec(block, lambda step: (step, 0, 0)))
        specs.append(pl.BlockSpec(block, lambda step: (step + 4, 0, 0)))
    out = pl.BlockSpec((1, rows, width_a + width_b), lambda step: (step, 0, 0))
    shape = (4, rows, width_a + width_b)
    return pl.pallas_call(
        two_kernel,
        grid=(4,),
        in_specs=specs * 2,
        out_specs=[out, out],
        out_shape=[jax.ShapeDtypeStruct(shape, f32), jax.ShapeDtypeStruct(shape, bf16)],
        cost_estimate=small_cost,
        compiler_params=pltpu.CompilerParams(vmem_limit_bytes=12 << 20),
        name="halve_two",
    )(held_a, held_a, held_b, held_b, part_a, part_a, part_b, part_b)


def column_kernel(held_ref, across_ref, own_ref, *sends):
    own_ref[...] = held_ref[0] + across_ref[0].astype(f32)
    for step, send in enumerate(sends, 1):
        send[...] = (held_ref[step] + across_ref[step].astype(f32)).astype(bf16)


def column_sends(held, across):
    _, rows, width = held.shape
    tile = 384
    out = pl.BlockSpec((rows, tile), lambda step: (0, step))
    block = pl.BlockSpec((4, rows, tile), lambda step: (0, 0, step))
    own, *sends = pl.pallas_call(
        column_kernel,
        grid=(width // tile,),
        in_specs=[block, block],
        out_specs=[out] * 4,
        out_shape=[jax.ShapeDtypeStruct((rows, width), f32)]
        + [jax.ShapeDtypeStruct((rows, width), bf16)] * 3,
        cost_estimate=small_cost,
        compiler_params=pltpu.CompilerParams(vmem_limit_bytes=12 << 20),
        name="column_sends",
    )(held, across)
    return own, sends


def column_arrivals(sends):
    return [exchange(send, 4 * step) for step, send in enumerate(sends, 1)]


def column_total(own, arrived):
    total = own
    for part in arrived:
        total = total + part.astype(f32)
    return total.astype(bf16)


def half_columns(values, first):
    half = values.shape[-1] // 2
    return jnp.where(first, values[..., :half], values[..., half:])


def summed_rows(pairs):
    grads = jnp.concatenate([plain_dot(*pair).astype(bf16) for pair in pairs], axis=1)
    shard = lax.psum_scatter(grads, "page", scatter_dimension=0, tiled=True)
    return shard.astype(f32) + swap(shard).astype(f32)


def page_bounds(segments, is_text):
    pages = jnp.arange(PAGES, dtype=jnp.int32)
    low = jnp.sum(segments[None, :] < pages[:, None], axis=1, dtype=jnp.int32)
    high = jnp.sum(segments[None, :] <= pages[:, None], axis=1, dtype=jnp.int32)
    own_low = jnp.where(is_text, low, pages * PATCH)
    own_high = jnp.where(is_text, high, (pages + 1) * PATCH)

    return jnp.concatenate([own_low, own_high, low, high])


def both_sum(values, mask):
    return values + exchange(values, mask)


def swap(values):
    return lax.ppermute(values, "mod", [(0, 1), (1, 0)])


def local(
    states,
    cotangent,
    segments,
    box_x,
    box_y,
    conv_weight,
    conv_bias,
    w_query,
    b_query,
    w_key,
    w_value,
    b_value,
    w_out,
    b_out,
    table_pos,
    table_x,
    table_y,
    gain_one,
    bias_one,
    w_up,
    b_up,
    w_down,
    b_down,
    gain_two,
    bias_two,
):
    is_text = lax.axis_index("mod") == 0
    d_model = states.shape[3]
    own_low = states[0, 0]
    rows_each = w_query.shape[0]
    d_ff = w_up.shape[1]
    fast = lax.axis_size("page") == 16 and rows_each % 16 == 0 and w_down.shape[0] % 16 == 0
    place = jnp.stack([lax.axis_index("page"), lax.axis_index("mod")]).astype(jnp.int32)
    pack_qkv = jnp.concatenate([w_query, w_key, w_value], axis=1)
    pack_rest = jnp.concatenate([w_out, w_up], axis=1)
    other_low = swap(own_low)
    if fast:
        column_qkv = column_of(half_columns(pack_qkv, is_text))
        table_pos, table_x, table_y, b_out, b_down, b_query, b_value, b_up = after(
            (table_pos, table_x, table_y, b_out, b_down, b_query, b_value, b_up), column_qkv
        )
        gain_one, bias_one, gain_two, bias_two, conv_weight = after(
            (gain_one, bias_one, gain_two, bias_two, conv_weight), column_qkv
        )
        segments, box_x, box_y = after((segments, box_x, box_y), column_qkv)
    page_ids, pos_bins, bins_x, bins_y = token_ids(segments[0], box_x[0], box_y[0])
    bounds = page_bounds(segments[0], is_text)
    own_pages = jnp.where(is_text, page_ids[0], page_ids[1])
    features = bin_features(pos_bins.reshape(-1), bins_x.reshape(-1), bins_y.reshape(-1))
    flipped = bin_features(
        POS_BINS - 1 - pos_bins.reshape(-1),
        BOX_BINS - 1 - bins_x.reshape(-1),
        BOX_BINS - 1 - bins_y.reshape(-1),
    )
    own_feats = jnp.where(is_text, features[:TEXT], features[TEXT:])
    own_flip = jnp.where(is_text, flipped[:TEXT], flipped[TEXT:])
    tables = jnp.stack(
        [
            jnp.pad(table_pos, ((0, 0), (0, LANES - table_pos.shape[1]))),
            jnp.pad(table_x, ((0, 0), (0, LANES - table_x.shape[1]))),
            jnp.pad(table_y, ((0, 0), (0, LANES - table_y.shape[1]))),
        ],
        axis=1,
    )
    tables = jnp.pad(tables, ((0, 0), (0, 5), (0, 0)))

    own_states = own_low.astype(f32)
    mixed = dilated_mix(own_states, own_pages, conv_weight, conv_bias)
    mixed_low = mixed.astype(bf16)
    other_pages = jnp.where(is_text, page_ids[1], page_ids[0])
    masks = jnp.pad(
        jnp.stack(
            [
                own_pages == shifted(own_pages, dilation, -1),
                own_pages == shifted(own_pages, -dilation, -1),
                other_pages == shifted(other_pages, dilation, -1),
                other_pages == shifted(other_pages, -dilation, -1),
            ],
            axis=1,
        ).astype(f32),
        ((0, 0), (0, LANES - 4)),
    )
    vectors = jnp.stack(
        [b_out, gain_one, bias_one, b_down, gain_two, bias_two, jnp.zeros_like(b_out), b_out]
    )
    biases = jnp.concatenate([b_query, jnp.zeros_like(b_value), b_value])[None]
    taps = jnp.pad(conv_weight, ((0, 5), (0, 0)))
    bias_up = b_up[None]
    if fast:
        split = (pack_rest.shape[1] * 2 // 3) // 256 * 256
        early = (features, own_feats, own_flip, tables, bounds, masks, vectors, biases, taps)
        parts_near = column_parts(after(half_columns(pack_rest[:, :split], is_text), column_qkv))
        w_down = after(w_down, column_qkv)
        pieces_qkv = half_pieces(column_qkv)
        column_near = jnp.stack([after(part, pieces_qkv[0]) for part in parts_near])
        parts_far = column_parts(after(pack_rest[:, split:], column_near))
        pieces_near = half_pieces(column_near)
        pieces_qkv[2] = after(pieces_qkv[2], pieces_near[0])
        pieces_qkv[3] = exchange(pieces_qkv[2], 1)
        groups_qkv = (("halves", 0),)
    else:
        groups_qkv = (("full", 0),)
        pieces_qkv = [lax.all_gather(pack_qkv, "page", axis=0, tiled=True)]
    full_down = lax.all_gather(w_down, "page", axis=0, tiled=True)

    other_mixed = dilated_mix(other_low.astype(f32), other_pages, conv_weight, conv_bias)
    other_mixed = other_mixed.astype(bf16)
    mixed_all = jnp.concatenate(
        [jnp.where(is_text, mixed_low, other_mixed), jnp.where(is_text, other_mixed, mixed_low)],
        axis=0,
    )
    if fast:
        pieces_qkv[0] = after(pieces_qkv[0], mixed_all, bias_up, *early)
    queries, keys_values, full_qkv, mixed_t = project(
        place, mixed_all, biases, groups_qkv, pieces_qkv
    )
    attend_in = queries
    if fast:
        column_far = jnp.stack([after(part, queries) for part in parts_far])
        across_far = exchange(column_far, 2)
        attend_in = after(queries, column_far)
    context = attend(bounds, attend_in, keys_values, features, own_feats, tables)
    if fast:
        pieces_near[2] = after(pieces_near[2], context)
        pieces_near[3] = exchange(pieces_near[2], 1)
        across_far = after(across_far, context)
        pieces_rest = pieces_near + row_pieces(column_far, across_far)
        groups_rest = (("halves", 0), ("rows", split))
    else:
        pieces_rest = [lax.all_gather(pack_rest, "page", axis=0, tiled=True)]
        groups_rest = (("full", 0),)
    unit, scale, normed_low, normed_t, context_t, active, active_t, slope, full_rest = up_forward(
        place, context, mixed, vectors, bias_up, groups_rest, pieces_rest
    )
    output_row, grad_sum_two, grad_ffn, small_two = down_forward(
        active, full_down, unit, vectors, cotangent[0, 0]
    )
    rows_down = grad_rows(active_t, grad_ffn)
    shard_down = lax.psum_scatter(rows_down, "page", scatter_dimension=0, tiled=True)
    grad_hidden, grad_b_up, grad_first, grad_branch, grad_context, small_one = ffn_back(
        after(grad_ffn, rows_down), slope, grad_sum_two, unit, scale, vectors, full_rest, full_down
    )
    attend_in = grad_context
    if fast:
        tiles = grad_hidden.shape[1] // d_model
        pairs = [
            (context_t, False, grad_branch, 0, 1),
            (normed_t, False, grad_hidden, 0, tiles // 2),
        ]
        keep_a, send_a = grad_by_columns(pairs, place, d_model)
        partner_a = exchange(send_a, 1)
        pairs = [(normed_t, False, after(grad_hidden, send_a), tiles // 2, tiles - tiles // 2)]
        keep_b, send_b = grad_by_columns(pairs, place, d_model)
        partner_b = exchange(send_b, 1)
        held_a, plane_a = halve_plane(place, keep_a, after(partner_a, send_b))
        far_a = swap(plane_a)
        held_b, plane_b = halve_plane(place, keep_b, after(partner_b, plane_a))
        far_b = swap(plane_b)
        attend_in = after(grad_context, plane_a, plane_b)
    else:
        shard_rest = summed_rows([(context_t, grad_branch), (normed_t, grad_hidden)])
    grad_queries, grad_keys, grad_values, grad_tables = attend_back(
        bounds, queries, keys_values, attend_in, features, own_feats, own_flip, tables
    )
    grad_keys_in, grad_queries_in = grad_keys, grad_queries
    if fast:
        far_a, far_b = after((far_a, far_b), grad_queries)
        held_rest, across_out = halve_two(held_a, far_a, held_b, far_b)
        across_rest = exchange(across_out, 2)
        grad_queries_in = after(grad_queries, across_out)
    pairs = [
        (mixed_t, True, grad_queries_in, 0, 1),
        (mixed_t, False, grad_keys, 0, 1),
        (mixed_t, False, grad_values, 0, 1),
    ]
    if fast:
        keep_qkv, send_qkv = grad_by_columns(pairs, place, d_model)
        partner_qkv = exchange(send_qkv, 1)
        grad_keys_in = after(grad_keys, send_qkv)
    else:
        shard_down = shard_down.astype(f32) + swap(shard_down).astype(f32)
        shard_qkv = summed_rows(
            [(mixed_low.T, grad_queries), (mixed_t, grad_keys), (mixed_t, grad_values)]
        )
    to_other = input_back(place, full_qkv, grad_keys_in, grad_values, ())
    from_other = swap(to_other)
    grad_values_in = grad_values
    if fast:
        partner_qkv = after(partner_qkv, to_other)
        held_qkv, across_out = halve_across(place, keep_qkv, partner_qkv)
        across_qkv = exchange(across_out, 2)
        grad_values_in = after(grad_values, across_out)
    own_part = input_back(place, full_qkv, grad_keys, grad_values_in, (grad_first, grad_queries))
    packed = small_sums(
        own_part,
        to_other,
        own_low,
        other_low,
        masks,
        grad_queries,
        grad_values,
        small_one,
        small_two,
        grad_b_up,
        grad_tables,
    )
    if fast:
        packed = both_sum(packed, 1)
        shard_down = after(shard_down, packed)
        across_rest = after(across_rest, packed, shard_down)
        shard_down = shard_down.astype(f32) + swap(shard_down).astype(f32)
        own_rest, sends_rest = column_sends(held_rest, across_rest)
        arrived_rest = column_arrivals(sends_rest)
        packed = after(packed, *sends_rest)
        packed = packed + swap(packed)
        from_other = after(from_other, packed)
    else:
        packed = lax.psum(packed, ("mod", "page"))
    grad_in = state_back(own_part, from_other, masks, taps)
    if fast:
        across_qkv = after(across_qkv, packed, grad_in)
        own_qkv, sends_qkv = column_sends(held_qkv, across_qkv)
        arrived_qkv = column_arrivals(sends_qkv)
    if fast:
        arrived_rest = [after(part, *sends_qkv) for part in arrived_rest]
        total_rest = column_total(own_rest, arrived_rest)
        far_rest = swap(total_rest)
        packed = both_sum(both_sum(after(packed, total_rest), 2), 4)
        arrived_qkv = [after(part, packed) for part in arrived_qkv]
        total_qkv = column_total(own_qkv, arrived_qkv)
        far_qkv = swap(total_qkv)
        packed = both_sum(after(packed, total_qkv), 8)
    g_tables = packed[28:34].reshape(HEADS, 3, LANES)
    if fast:
        cut = far_a.shape[2]
        first_plane = jnp.where(is_text, total_rest, far_rest)
        second_plane = jnp.where(is_text, far_rest, total_rest)
        shard_rest = jnp.concatenate(
            [first_plane[:, :cut], second_plane[:, :cut], first_plane[:, cut:], second_plane[:, cut:]],
            axis=1,
        ).astype(f32)
        shard_qkv = total_qkv.astype(f32) + far_qkv.astype(f32)
    return (
        output_row[None, None],
        grad_in[None, None],
        packed[0:3],
        packed[3],
        shard_qkv[:, :d_model],
        packed[4],
        shard_qkv[:, d_model : 2 * d_model],
        shard_qkv[:, 2 * d_model :],
        packed[5],
        shard_rest[:, :d_model],
        packed[10],
        g_tables[:, 0, : table_pos.shape[1]],
        g_tables[:, 1, 64 : 64 + table_x.shape[1]],
        g_tables[:, 2, 64 : 64 + table_y.shape[1]],
        packed[8],
        packed[9],
        shard_rest[:, d_model:],
        packed[24:28].reshape(d_ff),
        shard_down,
        packed[18],
        packed[16],
        packed[17],
    )


def solution(mesh):
    rows = P("mod", "page", None, None)
    ids = P("page", None)
    cut = P("page", None)
    return jax.shard_map(
        local,
        mesh=mesh,
        in_specs=(
            rows, rows, ids, ids, ids, P(), P(), cut, P(), cut, cut, P(), cut,
            P(), P(), P(), P(), P(), P(), cut, P(), cut, P(), P(), P(),
        ),
        out_specs=(
            rows, rows, P(), P(), cut, P(), cut, cut, P(), cut, P(), P(), P(),
            P(), P(), P(), cut, P(), cut, P(), P(), P(),
        ),
        check_vma=False,
    )
```

```python
import functools

import jax
import jax.numpy as jnp
import numpy as np
from jax import lax
from jax.experimental import pallas as pl
from jax.experimental.pallas import tpu as pltpu
from jax.sharding import PartitionSpec as P

HEADS = 12
HEAD = 64
GRID = 8
PAGES = 8
POS_BINS = 64
BOX_BINS = 32
PATCH = 64
TEXT = 512
PAIRS = HEADS // 2
LANES = 2 * HEAD
WINDOW = 144
SMALL = 96

dilation = 2
small_cost = pl.CostEstimate(flops=1000, bytes_accessed=1000, transcendentals=0)
norm_eps = 1e-05
mask_fill = -1000000000.0
erfc_poly = (
    0.2367515965428487,
    0.24062179898991767,
    0.18865103029313968,
    0.2877518531132804,
    -0.1648672439458568,
    0.4765735350541787,
    -0.34041833366480423,
    0.07493571514857543,
)
bf16 = jnp.bfloat16
f32 = jnp.float32


def shifted(values, offset, fill_value):
    padding = jnp.full((abs(offset),) + values.shape[1:], fill_value, values.dtype)
    if offset > 0:
        return jnp.concatenate([values[offset:], padding], axis=0)
    return jnp.concatenate([padding, values[:offset]], axis=0)


def dilated_mix(inputs, page_ids, conv_weight, conv_bias):
    summed = inputs + conv_bias + conv_weight[1] * inputs
    for tap_index, offset in ((0, -dilation), (2, dilation)):
        moved_rows = shifted(inputs, offset, 0.0)
        moved_pages = shifted(page_ids, offset, -1)
        same_page = (moved_pages == page_ids)[:, None]
        summed = summed + conv_weight[tap_index] * jnp.where(same_page, moved_rows, 0.0)
    return summed


def bin_features(pos_bins, bins_x, bins_y):
    return jnp.concatenate(
        [
            jax.nn.one_hot(pos_bins, POS_BINS, dtype=bf16),
            jax.nn.one_hot(bins_x, BOX_BINS, dtype=bf16),
            jax.nn.one_hot(bins_y, BOX_BINS, dtype=bf16),
        ],
        axis=1,
    )


def token_ids(text_pages, text_x, text_y):
    text_index = jnp.arange(TEXT, dtype=jnp.int32)
    text_pos = text_index * POS_BINS // TEXT
    patch_pos = text_index % PATCH * POS_BINS // PATCH
    patch_page = text_index // PATCH
    patch_x = text_index % GRID * BOX_BINS // GRID
    patch_y = text_index // GRID % GRID * BOX_BINS // GRID
    page_ids = jnp.stack([text_pages, patch_page])
    pos_bins = jnp.stack([text_pos, patch_pos])
    bins_x = jnp.stack([text_x, patch_x])
    bins_y = jnp.stack([text_y, patch_y])
    return (page_ids, pos_bins, bins_x, bins_y)


def plain_dot(left_side, right_side):
    return jnp.dot(left_side, right_side, preferred_element_type=f32)


def dot_left_t(left_side, right_side):
    return lax.dot_general(
        left_side, right_side, (((0,), (0,)), ((), ())), preferred_element_type=f32
    )


def dot_right_t(left_side, right_side):
    return lax.dot_general(
        left_side, right_side, (((1,), (1,)), ((), ())), preferred_element_type=f32
    )


def iota(shape, axis):
    return lax.broadcasted_iota(jnp.int32, shape, axis)


def bias_block(table_rows):
    pos_part = pltpu.roll(
        jnp.broadcast_to(table_rows[0:1], (POS_BINS, LANES)), 65, 1, stride=1, stride_axis=0
    )
    x_part = pltpu.roll(
        jnp.broadcast_to(table_rows[1:2], (BOX_BINS, LANES)), 33, 1, stride=1, stride_axis=0
    )
    y_part = pltpu.roll(
        jnp.broadcast_to(table_rows[2:3], (BOX_BINS, LANES)), 65, 1, stride=1, stride_axis=0
    )
    lane = iota((POS_BINS, LANES), 1)
    pos_part = jnp.where(lane < POS_BINS, pos_part, 0.0)
    lane = iota((BOX_BINS, LANES), 1)
    x_part = jnp.where((lane >= 64) & (lane < 96), x_part, 0.0)
    y_part = jnp.where(lane >= 96, y_part, 0.0)
    return jnp.concatenate([pos_part, x_part, y_part], axis=0).astype(bf16)


def diagonal_sums(grad_block):
    lane = iota((POS_BINS, LANES), 1)
    pos_part = jnp.where(lane < POS_BINS, grad_block[:64], 0.0)
    lane = iota((BOX_BINS, LANES), 1)
    x_part = jnp.where((lane >= 64) & (lane < 96), grad_block[64:96], 0.0)
    y_part = jnp.where(lane >= 96, grad_block[96:], 0.0)
    pos_part = pltpu.roll(pos_part, 0, 1, stride=1, stride_axis=0)
    x_part = pltpu.roll(x_part, 0, 1, stride=1, stride_axis=0)
    y_part = pltpu.roll(y_part, 96, 1, stride=1, stride_axis=0)
    rows = [jnp.sum(part, axis=0, keepdims=True) for part in (pos_part, x_part, y_part)]
    return jnp.concatenate(rows + [jnp.zeros((5, LANES), f32)], axis=0)


def stacked_heads(rows, low_lane):
    zero = jnp.zeros_like(rows)
    return jnp.concatenate(
        [jnp.where(low_lane, rows, zero), jnp.where(low_lane, zero, rows)], axis=0
    )


def window_start(first, window):
    return pl.multiple_of(jnp.minimum(first // 16 * 16, TEXT - window), 16)


def fits(first, end, window):
    return end - jnp.minimum(first // 16 * 16, TEXT - window) <= window


def for_each_page(bounds, step):
    def body(page, carry):
        own_low, own_high = bounds[page], bounds[PAGES + page]
        key_low, key_high = bounds[2 * PAGES + page], bounds[3 * PAGES + page]
        own_small = fits(own_low, own_high, SMALL)
        key_small = fits(key_low, key_high, SMALL)
        span = (own_low, own_high, key_low, key_high)
        small = own_small & key_small
        for chosen, own_window, key_window in (
            (small, SMALL, SMALL),
            (~small, WINDOW, WINDOW),
        ):

            @pl.when(chosen)
            def _():
                step(page, span, own_window, key_window)

        return carry

    lax.fori_loop(0, PAGES, body, 0)


def page_operands(page, span, own_window, key_window, pair, q_ref, k_ref, feat_ref, lookup):
    own_at = window_start(span[0], own_window)
    key_at = window_start(span[2], key_window)
    own_rows, text_rows = pl.ds(own_at, own_window), pl.ds(key_at, key_window)
    patch_at = TEXT + PATCH * page
    if not isinstance(page, int):
        patch_at = pl.multiple_of(patch_at, PATCH)
    patch_rows = pl.ds(patch_at, PATCH)
    lanes = slice(pair * LANES, (pair + 1) * LANES)
    low_lane = iota((own_window, LANES), 1) < HEAD
    queries = stacked_heads(q_ref[own_rows, lanes], low_lane)
    first = 2 * pair * LANES
    rel = jnp.concatenate(
        [
            lookup[own_rows, first : first + LANES],
            lookup[own_rows, first + LANES : first + 2 * LANES],
        ],
        axis=0,
    )
    query_side = jnp.concatenate([rel, queries], axis=1)
    key_side = jnp.concatenate(
        [
            jnp.concatenate([feat_ref[text_rows, :], k_ref[text_rows, lanes]], axis=1),
            jnp.concatenate([feat_ref[patch_rows, :], k_ref[patch_rows, lanes]], axis=1),
        ],
        axis=0,
    )
    own_row = iota((own_window, LANES), 0) + own_at
    own_ok = (own_row >= span[0]) & (own_row < span[1])
    return (
        lanes, low_lane, own_ok, queries, query_side, key_side, own_rows, text_rows, patch_rows, key_at
    )


def set_lookup(lookup, own_feat_ref, table_ref):
    blocks = [bias_block(table_ref[head]) for head in range(table_ref.shape[0])]
    product = jnp.dot(
        own_feat_ref[...], jnp.concatenate(blocks, axis=1), preferred_element_type=f32
    )
    lookup[...] = product.astype(bf16)


def attend_kernel(bounds, q_ref, k_ref, v_ref, feat_ref, own_feat_ref, table_ref, context_ref, lookup):
    set_lookup(lookup, own_feat_ref, table_ref)

    def step(page, span, own_window, key_window):
        column = iota((1, key_window + PATCH), 1)
        key_row = column + window_start(span[2], key_window)
        key_ok = (column >= key_window) | ((key_row >= span[2]) & (key_row < span[3]))
        for pair in range(q_ref.shape[1] // LANES):
            lanes, low_lane, own_ok, _, query_side, key_side, own_rows, text_rows, patch_rows, _ = (
                page_operands(
                    page, span, own_window, key_window, pair, q_ref, k_ref, feat_ref, lookup
                )
            )
            scores = jnp.where(key_ok, dot_right_t(query_side, key_side), mask_fill)
            row_max = jnp.max(scores, axis=1, keepdims=True)
            weights = jnp.exp(scores - row_max)
            total = jnp.sum(weights, axis=1, keepdims=True)
            prob = (weights * (1.0 / total)).astype(bf16)
            values = jnp.concatenate([v_ref[text_rows, lanes], v_ref[patch_rows, lanes]], axis=0)
            mixed = jnp.dot(prob, values, preferred_element_type=f32)
            picked = jnp.where(low_lane, mixed[:own_window], mixed[own_window:])
            before = context_ref[own_rows, lanes].astype(f32)
            context_ref[own_rows, lanes] = jnp.where(own_ok, picked, before).astype(bf16)

    for page in range(PAGES):
        span = [bounds[part * PAGES + page] for part in range(4)]
        step(page, span, WINDOW, WINDOW)


def attend_back_kernel(
    bounds,
    q_ref,
    k_ref,
    v_ref,
    grad_ref,
    feat_ref,
    own_feat_ref,
    flip_feat_ref,
    table_ref,
    grad_q_ref,
    grad_k_ref,
    grad_v_ref,
    grad_table_ref,
    lookup,
    grad_lookup,
):
    set_lookup(lookup, own_feat_ref, table_ref)

    def step(page, span, own_window, key_window):
        row = iota((key_window + PATCH, 1), 0)
        key_row = row + window_start(span[2], key_window)
        key_ok = (row >= key_window) | ((key_row >= span[2]) & (key_row < span[3]))
        for pair in range(q_ref.shape[1] // LANES):
            lanes, low_lane, own_ok, queries, query_side, key_side, own_rows, text_rows, patch_rows, key_at = (
                page_operands(
                    page, span, own_window, key_window, pair, q_ref, k_ref, feat_ref, lookup
                )
            )
            scores = jnp.where(key_ok, dot_right_t(key_side, query_side), mask_fill)
            col_max = jnp.max(scores, axis=0, keepdims=True)
            weights = jnp.exp(scores - col_max)
            total = jnp.sum(weights, axis=0, keepdims=True)
            prob = weights * (1.0 / total)
            grad_rows = grad_ref[own_rows, lanes]
            grad_rows = jnp.where(own_ok, grad_rows, jnp.zeros_like(grad_rows))
            grads = stacked_heads(grad_rows, low_lane)
            values = jnp.concatenate([v_ref[text_rows, lanes], v_ref[patch_rows, lanes]], axis=0)
            grad_prob = dot_right_t(values, grads)
            inner = jnp.sum(prob * grad_prob, axis=0, keepdims=True)
            grad_scores = (prob * (grad_prob - inner)).astype(bf16)
            grad_v = jnp.dot(prob.astype(bf16), grads, preferred_element_type=f32)
            grad_k = jnp.dot(grad_scores, queries, preferred_element_type=f32)
            back = dot_left_t(grad_scores, key_side)
            low, high = back[:own_window], back[own_window:]
            grad_q = jnp.where(low_lane, low[:, LANES:], high[:, LANES:]) * 0.125
            before = grad_q_ref[own_rows, lanes].astype(f32)
            grad_q_ref[own_rows, lanes] = jnp.where(own_ok, grad_q, before).astype(bf16)
            first = 2 * pair * LANES
            for part, at in ((low, first), (high, first + LANES)):
                place_at = slice(at, at + LANES)
                grad_lookup[own_rows, place_at] = jnp.where(
                    own_ok, part[:, :LANES], grad_lookup[own_rows, place_at]
                )
            wide_row = iota((key_window, LANES), 0) + key_at
            text_ok = (wide_row >= span[2]) & (wide_row < span[3])
            for grad, ref in ((grad_k, grad_k_ref), (grad_v, grad_v_ref)):
                before = ref[text_rows, lanes].astype(f32)
                ref[text_rows, lanes] = jnp.where(text_ok, grad[:key_window], before).astype(bf16)
                ref[patch_rows, lanes] = grad[key_window:].astype(bf16)

    for_each_page(bounds, step)
    grad_high = grad_lookup[...].astype(bf16)
    grad_rest = (grad_lookup[...] - grad_high.astype(f32)).astype(bf16)
    flip = flip_feat_ref[...]
    grad_block = dot_left_t(flip, grad_high) + dot_left_t(flip, grad_rest)
    for head in range(table_ref.shape[0]):
        grad_table_ref[head] = diagonal_sums(grad_block[:, head * LANES : (head + 1) * LANES])


def column_spec(rows, group, first=0):
    return pl.BlockSpec((rows, group * LANES), lambda step, bounds: (0, step + first))


def whole_spec(rows):
    return pl.BlockSpec((rows, LANES), lambda step, bounds: (0, 0))


def tables_spec(group):
    return pl.BlockSpec((2 * group, 8, LANES), lambda step, bounds: (step, 0, 0))


def attend(bounds, queries, keys_values, features, own_features, tables):
    group = 1
    return pl.pallas_call(
        attend_kernel,
        grid_spec=pltpu.PrefetchScalarGridSpec(
            num_scalar_prefetch=1,
            grid=(PAIRS // group,),
            in_specs=[
                column_spec(TEXT, group),
                column_spec(2 * TEXT, group),
                column_spec(2 * TEXT, group, PAIRS // group),
                whole_spec(2 * TEXT),
                whole_spec(TEXT),
                tables_spec(group),
            ],
            out_specs=column_spec(TEXT, group),
            scratch_shapes=[pltpu.VMEM((TEXT, 2 * group * LANES), bf16)],
        ),
        out_shape=jax.ShapeDtypeStruct((TEXT, HEADS * HEAD), bf16),
        cost_estimate=small_cost,
        name="attend",
    )(bounds, queries, keys_values, keys_values, features, own_features, tables)


def attend_back(
    bounds, queries, keys_values, grad_context, features, own_features, flip, tables
):
    group = 6
    return pl.pallas_call(
        attend_back_kernel,
        grid_spec=pltpu.PrefetchScalarGridSpec(
            num_scalar_prefetch=1,
            grid=(PAIRS // group,),
            in_specs=[
                column_spec(TEXT, group),
                column_spec(2 * TEXT, group),
                column_spec(2 * TEXT, group, PAIRS // group),
                column_spec(TEXT, group),
                whole_spec(2 * TEXT),
                whole_spec(TEXT),
                whole_spec(TEXT),
                tables_spec(group),
            ],
            out_specs=[
                column_spec(TEXT, group),
                column_spec(2 * TEXT, group),
                column_spec(2 * TEXT, group),
                tables_spec(group),
            ],
            scratch_shapes=[
                pltpu.VMEM((TEXT, 2 * group * LANES), bf16),
                pltpu.VMEM((TEXT, 2 * group * LANES), f32),
            ],
        ),
        out_shape=[
            jax.ShapeDtypeStruct((TEXT, HEADS * HEAD), bf16),
            jax.ShapeDtypeStruct((2 * TEXT, HEADS * HEAD), bf16),
            jax.ShapeDtypeStruct((2 * TEXT, HEADS * HEAD), bf16),
            jax.ShapeDtypeStruct((HEADS, 8, LANES), f32),
        ],
        cost_estimate=small_cost,
        name="attend_back",
    )(
        bounds,
        queries,
        keys_values,
        keys_values,
        grad_context,
        features,
        own_features,
        flip,
        tables,
    )


def exchange(values, mask):
    count = lax.axis_size("page")
    return lax.ppermute(values, "page", [(i, i ^ mask) for i in range(count)])


def after(value, *earlier):
    return lax.optimization_barrier((value, *earlier))[0]


def slot_mask(slot):
    return (slot & 3) * 4 + (slot >> 2) * 2


def project_kernel(groups, place, mixed_ref, bias_ref, *refs):
    *pieces, query_ref, both_ref, weight_ref, mixed_t_ref, sems = refs
    width = mixed_ref.shape[1]
    tokens = query_ref.shape[0]
    copies = start_rows(place, groups, pieces, weight_ref, sems)
    mixed_t_ref[...] = mixed_ref[...].T
    for copy in copies:
        copy.wait()
    own = mixed_ref[pl.ds(pl.multiple_of(place[1] * tokens, 16), tokens), :]
    queries = jnp.dot(own, weight_ref[:, :width], preferred_element_type=f32) + bias_ref[:, :width]
    query_ref[...] = (queries.astype(bf16).astype(f32) * 0.125).astype(bf16)
    for part in range(2):
        rows = pl.ds(part * tokens, tokens)
        for column in (1, 2):
            at = slice(column * width, (column + 1) * width)
            out = slice((column - 1) * width, column * width)
            values = jnp.dot(mixed_ref[rows, :], weight_ref[:, at], preferred_element_type=f32)
            both_ref[rows, out] = (values + bias_ref[:, at]).astype(bf16)


def project(place, mixed, biases, groups, pieces):
    rows, width = mixed.shape
    vmem = pl.BlockSpec(memory_space=pltpu.VMEM)
    return pl.pallas_call(
        functools.partial(project_kernel, groups),
        grid_spec=pltpu.PrefetchScalarGridSpec(
            num_scalar_prefetch=1,
            grid=(),
            in_specs=[vmem] * 2 + any_specs(len(pieces)),
            out_specs=[vmem] * 4,
            scratch_shapes=[pltpu.SemaphoreType.DMA((32,))],
        ),
        out_shape=[
            jax.ShapeDtypeStruct((rows // 2, width), bf16),
            jax.ShapeDtypeStruct((rows, 2 * width), bf16),
            jax.ShapeDtypeStruct((width, 3 * width), bf16),
            jax.ShapeDtypeStruct((width, rows), bf16),
        ],
        cost_estimate=small_cost,
        compiler_params=pltpu.CompilerParams(vmem_limit_bytes=16 << 20),
        name="project",
    )(place, mixed, biases, *pieces)


def column_parts(shard):
    return [shard] + [exchange(shard, 4 * step) for step in (1, 2, 3)]


def half_pieces(column):
    eight = jnp.concatenate([column, exchange(column, 2)])
    far = swap(eight)
    return [eight, exchange(eight, 1), far, exchange(far, 1)]


def row_pieces(column, across):
    return [column, exchange(column, 1), across, exchange(across, 1)]


def column_pairs(shard):
    far = exchange(shard, 8)
    near = exchange(jnp.stack([shard, far]), 4)
    return [shard, near[0], far, near[1]]


def column_of(shard):
    return jnp.stack(column_parts(shard))


def row_copies(place, groups, refs, full, sems, first=0):
    copies = []
    for kind, column in groups:
        if kind == "full":
            piece, *refs = refs
            width = piece.shape[1]
            target = full.at[:, pl.ds(column, width)]
            copies.append(pltpu.make_async_copy(piece, target, sems.at[first + len(copies)]))
            continue
        pieces, refs = refs[:4], refs[4:]
        _, rows, width = pieces[0].shape
        for index in range(32 if kind == "halves" else 16):
            at = column
            if kind == "halves":
                source, slot = index >> 3, index & 7
                mask = slot_mask(slot) + (source & 1)
                at = pl.multiple_of(column + (place[1] ^ (source >> 1)) * width, 128)
            else:
                source, slot = index & 3, index >> 2
                mask = slot * 4 + source
            row = pl.multiple_of((place[0] ^ mask) * rows, 16)
            copies.append(
                pltpu.make_async_copy(
                    pieces[source].at[slot],
                    full.at[pl.ds(row, rows), pl.ds(at, width)],
                    sems.at[first + len(copies)],
                )
            )
    return copies


def start_rows(place, groups, refs, full, sems):
    copies = row_copies(place, groups, refs, full, sems)
    for copy in copies:
        copy.start()
    return copies


def gelu_parts(values):
    size = jnp.abs(values)
    t = 1.0 / (1.0 + (0.42 * 0.7071067811865476) * size)
    poly = jnp.full_like(t, erfc_poly[-1])
    for coefficient in erfc_poly[-2::-1]:
        poly = poly * t + coefficient
    bell = jnp.exp(-0.5 * values * values)
    tail = (0.5 * t) * (poly * bell)
    cdf = jnp.where(values >= 0.0, 1.0 - tail, tail)
    return values * cdf, cdf + (values * 0.3989422804014327) * bell


def normalized(values):
    centered = values - jnp.mean(values, axis=1, keepdims=True)
    variance = jnp.mean(centered * centered, axis=1, keepdims=True)
    scale = lax.rsqrt(variance + norm_eps)
    return centered * scale, scale


def norm_back(grads, unit, scale, gain):
    scaled = grads * gain
    mean = jnp.mean(scaled, axis=1, keepdims=True)
    inner = jnp.mean(scaled * unit, axis=1, keepdims=True)
    return scale * (scaled - mean - unit * inner)


def up_kernel(groups, place, context_ref, mixed_ref, vec_ref, bias_ref, *refs):
    *pieces, unit_ref, scale_ref, low_t_ref, context_t_ref = refs[:-9]
    active_ref, active_t_ref, slope_ref, full_ref = refs[-9:-5]
    weight, hidden, low, sems, full_sem = refs[-5:]
    step = pl.program_id(0)
    tiles = pl.num_programs(0) - 1
    width = context_ref.shape[1]
    tile = active_ref.shape[1]
    last_group = 16 if len(groups) > 1 else 0

    def full_copy():
        return pltpu.make_async_copy(weight, full_ref, full_sem)

    @pl.when(step == 0)
    def _():
        copies = row_copies(place, groups, pieces, weight, sems)
        for copy in copies:
            copy.start()
        context_t_ref[...] = context_ref[...].T
        for copy in copies[: len(copies) - last_group]:
            copy.wait()
        branch = jnp.dot(context_ref[...], weight[:, :width], preferred_element_type=f32)
        unit, scale = normalized(mixed_ref[...] + branch + vec_ref[0:1])
        unit_ref[...] = unit
        scale_ref[...] = jnp.broadcast_to(scale, scale_ref.shape)
        normed = (unit * vec_ref[1:2] + vec_ref[2:3]).astype(bf16)
        low[...] = normed
        low_t_ref[...] = normed.T

    @pl.when(step == 1)
    def _():
        if last_group:
            for copy in row_copies(place, groups[1:], pieces[4:], weight, sems, 32):
                copy.wait()
        full_copy().start()

    def product():
        at = pl.multiple_of(width + step * tile, 128)
        return jnp.dot(low[...], weight[:, pl.ds(at, tile)], preferred_element_type=f32)

    def activate():
        active, slope = gelu_parts(hidden[(step + 1) % 2] + bias_ref[...])
        active = active.astype(bf16)
        active_ref[...] = active
        active_t_ref[...] = active.T
        slope_ref[...] = slope.astype(bf16)

    @pl.when(step == 0)
    def _():
        hidden[step % 2] = product()

    @pl.when((step > 0) & (step < tiles))
    def _():
        hidden[step % 2] = product()
        activate()

    @pl.when(step == tiles)
    def _():
        activate()
        full_copy().wait()


def any_specs(count):
    return [pl.BlockSpec(memory_space=pl.ANY)] * count


def up_forward(place, context, mixed, vectors, bias_up, groups, pieces):
    tokens, width = mixed.shape
    hidden_width = bias_up.shape[1]
    tile = 768
    whole = lambda step, place: (0, 0)
    last = lambda step, place: (0, jnp.maximum(step - 1, 0))
    last_t = lambda step, place: (jnp.maximum(step - 1, 0), 0)
    return pl.pallas_call(
        functools.partial(up_kernel, groups),
        grid_spec=pltpu.PrefetchScalarGridSpec(
            num_scalar_prefetch=1,
            grid=(hidden_width // tile + 1,),
            in_specs=[
                pl.BlockSpec((tokens, width), whole),
                pl.BlockSpec((tokens, width), whole),
                pl.BlockSpec(vectors.shape, whole),
                pl.BlockSpec((1, tile), last),
            ]
            + any_specs(len(pieces)),
            out_specs=[
                pl.BlockSpec((tokens, width), whole),
                pl.BlockSpec((tokens, 128), whole),
                pl.BlockSpec((width, tokens), whole),
                pl.BlockSpec((width, tokens), whole),
                pl.BlockSpec((tokens, tile), last),
                pl.BlockSpec((tile, tokens), last_t),
                pl.BlockSpec((tokens, tile), last),
                pl.BlockSpec(memory_space=pl.ANY),
            ],
            scratch_shapes=[
                pltpu.VMEM((width, width + hidden_width), bf16),
                pltpu.VMEM((2, tokens, tile), f32),
                pltpu.VMEM((tokens, width), bf16),
                pltpu.SemaphoreType.DMA((48,)),
                pltpu.SemaphoreType.DMA,
            ],
        ),
        out_shape=[
            jax.ShapeDtypeStruct((tokens, width), f32),
            jax.ShapeDtypeStruct((tokens, 128), f32),
            jax.ShapeDtypeStruct((width, tokens), bf16),
            jax.ShapeDtypeStruct((width, tokens), bf16),
            jax.ShapeDtypeStruct((tokens, hidden_width), bf16),
            jax.ShapeDtypeStruct((hidden_width, tokens), bf16),
            jax.ShapeDtypeStruct((tokens, hidden_width), bf16),
            jax.ShapeDtypeStruct((width, width + hidden_width), bf16),
        ],
        cost_estimate=small_cost,
        name="up_forward",
    )(place, context, mixed, vectors, bias_up, *pieces)


def down_kernel(active_ref, weight_ref, unit_ref, vec_ref, grad_ref, *refs):
    out_ref, sum_ref, low_ref, small_ref, total = refs
    step = pl.program_id(0)
    product = jnp.dot(active_ref[...], weight_ref[...], preferred_element_type=f32)

    @pl.when(step == 0)
    def _():
        total[...] = product

    @pl.when(step > 0)
    def _():
        total[...] += product

    @pl.when(step == pl.num_programs(0) - 1)
    def _():
        tokens, width = unit_ref.shape
        half = tokens // 2
        smalls = [jnp.zeros((1, width), f32)] * 3
        for part in range(2):
            rows = pl.ds(part * half, half)
            normed = unit_ref[rows, :] * vec_ref[1:2] + vec_ref[2:3]
            unit, scale = normalized(normed + total[rows, :] + vec_ref[3:4])
            out_ref[rows, :] = (unit * vec_ref[4:5] + vec_ref[5:6]).astype(bf16)
            grads = grad_ref[rows, :].astype(f32)
            back = norm_back(grads, unit, scale, vec_ref[4:5])
            low = back.astype(bf16)
            sum_ref[rows, :] = back
            low_ref[rows, :] = low
            for index, term in enumerate((grads * unit, grads, low.astype(f32))):
                smalls[index] = smalls[index] + jnp.sum(term, axis=0, keepdims=True)
        small_ref[...] = jnp.concatenate(smalls + [jnp.zeros((5, width), f32)], axis=0)


def down_forward(active, weight, unit, vectors, grads):
    tokens, width = unit.shape
    hidden_width = active.shape[1]
    tile = 1536
    whole = lambda step: (0, 0)
    token_block = pl.BlockSpec((tokens, width), whole)
    return pl.pallas_call(
        down_kernel,
        grid=(hidden_width // tile,),
        in_specs=[
            pl.BlockSpec((tokens, tile), lambda step: (0, step)),
            pl.BlockSpec((tile, width), lambda step: (step, 0)),
            token_block,
            pl.BlockSpec(vectors.shape, whole),
            token_block,
        ],
        out_specs=[token_block] * 3 + [pl.BlockSpec((8, width), whole)],
        scratch_shapes=[pltpu.VMEM((tokens, width), f32)],
        out_shape=[
            jax.ShapeDtypeStruct((tokens, width), bf16),
            jax.ShapeDtypeStruct((tokens, width), f32),
            jax.ShapeDtypeStruct((tokens, width), bf16),
            jax.ShapeDtypeStruct((8, width), f32),
        ],
        cost_estimate=small_cost,
        name="down_forward",
    )(active, weight, unit, vectors, grads)


def ffn_back_kernel(*refs):
    low_ref, slope_ref, sum_ref, unit_ref, scale_ref, vec_ref = refs[:6]
    down_ref, up_ref, out_weight_ref = refs[6:9]
    hidden_ref, bias_ref, first_ref, branch_ref, context_ref, small_ref, total = refs[9:]
    step = pl.program_id(0)
    tokens, width = unit_ref.shape
    tile = slope_ref.shape[1]
    half = tokens // 2

    @pl.when(step == 0)
    def _():
        total[...] = sum_ref[...]

    bias = jnp.zeros((1, tile), f32)
    for part in range(2):
        rows = pl.ds(part * half, half)
        grads = dot_right_t(low_ref[rows, :], down_ref[...]) * slope_ref[rows, :].astype(f32)
        grads = grads.astype(bf16)
        hidden_ref[rows, :] = grads
        bias = bias + jnp.sum(grads.astype(f32), axis=0, keepdims=True)
        total[rows, :] += dot_right_t(grads, up_ref[...])
    bias_ref[...] = bias

    @pl.when(step == pl.num_programs(0) - 1)
    def _():
        grads = total[...]
        unit = unit_ref[...]
        first = norm_back(grads, unit, scale_ref[:, 0:1], vec_ref[1:2])
        branch = first.astype(bf16)
        first_ref[...] = first
        branch_ref[...] = branch
        context_ref[...] = dot_right_t(branch, out_weight_ref[...]).astype(bf16)
        smalls = [
            jnp.sum(term, axis=0, keepdims=True)
            for term in (grads * unit, grads, branch.astype(f32))
        ]
        small_ref[...] = jnp.concatenate(smalls + [jnp.zeros((5, width), f32)], axis=0)


def ffn_back(low, slope, total, unit, scale, vectors, full_rest, full_down):
    tokens, width = unit.shape
    hidden_width = slope.shape[1]
    tile = 768
    whole = lambda step: (0, 0)
    column = lambda step: (0, step)
    token_block = pl.BlockSpec((tokens, width), whole)
    return pl.pallas_call(
        ffn_back_kernel,
        grid=(hidden_width // tile,),
        in_specs=[
            token_block,
            pl.BlockSpec((tokens, tile), column),
            token_block,
            token_block,
            pl.BlockSpec((tokens, 128), whole),
            pl.BlockSpec(vectors.shape, whole),
            pl.BlockSpec((tile, width), lambda step: (step, 0)),
            pl.BlockSpec((width, tile), lambda step: (0, step + 1)),
            pl.BlockSpec((width, width), whole),
        ],
        out_specs=[
            pl.BlockSpec((tokens, tile), column),
            pl.BlockSpec((1, tile), column),
            token_block,
            token_block,
            token_block,
            pl.BlockSpec((8, width), whole),
        ],
        scratch_shapes=[pltpu.VMEM((tokens, width), f32)],
        out_shape=[
            jax.ShapeDtypeStruct((tokens, hidden_width), bf16),
            jax.ShapeDtypeStruct((1, hidden_width), f32),
            jax.ShapeDtypeStruct((tokens, width), f32),
            jax.ShapeDtypeStruct((tokens, width), bf16),
            jax.ShapeDtypeStruct((tokens, width), bf16),
            jax.ShapeDtypeStruct((8, width), f32),
        ],
        cost_estimate=small_cost,
        name="ffn_back",
    )(low, slope, total, unit, scale, vectors, full_down, full_rest, full_rest)


def grad_rows_kernel(x_ref, h_ref, out_ref):
    out_ref[...] = jnp.dot(x_ref[...], h_ref[...], preferred_element_type=f32).astype(bf16)


def grad_rows(inputs_t, grads):
    width, tokens = inputs_t.shape
    columns = grads.shape[1]
    return pl.pallas_call(
        grad_rows_kernel,
        grid=(4,),
        in_specs=[
            pl.BlockSpec((width // 4, tokens), lambda step: (step, 0)),
            pl.BlockSpec((tokens, columns), lambda step: (0, 0)),
        ],
        out_specs=pl.BlockSpec((width // 4, columns), lambda step: (step, 0)),
        out_shape=jax.ShapeDtypeStruct((width, columns), bf16),
        cost_estimate=small_cost,
        name="grad_rows",
    )(inputs_t, grads)


def grad_columns_kernel(parts, place, *refs):
    count = len(parts)
    ins, keep_ref, send_ref, scratch = (
        refs[: 2 * count],
        refs[2 * count],
        refs[2 * count + 1],
        refs[2 * count + 2 :],
    )
    rows, tile = keep_ref.shape[1], keep_ref.shape[2]
    step = pl.program_id(0)
    first = 0
    for index, steps in enumerate(parts):
        x_ref, h_ref, ordered = ins[2 * index], ins[2 * index + 1], scratch[index]

        @pl.when(step == first)
        def _():
            for slot in range(16):
                mask = slot_mask(slot & 7) + (slot >> 3)
                at = pl.multiple_of((place[0] ^ mask) * rows, 16)
                ordered[pl.ds(slot * rows, rows), :] = x_ref[pl.ds(at, rows), :]

        @pl.when((step >= first) & (step < first + steps))
        def _():
            product = jnp.dot(ordered[...], h_ref[...], preferred_element_type=f32).astype(bf16)
            keep_ref[...] = product[: 8 * rows].reshape(8, rows, tile)
            send_ref[...] = product[8 * rows :].reshape(8, rows, tile)

        first = first + steps


def grad_by_columns(pairs, place, tile):
    width = pairs[0][0].shape[0]
    rows = width // 16
    parts = tuple(count for *_, count in pairs)
    steps = sum(parts)
    specs = []
    operands = []
    scratch = []
    first = 0
    for inputs_t, own, grads, start, count in pairs:
        tokens = grads.shape[0]
        block = (lambda step, place: (0, place[1])) if own else (lambda step, place: (0, 0))
        specs.append(pl.BlockSpec((width, tokens), block))

        def column(step, place, first=first, start=start, count=count):
            return (0, start + jnp.clip(step - first, 0, count - 1))

        specs.append(pl.BlockSpec((tokens, tile), column))
        operands += [inputs_t, grads]
        scratch.append(pltpu.VMEM((width, tokens), bf16))
        first = first + count
    half = jax.ShapeDtypeStruct((8, rows, steps * tile), bf16)
    return pl.pallas_call(
        functools.partial(grad_columns_kernel, parts),
        grid_spec=pltpu.PrefetchScalarGridSpec(
            num_scalar_prefetch=1,
            grid=(steps,),
            in_specs=specs,
            out_specs=[pl.BlockSpec((8, rows, tile), lambda step, place: (0, 0, step))] * 2,
            scratch_shapes=scratch,
        ),
        out_shape=[half, half],
        cost_estimate=small_cost,
        compiler_params=pltpu.CompilerParams(vmem_limit_bytes=16 << 20),
        name="grad_columns",
    )(place, *operands)


def key_back_kernel(place, gk_ref, gv_ref, wk_ref, wv_ref, out_ref):
    total = dot_right_t(gk_ref[...], wk_ref[...]) + dot_right_t(gv_ref[...], wv_ref[...])
    out_ref[...] = total.astype(out_ref.dtype)


def own_back_kernel(place, first_ref, gq_ref, gk_ref, gv_ref, wq_ref, wk_ref, wv_ref, out_ref):
    total = dot_right_t(gk_ref[...], wk_ref[...]) + dot_right_t(gv_ref[...], wv_ref[...])
    out_ref[...] = first_ref[...] + total + dot_right_t(gq_ref[...], wq_ref[...])


def input_back(place, weights, grad_keys, grad_values, others):
    width = weights.shape[0]
    tokens = grad_keys.shape[0] // 2
    whole = pl.BlockSpec((tokens, width), lambda step, place: (0, 0))
    row = lambda step, place: ((place[1] if others else 1 - place[1]), 0)
    if others:
        kernel, leading, first, dtype = own_back_kernel, [whole, whole], 0, f32
    else:
        kernel, leading, first, dtype = key_back_kernel, [], 1, bf16
    operands = list(others) + [grad_keys, grad_values] + [weights] * (3 - first)
    specs = [pl.BlockSpec((tokens, width), row)] * 2
    for block in range(first, 3):
        specs.append(pl.BlockSpec((width, width), lambda step, place, block=block: (0, block)))
    return pl.pallas_call(
        kernel,
        grid_spec=pltpu.PrefetchScalarGridSpec(
            num_scalar_prefetch=1, grid=(1,), in_specs=leading + specs, out_specs=whole
        ),
        out_shape=jax.ShapeDtypeStruct((tokens, width), dtype),
        cost_estimate=small_cost,
        compiler_params=pltpu.CompilerParams(vmem_limit_bytes=16 << 20),
        name="input_back",
    )(place, *operands)


def back_rows(values, mask):
    return jnp.where(mask, pltpu.roll(values, dilation, 0), 0.0)


def ahead_rows(values, mask):
    return jnp.where(mask, pltpu.roll(values, values.shape[0] - dilation, 0), 0.0)


def tap_sums(grads, inputs, ahead, back):
    terms = (grads * back_rows(inputs, back), grads * inputs, grads * ahead_rows(inputs, ahead), grads)
    return [jnp.sum(term, axis=0, keepdims=True) for term in terms]


def small_sums_kernel(
    own_ref, other_ref, x_ref, x_other_ref, mask_ref, gq_ref, gv_ref, one_ref, two_ref, up_ref, table_ref, out_ref
):
    width = own_ref.shape[1]
    mask = mask_ref[...] > 0.0
    own = tap_sums(own_ref[...], x_ref[...].astype(f32), mask[:, 0:1], mask[:, 1:2])
    other = tap_sums(
        other_ref[...].astype(f32), x_other_ref[...].astype(f32), mask[:, 2:3], mask[:, 3:4]
    )
    rows = [a + b for a, b in zip(own, other)]
    for ref in (gq_ref, gv_ref):
        rows.append(jnp.sum(ref[...].astype(f32), axis=0, keepdims=True))
    rows.append(jnp.zeros((2, width), f32))
    out_ref[0:8] = jnp.concatenate(rows, axis=0)
    out_ref[8:16] = one_ref[...]
    out_ref[16:24] = two_ref[...]
    count = up_ref.shape[1] // width
    for index in range(count):
        out_ref[24 + index : 25 + index] = up_ref[:, index * width : (index + 1) * width]
    for index in range(3 * HEADS):
        row, lane = 28 + index // 6, index % 6 * LANES
        table = table_ref[index // 3]
        out_ref[row : row + 1, lane : lane + LANES] = table[index % 3 : index % 3 + 1]
    out_ref[34:40] = jnp.zeros((6, width), f32)


def small_sums(*operands):
    return pl.pallas_call(
        small_sums_kernel,
        out_shape=jax.ShapeDtypeStruct((40, operands[0].shape[1]), f32),
        cost_estimate=small_cost,
        compiler_params=pltpu.CompilerParams(vmem_limit_bytes=24 << 20),
        name="small_sums",
    )(*operands)


def state_back_kernel(own_ref, other_ref, mask_ref, tap_ref, out_ref):
    grads = own_ref[...] + other_ref[...].astype(f32)
    mask = mask_ref[...] > 0.0
    total = grads + tap_ref[1:2] * grads
    total = total + tap_ref[0:1] * ahead_rows(grads, mask[:, 0:1])
    total = total + tap_ref[2:3] * back_rows(grads, mask[:, 1:2])
    out_ref[...] = total.astype(bf16)


def state_back(own, other, masks, taps):
    return pl.pallas_call(
        state_back_kernel,
        out_shape=jax.ShapeDtypeStruct(own.shape, bf16),
        cost_estimate=small_cost,
        compiler_params=pltpu.CompilerParams(vmem_limit_bytes=20 << 20),
        name="state_back",
    )(own, other, masks, taps)


def first_half_kernel(place, keep_near, part_near, keep_far, part_far, held_ref, out_ref):
    held_ref[...] = keep_near[...].astype(f32) + part_near[...].astype(f32)
    out_ref[...] = (keep_far[...].astype(f32) + part_far[...].astype(f32)).astype(bf16)


def halve_call(place, keep, partner, specs, half_shape, steps):
    near, far, out = specs
    return pl.pallas_call(
        first_half_kernel,
        grid_spec=pltpu.PrefetchScalarGridSpec(
            num_scalar_prefetch=1,
            grid=(steps,),
            in_specs=[near, near, far, far],
            out_specs=[out, out],
        ),
        out_shape=[
            jax.ShapeDtypeStruct(half_shape, f32),
            jax.ShapeDtypeStruct(half_shape, bf16),
        ],
        cost_estimate=small_cost,
        compiler_params=pltpu.CompilerParams(vmem_limit_bytes=12 << 20),
        name="halve",
    )(place, keep, partner, keep, partner)


def halve_across(place, keep, partner):
    _, rows, width = keep.shape
    near = pl.BlockSpec((1, rows, width), lambda step, place: (step, 0, 0))
    far = pl.BlockSpec((1, rows, width), lambda step, place: (step + 4, 0, 0))
    return halve_call(place, keep, partner, (near, far, near), (4, rows, width), 4)


def halve_plane(place, keep, partner):
    _, rows, width = keep.shape
    block = (2, rows, width // 2)
    near = pl.BlockSpec(block, lambda step, place: (step, 0, place[1]))
    far = pl.BlockSpec(block, lambda step, place: (step, 0, 1 - place[1]))
    out = pl.BlockSpec(block, lambda step, place: (step, 0, 0))
    return halve_call(place, keep, partner, (near, far, out), (8, rows, width // 2), 4)


def two_kernel(near_a, far_a, near_b, far_b, *refs):
    *partners, held_ref, out_ref = refs
    split = near_a.shape[2]
    for index, (near, far) in enumerate(((near_a, far_a), (near_b, far_b))):
        lanes = slice(0, split) if index == 0 else slice(split, None)
        part_near, part_far = partners[2 * index], partners[2 * index + 1]
        held_ref[:, :, lanes] = near[...] + part_near[...].astype(f32)
        out_ref[:, :, lanes] = (far[...] + part_far[...].astype(f32)).astype(bf16)


def halve_two(held_a, part_a, held_b, part_b):
    _, rows, width_a = held_a.shape
    width_b = held_b.shape[2]
    specs = []
    for width in (width_a, width_b):
        block = (1, rows, width)
        specs.append(pl.BlockSpec(block, lambda step: (step, 0, 0)))
        specs.append(pl.BlockSpec(block, lambda step: (step + 4, 0, 0)))
    out = pl.BlockSpec((1, rows, width_a + width_b), lambda step: (step, 0, 0))
    shape = (4, rows, width_a + width_b)
    return pl.pallas_call(
        two_kernel,
        grid=(4,),
        in_specs=specs * 2,
        out_specs=[out, out],
        out_shape=[jax.ShapeDtypeStruct(shape, f32), jax.ShapeDtypeStruct(shape, bf16)],
        cost_estimate=small_cost,
        compiler_params=pltpu.CompilerParams(vmem_limit_bytes=12 << 20),
        name="halve_two",
    )(held_a, held_a, held_b, held_b, part_a, part_a, part_b, part_b)


def column_kernel(held_ref, across_ref, own_ref, *sends):
    own_ref[...] = held_ref[0] + across_ref[0].astype(f32)
    for step, send in enumerate(sends, 1):
        send[...] = (held_ref[step] + across_ref[step].astype(f32)).astype(bf16)


def column_sends(held, across):
    _, rows, width = held.shape
    tile = 384
    out = pl.BlockSpec((rows, tile), lambda step: (0, step))
    block = pl.BlockSpec((4, rows, tile), lambda step: (0, 0, step))
    own, *sends = pl.pallas_call(
        column_kernel,
        grid=(width // tile,),
        in_specs=[block, block],
        out_specs=[out] * 4,
        out_shape=[jax.ShapeDtypeStruct((rows, width), f32)]
        + [jax.ShapeDtypeStruct((rows, width), bf16)] * 3,
        cost_estimate=small_cost,
        compiler_params=pltpu.CompilerParams(vmem_limit_bytes=12 << 20),
        name="column_sends",
    )(held, across)
    return own, sends


def column_arrivals(sends):
    return [exchange(send, 4 * step) for step, send in enumerate(sends, 1)]


def column_total(own, arrived):
    total = own
    for part in arrived:
        total = total + part.astype(f32)
    return total.astype(bf16)


def half_columns(values, first):
    half = values.shape[-1] // 2
    return jnp.where(first, values[..., :half], values[..., half:])


def summed_rows(pairs):
    grads = jnp.concatenate([plain_dot(*pair).astype(bf16) for pair in pairs], axis=1)
    shard = lax.psum_scatter(grads, "page", scatter_dimension=0, tiled=True)
    return shard.astype(f32) + swap(shard).astype(f32)


def page_bounds(segments, is_text):
    pages = jnp.arange(PAGES, dtype=jnp.int32)
    low = jnp.sum(segments[None, :] < pages[:, None], axis=1, dtype=jnp.int32)
    high = jnp.sum(segments[None, :] <= pages[:, None], axis=1, dtype=jnp.int32)
    own_low = jnp.where(is_text, low, pages * PATCH)
    own_high = jnp.where(is_text, high, (pages + 1) * PATCH)

    return jnp.concatenate([own_low, own_high, low, high])


def both_sum(values, mask):
    return values + exchange(values, mask)


def swap(values):
    return lax.ppermute(values, "mod", [(0, 1), (1, 0)])


def local(
    states,
    cotangent,
    segments,
    box_x,
    box_y,
    conv_weight,
    conv_bias,
    w_query,
    b_query,
    w_key,
    w_value,
    b_value,
    w_out,
    b_out,
    table_pos,
    table_x,
    table_y,
    gain_one,
    bias_one,
    w_up,
    b_up,
    w_down,
    b_down,
    gain_two,
    bias_two,
):
    is_text = lax.axis_index("mod") == 0
    d_model = states.shape[3]
    own_low = states[0, 0]
    rows_each = w_query.shape[0]
    d_ff = w_up.shape[1]
    fast = lax.axis_size("page") == 16 and rows_each % 16 == 0 and w_down.shape[0] % 16 == 0
    place = jnp.stack([lax.axis_index("page"), lax.axis_index("mod")]).astype(jnp.int32)
    pack_qkv = jnp.concatenate([w_query, w_key, w_value], axis=1)
    pack_rest = jnp.concatenate([w_out, w_up], axis=1)
    other_low = swap(own_low)
    if fast:
        column_qkv = column_of(half_columns(pack_qkv, is_text))
        table_pos, table_x, table_y, b_out, b_down, b_query, b_value, b_up = after(
            (table_pos, table_x, table_y, b_out, b_down, b_query, b_value, b_up), column_qkv
        )
        gain_one, bias_one, gain_two, bias_two, conv_weight = after(
            (gain_one, bias_one, gain_two, bias_two, conv_weight), column_qkv
        )
        segments, box_x, box_y = after((segments, box_x, box_y), column_qkv)
    page_ids, pos_bins, bins_x, bins_y = token_ids(segments[0], box_x[0], box_y[0])
    bounds = page_bounds(segments[0], is_text)
    own_pages = jnp.where(is_text, page_ids[0], page_ids[1])
    features = bin_features(pos_bins.reshape(-1), bins_x.reshape(-1), bins_y.reshape(-1))
    flipped = bin_features(
        POS_BINS - 1 - pos_bins.reshape(-1),
        BOX_BINS - 1 - bins_x.reshape(-1),
        BOX_BINS - 1 - bins_y.reshape(-1),
    )
    own_feats = jnp.where(is_text, features[:TEXT], features[TEXT:])
    own_flip = jnp.where(is_text, flipped[:TEXT], flipped[TEXT:])
    tables = jnp.stack(
        [
            jnp.pad(table_pos, ((0, 0), (0, LANES - table_pos.shape[1]))),
            jnp.pad(table_x, ((0, 0), (0, LANES - table_x.shape[1]))),
            jnp.pad(table_y, ((0, 0), (0, LANES - table_y.shape[1]))),
        ],
        axis=1,
    )
    tables = jnp.pad(tables, ((0, 0), (0, 5), (0, 0)))

    own_states = own_low.astype(f32)
    mixed = dilated_mix(own_states, own_pages, conv_weight, conv_bias)
    mixed_low = mixed.astype(bf16)
    other_pages = jnp.where(is_text, page_ids[1], page_ids[0])
    masks = jnp.pad(
        jnp.stack(
            [
                own_pages == shifted(own_pages, dilation, -1),
                own_pages == shifted(own_pages, -dilation, -1),
                other_pages == shifted(other_pages, dilation, -1),
                other_pages == shifted(other_pages, -dilation, -1),
            ],
            axis=1,
        ).astype(f32),
        ((0, 0), (0, LANES - 4)),
    )
    vectors = jnp.stack(
        [b_out, gain_one, bias_one, b_down, gain_two, bias_two, jnp.zeros_like(b_out), b_out]
    )
    biases = jnp.concatenate([b_query, jnp.zeros_like(b_value), b_value])[None]
    taps = jnp.pad(conv_weight, ((0, 5), (0, 0)))
    bias_up = b_up[None]
    if fast:
        split = (pack_rest.shape[1] * 2 // 3) // 256 * 256
        early = (features, own_feats, own_flip, tables, bounds, masks, vectors, biases, taps)
        parts_near = column_parts(after(half_columns(pack_rest[:, :split], is_text), column_qkv))
        w_down = after(w_down, column_qkv)
        pieces_qkv = half_pieces(column_qkv)
        column_near = jnp.stack([after(part, pieces_qkv[0]) for part in parts_near])
        parts_far = column_parts(after(pack_rest[:, split:], column_near))
        pieces_near = half_pieces(column_near)
        pieces_qkv[2] = after(pieces_qkv[2], pieces_near[0])
        pieces_qkv[3] = exchange(pieces_qkv[2], 1)
        groups_qkv = (("halves", 0),)
    else:
        groups_qkv = (("full", 0),)
        pieces_qkv = [lax.all_gather(pack_qkv, "page", axis=0, tiled=True)]
    full_down = lax.all_gather(w_down, "page", axis=0, tiled=True)

    other_mixed = dilated_mix(other_low.astype(f32), other_pages, conv_weight, conv_bias)
    other_mixed = other_mixed.astype(bf16)
    mixed_all = jnp.concatenate(
        [jnp.where(is_text, mixed_low, other_mixed), jnp.where(is_text, other_mixed, mixed_low)],
        axis=0,
    )
    if fast:
        pieces_qkv[0] = after(pieces_qkv[0], mixed_all, bias_up, *early)
    queries, keys_values, full_qkv, mixed_t = project(
        place, mixed_all, biases, groups_qkv, pieces_qkv
    )
    attend_in = queries
    if fast:
        column_far = jnp.stack([after(part, queries) for part in parts_far])
        across_far = exchange(column_far, 2)
        attend_in = after(queries, column_far)
    context = attend(bounds, attend_in, keys_values, features, own_feats, tables)
    if fast:
        pieces_near[2] = after(pieces_near[2], context)
        pieces_near[3] = exchange(pieces_near[2], 1)
        across_far = after(across_far, context)
        pieces_rest = pieces_near + row_pieces(column_far, across_far)
        groups_rest = (("halves", 0), ("rows", split))
    else:
        pieces_rest = [lax.all_gather(pack_rest, "page", axis=0, tiled=True)]
        groups_rest = (("full", 0),)
    unit, scale, normed_t, context_t, active, active_t, slope, full_rest = up_forward(
        place, context, mixed, vectors, bias_up, groups_rest, pieces_rest
    )
    output_row, grad_sum_two, grad_ffn, small_two = down_forward(
        active, full_down, unit, vectors, cotangent[0, 0]
    )
    rows_down = grad_rows(active_t, grad_ffn)
    shard_down = lax.psum_scatter(rows_down, "page", scatter_dimension=0, tiled=True)
    grad_hidden, grad_b_up, grad_first, grad_branch, grad_context, small_one = ffn_back(
        after(grad_ffn, rows_down), slope, grad_sum_two, unit, scale, vectors, full_rest, full_down
    )
    attend_in = grad_context
    if fast:
        tiles = grad_hidden.shape[1] // d_model
        pairs = [
            (context_t, False, grad_branch, 0, 1),
            (normed_t, False, grad_hidden, 0, tiles // 2),
        ]
        keep_a, send_a = grad_by_columns(pairs, place, d_model)
        partner_a = exchange(send_a, 1)
        pairs = [(normed_t, False, after(grad_hidden, send_a), tiles // 2, tiles - tiles // 2)]
        keep_b, send_b = grad_by_columns(pairs, place, d_model)
        partner_b = exchange(send_b, 1)
        held_a, plane_a = halve_plane(place, keep_a, after(partner_a, send_b))
        far_a = swap(plane_a)
        held_b, plane_b = halve_plane(place, keep_b, after(partner_b, plane_a))
        far_b = swap(plane_b)
        attend_in = after(grad_context, plane_a, plane_b)
    else:
        shard_rest = summed_rows([(context_t, grad_branch), (normed_t, grad_hidden)])
    grad_queries, grad_keys, grad_values, grad_tables = attend_back(
        bounds, queries, keys_values, attend_in, features, own_feats, own_flip, tables
    )
    grad_keys_in, grad_queries_in = grad_keys, grad_queries
    if fast:
        far_a, far_b = after((far_a, far_b), grad_queries)
        held_rest, across_out = halve_two(held_a, far_a, held_b, far_b)
        across_rest = exchange(across_out, 2)
        grad_queries_in = after(grad_queries, across_out)
    pairs = [
        (mixed_t, True, grad_queries_in, 0, 1),
        (mixed_t, False, grad_keys, 0, 1),
        (mixed_t, False, grad_values, 0, 1),
    ]
    if fast:
        keep_qkv, send_qkv = grad_by_columns(pairs, place, d_model)
        partner_qkv = exchange(send_qkv, 1)
        grad_keys_in = after(grad_keys, send_qkv)
    else:
        shard_down = shard_down.astype(f32) + swap(shard_down).astype(f32)
        shard_qkv = summed_rows(
            [(mixed_low.T, grad_queries), (mixed_t, grad_keys), (mixed_t, grad_values)]
        )
    to_other = input_back(place, full_qkv, grad_keys_in, grad_values, ())
    from_other = swap(to_other)
    grad_values_in = grad_values
    if fast:
        partner_qkv = after(partner_qkv, to_other)
        held_qkv, across_out = halve_across(place, keep_qkv, partner_qkv)
        across_qkv = exchange(across_out, 2)
        grad_values_in = after(grad_values, across_out)
    own_part = input_back(place, full_qkv, grad_keys, grad_values_in, (grad_first, grad_queries))
    packed = small_sums(
        own_part,
        to_other,
        own_low,
        other_low,
        masks,
        grad_queries,
        grad_values,
        small_one,
        small_two,
        grad_b_up,
        grad_tables,
    )
    if fast:
        packed = both_sum(packed, 1)
        shard_down = after(shard_down, packed)
        across_rest = after(across_rest, packed, shard_down)
        shard_down = shard_down.astype(f32) + swap(shard_down).astype(f32)
        own_rest, sends_rest = column_sends(held_rest, across_rest)
        arrived_rest = column_arrivals(sends_rest)
        packed = after(packed, *sends_rest)
        packed = packed + swap(packed)
        from_other = after(from_other, packed)
    else:
        packed = lax.psum(packed, ("mod", "page"))
    grad_in = state_back(own_part, from_other, masks, taps)
    if fast:
        across_qkv = after(across_qkv, packed, grad_in)
        own_qkv, sends_qkv = column_sends(held_qkv, across_qkv)
        arrived_qkv = column_arrivals(sends_qkv)
    if fast:
        arrived_rest = [after(part, *sends_qkv) for part in arrived_rest]
        total_rest = column_total(own_rest, arrived_rest)
        far_rest = swap(total_rest)
        packed = both_sum(both_sum(after(packed, total_rest), 2), 4)
        arrived_qkv = [after(part, packed) for part in arrived_qkv]
        total_qkv = column_total(own_qkv, arrived_qkv)
        far_qkv = swap(total_qkv)
        packed = both_sum(after(packed, total_qkv), 8)
    g_tables = packed[28:34].reshape(HEADS, 3, LANES)
    if fast:
        cut = far_a.shape[2]
        first_plane = jnp.where(is_text, total_rest, far_rest)
        second_plane = jnp.where(is_text, far_rest, total_rest)
        shard_rest = jnp.concatenate(
            [first_plane[:, :cut], second_plane[:, :cut], first_plane[:, cut:], second_plane[:, cut:]],
            axis=1,
        ).astype(f32)
        shard_qkv = total_qkv.astype(f32) + far_qkv.astype(f32)
    return (
        output_row[None, None],
        grad_in[None, None],
        packed[0:3],
        packed[3],
        shard_qkv[:, :d_model],
        packed[4],
        shard_qkv[:, d_model : 2 * d_model],
        shard_qkv[:, 2 * d_model :],
        packed[5],
        shard_rest[:, :d_model],
        packed[10],
        g_tables[:, 0, : table_pos.shape[1]],
        g_tables[:, 1, 64 : 64 + table_x.shape[1]],
        g_tables[:, 2, 64 : 64 + table_y.shape[1]],
        packed[8],
        packed[9],
        shard_rest[:, d_model:],
        packed[24:28].reshape(d_ff),
        shard_down,
        packed[18],
        packed[16],
        packed[17],
    )


def solution(mesh):
    rows = P("mod", "page", None, None)
    ids = P("page", None)
    cut = P("page", None)
    return jax.shard_map(
        local,
        mesh=mesh,
        in_specs=(
            rows, rows, ids, ids, ids, P(), P(), cut, P(), cut, cut, P(), cut,
            P(), P(), P(), P(), P(), P(), cut, P(), cut, P(), P(), P(),
        ),
        out_specs=(
            rows, rows, P(), P(), cut, P(), cut, cut, P(), cut, P(), P(), P(),
            P(), P(), P(), cut, P(), cut, P(), P(), P(),
        ),
        check_vma=False,
    )
```
